32 devices in a mesh: seq: 8 (over z, y), head: 4 (over x, core).
Axes of the slice: x: 2, y: 2, z: 4, core: 2. Of those that a mesh axis runs over, the one named last changes fastest.
Arguments:
- block_input: bfloat16 [8192, 1024], P(('seq', 'head')), may hold values from -6 to 6
- out_grad: bfloat16 [8192, 1024], P(('seq', 'head')), may hold values from -6 to 6
- lengths: int32 [16], replicated, may hold values from 1 to 4096, 8192 in all
- doc_sets: int32 [16], replicated, may hold values from 0 to 7
- norm1_gain: float32 [1024], replicated, may hold values from 0.5 to 1.5
- w_query: bfloat16 [1024, 1024], P(None, 'head'), may hold values from -0.1875 to 0.1875
- w_key: bfloat16 [1024, 1024], P(None, 'head'), may hold values from -0.1875 to 0.1875
- w_value: bfloat16 [1024, 2048], P(None, 'head'), may hold values from -0.1875 to 0.1875
- conv_query: bfloat16 [4, 1024], P(None, 'head'), may hold values from -0.59765625 to 0.59765625
- conv_key: bfloat16 [4, 1024], P(None, 'head'), may hold values from -0.59765625 to 0.59765625
- conv_value: bfloat16 [4, 2048], P(None, 'head'), may hold values from -0.59765625 to 0.59765625
- w_decay_beta: bfloat16 [1024, 2, 8], P(None, None, 'head'), may hold values from -0.1875 to 0.1875
- decay_rate: float32 [8], P('head'), may hold values from 0.0003 to 0.1
- decay_bias: float32 [8], P('head'), may hold values from -1 to 1
- w_gate_out: bfloat16 [1024, 2048], P(None, 'head'), may hold values from -0.1875 to 0.1875
- out_gain: float32 [256], replicated, may hold values from 0.5 to 1.5
- w_out: bfloat16 [2048, 1024], P('head'), may hold values from -0.1875 to 0.1875
- norm2_gain: float32 [1024], replicated, may hold values from 0.5 to 1.5
- w_gate: bfloat16 [1024, 2816], P(None, 'head'), may hold values from -0.1875 to 0.1875
- w_up: bfloat16 [1024, 2816], P(None, 'head'), may hold values from -0.1875 to 0.1875
- w_down: bfloat16 [2816, 1024], P('head'), may hold values from -0.15625 to 0.15625
- adapt_down: bfloat16 [6, 8, 1024, 16], replicated, may hold values from -0.1875 to 0.1875
- adapt_up_qk: bfloat16 [2, 8, 16, 1024], P(None, None, None, 'head'), may hold values from -0.75 to 0.75
- adapt_up_vg: bfloat16 [2, 8, 16, 2048], P(None, None, None, 'head'), may hold values from -0.75 to 0.75
- adapt_up_ff: bfloat16 [2, 8, 16, 2816], P(None, None, None, 'head'), may hold values from -0.75 to 0.75
- adapt_down_out: bfloat16 [8, 2048, 16], P(None, 'head'), may hold values from -0.125 to 0.125
- adapt_down_ffd: bfloat16 [8, 2816, 16], P(None, 'head'), may hold values from -0.109375 to 0.109375
- adapt_up_res: bfloat16 [2, 8, 16, 1024], replicated, may hold values from -0.75 to 0.75
Outputs:
- block_output: bfloat16 [8192, 1024], P(('seq', 'head'))
- input_grad: float32 [8192, 1024], P(('seq', 'head'))
- adapt_down_grad: float32 [6, 8, 1024, 16], replicated
- adapt_up_qk_grad: float32 [2, 8, 16, 1024], P(None, None, None, 'head')
- adapt_up_vg_grad: float32 [2, 8, 16, 2048], P(None, None, None, 'head')
- adapt_up_ff_grad: float32 [2, 8, 16, 2816], P(None, None, None, 'head')
- adapt_down_out_grad: float32 [8, 2048, 16], P(None, 'head')
- adapt_down_ffd_grad: float32 [8, 2816, 16], P(None, 'head')
- adapt_up_res_grad: float32 [2, 8, 16, 1024], replicated
The draws below stay inside these ranges and needn't reach their ends.
Inputs may be any that keep to these rules, and one draw needn't show every extreme that they name: Documents in stream order; the lengths sum to 8192 and one document has exactly 4096 tokens.
All inputs are finite; a program needn't handle non-finite values.
Results may differ from the reference program's by a relative error of at most 0.014.
Values may be sent and summed in bfloat16 or wider, within the bound.
No kernel may reach another device: no remote copies, remote signals or barrier semaphores. Data moves between devices by JAX's collectives and lax.ppermute only.
A program may use at most 256 MiB of HBM per device.

```python
import math
import jax
import jax.numpy as jnp
import numpy as np
from jax import lax

D = 1024
H = 8
DK = 128
DV = 256
FF = 2816
CONV = 4
SPAN = 64
RANK = 16
SETS = 8
DOC_MAX = 4096
TOKENS = 8192
DOCS = 16


def place_ends(values, own_key, low, largest):
    shape = values.shape
    index_at = [jax.random.randint(jax.random.fold_in(own_key, axis), (), 0, shape[axis]) for axis in range(len(shape))]
    values = values.at[tuple(index_at)].set(low)
    longest = shape.index(max(shape))
    index_at[longest] = (index_at[longest] + 1) % shape[longest]
    return values.at[tuple(index_at)].set(largest)


def steps_of(own_key, dims, shards, least, top_value):
    level, own = 1.0, jax.random.fold_in(own_key, 6)
    for dim, shards_of in shards:
        steps = jnp.exp(jax.random.uniform(jax.random.fold_in(own, dim), (shards_of,), jnp.float32, least / len(shards), top_value / len(shards)))
        level = level * jnp.repeat(steps, dims[dim] // shards_of).reshape([-1 if axis == dim else 1 for axis in range(len(dims))])
    return level


def length_profile(count, total, most, skew):
    weights = [(1 << 20) // math.isqrt(rank ** skew) + 1 for rank in range(2, count + 1)]
    rest, holding = total - most - (count - 1), [1] * (count - 1)
    while rest > 0:
        candidates = [i for i in range(count - 1) if holding[i] < most]
        mass, remaining = sum([weights[i] for i in candidates]), rest
        for i in candidates:
            more = min(most - holding[i], max(1, remaining * weights[i] // mass), rest)
            holding[i] = holding[i] + more
            rest = rest - more
    return np.array([most] + holding)


def uneven(key, number_of, total, most, lean):
    if number_of == 2:
        one = jax.random.randint(key, (), max(1, total - most), min(most, total - 1) + 1)
        return jnp.stack([one, total - one])
    sizes = jnp.asarray(length_profile(number_of, total, most, lean), jnp.int32)
    twos = (number_of - 1) // 2
    giver, taker = sizes[1:1 + 2 * twos:2], sizes[2:2 + 2 * twos:2]
    margin = jnp.minimum(giver - 1, most - taker)
    moved = jax.random.randint(jax.random.fold_in(key, 1), (twos,), 0, 1 << 20) % (margin + 1)
    sizes = sizes.at[1:1 + 2 * twos:2].set(giver - moved).at[2:2 + 2 * twos:2].set(taker + moved)
    return sizes[jax.random.permutation(jax.random.fold_in(key, 2), number_of)]


def centred(own_key, shape, spread, most, shards=(), kind=jnp.bfloat16):
    level = steps_of(own_key, shape, shards, -0.22, 0.18) if shards else 1.0
    entries = jax.random.normal(own_key, shape, jnp.float32) * spread * level
    return jnp.minimum(jnp.maximum(entries, -most), most).astype(kind)


def setup_inputs(seed: int = 0) -> dict:
    key_list = jax.random.split(jax.random.key(seed), 29)
    block_input = centred(key_list[0], (TOKENS, D), 1.0, 6.0, ((0, 32),))
    out_grad = centred(key_list[1], (TOKENS, D), 1.0, 6.0, ((0, 32),))
    lengths = uneven(key_list[2], DOCS, TOKENS, DOC_MAX, 2).astype(jnp.int32)
    doc_sets = place_ends(jax.random.randint(key_list[3], (DOCS,), 0, SETS), jax.random.fold_in(key_list[3], 1), 0, SETS - 1).astype(jnp.int32)
    norm1_gain = jnp.clip(1.0 + 0.1 * jax.random.normal(key_list[4], (D,), jnp.float32), 0.5, 1.5)
    w_query = centred(key_list[5], (D, H * DK), D ** -0.5, 0.1875, ((1, 4),))
    w_key = centred(key_list[6], (D, H * DK), D ** -0.5, 0.1875, ((1, 4),))
    w_value = centred(key_list[7], (D, H * DV), D ** -0.5, 0.1875, ((1, 4),))
    conv_query = jnp.clip(jax.random.uniform(key_list[8], (CONV, H * DK), jnp.float32, -0.59765625, 0.59765625) * steps_of(key_list[8], (CONV, H * DK), ((1, 4),), -0.4, 0.0), -0.59765625, 0.59765625).astype(jnp.bfloat16)
    conv_key = jnp.clip(jax.random.uniform(key_list[9], (CONV, H * DK), jnp.float32, -0.59765625, 0.59765625) * steps_of(key_list[9], (CONV, H * DK), ((1, 4),), -0.4, 0.0), -0.59765625, 0.59765625).astype(jnp.bfloat16)
    conv_value = jnp.clip(jax.random.uniform(key_list[10], (CONV, H * DV), jnp.float32, -0.59765625, 0.59765625) * steps_of(key_list[10], (CONV, H * DV), ((1, 4),), -0.4, 0.0), -0.59765625, 0.59765625).astype(jnp.bfloat16)
    w_decay_beta = centred(key_list[11], (D, 2, H), D ** -0.5, 0.1875, ((2, 4),))
    decay_rate = jnp.clip(jnp.exp(math.log(0.1) - 5.809143 * jax.random.uniform(key_list[12], (H,), jnp.float32) ** steps_of(key_list[12], (H,), ((0, 4),), -0.2, 0.2)), 0.0003, 0.1)
    decay_bias = jnp.clip(jax.random.uniform(key_list[13], (H,), jnp.float32, -1.0, 1.0) * steps_of(key_list[13], (H,), ((0, 4),), -0.4, 0.0), -1.0, 1.0)
    w_gate_out = centred(key_list[14], (D, H * DV), D ** -0.5, 0.1875, ((1, 4),))
    out_gain = jnp.clip(1.0 + 0.1 * jax.random.normal(key_list[15], (DV,), jnp.float32), 0.5, 1.5)
    w_out = centred(key_list[16], (H * DV, D), (H * DV // 2) ** -0.5, 0.1875, ((0, 4),))
    norm2_gain = jnp.clip(1.0 + 0.1 * jax.random.normal(key_list[17], (D,), jnp.float32), 0.5, 1.5)
    w_gate = centred(key_list[18], (D, FF), D ** -0.5, 0.1875, ((1, 4),))
    w_up = centred(key_list[19], (D, FF), D ** -0.5, 0.1875, ((1, 4),))
    w_down = centred(key_list[20], (FF, D), (FF // 2) ** -0.5, 0.15625, ((0, 4),))
    adapt_down = centred(key_list[21], (6, SETS, D, RANK), D ** -0.5, 0.1875)
    adapt_up_qk = centred(key_list[22], (2, SETS, RANK, H * DK), (4 * RANK) ** -0.5, 0.75, ((3, 4),))
    adapt_up_vg = centred(key_list[23], (2, SETS, RANK, H * DV), (4 * RANK) ** -0.5, 0.75, ((3, 4),))
    adapt_up_ff = centred(key_list[24], (2, SETS, RANK, FF), (4 * RANK) ** -0.5, 0.75, ((3, 4),))
    adapt_down_out = centred(key_list[25], (SETS, H * DV, RANK), (H * DV) ** -0.5, 0.125, ((1, 4),))
    adapt_down_ffd = centred(key_list[26], (SETS, FF, RANK), FF ** -0.5, 0.109375, ((1, 4),))
    adapt_up_res = centred(key_list[27], (2, SETS, RANK, D), (4 * RANK) ** -0.5, 0.75)
    return {"block_input": block_input, "out_grad": out_grad, "lengths": lengths, "doc_sets": doc_sets, "norm1_gain": norm1_gain, "w_query": w_query, "w_key": w_key, "w_value": w_value, "conv_query": conv_query, "conv_key": conv_key, "conv_value": conv_value, "w_decay_beta": w_decay_beta, "decay_rate": decay_rate, "decay_bias": decay_bias, "w_gate_out": w_gate_out, "out_gain": out_gain, "w_out": w_out, "norm2_gain": norm2_gain, "w_gate": w_gate, "w_up": w_up, "w_down": w_down, "adapt_down": adapt_down, "adapt_up_qk": adapt_up_qk, "adapt_up_vg": adapt_up_vg, "adapt_up_ff": adapt_up_ff, "adapt_down_out": adapt_down_out, "adapt_down_ffd": adapt_down_ffd, "adapt_up_res": adapt_up_res}


exact_mode = lax.Precision.HIGHEST
epsilon = 1e-06

@jax.custom_vjp
def low(v):
    return lax.optimization_barrier(v.astype(jnp.bfloat16)).astype(jnp.float32)

@jax.custom_vjp
def low_back(v):
    return v

def low_keep(v):
    return (low(v), None)

def low_pass(kept, grad):
    return (grad,)

def back_keep(v):
    return (v, None)

def back_low(kept, grad):
    return (low(grad),)
low.defvjp(low_keep, low_pass)
low_back.defvjp(back_keep, back_low)

def exact_product(left, right):
    return jnp.dot(left, right, precision=exact_mode, preferred_element_type=jnp.float32)

def rms_scale(rows, gain):
    return rows * lax.rsqrt(lax.optimization_barrier(jnp.mean(rows * rows, axis=-1, keepdims=True)) + epsilon) * gain

def doc_tables(lengths, doc_sets, count):
    starts = jnp.cumsum(lengths) - lengths
    positions = jnp.arange(count, dtype=jnp.int32)
    docs = lax.optimization_barrier(jnp.sum((positions[:, None] >= starts[None, :]).astype(jnp.int32), axis=1)) - 1
    first = lax.optimization_barrier(jnp.sum((positions[:, None] == starts[None, :]).astype(jnp.int32), axis=1))
    return (docs.astype(jnp.int32), first, doc_sets[docs].astype(jnp.int32))

def adapter(rows, down, upper, token_document_sets, rounded):
    flat_down = jnp.transpose(down, (1, 0, 2)).reshape(down.shape[1], SETS * RANK)
    inner = exact_product(rows, flat_down)
    if rounded:
        inner = low(inner)
    columns = (jnp.arange(SETS * RANK, dtype=jnp.int32) // RANK)[None, :]
    inner = jnp.where(columns == token_document_sets[:, None], inner, 0.0)
    return exact_product(inner, upper.reshape(SETS * RANK, -1))

def short_conv(before, kernel, docs):
    count = before.shape[0]
    padded = jnp.concatenate([jnp.zeros((CONV - 1, before.shape[1]), jnp.float32), before])
    padded_docs = jnp.concatenate([jnp.full((CONV - 1,), -1, jnp.int32), docs])
    total = jnp.zeros_like(before)
    for tap in range(CONV):
        same = (padded_docs[tap:tap + count] == docs)[:, None]
        total = total + jnp.where(same, padded[tap:tap + count] * kernel[tap][None, :], 0.0)
    return total

def delta_rule(query, key, value, factor, beta):
    blocks = query.shape[0] // SPAN

    def split(array):
        return array.reshape((blocks, SPAN) + array.shape[1:])

    def token_step(state, item):
        query_now, key_now, value_now, factor_now, beta_now = item
        kept = factor_now[:, None, None] * state
        predicted = jnp.einsum('hvk,hk->hv', kept, key_now, precision=exact_mode)
        state = kept + (beta_now[:, None] * (value_now - predicted))[:, :, None] * key_now[:, None, :]
        return (state, jnp.einsum('hvk,hk->hv', state, query_now, precision=exact_mode))

    def block_step(state, pieces):
        return lax.scan(token_step, state, pieces)
    start = jnp.zeros((H, DV, DK), jnp.float32)
    _, outputs = lax.scan(jax.checkpoint(block_step), start, (split(query), split(key), split(value), split(factor), split(beta)))
    return outputs.reshape(value.shape)

def reference(block_input, out_grad, lengths, doc_sets, norm1_gain, w_query, w_key, w_value, conv_query, conv_key, conv_value, w_decay_beta, decay_rate, decay_bias, w_gate_out, out_gain, w_out, norm2_gain, w_gate, w_up, w_down, adapt_down, adapt_up_qk, adapt_up_vg, adapt_up_ff, adapt_down_out, adapt_down_ffd, adapt_up_res):
    docs, first, token_document_sets = doc_tables(lengths, doc_sets, TOKENS)
    query_weight = w_query.astype(jnp.float32)
    key_weight = w_key.astype(jnp.float32)
    value_weight = w_value.astype(jnp.float32)
    kernel_query = conv_query.astype(jnp.float32)
    kernel_key = conv_key.astype(jnp.float32)
    kernel_value = conv_value.astype(jnp.float32)
    mix_weight = w_decay_beta.astype(jnp.float32).reshape(D, 2 * H)
    gate_out_weight = w_gate_out.astype(jnp.float32)
    out_weight = w_out.astype(jnp.float32)
    gate_weight = w_gate.astype(jnp.float32)
    up_weight = w_up.astype(jnp.float32)
    down_weight = w_down.astype(jnp.float32)
    keep = (1 - first).astype(jnp.float32)

    def forward(inputs, down_maps, up_qk, up_vg, up_ff, down_out, down_ffd, up_res):
        normed = low(rms_scale(inputs, norm1_gain))
        pre_query = low_back(low(exact_product(normed, query_weight) + adapter(normed, down_maps[0], up_qk[0], token_document_sets, True)))
        pre_key = low_back(low(exact_product(normed, key_weight) + adapter(normed, down_maps[1], up_qk[1], token_document_sets, True)))
        pre_value = low_back(low(exact_product(normed, value_weight) + adapter(normed, down_maps[2], up_vg[0], token_document_sets, True)))
        gate_input = low_back(exact_product(normed, gate_out_weight) + adapter(normed, down_maps[3], up_vg[1], token_document_sets, True))
        mixing = exact_product(normed, mix_weight).reshape(-1, 2, H)
        query = jax.nn.silu(short_conv(pre_query, kernel_query, docs)).reshape(-1, H, DK)
        key = jax.nn.silu(short_conv(pre_key, kernel_key, docs)).reshape(-1, H, DK)
        value = jax.nn.silu(short_conv(pre_value, kernel_value, docs)).reshape(-1, H, DV)
        query = query * lax.rsqrt(lax.optimization_barrier(jnp.sum(query * query, axis=-1, keepdims=True)) + epsilon) * DK ** (-0.5)
        key = key * lax.rsqrt(lax.optimization_barrier(jnp.sum(key * key, axis=-1, keepdims=True)) + epsilon)
        beta = jax.nn.sigmoid(mixing[:, 0, :])
        decay = -decay_rate[None, :] * jax.nn.softplus(mixing[:, 1, :] + decay_bias[None, :])
        factor = jnp.exp(decay) * keep[:, None]
        output = delta_rule(query, key, value, factor, beta)
        output = rms_scale(output, out_gain).reshape(-1, H * DV) * jax.nn.silu(gate_input)
        mixed = low(output)
        residual = inputs + low_back(exact_product(mixed, out_weight) + adapter(mixed, down_out, up_res[0], token_document_sets, False))
        normed_mid = low(rms_scale(residual, norm2_gain))
        gate_value = low_back(exact_product(normed_mid, gate_weight) + adapter(normed_mid, down_maps[4], up_ff[0], token_document_sets, True))
        up_value = low_back(exact_product(normed_mid, up_weight) + adapter(normed_mid, down_maps[5], up_ff[1], token_document_sets, True))
        hidden_activations = low(jax.nn.silu(gate_value) * up_value)
        return residual + low_back(exact_product(hidden_activations, down_weight) + adapter(hidden_activations, down_ffd, up_res[1], token_document_sets, False))
    result, back = jax.vjp(forward, block_input.astype(jnp.float32), adapt_down.astype(jnp.float32), adapt_up_qk.astype(jnp.float32), adapt_up_vg.astype(jnp.float32), adapt_up_ff.astype(jnp.float32), adapt_down_out.astype(jnp.float32), adapt_down_ffd.astype(jnp.float32), adapt_up_res.astype(jnp.float32))
    grads = back(out_grad.astype(jnp.float32))
    return (result.astype(jnp.bfloat16), grads[0], grads[1], grads[2], grads[3], grads[4], grads[5], grads[6], grads[7])
```

```python
import functools

import jax
import jax.numpy as jnp
from jax import lax
from jax.experimental import pallas as pl
from jax.experimental.pallas import tpu as pltpu
from jax.sharding import PartitionSpec as P

CHUNK = 128
STEP = 256
HALO = 16
DOC_MAX = 4096
EPS = 1e-06
VMEM_LIMIT = 56 * 1024 * 1024
bfloat = jnp.bfloat16
single = jnp.float32


def contract(left, right, left_dim, right_dim):
    return lax.dot_general(
        left,
        right,
        (((left_dim,), (right_dim,)), ((), ())),
        preferred_element_type=single,
    )


def nn(left, right):
    return contract(left, right, 1, 0)


def nt(left, right):
    return contract(left, right, 1, 1)


def tn(left, right):
    return contract(left, right, 0, 0)


def low(array):
    return array.astype(bfloat)


def iotas():
    rows = lax.broadcasted_iota(jnp.int32, (CHUNK, CHUNK), 0)
    columns = lax.broadcasted_iota(jnp.int32, (CHUNK, CHUNK), 1)
    return rows, columns


def split_two(array):
    high = low(array)
    return high, low(array - high.astype(single))


def near_exact(left, right):
    left_high, left_low = split_two(left)
    right_high, right_low = split_two(right)
    return nn(
        jnp.concatenate([left_high, left_high, left_low], axis=1),
        jnp.concatenate([right_high, right_low, right_high], axis=0),
    )


def ones_product(ones, array):
    high = low(array)
    rest = array - high.astype(single)
    middle = low(rest)
    lowest = low(rest - middle.astype(single))
    return nn(
        jnp.concatenate([ones, ones, ones], axis=1),
        jnp.concatenate([high, middle, lowest], axis=0),
    )


def unit_lower_inverse(strict, rows, columns):
    eye = (rows == columns).astype(single)
    block = 8
    inner = jnp.where((rows // block) == (columns // block), strict, 0.0)
    second = near_exact(inner, inner)
    fourth = near_exact(second, second)
    inverse = near_exact(near_exact(eye - inner, eye + second), eye + fourth)
    while block < CHUNK:
        pair = 2 * block
        off = jnp.where(
            ((rows // pair) == (columns // pair)) & ((rows // block) != (columns // block)),
            strict,
            0.0,
        )
        inverse = inverse - near_exact(inverse, near_exact(off, inverse))
        block = pair
    return inverse


def softplus(value):
    return jnp.maximum(value, 0.0) + jnp.log(1.0 + jnp.exp(-jnp.abs(value)))


def sigmoid(value):
    return 1.0 / (1.0 + jnp.exp(-value))


def gates(decay, start, rows, columns):
    lower_ones = low((rows >= columns).astype(single))
    total = ones_product(lower_ones, jnp.broadcast_to(decay, (CHUNK, CHUNK)))
    linked = (rows >= columns) & (columns >= start)
    within = jnp.where(linked, jnp.exp(jnp.where(linked, total - total.T, 0.0)), 0.0)
    running = total[:, :1]
    carried = jnp.where(start < 0, jnp.exp(running), 0.0)
    last = running[CHUNK - 1 : CHUNK]
    ending = jnp.where(
        rows[:, :1] >= start[CHUNK - 1 : CHUNK], jnp.exp(jnp.minimum(last - running, 0.0)), 0.0
    )
    return within, carried, ending


def convolved(window, starts, weights, base):
    positions = base + lax.broadcasted_iota(jnp.int32, (STEP, 1), 0)
    taps = weights.shape[0]
    total = None
    for tap in range(taps):
        back = taps - 1 - tap
        term = window[HALO - back : HALO - back + STEP, :] * weights[tap : tap + 1, :]
        if back:
            term = jnp.where(positions - back >= starts, term, 0.0)
        total = term if total is None else total + term
    return total


def head_scales(rows, width):
    return lax.rsqrt(jnp.sum(rows * rows, axis=-1, keepdims=True) + EPS)


def forward_kernel(
    place,
    rows_ref,
    halo_ref,
    column_ref,
    weight_ref,
    scalar_ref,
    out_ref,
    map_ref,
    written_ref,
    state_ref,
    inverse_ref,
    end_ref,
    window,
    state,
    *,
    heads,
    key_width,
    value_width,
):
    step = pl.program_id(0)
    wide = value_width + key_width
    base = step * STEP
    rows, columns = iotas()

    @pl.when(step == 0)
    def _():
        window[0:HALO, :] = halo_ref[...].astype(single)
        for h in range(heads):
            state[h, :, :value_width] = jnp.zeros((key_width, value_width), single)
            state[h, :, value_width:] = (rows == columns).astype(single)

    @pl.when(step > 0)
    def _():
        window[0:HALO, :] = window[STEP : STEP + HALO, :]

    window[HALO:, :] = rows_ref[...].astype(single)
    info = column_ref[...]
    starts = info[:, 2 * heads : 2 * heads + 1].astype(jnp.int32)
    before = convolved(window, starts, weight_ref[...], base)
    active = before * sigmoid(before)
    qk_lanes = heads * key_width
    chunks = STEP // CHUNK
    local = []
    for c in range(chunks):
        span = slice(c * CHUNK, (c + 1) * CHUNK)
        for h in range(heads):
            query = active[span, h * key_width : (h + 1) * key_width]
            key = active[span, qk_lanes + h * key_width : qk_lanes + (h + 1) * key_width]
            value = active[
                span, 2 * qk_lanes + h * value_width : 2 * qk_lanes + (h + 1) * value_width
            ]
            query = query * (head_scales(query, key_width) * key_width ** (-0.5))
            key = key * head_scales(key, key_width)
            beta = sigmoid(info[span, h : h + 1])
            decay = -scalar_ref[0, h] * softplus(
                info[span, heads + h : heads + h + 1] + scalar_ref[1, h]
            )
            within, carried, ending = gates(
                decay, starts[span] - (base + c * CHUNK), rows, columns
            )
            query, key = low(query), low(key)
            strict = jnp.where(rows > columns, within * nt(key, key), 0.0) * beta
            inverse = low(unit_lower_inverse(strict, rows, columns))
            mixed = low(within * nt(query, key))
            inverse_ref[span, h * CHUNK : (h + 1) * CHUNK] = inverse
            local.append((query, key, value, beta, carried, ending, inverse, mixed))
    for c in range(chunks):
        span = slice(c * CHUNK, (c + 1) * CHUNK)
        for h in range(heads):
            query, key, value, beta, carried, ending, inverse, mixed = local[c * heads + h]
            now = state[h]
            now_low = low(now)
            state_ref[c, h] = now_low
            read = nn(key, now_low)
            gap = -(carried * beta) * read
            target = jnp.concatenate(
                [beta * value + gap[:, :value_width], gap[:, value_width:]], axis=1
            )
            written = nn(inverse, low(target))
            written_ref[span, h * wide : (h + 1) * wide] = low(written)
            output = carried * nn(query, now_low) + nn(mixed, low(written))
            out_ref[span, h * value_width : (h + 1) * value_width] = output[:, :value_width]
            map_ref[span, h * key_width : (h + 1) * key_width] = low(output[:, value_width:])
            state[h] = carried[CHUNK - 1 : CHUNK] * now + tn(key, low(ending * written))

    @pl.when(step == pl.num_programs(0) - 1)
    def _():
        end_ref[...] = state[...]


def backward_kernel(
    place,
    rows_ref,
    before_ref,
    column_ref,
    weight_ref,
    scalar_ref,
    grad_ref,
    written_ref,
    state_ref,
    inverse_ref,
    end_ref,
    entering_ref,
    later_ref,
    out_ref,
    mix_ref,
    tail_ref,
    edge_ref,
    window,
    shifted,
    shifted_start,
    cotangent,
    ahead,
    *,
    heads,
    key_width,
    value_width,
):
    step = pl.program_id(0)
    steps = pl.num_programs(0)
    wide = value_width + key_width
    base = (steps - 1 - step) * STEP
    rows, columns = iotas()
    qk_lanes = heads * key_width
    lanes = window.shape[1]
    taps = weight_ref.shape[0]

    @pl.when(step == 0)
    def _():
        shifted[STEP : STEP + 8, :] = jnp.zeros((8, lanes), single)
        shifted_start[STEP : STEP + 8, :] = jnp.zeros((8, 1), jnp.int32)
        for h in range(heads):
            cotangent[h] = later_ref[h].astype(single)
            ahead[h] = end_ref[h, :, :value_width] + nn(
                low(end_ref[h, :, value_width:]), low(entering_ref[h])
            )

    @pl.when(step > 0)
    def _():
        shifted[STEP : STEP + 8, :] = shifted[0:8, :]
        shifted_start[STEP : STEP + 8, :] = shifted_start[0:8, :]

    window[0:HALO, :] = before_ref[...].astype(single)
    window[HALO:, :] = rows_ref[...].astype(single)
    info = column_ref[...]
    starts = info[:, 2 * heads : 2 * heads + 1].astype(jnp.int32)
    positions = base + lax.broadcasted_iota(jnp.int32, (STEP, 1), 0)
    before = convolved(window, starts, weight_ref[...], base)
    gate = sigmoid(before)
    active = before * gate
    slope = gate * (1.0 + before * (1.0 - gate))
    upper_ones = low((rows <= columns).astype(single))
    last_row = rows[:, :1] == CHUNK - 1
    chunks = STEP // CHUNK
    for c in reversed(range(chunks)):
        span = slice(c * CHUNK, (c + 1) * CHUNK)
        beta_grads, decay_grads = [], []
        for h in range(heads):
            q_lanes = slice(h * key_width, (h + 1) * key_width)
            k_lanes = slice(qk_lanes + h * key_width, qk_lanes + (h + 1) * key_width)
            v_lanes = slice(2 * qk_lanes + h * value_width, 2 * qk_lanes + (h + 1) * value_width)
            query_raw, key_raw = active[span, q_lanes], active[span, k_lanes]
            query_scale = head_scales(query_raw, key_width)
            key_scale = head_scales(key_raw, key_width)
            query = query_raw * (query_scale * key_width ** (-0.5))
            key = key_raw * key_scale
            beta = sigmoid(info[span, h : h + 1])
            beta_left = sigmoid(-info[span, h : h + 1])
            raw = info[span, heads + h : heads + h + 1] + scalar_ref[1, h]
            decay = -scalar_ref[0, h] * softplus(raw)
            within, carried, ending = gates(
                decay, starts[span] - (base + c * CHUNK), rows, columns
            )
            query_low, key_low = low(query), low(key)
            mixed = low(within * nt(query_low, key_low))
            entering = low(entering_ref[h])
            kept = written_ref[span, h * wide : (h + 1) * wide]
            written = kept[:, :value_width].astype(single) + nn(kept[:, value_width:], entering)
            written_low = low(written)
            saved = state_ref[c, h]
            start_state = saved[:, :value_width].astype(single) + nn(
                saved[:, value_width:], entering
            )
            start_low = low(start_state)
            grad = grad_ref[span, h * value_width : (h + 1) * value_width]
            grad_low = low(grad)
            later = cotangent[h]
            later_low = low(later)
            inverse = inverse_ref[span, h * CHUNK : (h + 1) * CHUNK]
            written_grad = tn(mixed, grad_low) + ending * nn(key_low, later_low)
            solved = tn(inverse, low(written_grad))
            value_grad = beta * solved
            value_grad_low = low(value_grad)
            read_grad = low(-carried * value_grad)
            carried_grad = low(carried * grad)
            mixed_grad = low(within * nt(grad_low, written_low))
            strict_grad = low(
                jnp.where(rows > columns, -within * nt(value_grad_low, written_low), 0.0)
            )
            query_grad = nt(carried_grad, start_low) + nn(mixed_grad, key_low)
            key_read = nt(read_grad, start_low) + nn(strict_grad, key_low)
            key_write = (
                tn(strict_grad, key_low)
                + tn(mixed_grad, query_low)
                + nt(low(ending * written), later_low)
            )
            cotangent[h] = (
                carried[CHUNK - 1 : CHUNK] * later + tn(query_low, carried_grad) + tn(key_low, read_grad)
            )
            query_dot = jnp.sum(query * query_grad, axis=-1, keepdims=True)
            at_end = jnp.sum(later * ahead[h], keepdims=True)
            running_grad = (
                query_dot
                + jnp.sum(key * (key_read - key_write), axis=-1, keepdims=True)
                + jnp.where(last_row, at_end, 0.0)
            )
            ahead[h] = start_state
            decay_grad = ones_product(
                upper_ones, jnp.broadcast_to(running_grad, (CHUNK, CHUNK))
            )[:, :1]
            decay_grad = jnp.where(positions[span] == starts[span], 0.0, decay_grad)
            beta_grads.append(jnp.sum(solved * written, axis=-1, keepdims=True) * beta_left)
            decay_grads.append(-scalar_ref[0, h] * sigmoid(raw) * decay_grad)
            key_grad = key_read + key_write
            key_dot = jnp.sum(key * key_grad, axis=-1, keepdims=True)
            query_active = (query_scale * key_width ** (-0.5)) * query_grad - query_raw * (
                query_scale * query_scale * query_dot
            )
            key_active = key_scale * (key_grad - key * key_dot)
            shifted[span, q_lanes] = query_active * slope[span, q_lanes]
            shifted[span, k_lanes] = key_active * slope[span, k_lanes]
            shifted[span, v_lanes] = value_grad * slope[span, v_lanes]
        mix_ref[span, :] = jnp.concatenate(
            beta_grads + decay_grads + [jnp.zeros((CHUNK, mix_ref.shape[1] - 2 * heads), single)],
            axis=1,
        )
    shifted_start[0:STEP, :] = starts
    total = None
    for tap in range(taps):
        back = taps - 1 - tap
        term = shifted[back : back + STEP, :] * weight_ref[tap : tap + 1, :]
        if back:
            term = jnp.where(positions >= shifted_start[back : back + STEP, :], term, 0.0)
        total = term if total is None else total + term
    out_ref[...] = low(total)

    @pl.when(step == 0)
    def _():
        tail_ref[...] = total[STEP - HALO :, :]

    @pl.when(step == steps - 1)
    def _():
        window[0:8, :] = jnp.zeros((8, lanes), single)
        window[8:16, :] = shifted[0:8, :]
        early = lax.broadcasted_iota(jnp.int32, (8, 1), 0) - 8
        collected = jnp.zeros((8, lanes), single)
        for tap in range(taps - 1):
            back = taps - 1 - tap
            reader = early + back
            reader_start = jnp.zeros((8, 1), jnp.int32)
            for t in range(back):
                reader_start = jnp.where(reader == t, shifted_start[t : t + 1, :], reader_start)
            term = window[back : back + 8, :] * weight_ref[tap : tap + 1, :]
            collected = collected + jnp.where(
                (reader >= 0) & (early >= reader_start), term, 0.0
            )
        edge_ref[0:8, :] = jnp.zeros((8, lanes), single)
        edge_ref[8:16, :] = collected


def block_place(step, place, per_quarter):
    return ((step // per_quarter) ^ place[0]) * per_quarter + step % per_quarter


def run_forward(place, rows, columns, weights, scalars, heads, key_width, value_width, quarter):
    count, lanes = columns.shape[0], rows.shape[1]
    steps, per_quarter = count // STEP, quarter // STEP
    wide = value_width + key_width
    chunks = STEP // CHUNK
    at = lambda i, place: (block_place(i, place, per_quarter), 0)
    fixed = lambda i, place: (0, 0)
    body = functools.partial(
        forward_kernel, heads=heads, key_width=key_width, value_width=value_width
    )
    shapes = (
        jax.ShapeDtypeStruct((count, heads * value_width), single),
        jax.ShapeDtypeStruct((count, heads * key_width), bfloat),
        jax.ShapeDtypeStruct((count, heads * wide), bfloat),
        jax.ShapeDtypeStruct((count // CHUNK, heads, key_width, wide), bfloat),
        jax.ShapeDtypeStruct((count, heads * CHUNK), bfloat),
        jax.ShapeDtypeStruct((heads, key_width, wide), single),
    )
    return pl.pallas_call(
        body,
        out_shape=shapes,
        grid_spec=pltpu.PrefetchScalarGridSpec(
            num_scalar_prefetch=1,
            grid=(steps,),
            in_specs=[
                pl.BlockSpec((STEP, lanes), at),
                pl.BlockSpec((HALO, lanes), lambda i, place: (count // HALO, 0)),
                pl.BlockSpec((STEP, columns.shape[1]), at),
                pl.BlockSpec(weights.shape, fixed),
                pl.BlockSpec(memory_space=pltpu.SMEM),
            ],
            out_specs=[
                pl.BlockSpec((STEP, heads * value_width), at),
                pl.BlockSpec((STEP, heads * key_width), at),
                pl.BlockSpec((STEP, heads * wide), at),
                pl.BlockSpec((chunks, heads, key_width, wide), lambda i, place: (i, 0, 0, 0)),
                pl.BlockSpec((STEP, heads * CHUNK), at),
                pl.BlockSpec((heads, key_width, wide), lambda i, place: (0, 0, 0)),
            ],
            scratch_shapes=[
                pltpu.VMEM((STEP + HALO, lanes), single),
                pltpu.VMEM((heads, key_width, wide), single),
            ],
        ),
        compiler_params=pltpu.CompilerParams(
            dimension_semantics=("arbitrary",), vmem_limit_bytes=VMEM_LIMIT
        ),
        cost_estimate=pl.CostEstimate(
            flops=count * 2_000_000, bytes_accessed=count * 10_000, transcendentals=count * 2000
        ),
        name="delta_forward",
    )(place, rows, rows, columns, weights, scalars)


def run_backward(
    place, rows, columns, weights, scalars, grad, saved, entering, later, heads, key_width,
    value_width, quarter,
):
    written, states, inverses, end = saved
    count, lanes = columns.shape[0], rows.shape[1]
    steps, per_quarter = count // STEP, quarter // STEP
    wide = value_width + key_width
    chunks = STEP // CHUNK

    def at(i, place):
        return (block_place(steps - 1 - i, place, per_quarter), 0)

    def halo_at(i, place):
        here = steps - 1 - i
        inner = block_place(jnp.maximum(here - 1, 0), place, per_quarter)
        ratio = STEP // HALO
        return (jnp.where(here > 0, inner * ratio + ratio - 1, count // HALO), 0)

    fixed = lambda i, place: (0, 0)
    whole = lambda i, place: (0, 0, 0)
    body = functools.partial(
        backward_kernel, heads=heads, key_width=key_width, value_width=value_width
    )
    shapes = (
        jax.ShapeDtypeStruct((count, lanes), bfloat),
        jax.ShapeDtypeStruct((count, columns.shape[1]), single),
        jax.ShapeDtypeStruct((HALO, lanes), single),
        jax.ShapeDtypeStruct((HALO, lanes), single),
    )
    return pl.pallas_call(
        body,
        out_shape=shapes,
        grid_spec=pltpu.PrefetchScalarGridSpec(
            num_scalar_prefetch=1,
            grid=(steps,),
            in_specs=[
                pl.BlockSpec((STEP, lanes), at),
                pl.BlockSpec((HALO, lanes), halo_at),
                pl.BlockSpec((STEP, columns.shape[1]), at),
                pl.BlockSpec(weights.shape, fixed),
                pl.BlockSpec(memory_space=pltpu.SMEM),
                pl.BlockSpec((STEP, heads * value_width), at),
                pl.BlockSpec((STEP, heads * wide), at),
                pl.BlockSpec(
                    (chunks, heads, key_width, wide), lambda i, place: (steps - 1 - i, 0, 0, 0)
                ),
                pl.BlockSpec((STEP, heads * CHUNK), at),
                pl.BlockSpec(end.shape, whole),
                pl.BlockSpec(entering.shape, whole),
                pl.BlockSpec(later.shape, whole),
            ],
            out_specs=[
                pl.BlockSpec((STEP, lanes), at),
                pl.BlockSpec((STEP, columns.shape[1]), at),
                pl.BlockSpec((HALO, lanes), fixed),
                pl.BlockSpec((HALO, lanes), fixed),
            ],
            scratch_shapes=[
                pltpu.VMEM((STEP + HALO, lanes), single),
                pltpu.VMEM((STEP + 8, lanes), single),
                pltpu.VMEM((STEP + 8, 1), jnp.int32),
                pltpu.VMEM((heads, key_width, value_width), single),
                pltpu.VMEM((heads, key_width, value_width), single),
            ],
        ),
        compiler_params=pltpu.CompilerParams(
            dimension_semantics=("arbitrary",), vmem_limit_bytes=VMEM_LIMIT
        ),
        cost_estimate=pl.CostEstimate(
            flops=count * 3_000_000, bytes_accessed=count * 12_000, transcendentals=count * 3000
        ),
        name="delta_backward",
    )(
        place, rows, rows, columns, weights, scalars, grad, written, states, inverses, end,
        entering, later,
    )


def flip(array, bit):
    groups = lax.axis_size("head")
    return lax.ppermute(array, "head", [(i, i ^ bit) for i in range(groups)])


def gather_rows(array):
    far = flip(array, 2)
    near = flip(array, 1)
    return jnp.concatenate([array, near, far, flip(far, 1)], axis=0)


def scatter_sum(blocks):
    near, corner = flip((low(blocks[1]), low(blocks[3])), 1)
    far = blocks[2] + corner.astype(single)
    return blocks[0] + near.astype(single) + flip(low(far), 2).astype(single)


def scatter_rows(partial):
    size = partial.shape[0] // 4
    return scatter_sum([partial[b * size : (b + 1) * size] for b in range(4)])


def shifted_along(array, axis, by):
    length = lax.axis_size(axis)
    pairs = [(i, i + by) for i in range(length) if 0 <= i + by < length]
    return lax.ppermute(array, axis, pairs)


def reduce_maps(shared, owned):
    members = lax.axis_size("seq")
    place = lax.axis_index("head")
    widths = [part.shape[1] // 4 for part in shared]

    def block(part, relative):
        size = part.shape[1] // 4
        return lax.dynamic_slice_in_dim(part, (place ^ relative) * size, size, 1)

    mine = scatter_sum(
        [jnp.concatenate([block(part, b) for part in shared], axis=1) for b in range(4)]
    )
    flat = jnp.concatenate([low(mine)] + [low(part) for part in owned], axis=1)
    rows, lanes = flat.shape
    parts = lax.all_to_all(flat.reshape(members, rows // members, lanes), "seq", 0, 0)
    summed = low(jnp.sum(parts.astype(single), axis=0))
    spread = jnp.broadcast_to(summed[None], (members,) + summed.shape)
    total = lax.all_to_all(spread, "seq", 0, 0).reshape(rows, lanes)
    shared_lanes = sum(widths)
    piece = total[:, :shared_lanes]
    far = flip(piece, 2)
    pieces = jnp.stack([piece, flip(piece, 1), far, flip(far, 1)])
    ordered = [lax.dynamic_index_in_dim(pieces, place ^ b, 0, False) for b in range(4)]
    full, at = [], 0
    for width in widths:
        full.append(
            jnp.concatenate(
                [ordered[b][:, at : at + width].astype(single) for b in range(4)], axis=1
            )
        )
        at += width
    local, at = [], shared_lanes
    for part in owned:
        local.append(total[:, at : at + part.shape[1]].astype(single))
        at += part.shape[1]
    return full, local


def rms_scale(rows, gain):
    return rows * lax.rsqrt(jnp.mean(rows * rows, axis=-1, keepdims=True) + EPS) * gain


def rms_back(rows, gain, incoming):
    _, back = jax.vjp(lambda value: rms_scale(value, gain), rows)
    return back(incoming)[0]


def silu_slope(value):
    logistic = jax.nn.sigmoid(value)
    return logistic * (1.0 + value * (1.0 - logistic))


def on_device(
    block_input,
    out_grad,
    lengths,
    doc_sets,
    norm1_gain,
    w_query,
    w_key,
    w_value,
    conv_query,
    conv_key,
    conv_value,
    w_decay_beta,
    decay_rate,
    decay_bias,
    w_gate_out,
    out_gain,
    w_out,
    norm2_gain,
    w_gate,
    w_up,
    w_down,
    adapt_down,
    adapt_up_qk,
    adapt_up_vg,
    adapt_up_ff,
    adapt_down_out,
    adapt_down_ffd,
    adapt_up_res,
):
    groups = lax.axis_size("head")
    members = lax.axis_size("seq")
    place = lax.axis_index("head")
    quarter, width = block_input.shape
    count = quarter * groups
    heads = decay_rate.shape[0]
    key_width = w_query.shape[1] // heads
    value_width = w_value.shape[1] // heads
    sets, rank = adapt_down.shape[1], adapt_down.shape[3]
    low_rank = sets * rank
    qk = heads * key_width
    device_start = lax.axis_index("seq") * count
    starts = jnp.sum(
        jnp.where(
            jnp.arange(lengths.shape[0])[None, :] < jnp.arange(lengths.shape[0])[:, None],
            lengths[None, :],
            0,
        ),
        axis=1,
    )
    order = jnp.arange(groups, dtype=jnp.int32) ^ place
    positions = (
        device_start + order[:, None] * quarter + jnp.arange(quarter, dtype=jnp.int32)[None, :]
    ).reshape(-1)
    positions = jnp.concatenate(
        [positions, device_start + jnp.arange(-HALO, 0, dtype=jnp.int32)]
    )
    reached = positions[:, None] >= starts[None, :]
    token_start = jnp.max(jnp.where(reached, starts[None, :], -1), axis=1)
    ended = positions[:, None] >= (starts + lengths)[None, :]
    token_set = jnp.sum(jnp.where(reached & ~ended, doc_sets[None, :], 0), axis=1)
    set_columns = jnp.arange(low_rank, dtype=jnp.int32) // rank
    mask_ext = set_columns[None, :] == token_set[:, None]
    mask = mask_ext[:count]
    relative_start = (token_start[:count] - device_start).astype(single)

    down = adapt_down.transpose(0, 1, 3, 2).reshape(6, low_rank, width)
    up_query = adapt_up_qk[0].reshape(low_rank, -1)
    up_key = adapt_up_qk[1].reshape(low_rank, -1)
    up_value = adapt_up_vg[0].reshape(low_rank, -1)
    up_outgate = adapt_up_vg[1].reshape(low_rank, -1)
    up_ffgate = adapt_up_ff[0].reshape(low_rank, -1)
    up_ffup = adapt_up_ff[1].reshape(low_rank, -1)
    down_out = adapt_down_out.transpose(0, 2, 1).reshape(low_rank, -1)
    down_ffd = adapt_down_ffd.transpose(0, 2, 1).reshape(low_rank, -1)
    up_res = adapt_up_res.reshape(2, low_rank, width)
    conv = jnp.concatenate([conv_query, conv_key, conv_value], axis=1).astype(single)
    scalars = jnp.stack([decay_rate, decay_bias])
    where = place.reshape(1).astype(jnp.int32)
    weight_mix = w_decay_beta.reshape(width, 2 * heads)

    input_float = block_input.astype(single)
    normed = low(rms_scale(input_float, norm1_gain))
    tail = normed[quarter - HALO :]
    halo = sum(
        lax.ppermute(
            tail,
            ("seq", "head"),
            [((s * groups) + groups - 1, (s + 1) * groups + h) for s in range(members - 1)],
        )
        for h in range(groups)
    )
    normed_ext = jnp.concatenate([gather_rows(normed), halo], axis=0)
    normed_all = normed_ext[:count]

    def inner(rows, maps, chosen):
        return low(jnp.where(chosen, nt(rows, maps), 0.0))

    u_query = inner(normed_ext, down[0], mask_ext)
    u_key = inner(normed_ext, down[1], mask_ext)
    u_value = inner(normed_ext, down[2], mask_ext)
    u_outgate = inner(normed_all, down[3], mask)
    pre = jnp.concatenate(
        [
            low(nn(normed_ext, w_query) + nn(u_query, up_query)),
            low(nn(normed_ext, w_key) + nn(u_key, up_key)),
            low(nn(normed_ext, w_value) + nn(u_value, up_value)),
        ],
        axis=1,
    )
    gate_input = nn(normed_all, w_gate_out) + nn(u_outgate, up_outgate)
    mixing = nn(normed_all, weight_mix)
    columns = jnp.concatenate(
        [
            mixing,
            relative_start[:, None],
            jnp.zeros((count, 8 - 2 * heads - 1), single),
        ],
        axis=1,
    )
    raw_local, mapped, *saved = run_forward(
        where, pre, columns, conv, scalars, heads, key_width, value_width, quarter
    )
    end = saved[-1]

    hops = min(members - 1, -(-(DOC_MAX - 1) // count))
    end_low = low(end)
    entering = None
    for hop in range(hops, 0, -1):
        if entering is None:
            entering = shifted_along(end_low[:, :, :value_width], "seq", hop).astype(single)
        else:
            got = shifted_along(end_low, "seq", hop)
            entering = got[:, :, :value_width].astype(single) + jnp.einsum(
                "hij,hjk->hik",
                got[:, :, value_width:],
                low(entering),
                preferred_element_type=single,
            )
    maps_after = [
        shifted_along(end_low[:, :, value_width:], "seq", -hop) for hop in range(1, hops)
    ]
    entering_low = low(entering)

    raw = jnp.concatenate(
        [
            raw_local[:, h * value_width : (h + 1) * value_width]
            + nn(mapped[:, h * key_width : (h + 1) * key_width], entering_low[h])
            for h in range(heads)
        ],
        axis=1,
    )

    def finish(values, gated):
        parts = [
            rms_scale(values[:, h * value_width : (h + 1) * value_width], out_gain)
            for h in range(heads)
        ]
        return jnp.concatenate(parts, axis=1) * jax.nn.silu(gated)

    finished, finish_back = jax.vjp(finish, raw, gate_input)
    mixed = low(finished)
    u_out = inner(mixed, down_out, mask)
    attention = scatter_rows(nn(mixed, w_out) + nn(u_out, up_res[0]))
    residual = input_float + attention
    normed_mid = low(rms_scale(residual, norm2_gain))
    mid_all = gather_rows(normed_mid)
    grad_all = gather_rows(out_grad)

    u_gate = inner(mid_all, down[4], mask)
    u_up = inner(mid_all, down[5], mask)
    gate_value = nn(mid_all, w_gate) + nn(u_gate, up_ffgate)
    up_values = nn(mid_all, w_up) + nn(u_up, up_ffup)
    hidden = low(jax.nn.silu(gate_value) * up_values)
    u_ffd = inner(hidden, down_ffd, mask)
    result = residual + scatter_rows(nn(hidden, w_down) + nn(u_ffd, up_res[1]))

    du_ffd = inner(grad_all, up_res[1], mask)
    hidden_grad = nt(grad_all, w_down) + nn(du_ffd, down_ffd)
    gate_grad = low(hidden_grad * up_values * silu_slope(gate_value))
    up_grad = low(hidden_grad * jax.nn.silu(gate_value))
    du_gate = inner(gate_grad, up_ffgate, mask)
    du_up = inner(up_grad, up_ffup, mask)
    mid_grad = scatter_rows(
        nt(gate_grad, w_gate)
        + nt(up_grad, w_up)
        + nn(du_gate, down[4])
        + nn(du_up, down[5])
    )
    residual_grad = out_grad.astype(single) + rms_back(residual, norm2_gain, mid_grad)
    branch_grad = gather_rows(low(residual_grad))
    du_out = inner(branch_grad, up_res[0], mask)
    mixed_grad = nt(branch_grad, w_out) + nn(du_out, down_out)
    raw_grad, gate_input_grad = finish_back(mixed_grad)
    gate_low = low(gate_input_grad)
    du_outgate = inner(gate_low, up_outgate, mask)

    state_grad = low(
        jnp.stack(
            [
                tn(
                    mapped[:, h * key_width : (h + 1) * key_width],
                    low(raw_grad[:, h * value_width : (h + 1) * value_width]),
                )
                for h in range(heads)
            ]
        )
    )
    later = None
    for hop in range(hops, 0, -1):
        got = shifted_along(state_grad, "seq", -hop).astype(single)
        if later is None:
            later = got
        else:
            later = got + jnp.einsum(
                "hji,hjk->hik", maps_after[hop - 1], low(later), preferred_element_type=single
            )

    first_shared, first_owned = reduce_maps(
        [
            tn(du_outgate, normed_all),
            tn(du_gate, mid_all),
            tn(du_up, mid_all),
            tn(u_out, branch_grad),
            tn(u_ffd, grad_all),
        ],
        [
            tn(u_outgate, gate_low),
            tn(u_gate, gate_grad),
            tn(u_up, up_grad),
            tn(du_out, mixed),
            tn(du_ffd, hidden),
        ],
    )

    pre_grad, mix_grad, tail_grad, edge_grad = run_backward(
        where, pre, columns, conv, scalars, raw_grad, saved, entering_low, low(later), heads,
        key_width, value_width, quarter,
    )
    arrived = shifted_along(edge_grad, "seq", -1)
    tail_at = ((groups - 1) ^ place) * quarter + quarter - HALO
    pre_grad = lax.dynamic_update_slice_in_dim(pre_grad, low(tail_grad + arrived), tail_at, 0)
    query_grad, key_grad, value_grad = (
        pre_grad[:, :qk],
        pre_grad[:, qk : 2 * qk],
        pre_grad[:, 2 * qk :],
    )
    du_query = inner(query_grad, up_query, mask)
    du_key = inner(key_grad, up_key, mask)
    du_value = inner(value_grad, up_value, mask)
    normed_grad = scatter_rows(
        nt(query_grad, w_query)
        + nt(key_grad, w_key)
        + nt(value_grad, w_value)
        + nt(gate_low, w_gate_out)
        + nn(du_query, down[0])
        + nn(du_key, down[1])
        + nn(du_value, down[2])
        + nn(du_outgate, down[3])
        + nt(low(mix_grad[:, : 2 * heads]), weight_mix)
    )
    input_grad = residual_grad + rms_back(input_float, norm1_gain, normed_grad)
    last_shared, last_owned = reduce_maps(
        [tn(du_query, normed_all), tn(du_key, normed_all), tn(du_value, normed_all)],
        [tn(u_query[:count], query_grad), tn(u_key[:count], key_grad), tn(u_value[:count], value_grad)],
    )

    def as_down(rows):
        return rows.reshape(sets, rank, -1).transpose(0, 2, 1)

    def as_up(rows):
        return rows.reshape(sets, rank, -1)

    down_total = jnp.stack([as_down(part) for part in last_shared + first_shared[:3]])
    return (
        low(result),
        input_grad,
        down_total,
        jnp.stack([as_up(last_owned[0]), as_up(last_owned[1])]),
        jnp.stack([as_up(last_owned[2]), as_up(first_owned[0])]),
        jnp.stack([as_up(first_owned[1]), as_up(first_owned[2])]),
        as_down(first_owned[3]),
        as_down(first_owned[4]),
        jnp.stack([as_up(first_shared[3]), as_up(first_shared[4])]),
    )


def solution(mesh):
    rows = P(("seq", "head"), None)
    lanes = P(None, "head")
    last = P(None, None, None, "head")
    middle = P(None, "head", None)
    in_specs = (
        rows, rows, P(), P(), P(), lanes, lanes, lanes, lanes, lanes, lanes,
        P(None, None, "head"), P("head"), P("head"), lanes, P(), P("head", None), P(), lanes,
        lanes, P("head", None), P(), last, last, last, middle, middle, P(),
    )
    out_specs = (rows, rows, P(), last, last, last, middle, middle, P())
    return jax.shard_map(
        on_device, mesh=mesh, in_specs=in_specs, out_specs=out_specs, check_vma=False
    )
```

```python
import functools

import jax
import jax.numpy as jnp
from jax import lax
from jax.experimental import pallas as pl
from jax.experimental.pallas import tpu as pltpu
from jax.sharding import PartitionSpec as P

CHUNK = 128
STEP = 256
HALO = 16
DOC_MAX = 4096
EPS = 1e-06
VMEM_LIMIT = 56 * 1024 * 1024
bfloat = jnp.bfloat16
single = jnp.float32


def contract(left, right, left_dim, right_dim):
    return lax.dot_general(
        left,
        right,
        (((left_dim,), (right_dim,)), ((), ())),
        preferred_element_type=single,
    )


def nn(left, right):
    return contract(left, right, 1, 0)


def nt(left, right):
    return contract(left, right, 1, 1)


def tn(left, right):
    return contract(left, right, 0, 0)


def low(array):
    return array.astype(bfloat)


def iotas():
    rows = lax.broadcasted_iota(jnp.int32, (CHUNK, CHUNK), 0)
    columns = lax.broadcasted_iota(jnp.int32, (CHUNK, CHUNK), 1)
    return rows, columns


def split_two(array):
    high = low(array)
    return high, low(array - high.astype(single))


def near_exact(left, right):
    left_high, left_low = split_two(left)
    right_high, right_low = split_two(right)
    return nn(
        jnp.concatenate([left_high, left_high, left_low], axis=1),
        jnp.concatenate([right_high, right_low, right_high], axis=0),
    )


def ones_product(ones, array):
    high = low(array)
    rest = array - high.astype(single)
    middle = low(rest)
    lowest = low(rest - middle.astype(single))
    return nn(
        jnp.concatenate([ones, ones, ones], axis=1),
        jnp.concatenate([high, middle, lowest], axis=0),
    )


def unit_lower_inverses(stricts, rows, columns):
    eye = (rows == columns).astype(single)
    differ = rows ^ columns
    block = 8
    inner = [jnp.where(differ < block, strict, 0.0) for strict in stricts]
    second = [near_exact(a, a) for a in inner]
    inverse = [near_exact(eye - a, eye + b) for a, b in zip(inner, second)]
    fourth = [near_exact(b, b) for b in second]
    inverse = [near_exact(a, eye + b) for a, b in zip(inverse, fourth)]
    while block < CHUNK:
        between = (differ >= block) & (differ < 2 * block)
        off = [jnp.where(between, strict, 0.0) for strict in stricts]
        part = [near_exact(a, b) for a, b in zip(off, inverse)]
        inverse = [a - near_exact(a, b) for a, b in zip(inverse, part)]
        block = 2 * block
    return inverse


def softplus(value):
    return jnp.maximum(value, 0.0) + jnp.log(1.0 + jnp.exp(-jnp.abs(value)))


def sigmoid(value):
    return 1.0 / (1.0 + jnp.exp(-value))


def gates(decay, start, rows, columns):
    lower_ones = low((rows >= columns).astype(single))
    total = ones_product(lower_ones, jnp.broadcast_to(decay, (CHUNK, CHUNK)))
    linked = (rows >= columns) & (columns >= start)
    within = jnp.where(linked, jnp.exp(jnp.where(linked, total - total.T, 0.0)), 0.0)
    running = total[:, :1]
    carried = jnp.where(start < 0, jnp.exp(running), 0.0)
    last = running[CHUNK - 1 : CHUNK]
    ending = jnp.where(
        rows[:, :1] >= start[CHUNK - 1 : CHUNK], jnp.exp(jnp.minimum(last - running, 0.0)), 0.0
    )
    return within, carried, ending


def convolved(window, starts, weights, base):
    positions = base + lax.broadcasted_iota(jnp.int32, (STEP, 1), 0)
    taps = weights.shape[0]
    total = None
    for tap in range(taps):
        back = taps - 1 - tap
        term = window[HALO - back : HALO - back + STEP, :] * weights[tap : tap + 1, :]
        if back:
            term = jnp.where(positions - back >= starts, term, 0.0)
        total = term if total is None else total + term
    return total


def head_scales(rows, width):
    return lax.rsqrt(jnp.sum(rows * rows, axis=-1, keepdims=True) + EPS)


def forward_kernel(
    place,
    rows_ref,
    halo_ref,
    column_ref,
    weight_ref,
    scalar_ref,
    out_ref,
    map_ref,
    written_ref,
    state_ref,
    inverse_ref,
    end_ref,
    window,
    state,
    *,
    heads,
    key_width,
    value_width,
):
    step = pl.program_id(0)
    wide = value_width + key_width
    base = step * STEP
    rows, columns = iotas()

    @pl.when(step == 0)
    def _():
        window[0:HALO, :] = halo_ref[...].astype(single)
        for h in range(heads):
            state[h, :, :value_width] = jnp.zeros((key_width, value_width), single)
            state[h, :, value_width:] = (rows == columns).astype(single)

    @pl.when(step > 0)
    def _():
        window[0:HALO, :] = window[STEP : STEP + HALO, :]

    window[HALO:, :] = rows_ref[...].astype(single)
    info = column_ref[...]
    starts = info[:, 2 * heads : 2 * heads + 1].astype(jnp.int32)
    before = convolved(window, starts, weight_ref[...], base)
    active = before * sigmoid(before)
    qk_lanes = heads * key_width
    chunks = STEP // CHUNK
    local, stricts = [], []
    for c in range(chunks):
        span = slice(c * CHUNK, (c + 1) * CHUNK)
        for h in range(heads):
            query = active[span, h * key_width : (h + 1) * key_width]
            key = active[span, qk_lanes + h * key_width : qk_lanes + (h + 1) * key_width]
            value = active[
                span, 2 * qk_lanes + h * value_width : 2 * qk_lanes + (h + 1) * value_width
            ]
            query = query * (head_scales(query, key_width) * key_width ** (-0.5))
            key = key * head_scales(key, key_width)
            beta = sigmoid(info[span, h : h + 1])
            decay = -scalar_ref[0, h] * softplus(
                info[span, heads + h : heads + h + 1] + scalar_ref[1, h]
            )
            within, carried, ending = gates(
                decay, starts[span] - (base + c * CHUNK), rows, columns
            )
            query, key = low(query), low(key)
            strict = jnp.where(rows > columns, within * nt(key, key), 0.0) * beta
            mixed = low(within * nt(query, key))
            stricts.append(strict)
            local.append((query, key, value, beta, carried, ending, mixed))
    inverses = [low(a) for a in unit_lower_inverses(stricts, rows, columns)]
    each = range(heads)
    now = [state[h] for h in each]
    for c in range(chunks):
        span = slice(c * CHUNK, (c + 1) * CHUNK)
        here = [local[c * heads + h] for h in each]
        inverse = [inverses[c * heads + h] for h in each]
        now_low = [low(a) for a in now]
        read = [nn(here[h][1], now_low[h]) for h in each]
        asked = [nn(here[h][0], now_low[h]) for h in each]
        target = []
        for h in each:
            query, key, value, beta, carried, ending, mixed = here[h]
            gap = -(carried * beta) * read[h]
            target.append(
                jnp.concatenate(
                    [beta * value + gap[:, :value_width], gap[:, value_width:]], axis=1
                )
            )
        written = [nn(inverse[h], low(target[h])) for h in each]
        added = [tn(here[h][1], low(here[h][5] * written[h])) for h in each]
        inner = [nn(here[h][6], low(written[h])) for h in each]
        for h in each:
            carried = here[h][4]
            inverse_ref[span, h * CHUNK : (h + 1) * CHUNK] = inverse[h]
            state_ref[c, h] = now_low[h]
            written_ref[span, h * wide : (h + 1) * wide] = low(written[h])
            output = carried * asked[h] + inner[h]
            out_ref[span, h * value_width : (h + 1) * value_width] = output[:, :value_width]
            map_ref[span, h * key_width : (h + 1) * key_width] = low(output[:, value_width:])
        now = [here[h][4][CHUNK - 1 : CHUNK] * now[h] + added[h] for h in each]
    for h in each:
        state[h] = now[h]

    @pl.when(step == pl.num_programs(0) - 1)
    def _():
        end_ref[...] = state[...]


def backward_kernel(
    place,
    rows_ref,
    before_ref,
    halo_ref,
    column_ref,
    weight_ref,
    scalar_ref,
    grad_ref,
    written_ref,
    state_ref,
    inverse_ref,
    end_ref,
    entering_ref,
    later_ref,
    out_ref,
    mix_ref,
    tail_ref,
    edge_ref,
    window,
    shifted,
    shifted_start,
    cotangent,
    ahead,
    *,
    heads,
    key_width,
    value_width,
):
    step = pl.program_id(0)
    steps = pl.num_programs(0)
    wide = value_width + key_width
    base = (steps - 1 - step) * STEP
    rows, columns = iotas()
    qk_lanes = heads * key_width
    lanes = window.shape[1]
    taps = weight_ref.shape[0]

    @pl.when(step == 0)
    def _():
        shifted[STEP : STEP + 8, :] = jnp.zeros((8, lanes), single)
        shifted_start[STEP : STEP + 8, :] = jnp.zeros((8, 1), jnp.int32)
        for h in range(heads):
            cotangent[h] = later_ref[h].astype(single)
            ahead[h] = end_ref[h, :, :value_width] + nn(
                low(end_ref[h, :, value_width:]), low(entering_ref[h])
            )

    @pl.when(step > 0)
    def _():
        shifted[STEP : STEP + 8, :] = shifted[0:8, :]
        shifted_start[STEP : STEP + 8, :] = shifted_start[0:8, :]

    window[0:HALO, :] = jnp.where(
        step == steps - 1, halo_ref[...].astype(single), before_ref[...].astype(single)
    )
    window[HALO:, :] = rows_ref[...].astype(single)
    info = column_ref[...]
    starts = info[:, 2 * heads : 2 * heads + 1].astype(jnp.int32)
    positions = base + lax.broadcasted_iota(jnp.int32, (STEP, 1), 0)
    before = convolved(window, starts, weight_ref[...], base)
    gate = sigmoid(before)
    active = before * gate
    slope = gate * (1.0 + before * (1.0 - gate))
    upper_ones = low((rows <= columns).astype(single))
    last_row = rows[:, :1] == CHUNK - 1
    chunks = STEP // CHUNK
    each = range(heads)
    items = [(c, h) for c in range(chunks) for h in each]
    spans = {item: slice(item[0] * CHUNK, (item[0] + 1) * CHUNK) for item in items}
    entering = [low(entering_ref[h]) for h in each]
    root = key_width ** (-0.5)

    def per(function):
        return {item: function(*item) for item in items}

    def q_lanes(h):
        return slice(h * key_width, (h + 1) * key_width)

    def k_lanes(h):
        return slice(qk_lanes + h * key_width, qk_lanes + (h + 1) * key_width)

    def v_lanes(h):
        return slice(2 * qk_lanes + h * value_width, 2 * qk_lanes + (h + 1) * value_width)

    def kept(c, h, part):
        return written_ref[spans[c, h], h * wide : (h + 1) * wide][:, part]

    values, maps = slice(0, value_width), slice(value_width, wide)
    query_raw = per(lambda c, h: active[spans[c, h], q_lanes(h)])
    key_raw = per(lambda c, h: active[spans[c, h], k_lanes(h)])
    query_scale = per(lambda c, h: head_scales(query_raw[c, h], key_width))
    key_scale = per(lambda c, h: head_scales(key_raw[c, h], key_width))
    query = per(lambda c, h: query_raw[c, h] * (query_scale[c, h] * root))
    key = per(lambda c, h: key_raw[c, h] * key_scale[c, h])
    query_low = per(lambda c, h: low(query[c, h]))
    key_low = per(lambda c, h: low(key[c, h]))
    beta = per(lambda c, h: sigmoid(info[spans[c, h], h : h + 1]))
    raw = per(lambda c, h: info[spans[c, h], heads + h : heads + h + 1] + scalar_ref[1, h])
    gated = per(
        lambda c, h: gates(
            -scalar_ref[0, h] * softplus(raw[c, h]),
            starts[spans[c, h]] - (base + c * CHUNK),
            rows,
            columns,
        )
    )
    within = per(lambda c, h: gated[c, h][0])
    carried = per(lambda c, h: gated[c, h][1])
    ending = per(lambda c, h: gated[c, h][2])
    mixed = per(lambda c, h: low(within[c, h] * nt(query_low[c, h], key_low[c, h])))
    written = per(
        lambda c, h: kept(c, h, values).astype(single) + nn(kept(c, h, maps), entering[h])
    )
    start_state = per(
        lambda c, h: state_ref[c, h][:, values].astype(single)
        + nn(state_ref[c, h][:, maps], entering[h])
    )
    written_low = per(lambda c, h: low(written[c, h]))
    start_low = per(lambda c, h: low(start_state[c, h]))
    grad = per(lambda c, h: grad_ref[spans[c, h], h * value_width : (h + 1) * value_width])
    grad_low = grad
    carried_grad = per(lambda c, h: low(carried[c, h] * grad[c, h].astype(single)))
    from_output = per(lambda c, h: tn(mixed[c, h], grad_low[c, h]))
    state_part = per(lambda c, h: tn(query_low[c, h], carried_grad[c, h]))
    mixed_grad = per(lambda c, h: low(within[c, h] * nt(grad_low[c, h], written_low[c, h])))
    query_grad = per(
        lambda c, h: nt(carried_grad[c, h], start_low[c, h]) + nn(mixed_grad[c, h], key_low[c, h])
    )
    key_write = per(lambda c, h: tn(mixed_grad[c, h], query_low[c, h]))
    later, later_low, solved, value_grad, read_grad = {}, {}, {}, {}, {}
    now = [cotangent[h] for h in each]
    for c in reversed(range(chunks)):
        for h in each:
            later[c, h], later_low[c, h] = now[h], low(now[h])
        from_state = [nn(key_low[c, h], later_low[c, h]) for h in each]
        written_grad = [low(from_output[c, h] + ending[c, h] * from_state[h]) for h in each]
        for h in each:
            inverse = inverse_ref[spans[c, h], h * CHUNK : (h + 1) * CHUNK]
            solved[c, h] = tn(inverse, written_grad[h])
        for h in each:
            value_grad[c, h] = beta[c, h] * solved[c, h]
            read_grad[c, h] = low(-carried[c, h] * value_grad[c, h])
        now = [
            carried[c, h][CHUNK - 1 : CHUNK] * now[h]
            + state_part[c, h]
            + tn(key_low[c, h], read_grad[c, h])
            for h in each
        ]
    following = {
        (c, h): start_state[c + 1, h] if c + 1 < chunks else ahead[h] for c, h in items
    }
    at_end = per(lambda c, h: jnp.sum(later[c, h] * following[c, h], keepdims=True))
    for h in each:
        cotangent[h] = now[h]
        ahead[h] = start_state[0, h]
    strict_grad = per(
        lambda c, h: low(
            jnp.where(
                rows > columns, -within[c, h] * nt(low(value_grad[c, h]), written_low[c, h]), 0.0
            )
        )
    )
    key_read = per(
        lambda c, h: nt(read_grad[c, h], start_low[c, h]) + nn(strict_grad[c, h], key_low[c, h])
    )
    key_write = per(
        lambda c, h: key_write[c, h]
        + tn(strict_grad[c, h], key_low[c, h])
        + nt(low(ending[c, h] * written[c, h]), later_low[c, h])
    )
    query_dot = per(
        lambda c, h: jnp.sum(query[c, h] * query_grad[c, h], axis=-1, keepdims=True)
    )
    running_grad = per(
        lambda c, h: query_dot[c, h]
        + jnp.sum(key[c, h] * (key_read[c, h] - key_write[c, h]), axis=-1, keepdims=True)
        + jnp.where(last_row, at_end[c, h], 0.0)
    )
    decay_sum = per(
        lambda c, h: ones_product(
            upper_ones, jnp.broadcast_to(running_grad[c, h], (CHUNK, CHUNK))
        )[:, :1]
    )
    decay_grad = per(
        lambda c, h: jnp.where(
            positions[spans[c, h]] == starts[spans[c, h]],
            0.0,
            -scalar_ref[0, h] * sigmoid(raw[c, h]) * decay_sum[c, h],
        )
    )
    beta_grad = per(
        lambda c, h: jnp.sum(solved[c, h] * written[c, h], axis=-1, keepdims=True)
        * sigmoid(-info[spans[c, h], h : h + 1])
    )
    for c, h in items:
        span = spans[c, h]
        key_grad = key_read[c, h] + key_write[c, h]
        key_dot = jnp.sum(key[c, h] * key_grad, axis=-1, keepdims=True)
        query_active = (query_scale[c, h] * root) * query_grad[c, h] - query_raw[c, h] * (
            query_scale[c, h] * query_scale[c, h] * query_dot[c, h]
        )
        key_active = key_scale[c, h] * (key_grad - key[c, h] * key_dot)
        shifted[span, q_lanes(h)] = query_active * slope[span, q_lanes(h)]
        shifted[span, k_lanes(h)] = key_active * slope[span, k_lanes(h)]
        shifted[span, v_lanes(h)] = value_grad[c, h] * slope[span, v_lanes(h)]
    for c in range(chunks):
        mix_ref[c * CHUNK : (c + 1) * CHUNK, :] = jnp.concatenate(
            [beta_grad[c, h] for h in each]
            + [decay_grad[c, h] for h in each]
            + [jnp.zeros((CHUNK, mix_ref.shape[1] - 2 * heads), single)],
            axis=1,
        )
    shifted_start[0:STEP, :] = starts
    total = None
    for tap in range(taps):
        back = taps - 1 - tap
        term = shifted[back : back + STEP, :] * weight_ref[tap : tap + 1, :]
        if back:
            term = jnp.where(positions >= shifted_start[back : back + STEP, :], term, 0.0)
        total = term if total is None else total + term
    out_ref[...] = low(total)

    @pl.when(step == 0)
    def _():
        tail_ref[...] = total[STEP - HALO :, :]

    @pl.when(step == steps - 1)
    def _():
        window[0:8, :] = jnp.zeros((8, lanes), single)
        window[8:16, :] = shifted[0:8, :]
        early = lax.broadcasted_iota(jnp.int32, (8, 1), 0) - 8
        collected = jnp.zeros((8, lanes), single)
        for tap in range(taps - 1):
            back = taps - 1 - tap
            reader = early + back
            reader_start = jnp.zeros((8, 1), jnp.int32)
            for t in range(back):
                reader_start = jnp.where(reader == t, shifted_start[t : t + 1, :], reader_start)
            term = window[back : back + 8, :] * weight_ref[tap : tap + 1, :]
            collected = collected + jnp.where(
                (reader >= 0) & (early >= reader_start), term, 0.0
            )
        edge_ref[0:8, :] = jnp.zeros((8, lanes), single)
        edge_ref[8:16, :] = collected


def block_place(step, place, per_quarter):
    return ((step // per_quarter) ^ place[0]) * per_quarter + step % per_quarter


def run_forward(place, rows, halo, columns, weights, scalars, heads, key_width, value_width, quarter):
    count, lanes = columns.shape[0], rows.shape[1]
    steps, per_quarter = count // STEP, quarter // STEP
    wide = value_width + key_width
    chunks = STEP // CHUNK
    at = lambda i, place: (block_place(i, place, per_quarter), 0)
    fixed = lambda i, place: (0, 0)
    body = functools.partial(
        forward_kernel, heads=heads, key_width=key_width, value_width=value_width
    )
    shapes = (
        jax.ShapeDtypeStruct((count, heads * value_width), single),
        jax.ShapeDtypeStruct((count, heads * key_width), bfloat),
        jax.ShapeDtypeStruct((count, heads * wide), bfloat),
        jax.ShapeDtypeStruct((count // CHUNK, heads, key_width, wide), bfloat),
        jax.ShapeDtypeStruct((count, heads * CHUNK), bfloat),
        jax.ShapeDtypeStruct((heads, key_width, wide), single),
    )
    return pl.pallas_call(
        body,
        out_shape=shapes,
        grid_spec=pltpu.PrefetchScalarGridSpec(
            num_scalar_prefetch=1,
            grid=(steps,),
            in_specs=[
                pl.BlockSpec((STEP, lanes), at),
                pl.BlockSpec((HALO, lanes), lambda i, place: (0, 0)),
                pl.BlockSpec((STEP, columns.shape[1]), at),
                pl.BlockSpec(weights.shape, fixed),
                pl.BlockSpec(memory_space=pltpu.SMEM),
            ],
            out_specs=[
                pl.BlockSpec((STEP, heads * value_width), at),
                pl.BlockSpec((STEP, heads * key_width), at),
                pl.BlockSpec((STEP, heads * wide), at),
                pl.BlockSpec((chunks, heads, key_width, wide), lambda i, place: (i, 0, 0, 0)),
                pl.BlockSpec((STEP, heads * CHUNK), at),
                pl.BlockSpec((heads, key_width, wide), lambda i, place: (0, 0, 0)),
            ],
            scratch_shapes=[
                pltpu.VMEM((STEP + HALO, lanes), single),
                pltpu.VMEM((heads, key_width, wide), single),
            ],
        ),
        compiler_params=pltpu.CompilerParams(
            dimension_semantics=("arbitrary",), vmem_limit_bytes=VMEM_LIMIT
        ),
        cost_estimate=pl.CostEstimate(
            flops=count * 2_000_000, bytes_accessed=count * 10_000, transcendentals=count * 2000
        ),
        name="delta_forward",
    )(place, rows, halo, columns, weights, scalars)


def run_backward(
    place, rows, halo, columns, weights, scalars, grad, saved, entering, later, heads, key_width,
    value_width, quarter,
):
    written, states, inverses, end = saved
    count, lanes = columns.shape[0], rows.shape[1]
    steps, per_quarter = count // STEP, quarter // STEP
    wide = value_width + key_width
    chunks = STEP // CHUNK

    def at(i, place):
        return (block_place(steps - 1 - i, place, per_quarter), 0)

    def halo_at(i, place):
        here = steps - 1 - i
        inner = block_place(jnp.maximum(here - 1, 0), place, per_quarter)
        ratio = STEP // HALO
        return (inner * ratio + ratio - 1, 0)

    fixed = lambda i, place: (0, 0)
    whole = lambda i, place: (0, 0, 0)
    body = functools.partial(
        backward_kernel, heads=heads, key_width=key_width, value_width=value_width
    )
    shapes = (
        jax.ShapeDtypeStruct((count, lanes), bfloat),
        jax.ShapeDtypeStruct((count, columns.shape[1]), single),
        jax.ShapeDtypeStruct((HALO, lanes), single),
        jax.ShapeDtypeStruct((HALO, lanes), single),
    )
    return pl.pallas_call(
        body,
        out_shape=shapes,
        grid_spec=pltpu.PrefetchScalarGridSpec(
            num_scalar_prefetch=1,
            grid=(steps,),
            in_specs=[
                pl.BlockSpec((STEP, lanes), at),
                pl.BlockSpec((HALO, lanes), halo_at),
                pl.BlockSpec((HALO, lanes), fixed),
                pl.BlockSpec((STEP, columns.shape[1]), at),
                pl.BlockSpec(weights.shape, fixed),
                pl.BlockSpec(memory_space=pltpu.SMEM),
                pl.BlockSpec((STEP, heads * value_width), at),
                pl.BlockSpec((STEP, heads * wide), at),
                pl.BlockSpec(
                    (chunks, heads, key_width, wide), lambda i, place: (steps - 1 - i, 0, 0, 0)
                ),
                pl.BlockSpec((STEP, heads * CHUNK), at),
                pl.BlockSpec(end.shape, whole),
                pl.BlockSpec(entering.shape, whole),
                pl.BlockSpec(later.shape, whole),
            ],
            out_specs=[
                pl.BlockSpec((STEP, lanes), at),
                pl.BlockSpec((STEP, columns.shape[1]), at),
                pl.BlockSpec((HALO, lanes), fixed),
                pl.BlockSpec((HALO, lanes), fixed),
            ],
            scratch_shapes=[
                pltpu.VMEM((STEP + HALO, lanes), single),
                pltpu.VMEM((STEP + 8, lanes), single),
                pltpu.VMEM((STEP + 8, 1), jnp.int32),
                pltpu.VMEM((heads, key_width, value_width), single),
                pltpu.VMEM((heads, key_width, value_width), single),
            ],
        ),
        compiler_params=pltpu.CompilerParams(
            dimension_semantics=("arbitrary",), vmem_limit_bytes=VMEM_LIMIT
        ),
        cost_estimate=pl.CostEstimate(
            flops=count * 3_000_000, bytes_accessed=count * 12_000, transcendentals=count * 3000
        ),
        name="delta_backward",
    )(
        place, rows, rows, halo, columns, weights, scalars, grad, written, states, inverses, end,
        entering, later,
    )


def chosen_columns(table, column_sets):
    return column_sets[0:1, :] == table[:, 1:2]


def masked(product, chosen):
    return low(jnp.where(chosen, product, 0.0))


def silu_parts(value):
    logistic = sigmoid(value)
    return logistic, value * logistic


def accumulate(ref, value, first):
    @pl.when(first)
    def _():
        ref[...] = value

    @pl.when(jnp.logical_not(first))
    def _():
        ref[...] += value


def project_kernel(
    rows_ref, table_ref, halo_ref, halo_table_ref, sets_ref, down_ref, wq_ref, wk_ref, wv_ref,
    wg_ref, wm_ref, up_qk_ref, up_vg_ref,
    pre_ref, gate_ref, inner_ref, column_ref, pre_halo_ref,
):
    low_rank = sets_ref.shape[1]
    q_width, v_width = wq_ref.shape[1], wv_ref.shape[1]

    def projections(rows, chosen, store):
        inner = masked(
            nt(rows, down_ref[: 3 * low_rank, :]), jnp.concatenate([chosen] * 3, axis=1)
        )
        store[:, :q_width] = low(
            nn(rows, wq_ref[...]) + nn(inner[:, :low_rank], up_qk_ref[0])
        )
        store[:, q_width : 2 * q_width] = low(
            nn(rows, wk_ref[...]) + nn(inner[:, low_rank : 2 * low_rank], up_qk_ref[1])
        )
        store[:, 2 * q_width :] = low(
            nn(rows, wv_ref[...]) + nn(inner[:, 2 * low_rank :], up_vg_ref[0])
        )
        return inner

    @pl.when(pl.program_id(0) == 0)
    def _():
        projections(
            halo_ref[...], chosen_columns(halo_table_ref[...], sets_ref[...]), pre_halo_ref
        )

    rows = rows_ref[...]
    table = table_ref[...]
    chosen = chosen_columns(table, sets_ref[...])
    inner_ref[:, : 3 * low_rank] = projections(rows, chosen, pre_ref)
    last = masked(nt(rows, down_ref[3 * low_rank :, :]), chosen)
    inner_ref[:, 3 * low_rank :] = last
    gate_ref[...] = nn(rows, wg_ref[...]) + nn(last, up_vg_ref[1])
    mixing = nt(rows, wm_ref[...])
    spare = column_ref.shape[1] - mixing.shape[1]
    column_ref[...] = jnp.concatenate([mixing, table[:, :spare]], axis=1)


def head_outputs(raw_ref, map_ref, entering_ref, heads, key_width, value_width):
    outputs = []
    for h in range(heads):
        outputs.append(
            raw_ref[:, h * value_width : (h + 1) * value_width]
            + nn(map_ref[:, h * key_width : (h + 1) * key_width], entering_ref[h])
        )
    return outputs


def attend_kernel(
    raw_ref, map_ref, gate_ref, table_ref, entering_ref, gain_ref, sets_ref, wo_ref, down_ref,
    up_ref,
    part_ref, z_ref, inner_ref,
    *, heads, key_width, value_width,
):
    chosen = chosen_columns(table_ref[...], sets_ref[...])
    outputs = head_outputs(raw_ref, map_ref, entering_ref, heads, key_width, value_width)
    for h, output in enumerate(outputs):
        lanes = slice(h * value_width, (h + 1) * value_width)
        scale = lax.rsqrt(jnp.mean(output * output, axis=-1, keepdims=True) + EPS)
        _, gate = silu_parts(gate_ref[:, lanes])
        z_ref[:, lanes] = low(output * scale * gain_ref[0:1, :] * gate)
    z = z_ref[...]
    inner = masked(nt(z, down_ref[...]), chosen)
    inner_ref[...] = inner
    part_ref[...] = low(nn(z, wo_ref[...]) + nn(inner, up_ref[...]))


def feed_kernel(
    rows_ref, grad_ref, table_ref, sets_ref, down_ref, wg_ref, wu_ref, wd_ref, up_ff_ref,
    down_ffd_ref, up_ref,
    out_ref, back_ref, down_grad_ref, res_grad_ref, up_grad_ref, ffd_grad_ref,
):
    first = pl.program_id(0) == 0
    low_rank = sets_ref.shape[1]
    chosen = chosen_columns(table_ref[...], sets_ref[...])
    rows, grad = rows_ref[...], grad_ref[...]
    u_gate = masked(nt(rows, down_ref[:low_rank, :]), chosen)
    u_up = masked(nt(rows, down_ref[low_rank:, :]), chosen)
    gate = nt(rows, wg_ref[...]) + nn(u_gate, up_ff_ref[0])
    up = nt(rows, wu_ref[...]) + nn(u_up, up_ff_ref[1])
    logistic, active = silu_parts(gate)
    hidden = low(active * up)
    u_down = masked(nt(hidden, down_ffd_ref[...]), chosen)
    out_ref[...] = low(nn(hidden, wd_ref[...]) + nn(u_down, up_ref[...]))
    du_down = masked(nt(grad, up_ref[...]), chosen)
    hidden_grad = nt(grad, wd_ref[...]) + nn(du_down, down_ffd_ref[...])
    gate_grad = low(hidden_grad * up * logistic * (1.0 + gate * (1.0 - logistic)))
    up_grad = low(hidden_grad * active)
    du_gate = masked(nt(gate_grad, up_ff_ref[0]), chosen)
    du_up = masked(nt(up_grad, up_ff_ref[1]), chosen)
    back_ref[...] = low(
        nn(gate_grad, wg_ref[...])
        + nn(up_grad, wu_ref[...])
        + nn(du_gate, down_ref[:low_rank, :])
        + nn(du_up, down_ref[low_rank:, :])
    )
    accumulate(down_grad_ref.at[0], tn(du_gate, rows), first)
    accumulate(down_grad_ref.at[1], tn(du_up, rows), first)
    accumulate(res_grad_ref, tn(u_down, grad), first)
    accumulate(up_grad_ref.at[0], tn(u_gate, gate_grad), first)
    accumulate(up_grad_ref.at[1], tn(u_up, up_grad), first)
    accumulate(ffd_grad_ref, tn(du_down, hidden), first)


def branch_kernel(
    branch_ref, raw_ref, map_ref, gate_ref, z_ref, u_out_ref, rows_ref, inner_ref, table_ref,
    entering_ref, gain_ref, sets_ref, wo_ref, down_out_ref, up_ref, up_vg_ref,
    raw_grad_ref, gate_grad_ref, du_ref, state_grad_ref, res_grad_ref, out_grad_ref,
    up_grad_ref, down_grad_ref,
    *, heads, key_width, value_width,
):
    first = pl.program_id(0) == 0
    low_rank = sets_ref.shape[1]
    chosen = chosen_columns(table_ref[...], sets_ref[...])
    branch = branch_ref[...]
    outputs = head_outputs(raw_ref, map_ref, entering_ref, heads, key_width, value_width)
    du_out = masked(nt(branch, up_ref[...]), chosen)
    mixed_grad = nt(branch, wo_ref[...]) + nn(du_out, down_out_ref[...])
    gain = gain_ref[0:1, :]
    for h, output in enumerate(outputs):
        lanes = slice(h * value_width, (h + 1) * value_width)
        scale = lax.rsqrt(jnp.mean(output * output, axis=-1, keepdims=True) + EPS)
        value = gate_ref[:, lanes]
        logistic, active = silu_parts(value)
        incoming = mixed_grad[:, lanes]
        gate_grad_ref[:, lanes] = low(
            incoming
            * (output * scale * gain)
            * (logistic * (1.0 + value * (1.0 - logistic)))
        )
        scaled = gain * (incoming * active)
        dot = jnp.mean(output * scaled, axis=-1, keepdims=True)
        raw_grad = low(scale * scaled - output * (scale * scale * scale * dot))
        raw_grad_ref[:, lanes] = raw_grad
        accumulate(
            state_grad_ref.at[h],
            tn(map_ref[:, h * key_width : (h + 1) * key_width], raw_grad),
            first,
        )
    gate_grad = gate_grad_ref[...]
    du_gate = masked(nt(gate_grad, up_vg_ref[1]), chosen)
    du_ref[...] = du_gate
    accumulate(res_grad_ref, tn(u_out_ref[...], branch), first)
    accumulate(out_grad_ref, tn(du_out, z_ref[...]), first)
    accumulate(up_grad_ref, tn(inner_ref[...], gate_grad), first)
    accumulate(down_grad_ref, tn(du_gate, rows_ref[...]), first)


def settle_kernel(
    pre_ref, gate_grad_ref, du_gate_ref, mix_ref, rows_ref, inner_ref, table_ref, sets_ref,
    down_ref, wq_ref, wk_ref, wv_ref, wg_ref, wm_ref, up_qk_ref, up_vg_ref,
    part_ref, down_grad_ref, up_qk_grad_ref, up_v_grad_ref,
):
    first = pl.program_id(0) == 0
    low_rank = sets_ref.shape[1]
    q_width = wq_ref.shape[1]
    chosen = chosen_columns(table_ref[...], sets_ref[...])
    query, key = pre_ref[:, :q_width], pre_ref[:, q_width : 2 * q_width]
    value = pre_ref[:, 2 * q_width :]
    rows = rows_ref[...]
    du = jnp.concatenate(
        [
            masked(nt(query, up_qk_ref[0]), chosen),
            masked(nt(key, up_qk_ref[1]), chosen),
            masked(nt(value, up_vg_ref[0]), chosen),
            du_gate_ref[...],
        ],
        axis=1,
    )
    part_ref[...] = low(
        nt(query, wq_ref[...])
        + nt(key, wk_ref[...])
        + nt(value, wv_ref[...])
        + nt(gate_grad_ref[...], wg_ref[...])
        + nn(du, down_ref[...])
        + nn(low(mix_ref[...]), wm_ref[...])
    )
    accumulate(down_grad_ref, tn(du[:, : 3 * low_rank], rows), first)
    accumulate(up_qk_grad_ref.at[0], tn(inner_ref[:, :low_rank], query), first)
    accumulate(up_qk_grad_ref.at[1], tn(inner_ref[:, low_rank : 2 * low_rank], key), first)
    accumulate(up_v_grad_ref, tn(inner_ref[:, 2 * low_rank : 3 * low_rank], value), first)


def by_rows(width, lane_block=0):
    return ("rows", width, lane_block)


def blocked_call(body, name, count, inputs, outputs, flops):
    block = min(STEP, count)
    in_specs, arrays, moved = [], [], 0
    for array, kind in inputs:
        arrays.append(array)
        moved += array.size * array.dtype.itemsize
        if kind is None:
            zeros = (0,) * array.ndim
            in_specs.append(
                pl.BlockSpec(
                    array.shape, lambda i, zeros=zeros: zeros, pipeline_mode=pl.Buffered(1)
                )
            )
        else:
            in_specs.append(
                pl.BlockSpec((block, kind[1]), lambda i, lane=kind[2]: (i, lane))
            )
    out_specs, shapes = [], []
    for shape, dtype, rowwise in outputs:
        shapes.append(jax.ShapeDtypeStruct(shape, dtype))
        if rowwise:
            out_specs.append(pl.BlockSpec((block, shape[1]), lambda i: (i, 0)))
        else:
            zeros = (0,) * len(shape)
            out_specs.append(pl.BlockSpec(shape, lambda i, zeros=zeros: zeros))
    return pl.pallas_call(
        body,
        out_shape=tuple(shapes),
        grid=(count // block,),
        in_specs=in_specs,
        out_specs=out_specs,
        compiler_params=pltpu.CompilerParams(
            dimension_semantics=("arbitrary",), vmem_limit_bytes=VMEM_LIMIT
        ),
        cost_estimate=pl.CostEstimate(flops=flops, bytes_accessed=moved, transcendentals=0),
        name=name,
    )(*arrays)


def flip(array, bit):
    groups = lax.axis_size("head")
    return lax.ppermute(array, "head", [(i, i ^ bit) for i in range(groups)])


def gather_rows(array):
    far = flip(array, 2)
    near = flip(array, 1)
    return jnp.concatenate([array, near, far, flip(far, 1)], axis=0)


def scatter_sum(blocks):
    near, corner = flip(low(blocks[1]), 1), flip(low(blocks[3]), 1)
    far = blocks[2].astype(single) + corner.astype(single)
    return blocks[0].astype(single) + near.astype(single) + flip(low(far), 2).astype(single)


def scatter_rows(partial):
    size = partial.shape[0] // 4
    return scatter_sum([partial[b * size : (b + 1) * size] for b in range(4)])


def shifted_along(array, axis, by):
    length = lax.axis_size(axis)
    pairs = [(i, i + by) for i in range(length) if 0 <= i + by < length]
    return lax.ppermute(array, axis, pairs)


def reduce_maps(shared, owned):
    members = lax.axis_size("seq")
    place = lax.axis_index("head")
    widths = [part.shape[1] // 4 for part in shared]

    def block(part, relative):
        size = part.shape[1] // 4
        return lax.dynamic_slice_in_dim(part, (place ^ relative) * size, size, 1)

    mine = scatter_sum(
        [jnp.concatenate([block(part, b) for part in shared], axis=1) for b in range(4)]
    )
    flat = jnp.concatenate([low(mine)] + [low(part) for part in owned], axis=1)
    rows, lanes = flat.shape
    parts = lax.all_to_all(flat.reshape(members, rows // members, lanes), "seq", 0, 0)
    summed = low(jnp.sum(parts.astype(single), axis=0))
    spread = jnp.broadcast_to(summed[None], (members,) + summed.shape)
    total = lax.all_to_all(spread, "seq", 0, 0).reshape(rows, lanes)
    shared_lanes = sum(widths)
    piece = total[:, :shared_lanes]
    far = flip(piece, 2)
    pieces = jnp.stack([piece, flip(piece, 1), far, flip(far, 1)])
    ordered = [lax.dynamic_index_in_dim(pieces, place ^ b, 0, False) for b in range(4)]
    full, at = [], 0
    for width in widths:
        full.append(
            jnp.concatenate(
                [ordered[b][:, at : at + width].astype(single) for b in range(4)], axis=1
            )
        )
        at += width
    local, at = [], shared_lanes
    for part in owned:
        local.append(total[:, at : at + part.shape[1]].astype(single))
        at += part.shape[1]
    return full, local


def rms_scale(rows, gain):
    return rows * lax.rsqrt(jnp.mean(rows * rows, axis=-1, keepdims=True) + EPS) * gain


def rms_back(rows, gain, incoming):
    _, back = jax.vjp(lambda value: rms_scale(value, gain), rows)
    return back(incoming)[0]


def on_device(
    block_input,
    out_grad,
    lengths,
    doc_sets,
    norm1_gain,
    w_query,
    w_key,
    w_value,
    conv_query,
    conv_key,
    conv_value,
    w_decay_beta,
    decay_rate,
    decay_bias,
    w_gate_out,
    out_gain,
    w_out,
    norm2_gain,
    w_gate,
    w_up,
    w_down,
    adapt_down,
    adapt_up_qk,
    adapt_up_vg,
    adapt_up_ff,
    adapt_down_out,
    adapt_down_ffd,
    adapt_up_res,
):
    groups = lax.axis_size("head")
    members = lax.axis_size("seq")
    place = lax.axis_index("head")
    quarter, width = block_input.shape
    count = quarter * groups
    heads = decay_rate.shape[0]
    key_width = w_query.shape[1] // heads
    value_width = w_value.shape[1] // heads
    sets, rank = adapt_down.shape[1], adapt_down.shape[3]
    low_rank = sets * rank
    qk = heads * key_width
    device_start = lax.axis_index("seq") * count
    starts = jnp.sum(
        jnp.where(
            jnp.arange(lengths.shape[0])[None, :] < jnp.arange(lengths.shape[0])[:, None],
            lengths[None, :],
            0,
        ),
        axis=1,
    )
    order = jnp.arange(groups, dtype=jnp.int32) ^ place

    def tables(positions):
        reached = positions[:, None] >= starts[None, :]
        token_start = jnp.max(jnp.where(reached, starts[None, :], -1), axis=1)
        ended = positions[:, None] >= (starts + lengths)[None, :]
        token_set = jnp.sum(jnp.where(reached & ~ended, doc_sets[None, :], 0), axis=1)
        pair = jnp.stack([token_start - device_start, token_set], axis=1).astype(single)
        return jnp.pad(pair, ((0, 0), (0, 8 - pair.shape[1])))

    table = tables(
        (
            device_start + order[:, None] * quarter + jnp.arange(quarter, dtype=jnp.int32)[None, :]
        ).reshape(-1)
    )
    halo_table = tables(device_start + jnp.arange(-HALO, 0, dtype=jnp.int32))
    column_sets = jnp.broadcast_to(
        (jnp.arange(low_rank, dtype=jnp.int32) // rank).astype(single)[None, :], (8, low_rank)
    )

    down = adapt_down.transpose(0, 1, 3, 2).reshape(6 * low_rank, width)
    mixer_down, feed_down = down[: 4 * low_rank], down[4 * low_rank :]
    up_qk = adapt_up_qk.reshape(2, low_rank, -1)
    up_vg = adapt_up_vg.reshape(2, low_rank, -1)
    up_ff = adapt_up_ff.reshape(2, low_rank, -1)
    down_out = adapt_down_out.transpose(0, 2, 1).reshape(low_rank, -1)
    down_ffd = adapt_down_ffd.transpose(0, 2, 1).reshape(low_rank, -1)
    up_res = adapt_up_res.reshape(2, low_rank, width)
    conv = jnp.concatenate([conv_query, conv_key, conv_value], axis=1).astype(single)
    scalars = jnp.stack([decay_rate, decay_bias])
    where = place.reshape(1).astype(jnp.int32)
    weight_mix = w_decay_beta.transpose(1, 2, 0).reshape(2 * heads, width)
    weight_mix_padded = jnp.pad(weight_mix, ((0, 8 - 2 * heads), (0, 0)))
    gain = jnp.broadcast_to(out_gain[None, :], (8, value_width))
    hidden_width = w_down.shape[0]
    value_lanes = heads * value_width

    input_float = block_input.astype(single)
    normed = low(rms_scale(input_float, norm1_gain))
    tail = normed[quarter - HALO :]
    halo = sum(
        lax.ppermute(
            tail,
            ("seq", "head"),
            [((s * groups) + groups - 1, (s + 1) * groups + h) for s in range(members - 1)],
        )
        for h in range(groups)
    )
    normed_all = gather_rows(normed)
    grad_all = gather_rows(out_grad)
    pre, gate_input, inner, columns, pre_halo = blocked_call(
        project_kernel,
        "project",
        count,
        [
            (normed_all, by_rows(width)),
            (table, by_rows(8)),
            (halo, None),
            (halo_table, None),
            (column_sets, None),
            (mixer_down, None),
            (w_query, None),
            (w_key, None),
            (w_value, None),
            (w_gate_out, None),
            (weight_mix, None),
            (up_qk, None),
            (up_vg, None),
        ],
        [
            ((count, 2 * qk + value_lanes), bfloat, True),
            ((count, value_lanes), single, True),
            ((count, 4 * low_rank), bfloat, True),
            ((count, 8), single, True),
            ((HALO, 2 * qk + value_lanes), bfloat, False),
        ],
        count * 5_000_000,
    )
    raw_local, mapped, *saved = run_forward(
        where, pre, pre_halo, columns, conv, scalars, heads, key_width, value_width, quarter
    )
    end = saved[-1]

    hops = min(members - 1, -(-(DOC_MAX - 1) // count))
    end_low = low(end)
    entering = None
    for hop in range(hops, 0, -1):
        if entering is None:
            entering = shifted_along(end_low[:, :, :value_width], "seq", hop).astype(single)
        else:
            got = shifted_along(end_low, "seq", hop)
            entering = got[:, :, :value_width].astype(single) + jnp.einsum(
                "hij,hjk->hik",
                got[:, :, value_width:],
                low(entering),
                preferred_element_type=single,
            )
    maps_after = [
        shifted_along(end_low[:, :, value_width:], "seq", -hop) for hop in range(1, hops)
    ]
    entering_low = low(entering)

    sizes = dict(heads=heads, key_width=key_width, value_width=value_width)
    attention_part, mixed, u_out = blocked_call(
        functools.partial(attend_kernel, **sizes),
        "attend",
        count,
        [
            (raw_local, by_rows(value_lanes)),
            (mapped, by_rows(qk)),
            (gate_input, by_rows(value_lanes)),
            (table, by_rows(8)),
            (entering_low, None),
            (gain, None),
            (column_sets, None),
            (w_out, None),
            (down_out, None),
            (up_res[0], None),
        ],
        [
            ((count, width), bfloat, True),
            ((count, value_lanes), bfloat, True),
            ((count, low_rank), bfloat, True),
        ],
        count * 1_600_000,
    )
    residual = input_float + scatter_rows(attention_part)
    normed_mid = low(rms_scale(residual, norm2_gain))
    mid_all = gather_rows(normed_mid)

    out_part, mid_part, feed_down_grad, feed_res_grad, feed_up_grad, ffd_grad = blocked_call(
        feed_kernel,
        "feed",
        count,
        [
            (mid_all, by_rows(width)),
            (grad_all, by_rows(width)),
            (table, by_rows(8)),
            (column_sets, None),
            (feed_down, None),
            (w_gate.T, None),
            (w_up.T, None),
            (w_down, None),
            (up_ff, None),
            (down_ffd, None),
            (up_res[1], None),
        ],
        [
            ((count, width), bfloat, True),
            ((count, width), bfloat, True),
            ((2, low_rank, width), single, False),
            ((low_rank, width), single, False),
            ((2, low_rank, hidden_width), single, False),
            ((low_rank, hidden_width), single, False),
        ],
        count * 13_000_000,
    )
    mid_grad = scatter_rows(mid_part)
    residual_grad = out_grad.astype(single) + rms_back(residual, norm2_gain, mid_grad)
    branch_grad = gather_rows(low(residual_grad))
    result = residual + scatter_rows(out_part)

    (
        raw_grad,
        gate_grad,
        du_outgate,
        state_grad,
        branch_res_grad,
        out_down_grad,
        outgate_up_grad,
        outgate_down_grad,
    ) = blocked_call(
        functools.partial(branch_kernel, **sizes),
        "branch",
        count,
        [
            (branch_grad, by_rows(width)),
            (raw_local, by_rows(value_lanes)),
            (mapped, by_rows(qk)),
            (gate_input, by_rows(value_lanes)),
            (mixed, by_rows(value_lanes)),
            (u_out, by_rows(low_rank)),
            (normed_all, by_rows(width)),
            (inner, by_rows(low_rank, 3)),
            (table, by_rows(8)),
            (entering_low, None),
            (gain, None),
            (column_sets, None),
            (w_out, None),
            (down_out, None),
            (up_res[0], None),
            (up_vg, None),
        ],
        [
            ((count, value_lanes), bfloat, True),
            ((count, value_lanes), bfloat, True),
            ((count, low_rank), bfloat, True),
            ((heads, key_width, value_width), single, False),
            ((low_rank, width), single, False),
            ((low_rank, value_lanes), single, False),
            ((low_rank, value_lanes), single, False),
            ((low_rank, width), single, False),
        ],
        count * 3_000_000,
    )
    state_low = low(state_grad)
    later = None
    for hop in range(hops, 0, -1):
        got = shifted_along(state_low, "seq", -hop).astype(single)
        if later is None:
            later = got
        else:
            later = got + jnp.einsum(
                "hji,hjk->hik", maps_after[hop - 1], low(later), preferred_element_type=single
            )

    first_shared, first_owned = reduce_maps(
        [outgate_down_grad, feed_down_grad[0], feed_down_grad[1], branch_res_grad, feed_res_grad],
        [outgate_up_grad, feed_up_grad[0], feed_up_grad[1], out_down_grad, ffd_grad],
    )

    pre_grad, mix_grad, tail_grad, edge_grad = run_backward(
        where, pre, pre_halo, columns, conv, scalars, raw_grad, saved, entering_low, low(later),
        heads, key_width, value_width, quarter,
    )
    arrived = shifted_along(edge_grad, "seq", -1)
    tail_at = ((groups - 1) ^ place) * quarter + quarter - HALO
    pre_grad = lax.dynamic_update_slice_in_dim(pre_grad, low(tail_grad + arrived), tail_at, 0)
    normed_part, mixer_down_grad, up_qk_grad, up_v_grad = blocked_call(
        settle_kernel,
        "settle",
        count,
        [
            (pre_grad, by_rows(2 * qk + value_lanes)),
            (gate_grad, by_rows(value_lanes)),
            (du_outgate, by_rows(low_rank)),
            (mix_grad, by_rows(8)),
            (normed_all, by_rows(width)),
            (inner, by_rows(4 * low_rank)),
            (table, by_rows(8)),
            (column_sets, None),
            (mixer_down, None),
            (w_query, None),
            (w_key, None),
            (w_value, None),
            (w_gate_out, None),
            (weight_mix_padded, None),
            (up_qk, None),
            (up_vg, None),
        ],
        [
            ((count, width), bfloat, True),
            ((3 * low_rank, width), single, False),
            ((2, low_rank, qk), single, False),
            ((low_rank, value_lanes), single, False),
        ],
        count * 7_000_000,
    )
    last_shared, last_owned = reduce_maps(
        [mixer_down_grad[p * low_rank : (p + 1) * low_rank] for p in range(3)],
        [up_qk_grad[0], up_qk_grad[1], up_v_grad],
    )
    normed_grad = scatter_rows(normed_part)
    input_grad = residual_grad + rms_back(input_float, norm1_gain, normed_grad)

    def as_down(rows):
        return rows.reshape(sets, rank, -1).transpose(0, 2, 1)

    def as_up(rows):
        return rows.reshape(sets, rank, -1)

    down_total = jnp.stack([as_down(part) for part in last_shared + first_shared[:3]])
    return (
        low(result),
        input_grad,
        down_total,
        jnp.stack([as_up(last_owned[0]), as_up(last_owned[1])]),
        jnp.stack([as_up(last_owned[2]), as_up(first_owned[0])]),
        jnp.stack([as_up(first_owned[1]), as_up(first_owned[2])]),
        as_down(first_owned[3]),
        as_down(first_owned[4]),
        jnp.stack([as_up(first_shared[3]), as_up(first_shared[4])]),
    )


def solution(mesh):
    rows = P(("seq", "head"), None)
    lanes = P(None, "head")
    last = P(None, None, None, "head")
    middle = P(None, "head", None)
    in_specs = (
        rows, rows, P(), P(), P(), lanes, lanes, lanes, lanes, lanes, lanes,
        P(None, None, "head"), P("head"), P("head"), lanes, P(), P("head", None), P(), lanes,
        lanes, P("head", None), P(), last, last, last, middle, middle, P(),
    )
    out_specs = (rows, rows, P(), last, last, last, middle, middle, P())
    return jax.shard_map(
        on_device, mesh=mesh, in_specs=in_specs, out_specs=out_specs, check_vma=False
    )
```

```python
import functools

import jax
import jax.numpy as jnp
from jax import lax
from jax.experimental import pallas as pl
from jax.experimental.pallas import tpu as pltpu
from jax.sharding import PartitionSpec as P

CHUNK = 128
STEP = 256
HALO = 16
DOC_MAX = 4096
EPS = 1e-06
VMEM_LIMIT = 56 * 1024 * 1024
bfloat = jnp.bfloat16
single = jnp.float32


def contract(left, right, left_dim, right_dim):
    return lax.dot_general(
        left,
        right,
        (((left_dim,), (right_dim,)), ((), ())),
        preferred_element_type=single,
    )


def nn(left, right):
    return contract(left, right, 1, 0)


def nt(left, right):
    return contract(left, right, 1, 1)


def tn(left, right):
    return contract(left, right, 0, 0)


def low(array):
    return array.astype(bfloat)


def iotas():
    rows = lax.broadcasted_iota(jnp.int32, (CHUNK, CHUNK), 0)
    columns = lax.broadcasted_iota(jnp.int32, (CHUNK, CHUNK), 1)
    return rows, columns


def split_two(array):
    high = low(array)
    return high, low(array - high.astype(single))


def near_exact(left, right):
    left_high, left_low = split_two(left)
    right_high, right_low = split_two(right)
    return nn(
        jnp.concatenate([left_high, left_high, left_low], axis=1),
        jnp.concatenate([right_high, right_low, right_high], axis=0),
    )


def ones_product(ones, array):
    high = low(array)
    rest = array - high.astype(single)
    middle = low(rest)
    lowest = low(rest - middle.astype(single))
    return nn(
        jnp.concatenate([ones, ones, ones], axis=1),
        jnp.concatenate([high, middle, lowest], axis=0),
    )


def unit_lower_inverses(stricts, rows, columns):
    eye = (rows == columns).astype(single)
    differ = rows ^ columns
    block = 8
    inner = [jnp.where(differ < block, strict, 0.0) for strict in stricts]
    second = [near_exact(a, a) for a in inner]
    inverse = [near_exact(eye - a, eye + b) for a, b in zip(inner, second)]
    fourth = [near_exact(b, b) for b in second]
    inverse = [near_exact(a, eye + b) for a, b in zip(inverse, fourth)]
    while block < CHUNK:
        between = (differ >= block) & (differ < 2 * block)
        off = [jnp.where(between, strict, 0.0) for strict in stricts]
        part = [near_exact(a, b) for a, b in zip(off, inverse)]
        inverse = [a - near_exact(a, b) for a, b in zip(inverse, part)]
        block = 2 * block
    return inverse


def softplus(value):
    return jnp.maximum(value, 0.0) + jnp.log(1.0 + jnp.exp(-jnp.abs(value)))


def sigmoid(value):
    return 1.0 / (1.0 + jnp.exp(-value))


def gates(decay, start, rows, columns):
    lower_ones = low((rows >= columns).astype(single))
    total = ones_product(lower_ones, jnp.broadcast_to(decay, (CHUNK, CHUNK)))
    linked = (rows >= columns) & (columns >= start)
    within = jnp.where(linked, jnp.exp(jnp.where(linked, total - total.T, 0.0)), 0.0)
    running = total[:, :1]
    carried = jnp.where(start < 0, jnp.exp(running), 0.0)
    last = running[CHUNK - 1 : CHUNK]
    ending = jnp.where(
        rows[:, :1] >= start[CHUNK - 1 : CHUNK], jnp.exp(jnp.minimum(last - running, 0.0)), 0.0
    )
    return within, carried, ending


def convolved(window, starts, weights, base):
    positions = base + lax.broadcasted_iota(jnp.int32, (STEP, 1), 0)
    taps = weights.shape[0]
    total = None
    for tap in range(taps):
        back = taps - 1 - tap
        term = window[HALO - back : HALO - back + STEP, :] * weights[tap : tap + 1, :]
        if back:
            term = jnp.where(positions - back >= starts, term, 0.0)
        total = term if total is None else total + term
    return total


def head_scales(rows, width):
    return lax.rsqrt(jnp.sum(rows * rows, axis=-1, keepdims=True) + EPS)


def forward_kernel(
    place,
    rows_ref,
    halo_ref,
    column_ref,
    weight_ref,
    scalar_ref,
    out_ref,
    map_ref,
    written_ref,
    state_ref,
    inverse_ref,
    end_ref,
    sent_ref,
    sent_state_ref,
    sent_map_ref,
    window,
    state,
    *,
    heads,
    key_width,
    value_width,
):
    step = pl.program_id(0)
    wide = value_width + key_width
    base = step * STEP
    rows, columns = iotas()

    @pl.when(step == 0)
    def _():
        window[0:HALO, :] = halo_ref[...].astype(single)
        for h in range(heads):
            state[h, :, :value_width] = jnp.zeros((key_width, value_width), single)
            state[h, :, value_width:] = (rows == columns).astype(single)

    @pl.when(step > 0)
    def _():
        window[0:HALO, :] = window[STEP : STEP + HALO, :]

    window[HALO:, :] = rows_ref[...].astype(single)
    info = column_ref[...]
    starts = info[:, 2 * heads : 2 * heads + 1].astype(jnp.int32)
    before = convolved(window, starts, weight_ref[...], base)
    active = before * sigmoid(before)
    qk_lanes = heads * key_width
    chunks = STEP // CHUNK
    local, stricts = [], []
    for c in range(chunks):
        span = slice(c * CHUNK, (c + 1) * CHUNK)
        for h in range(heads):
            query = active[span, h * key_width : (h + 1) * key_width]
            key = active[span, qk_lanes + h * key_width : qk_lanes + (h + 1) * key_width]
            value = active[
                span, 2 * qk_lanes + h * value_width : 2 * qk_lanes + (h + 1) * value_width
            ]
            query = query * (head_scales(query, key_width) * key_width ** (-0.5))
            key = key * head_scales(key, key_width)
            beta = sigmoid(info[span, h : h + 1])
            decay = -scalar_ref[0, h] * softplus(
                info[span, heads + h : heads + h + 1] + scalar_ref[1, h]
            )
            within, carried, ending = gates(
                decay, starts[span] - (base + c * CHUNK), rows, columns
            )
            query, key = low(query), low(key)
            strict = jnp.where(rows > columns, within * nt(key, key), 0.0) * beta
            mixed = low(within * nt(query, key))
            stricts.append(strict)
            local.append((query, key, value, beta, carried, ending, mixed))
    inverses = [low(a) for a in unit_lower_inverses(stricts, rows, columns)]
    each = range(heads)
    now = [state[h] for h in each]
    for c in range(chunks):
        span = slice(c * CHUNK, (c + 1) * CHUNK)
        here = [local[c * heads + h] for h in each]
        inverse = [inverses[c * heads + h] for h in each]
        now_low = [low(a) for a in now]
        read = [nn(here[h][1], now_low[h]) for h in each]
        asked = [nn(here[h][0], now_low[h]) for h in each]
        target = []
        for h in each:
            query, key, value, beta, carried, ending, mixed = here[h]
            gap = -(carried * beta) * read[h]
            target.append(
                jnp.concatenate(
                    [beta * value + gap[:, :value_width], gap[:, value_width:]], axis=1
                )
            )
        written = [nn(inverse[h], low(target[h])) for h in each]
        added = [tn(here[h][1], low(here[h][5] * written[h])) for h in each]
        inner = [nn(here[h][6], low(written[h])) for h in each]
        for h in each:
            carried = here[h][4]
            inverse_ref[span, h * CHUNK : (h + 1) * CHUNK] = inverse[h]
            state_ref[c, h] = now_low[h]
            written_ref[span, h * wide : (h + 1) * wide] = low(written[h])
            output = carried * asked[h] + inner[h]
            out_ref[span, h * value_width : (h + 1) * value_width] = output[:, :value_width]
            map_ref[span, h * key_width : (h + 1) * key_width] = low(output[:, value_width:])
        now = [here[h][4][CHUNK - 1 : CHUNK] * now[h] + added[h] for h in each]
    for h in each:
        state[h] = now[h]

    @pl.when(step == pl.num_programs(0) - 1)
    def _():
        final = state[...]
        end_ref[...] = final
        sent_ref[...] = low(final)
        sent_state_ref[...] = low(final[:, :, :value_width])
        sent_map_ref[...] = low(final[:, :, value_width:])


def backward_kernel(
    place,
    rows_ref,
    before_ref,
    halo_ref,
    column_ref,
    weight_ref,
    scalar_ref,
    grad_ref,
    written_ref,
    state_ref,
    inverse_ref,
    end_ref,
    entering_ref,
    *rest,
    hops,
    heads,
    key_width,
    value_width,
):
    got_refs, after_refs, rest = rest[:hops], rest[hops : 2 * hops - 1], rest[2 * hops - 1 :]
    out_ref, mix_ref, tail_ref, edge_ref, window, shifted, shifted_start, cotangent, ahead = rest
    step = pl.program_id(0)
    steps = pl.num_programs(0)
    wide = value_width + key_width
    base = (steps - 1 - step) * STEP
    rows, columns = iotas()
    qk_lanes = heads * key_width
    lanes = window.shape[1]
    taps = weight_ref.shape[0]

    @pl.when(step == 0)
    def _():
        shifted[STEP : STEP + 8, :] = jnp.zeros((8, lanes), single)
        shifted_start[STEP : STEP + 8, :] = jnp.zeros((8, 1), jnp.int32)
        for h in range(heads):
            passed = got_refs[hops - 1][h].astype(single)
            for hop in range(hops - 1, 0, -1):
                passed = got_refs[hop - 1][h].astype(single) + tn(
                    after_refs[hop - 1][h], low(passed)
                )
            cotangent[h] = passed
            ahead[h] = end_ref[h, :, :value_width] + nn(
                low(end_ref[h, :, value_width:]), low(entering_ref[h])
            )

    @pl.when(step > 0)
    def _():
        shifted[STEP : STEP + 8, :] = shifted[0:8, :]
        shifted_start[STEP : STEP + 8, :] = shifted_start[0:8, :]

    window[0:HALO, :] = jnp.where(
        step == steps - 1, halo_ref[...].astype(single), before_ref[...].astype(single)
    )
    window[HALO:, :] = rows_ref[...].astype(single)
    info = column_ref[...]
    starts = info[:, 2 * heads : 2 * heads + 1].astype(jnp.int32)
    positions = base + lax.broadcasted_iota(jnp.int32, (STEP, 1), 0)
    before = convolved(window, starts, weight_ref[...], base)
    gate = sigmoid(before)
    active = before * gate
    slope = gate * (1.0 + before * (1.0 - gate))
    upper_ones = low((rows <= columns).astype(single))
    last_row = rows[:, :1] == CHUNK - 1
    chunks = STEP // CHUNK
    each = range(heads)
    items = [(c, h) for c in range(chunks) for h in each]
    spans = {item: slice(item[0] * CHUNK, (item[0] + 1) * CHUNK) for item in items}
    entering = [low(entering_ref[h]) for h in each]
    root = key_width ** (-0.5)

    def per(function):
        return {item: function(*item) for item in items}

    def q_lanes(h):
        return slice(h * key_width, (h + 1) * key_width)

    def k_lanes(h):
        return slice(qk_lanes + h * key_width, qk_lanes + (h + 1) * key_width)

    def v_lanes(h):
        return slice(2 * qk_lanes + h * value_width, 2 * qk_lanes + (h + 1) * value_width)

    def kept(c, h, part):
        return written_ref[spans[c, h], h * wide : (h + 1) * wide][:, part]

    values, maps = slice(0, value_width), slice(value_width, wide)
    query_raw = per(lambda c, h: active[spans[c, h], q_lanes(h)])
    key_raw = per(lambda c, h: active[spans[c, h], k_lanes(h)])
    query_scale = per(lambda c, h: head_scales(query_raw[c, h], key_width))
    key_scale = per(lambda c, h: head_scales(key_raw[c, h], key_width))
    query = per(lambda c, h: query_raw[c, h] * (query_scale[c, h] * root))
    key = per(lambda c, h: key_raw[c, h] * key_scale[c, h])
    query_low = per(lambda c, h: low(query[c, h]))
    key_low = per(lambda c, h: low(key[c, h]))
    beta = per(lambda c, h: sigmoid(info[spans[c, h], h : h + 1]))
    raw = per(lambda c, h: info[spans[c, h], heads + h : heads + h + 1] + scalar_ref[1, h])
    gated = per(
        lambda c, h: gates(
            -scalar_ref[0, h] * softplus(raw[c, h]),
            starts[spans[c, h]] - (base + c * CHUNK),
            rows,
            columns,
        )
    )
    within = per(lambda c, h: gated[c, h][0])
    carried = per(lambda c, h: gated[c, h][1])
    ending = per(lambda c, h: gated[c, h][2])
    mixed = per(lambda c, h: low(within[c, h] * nt(query_low[c, h], key_low[c, h])))
    written = per(
        lambda c, h: kept(c, h, values).astype(single) + nn(kept(c, h, maps), entering[h])
    )
    start_state = per(
        lambda c, h: state_ref[c, h][:, values].astype(single)
        + nn(state_ref[c, h][:, maps], entering[h])
    )
    written_low = per(lambda c, h: low(written[c, h]))
    start_low = per(lambda c, h: low(start_state[c, h]))
    grad = per(lambda c, h: grad_ref[spans[c, h], h * value_width : (h + 1) * value_width])
    grad_low = grad
    carried_grad = per(lambda c, h: low(carried[c, h] * grad[c, h].astype(single)))
    from_output = per(lambda c, h: tn(mixed[c, h], grad_low[c, h]))
    state_part = per(lambda c, h: tn(query_low[c, h], carried_grad[c, h]))
    mixed_grad = per(lambda c, h: low(within[c, h] * nt(grad_low[c, h], written_low[c, h])))
    query_grad = per(
        lambda c, h: nt(carried_grad[c, h], start_low[c, h]) + nn(mixed_grad[c, h], key_low[c, h])
    )
    key_write = per(lambda c, h: tn(mixed_grad[c, h], query_low[c, h]))
    later, later_low, solved, value_grad, read_grad = {}, {}, {}, {}, {}
    now = [cotangent[h] for h in each]
    for c in reversed(range(chunks)):
        for h in each:
            later[c, h], later_low[c, h] = now[h], low(now[h])
        from_state = [nn(key_low[c, h], later_low[c, h]) for h in each]
        written_grad = [low(from_output[c, h] + ending[c, h] * from_state[h]) for h in each]
        for h in each:
            inverse = inverse_ref[spans[c, h], h * CHUNK : (h + 1) * CHUNK]
            solved[c, h] = tn(inverse, written_grad[h])
        for h in each:
            value_grad[c, h] = beta[c, h] * solved[c, h]
            read_grad[c, h] = low(-carried[c, h] * value_grad[c, h])
        now = [
            carried[c, h][CHUNK - 1 : CHUNK] * now[h]
            + state_part[c, h]
            + tn(key_low[c, h], read_grad[c, h])
            for h in each
        ]
    following = {
        (c, h): start_state[c + 1, h] if c + 1 < chunks else ahead[h] for c, h in items
    }
    at_end = per(lambda c, h: jnp.sum(later[c, h] * following[c, h], keepdims=True))
    for h in each:
        cotangent[h] = now[h]
        ahead[h] = start_state[0, h]
    strict_grad = per(
        lambda c, h: low(
            jnp.where(
                rows > columns, -within[c, h] * nt(low(value_grad[c, h]), written_low[c, h]), 0.0
            )
        )
    )
    key_read = per(
        lambda c, h: nt(read_grad[c, h], start_low[c, h]) + nn(strict_grad[c, h], key_low[c, h])
    )
    key_write = per(
        lambda c, h: key_write[c, h]
        + tn(strict_grad[c, h], key_low[c, h])
        + nt(low(ending[c, h] * written[c, h]), later_low[c, h])
    )
    query_dot = per(
        lambda c, h: jnp.sum(query[c, h] * query_grad[c, h], axis=-1, keepdims=True)
    )
    running_grad = per(
        lambda c, h: query_dot[c, h]
        + jnp.sum(key[c, h] * (key_read[c, h] - key_write[c, h]), axis=-1, keepdims=True)
        + jnp.where(last_row, at_end[c, h], 0.0)
    )
    decay_sum = per(
        lambda c, h: ones_product(
            upper_ones, jnp.broadcast_to(running_grad[c, h], (CHUNK, CHUNK))
        )[:, :1]
    )
    decay_grad = per(
        lambda c, h: jnp.where(
            positions[spans[c, h]] == starts[spans[c, h]],
            0.0,
            -scalar_ref[0, h] * sigmoid(raw[c, h]) * decay_sum[c, h],
        )
    )
    beta_grad = per(
        lambda c, h: jnp.sum(solved[c, h] * written[c, h], axis=-1, keepdims=True)
        * sigmoid(-info[spans[c, h], h : h + 1])
    )
    for c, h in items:
        span = spans[c, h]
        key_grad = key_read[c, h] + key_write[c, h]
        key_dot = jnp.sum(key[c, h] * key_grad, axis=-1, keepdims=True)
        query_active = (query_scale[c, h] * root) * query_grad[c, h] - query_raw[c, h] * (
            query_scale[c, h] * query_scale[c, h] * query_dot[c, h]
        )
        key_active = key_scale[c, h] * (key_grad - key[c, h] * key_dot)
        shifted[span, q_lanes(h)] = query_active * slope[span, q_lanes(h)]
        shifted[span, k_lanes(h)] = key_active * slope[span, k_lanes(h)]
        shifted[span, v_lanes(h)] = value_grad[c, h] * slope[span, v_lanes(h)]
    for c in range(chunks):
        mix_ref[c * CHUNK : (c + 1) * CHUNK, :] = jnp.concatenate(
            [beta_grad[c, h] for h in each]
            + [decay_grad[c, h] for h in each]
            + [jnp.zeros((CHUNK, mix_ref.shape[1] - 2 * heads), single)],
            axis=1,
        )
    shifted_start[0:STEP, :] = starts
    total = None
    for tap in range(taps):
        back = taps - 1 - tap
        term = shifted[back : back + STEP, :] * weight_ref[tap : tap + 1, :]
        if back:
            term = jnp.where(positions >= shifted_start[back : back + STEP, :], term, 0.0)
        total = term if total is None else total + term
    out_ref[...] = low(total)

    @pl.when(step == 0)
    def _():
        tail_ref[...] = total[STEP - HALO :, :]

    @pl.when(step == steps - 1)
    def _():
        window[0:8, :] = jnp.zeros((8, lanes), single)
        window[8:16, :] = shifted[0:8, :]
        early = lax.broadcasted_iota(jnp.int32, (8, 1), 0) - 8
        collected = jnp.zeros((8, lanes), single)
        for tap in range(taps - 1):
            back = taps - 1 - tap
            reader = early + back
            reader_start = jnp.zeros((8, 1), jnp.int32)
            for t in range(back):
                reader_start = jnp.where(reader == t, shifted_start[t : t + 1, :], reader_start)
            term = window[back : back + 8, :] * weight_ref[tap : tap + 1, :]
            collected = collected + jnp.where(
                (reader >= 0) & (early >= reader_start), term, 0.0
            )
        edge_ref[0:8, :] = jnp.zeros((8, lanes), single)
        edge_ref[8:16, :] = collected


def block_place(step, place, per_quarter):
    return ((step // per_quarter) ^ place[0]) * per_quarter + step % per_quarter


def run_forward(place, rows, halo, columns, weights, scalars, heads, key_width, value_width, quarter):
    count, lanes = columns.shape[0], rows.shape[1]
    steps, per_quarter = count // STEP, quarter // STEP
    wide = value_width + key_width
    chunks = STEP // CHUNK
    at = lambda i, place: (block_place(i, place, per_quarter), 0)
    fixed = lambda i, place: (0, 0)
    body = functools.partial(
        forward_kernel, heads=heads, key_width=key_width, value_width=value_width
    )
    shapes = (
        jax.ShapeDtypeStruct((count, heads * value_width), single),
        jax.ShapeDtypeStruct((count, heads * key_width), bfloat),
        jax.ShapeDtypeStruct((count, heads * wide), bfloat),
        jax.ShapeDtypeStruct((count // CHUNK, heads, key_width, wide), bfloat),
        jax.ShapeDtypeStruct((count, heads * CHUNK), bfloat),
        jax.ShapeDtypeStruct((heads, key_width, wide), single),
        jax.ShapeDtypeStruct((heads, key_width, wide), bfloat),
        jax.ShapeDtypeStruct((heads, key_width, value_width), bfloat),
        jax.ShapeDtypeStruct((heads, key_width, key_width), bfloat),
    )
    return pl.pallas_call(
        body,
        out_shape=shapes,
        grid_spec=pltpu.PrefetchScalarGridSpec(
            num_scalar_prefetch=1,
            grid=(steps,),
            in_specs=[
                pl.BlockSpec((STEP, lanes), at),
                pl.BlockSpec((HALO, lanes), lambda i, place: (0, 0)),
                pl.BlockSpec((STEP, columns.shape[1]), at),
                pl.BlockSpec(weights.shape, fixed),
                pl.BlockSpec(memory_space=pltpu.SMEM),
            ],
            out_specs=[
                pl.BlockSpec((STEP, heads * value_width), at),
                pl.BlockSpec((STEP, heads * key_width), at),
                pl.BlockSpec((STEP, heads * wide), at),
                pl.BlockSpec((chunks, heads, key_width, wide), lambda i, place: (i, 0, 0, 0)),
                pl.BlockSpec((STEP, heads * CHUNK), at),
                pl.BlockSpec((heads, key_width, wide), lambda i, place: (0, 0, 0)),
                pl.BlockSpec((heads, key_width, wide), lambda i, place: (0, 0, 0)),
                pl.BlockSpec((heads, key_width, value_width), lambda i, place: (0, 0, 0)),
                pl.BlockSpec((heads, key_width, key_width), lambda i, place: (0, 0, 0)),
            ],
            scratch_shapes=[
                pltpu.VMEM((STEP + HALO, lanes), single),
                pltpu.VMEM((heads, key_width, wide), single),
            ],
        ),
        compiler_params=pltpu.CompilerParams(
            dimension_semantics=("arbitrary",), vmem_limit_bytes=VMEM_LIMIT
        ),
        cost_estimate=pl.CostEstimate(
            flops=count * 2_000_000, bytes_accessed=count * 10_000, transcendentals=count * 2000
        ),
        name="delta_forward",
    )(place, rows, halo, columns, weights, scalars)


def run_backward(
    place, rows, halo, columns, weights, scalars, grad, saved, entering, got, after, heads,
    key_width, value_width, quarter,
):
    written, states, inverses, end = saved
    count, lanes = columns.shape[0], rows.shape[1]
    steps, per_quarter = count // STEP, quarter // STEP
    wide = value_width + key_width
    chunks = STEP // CHUNK

    def at(i, place):
        return (block_place(steps - 1 - i, place, per_quarter), 0)

    def halo_at(i, place):
        here = steps - 1 - i
        inner = block_place(jnp.maximum(here - 1, 0), place, per_quarter)
        ratio = STEP // HALO
        return (inner * ratio + ratio - 1, 0)

    fixed = lambda i, place: (0, 0)
    whole = lambda i, place: (0, 0, 0)
    body = functools.partial(
        backward_kernel,
        hops=len(got),
        heads=heads,
        key_width=key_width,
        value_width=value_width,
    )
    shapes = (
        jax.ShapeDtypeStruct((count, lanes), bfloat),
        jax.ShapeDtypeStruct((count, columns.shape[1]), single),
        jax.ShapeDtypeStruct((HALO, lanes), single),
        jax.ShapeDtypeStruct((HALO, lanes), single),
    )
    return pl.pallas_call(
        body,
        out_shape=shapes,
        grid_spec=pltpu.PrefetchScalarGridSpec(
            num_scalar_prefetch=1,
            grid=(steps,),
            in_specs=[
                pl.BlockSpec((STEP, lanes), at),
                pl.BlockSpec((HALO, lanes), halo_at),
                pl.BlockSpec((HALO, lanes), fixed),
                pl.BlockSpec((STEP, columns.shape[1]), at),
                pl.BlockSpec(weights.shape, fixed),
                pl.BlockSpec(memory_space=pltpu.SMEM),
                pl.BlockSpec((STEP, heads * value_width), at),
                pl.BlockSpec((STEP, heads * wide), at),
                pl.BlockSpec(
                    (chunks, heads, key_width, wide), lambda i, place: (steps - 1 - i, 0, 0, 0)
                ),
                pl.BlockSpec((STEP, heads * CHUNK), at),
                pl.BlockSpec(end.shape, whole),
                pl.BlockSpec(entering.shape, whole),
            ]
            + [pl.BlockSpec(part.shape, whole) for part in (*got, *after)],
            out_specs=[
                pl.BlockSpec((STEP, lanes), at),
                pl.BlockSpec((STEP, columns.shape[1]), at),
                pl.BlockSpec((HALO, lanes), fixed),
                pl.BlockSpec((HALO, lanes), fixed),
            ],
            scratch_shapes=[
                pltpu.VMEM((STEP + HALO, lanes), single),
                pltpu.VMEM((STEP + 8, lanes), single),
                pltpu.VMEM((STEP + 8, 1), jnp.int32),
                pltpu.VMEM((heads, key_width, value_width), single),
                pltpu.VMEM((heads, key_width, value_width), single),
            ],
        ),
        compiler_params=pltpu.CompilerParams(
            dimension_semantics=("arbitrary",), vmem_limit_bytes=VMEM_LIMIT
        ),
        cost_estimate=pl.CostEstimate(
            flops=count * 3_000_000, bytes_accessed=count * 12_000, transcendentals=count * 3000
        ),
        name="delta_backward",
    )(
        place, rows, rows, halo, columns, weights, scalars, grad, written, states, inverses, end,
        entering, *got, *after,
    )


def chosen_columns(table, column_sets):
    return column_sets[0:1, :] == table[:, 1:2]


def masked(product, chosen):
    return low(jnp.where(chosen, product, 0.0))


def silu_parts(value):
    logistic = sigmoid(value)
    return logistic, value * logistic


def accumulate(ref, value, first):
    ref[...] = jnp.where(first, value, ref[...] + value)


def at_start(fill):
    pl.when(pl.program_id(0) == 0)(fill)


def project_kernel(
    rows_ref, table_ref, halo_ref, halo_table_ref, sets_ref, down_mix_ref, wq_ref, wk_ref, wv_ref,
    wg_ref, up_qk_ref, up_vg_ref,
    pre_ref, gate_ref, inner_ref, column_ref, pre_halo_ref,
    joined,
):
    low_rank = sets_ref.shape[1]
    width, q_width = wq_ref.shape
    v_width = wv_ref.shape[1]
    bounds = [0, q_width, 2 * q_width, 2 * q_width + v_width, 2 * q_width + 2 * v_width]

    @at_start
    def _():
        weights = (wq_ref, wk_ref, wv_ref, wg_ref)
        ups = (up_qk_ref[0], up_qk_ref[1], up_vg_ref[0], up_vg_ref[1])
        for p in range(4):
            joined[:width, bounds[p] : bounds[p + 1]] = weights[p][...]
            joined[width:, bounds[p] : bounds[p + 1]] = ups[p]

    def projections(rows, table, store, last):
        chosen = chosen_columns(table, sets_ref[...])
        product = nt(rows, down_mix_ref[...])
        inner = [
            masked(product[:, p * low_rank : (p + 1) * low_rank], chosen) for p in range(last)
        ]
        outputs = [
            nn(
                jnp.concatenate([rows, inner[p]], axis=1), joined[:, bounds[p] : bounds[p + 1]]
            )
            for p in range(last)
        ]
        for p in range(3):
            store[:, bounds[p] : bounds[p + 1]] = low(outputs[p])
        return product, inner, outputs

    @at_start
    def _():
        projections(halo_ref[...], halo_table_ref[...], pre_halo_ref, 3)

    table = table_ref[...]
    product, inner, outputs = projections(rows_ref[...], table, pre_ref, 4)
    for p in range(4):
        inner_ref[:, p * low_rank : (p + 1) * low_rank] = inner[p]
    gate_ref[...] = outputs[3]
    column_ref[...] = jnp.concatenate(
        [product[:, 4 * low_rank : 4 * low_rank + 4], table[:, :4]], axis=1
    )


def head_outputs(raw_ref, map_ref, entering_ref, heads, key_width, value_width):
    outputs = []
    for h in range(heads):
        outputs.append(
            raw_ref[:, h * value_width : (h + 1) * value_width]
            + nn(map_ref[:, h * key_width : (h + 1) * key_width], entering_ref[h])
        )
    return outputs


def attend_kernel(
    raw_ref, map_ref, gate_ref, table_ref, gain_ref, sets_ref, wo_ref, down_ref, up_ref, *rest,
    heads, key_width, value_width, hops,
):
    got_refs, rest = rest[:hops], rest[hops:]
    part_ref, z_ref, inner_ref, entering_ref, joined = rest
    value_lanes = wo_ref.shape[0]

    @at_start
    def _():
        joined[:value_lanes, :] = wo_ref[...]
        joined[value_lanes:, :] = up_ref[...]
        for h in range(heads):
            state = got_refs[hops - 1][h].astype(single)
            for hop in range(hops - 1, 0, -1):
                got = got_refs[hop - 1][h]
                state = got[:, :value_width].astype(single) + nn(got[:, value_width:], low(state))
            entering_ref[h] = low(state)

    chosen = chosen_columns(table_ref[...], sets_ref[...])
    outputs = head_outputs(raw_ref, map_ref, entering_ref, heads, key_width, value_width)
    parts = []
    for h, output in enumerate(outputs):
        lanes = slice(h * value_width, (h + 1) * value_width)
        scale = lax.rsqrt(jnp.mean(output * output, axis=-1, keepdims=True) + EPS)
        _, gate = silu_parts(gate_ref[:, lanes])
        parts.append(low(output * scale * gain_ref[0:1, :] * gate))
    z = jnp.concatenate(parts, axis=1)
    z_ref[...] = z
    inner = masked(nt(z, down_ref[...]), chosen)
    inner_ref[...] = inner
    part_ref[...] = low(nn(jnp.concatenate([z, inner], axis=1), joined[...]))


def feed_before_kernel(
    grad_ref, table_ref, sets_ref, wd_ref, down_ffd_t_ref, up_ref, hidden_grad_ref, du_ref, joined
):
    hidden, width = wd_ref.shape

    @at_start
    def _():
        joined[:hidden, :width] = wd_ref[...]
        joined[:hidden, width:] = down_ffd_t_ref[...]
        joined[hidden:, :] = jnp.zeros((joined.shape[0] - hidden, joined.shape[1]), bfloat)

    grad = grad_ref[...]
    du_down = masked(nt(grad, up_ref[...]), chosen_columns(table_ref[...], sets_ref[...]))
    du_ref[...] = du_down
    hidden_grad_ref[...] = nt(jnp.concatenate([grad, du_down], axis=1), joined[...])


def feed_kernel(
    rows_ref, hidden_grad_ref, table_ref, sets_ref, down_ref, wg_ref, wu_ref, up_t_ref, up_ref,
    back_ref, hidden_ref, ff_grad_ref, inner_ref, du_ref,
    joined_gate, joined_up, joined_back,
):
    low_rank = sets_ref.shape[1]
    hidden, width = wg_ref.shape
    padded = joined_gate.shape[0]

    @at_start
    def _():
        for p, (joined, weight) in enumerate(((joined_gate, wg_ref), (joined_up, wu_ref))):
            joined[:hidden, :width] = weight[...]
            joined[:hidden, width:] = up_t_ref[p]
            joined[hidden:, :] = jnp.zeros((padded - hidden, joined.shape[1]), bfloat)
            joined_back[p * padded : p * padded + hidden, :] = weight[...]
            joined_back[p * padded + hidden : (p + 1) * padded, :] = jnp.zeros(
                (padded - hidden, width), bfloat
            )
        joined_back[2 * padded :, :] = down_ref[...]

    chosen = chosen_columns(table_ref[...], sets_ref[...])
    both = jnp.concatenate([chosen, chosen], axis=1)
    rows = rows_ref[...]
    inner = masked(nt(rows, down_ref[...]), both)
    inner_ref[...] = inner
    gate = nt(jnp.concatenate([rows, inner[:, :low_rank]], axis=1), joined_gate[...])
    up = nt(jnp.concatenate([rows, inner[:, low_rank:]], axis=1), joined_up[...])
    logistic, active = silu_parts(gate)
    hidden_ref[...] = low(active * up)
    hidden_grad = hidden_grad_ref[...]
    gate_grad = low(hidden_grad * up * logistic * (1.0 + gate * (1.0 - logistic)))
    up_grad = low(hidden_grad * active)
    du_gate = masked(nt(gate_grad, up_ref[0]), chosen)
    du_up = masked(nt(up_grad, up_ref[1]), chosen)
    du_ref[:, :low_rank] = du_gate
    du_ref[:, low_rank:] = du_up
    ff_grad_ref[:, :padded] = gate_grad
    ff_grad_ref[:, padded:] = up_grad
    back_ref[...] = low(
        nn(jnp.concatenate([gate_grad, up_grad, du_gate, du_up], axis=1), joined_back[...])
    )


def feed_after_kernel(
    rows_ref, grad_ref, hidden_ref, ff_grad_ref, inner_ref, du_ref, du_down_ref, table_ref,
    sets_ref, wd_ref, down_ffd_ref, up_ref,
    out_ref, down_grad_ref, res_grad_ref, up_grad_ref, ffd_grad_ref,
    joined,
):
    first = pl.program_id(0) == 0
    low_rank = sets_ref.shape[1]
    width_hidden = wd_ref.shape[0]
    padded = down_ffd_ref.shape[1]

    @at_start
    def _():
        joined[:width_hidden, :] = wd_ref[...]
        joined[width_hidden:padded, :] = jnp.zeros(
            (padded - width_hidden, joined.shape[1]), bfloat
        )
        joined[padded:, :] = up_ref[...]

    hidden = hidden_ref[...]
    inner = inner_ref[...]
    u_down = masked(
        nt(hidden, down_ffd_ref[...]), chosen_columns(table_ref[...], sets_ref[...])
    )
    out_ref[...] = low(nn(jnp.concatenate([hidden, u_down], axis=1), joined[...]))
    accumulate(down_grad_ref, tn(du_ref[...], rows_ref[...]), first)
    accumulate(res_grad_ref, tn(u_down, grad_ref[...]), first)
    accumulate(up_grad_ref.at[0], tn(inner[:, :low_rank], ff_grad_ref[:, :padded]), first)
    accumulate(up_grad_ref.at[1], tn(inner[:, low_rank:], ff_grad_ref[:, padded:]), first)
    accumulate(ffd_grad_ref, tn(du_down_ref[...], hidden), first)


def branch_kernel(
    branch_ref, raw_ref, map_ref, gate_ref, table_ref, entering_ref, gain_ref, sets_ref, wo_ref,
    down_out_t_ref, up_ref, up_gate_ref,
    raw_grad_ref, gate_grad_ref, du_out_ref, du_gate_ref, state_grad_ref,
    joined, total,
    *, heads, key_width, value_width,
):
    first = pl.program_id(0) == 0
    width = wo_ref.shape[1]

    @at_start
    def _():
        joined[:, :width] = wo_ref[...]
        joined[:, width:] = down_out_t_ref[...]

    chosen = chosen_columns(table_ref[...], sets_ref[...])
    branch = branch_ref[...]
    outputs = head_outputs(raw_ref, map_ref, entering_ref, heads, key_width, value_width)
    du_out = masked(nt(branch, up_ref[...]), chosen)
    du_out_ref[...] = du_out
    mixed_grad = nt(jnp.concatenate([branch, du_out], axis=1), joined[...])
    gain = gain_ref[0:1, :]
    gate_grads = []
    for h, output in enumerate(outputs):
        lanes = slice(h * value_width, (h + 1) * value_width)
        scale = lax.rsqrt(jnp.mean(output * output, axis=-1, keepdims=True) + EPS)
        value = gate_ref[:, lanes]
        logistic, active = silu_parts(value)
        incoming = mixed_grad[:, lanes]
        gate_grads.append(
            low(
                incoming
                * (output * scale * gain)
                * (logistic * (1.0 + value * (1.0 - logistic)))
            )
        )
        scaled = gain * (incoming * active)
        dot = jnp.mean(output * scaled, axis=-1, keepdims=True)
        raw_grad = low(scale * scaled - output * (scale * scale * scale * dot))
        raw_grad_ref[:, lanes] = raw_grad
        accumulate(
            total.at[h], tn(map_ref[:, h * key_width : (h + 1) * key_width], raw_grad), first
        )
    gate_grad = jnp.concatenate(gate_grads, axis=1)
    gate_grad_ref[...] = gate_grad
    du_gate_ref[...] = masked(nt(gate_grad, up_gate_ref[...]), chosen)

    @pl.when(pl.program_id(0) == pl.num_programs(0) - 1)
    def _():
        state_grad_ref[...] = low(total[...])


def branch_after_kernel(
    branch_ref, z_ref, u_out_ref, rows_ref, inner_ref, du_out_ref, du_gate_ref, gate_grad_ref,
    down_grad_ref, res_grad_ref, out_grad_ref, up_grad_ref,
):
    first = pl.program_id(0) == 0
    accumulate(down_grad_ref, tn(du_gate_ref[...], rows_ref[...]), first)
    accumulate(res_grad_ref, tn(u_out_ref[...], branch_ref[...]), first)
    accumulate(out_grad_ref, tn(du_out_ref[...], z_ref[...]), first)
    accumulate(up_grad_ref, tn(inner_ref[...], gate_grad_ref[...]), first)


def settled_rows(pre_ref, tail_ref, arrived_ref, place_ref, quarters, window):
    per_quarter = pl.num_programs(0) // quarters
    last = ((quarters - 1) ^ place_ref[0]) * per_quarter + per_quarter - 1
    window[...] = pre_ref[...]

    @pl.when(pl.program_id(0) == last)
    def _():
        window[window.shape[0] - HALO :, :] = low(tail_ref[...] + arrived_ref[...])

    return window[...]


def settle_grads_kernel(
    pre_ref, rows_ref, inner_ref, table_ref, tail_ref, arrived_ref, place_ref, sets_ref,
    up_qk_ref, up_value_ref,
    du_ref, down_grad_ref, up_qk_grad_ref, up_v_grad_ref,
    window,
):
    first = pl.program_id(0) == 0
    low_rank = sets_ref.shape[1]
    q_width = up_qk_ref.shape[2]
    chosen = chosen_columns(table_ref[...], sets_ref[...])
    pre = settled_rows(pre_ref, tail_ref, arrived_ref, place_ref, 4, window)
    query, key, value = pre[:, :q_width], pre[:, q_width : 2 * q_width], pre[:, 2 * q_width :]
    inner = inner_ref[...]
    du = jnp.concatenate(
        [
            masked(nt(query, up_qk_ref[0]), chosen),
            masked(nt(key, up_qk_ref[1]), chosen),
            masked(nt(value, up_value_ref[...]), chosen),
        ],
        axis=1,
    )
    du_ref[...] = du
    accumulate(down_grad_ref, tn(du, rows_ref[...]), first)
    accumulate(up_qk_grad_ref.at[0], tn(inner[:, :low_rank], query), first)
    accumulate(up_qk_grad_ref.at[1], tn(inner[:, low_rank : 2 * low_rank], key), first)
    accumulate(up_v_grad_ref, tn(inner[:, 2 * low_rank : 3 * low_rank], value), first)


def settle_kernel(
    pre_ref, gate_grad_ref, du_ref, du_gate_ref, mix_ref, tail_ref, arrived_ref, place_ref,
    down_mix_ref, wq_ref, wk_ref, wv_ref, wg_ref,
    part_ref,
    window, joined,
):
    q_width, v_width = wq_ref.shape[1], wv_ref.shape[1]

    @at_start
    def _():
        joined[:, :q_width] = wq_ref[...]
        joined[:, q_width : 2 * q_width] = wk_ref[...]
        joined[:, 2 * q_width : 2 * q_width + v_width] = wv_ref[...]
        joined[:, 2 * q_width + v_width :] = wg_ref[...]

    pre = settled_rows(pre_ref, tail_ref, arrived_ref, place_ref, 4, window)
    mix = low(mix_ref[...])
    spare = down_mix_ref.shape[0] - du_ref.shape[1] - du_gate_ref.shape[1] - mix.shape[1]
    small = jnp.concatenate(
        [du_ref[...], du_gate_ref[...], mix, jnp.zeros((mix.shape[0], spare), bfloat)], axis=1
    )
    part_ref[...] = low(
        nt(jnp.concatenate([pre, gate_grad_ref[...]], axis=1), joined[...])
        + nn(small, down_mix_ref[...])
    )


WHOLE, SCALAR = "whole", "scalar"


def by_rows(width, lane_block=0):
    return ("rows", width, lane_block)


def pieces(width):
    return ("pieces", width)


def blocked_call(body, name, count, inputs, outputs, scratch, flops, block=STEP):
    steps = count // block
    per = max(steps // 4, 1)
    in_specs, arrays, moved, groups_in, extra = [], [], 0, [], []
    for array, kind in inputs:
        members = array if isinstance(array, (list, tuple)) else [array]
        groups_in.append(len(members))
        arrays += members
        moved += sum(a.size * a.dtype.itemsize for a in members)
        if kind == WHOLE:
            zeros = (0,) * array.ndim
            in_specs.append(
                pl.BlockSpec(
                    array.shape, lambda i, zeros=zeros: zeros, pipeline_mode=pl.Buffered(1)
                )
            )
        elif kind == SCALAR:
            in_specs.append(pl.BlockSpec(memory_space=pltpu.SMEM))
        elif kind[0] == "rows":
            in_specs.append(
                pl.BlockSpec((block, kind[1]), lambda i, lane=kind[2]: (i, lane))
            )
        else:
            for b in range(4):
                in_specs.append(
                    pl.BlockSpec(
                        (block, kind[1]), lambda i, b=b: (jnp.clip(i - b * per, 0, per - 1), 0)
                    )
                )
            extra.append(pltpu.VMEM((block, kind[1]), members[0].dtype))
    out_specs, shapes, groups_out = [], [], []
    for shape, dtype, kind in outputs:
        if kind == "parts":
            quarter = shape[0] // 4
            for rows in (quarter, quarter, 2 * quarter):
                shapes.append(jax.ShapeDtypeStruct((rows, shape[1]), dtype))
            spec = (block, shape[1])
            out_specs += [
                pl.BlockSpec(spec, lambda i: (jnp.clip(i, 0, per - 1), 0)),
                pl.BlockSpec(spec, lambda i: (jnp.clip(i - 2 * per, 0, per - 1), 0)),
                pl.BlockSpec(
                    spec,
                    lambda i: (
                        jnp.clip(i - per, 0, per - 1) + jnp.clip(i - 3 * per + 1, 0, per), 0
                    ),
                ),
            ]
            groups_out.append(3)
            extra.append(pltpu.VMEM(spec, dtype))
        else:
            groups_out.append(1)
            shapes.append(jax.ShapeDtypeStruct(shape, dtype))
            if kind == "rows":
                out_specs.append(pl.BlockSpec((block, shape[1]), lambda i: (i, 0)))
            else:
                zeros = (0,) * len(shape)
                out_specs.append(pl.BlockSpec(shape, lambda i, zeros=zeros: zeros))

    def wrapped(*refs):
        refs = list(refs)
        spare = refs[len(in_specs) + len(out_specs) + len(scratch) :]
        own_scratch = refs[len(in_specs) + len(out_specs) : len(refs) - len(spare)]
        quarter = pl.program_id(0) // per
        given, later, at, used = [], [], 0, 0
        for size in groups_in:
            if size == 1:
                given.append(refs[at])
            else:
                held = spare[used]
                used += 1
                for b in range(size):

                    @pl.when(quarter == b)
                    def _(held=held, source=refs[at + b]):
                        held[...] = source[...]

                given.append(held)
            at += size
        for size in groups_out:
            if size == 1:
                given.append(refs[at])
            else:
                given.append(spare[used])
                later.append((spare[used], refs[at : at + size]))
                used += 1
            at += size
        body(*given, *own_scratch)
        for held, targets in later:
            for b, target in ((0, targets[0]), (2, targets[1]), (1, targets[2]), (3, targets[2])):

                @pl.when(quarter == b)
                def _(held=held, target=target):
                    target[...] = held[...]

    results = pl.pallas_call(
        wrapped,
        out_shape=tuple(shapes),
        grid=(steps,),
        in_specs=in_specs,
        out_specs=out_specs,
        scratch_shapes=list(scratch) + extra,
        compiler_params=pltpu.CompilerParams(
            dimension_semantics=("arbitrary",), vmem_limit_bytes=VMEM_LIMIT
        ),
        cost_estimate=pl.CostEstimate(flops=flops, bytes_accessed=moved, transcendentals=0),
        name=name,
    )(*arrays)
    grouped, at = [], 0
    for size in groups_out:
        grouped.append(results[at] if size == 1 else results[at : at + size])
        at += size
    return grouped


def flip(array, bit):
    groups = lax.axis_size("head")
    return lax.ppermute(array, "head", [(i, i ^ bit) for i in range(groups)])


def gather_rows(array):
    far = flip(array, 2)
    near = flip(array, 1)
    return [array, near, far, flip(far, 1)]


def tie(*arrays):
    return lax.optimization_barrier(arrays)


def near_sum(parts):
    own, far, pair = parts
    size = own.shape[0]
    arrived = flip(pair, 1)
    return (
        own.astype(single) + arrived[:size].astype(single),
        low(far.astype(single) + arrived[size:].astype(single)),
    )


def far_sum(own, far):
    return own + flip(far, 2).astype(single)


def shifted_along(array, axis, by):
    length = lax.axis_size(axis)
    pairs = [(i, i + by) for i in range(length) if 0 <= i + by < length]
    return lax.ppermute(array, axis, pairs)


def head_blocks(parts):
    place = lax.axis_index("head")

    def block(relative):
        blocks = []
        for part in parts:
            size = part.shape[1] // 4
            blocks.append(
                low(lax.dynamic_slice_in_dim(part, (place ^ relative) * size, size, 1))
            )
        return jnp.concatenate(blocks, axis=1)

    return block(0), block(2), jnp.concatenate([block(1), block(3)], axis=0)


def seq_parts(flat):
    members = lax.axis_size("seq")
    rows, lanes = flat.shape
    return lax.all_to_all(flat.reshape(members, rows // members, lanes), "seq", 0, 0)


def seq_spread(parts):
    members, rows, lanes = parts.shape
    summed = low(jnp.sum(parts.astype(single), axis=0))
    spread = jnp.broadcast_to(summed[None], parts.shape)
    return lax.all_to_all(spread, "seq", 0, 0).reshape(members * rows, lanes)


def head_spread(piece, count):
    place = lax.axis_index("head")
    far = flip(piece, 2)
    blocks = jnp.stack([piece, flip(piece, 1), far, flip(far, 1)])
    ordered = [lax.dynamic_index_in_dim(blocks, place ^ b, 0, False) for b in range(4)]
    size = piece.shape[1] // count
    return [
        jnp.concatenate(
            [o[:, k * size : (k + 1) * size].astype(single) for o in ordered], axis=1
        )
        for k in range(count)
    ]


def rms_scale(rows, gain):
    return rows * lax.rsqrt(jnp.mean(rows * rows, axis=-1, keepdims=True) + EPS) * gain


def rms_back(rows, gain, incoming):
    _, back = jax.vjp(lambda value: rms_scale(value, gain), rows)
    return back(incoming)[0]


def on_device(
    block_input,
    out_grad,
    lengths,
    doc_sets,
    norm1_gain,
    w_query,
    w_key,
    w_value,
    conv_query,
    conv_key,
    conv_value,
    w_decay_beta,
    decay_rate,
    decay_bias,
    w_gate_out,
    out_gain,
    w_out,
    norm2_gain,
    w_gate,
    w_up,
    w_down,
    adapt_down,
    adapt_up_qk,
    adapt_up_vg,
    adapt_up_ff,
    adapt_down_out,
    adapt_down_ffd,
    adapt_up_res,
):
    groups = lax.axis_size("head")
    members = lax.axis_size("seq")
    place = lax.axis_index("head")
    quarter, width = block_input.shape
    count = quarter * groups
    heads = decay_rate.shape[0]
    key_width = w_query.shape[1] // heads
    value_width = w_value.shape[1] // heads
    sets, rank = adapt_down.shape[1], adapt_down.shape[3]
    low_rank = sets * rank
    qk = heads * key_width
    device_start = lax.axis_index("seq") * count
    starts = jnp.sum(
        jnp.where(
            jnp.arange(lengths.shape[0])[None, :] < jnp.arange(lengths.shape[0])[:, None],
            lengths[None, :],
            0,
        ),
        axis=1,
    )
    order = jnp.arange(groups, dtype=jnp.int32) ^ place

    def tables(positions):
        reached = positions[:, None] >= starts[None, :]
        token_start = jnp.max(jnp.where(reached, starts[None, :], -1), axis=1)
        ended = positions[:, None] >= (starts + lengths)[None, :]
        token_set = jnp.sum(jnp.where(reached & ~ended, doc_sets[None, :], 0), axis=1)
        pair = jnp.stack([token_start - device_start, token_set], axis=1).astype(single)
        return jnp.pad(pair, ((0, 0), (0, 8 - pair.shape[1])))

    table = tables(
        (
            device_start + order[:, None] * quarter + jnp.arange(quarter, dtype=jnp.int32)[None, :]
        ).reshape(-1)
    )
    halo_table = tables(device_start + jnp.arange(-HALO, 0, dtype=jnp.int32))
    column_sets = jnp.broadcast_to(
        (jnp.arange(low_rank, dtype=jnp.int32) // rank).astype(single)[None, :], (8, low_rank)
    )

    down = adapt_down.transpose(0, 1, 3, 2).reshape(6 * low_rank, width)
    mixer_down, feed_down = down[: 4 * low_rank], down[4 * low_rank :]
    up_qk = adapt_up_qk.reshape(2, low_rank, -1)
    up_vg = adapt_up_vg.reshape(2, low_rank, -1)
    up_ff = adapt_up_ff.reshape(2, low_rank, -1)
    down_out = adapt_down_out.transpose(0, 2, 1).reshape(low_rank, -1)
    down_ffd = adapt_down_ffd.transpose(0, 2, 1).reshape(low_rank, -1)
    up_res = adapt_up_res.reshape(2, low_rank, width)
    conv = jnp.concatenate([conv_query, conv_key, conv_value], axis=1).astype(single)
    scalars = jnp.stack([decay_rate, decay_bias])
    where = place.reshape(1).astype(jnp.int32)
    down_mix = jnp.concatenate(
        [
            mixer_down,
            w_decay_beta.transpose(1, 2, 0).reshape(2 * heads, width),
            jnp.zeros((low_rank - 2 * heads, width), bfloat),
        ],
        axis=0,
    )
    gain = jnp.broadcast_to(out_gain[None, :], (8, value_width))
    hidden_width = w_down.shape[0]
    padded = -(-hidden_width // 256) * 256
    value_lanes = heads * value_width
    widen = lambda a: jnp.pad(a, [(0, 0)] * (a.ndim - 1) + [(0, padded - hidden_width)])
    up_ff_padded, down_ffd_padded = widen(up_ff), widen(down_ffd)

    input_float = block_input.astype(single)
    normed = low(rms_scale(input_float, norm1_gain))
    tail = normed[quarter - HALO :]
    halo = sum(
        lax.ppermute(
            tail,
            ("seq", "head"),
            [((s * groups) + groups - 1, (s + 1) * groups + h) for s in range(members - 1)],
        )
        for h in range(groups)
    )
    normed_all = gather_rows(normed)
    pre, gate_input, inner, columns, pre_halo = blocked_call(
        project_kernel,
        "project",
        count,
        [
            (normed_all, pieces(width)),
            (table, by_rows(8)),
            (halo, WHOLE),
            (halo_table, WHOLE),
            (column_sets, WHOLE),
            (down_mix, WHOLE),
            (w_query, WHOLE),
            (w_key, WHOLE),
            (w_value, WHOLE),
            (w_gate_out, WHOLE),
            (up_qk, WHOLE),
            (up_vg, WHOLE),
        ],
        [
            ((count, 2 * qk + value_lanes), bfloat, "rows"),
            ((count, value_lanes), single, "rows"),
            ((count, 4 * low_rank), bfloat, "rows"),
            ((count, 8), single, "rows"),
            ((HALO, 2 * qk + value_lanes), bfloat, "whole"),
        ],
        [pltpu.VMEM((width + low_rank, 2 * qk + 2 * value_lanes), bfloat)],
        count * 9_000_000,
    )
    out_grad_late, pre = tie(out_grad, pre)
    grad_all = gather_rows(out_grad_late)
    raw_local, mapped, *saved, sent, sent_state, sent_map = run_forward(
        where, pre, pre_halo, columns, conv, scalars, heads, key_width, value_width, quarter
    )

    hops = min(members - 1, -(-(DOC_MAX - 1) // count))
    got = [shifted_along(sent, "seq", hop) for hop in range(1, hops)]
    got.append(shifted_along(sent_state, "seq", hops))
    *grad_all, sent_map = tie(*grad_all, sent_map)
    hidden_grad, du_down = blocked_call(
        feed_before_kernel,
        "feed_before",
        count,
        [
            (grad_all, pieces(width)),
            (table, by_rows(8)),
            (column_sets, WHOLE),
            (w_down, WHOLE),
            (down_ffd.T, WHOLE),
            (up_res[1], WHOLE),
        ],
        [((count, padded), single, "rows"), ((count, low_rank), bfloat, "rows")],
        [pltpu.VMEM((padded, width + low_rank), bfloat)],
        count * 6_000_000,
    )
    raw_local, hidden_grad = tie(raw_local, hidden_grad)

    sizes = dict(heads=heads, key_width=key_width, value_width=value_width)
    attention_part, mixed, u_out, entering = blocked_call(
        functools.partial(attend_kernel, hops=hops, **sizes),
        "attend",
        count,
        [
            (raw_local, by_rows(value_lanes)),
            (mapped, by_rows(qk)),
            (gate_input, by_rows(value_lanes)),
            (table, by_rows(8)),
            (gain, WHOLE),
            (column_sets, WHOLE),
            (w_out, WHOLE),
            (down_out, WHOLE),
            (up_res[0], WHOLE),
        ]
        + [(part, WHOLE) for part in got],
        [
            ((count, width), bfloat, "parts"),
            ((count, value_lanes), bfloat, "rows"),
            ((count, low_rank), bfloat, "rows"),
            ((heads, key_width, value_width), bfloat, "whole"),
        ],
        [pltpu.VMEM((value_lanes + low_rank, width), bfloat)],
        count * 5_000_000,
    )
    residual = input_float + far_sum(*near_sum(attention_part))
    normed_mid = low(rms_scale(residual, norm2_gain))
    mid_all = gather_rows(normed_mid)
    normed_mid_done, sent_map = tie(mid_all[3], sent_map)
    mid_all = mid_all[:3] + [normed_mid_done]

    mid_part, hidden, ff_grad, u_ff, du_ff = blocked_call(
        feed_kernel,
        "feed",
        count,
        [
            (mid_all, pieces(width)),
            (hidden_grad, by_rows(padded)),
            (table, by_rows(8)),
            (column_sets, WHOLE),
            (feed_down, WHOLE),
            (w_gate.T, WHOLE),
            (w_up.T, WHOLE),
            (up_ff.transpose(0, 2, 1), WHOLE),
            (up_ff_padded, WHOLE),
        ],
        [
            ((count, width), bfloat, "parts"),
            ((count, padded), bfloat, "rows"),
            ((count, 2 * padded), bfloat, "rows"),
            ((count, 2 * low_rank), bfloat, "rows"),
            ((count, 2 * low_rank), bfloat, "rows"),
        ],
        [
            pltpu.VMEM((padded, width + low_rank), bfloat),
            pltpu.VMEM((padded, width + low_rank), bfloat),
            pltpu.VMEM((2 * padded + 2 * low_rank, width), bfloat),
        ],
        count * 15_000_000,
    )
    mid_own, mid_far = near_sum(mid_part)
    mid_far, hidden = tie(mid_far, hidden)
    mid_grad = far_sum(mid_own, mid_far)
    out_part, feed_down_grad, feed_res_grad, feed_up_grad, ffd_grad = blocked_call(
        feed_after_kernel,
        "feed_after",
        count,
        [
            (mid_all, pieces(width)),
            (grad_all, pieces(width)),
            (hidden, by_rows(padded)),
            (ff_grad, by_rows(2 * padded)),
            (u_ff, by_rows(2 * low_rank)),
            (du_ff, by_rows(2 * low_rank)),
            (du_down, by_rows(low_rank)),
            (table, by_rows(8)),
            (column_sets, WHOLE),
            (w_down, WHOLE),
            (down_ffd_padded, WHOLE),
            (up_res[1], WHOLE),
        ],
        [
            ((count, width), bfloat, "parts"),
            ((2 * low_rank, width), single, "whole"),
            ((low_rank, width), single, "whole"),
            ((2, low_rank, padded), single, "whole"),
            ((low_rank, padded), single, "whole"),
        ],
        [pltpu.VMEM((padded + low_rank, width), bfloat)],
        count * 12_000_000,
    )
    residual_grad = out_grad.astype(single) + rms_back(residual, norm2_gain, mid_grad)
    branch_low = low(residual_grad)
    branch_all = gather_rows(branch_low)
    feed_own, feed_far = near_sum(
        head_blocks([feed_down_grad[:low_rank], feed_down_grad[low_rank:], feed_res_grad])
    )
    feed_flat = jnp.concatenate(
        [
            low(far_sum(feed_own, feed_far)),
            low(feed_up_grad[0]),
            low(feed_up_grad[1]),
            low(ffd_grad),
        ],
        axis=1,
    )
    corner, feed_flat = tie(branch_all[3], feed_flat)
    branch_all = branch_all[:3] + [corner]
    feed_parts = seq_parts(feed_flat)

    raw_grad, gate_grad, du_out, du_outgate, state_grad = blocked_call(
        functools.partial(branch_kernel, **sizes),
        "branch",
        count,
        [
            (branch_all, pieces(width)),
            (raw_local, by_rows(value_lanes)),
            (mapped, by_rows(qk)),
            (gate_input, by_rows(value_lanes)),
            (table, by_rows(8)),
            (entering, WHOLE),
            (gain, WHOLE),
            (column_sets, WHOLE),
            (w_out, WHOLE),
            (down_out.T, WHOLE),
            (up_res[0], WHOLE),
            (up_vg[1], WHOLE),
        ],
        [
            ((count, value_lanes), bfloat, "rows"),
            ((count, value_lanes), bfloat, "rows"),
            ((count, low_rank), bfloat, "rows"),
            ((count, low_rank), bfloat, "rows"),
            ((heads, key_width, value_width), bfloat, "whole"),
        ],
        [
            pltpu.VMEM((value_lanes, width + low_rank), bfloat),
            pltpu.VMEM((heads, key_width, value_width), single),
        ],
        count * 7_000_000,
    )
    feed_parts, state_grad = tie(feed_parts, state_grad)
    maps_after = [shifted_along(sent_map, "seq", -hop) for hop in range(1, hops)]
    state_got = [shifted_along(state_grad, "seq", -hop) for hop in range(1, hops + 1)]
    mixer_down_late, branch_res_grad, out_down_grad, outgate_up_grad = blocked_call(
        branch_after_kernel,
        "branch_after",
        count,
        [
            (branch_all, pieces(width)),
            (mixed, by_rows(value_lanes)),
            (u_out, by_rows(low_rank)),
            (normed_all, pieces(width)),
            (inner, by_rows(low_rank, 3)),
            (du_out, by_rows(low_rank)),
            (du_outgate, by_rows(low_rank)),
            (gate_grad, by_rows(value_lanes)),
        ],
        [
            ((low_rank, width), single, "whole"),
            ((low_rank, width), single, "whole"),
            ((low_rank, value_lanes), single, "whole"),
            ((low_rank, value_lanes), single, "whole"),
        ],
        [],
        count * 3_000_000,
    )
    branch_flat = jnp.concatenate(
        [
            low(far_sum(*near_sum(head_blocks([mixer_down_late, branch_res_grad])))),
            low(out_down_grad),
            low(outgate_up_grad),
        ],
        axis=1,
    )
    out_own, out_far = near_sum(out_part)
    raw_grad, branch_flat, feed_parts, out_far = tie(raw_grad, branch_flat, feed_parts, out_far)
    result = residual + far_sum(out_own, out_far)
    feed_total = seq_spread(feed_parts)
    branch_parts = seq_parts(branch_flat)

    pre_grad, mix_grad, tail_grad, edge_grad = run_backward(
        where, pre, pre_halo, columns, conv, scalars, raw_grad, saved, entering, state_got,
        maps_after, heads, key_width, value_width, quarter,
    )
    arrived = shifted_along(edge_grad, "seq", -1)
    arrived, feed_total, branch_parts = tie(arrived, feed_total, branch_parts)
    branch_total = seq_spread(branch_parts)
    settled = [
        (pre_grad, by_rows(2 * qk + value_lanes)),
        (tail_grad, WHOLE),
        (arrived, WHOLE),
        (where, SCALAR),
    ]
    du_mix, mixer_down_grad, up_qk_grad, up_v_grad = blocked_call(
        settle_grads_kernel,
        "settle_grads",
        count,
        [
            settled[0],
            (normed_all, pieces(width)),
            (inner, by_rows(4 * low_rank)),
            (table, by_rows(8)),
            *settled[1:],
            (column_sets, WHOLE),
            (up_qk, WHOLE),
            (up_vg[0], WHOLE),
        ],
        [
            ((count, 3 * low_rank), bfloat, "rows"),
            ((3 * low_rank, width), single, "whole"),
            ((2, low_rank, qk), single, "whole"),
            ((low_rank, value_lanes), single, "whole"),
        ],
        [pltpu.VMEM((STEP, 2 * qk + value_lanes), bfloat)],
        count * 4_000_000,
    )
    last_own, last_far = near_sum(
        head_blocks([mixer_down_grad[p * low_rank : (p + 1) * low_rank] for p in range(3)])
    )
    last_far, gate_grad = tie(last_far, gate_grad)
    (normed_part,) = blocked_call(
        settle_kernel,
        "settle",
        count,
        [
            settled[0],
            (gate_grad, by_rows(value_lanes)),
            (du_mix, by_rows(3 * low_rank)),
            (du_outgate, by_rows(low_rank)),
            (mix_grad, by_rows(8)),
            *settled[1:],
            (down_mix, WHOLE),
            (w_query, WHOLE),
            (w_key, WHOLE),
            (w_value, WHOLE),
            (w_gate_out, WHOLE),
        ],
        [((count, width), bfloat, "parts")],
        [
            pltpu.VMEM((STEP, 2 * qk + value_lanes), bfloat),
            pltpu.VMEM((width, 2 * qk + 2 * value_lanes), bfloat),
        ],
        count * 10_000_000,
    )
    last_flat = jnp.concatenate(
        [
            low(far_sum(last_own, last_far)),
            low(up_qk_grad[0]),
            low(up_qk_grad[1]),
            low(up_v_grad),
        ],
        axis=1,
    )
    last_parts = seq_parts(last_flat)
    normed_grad = far_sum(*near_sum(normed_part))
    input_grad = residual_grad + rms_back(input_float, norm1_gain, normed_grad)
    last_total = seq_spread(last_parts)
    block_width = width // groups
    shared = head_spread(
        jnp.concatenate(
            [
                last_total[:, : 3 * block_width],
                branch_total[:, : 2 * block_width],
                feed_total[:, : 3 * block_width],
            ],
            axis=1,
        ),
        8,
    )

    def lanes_of(total, start, size):
        return total[:, start : start + size].astype(single)

    owned_qk = [lanes_of(last_total, 3 * block_width + k * qk, qk) for k in range(2)]
    owned_value = lanes_of(last_total, 3 * block_width + 2 * qk, value_lanes)
    owned_out = lanes_of(branch_total, 2 * block_width, value_lanes)
    owned_outgate = lanes_of(branch_total, 2 * block_width + value_lanes, value_lanes)
    owned_ff = [lanes_of(feed_total, 3 * block_width + k * padded, hidden_width) for k in range(2)]
    owned_ffd = lanes_of(feed_total, 3 * block_width + 2 * padded, hidden_width)

    def as_down(rows):
        return rows.reshape(sets, rank, -1).transpose(0, 2, 1)

    def as_up(rows):
        return rows.reshape(sets, rank, -1)

    return (
        low(result),
        input_grad,
        jnp.stack([as_down(shared[k]) for k in (0, 1, 2, 3, 5, 6)]),
        jnp.stack([as_up(part) for part in owned_qk]),
        jnp.stack([as_up(owned_value), as_up(owned_outgate)]),
        jnp.stack([as_up(part) for part in owned_ff]),
        as_down(owned_out),
        as_down(owned_ffd),
        jnp.stack([as_up(shared[4]), as_up(shared[7])]),
    )


def solution(mesh):
    rows = P(("seq", "head"), None)
    lanes = P(None, "head")
    last = P(None, None, None, "head")
    middle = P(None, "head", None)
    in_specs = (
        rows, rows, P(), P(), P(), lanes, lanes, lanes, lanes, lanes, lanes,
        P(None, None, "head"), P("head"), P("head"), lanes, P(), P("head", None), P(), lanes,
        lanes, P("head", None), P(), last, last, last, middle, middle, P(),
    )
    out_specs = (rows, rows, P(), last, last, last, middle, middle, P())
    return jax.shard_map(
        on_device, mesh=mesh, in_specs=in_specs, out_specs=out_specs, check_vma=False
    )
```

```python
import functools

import jax
import jax.numpy as jnp
from jax import lax
from jax.experimental import pallas as pl
from jax.experimental.pallas import tpu as pltpu
from jax.sharding import PartitionSpec as P

CHUNK = 128
STEP = 256
HALO = 16
DOC_MAX = 4096
EPS = 1e-06
VMEM_LIMIT = 56 * 1024 * 1024
bfloat = jnp.bfloat16
single = jnp.float32


def contract(left, right, left_dim, right_dim):
    return lax.dot_general(
        left,
        right,
        (((left_dim,), (right_dim,)), ((), ())),
        preferred_element_type=single,
    )


def nn(left, right):
    return contract(left, right, 1, 0)


def nt(left, right):
    return contract(left, right, 1, 1)


def tn(left, right):
    return contract(left, right, 0, 0)


def low(array):
    return array.astype(bfloat)


def iotas():
    rows = lax.broadcasted_iota(jnp.int32, (CHUNK, CHUNK), 0)
    columns = lax.broadcasted_iota(jnp.int32, (CHUNK, CHUNK), 1)
    return rows, columns


def split_two(array):
    high = low(array)
    return high, low(array - high.astype(single))


def near_exact(left, right):
    left_high, left_low = split_two(left)
    right_high, right_low = split_two(right)
    return nn(
        jnp.concatenate([left_high, left_high, left_low], axis=1),
        jnp.concatenate([right_high, right_low, right_high], axis=0),
    )


def ones_product(ones, array):
    high = low(array)
    rest = array - high.astype(single)
    middle = low(rest)
    lowest = low(rest - middle.astype(single))
    return nn(
        jnp.concatenate([ones, ones, ones], axis=1),
        jnp.concatenate([high, middle, lowest], axis=0),
    )


def unit_lower_inverses(stricts, rows, columns):
    eye = (rows == columns).astype(single)
    differ = rows ^ columns
    block = 8
    inner = [jnp.where(differ < block, strict, 0.0) for strict in stricts]
    second = [near_exact(a, a) for a in inner]
    inverse = [near_exact(eye - a, eye + b) for a, b in zip(inner, second)]
    fourth = [near_exact(b, b) for b in second]
    inverse = [near_exact(a, eye + b) for a, b in zip(inverse, fourth)]
    while block < CHUNK:
        between = (differ >= block) & (differ < 2 * block)
        off = [jnp.where(between, strict, 0.0) for strict in stricts]
        part = [near_exact(a, b) for a, b in zip(off, inverse)]
        inverse = [a - near_exact(a, b) for a, b in zip(inverse, part)]
        block = 2 * block
    return inverse


def softplus(value):
    return jnp.maximum(value, 0.0) + jnp.log(1.0 + jnp.exp(-jnp.abs(value)))


def sigmoid(value):
    return 1.0 / (1.0 + jnp.exp(-value))


def gates(decay, start, rows, columns):
    lower_ones = low((rows >= columns).astype(single))
    total = ones_product(lower_ones, jnp.broadcast_to(decay, (CHUNK, CHUNK)))
    linked = (rows >= columns) & (columns >= start)
    within = jnp.where(linked, jnp.exp(jnp.where(linked, total - total.T, 0.0)), 0.0)
    running = total[:, :1]
    carried = jnp.where(start < 0, jnp.exp(running), 0.0)
    last = running[CHUNK - 1 : CHUNK]
    ending = jnp.where(
        rows[:, :1] >= start[CHUNK - 1 : CHUNK], jnp.exp(jnp.minimum(last - running, 0.0)), 0.0
    )
    return within, carried, ending


def convolved(window, starts, weights, base):
    positions = base + lax.broadcasted_iota(jnp.int32, (STEP, 1), 0)
    taps = weights.shape[0]
    total = None
    for tap in range(taps):
        back = taps - 1 - tap
        term = window[HALO - back : HALO - back + STEP, :] * weights[tap : tap + 1, :]
        if back:
            term = jnp.where(positions - back >= starts, term, 0.0)
        total = term if total is None else total + term
    return total


def head_scales(rows, width):
    return lax.rsqrt(jnp.sum(rows * rows, axis=-1, keepdims=True) + EPS)


def forward_kernel(
    place,
    rows_ref,
    halo_ref,
    column_ref,
    weight_ref,
    scalar_ref,
    out_ref,
    map_ref,
    written_ref,
    state_ref,
    inverse_ref,
    end_ref,
    sent_ref,
    sent_state_ref,
    sent_map_ref,
    window,
    state,
    *,
    heads,
    key_width,
    value_width,
):
    step = pl.program_id(0)
    wide = value_width + key_width
    base = step * STEP
    rows, columns = iotas()

    @pl.when(step == 0)
    def _():
        window[0:HALO, :] = halo_ref[...].astype(single)
        for h in range(heads):
            state[h, :, :value_width] = jnp.zeros((key_width, value_width), single)
            state[h, :, value_width:] = (rows == columns).astype(single)

    @pl.when(step > 0)
    def _():
        window[0:HALO, :] = window[STEP : STEP + HALO, :]

    window[HALO:, :] = rows_ref[...].astype(single)
    info = column_ref[...]
    starts = info[:, 2 * heads : 2 * heads + 1].astype(jnp.int32)
    before = convolved(window, starts, weight_ref[...], base)
    active = before * sigmoid(before)
    qk_lanes = heads * key_width
    chunks = STEP // CHUNK
    local, stricts = [], []
    for c in range(chunks):
        span = slice(c * CHUNK, (c + 1) * CHUNK)
        for h in range(heads):
            query = active[span, h * key_width : (h + 1) * key_width]
            key = active[span, qk_lanes + h * key_width : qk_lanes + (h + 1) * key_width]
            value = active[
                span, 2 * qk_lanes + h * value_width : 2 * qk_lanes + (h + 1) * value_width
            ]
            query = query * (head_scales(query, key_width) * key_width ** (-0.5))
            key = key * head_scales(key, key_width)
            beta = sigmoid(info[span, h : h + 1])
            decay = -scalar_ref[0, h] * softplus(
                info[span, heads + h : heads + h + 1] + scalar_ref[1, h]
            )
            within, carried, ending = gates(
                decay, starts[span] - (base + c * CHUNK), rows, columns
            )
            query, key = low(query), low(key)
            strict = jnp.where(rows > columns, within * nt(key, key), 0.0) * beta
            mixed = low(within * nt(query, key))
            stricts.append(strict)
            local.append((query, key, value, beta, carried, ending, mixed))
    inverses = [low(a) for a in unit_lower_inverses(stricts, rows, columns)]
    each = range(heads)
    now = [state[h] for h in each]
    for c in range(chunks):
        span = slice(c * CHUNK, (c + 1) * CHUNK)
        here = [local[c * heads + h] for h in each]
        inverse = [inverses[c * heads + h] for h in each]
        now_low = [low(a) for a in now]
        read = [nn(here[h][1], now_low[h]) for h in each]
        asked = [nn(here[h][0], now_low[h]) for h in each]
        target = []
        for h in each:
            query, key, value, beta, carried, ending, mixed = here[h]
            gap = -(carried * beta) * read[h]
            target.append(
                jnp.concatenate(
                    [beta * value + gap[:, :value_width], gap[:, value_width:]], axis=1
                )
            )
        written = [nn(inverse[h], low(target[h])) for h in each]
        added = [tn(here[h][1], low(here[h][5] * written[h])) for h in each]
        inner = [nn(here[h][6], low(written[h])) for h in each]
        for h in each:
            carried = here[h][4]
            inverse_ref[span, h * CHUNK : (h + 1) * CHUNK] = inverse[h]
            state_ref[c, h] = now_low[h]
            written_ref[span, h * wide : (h + 1) * wide] = low(written[h])
            output = carried * asked[h] + inner[h]
            out_ref[span, h * value_width : (h + 1) * value_width] = output[:, :value_width]
            map_ref[span, h * key_width : (h + 1) * key_width] = low(output[:, value_width:])
        now = [here[h][4][CHUNK - 1 : CHUNK] * now[h] + added[h] for h in each]
    for h in each:
        state[h] = now[h]

    @pl.when(step == pl.num_programs(0) - 1)
    def _():
        final = state[...]
        end_ref[...] = final
        sent_ref[...] = low(final)
        sent_state_ref[...] = low(final[:, :, :value_width])
        sent_map_ref[...] = low(final[:, :, value_width:])


def backward_kernel(
    place,
    rows_ref,
    before_ref,
    halo_ref,
    column_ref,
    weight_ref,
    scalar_ref,
    grad_ref,
    written_ref,
    state_ref,
    inverse_ref,
    end_ref,
    entering_ref,
    *rest,
    hops,
    heads,
    key_width,
    value_width,
):
    got_refs, after_refs, rest = rest[:hops], rest[hops : 2 * hops - 1], rest[2 * hops - 1 :]
    out_ref, mix_ref, tail_ref, edge_ref, window, shifted, shifted_start, cotangent, ahead = rest
    step = pl.program_id(0)
    steps = pl.num_programs(0)
    wide = value_width + key_width
    base = (steps - 1 - step) * STEP
    rows, columns = iotas()
    qk_lanes = heads * key_width
    lanes = window.shape[1]
    taps = weight_ref.shape[0]

    @pl.when(step == 0)
    def _():
        shifted[STEP : STEP + 8, :] = jnp.zeros((8, lanes), single)
        shifted_start[STEP : STEP + 8, :] = jnp.zeros((8, 1), jnp.int32)
        for h in range(heads):
            passed = got_refs[hops - 1][h].astype(single)
            for hop in range(hops - 1, 0, -1):
                passed = got_refs[hop - 1][h].astype(single) + tn(
                    after_refs[hop - 1][h], low(passed)
                )
            cotangent[h] = passed
            ahead[h] = end_ref[h, :, :value_width] + nn(
                low(end_ref[h, :, value_width:]), low(entering_ref[h])
            )

    @pl.when(step > 0)
    def _():
        shifted[STEP : STEP + 8, :] = shifted[0:8, :]
        shifted_start[STEP : STEP + 8, :] = shifted_start[0:8, :]

    window[0:HALO, :] = jnp.where(
        step == steps - 1, halo_ref[...].astype(single), before_ref[...].astype(single)
    )
    window[HALO:, :] = rows_ref[...].astype(single)
    info = column_ref[...]
    starts = info[:, 2 * heads : 2 * heads + 1].astype(jnp.int32)
    positions = base + lax.broadcasted_iota(jnp.int32, (STEP, 1), 0)
    before = convolved(window, starts, weight_ref[...], base)
    gate = sigmoid(before)
    active = before * gate
    slope = gate * (1.0 + before * (1.0 - gate))
    upper_ones = low((rows <= columns).astype(single))
    last_row = rows[:, :1] == CHUNK - 1
    chunks = STEP // CHUNK
    each = range(heads)
    items = [(c, h) for c in range(chunks) for h in each]
    spans = {item: slice(item[0] * CHUNK, (item[0] + 1) * CHUNK) for item in items}
    entering = [low(entering_ref[h]) for h in each]
    root = key_width ** (-0.5)

    def per(function):
        return {item: function(*item) for item in items}

    def q_lanes(h):
        return slice(h * key_width, (h + 1) * key_width)

    def k_lanes(h):
        return slice(qk_lanes + h * key_width, qk_lanes + (h + 1) * key_width)

    def v_lanes(h):
        return slice(2 * qk_lanes + h * value_width, 2 * qk_lanes + (h + 1) * value_width)

    def kept(c, h, part):
        return written_ref[spans[c, h], h * wide : (h + 1) * wide][:, part]

    values, maps = slice(0, value_width), slice(value_width, wide)
    query_raw = per(lambda c, h: active[spans[c, h], q_lanes(h)])
    key_raw = per(lambda c, h: active[spans[c, h], k_lanes(h)])
    query_scale = per(lambda c, h: head_scales(query_raw[c, h], key_width))
    key_scale = per(lambda c, h: head_scales(key_raw[c, h], key_width))
    query = per(lambda c, h: query_raw[c, h] * (query_scale[c, h] * root))
    key = per(lambda c, h: key_raw[c, h] * key_scale[c, h])
    query_low = per(lambda c, h: low(query[c, h]))
    key_low = per(lambda c, h: low(key[c, h]))
    beta = per(lambda c, h: sigmoid(info[spans[c, h], h : h + 1]))
    raw = per(lambda c, h: info[spans[c, h], heads + h : heads + h + 1] + scalar_ref[1, h])
    gated = per(
        lambda c, h: gates(
            -scalar_ref[0, h] * softplus(raw[c, h]),
            starts[spans[c, h]] - (base + c * CHUNK),
            rows,
            columns,
        )
    )
    within = per(lambda c, h: gated[c, h][0])
    carried = per(lambda c, h: gated[c, h][1])
    ending = per(lambda c, h: gated[c, h][2])
    mixed = per(lambda c, h: low(within[c, h] * nt(query_low[c, h], key_low[c, h])))
    written = per(
        lambda c, h: kept(c, h, values).astype(single) + nn(kept(c, h, maps), entering[h])
    )
    start_state = per(
        lambda c, h: state_ref[c, h][:, values].astype(single)
        + nn(state_ref[c, h][:, maps], entering[h])
    )
    written_low = per(lambda c, h: low(written[c, h]))
    start_low = per(lambda c, h: low(start_state[c, h]))
    grad = per(lambda c, h: grad_ref[spans[c, h], h * value_width : (h + 1) * value_width])
    grad_low = grad
    carried_grad = per(lambda c, h: low(carried[c, h] * grad[c, h].astype(single)))
    from_output = per(lambda c, h: tn(mixed[c, h], grad_low[c, h]))
    state_part = per(lambda c, h: tn(query_low[c, h], carried_grad[c, h]))
    mixed_grad = per(lambda c, h: low(within[c, h] * nt(grad_low[c, h], written_low[c, h])))
    query_grad = per(
        lambda c, h: nt(carried_grad[c, h], start_low[c, h]) + nn(mixed_grad[c, h], key_low[c, h])
    )
    key_write = per(lambda c, h: tn(mixed_grad[c, h], query_low[c, h]))
    later, later_low, solved, value_grad, read_grad = {}, {}, {}, {}, {}
    now = [cotangent[h] for h in each]
    for c in reversed(range(chunks)):
        for h in each:
            later[c, h], later_low[c, h] = now[h], low(now[h])
        from_state = [nn(key_low[c, h], later_low[c, h]) for h in each]
        written_grad = [low(from_output[c, h] + ending[c, h] * from_state[h]) for h in each]
        for h in each:
            inverse = inverse_ref[spans[c, h], h * CHUNK : (h + 1) * CHUNK]
            solved[c, h] = tn(inverse, written_grad[h])
        for h in each:
            value_grad[c, h] = beta[c, h] * solved[c, h]
            read_grad[c, h] = low(-carried[c, h] * value_grad[c, h])
        now = [
            carried[c, h][CHUNK - 1 : CHUNK] * now[h]
            + state_part[c, h]
            + tn(key_low[c, h], read_grad[c, h])
            for h in each
        ]
    following = {
        (c, h): start_state[c + 1, h] if c + 1 < chunks else ahead[h] for c, h in items
    }
    at_end = per(lambda c, h: jnp.sum(later[c, h] * following[c, h], keepdims=True))
    for h in each:
        cotangent[h] = now[h]
        ahead[h] = start_state[0, h]
    strict_grad = per(
        lambda c, h: low(
            jnp.where(
                rows > columns, -within[c, h] * nt(low(value_grad[c, h]), written_low[c, h]), 0.0
            )
        )
    )
    key_read = per(
        lambda c, h: nt(read_grad[c, h], start_low[c, h]) + nn(strict_grad[c, h], key_low[c, h])
    )
    key_write = per(
        lambda c, h: key_write[c, h]
        + tn(strict_grad[c, h], key_low[c, h])
        + nt(low(ending[c, h] * written[c, h]), later_low[c, h])
    )
    query_dot = per(
        lambda c, h: jnp.sum(query[c, h] * query_grad[c, h], axis=-1, keepdims=True)
    )
    running_grad = per(
        lambda c, h: query_dot[c, h]
        + jnp.sum(key[c, h] * (key_read[c, h] - key_write[c, h]), axis=-1, keepdims=True)
        + jnp.where(last_row, at_end[c, h], 0.0)
    )
    decay_sum = per(
        lambda c, h: ones_product(
            upper_ones, jnp.broadcast_to(running_grad[c, h], (CHUNK, CHUNK))
        )[:, :1]
    )
    decay_grad = per(
        lambda c, h: jnp.where(
            positions[spans[c, h]] == starts[spans[c, h]],
            0.0,
            -scalar_ref[0, h] * sigmoid(raw[c, h]) * decay_sum[c, h],
        )
    )
    beta_grad = per(
        lambda c, h: jnp.sum(solved[c, h] * written[c, h], axis=-1, keepdims=True)
        * sigmoid(-info[spans[c, h], h : h + 1])
    )
    for c, h in items:
        span = spans[c, h]
        key_grad = key_read[c, h] + key_write[c, h]
        key_dot = jnp.sum(key[c, h] * key_grad, axis=-1, keepdims=True)
        query_active = (query_scale[c, h] * root) * query_grad[c, h] - query_raw[c, h] * (
            query_scale[c, h] * query_scale[c, h] * query_dot[c, h]
        )
        key_active = key_scale[c, h] * (key_grad - key[c, h] * key_dot)
        shifted[span, q_lanes(h)] = query_active * slope[span, q_lanes(h)]
        shifted[span, k_lanes(h)] = key_active * slope[span, k_lanes(h)]
        shifted[span, v_lanes(h)] = value_grad[c, h] * slope[span, v_lanes(h)]
    for c in range(chunks):
        mix_ref[c * CHUNK : (c + 1) * CHUNK, :] = jnp.concatenate(
            [beta_grad[c, h] for h in each]
            + [decay_grad[c, h] for h in each]
            + [jnp.zeros((CHUNK, mix_ref.shape[1] - 2 * heads), single)],
            axis=1,
        )
    shifted_start[0:STEP, :] = starts
    total = None
    for tap in range(taps):
        back = taps - 1 - tap
        term = shifted[back : back + STEP, :] * weight_ref[tap : tap + 1, :]
        if back:
            term = jnp.where(positions >= shifted_start[back : back + STEP, :], term, 0.0)
        total = term if total is None else total + term
    out_ref[...] = low(total)

    @pl.when(step == 0)
    def _():
        tail_ref[...] = total[STEP - HALO :, :]

    @pl.when(step == steps - 1)
    def _():
        window[0:8, :] = jnp.zeros((8, lanes), single)
        window[8:16, :] = shifted[0:8, :]
        early = lax.broadcasted_iota(jnp.int32, (8, 1), 0) - 8
        collected = jnp.zeros((8, lanes), single)
        for tap in range(taps - 1):
            back = taps - 1 - tap
            reader = early + back
            reader_start = jnp.zeros((8, 1), jnp.int32)
            for t in range(back):
                reader_start = jnp.where(reader == t, shifted_start[t : t + 1, :], reader_start)
            term = window[back : back + 8, :] * weight_ref[tap : tap + 1, :]
            collected = collected + jnp.where(
                (reader >= 0) & (early >= reader_start), term, 0.0
            )
        edge_ref[0:8, :] = jnp.zeros((8, lanes), single)
        edge_ref[8:16, :] = collected


def block_place(step, place, per_quarter):
    return ((step // per_quarter) ^ place[0]) * per_quarter + step % per_quarter


def run_forward(place, rows, halo, columns, weights, scalars, heads, key_width, value_width, quarter):
    count, lanes = columns.shape[0], rows.shape[1]
    steps, per_quarter = count // STEP, quarter // STEP
    wide = value_width + key_width
    chunks = STEP // CHUNK
    at = lambda i, place: (block_place(i, place, per_quarter), 0)
    fixed = lambda i, place: (0, 0)
    body = functools.partial(
        forward_kernel, heads=heads, key_width=key_width, value_width=value_width
    )
    shapes = (
        jax.ShapeDtypeStruct((count, heads * value_width), single),
        jax.ShapeDtypeStruct((count, heads * key_width), bfloat),
        jax.ShapeDtypeStruct((count, heads * wide), bfloat),
        jax.ShapeDtypeStruct((count // CHUNK, heads, key_width, wide), bfloat),
        jax.ShapeDtypeStruct((count, heads * CHUNK), bfloat),
        jax.ShapeDtypeStruct((heads, key_width, wide), single),
        jax.ShapeDtypeStruct((heads, key_width, wide), bfloat),
        jax.ShapeDtypeStruct((heads, key_width, value_width), bfloat),
        jax.ShapeDtypeStruct((heads, key_width, key_width), bfloat),
    )
    return pl.pallas_call(
        body,
        out_shape=shapes,
        grid_spec=pltpu.PrefetchScalarGridSpec(
            num_scalar_prefetch=1,
            grid=(steps,),
            in_specs=[
                pl.BlockSpec((STEP, lanes), at),
                pl.BlockSpec((HALO, lanes), lambda i, place: (0, 0)),
                pl.BlockSpec((STEP, columns.shape[1]), at),
                pl.BlockSpec(weights.shape, fixed),
                pl.BlockSpec(memory_space=pltpu.SMEM),
            ],
            out_specs=[
                pl.BlockSpec((STEP, heads * value_width), at),
                pl.BlockSpec((STEP, heads * key_width), at),
                pl.BlockSpec((STEP, heads * wide), at),
                pl.BlockSpec((chunks, heads, key_width, wide), lambda i, place: (i, 0, 0, 0)),
                pl.BlockSpec((STEP, heads * CHUNK), at),
                pl.BlockSpec((heads, key_width, wide), lambda i, place: (0, 0, 0)),
                pl.BlockSpec((heads, key_width, wide), lambda i, place: (0, 0, 0)),
                pl.BlockSpec((heads, key_width, value_width), lambda i, place: (0, 0, 0)),
                pl.BlockSpec((heads, key_width, key_width), lambda i, place: (0, 0, 0)),
            ],
            scratch_shapes=[
                pltpu.VMEM((STEP + HALO, lanes), single),
                pltpu.VMEM((heads, key_width, wide), single),
            ],
        ),
        compiler_params=pltpu.CompilerParams(
            dimension_semantics=("arbitrary",), vmem_limit_bytes=VMEM_LIMIT
        ),
        cost_estimate=pl.CostEstimate(
            flops=count * 2_000_000, bytes_accessed=count * 10_000, transcendentals=count * 2000
        ),
        name="delta_forward",
    )(place, rows, halo, columns, weights, scalars)


def run_backward(
    place, rows, halo, columns, weights, scalars, grad, saved, entering, got, after, heads,
    key_width, value_width, quarter,
):
    written, states, inverses, end = saved
    count, lanes = columns.shape[0], rows.shape[1]
    steps, per_quarter = count // STEP, quarter // STEP
    wide = value_width + key_width
    chunks = STEP // CHUNK

    def at(i, place):
        return (block_place(steps - 1 - i, place, per_quarter), 0)

    def halo_at(i, place):
        here = steps - 1 - i
        inner = block_place(jnp.maximum(here - 1, 0), place, per_quarter)
        ratio = STEP // HALO
        return (inner * ratio + ratio - 1, 0)

    fixed = lambda i, place: (0, 0)
    whole = lambda i, place: (0, 0, 0)
    body = functools.partial(
        backward_kernel,
        hops=len(got),
        heads=heads,
        key_width=key_width,
        value_width=value_width,
    )
    shapes = (
        jax.ShapeDtypeStruct((count, lanes), bfloat),
        jax.ShapeDtypeStruct((count, columns.shape[1]), single),
        jax.ShapeDtypeStruct((HALO, lanes), single),
        jax.ShapeDtypeStruct((HALO, lanes), single),
    )
    return pl.pallas_call(
        body,
        out_shape=shapes,
        grid_spec=pltpu.PrefetchScalarGridSpec(
            num_scalar_prefetch=1,
            grid=(steps,),
            in_specs=[
                pl.BlockSpec((STEP, lanes), at),
                pl.BlockSpec((HALO, lanes), halo_at),
                pl.BlockSpec((HALO, lanes), fixed),
                pl.BlockSpec((STEP, columns.shape[1]), at),
                pl.BlockSpec(weights.shape, fixed),
                pl.BlockSpec(memory_space=pltpu.SMEM),
                pl.BlockSpec((STEP, heads * value_width), at),
                pl.BlockSpec((STEP, heads * wide), at),
                pl.BlockSpec(
                    (chunks, heads, key_width, wide), lambda i, place: (steps - 1 - i, 0, 0, 0)
                ),
                pl.BlockSpec((STEP, heads * CHUNK), at),
                pl.BlockSpec(end.shape, whole),
                pl.BlockSpec(entering.shape, whole),
            ]
            + [pl.BlockSpec(part.shape, whole) for part in (*got, *after)],
            out_specs=[
                pl.BlockSpec((STEP, lanes), at),
                pl.BlockSpec((STEP, columns.shape[1]), at),
                pl.BlockSpec((HALO, lanes), fixed),
                pl.BlockSpec((HALO, lanes), fixed),
            ],
            scratch_shapes=[
                pltpu.VMEM((STEP + HALO, lanes), single),
                pltpu.VMEM((STEP + 8, lanes), single),
                pltpu.VMEM((STEP + 8, 1), jnp.int32),
                pltpu.VMEM((heads, key_width, value_width), single),
                pltpu.VMEM((heads, key_width, value_width), single),
            ],
        ),
        compiler_params=pltpu.CompilerParams(
            dimension_semantics=("arbitrary",), vmem_limit_bytes=VMEM_LIMIT
        ),
        cost_estimate=pl.CostEstimate(
            flops=count * 3_000_000, bytes_accessed=count * 12_000, transcendentals=count * 3000
        ),
        name="delta_backward",
    )(
        place, rows, rows, halo, columns, weights, scalars, grad, written, states, inverses, end,
        entering, *got, *after,
    )


def chosen_columns(table, column_sets):
    return column_sets[0:1, :] == table[:, 1:2]


def masked(product, chosen):
    return low(jnp.where(chosen, product, 0.0))


def silu_parts(value):
    logistic = sigmoid(value)
    return logistic, value * logistic


def accumulate(ref, value, first):
    ref[...] = jnp.where(first, value, ref[...] + value)


def emit_blocks(parts, place, own_ref, far_ref, pair_ref):
    for k, part in enumerate(parts):
        rows, size = part.shape[0], part.shape[1] // 4
        lanes = slice(k * size, (k + 1) * size)
        for relative, target, row in (
            (0, own_ref, 0), (2, far_ref, 0), (1, pair_ref, 0), (3, pair_ref, rows)
        ):
            start = pl.multiple_of((place ^ relative) * size, 128)
            target[row : row + rows, lanes] = low(part[:, pl.ds(start, size)])


def at_end(fill):
    pl.when(pl.program_id(0) == pl.num_programs(0) - 1)(fill)


def at_start(fill):
    pl.when(pl.program_id(0) == 0)(fill)


def project_kernel(
    rows_ref, table_ref, halo_ref, halo_table_ref, sets_ref, down_mix_ref, wq_ref, wk_ref, wv_ref,
    wg_ref, up_qk_ref, up_vg_ref,
    pre_ref, gate_ref, inner_ref, column_ref, pre_halo_ref,
    joined,
):
    low_rank = sets_ref.shape[1]
    width, q_width = wq_ref.shape
    v_width = wv_ref.shape[1]
    bounds = [0, q_width, 2 * q_width, 2 * q_width + v_width, 2 * q_width + 2 * v_width]

    @at_start
    def _():
        weights = (wq_ref, wk_ref, wv_ref, wg_ref)
        ups = (up_qk_ref[0], up_qk_ref[1], up_vg_ref[0], up_vg_ref[1])
        for p in range(4):
            joined[:width, bounds[p] : bounds[p + 1]] = weights[p][...]
            joined[width:, bounds[p] : bounds[p + 1]] = ups[p]

    def projections(rows, table, store, last):
        chosen = chosen_columns(table, sets_ref[...])
        product = nt(rows, down_mix_ref[...])
        inner = [
            masked(product[:, p * low_rank : (p + 1) * low_rank], chosen) for p in range(last)
        ]
        outputs = [
            nn(
                jnp.concatenate([rows, inner[p]], axis=1), joined[:, bounds[p] : bounds[p + 1]]
            )
            for p in range(last)
        ]
        for p in range(3):
            store[:, bounds[p] : bounds[p + 1]] = low(outputs[p])
        return product, inner, outputs

    @at_start
    def _():
        projections(halo_ref[...], halo_table_ref[...], pre_halo_ref, 3)

    table = table_ref[...]
    product, inner, outputs = projections(rows_ref[...], table, pre_ref, 4)
    for p in range(4):
        inner_ref[:, p * low_rank : (p + 1) * low_rank] = inner[p]
    gate_ref[...] = outputs[3]
    column_ref[...] = jnp.concatenate(
        [product[:, 4 * low_rank : 4 * low_rank + 4], table[:, :4]], axis=1
    )


def head_outputs(raw_ref, map_ref, entering_ref, heads, key_width, value_width):
    outputs = []
    for h in range(heads):
        outputs.append(
            raw_ref[:, h * value_width : (h + 1) * value_width]
            + nn(map_ref[:, h * key_width : (h + 1) * key_width], entering_ref[h])
        )
    return outputs


def attend_kernel(
    raw_ref, map_ref, gate_ref, table_ref, gain_ref, sets_ref, wo_ref, down_ref, up_ref, *rest,
    heads, key_width, value_width, hops,
):
    got_refs, rest = rest[:hops], rest[hops:]
    part_ref, z_ref, inner_ref, entering_ref, joined = rest
    value_lanes = wo_ref.shape[0]

    @at_start
    def _():
        joined[:value_lanes, :] = wo_ref[...]
        joined[value_lanes:, :] = up_ref[...]
        for h in range(heads):
            state = got_refs[hops - 1][h].astype(single)
            for hop in range(hops - 1, 0, -1):
                got = got_refs[hop - 1][h]
                state = got[:, :value_width].astype(single) + nn(got[:, value_width:], low(state))
            entering_ref[h] = low(state)

    chosen = chosen_columns(table_ref[...], sets_ref[...])
    outputs = head_outputs(raw_ref, map_ref, entering_ref, heads, key_width, value_width)
    parts = []
    for h, output in enumerate(outputs):
        lanes = slice(h * value_width, (h + 1) * value_width)
        scale = lax.rsqrt(jnp.mean(output * output, axis=-1, keepdims=True) + EPS)
        _, gate = silu_parts(gate_ref[:, lanes])
        parts.append(low(output * scale * gain_ref[0:1, :] * gate))
    z = jnp.concatenate(parts, axis=1)
    z_ref[...] = z
    inner = masked(nt(z, down_ref[...]), chosen)
    inner_ref[...] = inner
    part_ref[...] = low(nn(jnp.concatenate([z, inner], axis=1), joined[...]))


def feed_before_kernel(
    grad_ref, table_ref, sets_ref, wd_ref, down_ffd_t_ref, up_ref, hidden_grad_ref, du_ref, joined
):
    hidden, width = wd_ref.shape

    @at_start
    def _():
        joined[:hidden, :width] = wd_ref[...]
        joined[:hidden, width:] = down_ffd_t_ref[...]
        joined[hidden:, :] = jnp.zeros((joined.shape[0] - hidden, joined.shape[1]), bfloat)

    grad = grad_ref[...]
    du_down = masked(nt(grad, up_ref[...]), chosen_columns(table_ref[...], sets_ref[...]))
    du_ref[...] = du_down
    hidden_grad_ref[...] = nt(jnp.concatenate([grad, du_down], axis=1), joined[...])


def feed_kernel(
    rows_ref, hidden_grad_ref, table_ref, sets_ref, down_ref, wg_ref, wu_ref, up_t_ref, up_ref,
    back_ref, hidden_ref, ff_grad_ref, inner_ref, du_ref,
    joined_gate, joined_up, joined_back,
):
    low_rank = sets_ref.shape[1]
    hidden, width = wg_ref.shape
    padded = joined_gate.shape[0]

    @at_start
    def _():
        for p, (joined, weight) in enumerate(((joined_gate, wg_ref), (joined_up, wu_ref))):
            joined[:hidden, :width] = weight[...]
            joined[:hidden, width:] = up_t_ref[p]
            joined[hidden:, :] = jnp.zeros((padded - hidden, joined.shape[1]), bfloat)
            joined_back[p * padded : p * padded + hidden, :] = weight[...]
            joined_back[p * padded + hidden : (p + 1) * padded, :] = jnp.zeros(
                (padded - hidden, width), bfloat
            )
        joined_back[2 * padded :, :] = down_ref[...]

    chosen = chosen_columns(table_ref[...], sets_ref[...])
    both = jnp.concatenate([chosen, chosen], axis=1)
    rows = rows_ref[...]
    inner = masked(nt(rows, down_ref[...]), both)
    inner_ref[...] = inner
    gate = nt(jnp.concatenate([rows, inner[:, :low_rank]], axis=1), joined_gate[...])
    up = nt(jnp.concatenate([rows, inner[:, low_rank:]], axis=1), joined_up[...])
    logistic, active = silu_parts(gate)
    hidden_ref[...] = low(active * up)
    hidden_grad = hidden_grad_ref[...]
    gate_grad = low(hidden_grad * up * logistic * (1.0 + gate * (1.0 - logistic)))
    up_grad = low(hidden_grad * active)
    du_gate = masked(nt(gate_grad, up_ref[0]), chosen)
    du_up = masked(nt(up_grad, up_ref[1]), chosen)
    du_ref[:, :low_rank] = du_gate
    du_ref[:, low_rank:] = du_up
    ff_grad_ref[:, :padded] = gate_grad
    ff_grad_ref[:, padded:] = up_grad
    back_ref[...] = low(
        nn(jnp.concatenate([gate_grad, up_grad, du_gate, du_up], axis=1), joined_back[...])
    )


def feed_after_kernel(
    rows_ref, grad_ref, hidden_ref, ff_grad_ref, inner_ref, du_ref, du_down_ref, table_ref,
    sets_ref, place_ref, wd_ref, down_ffd_ref, up_ref,
    out_ref, own_ref, far_ref, pair_ref, flat_ref,
    joined, down_sum, res_sum, flat_sum,
):
    first = pl.program_id(0) == 0
    low_rank = sets_ref.shape[1]
    width_hidden = wd_ref.shape[0]
    padded = down_ffd_ref.shape[1]

    @at_start
    def _():
        joined[:width_hidden, :] = wd_ref[...]
        joined[width_hidden:padded, :] = jnp.zeros(
            (padded - width_hidden, joined.shape[1]), bfloat
        )
        joined[padded:, :] = up_ref[...]

    hidden = hidden_ref[...]
    inner = inner_ref[...]
    u_down = masked(
        nt(hidden, down_ffd_ref[...]), chosen_columns(table_ref[...], sets_ref[...])
    )
    out_ref[...] = low(nn(jnp.concatenate([hidden, u_down], axis=1), joined[...]))
    accumulate(down_sum, tn(du_ref[...], rows_ref[...]), first)
    accumulate(res_sum, tn(u_down, grad_ref[...]), first)
    for k, grown in enumerate(
        (
            tn(inner[:, :low_rank], ff_grad_ref[:, :padded]),
            tn(inner[:, low_rank:], ff_grad_ref[:, padded:]),
            tn(du_down_ref[...], hidden),
        )
    ):
        accumulate(flat_sum.at[:, k * padded : (k + 1) * padded], grown, first)

    @at_end
    def _():
        flat_ref[...] = low(flat_sum[...])
        emit_blocks(
            (down_sum.at[:low_rank], down_sum.at[low_rank:], res_sum),
            place_ref[0], own_ref, far_ref, pair_ref,
        )


def branch_kernel(
    branch_ref, raw_ref, map_ref, gate_ref, table_ref, entering_ref, gain_ref, sets_ref, wo_ref,
    down_out_t_ref, up_ref, up_gate_ref,
    raw_grad_ref, gate_grad_ref, du_out_ref, du_gate_ref, state_grad_ref,
    joined, total,
    *, heads, key_width, value_width,
):
    first = pl.program_id(0) == 0
    width = wo_ref.shape[1]

    @at_start
    def _():
        joined[:, :width] = wo_ref[...]
        joined[:, width:] = down_out_t_ref[...]

    chosen = chosen_columns(table_ref[...], sets_ref[...])
    branch = branch_ref[...]
    outputs = head_outputs(raw_ref, map_ref, entering_ref, heads, key_width, value_width)
    du_out = masked(nt(branch, up_ref[...]), chosen)
    du_out_ref[...] = du_out
    mixed_grad = nt(jnp.concatenate([branch, du_out], axis=1), joined[...])
    gain = gain_ref[0:1, :]
    gate_grads = []
    for h, output in enumerate(outputs):
        lanes = slice(h * value_width, (h + 1) * value_width)
        scale = lax.rsqrt(jnp.mean(output * output, axis=-1, keepdims=True) + EPS)
        value = gate_ref[:, lanes]
        logistic, active = silu_parts(value)
        incoming = mixed_grad[:, lanes]
        gate_grads.append(
            low(
                incoming
                * (output * scale * gain)
                * (logistic * (1.0 + value * (1.0 - logistic)))
            )
        )
        scaled = gain * (incoming * active)
        dot = jnp.mean(output * scaled, axis=-1, keepdims=True)
        raw_grad = low(scale * scaled - output * (scale * scale * scale * dot))
        raw_grad_ref[:, lanes] = raw_grad
        accumulate(
            total.at[h], tn(map_ref[:, h * key_width : (h + 1) * key_width], raw_grad), first
        )
    gate_grad = jnp.concatenate(gate_grads, axis=1)
    gate_grad_ref[...] = gate_grad
    du_gate_ref[...] = masked(nt(gate_grad, up_gate_ref[...]), chosen)

    @pl.when(pl.program_id(0) == pl.num_programs(0) - 1)
    def _():
        state_grad_ref[...] = low(total[...])


def branch_after_kernel(
    branch_ref, z_ref, u_out_ref, rows_ref, inner_ref, du_out_ref, du_gate_ref, gate_grad_ref,
    down_grad_ref, res_grad_ref, flat_ref,
    flat_sum,
):
    first = pl.program_id(0) == 0
    lanes = z_ref.shape[1]
    accumulate(down_grad_ref, tn(du_gate_ref[...], rows_ref[...]), first)
    accumulate(res_grad_ref, tn(u_out_ref[...], branch_ref[...]), first)
    accumulate(flat_sum.at[:, :lanes], tn(du_out_ref[...], z_ref[...]), first)
    accumulate(flat_sum.at[:, lanes:], tn(inner_ref[...], gate_grad_ref[...]), first)

    @at_end
    def _():
        flat_ref[...] = low(flat_sum[...])


def settled_rows(pre_ref, tail_ref, arrived_ref, place_ref, quarters, window):
    per_quarter = pl.num_programs(0) // quarters
    last = ((quarters - 1) ^ place_ref[0]) * per_quarter + per_quarter - 1
    window[...] = pre_ref[...]

    @pl.when(pl.program_id(0) == last)
    def _():
        window[window.shape[0] - HALO :, :] = low(tail_ref[...] + arrived_ref[...])

    return window[...]


def settle_grads_kernel(
    pre_ref, rows_ref, inner_ref, table_ref, tail_ref, arrived_ref, place_ref, sets_ref,
    up_qk_ref, up_value_ref, down_late_ref, res_late_ref,
    du_ref, own_ref, far_ref, pair_ref, flat_ref,
    window, down_sum, flat_sum,
):
    first = pl.program_id(0) == 0
    low_rank = sets_ref.shape[1]
    q_width = up_qk_ref.shape[2]
    chosen = chosen_columns(table_ref[...], sets_ref[...])
    pre = settled_rows(pre_ref, tail_ref, arrived_ref, place_ref, 4, window)
    query, key, value = pre[:, :q_width], pre[:, q_width : 2 * q_width], pre[:, 2 * q_width :]
    inner = inner_ref[...]
    du = jnp.concatenate(
        [
            masked(nt(query, up_qk_ref[0]), chosen),
            masked(nt(key, up_qk_ref[1]), chosen),
            masked(nt(value, up_value_ref[...]), chosen),
        ],
        axis=1,
    )
    du_ref[...] = du
    accumulate(down_sum, tn(du, rows_ref[...]), first)
    at = 0
    for p, part in enumerate((query, key, value)):
        accumulate(
            flat_sum.at[:, at : at + part.shape[1]],
            tn(inner[:, p * low_rank : (p + 1) * low_rank], part),
            first,
        )
        at += part.shape[1]

    @at_end
    def _():
        flat_ref[...] = low(flat_sum[...])
        emit_blocks(
            [down_sum.at[p * low_rank : (p + 1) * low_rank] for p in range(3)]
            + [down_late_ref, res_late_ref],
            place_ref[0], own_ref, far_ref, pair_ref,
        )


def settle_kernel(
    pre_ref, gate_grad_ref, du_ref, du_gate_ref, mix_ref, tail_ref, arrived_ref, place_ref,
    down_mix_ref, wq_ref, wk_ref, wv_ref, wg_ref,
    part_ref,
    window, joined,
):
    q_width, v_width = wq_ref.shape[1], wv_ref.shape[1]

    @at_start
    def _():
        joined[:, :q_width] = wq_ref[...]
        joined[:, q_width : 2 * q_width] = wk_ref[...]
        joined[:, 2 * q_width : 2 * q_width + v_width] = wv_ref[...]
        joined[:, 2 * q_width + v_width :] = wg_ref[...]

    pre = settled_rows(pre_ref, tail_ref, arrived_ref, place_ref, 4, window)
    mix = low(mix_ref[...])
    spare = down_mix_ref.shape[0] - du_ref.shape[1] - du_gate_ref.shape[1] - mix.shape[1]
    small = jnp.concatenate(
        [du_ref[...], du_gate_ref[...], mix, jnp.zeros((mix.shape[0], spare), bfloat)], axis=1
    )
    part_ref[...] = low(
        nt(jnp.concatenate([pre, gate_grad_ref[...]], axis=1), joined[...])
        + nn(small, down_mix_ref[...])
    )


def assemble_kernel(
    place_ref, own_ref, near_ref, far_ref, corner_ref, last_ref, feed_ref, branch_ref,
    down_ref, qk_ref, vg_ref, ff_ref, out_ref, ffd_ref, res_ref,
):
    place = place_ref[0]
    size = own_ref.shape[1] // 8
    targets = [down_ref.at[p] for p in range(4)] + [res_ref.at[0]]
    targets += [down_ref.at[4], down_ref.at[5], res_ref.at[1]]
    for relative, piece in enumerate((own_ref, near_ref, far_ref, corner_ref)):
        start = pl.multiple_of((place ^ relative) * size, 128)
        for k, target in enumerate(targets):
            target[:, pl.ds(start, size)] = piece[:, k * size : (k + 1) * size].astype(single)
    last = last_ref[...].astype(single)
    qk, values = qk_ref.shape[2], vg_ref.shape[2]
    qk_ref[0], qk_ref[1] = last[:, :qk], last[:, qk : 2 * qk]
    vg_ref[0] = last[:, 2 * qk :]
    branch = branch_ref[...].astype(single)
    out_ref[...] = branch[:, :values]
    vg_ref[1] = branch[:, values:]
    hidden = ff_ref.shape[2]
    padded = feed_ref.shape[1] // 3
    feed = feed_ref[...].astype(single)
    ff_ref[0] = feed[:, :hidden]
    ff_ref[1] = feed[:, padded : padded + hidden]
    ffd_ref[...] = feed[:, 2 * padded : 2 * padded + hidden]


def assemble(where, shared, last, feed, branch, shapes):
    rows = last.shape[0]
    block = min(32, rows)

    def spec(shape):
        if len(shape) == 2:
            return pl.BlockSpec((block, shape[1]), lambda i: (i, 0))
        return pl.BlockSpec((shape[0], block, shape[2]), lambda i: (0, i, 0))

    arrays = [*shared, last, feed, branch]
    return pl.pallas_call(
        assemble_kernel,
        out_shape=tuple(jax.ShapeDtypeStruct(shape, single) for shape in shapes),
        grid=(rows // block,),
        in_specs=[pl.BlockSpec(memory_space=pltpu.SMEM)] + [spec(a.shape) for a in arrays],
        out_specs=[spec(shape) for shape in shapes],
        compiler_params=pltpu.CompilerParams(
            dimension_semantics=("arbitrary",), vmem_limit_bytes=VMEM_LIMIT
        ),
        name="assemble",
    )(where, *arrays)


WHOLE, SCALAR = "whole", "scalar"


def by_rows(width, lane_block=0):
    return ("rows", width, lane_block)


def pieces(width):
    return ("pieces", width)


def blocked_call(body, name, count, inputs, outputs, scratch, flops, block=STEP):
    steps = count // block
    per = max(steps // 4, 1)
    in_specs, arrays, moved, groups_in, extra = [], [], 0, [], []
    for array, kind in inputs:
        members = array if isinstance(array, (list, tuple)) else [array]
        groups_in.append(len(members))
        arrays += members
        moved += sum(a.size * a.dtype.itemsize for a in members)
        if kind == WHOLE:
            zeros = (0,) * array.ndim
            in_specs.append(
                pl.BlockSpec(
                    array.shape, lambda i, zeros=zeros: zeros, pipeline_mode=pl.Buffered(1)
                )
            )
        elif kind == SCALAR:
            in_specs.append(pl.BlockSpec(memory_space=pltpu.SMEM))
        elif kind[0] == "rows":
            in_specs.append(
                pl.BlockSpec((block, kind[1]), lambda i, lane=kind[2]: (i, lane))
            )
        else:
            for b in range(4):
                in_specs.append(
                    pl.BlockSpec(
                        (block, kind[1]), lambda i, b=b: (jnp.clip(i - b * per, 0, per - 1), 0)
                    )
                )
            extra.append(pltpu.VMEM((block, kind[1]), members[0].dtype))
    out_specs, shapes, groups_out = [], [], []
    for shape, dtype, kind in outputs:
        if kind == "parts":
            quarter = shape[0] // 4
            for rows in (quarter, quarter, 2 * quarter):
                shapes.append(jax.ShapeDtypeStruct((rows, shape[1]), dtype))
            spec = (block, shape[1])
            out_specs += [
                pl.BlockSpec(spec, lambda i: (jnp.clip(i, 0, per - 1), 0)),
                pl.BlockSpec(spec, lambda i: (jnp.clip(i - 2 * per, 0, per - 1), 0)),
                pl.BlockSpec(
                    spec,
                    lambda i: (
                        jnp.clip(i - per, 0, per - 1) + jnp.clip(i - 3 * per + 1, 0, per), 0
                    ),
                ),
            ]
            groups_out.append(3)
            extra.append(pltpu.VMEM(spec, dtype))
        else:
            groups_out.append(1)
            shapes.append(jax.ShapeDtypeStruct(shape, dtype))
            if kind == "rows":
                out_specs.append(pl.BlockSpec((block, shape[1]), lambda i: (i, 0)))
            else:
                zeros = (0,) * len(shape)
                out_specs.append(pl.BlockSpec(shape, lambda i, zeros=zeros: zeros))

    def wrapped(*refs):
        refs = list(refs)
        spare = refs[len(in_specs) + len(out_specs) + len(scratch) :]
        own_scratch = refs[len(in_specs) + len(out_specs) : len(refs) - len(spare)]
        quarter = pl.program_id(0) // per
        given, later, at, used = [], [], 0, 0
        for size in groups_in:
            if size == 1:
                given.append(refs[at])
            else:
                held = spare[used]
                used += 1
                for b in range(size):

                    @pl.when(quarter == b)
                    def _(held=held, source=refs[at + b]):
                        held[...] = source[...]

                given.append(held)
            at += size
        for size in groups_out:
            if size == 1:
                given.append(refs[at])
            else:
                given.append(spare[used])
                later.append((spare[used], refs[at : at + size]))
                used += 1
            at += size
        body(*given, *own_scratch)
        for held, targets in later:
            for b, target in ((0, targets[0]), (2, targets[1]), (1, targets[2]), (3, targets[2])):

                @pl.when(quarter == b)
                def _(held=held, target=target):
                    target[...] = held[...]

    results = pl.pallas_call(
        wrapped,
        out_shape=tuple(shapes),
        grid=(steps,),
        in_specs=in_specs,
        out_specs=out_specs,
        scratch_shapes=list(scratch) + extra,
        compiler_params=pltpu.CompilerParams(
            dimension_semantics=("arbitrary",), vmem_limit_bytes=VMEM_LIMIT
        ),
        cost_estimate=pl.CostEstimate(flops=flops, bytes_accessed=moved, transcendentals=0),
        name=name,
    )(*arrays)
    grouped, at = [], 0
    for size in groups_out:
        grouped.append(results[at] if size == 1 else results[at : at + size])
        at += size
    return grouped


def flip(array, bit):
    groups = lax.axis_size("head")
    return lax.ppermute(array, "head", [(i, i ^ bit) for i in range(groups)])


def gather_rows(array):
    far = flip(array, 2)
    near = flip(array, 1)
    return [array, near, far, flip(far, 1)]


def tie(*arrays):
    return lax.optimization_barrier(arrays)


def near_sum(parts):
    own, far, pair = parts
    size = own.shape[0]
    arrived = flip(pair, 1)
    return (
        own.astype(single) + arrived[:size].astype(single),
        low(far.astype(single) + arrived[size:].astype(single)),
    )


def far_sum(own, far):
    return own + flip(far, 2).astype(single)


def shifted_along(array, axis, by):
    length = lax.axis_size(axis)
    pairs = [(i, i + by) for i in range(length) if 0 <= i + by < length]
    return lax.ppermute(array, axis, pairs)


def seq_rows(flat):
    members = lax.axis_size("seq")
    return flat.reshape(members, flat.shape[0] // members, flat.shape[1])


def share_sum(parts):
    summed = low(jnp.sum(parts.astype(single), axis=0))
    return jnp.broadcast_to(summed[None], parts.shape)


def exchange(parts):
    return lax.all_to_all(parts, "seq", 0, 0)


def all_rows(parts):
    return parts.reshape(-1, parts.shape[-1])


def rms_scale(rows, gain):
    return rows * lax.rsqrt(jnp.mean(rows * rows, axis=-1, keepdims=True) + EPS) * gain


def rms_back(rows, gain, incoming):
    _, back = jax.vjp(lambda value: rms_scale(value, gain), rows)
    return back(incoming)[0]


def on_device(
    block_input,
    out_grad,
    lengths,
    doc_sets,
    norm1_gain,
    w_query,
    w_key,
    w_value,
    conv_query,
    conv_key,
    conv_value,
    w_decay_beta,
    decay_rate,
    decay_bias,
    w_gate_out,
    out_gain,
    w_out,
    norm2_gain,
    w_gate,
    w_up,
    w_down,
    adapt_down,
    adapt_up_qk,
    adapt_up_vg,
    adapt_up_ff,
    adapt_down_out,
    adapt_down_ffd,
    adapt_up_res,
):
    groups = lax.axis_size("head")
    members = lax.axis_size("seq")
    place = lax.axis_index("head")
    quarter, width = block_input.shape
    count = quarter * groups
    heads = decay_rate.shape[0]
    key_width = w_query.shape[1] // heads
    value_width = w_value.shape[1] // heads
    sets, rank = adapt_down.shape[1], adapt_down.shape[3]
    low_rank = sets * rank
    qk = heads * key_width
    device_start = lax.axis_index("seq") * count
    starts = jnp.sum(
        jnp.where(
            jnp.arange(lengths.shape[0])[None, :] < jnp.arange(lengths.shape[0])[:, None],
            lengths[None, :],
            0,
        ),
        axis=1,
    )
    order = jnp.arange(groups, dtype=jnp.int32) ^ place

    def tables(positions):
        reached = positions[:, None] >= starts[None, :]
        token_start = jnp.max(jnp.where(reached, starts[None, :], -1), axis=1)
        ended = positions[:, None] >= (starts + lengths)[None, :]
        token_set = jnp.sum(jnp.where(reached & ~ended, doc_sets[None, :], 0), axis=1)
        pair = jnp.stack([token_start - device_start, token_set], axis=1).astype(single)
        return jnp.pad(pair, ((0, 0), (0, 8 - pair.shape[1])))

    table = tables(
        (
            device_start + order[:, None] * quarter + jnp.arange(quarter, dtype=jnp.int32)[None, :]
        ).reshape(-1)
    )
    halo_table = tables(device_start + jnp.arange(-HALO, 0, dtype=jnp.int32))
    column_sets = jnp.broadcast_to(
        (jnp.arange(low_rank, dtype=jnp.int32) // rank).astype(single)[None, :], (8, low_rank)
    )

    down = adapt_down.transpose(0, 1, 3, 2).reshape(6 * low_rank, width)
    mixer_down, feed_down = down[: 4 * low_rank], down[4 * low_rank :]
    up_qk = adapt_up_qk.reshape(2, low_rank, -1)
    up_vg = adapt_up_vg.reshape(2, low_rank, -1)
    up_ff = adapt_up_ff.reshape(2, low_rank, -1)
    down_out = adapt_down_out.transpose(0, 2, 1).reshape(low_rank, -1)
    down_ffd = adapt_down_ffd.transpose(0, 2, 1).reshape(low_rank, -1)
    up_res = adapt_up_res.reshape(2, low_rank, width)
    conv = jnp.concatenate([conv_query, conv_key, conv_value], axis=1).astype(single)
    scalars = jnp.stack([decay_rate, decay_bias])
    where = place.reshape(1).astype(jnp.int32)
    down_mix = jnp.concatenate(
        [
            mixer_down,
            w_decay_beta.transpose(1, 2, 0).reshape(2 * heads, width),
            jnp.zeros((low_rank - 2 * heads, width), bfloat),
        ],
        axis=0,
    )
    gain = jnp.broadcast_to(out_gain[None, :], (8, value_width))
    hidden_width = w_down.shape[0]
    padded = -(-hidden_width // 256) * 256
    value_lanes = heads * value_width
    block_width = width // groups
    widen = lambda a: jnp.pad(a, [(0, 0)] * (a.ndim - 1) + [(0, padded - hidden_width)])
    up_ff_padded, down_ffd_padded = widen(up_ff), widen(down_ffd)

    input_float = block_input.astype(single)
    normed = low(rms_scale(input_float, norm1_gain))
    tail = normed[quarter - HALO :]
    halo = sum(
        lax.ppermute(
            tail,
            ("seq", "head"),
            [((s * groups) + groups - 1, (s + 1) * groups + h) for s in range(members - 1)],
        )
        for h in range(groups)
    )
    normed_all = gather_rows(normed)
    pre, gate_input, inner, columns, pre_halo = blocked_call(
        project_kernel,
        "project",
        count,
        [
            (normed_all, pieces(width)),
            (table, by_rows(8)),
            (halo, WHOLE),
            (halo_table, WHOLE),
            (column_sets, WHOLE),
            (down_mix, WHOLE),
            (w_query, WHOLE),
            (w_key, WHOLE),
            (w_value, WHOLE),
            (w_gate_out, WHOLE),
            (up_qk, WHOLE),
            (up_vg, WHOLE),
        ],
        [
            ((count, 2 * qk + value_lanes), bfloat, "rows"),
            ((count, value_lanes), single, "rows"),
            ((count, 4 * low_rank), bfloat, "rows"),
            ((count, 8), single, "rows"),
            ((HALO, 2 * qk + value_lanes), bfloat, "whole"),
        ],
        [pltpu.VMEM((width + low_rank, 2 * qk + 2 * value_lanes), bfloat)],
        count * 9_000_000,
    )
    out_grad_late, pre = tie(out_grad, pre)
    grad_near, grad_far = flip(out_grad_late, 1), flip(out_grad_late, 2)
    raw_local, mapped, *saved, sent, sent_state, sent_map = run_forward(
        where, pre, pre_halo, columns, conv, scalars, heads, key_width, value_width, quarter
    )

    hops = min(members - 1, -(-(DOC_MAX - 1) // count))
    got = [shifted_along(sent, "seq", hop) for hop in range(1, hops)]
    got.append(shifted_along(sent_state, "seq", hops))
    grad_near, grad_far, sent_map = tie(grad_near, grad_far, sent_map)
    grad_all = [out_grad, grad_near, grad_far, flip(grad_far, 1)]
    hidden_grad, du_down = blocked_call(
        feed_before_kernel,
        "feed_before",
        count,
        [
            (grad_all, pieces(width)),
            (table, by_rows(8)),
            (column_sets, WHOLE),
            (w_down, WHOLE),
            (down_ffd.T, WHOLE),
            (up_res[1], WHOLE),
        ],
        [((count, padded), single, "rows"), ((count, low_rank), bfloat, "rows")],
        [pltpu.VMEM((padded, width + low_rank), bfloat)],
        count * 6_000_000,
    )
    raw_local, hidden_grad = tie(raw_local, hidden_grad)

    sizes = dict(heads=heads, key_width=key_width, value_width=value_width)
    attention_part, mixed, u_out, entering = blocked_call(
        functools.partial(attend_kernel, hops=hops, **sizes),
        "attend",
        count,
        [
            (raw_local, by_rows(value_lanes)),
            (mapped, by_rows(qk)),
            (gate_input, by_rows(value_lanes)),
            (table, by_rows(8)),
            (gain, WHOLE),
            (column_sets, WHOLE),
            (w_out, WHOLE),
            (down_out, WHOLE),
            (up_res[0], WHOLE),
        ]
        + [(part, WHOLE) for part in got],
        [
            ((count, width), bfloat, "parts"),
            ((count, value_lanes), bfloat, "rows"),
            ((count, low_rank), bfloat, "rows"),
            ((heads, key_width, value_width), bfloat, "whole"),
        ],
        [pltpu.VMEM((value_lanes + low_rank, width), bfloat)],
        count * 5_000_000,
    )
    attention_own, attention_far = near_sum(attention_part)
    attention_far, sent_map = tie(attention_far, sent_map)
    maps_after = [shifted_along(sent_map, "seq", -hop) for hop in range(1, hops)]
    residual = input_float + far_sum(attention_own, attention_far)
    normed_mid = low(rms_scale(residual, norm2_gain))
    mid_all = gather_rows(normed_mid)
    corner_mid, *maps_after = tie(mid_all[3], *maps_after)
    mid_all = mid_all[:3] + [corner_mid]

    mid_part, hidden, ff_grad, u_ff, du_ff = blocked_call(
        feed_kernel,
        "feed",
        count,
        [
            (mid_all, pieces(width)),
            (hidden_grad, by_rows(padded)),
            (table, by_rows(8)),
            (column_sets, WHOLE),
            (feed_down, WHOLE),
            (w_gate.T, WHOLE),
            (w_up.T, WHOLE),
            (up_ff.transpose(0, 2, 1), WHOLE),
            (up_ff_padded, WHOLE),
        ],
        [
            ((count, width), bfloat, "parts"),
            ((count, padded), bfloat, "rows"),
            ((count, 2 * padded), bfloat, "rows"),
            ((count, 2 * low_rank), bfloat, "rows"),
            ((count, 2 * low_rank), bfloat, "rows"),
        ],
        [
            pltpu.VMEM((padded, width + low_rank), bfloat),
            pltpu.VMEM((padded, width + low_rank), bfloat),
            pltpu.VMEM((2 * padded + 2 * low_rank, width), bfloat),
        ],
        count * 15_000_000,
    )
    mid_own, mid_far = near_sum(mid_part)
    mid_far, hidden = tie(mid_far, hidden)
    mid_grad = far_sum(mid_own, mid_far)
    out_part, feed_own, feed_far, feed_pair, feed_owned = blocked_call(
        feed_after_kernel,
        "feed_after",
        count,
        [
            (mid_all, pieces(width)),
            (grad_all, pieces(width)),
            (hidden, by_rows(padded)),
            (ff_grad, by_rows(2 * padded)),
            (u_ff, by_rows(2 * low_rank)),
            (du_ff, by_rows(2 * low_rank)),
            (du_down, by_rows(low_rank)),
            (table, by_rows(8)),
            (column_sets, WHOLE),
            (where, SCALAR),
            (w_down, WHOLE),
            (down_ffd_padded, WHOLE),
            (up_res[1], WHOLE),
        ],
        [
            ((count, width), bfloat, "parts"),
            ((low_rank, 3 * block_width), bfloat, "whole"),
            ((low_rank, 3 * block_width), bfloat, "whole"),
            ((2 * low_rank, 3 * block_width), bfloat, "whole"),
            ((low_rank, 3 * padded), bfloat, "whole"),
        ],
        [
            pltpu.VMEM((padded + low_rank, width), bfloat),
            pltpu.VMEM((2 * low_rank, width), single),
            pltpu.VMEM((low_rank, width), single),
            pltpu.VMEM((low_rank, 3 * padded), single),
        ],
        count * 12_000_000,
    )
    residual_grad = out_grad.astype(single) + rms_back(residual, norm2_gain, mid_grad)
    out_own, out_far = near_sum(out_part)
    branch_low = low(residual_grad)
    branch_all = gather_rows(branch_low)
    feed_flat = jnp.concatenate(
        [low(far_sum(*near_sum((feed_own, feed_far, feed_pair)))), feed_owned], axis=1
    )
    corner_branch, feed_flat = tie(branch_all[3], feed_flat)
    branch_all = branch_all[:3] + [corner_branch]
    feed_parts = exchange(seq_rows(feed_flat))

    raw_grad, gate_grad, du_out, du_outgate, state_grad = blocked_call(
        functools.partial(branch_kernel, **sizes),
        "branch",
        count,
        [
            (branch_all, pieces(width)),
            (raw_local, by_rows(value_lanes)),
            (mapped, by_rows(qk)),
            (gate_input, by_rows(value_lanes)),
            (table, by_rows(8)),
            (entering, WHOLE),
            (gain, WHOLE),
            (column_sets, WHOLE),
            (w_out, WHOLE),
            (down_out.T, WHOLE),
            (up_res[0], WHOLE),
            (up_vg[1], WHOLE),
        ],
        [
            ((count, value_lanes), bfloat, "rows"),
            ((count, value_lanes), bfloat, "rows"),
            ((count, low_rank), bfloat, "rows"),
            ((count, low_rank), bfloat, "rows"),
            ((heads, key_width, value_width), bfloat, "whole"),
        ],
        [
            pltpu.VMEM((value_lanes, width + low_rank), bfloat),
            pltpu.VMEM((heads, key_width, value_width), single),
        ],
        count * 7_000_000,
    )
    state_got = [shifted_along(state_grad, "seq", -hop) for hop in range(1, hops + 1)]
    du_out, feed_parts = tie(du_out, feed_parts)
    mixer_down_late, branch_res_grad, branch_flat = blocked_call(
        branch_after_kernel,
        "branch_after",
        count,
        [
            (branch_all, pieces(width)),
            (mixed, by_rows(value_lanes)),
            (u_out, by_rows(low_rank)),
            (normed_all, pieces(width)),
            (inner, by_rows(low_rank, 3)),
            (du_out, by_rows(low_rank)),
            (du_outgate, by_rows(low_rank)),
            (gate_grad, by_rows(value_lanes)),
        ],
        [
            ((low_rank, width), single, "whole"),
            ((low_rank, width), single, "whole"),
            ((low_rank, 2 * value_lanes), bfloat, "whole"),
        ],
        [pltpu.VMEM((low_rank, 2 * value_lanes), single)],
        count * 20_000_000,
    )
    feed_lanes = feed_parts.shape[-1]
    both = jnp.concatenate([share_sum(feed_parts), seq_rows(branch_flat)], axis=2)
    raw_grad, both, out_far, *state_got = tie(raw_grad, both, out_far, *state_got)
    out_arrived = flip(out_far, 2)
    both = exchange(both)

    pre_grad, mix_grad, tail_grad, edge_grad = run_backward(
        where, pre, pre_halo, columns, conv, scalars, raw_grad, saved, entering, state_got,
        maps_after, heads, key_width, value_width, quarter,
    )
    arrived = shifted_along(edge_grad, "seq", -1)
    arrived, both, out_arrived = tie(arrived, both, out_arrived)
    result = residual + (out_own + out_arrived.astype(single))
    feed_total = all_rows(both[:, :, :feed_lanes])
    branch_parts = both[:, :, feed_lanes:]
    settled = [
        (pre_grad, by_rows(2 * qk + value_lanes)),
        (tail_grad, WHOLE),
        (arrived, WHOLE),
        (where, SCALAR),
    ]
    du_mix, last_own, last_far, last_pair, last_owned = blocked_call(
        settle_grads_kernel,
        "settle_grads",
        count,
        [
            settled[0],
            (normed_all, pieces(width)),
            (inner, by_rows(4 * low_rank)),
            (table, by_rows(8)),
            *settled[1:],
            (column_sets, WHOLE),
            (up_qk, WHOLE),
            (up_vg[0], WHOLE),
            (mixer_down_late, WHOLE),
            (branch_res_grad, WHOLE),
        ],
        [
            ((count, 3 * low_rank), bfloat, "rows"),
            ((low_rank, 5 * block_width), bfloat, "whole"),
            ((low_rank, 5 * block_width), bfloat, "whole"),
            ((2 * low_rank, 5 * block_width), bfloat, "whole"),
            ((low_rank, 2 * qk + value_lanes), bfloat, "whole"),
        ],
        [
            pltpu.VMEM((STEP, 2 * qk + value_lanes), bfloat),
            pltpu.VMEM((3 * low_rank, width), single),
            pltpu.VMEM((low_rank, 2 * qk + value_lanes), single),
        ],
        count * 4_000_000,
    )
    last_own, last_far = near_sum((last_own, last_far, last_pair))
    last_far, gate_grad = tie(last_far, gate_grad)
    (normed_part,) = blocked_call(
        settle_kernel,
        "settle",
        count,
        [
            settled[0],
            (gate_grad, by_rows(value_lanes)),
            (du_mix, by_rows(3 * low_rank)),
            (du_outgate, by_rows(low_rank)),
            (mix_grad, by_rows(8)),
            *settled[1:],
            (down_mix, WHOLE),
            (w_query, WHOLE),
            (w_key, WHOLE),
            (w_value, WHOLE),
            (w_gate_out, WHOLE),
        ],
        [((count, width), bfloat, "parts")],
        [
            pltpu.VMEM((STEP, 2 * qk + value_lanes), bfloat),
            pltpu.VMEM((width, 2 * qk + 2 * value_lanes), bfloat),
        ],
        count * 10_000_000,
    )
    last_flat = jnp.concatenate([low(far_sum(last_own, last_far)), last_owned], axis=1)
    last_lanes = last_flat.shape[1]
    both = exchange(jnp.concatenate([seq_rows(last_flat), share_sum(branch_parts)], axis=2))
    last_parts, branch_total = both[:, :, :last_lanes], all_rows(both[:, :, last_lanes:])
    normed_grad = far_sum(*near_sum(normed_part))
    input_grad = residual_grad + rms_back(input_float, norm1_gain, normed_grad)
    last_total = all_rows(exchange(share_sum(last_parts)))
    piece = jnp.concatenate(
        [last_total[:, : 5 * block_width], feed_total[:, : 3 * block_width]], axis=1
    )
    down_grad, qk_grad, vg_grad, ff_grads, out_grads, ffd_grads, res_grad = assemble(
        where,
        gather_rows(piece),
        last_total[:, 5 * block_width :],
        feed_total[:, 3 * block_width :],
        branch_total,
        [
            (6, low_rank, width),
            (2, low_rank, qk),
            (2, low_rank, value_lanes),
            (2, low_rank, hidden_width),
            (low_rank, value_lanes),
            (low_rank, hidden_width),
            (2, low_rank, width),
        ],
    )

    def as_down(rows):
        return rows.reshape(rows.shape[:-2] + (sets, rank, -1)).swapaxes(-1, -2)

    def as_up(rows):
        return rows.reshape(rows.shape[0], sets, rank, -1)

    return (
        low(result),
        input_grad,
        as_down(down_grad),
        as_up(qk_grad),
        as_up(vg_grad),
        as_up(ff_grads),
        as_down(out_grads),
        as_down(ffd_grads),
        as_up(res_grad),
    )


def solution(mesh):
    rows = P(("seq", "head"), None)
    lanes = P(None, "head")
    last = P(None, None, None, "head")
    middle = P(None, "head", None)
    in_specs = (
        rows, rows, P(), P(), P(), lanes, lanes, lanes, lanes, lanes, lanes,
        P(None, None, "head"), P("head"), P("head"), lanes, P(), P("head", None), P(), lanes,
        lanes, P("head", None), P(), last, last, last, middle, middle, P(),
    )
    out_specs = (rows, rows, P(), last, last, last, middle, middle, P())
    return jax.shard_map(
        on_device, mesh=mesh, in_specs=in_specs, out_specs=out_specs, check_vma=False
    )
```

```python
import functools

import jax
import jax.numpy as jnp
from jax import lax
from jax.experimental import pallas as pl
from jax.experimental.pallas import tpu as pltpu
from jax.sharding import PartitionSpec as P

CHUNK = 128
STEP = 256
HALO = 16
DOC_MAX = 4096
EPS = 1e-06
VMEM_LIMIT = 56 * 1024 * 1024
bfloat = jnp.bfloat16
single = jnp.float32


def contract(left, right, left_dim, right_dim):
    return lax.dot_general(
        left,
        right,
        (((left_dim,), (right_dim,)), ((), ())),
        preferred_element_type=single,
    )


def nn(left, right):
    return contract(left, right, 1, 0)


def nt(left, right):
    return contract(left, right, 1, 1)


def tn(left, right):
    return contract(left, right, 0, 0)


def low(array):
    return array.astype(bfloat)


def iotas():
    rows = lax.broadcasted_iota(jnp.int32, (CHUNK, CHUNK), 0)
    columns = lax.broadcasted_iota(jnp.int32, (CHUNK, CHUNK), 1)
    return rows, columns


def split_two(array):
    high = low(array)
    return high, low(array - high.astype(single))


def near_exact(left, right):
    left_high, left_low = split_two(left)
    right_high, right_low = split_two(right)
    return nn(
        jnp.concatenate([left_high, left_high, left_low], axis=1),
        jnp.concatenate([right_high, right_low, right_high], axis=0),
    )


def ones_product(ones, array):
    high = low(array)
    rest = array - high.astype(single)
    middle = low(rest)
    lowest = low(rest - middle.astype(single))
    return nn(
        jnp.concatenate([ones, ones, ones], axis=1),
        jnp.concatenate([high, middle, lowest], axis=0),
    )


def unit_lower_inverses(stricts, rows, columns):
    eye = (rows == columns).astype(single)
    differ = rows ^ columns
    block = 8
    inner = [jnp.where(differ < block, strict, 0.0) for strict in stricts]
    second = [near_exact(a, a) for a in inner]
    inverse = [near_exact(eye - a, eye + b) for a, b in zip(inner, second)]
    fourth = [near_exact(b, b) for b in second]
    inverse = [near_exact(a, eye + b) for a, b in zip(inverse, fourth)]
    while block < CHUNK:
        between = (differ >= block) & (differ < 2 * block)
        off = [jnp.where(between, strict, 0.0) for strict in stricts]
        part = [near_exact(a, b) for a, b in zip(off, inverse)]
        inverse = [a - near_exact(a, b) for a, b in zip(inverse, part)]
        block = 2 * block
    return inverse


def softplus(value):
    return jnp.maximum(value, 0.0) + jnp.log(1.0 + jnp.exp(-jnp.abs(value)))


def sigmoid(value):
    return 1.0 / (1.0 + jnp.exp(-value))


def gates(decay, start, rows, columns):
    lower_ones = low((rows >= columns).astype(single))
    total = ones_product(lower_ones, jnp.broadcast_to(decay, (CHUNK, CHUNK)))
    linked = (rows >= columns) & (columns >= start)
    within = jnp.where(linked, jnp.exp(jnp.where(linked, total - total.T, 0.0)), 0.0)
    running = total[:, :1]
    carried = jnp.where(start < 0, jnp.exp(running), 0.0)
    last = running[CHUNK - 1 : CHUNK]
    ending = jnp.where(
        rows[:, :1] >= start[CHUNK - 1 : CHUNK], jnp.exp(jnp.minimum(last - running, 0.0)), 0.0
    )
    return within, carried, ending


def convolved(window, starts, weights, base):
    positions = base + lax.broadcasted_iota(jnp.int32, (STEP, 1), 0)
    taps = weights.shape[0]
    total = None
    for tap in range(taps):
        back = taps - 1 - tap
        term = window[HALO - back : HALO - back + STEP, :] * weights[tap : tap + 1, :]
        if back:
            term = jnp.where(positions - back >= starts, term, 0.0)
        total = term if total is None else total + term
    return total


def head_scales(rows, width):
    return lax.rsqrt(jnp.sum(rows * rows, axis=-1, keepdims=True) + EPS)


def forward_kernel(
    place,
    rows_ref,
    halo_ref,
    column_ref,
    weight_ref,
    scalar_ref,
    out_ref,
    map_ref,
    written_ref,
    state_ref,
    inverse_ref,
    end_ref,
    sent_ref,
    sent_state_ref,
    window,
    state,
    *,
    heads,
    key_width,
    value_width,
):
    step = pl.program_id(0)
    wide = value_width + key_width
    base = step * STEP
    rows, columns = iotas()

    @pl.when(step == 0)
    def _():
        window[0:HALO, :] = halo_ref[...].astype(single)
        for h in range(heads):
            state[h, :, :value_width] = jnp.zeros((key_width, value_width), single)
            state[h, :, value_width:] = (rows == columns).astype(single)

    @pl.when(step > 0)
    def _():
        window[0:HALO, :] = window[STEP : STEP + HALO, :]

    window[HALO:, :] = rows_ref[...].astype(single)
    info = column_ref[...]
    starts = info[:, 2 * heads : 2 * heads + 1].astype(jnp.int32)
    before = convolved(window, starts, weight_ref[...], base)
    active = before * sigmoid(before)
    qk_lanes = heads * key_width
    chunks = STEP // CHUNK
    local, stricts = [], []
    for c in range(chunks):
        span = slice(c * CHUNK, (c + 1) * CHUNK)
        for h in range(heads):
            query = active[span, h * key_width : (h + 1) * key_width]
            key = active[span, qk_lanes + h * key_width : qk_lanes + (h + 1) * key_width]
            value = active[
                span, 2 * qk_lanes + h * value_width : 2 * qk_lanes + (h + 1) * value_width
            ]
            query = query * (head_scales(query, key_width) * key_width ** (-0.5))
            key = key * head_scales(key, key_width)
            beta = sigmoid(info[span, h : h + 1])
            decay = -scalar_ref[0, h] * softplus(
                info[span, heads + h : heads + h + 1] + scalar_ref[1, h]
            )
            within, carried, ending = gates(
                decay, starts[span] - (base + c * CHUNK), rows, columns
            )
            query, key = low(query), low(key)
            strict = jnp.where(rows > columns, within * nt(key, key), 0.0) * beta
            mixed = low(within * nt(query, key))
            stricts.append(strict)
            local.append((query, key, value, beta, carried, ending, mixed))
    inverses = [low(a) for a in unit_lower_inverses(stricts, rows, columns)]
    each = range(heads)
    now = [state[h] for h in each]
    for c in range(chunks):
        span = slice(c * CHUNK, (c + 1) * CHUNK)
        here = [local[c * heads + h] for h in each]
        inverse = [inverses[c * heads + h] for h in each]
        now_low = [low(a) for a in now]
        read = [nn(here[h][1], now_low[h]) for h in each]
        asked = [nn(here[h][0], now_low[h]) for h in each]
        target = []
        for h in each:
            query, key, value, beta, carried, ending, mixed = here[h]
            gap = -(carried * beta) * read[h]
            target.append(
                jnp.concatenate(
                    [beta * value + gap[:, :value_width], gap[:, value_width:]], axis=1
                )
            )
        written = [nn(inverse[h], low(target[h])) for h in each]
        added = [tn(here[h][1], low(here[h][5] * written[h])) for h in each]
        inner = [nn(here[h][6], low(written[h])) for h in each]
        for h in each:
            carried = here[h][4]
            inverse_ref[span, h * CHUNK : (h + 1) * CHUNK] = inverse[h]
            state_ref[c, h] = now_low[h]
            written_ref[span, h * wide : (h + 1) * wide] = low(written[h])
            output = carried * asked[h] + inner[h]
            out_ref[span, h * value_width : (h + 1) * value_width] = output[:, :value_width]
            map_ref[span, h * key_width : (h + 1) * key_width] = low(output[:, value_width:])
        now = [here[h][4][CHUNK - 1 : CHUNK] * now[h] + added[h] for h in each]
    for h in each:
        state[h] = now[h]

    @pl.when(step == pl.num_programs(0) - 1)
    def _():
        final = state[...]
        end_ref[...] = final
        sent_ref[...] = low(final)
        sent_state_ref[...] = low(final[:, :, :value_width])


def backward_kernel(
    place,
    rows_ref,
    before_ref,
    halo_ref,
    column_ref,
    weight_ref,
    scalar_ref,
    grad_ref,
    written_ref,
    state_ref,
    inverse_ref,
    end_ref,
    entering_ref,
    *rest,
    hops,
    heads,
    key_width,
    value_width,
):
    got_refs, rest = rest[:hops], rest[hops:]
    out_ref, mix_ref, tail_ref, edge_ref, window, shifted, shifted_start, cotangent, ahead = rest
    step = pl.program_id(0)
    steps = pl.num_programs(0)
    wide = value_width + key_width
    base = (steps - 1 - step) * STEP
    rows, columns = iotas()
    qk_lanes = heads * key_width
    lanes = window.shape[1]
    taps = weight_ref.shape[0]

    @pl.when(step == 0)
    def _():
        shifted[STEP : STEP + 8, :] = jnp.zeros((8, lanes), single)
        shifted_start[STEP : STEP + 8, :] = jnp.zeros((8, 1), jnp.int32)
        for h in range(heads):
            passed = got_refs[0][h].astype(single)
            for hop in range(1, hops):
                passed = passed + got_refs[hop][h].astype(single)
            cotangent[h] = passed
            ahead[h] = end_ref[h, :, :value_width] + nn(
                low(end_ref[h, :, value_width:]), low(entering_ref[h])
            )

    @pl.when(step > 0)
    def _():
        shifted[STEP : STEP + 8, :] = shifted[0:8, :]
        shifted_start[STEP : STEP + 8, :] = shifted_start[0:8, :]

    window[0:HALO, :] = jnp.where(
        step == steps - 1, halo_ref[...].astype(single), before_ref[...].astype(single)
    )
    window[HALO:, :] = rows_ref[...].astype(single)
    info = column_ref[...]
    starts = info[:, 2 * heads : 2 * heads + 1].astype(jnp.int32)
    positions = base + lax.broadcasted_iota(jnp.int32, (STEP, 1), 0)
    before = convolved(window, starts, weight_ref[...], base)
    gate = sigmoid(before)
    active = before * gate
    slope = gate * (1.0 + before * (1.0 - gate))
    upper_ones = low((rows <= columns).astype(single))
    last_row = rows[:, :1] == CHUNK - 1
    chunks = STEP // CHUNK
    each = range(heads)
    items = [(c, h) for c in range(chunks) for h in each]
    spans = {item: slice(item[0] * CHUNK, (item[0] + 1) * CHUNK) for item in items}
    entering = [low(entering_ref[h]) for h in each]
    root = key_width ** (-0.5)

    def per(function):
        return {item: function(*item) for item in items}

    def q_lanes(h):
        return slice(h * key_width, (h + 1) * key_width)

    def k_lanes(h):
        return slice(qk_lanes + h * key_width, qk_lanes + (h + 1) * key_width)

    def v_lanes(h):
        return slice(2 * qk_lanes + h * value_width, 2 * qk_lanes + (h + 1) * value_width)

    def kept(c, h, part):
        return written_ref[spans[c, h], h * wide : (h + 1) * wide][:, part]

    values, maps = slice(0, value_width), slice(value_width, wide)
    query_raw = per(lambda c, h: active[spans[c, h], q_lanes(h)])
    key_raw = per(lambda c, h: active[spans[c, h], k_lanes(h)])
    query_scale = per(lambda c, h: head_scales(query_raw[c, h], key_width))
    key_scale = per(lambda c, h: head_scales(key_raw[c, h], key_width))
    query = per(lambda c, h: query_raw[c, h] * (query_scale[c, h] * root))
    key = per(lambda c, h: key_raw[c, h] * key_scale[c, h])
    query_low = per(lambda c, h: low(query[c, h]))
    key_low = per(lambda c, h: low(key[c, h]))
    beta = per(lambda c, h: sigmoid(info[spans[c, h], h : h + 1]))
    raw = per(lambda c, h: info[spans[c, h], heads + h : heads + h + 1] + scalar_ref[1, h])
    gated = per(
        lambda c, h: gates(
            -scalar_ref[0, h] * softplus(raw[c, h]),
            starts[spans[c, h]] - (base + c * CHUNK),
            rows,
            columns,
        )
    )
    within = per(lambda c, h: gated[c, h][0])
    carried = per(lambda c, h: gated[c, h][1])
    ending = per(lambda c, h: gated[c, h][2])
    mixed = per(lambda c, h: low(within[c, h] * nt(query_low[c, h], key_low[c, h])))
    written = per(
        lambda c, h: kept(c, h, values).astype(single) + nn(kept(c, h, maps), entering[h])
    )
    start_state = per(
        lambda c, h: state_ref[c, h][:, values].astype(single)
        + nn(state_ref[c, h][:, maps], entering[h])
    )
    written_low = per(lambda c, h: low(written[c, h]))
    start_low = per(lambda c, h: low(start_state[c, h]))
    grad = per(lambda c, h: grad_ref[spans[c, h], h * value_width : (h + 1) * value_width])
    grad_low = grad
    carried_grad = per(lambda c, h: low(carried[c, h] * grad[c, h].astype(single)))
    from_output = per(lambda c, h: tn(mixed[c, h], grad_low[c, h]))
    state_part = per(lambda c, h: tn(query_low[c, h], carried_grad[c, h]))
    mixed_grad = per(lambda c, h: low(within[c, h] * nt(grad_low[c, h], written_low[c, h])))
    query_grad = per(
        lambda c, h: nt(carried_grad[c, h], start_low[c, h]) + nn(mixed_grad[c, h], key_low[c, h])
    )
    key_write = per(lambda c, h: tn(mixed_grad[c, h], query_low[c, h]))
    later, later_low, solved, value_grad, read_grad = {}, {}, {}, {}, {}
    now = [cotangent[h] for h in each]
    for c in reversed(range(chunks)):
        for h in each:
            later[c, h], later_low[c, h] = now[h], low(now[h])
        from_state = [nn(key_low[c, h], later_low[c, h]) for h in each]
        written_grad = [low(from_output[c, h] + ending[c, h] * from_state[h]) for h in each]
        for h in each:
            inverse = inverse_ref[spans[c, h], h * CHUNK : (h + 1) * CHUNK]
            solved[c, h] = tn(inverse, written_grad[h])
        for h in each:
            value_grad[c, h] = beta[c, h] * solved[c, h]
            read_grad[c, h] = low(-carried[c, h] * value_grad[c, h])
        now = [
            carried[c, h][CHUNK - 1 : CHUNK] * now[h]
            + state_part[c, h]
            + tn(key_low[c, h], read_grad[c, h])
            for h in each
        ]
    following = {
        (c, h): start_state[c + 1, h] if c + 1 < chunks else ahead[h] for c, h in items
    }
    at_end = per(lambda c, h: jnp.sum(later[c, h] * following[c, h], keepdims=True))
    for h in each:
        cotangent[h] = now[h]
        ahead[h] = start_state[0, h]
    strict_grad = per(
        lambda c, h: low(
            jnp.where(
                rows > columns, -within[c, h] * nt(low(value_grad[c, h]), written_low[c, h]), 0.0
            )
        )
    )
    key_read = per(
        lambda c, h: nt(read_grad[c, h], start_low[c, h]) + nn(strict_grad[c, h], key_low[c, h])
    )
    key_write = per(
        lambda c, h: key_write[c, h]
        + tn(strict_grad[c, h], key_low[c, h])
        + nt(low(ending[c, h] * written[c, h]), later_low[c, h])
    )
    query_dot = per(
        lambda c, h: jnp.sum(query[c, h] * query_grad[c, h], axis=-1, keepdims=True)
    )
    running_grad = per(
        lambda c, h: query_dot[c, h]
        + jnp.sum(key[c, h] * (key_read[c, h] - key_write[c, h]), axis=-1, keepdims=True)
        + jnp.where(last_row, at_end[c, h], 0.0)
    )
    decay_sum = per(
        lambda c, h: ones_product(
            upper_ones, jnp.broadcast_to(running_grad[c, h], (CHUNK, CHUNK))
        )[:, :1]
    )
    decay_grad = per(
        lambda c, h: jnp.where(
            positions[spans[c, h]] == starts[spans[c, h]],
            0.0,
            -scalar_ref[0, h] * sigmoid(raw[c, h]) * decay_sum[c, h],
        )
    )
    beta_grad = per(
        lambda c, h: jnp.sum(solved[c, h] * written[c, h], axis=-1, keepdims=True)
        * sigmoid(-info[spans[c, h], h : h + 1])
    )
    for c, h in items:
        span = spans[c, h]
        key_grad = key_read[c, h] + key_write[c, h]
        key_dot = jnp.sum(key[c, h] * key_grad, axis=-1, keepdims=True)
        query_active = (query_scale[c, h] * root) * query_grad[c, h] - query_raw[c, h] * (
            query_scale[c, h] * query_scale[c, h] * query_dot[c, h]
        )
        key_active = key_scale[c, h] * (key_grad - key[c, h] * key_dot)
        shifted[span, q_lanes(h)] = query_active * slope[span, q_lanes(h)]
        shifted[span, k_lanes(h)] = key_active * slope[span, k_lanes(h)]
        shifted[span, v_lanes(h)] = value_grad[c, h] * slope[span, v_lanes(h)]
    for c in range(chunks):
        mix_ref[c * CHUNK : (c + 1) * CHUNK, :] = jnp.concatenate(
            [beta_grad[c, h] for h in each]
            + [decay_grad[c, h] for h in each]
            + [jnp.zeros((CHUNK, mix_ref.shape[1] - 2 * heads), single)],
            axis=1,
        )
    shifted_start[0:STEP, :] = starts
    total = None
    for tap in range(taps):
        back = taps - 1 - tap
        term = shifted[back : back + STEP, :] * weight_ref[tap : tap + 1, :]
        if back:
            term = jnp.where(positions >= shifted_start[back : back + STEP, :], term, 0.0)
        total = term if total is None else total + term
    out_ref[...] = low(total)

    @pl.when(step == 0)
    def _():
        tail_ref[...] = total[STEP - HALO :, :]

    @pl.when(step == steps - 1)
    def _():
        window[0:8, :] = jnp.zeros((8, lanes), single)
        window[8:16, :] = shifted[0:8, :]
        early = lax.broadcasted_iota(jnp.int32, (8, 1), 0) - 8
        collected = jnp.zeros((8, lanes), single)
        for tap in range(taps - 1):
            back = taps - 1 - tap
            reader = early + back
            reader_start = jnp.zeros((8, 1), jnp.int32)
            for t in range(back):
                reader_start = jnp.where(reader == t, shifted_start[t : t + 1, :], reader_start)
            term = window[back : back + 8, :] * weight_ref[tap : tap + 1, :]
            collected = collected + jnp.where(
                (reader >= 0) & (early >= reader_start), term, 0.0
            )
        edge_ref[0:8, :] = jnp.zeros((8, lanes), single)
        edge_ref[8:16, :] = collected


def block_place(step, place, per_quarter):
    return ((step // per_quarter) ^ place[0]) * per_quarter + step % per_quarter


def run_forward(place, rows, halo, columns, weights, scalars, heads, key_width, value_width, quarter):
    count, lanes = columns.shape[0], rows.shape[1]
    steps, per_quarter = count // STEP, quarter // STEP
    wide = value_width + key_width
    chunks = STEP // CHUNK
    at = lambda i, place: (block_place(i, place, per_quarter), 0)
    fixed = lambda i, place: (0, 0)
    body = functools.partial(
        forward_kernel, heads=heads, key_width=key_width, value_width=value_width
    )
    shapes = (
        jax.ShapeDtypeStruct((count, heads * value_width), single),
        jax.ShapeDtypeStruct((count, heads * key_width), bfloat),
        jax.ShapeDtypeStruct((count, heads * wide), bfloat),
        jax.ShapeDtypeStruct((count // CHUNK, heads, key_width, wide), bfloat),
        jax.ShapeDtypeStruct((count, heads * CHUNK), bfloat),
        jax.ShapeDtypeStruct((heads, key_width, wide), single),
        jax.ShapeDtypeStruct((heads, key_width, wide), bfloat),
        jax.ShapeDtypeStruct((heads, key_width, value_width), bfloat),
    )
    return pl.pallas_call(
        body,
        out_shape=shapes,
        grid_spec=pltpu.PrefetchScalarGridSpec(
            num_scalar_prefetch=1,
            grid=(steps,),
            in_specs=[
                pl.BlockSpec((STEP, lanes), at),
                pl.BlockSpec((HALO, lanes), lambda i, place: (0, 0)),
                pl.BlockSpec((STEP, columns.shape[1]), at),
                pl.BlockSpec(weights.shape, fixed),
                pl.BlockSpec(memory_space=pltpu.SMEM),
            ],
            out_specs=[
                pl.BlockSpec((STEP, heads * value_width), at),
                pl.BlockSpec((STEP, heads * key_width), at),
                pl.BlockSpec((STEP, heads * wide), at),
                pl.BlockSpec((chunks, heads, key_width, wide), lambda i, place: (i, 0, 0, 0)),
                pl.BlockSpec((STEP, heads * CHUNK), at),
                pl.BlockSpec((heads, key_width, wide), lambda i, place: (0, 0, 0)),
                pl.BlockSpec((heads, key_width, wide), lambda i, place: (0, 0, 0)),
                pl.BlockSpec((heads, key_width, value_width), lambda i, place: (0, 0, 0)),
            ],
            scratch_shapes=[
                pltpu.VMEM((STEP + HALO, lanes), single),
                pltpu.VMEM((heads, key_width, wide), single),
            ],
        ),
        compiler_params=pltpu.CompilerParams(
            dimension_semantics=("arbitrary",), vmem_limit_bytes=VMEM_LIMIT
        ),
        cost_estimate=pl.CostEstimate(
            flops=count * 2_000_000, bytes_accessed=count * 10_000, transcendentals=count * 2000
        ),
        name="delta_forward",
    )(place, rows, halo, columns, weights, scalars)


def run_backward(
    place, rows, halo, columns, weights, scalars, grad, saved, entering, got, heads,
    key_width, value_width, quarter,
):
    written, states, inverses, end = saved
    count, lanes = columns.shape[0], rows.shape[1]
    steps, per_quarter = count // STEP, quarter // STEP
    wide = value_width + key_width
    chunks = STEP // CHUNK

    def at(i, place):
        return (block_place(steps - 1 - i, place, per_quarter), 0)

    def halo_at(i, place):
        here = steps - 1 - i
        inner = block_place(jnp.maximum(here - 1, 0), place, per_quarter)
        ratio = STEP // HALO
        return (inner * ratio + ratio - 1, 0)

    fixed = lambda i, place: (0, 0)
    whole = lambda i, place: (0, 0, 0)
    body = functools.partial(
        backward_kernel,
        hops=len(got),
        heads=heads,
        key_width=key_width,
        value_width=value_width,
    )
    shapes = (
        jax.ShapeDtypeStruct((count, lanes), bfloat),
        jax.ShapeDtypeStruct((count, columns.shape[1]), single),
        jax.ShapeDtypeStruct((HALO, lanes), single),
        jax.ShapeDtypeStruct((HALO, lanes), single),
    )
    return pl.pallas_call(
        body,
        out_shape=shapes,
        grid_spec=pltpu.PrefetchScalarGridSpec(
            num_scalar_prefetch=1,
            grid=(steps,),
            in_specs=[
                pl.BlockSpec((STEP, lanes), at),
                pl.BlockSpec((HALO, lanes), halo_at),
                pl.BlockSpec((HALO, lanes), fixed),
                pl.BlockSpec((STEP, columns.shape[1]), at),
                pl.BlockSpec(weights.shape, fixed),
                pl.BlockSpec(memory_space=pltpu.SMEM),
                pl.BlockSpec((STEP, heads * value_width), at),
                pl.BlockSpec((STEP, heads * wide), at),
                pl.BlockSpec(
                    (chunks, heads, key_width, wide), lambda i, place: (steps - 1 - i, 0, 0, 0)
                ),
                pl.BlockSpec((STEP, heads * CHUNK), at),
                pl.BlockSpec(end.shape, whole),
                pl.BlockSpec(entering.shape, whole),
            ]
            + [pl.BlockSpec(part.shape, whole) for part in got],
            out_specs=[
                pl.BlockSpec((STEP, lanes), at),
                pl.BlockSpec((STEP, columns.shape[1]), at),
                pl.BlockSpec((HALO, lanes), fixed),
                pl.BlockSpec((HALO, lanes), fixed),
            ],
            scratch_shapes=[
                pltpu.VMEM((STEP + HALO, lanes), single),
                pltpu.VMEM((STEP + 8, lanes), single),
                pltpu.VMEM((STEP + 8, 1), jnp.int32),
                pltpu.VMEM((heads, key_width, value_width), single),
                pltpu.VMEM((heads, key_width, value_width), single),
            ],
        ),
        compiler_params=pltpu.CompilerParams(
            dimension_semantics=("arbitrary",), vmem_limit_bytes=VMEM_LIMIT
        ),
        cost_estimate=pl.CostEstimate(
            flops=count * 3_000_000, bytes_accessed=count * 12_000, transcendentals=count * 3000
        ),
        name="delta_backward",
    )(
        place, rows, rows, halo, columns, weights, scalars, grad, written, states, inverses, end,
        entering, *got,
    )


def chosen_columns(table, column_sets):
    return column_sets[0:1, :] == table[:, 1:2]


def masked(product, chosen):
    return low(jnp.where(chosen, product, 0.0))


def silu_parts(value):
    logistic = sigmoid(value)
    return logistic, value * logistic


def accumulate(ref, value, first):
    if first is True:
        ref[...] = value
    else:
        ref[...] = jnp.where(first, value, ref[...] + value)


def emit_blocks(parts, place, own_ref, far_ref, pair_ref):
    for k, part in enumerate(parts):
        rows, size = part.shape[0], part.shape[1] // 4
        lanes = slice(k * size, (k + 1) * size)
        for relative, target, row in (
            (0, own_ref, 0), (2, far_ref, 0), (1, pair_ref, 0), (3, pair_ref, rows)
        ):
            start = pl.multiple_of((place ^ relative) * size, 128)
            target[row : row + rows, lanes] = low(part[:, pl.ds(start, size)])


def at_end(fill):
    pl.when(pl.program_id(0) == pl.num_programs(0) - 1)(fill)


def at_start(fill):
    pl.when(pl.program_id(0) == 0)(fill)


def project_kernel(
    rows_ref, table_ref, halo_ref, halo_table_ref, sets_ref, down_mix_ref, wq_ref, wk_ref, wv_ref,
    wg_ref, up_qk_ref, up_vg_ref,
    pre_ref, gate_ref, inner_ref, column_ref, pre_halo_ref,
    joined,
):
    low_rank = sets_ref.shape[1]
    width, q_width = wq_ref.shape
    v_width = wv_ref.shape[1]
    bounds = [0, q_width, 2 * q_width, 2 * q_width + v_width, 2 * q_width + 2 * v_width]

    @at_start
    def _():
        weights = (wq_ref, wk_ref, wv_ref, wg_ref)
        ups = (up_qk_ref[0], up_qk_ref[1], up_vg_ref[0], up_vg_ref[1])
        for p in range(4):
            joined[:width, bounds[p] : bounds[p + 1]] = weights[p][...]
            joined[width:, bounds[p] : bounds[p + 1]] = ups[p]

    def projections(rows, table, store, last):
        chosen = chosen_columns(table, sets_ref[...])
        product = nt(rows, down_mix_ref[...])
        inner = [
            masked(product[:, p * low_rank : (p + 1) * low_rank], chosen) for p in range(last)
        ]
        outputs = [
            nn(
                jnp.concatenate([rows, inner[p]], axis=1), joined[:, bounds[p] : bounds[p + 1]]
            )
            for p in range(last)
        ]
        for p in range(3):
            store[:, bounds[p] : bounds[p + 1]] = low(outputs[p])
        return product, inner, outputs

    @at_start
    def _():
        projections(halo_ref[...], halo_table_ref[...], pre_halo_ref, 3)

    table = table_ref[...]
    product, inner, outputs = projections(rows_ref[...], table, pre_ref, 4)
    for p in range(4):
        inner_ref[:, p * low_rank : (p + 1) * low_rank] = inner[p]
    gate_ref[...] = outputs[3]
    column_ref[...] = jnp.concatenate(
        [product[:, 4 * low_rank : 4 * low_rank + 4], table[:, :4]], axis=1
    )


def head_outputs(raw_ref, map_ref, entering_ref, heads, key_width, value_width):
    outputs = []
    for h in range(heads):
        outputs.append(
            raw_ref[:, h * value_width : (h + 1) * value_width]
            + nn(map_ref[:, h * key_width : (h + 1) * key_width], entering_ref[h])
        )
    return outputs


def attend_kernel(
    raw_ref, map_ref, gate_ref, table_ref, gain_ref, sets_ref, wo_ref, down_ref, up_ref, *rest,
    heads, key_width, value_width, hops,
):
    got_refs, rest = rest[:hops], rest[hops:]
    part_ref, z_ref, inner_ref, entering_ref, joined = rest
    value_lanes = wo_ref.shape[0]

    @at_start
    def _():
        joined[:value_lanes, :] = wo_ref[...]
        joined[value_lanes:, :] = up_ref[...]
        for h in range(heads):
            state = got_refs[hops - 1][h].astype(single)
            for hop in range(hops - 1, 0, -1):
                got = got_refs[hop - 1][h]
                state = got[:, :value_width].astype(single) + nn(got[:, value_width:], low(state))
            entering_ref[h] = low(state)

    chosen = chosen_columns(table_ref[...], sets_ref[...])
    outputs = head_outputs(raw_ref, map_ref, entering_ref, heads, key_width, value_width)
    parts = []
    for h, output in enumerate(outputs):
        lanes = slice(h * value_width, (h + 1) * value_width)
        scale = lax.rsqrt(jnp.mean(output * output, axis=-1, keepdims=True) + EPS)
        _, gate = silu_parts(gate_ref[:, lanes])
        parts.append(low(output * scale * gain_ref[0:1, :] * gate))
    z = jnp.concatenate(parts, axis=1)
    z_ref[...] = z
    inner = masked(nt(z, down_ref[...]), chosen)
    inner_ref[...] = inner
    part_ref[...] = low(nn(jnp.concatenate([z, inner], axis=1), joined[...]))


def feed_before_kernel(
    grad_ref, table_ref, sets_ref, wd_ref, down_ffd_t_ref, up_ref, hidden_grad_ref, du_ref, joined
):
    hidden, width = wd_ref.shape

    @at_start
    def _():
        joined[:hidden, :width] = wd_ref[...]
        joined[:hidden, width:] = down_ffd_t_ref[...]
        joined[hidden:, :] = jnp.zeros((joined.shape[0] - hidden, joined.shape[1]), bfloat)

    grad = grad_ref[...]
    du_down = masked(nt(grad, up_ref[...]), chosen_columns(table_ref[...], sets_ref[...]))
    du_ref[...] = du_down
    hidden_grad_ref[...] = nt(jnp.concatenate([grad, du_down], axis=1), joined[...])


def feed_kernel(
    rows_ref, hidden_grad_ref, table_ref, sets_ref, down_ref, wg_ref, wu_ref, up_t_ref, up_ref,
    back_ref, hidden_ref, ff_grad_ref, inner_ref, du_ref,
    joined_gate, joined_up, joined_back,
):
    low_rank = sets_ref.shape[1]
    hidden, width = wg_ref.shape
    padded = joined_gate.shape[0]

    @at_start
    def _():
        for p, (joined, weight) in enumerate(((joined_gate, wg_ref), (joined_up, wu_ref))):
            joined[:hidden, :width] = weight[...]
            joined[:hidden, width:] = up_t_ref[p]
            joined[hidden:, :] = jnp.zeros((padded - hidden, joined.shape[1]), bfloat)
            joined_back[p * padded : p * padded + hidden, :] = weight[...]
            joined_back[p * padded + hidden : (p + 1) * padded, :] = jnp.zeros(
                (padded - hidden, width), bfloat
            )
        joined_back[2 * padded :, :] = down_ref[...]

    chosen = chosen_columns(table_ref[...], sets_ref[...])
    both = jnp.concatenate([chosen, chosen], axis=1)
    rows = rows_ref[...]
    inner = masked(nt(rows, down_ref[...]), both)
    inner_ref[...] = inner
    gate = nt(jnp.concatenate([rows, inner[:, :low_rank]], axis=1), joined_gate[...])
    up = nt(jnp.concatenate([rows, inner[:, low_rank:]], axis=1), joined_up[...])
    logistic, active = silu_parts(gate)
    hidden_ref[...] = low(active * up)
    hidden_grad = hidden_grad_ref[...]
    gate_grad = low(hidden_grad * up * logistic * (1.0 + gate * (1.0 - logistic)))
    up_grad = low(hidden_grad * active)
    du_gate = masked(nt(gate_grad, up_ref[0]), chosen)
    du_up = masked(nt(up_grad, up_ref[1]), chosen)
    du_ref[:, :low_rank] = du_gate
    du_ref[:, low_rank:] = du_up
    ff_grad_ref[:, :padded] = gate_grad
    ff_grad_ref[:, padded:] = up_grad
    back_ref[...] = low(
        nn(jnp.concatenate([gate_grad, up_grad, du_gate, du_up], axis=1), joined_back[...])
    )


def feed_after_kernel(
    rows_ref, grad_ref, hidden_ref, ff_grad_ref, inner_ref, du_ref, du_down_ref, table_ref,
    sets_ref, place_ref, wd_ref, down_ffd_ref, up_ref,
    out_ref, own_ref, far_ref, pair_ref, flat_ref,
    joined, down_sum, res_sum, flat_sum,
):
    first = pl.program_id(0) == 0
    low_rank = sets_ref.shape[1]
    width_hidden = wd_ref.shape[0]
    padded = down_ffd_ref.shape[1]

    @at_start
    def _():
        joined[:width_hidden, :] = wd_ref[...]
        joined[width_hidden:padded, :] = jnp.zeros(
            (padded - width_hidden, joined.shape[1]), bfloat
        )
        joined[padded:, :] = up_ref[...]

    hidden = hidden_ref[...]
    inner = inner_ref[...]
    u_down = masked(
        nt(hidden, down_ffd_ref[...]), chosen_columns(table_ref[...], sets_ref[...])
    )
    out_ref[...] = low(nn(jnp.concatenate([hidden, u_down], axis=1), joined[...]))
    accumulate(down_sum, tn(du_ref[...], rows_ref[...]), first)
    accumulate(res_sum, tn(u_down, grad_ref[...]), first)
    for k, grown in enumerate(
        (
            tn(inner[:, :low_rank], ff_grad_ref[:, :padded]),
            tn(inner[:, low_rank:], ff_grad_ref[:, padded:]),
            tn(du_down_ref[...], hidden),
        )
    ):
        accumulate(flat_sum.at[:, k * padded : (k + 1) * padded], grown, first)

    @at_end
    def _():
        flat_ref[...] = low(flat_sum[...])
        emit_blocks(
            (down_sum.at[:low_rank], down_sum.at[low_rank:], res_sum),
            place_ref[0], own_ref, far_ref, pair_ref,
        )


def branch_kernel(
    branch_ref, raw_ref, map_ref, gate_ref, table_ref, entering_ref, gain_ref, sets_ref, wo_ref,
    down_out_t_ref, up_ref, up_gate_ref, *rest,
    heads, key_width, value_width, hops,
):
    got_refs, rest = rest[: hops - 1], rest[hops - 1 :]
    raw_grad_ref, gate_grad_ref, du_out_ref, du_gate_ref, *rest = rest
    sent_refs, (joined, total) = rest[:hops], rest[hops:]
    first = pl.program_id(0) == 0
    width = wo_ref.shape[1]

    @at_start
    def _():
        joined[:, :width] = wo_ref[...]
        joined[:, width:] = down_out_t_ref[...]

    chosen = chosen_columns(table_ref[...], sets_ref[...])
    branch = branch_ref[...]
    outputs = head_outputs(raw_ref, map_ref, entering_ref, heads, key_width, value_width)
    du_out = masked(nt(branch, up_ref[...]), chosen)
    du_out_ref[...] = du_out
    mixed_grad = nt(jnp.concatenate([branch, du_out], axis=1), joined[...])
    gain = gain_ref[0:1, :]
    gate_grads = []
    for h, output in enumerate(outputs):
        lanes = slice(h * value_width, (h + 1) * value_width)
        scale = lax.rsqrt(jnp.mean(output * output, axis=-1, keepdims=True) + EPS)
        value = gate_ref[:, lanes]
        logistic, active = silu_parts(value)
        incoming = mixed_grad[:, lanes]
        gate_grads.append(
            low(
                incoming
                * (output * scale * gain)
                * (logistic * (1.0 + value * (1.0 - logistic)))
            )
        )
        scaled = gain * (incoming * active)
        dot = jnp.mean(output * scaled, axis=-1, keepdims=True)
        raw_grad = low(scale * scaled - output * (scale * scale * scale * dot))
        raw_grad_ref[:, lanes] = raw_grad
        accumulate(
            total.at[h], tn(map_ref[:, h * key_width : (h + 1) * key_width], raw_grad), first
        )
    gate_grad = jnp.concatenate(gate_grads, axis=1)
    gate_grad_ref[...] = gate_grad
    du_gate_ref[...] = masked(nt(gate_grad, up_gate_ref[...]), chosen)

    @at_end
    def _():
        for h in range(heads):
            passed = low(total[h])
            sent_refs[0][h] = passed
            for hop in range(1, hops):
                passed = low(tn(got_refs[hop - 1][h][:, value_width:], passed))
                sent_refs[hop][h] = passed


def branch_after_kernel(
    branch_ref, z_ref, u_out_ref, rows_ref, inner_ref, du_out_ref, du_gate_ref, gate_grad_ref,
    down_grad_ref, res_grad_ref, flat_ref,
    flat_sum,
):
    lanes = z_ref.shape[1]
    accumulate(down_grad_ref, tn(du_gate_ref[...], rows_ref[...]), True)
    accumulate(res_grad_ref, tn(u_out_ref[...], branch_ref[...]), True)
    accumulate(flat_sum.at[:, :lanes], tn(du_out_ref[...], z_ref[...]), True)
    accumulate(flat_sum.at[:, lanes:], tn(inner_ref[...], gate_grad_ref[...]), True)

    @at_end
    def _():
        flat_ref[...] = low(flat_sum[...])


def settled_rows(pre_ref, tail_ref, arrived_ref, place_ref, quarter, window):
    block = window.shape[0]
    start = ((3 ^ place_ref[0]) + 1) * quarter - HALO - pl.program_id(0) * block
    window[...] = pre_ref[...]

    @pl.when((start >= 0) & (start < block))
    def _():
        window[pl.ds(pl.multiple_of(start, HALO), HALO), :] = low(tail_ref[...] + arrived_ref[...])

    return window[...]


def settle_grads_kernel(
    pre_ref, rows_ref, inner_ref, table_ref, tail_ref, arrived_ref, place_ref, sets_ref,
    up_qk_ref, up_value_ref, down_late_ref, res_late_ref,
    du_ref, own_ref, far_ref, pair_ref, flat_ref,
    window, down_sum, flat_sum,
    *, quarter,
):
    low_rank = sets_ref.shape[1]
    q_width = up_qk_ref.shape[2]
    chosen = chosen_columns(table_ref[...], sets_ref[...])
    pre = settled_rows(pre_ref, tail_ref, arrived_ref, place_ref, quarter, window)
    query, key, value = pre[:, :q_width], pre[:, q_width : 2 * q_width], pre[:, 2 * q_width :]
    inner = inner_ref[...]
    du = jnp.concatenate(
        [
            masked(nt(query, up_qk_ref[0]), chosen),
            masked(nt(key, up_qk_ref[1]), chosen),
            masked(nt(value, up_value_ref[...]), chosen),
        ],
        axis=1,
    )
    du_ref[...] = du
    accumulate(down_sum, tn(du, rows_ref[...]), True)
    at = 0
    for p, part in enumerate((query, key, value)):
        accumulate(
            flat_sum.at[:, at : at + part.shape[1]],
            tn(inner[:, p * low_rank : (p + 1) * low_rank], part),
            True,
        )
        at += part.shape[1]

    @at_end
    def _():
        flat_ref[...] = low(flat_sum[...])
        emit_blocks(
            [down_sum.at[p * low_rank : (p + 1) * low_rank] for p in range(3)]
            + [down_late_ref, res_late_ref],
            place_ref[0], own_ref, far_ref, pair_ref,
        )


def settle_kernel(
    pre_ref, gate_grad_ref, du_ref, du_gate_ref, mix_ref, tail_ref, arrived_ref, place_ref,
    down_mix_ref, wq_ref, wk_ref, wv_ref, wg_ref,
    part_ref,
    window, joined,
    *, quarter,
):
    q_width, v_width = wq_ref.shape[1], wv_ref.shape[1]

    @at_start
    def _():
        joined[:, :q_width] = wq_ref[...]
        joined[:, q_width : 2 * q_width] = wk_ref[...]
        joined[:, 2 * q_width : 2 * q_width + v_width] = wv_ref[...]
        joined[:, 2 * q_width + v_width :] = wg_ref[...]

    pre = settled_rows(pre_ref, tail_ref, arrived_ref, place_ref, quarter, window)
    mix = low(mix_ref[...])
    spare = down_mix_ref.shape[0] - du_ref.shape[1] - du_gate_ref.shape[1] - mix.shape[1]
    small = jnp.concatenate(
        [du_ref[...], du_gate_ref[...], mix, jnp.zeros((mix.shape[0], spare), bfloat)], axis=1
    )
    part_ref[...] = low(
        nt(jnp.concatenate([pre, gate_grad_ref[...]], axis=1), joined[...])
        + nn(small, down_mix_ref[...])
    )


def assemble_kernel(
    place_ref, *refs, padded,
):
    pieces_last, pieces_feed = refs[:4], refs[4:8]
    last_ref, feed_ref, branch_ref = refs[8:11]
    down_ref, qk_ref, vg_ref, ff_ref, out_ref, ffd_ref, res_ref = refs[11:]
    place = place_ref[0]
    size = pieces_last[0].shape[1] // 5
    first = [down_ref.at[p] for p in range(4)] + [res_ref.at[0]]
    second = [down_ref.at[4], down_ref.at[5], res_ref.at[1]]
    for relative in range(4):
        start = pl.multiple_of((place ^ relative) * size, 128)
        for targets, piece in ((first, pieces_last[relative]), (second, pieces_feed[relative])):
            for k, target in enumerate(targets):
                target[:, pl.ds(start, size)] = piece[:, k * size : (k + 1) * size].astype(single)
    qk, values, hidden = qk_ref.shape[2], vg_ref.shape[2], ff_ref.shape[2]

    def lanes(ref, start, width):
        return ref[:, start : start + width].astype(single)

    own = 5 * size
    qk_ref[0], qk_ref[1] = lanes(last_ref, own, qk), lanes(last_ref, own + qk, qk)
    vg_ref[0] = lanes(last_ref, own + 2 * qk, values)
    at = last_ref.shape[1]
    out_ref[...] = lanes(branch_ref, at, values)
    vg_ref[1] = lanes(branch_ref, at + values, values)
    own = 3 * size
    ff_ref[0] = lanes(feed_ref, own, hidden)
    ff_ref[1] = lanes(feed_ref, own + padded, hidden)
    ffd_ref[...] = lanes(feed_ref, own + 2 * padded, hidden)


def assemble(where, shared, last, feed, branch, padded, shapes):
    rows = last.shape[0]
    block = min(32, rows)

    def spec(shape):
        if len(shape) == 2:
            return pl.BlockSpec((block, shape[1]), lambda i: (i, 0))
        return pl.BlockSpec((shape[0], block, shape[2]), lambda i: (0, i, 0))

    arrays = [*shared, last, feed, branch]
    return pl.pallas_call(
        functools.partial(assemble_kernel, padded=padded),
        out_shape=tuple(jax.ShapeDtypeStruct(shape, single) for shape in shapes),
        grid=(rows // block,),
        in_specs=[pl.BlockSpec(memory_space=pltpu.SMEM)] + [spec(a.shape) for a in arrays],
        out_specs=[spec(shape) for shape in shapes],
        compiler_params=pltpu.CompilerParams(
            dimension_semantics=("arbitrary",), vmem_limit_bytes=VMEM_LIMIT
        ),
        name="assemble",
    )(where, *arrays)


WHOLE, SCALAR = "whole", "scalar"


def by_rows(width, lane_block=0):
    return ("rows", width, lane_block)


def pieces(width):
    return ("pieces", width)


def blocked_call(body, name, count, inputs, outputs, scratch, flops, block=STEP):
    steps = count // block
    per = max(steps // 4, 1)
    in_specs, arrays, moved, groups_in, extra = [], [], 0, [], []
    for array, kind in inputs:
        members = array if isinstance(array, (list, tuple)) else [array]
        groups_in.append(len(members))
        arrays += members
        moved += sum(a.size * a.dtype.itemsize for a in members)
        if kind == WHOLE:
            zeros = (0,) * array.ndim
            in_specs.append(
                pl.BlockSpec(
                    array.shape, lambda i, zeros=zeros: zeros, pipeline_mode=pl.Buffered(1)
                )
            )
        elif kind == SCALAR:
            in_specs.append(pl.BlockSpec(memory_space=pltpu.SMEM))
        elif kind[0] == "rows":
            in_specs.append(
                pl.BlockSpec((block, kind[1]), lambda i, lane=kind[2]: (i, lane))
            )
        else:
            for b in range(4):
                in_specs.append(
                    pl.BlockSpec(
                        (block, kind[1]), lambda i, b=b: (jnp.clip(i - b * per, 0, per - 1), 0)
                    )
                )
            extra.append(pltpu.VMEM((block, kind[1]), members[0].dtype))
            if steps == 1:
                for b in range(4):
                    in_specs[b - 4] = pl.BlockSpec(members[b].shape, lambda i: (0, 0))
    out_specs, shapes, groups_out = [], [], []
    for shape, dtype, kind in outputs:
        if kind == "parts":
            quarter = shape[0] // 4
            for rows in (quarter, quarter, 2 * quarter):
                shapes.append(jax.ShapeDtypeStruct((rows, shape[1]), dtype))
            spec = (block, shape[1])
            out_specs += [
                pl.BlockSpec(spec, lambda i: (jnp.clip(i, 0, per - 1), 0)),
                pl.BlockSpec(spec, lambda i: (jnp.clip(i - 2 * per, 0, per - 1), 0)),
                pl.BlockSpec(
                    spec,
                    lambda i: (
                        jnp.clip(i - per, 0, per - 1) + jnp.clip(i - 3 * per + 1, 0, per), 0
                    ),
                ),
            ]
            groups_out.append(3)
            extra.append(pltpu.VMEM(spec, dtype))
        else:
            groups_out.append(1)
            shapes.append(jax.ShapeDtypeStruct(shape, dtype))
            if kind == "rows":
                out_specs.append(pl.BlockSpec((block, shape[1]), lambda i: (i, 0)))
            else:
                zeros = (0,) * len(shape)
                out_specs.append(pl.BlockSpec(shape, lambda i, zeros=zeros: zeros))

    def wrapped(*refs):
        refs = list(refs)
        spare = refs[len(in_specs) + len(out_specs) + len(scratch) :]
        own_scratch = refs[len(in_specs) + len(out_specs) : len(refs) - len(spare)]
        quarter = pl.program_id(0) // per
        given, later, at, used = [], [], 0, 0
        for size in groups_in:
            if size == 1:
                given.append(refs[at])
            else:
                held = spare[used]
                used += 1
                if steps == 1:
                    for b in range(size):
                        piece = refs[at + b]
                        held[b * piece.shape[0] : (b + 1) * piece.shape[0], :] = piece[...]
                for b in range(size if steps > 1 else 0):

                    @pl.when(quarter == b)
                    def _(held=held, source=refs[at + b]):
                        held[...] = source[...]

                given.append(held)
            at += size
        for size in groups_out:
            if size == 1:
                given.append(refs[at])
            else:
                given.append(spare[used])
                later.append((spare[used], refs[at : at + size]))
                used += 1
            at += size
        body(*given, *own_scratch)
        for held, targets in later:
            for b, target in ((0, targets[0]), (2, targets[1]), (1, targets[2]), (3, targets[2])):

                @pl.when(quarter == b)
                def _(held=held, target=target):
                    target[...] = held[...]

    results = pl.pallas_call(
        wrapped,
        out_shape=tuple(shapes),
        grid=(steps,),
        in_specs=in_specs,
        out_specs=out_specs,
        scratch_shapes=list(scratch) + extra,
        compiler_params=pltpu.CompilerParams(
            dimension_semantics=("arbitrary",), vmem_limit_bytes=VMEM_LIMIT
        ),
        cost_estimate=pl.CostEstimate(flops=flops, bytes_accessed=moved, transcendentals=0),
        name=name,
    )(*arrays)
    grouped, at = [], 0
    for size in groups_out:
        grouped.append(results[at] if size == 1 else results[at : at + size])
        at += size
    return grouped


def flip(array, bit):
    groups = lax.axis_size("head")
    return lax.ppermute(array, "head", [(i, i ^ bit) for i in range(groups)])


def gather_rows(array):
    far = flip(array, 2)
    near = flip(array, 1)
    return [array, near, far, flip(far, 1)]


def tie(*arrays):
    return lax.optimization_barrier(arrays)


def near_sum(parts):
    own, far, pair = parts
    size = own.shape[0]
    arrived = flip(pair, 1)
    return (
        own.astype(single) + arrived[:size].astype(single),
        low(far.astype(single) + arrived[size:].astype(single)),
    )


def far_sum(own, far):
    return own + flip(far, 2).astype(single)


def shifted_along(array, axis, by):
    length = lax.axis_size(axis)
    pairs = [(i, i + by) for i in range(length) if 0 <= i + by < length]
    return lax.ppermute(array, axis, pairs)


def seq_rows(flat):
    members = lax.axis_size("seq")
    return flat.reshape(members, flat.shape[0] // members, flat.shape[1])


def share_sum(parts):
    summed = low(jnp.sum(parts.astype(single), axis=0))
    return jnp.broadcast_to(summed[None], parts.shape)


def exchange(parts):
    return lax.all_to_all(parts, "seq", 0, 0)


def all_rows(parts):
    return parts.reshape(-1, parts.shape[-1])


def rms_scale(rows, gain):
    return rows * lax.rsqrt(jnp.mean(rows * rows, axis=-1, keepdims=True) + EPS) * gain


def rms_back(rows, gain, incoming):
    _, back = jax.vjp(lambda value: rms_scale(value, gain), rows)
    return back(incoming)[0]


def on_device(
    block_input,
    out_grad,
    lengths,
    doc_sets,
    norm1_gain,
    w_query,
    w_key,
    w_value,
    conv_query,
    conv_key,
    conv_value,
    w_decay_beta,
    decay_rate,
    decay_bias,
    w_gate_out,
    out_gain,
    w_out,
    norm2_gain,
    w_gate,
    w_up,
    w_down,
    adapt_down,
    adapt_up_qk,
    adapt_up_vg,
    adapt_up_ff,
    adapt_down_out,
    adapt_down_ffd,
    adapt_up_res,
):
    groups = lax.axis_size("head")
    members = lax.axis_size("seq")
    place = lax.axis_index("head")
    quarter, width = block_input.shape
    count = quarter * groups
    heads = decay_rate.shape[0]
    key_width = w_query.shape[1] // heads
    value_width = w_value.shape[1] // heads
    sets, rank = adapt_down.shape[1], adapt_down.shape[3]
    low_rank = sets * rank
    qk = heads * key_width
    device_start = lax.axis_index("seq") * count
    starts = jnp.sum(
        jnp.where(
            jnp.arange(lengths.shape[0])[None, :] < jnp.arange(lengths.shape[0])[:, None],
            lengths[None, :],
            0,
        ),
        axis=1,
    )
    order = jnp.arange(groups, dtype=jnp.int32) ^ place

    def tables(positions):
        reached = positions[:, None] >= starts[None, :]
        token_start = jnp.max(jnp.where(reached, starts[None, :], -1), axis=1)
        ended = positions[:, None] >= (starts + lengths)[None, :]
        token_set = jnp.sum(jnp.where(reached & ~ended, doc_sets[None, :], 0), axis=1)
        pair = jnp.stack([token_start - device_start, token_set], axis=1).astype(single)
        return jnp.pad(pair, ((0, 0), (0, 8 - pair.shape[1])))

    table = tables(
        (
            device_start + order[:, None] * quarter + jnp.arange(quarter, dtype=jnp.int32)[None, :]
        ).reshape(-1)
    )
    halo_table = tables(device_start + jnp.arange(-HALO, 0, dtype=jnp.int32))
    column_sets = jnp.broadcast_to(
        (jnp.arange(low_rank, dtype=jnp.int32) // rank).astype(single)[None, :], (8, low_rank)
    )

    down = adapt_down.transpose(0, 1, 3, 2).reshape(6 * low_rank, width)
    mixer_down, feed_down = down[: 4 * low_rank], down[4 * low_rank :]
    up_qk = adapt_up_qk.reshape(2, low_rank, -1)
    up_vg = adapt_up_vg.reshape(2, low_rank, -1)
    up_ff = adapt_up_ff.reshape(2, low_rank, -1)
    down_out = adapt_down_out.transpose(0, 2, 1).reshape(low_rank, -1)
    down_ffd = adapt_down_ffd.transpose(0, 2, 1).reshape(low_rank, -1)
    up_res = adapt_up_res.reshape(2, low_rank, width)
    conv = jnp.concatenate([conv_query, conv_key, conv_value], axis=1).astype(single)
    scalars = jnp.stack([decay_rate, decay_bias])
    where = place.reshape(1).astype(jnp.int32)
    down_mix = jnp.concatenate(
        [
            mixer_down,
            w_decay_beta.transpose(1, 2, 0).reshape(2 * heads, width),
            jnp.zeros((low_rank - 2 * heads, width), bfloat),
        ],
        axis=0,
    )
    gain = jnp.broadcast_to(out_gain[None, :], (8, value_width))
    hidden_width = w_down.shape[0]
    padded = -(-hidden_width // 256) * 256
    value_lanes = heads * value_width
    block_width = width // groups
    widen = lambda a: jnp.pad(a, [(0, 0)] * (a.ndim - 1) + [(0, padded - hidden_width)])
    up_ff_padded, down_ffd_padded = widen(up_ff), widen(down_ffd)

    input_float = block_input.astype(single)
    normed = low(rms_scale(input_float, norm1_gain))
    tail = normed[quarter - HALO :]
    halo = sum(
        lax.ppermute(
            tail,
            ("seq", "head"),
            [((s * groups) + groups - 1, (s + 1) * groups + h) for s in range(members - 1)],
        )
        for h in range(groups)
    )
    normed_all = gather_rows(normed)
    pre, gate_input, inner, columns, pre_halo = blocked_call(
        project_kernel,
        "project",
        count,
        [
            (normed_all, pieces(width)),
            (table, by_rows(8)),
            (halo, WHOLE),
            (halo_table, WHOLE),
            (column_sets, WHOLE),
            (down_mix, WHOLE),
            (w_query, WHOLE),
            (w_key, WHOLE),
            (w_value, WHOLE),
            (w_gate_out, WHOLE),
            (up_qk, WHOLE),
            (up_vg, WHOLE),
        ],
        [
            ((count, 2 * qk + value_lanes), bfloat, "rows"),
            ((count, value_lanes), single, "rows"),
            ((count, 4 * low_rank), bfloat, "rows"),
            ((count, 8), single, "rows"),
            ((HALO, 2 * qk + value_lanes), bfloat, "whole"),
        ],
        [pltpu.VMEM((width + low_rank, 2 * qk + 2 * value_lanes), bfloat)],
        count * 9_000_000,
    )
    out_grad_late, pre = tie(out_grad, pre)
    grad_near, grad_far = flip(out_grad_late, 1), flip(out_grad_late, 2)
    raw_local, mapped, *saved, sent, sent_state = run_forward(
        where, pre, pre_halo, columns, conv, scalars, heads, key_width, value_width, quarter
    )

    hops = min(members - 1, -(-(DOC_MAX - 1) // count))
    got = [shifted_along(sent, "seq", hop) for hop in range(1, hops)]
    got.append(shifted_along(sent_state, "seq", hops))
    grad_near, grad_far, sent_state = tie(grad_near, grad_far, sent_state)
    grad_all = [out_grad, grad_near, grad_far, flip(grad_far, 1)]
    hidden_grad, du_down = blocked_call(
        feed_before_kernel,
        "feed_before",
        count,
        [
            (grad_all, pieces(width)),
            (table, by_rows(8)),
            (column_sets, WHOLE),
            (w_down, WHOLE),
            (down_ffd.T, WHOLE),
            (up_res[1], WHOLE),
        ],
        [((count, padded), single, "rows"), ((count, low_rank), bfloat, "rows")],
        [pltpu.VMEM((padded, width + low_rank), bfloat)],
        count * 6_000_000,
    )
    raw_local, hidden_grad = tie(raw_local, hidden_grad)

    sizes = dict(heads=heads, key_width=key_width, value_width=value_width)
    attention_part, mixed, u_out, entering = blocked_call(
        functools.partial(attend_kernel, hops=hops, **sizes),
        "attend",
        count,
        [
            (raw_local, by_rows(value_lanes)),
            (mapped, by_rows(qk)),
            (gate_input, by_rows(value_lanes)),
            (table, by_rows(8)),
            (gain, WHOLE),
            (column_sets, WHOLE),
            (w_out, WHOLE),
            (down_out, WHOLE),
            (up_res[0], WHOLE),
        ]
        + [(part, WHOLE) for part in got],
        [
            ((count, width), bfloat, "parts"),
            ((count, value_lanes), bfloat, "rows"),
            ((count, low_rank), bfloat, "rows"),
            ((heads, key_width, value_width), bfloat, "whole"),
        ],
        [pltpu.VMEM((value_lanes + low_rank, width), bfloat)],
        count * 5_000_000,
    )
    attention_own, attention_far = near_sum(attention_part)
    residual = input_float + far_sum(attention_own, attention_far)
    normed_mid = low(rms_scale(residual, norm2_gain))
    mid_all = gather_rows(normed_mid)

    mid_part, hidden, ff_grad, u_ff, du_ff = blocked_call(
        feed_kernel,
        "feed",
        count,
        [
            (mid_all, pieces(width)),
            (hidden_grad, by_rows(padded)),
            (table, by_rows(8)),
            (column_sets, WHOLE),
            (feed_down, WHOLE),
            (w_gate.T, WHOLE),
            (w_up.T, WHOLE),
            (up_ff.transpose(0, 2, 1), WHOLE),
            (up_ff_padded, WHOLE),
        ],
        [
            ((count, width), bfloat, "parts"),
            ((count, padded), bfloat, "rows"),
            ((count, 2 * padded), bfloat, "rows"),
            ((count, 2 * low_rank), bfloat, "rows"),
            ((count, 2 * low_rank), bfloat, "rows"),
        ],
        [
            pltpu.VMEM((padded, width + low_rank), bfloat),
            pltpu.VMEM((padded, width + low_rank), bfloat),
            pltpu.VMEM((2 * padded + 2 * low_rank, width), bfloat),
        ],
        count * 15_000_000,
    )
    mid_own, mid_far = near_sum(mid_part)
    mid_far, hidden = tie(mid_far, hidden)
    mid_grad = far_sum(mid_own, mid_far)
    out_part, feed_own, feed_far, feed_pair, feed_owned = blocked_call(
        feed_after_kernel,
        "feed_after",
        count,
        [
            (mid_all, pieces(width)),
            (grad_all, pieces(width)),
            (hidden, by_rows(padded)),
            (ff_grad, by_rows(2 * padded)),
            (u_ff, by_rows(2 * low_rank)),
            (du_ff, by_rows(2 * low_rank)),
            (du_down, by_rows(low_rank)),
            (table, by_rows(8)),
            (column_sets, WHOLE),
            (where, SCALAR),
            (w_down, WHOLE),
            (down_ffd_padded, WHOLE),
            (up_res[1], WHOLE),
        ],
        [
            ((count, width), bfloat, "parts"),
            ((low_rank, 3 * block_width), bfloat, "whole"),
            ((low_rank, 3 * block_width), bfloat, "whole"),
            ((2 * low_rank, 3 * block_width), bfloat, "whole"),
            ((low_rank, 3 * padded), bfloat, "whole"),
        ],
        [
            pltpu.VMEM((padded + low_rank, width), bfloat),
            pltpu.VMEM((2 * low_rank, width), single),
            pltpu.VMEM((low_rank, width), single),
            pltpu.VMEM((low_rank, 3 * padded), single),
        ],
        count * 12_000_000,
    )
    residual_grad = out_grad.astype(single) + rms_back(residual, norm2_gain, mid_grad)
    branch_low = low(residual_grad)
    branch_all = gather_rows(branch_low)
    feed_flat = jnp.concatenate(
        [low(far_sum(*near_sum((feed_own, feed_far, feed_pair)))), feed_owned], axis=1
    )
    corner_branch, feed_flat = tie(branch_all[3], feed_flat)
    branch_all = branch_all[:3] + [corner_branch]
    feed_parts = exchange(seq_rows(feed_flat))

    raw_grad, gate_grad, du_out, du_outgate, *state_grads = blocked_call(
        functools.partial(branch_kernel, hops=hops, **sizes),
        "branch",
        count,
        [
            (branch_all, pieces(width)),
            (raw_local, by_rows(value_lanes)),
            (mapped, by_rows(qk)),
            (gate_input, by_rows(value_lanes)),
            (table, by_rows(8)),
            (entering, WHOLE),
            (gain, WHOLE),
            (column_sets, WHOLE),
            (w_out, WHOLE),
            (down_out.T, WHOLE),
            (up_res[0], WHOLE),
            (up_vg[1], WHOLE),
        ]
        + [(part, WHOLE) for part in got[:-1]],
        [
            ((count, value_lanes), bfloat, "rows"),
            ((count, value_lanes), bfloat, "rows"),
            ((count, low_rank), bfloat, "rows"),
            ((count, low_rank), bfloat, "rows"),
        ]
        + [((heads, key_width, value_width), bfloat, "whole")] * hops,
        [
            pltpu.VMEM((value_lanes, width + low_rank), bfloat),
            pltpu.VMEM((heads, key_width, value_width), single),
        ],
        count * 7_000_000,
    )
    state_got = [
        shifted_along(part, "seq", -hop) for hop, part in enumerate(state_grads, start=1)
    ]
    du_out, feed_parts, out_pair = tie(du_out, feed_parts, out_part[2])
    out_own, out_far = near_sum((out_part[0], out_part[1], out_pair))
    mixer_down_late, branch_res_grad, branch_flat = blocked_call(
        branch_after_kernel,
        "branch_after",
        count,
        [
            (branch_all, pieces(width)),
            (mixed, by_rows(value_lanes)),
            (u_out, by_rows(low_rank)),
            (normed_all, pieces(width)),
            (inner, by_rows(low_rank, 3)),
            (du_out, by_rows(low_rank)),
            (du_outgate, by_rows(low_rank)),
            (gate_grad, by_rows(value_lanes)),
        ],
        [
            ((low_rank, width), single, "whole"),
            ((low_rank, width), single, "whole"),
            ((low_rank, 2 * value_lanes), bfloat, "whole"),
        ],
        [pltpu.VMEM((low_rank, 2 * value_lanes), single)],
        count * 20_000_000,
        block=count,
    )
    feed_lanes = feed_parts.shape[-1]
    both = jnp.concatenate([share_sum(feed_parts), seq_rows(branch_flat)], axis=2)
    raw_grad, both, out_far, *state_got = tie(raw_grad, both, out_far, *state_got)
    out_arrived = flip(out_far, 2)
    both = exchange(both)

    pre_grad, mix_grad, tail_grad, edge_grad = run_backward(
        where, pre, pre_halo, columns, conv, scalars, raw_grad, saved, entering, state_got,
        heads, key_width, value_width, quarter,
    )
    arrived = shifted_along(edge_grad, "seq", -1)
    arrived, both, out_arrived = tie(arrived, both, out_arrived)
    result = residual + (out_own + out_arrived.astype(single))
    branch_parts = both[:, :, feed_lanes:]
    settled = [
        (pre_grad, by_rows(2 * qk + value_lanes)),
        (tail_grad, WHOLE),
        (arrived, WHOLE),
        (where, SCALAR),
    ]
    du_mix, last_own, last_far, last_pair, last_owned = blocked_call(
        functools.partial(settle_grads_kernel, quarter=quarter),
        "settle_grads",
        count,
        [
            settled[0],
            (normed_all, pieces(width)),
            (inner, by_rows(4 * low_rank)),
            (table, by_rows(8)),
            *settled[1:],
            (column_sets, WHOLE),
            (up_qk, WHOLE),
            (up_vg[0], WHOLE),
            (mixer_down_late, WHOLE),
            (branch_res_grad, WHOLE),
        ],
        [
            ((count, 3 * low_rank), bfloat, "rows"),
            ((low_rank, 5 * block_width), bfloat, "whole"),
            ((low_rank, 5 * block_width), bfloat, "whole"),
            ((2 * low_rank, 5 * block_width), bfloat, "whole"),
            ((low_rank, 2 * qk + value_lanes), bfloat, "whole"),
        ],
        [
            pltpu.VMEM((count, 2 * qk + value_lanes), bfloat),
            pltpu.VMEM((3 * low_rank, width), single),
            pltpu.VMEM((low_rank, 2 * qk + value_lanes), single),
        ],
        count * 4_000_000,
        block=count,
    )
    last_own, last_far = near_sum((last_own, last_far, last_pair))
    last_far, gate_grad = tie(last_far, gate_grad)
    (normed_part,) = blocked_call(
        functools.partial(settle_kernel, quarter=quarter),
        "settle",
        count,
        [
            settled[0],
            (gate_grad, by_rows(value_lanes)),
            (du_mix, by_rows(3 * low_rank)),
            (du_outgate, by_rows(low_rank)),
            (mix_grad, by_rows(8)),
            *settled[1:],
            (down_mix, WHOLE),
            (w_query, WHOLE),
            (w_key, WHOLE),
            (w_value, WHOLE),
            (w_gate_out, WHOLE),
        ],
        [((count, width), bfloat, "parts")],
        [
            pltpu.VMEM((STEP, 2 * qk + value_lanes), bfloat),
            pltpu.VMEM((width, 2 * qk + 2 * value_lanes), bfloat),
        ],
        count * 10_000_000,
    )
    last_flat = jnp.concatenate([low(far_sum(last_own, last_far)), last_owned], axis=1)
    feed_rows = all_rows(both)
    feed_pieces = gather_rows(feed_rows[:, : 3 * block_width])
    last_lanes = last_flat.shape[1]
    both = exchange(jnp.concatenate([seq_rows(last_flat), share_sum(branch_parts)], axis=2))
    branch_rows = all_rows(both)
    last_parts = both[:, :, :last_lanes]
    normed_grad = far_sum(*near_sum(normed_part))
    input_grad = residual_grad + rms_back(input_float, norm1_gain, normed_grad)
    last_parts, *feed_pieces = tie(last_parts, *feed_pieces)
    last_rows = all_rows(exchange(share_sum(last_parts)))
    last_pieces = gather_rows(last_rows[:, : 5 * block_width])
    down_grad, qk_grad, vg_grad, ff_grads, out_grads, ffd_grads, res_grad = assemble(
        where,
        [*last_pieces, *feed_pieces],
        last_rows,
        feed_rows,
        branch_rows,
        padded,
        [
            (6, low_rank, width),
            (2, low_rank, qk),
            (2, low_rank, value_lanes),
            (2, low_rank, hidden_width),
            (low_rank, value_lanes),
            (low_rank, hidden_width),
            (2, low_rank, width),
        ],
    )

    def as_down(rows):
        return rows.reshape(rows.shape[:-2] + (sets, rank, -1)).swapaxes(-1, -2)

    def as_up(rows):
        return rows.reshape(rows.shape[0], sets, rank, -1)

    return (
        low(result),
        input_grad,
        as_down(down_grad),
        as_up(qk_grad),
        as_up(vg_grad),
        as_up(ff_grads),
        as_down(out_grads),
        as_down(ffd_grads),
        as_up(res_grad),
    )


def solution(mesh):
    rows = P(("seq", "head"), None)
    lanes = P(None, "head")
    last = P(None, None, None, "head")
    middle = P(None, "head", None)
    in_specs = (
        rows, rows, P(), P(), P(), lanes, lanes, lanes, lanes, lanes, lanes,
        P(None, None, "head"), P("head"), P("head"), lanes, P(), P("head", None), P(), lanes,
        lanes, P("head", None), P(), last, last, last, middle, middle, P(),
    )
    out_specs = (rows, rows, P(), last, last, last, middle, middle, P())
    return jax.shard_map(
        on_device, mesh=mesh, in_specs=in_specs, out_specs=out_specs, check_vma=False
    )
```

```python
import functools

import jax
import jax.numpy as jnp
from jax import lax
from jax.experimental import pallas as pl
from jax.experimental.pallas import tpu as pltpu
from jax.sharding import PartitionSpec as P

CHUNK = 128
STEP = 256
HALO = 16
DOC_MAX = 4096
EPS = 1e-06
VMEM_LIMIT = 56 * 1024 * 1024
bfloat = jnp.bfloat16
single = jnp.float32


def contract(left, right, left_dim, right_dim):
    return lax.dot_general(
        left,
        right,
        (((left_dim,), (right_dim,)), ((), ())),
        preferred_element_type=single,
    )


def nn(left, right):
    return contract(left, right, 1, 0)


def nt(left, right):
    return contract(left, right, 1, 1)


def tn(left, right):
    return contract(left, right, 0, 0)


def low(array):
    return array.astype(bfloat)


def iotas():
    rows = lax.broadcasted_iota(jnp.int32, (CHUNK, CHUNK), 0)
    columns = lax.broadcasted_iota(jnp.int32, (CHUNK, CHUNK), 1)
    return rows, columns


def split_two(array):
    high = low(array)
    return high, low(array - high.astype(single))


def near_exact(left, right):
    left_high, left_low = split_two(left)
    right_high, right_low = split_two(right)
    return nn(
        jnp.concatenate([left_high, left_high, left_low], axis=1),
        jnp.concatenate([right_high, right_low, right_high], axis=0),
    )


def ones_product(ones, array):
    high = low(array)
    rest = array - high.astype(single)
    middle = low(rest)
    lowest = low(rest - middle.astype(single))
    return nn(
        jnp.concatenate([ones, ones, ones], axis=1),
        jnp.concatenate([high, middle, lowest], axis=0),
    )


def unit_lower_inverses(stricts, rows, columns):
    eye = (rows == columns).astype(single)
    differ = rows ^ columns
    block = 8
    inner = [jnp.where(differ < block, strict, 0.0) for strict in stricts]
    second = [near_exact(a, a) for a in inner]
    inverse = [near_exact(eye - a, eye + b) for a, b in zip(inner, second)]
    fourth = [near_exact(b, b) for b in second]
    inverse = [near_exact(a, eye + b) for a, b in zip(inverse, fourth)]
    while block < CHUNK:
        between = (differ >= block) & (differ < 2 * block)
        off = [jnp.where(between, strict, 0.0) for strict in stricts]
        part = [near_exact(a, b) for a, b in zip(off, inverse)]
        inverse = [a - near_exact(a, b) for a, b in zip(inverse, part)]
        block = 2 * block
    return inverse


def softplus(value):
    return jnp.maximum(value, 0.0) + jnp.log(1.0 + jnp.exp(-jnp.abs(value)))


def sigmoid(value):
    return 1.0 / (1.0 + jnp.exp(-value))


def gates(decay, start, rows, columns):
    lower_ones = low((rows >= columns).astype(single))
    total = ones_product(lower_ones, jnp.broadcast_to(decay, (CHUNK, CHUNK)))
    linked = (rows >= columns) & (columns >= start)
    within = jnp.where(linked, jnp.exp(jnp.where(linked, total - total.T, 0.0)), 0.0)
    running = total[:, :1]
    carried = jnp.where(start < 0, jnp.exp(running), 0.0)
    last = running[CHUNK - 1 : CHUNK]
    ending = jnp.where(
        rows[:, :1] >= start[CHUNK - 1 : CHUNK], jnp.exp(jnp.minimum(last - running, 0.0)), 0.0
    )
    return within, carried, ending


def convolved(window, starts, weights, base):
    positions = base + lax.broadcasted_iota(jnp.int32, (STEP, 1), 0)
    taps = weights.shape[0]
    total = None
    for tap in range(taps):
        back = taps - 1 - tap
        term = window[HALO - back : HALO - back + STEP, :] * weights[tap : tap + 1, :]
        if back:
            term = jnp.where(positions - back >= starts, term, 0.0)
        total = term if total is None else total + term
    return total


def head_scales(rows, width):
    return lax.rsqrt(jnp.sum(rows * rows, axis=-1, keepdims=True) + EPS)


def forward_kernel(
    place,
    rows_ref,
    halo_ref,
    column_ref,
    weight_ref,
    scalar_ref,
    out_ref,
    map_ref,
    written_ref,
    state_ref,
    inverse_ref,
    end_ref,
    sent_ref,
    sent_state_ref,
    window,
    state,
    *,
    heads,
    key_width,
    value_width,
):
    step = pl.program_id(0)
    wide = value_width + key_width
    base = step * STEP
    rows, columns = iotas()

    @pl.when(step == 0)
    def _():
        window[0:HALO, :] = halo_ref[...].astype(single)
        for h in range(heads):
            state[h, :, :value_width] = jnp.zeros((key_width, value_width), single)
            state[h, :, value_width:] = (rows == columns).astype(single)

    @pl.when(step > 0)
    def _():
        window[0:HALO, :] = window[STEP : STEP + HALO, :]

    window[HALO:, :] = rows_ref[...].astype(single)
    info = column_ref[...]
    starts = info[:, 2 * heads : 2 * heads + 1].astype(jnp.int32)
    before = convolved(window, starts, weight_ref[...], base)
    active = before * sigmoid(before)
    qk_lanes = heads * key_width
    chunks = STEP // CHUNK
    local, stricts = [], []
    for c in range(chunks):
        span = slice(c * CHUNK, (c + 1) * CHUNK)
        for h in range(heads):
            query = active[span, h * key_width : (h + 1) * key_width]
            key = active[span, qk_lanes + h * key_width : qk_lanes + (h + 1) * key_width]
            value = active[
                span, 2 * qk_lanes + h * value_width : 2 * qk_lanes + (h + 1) * value_width
            ]
            query = query * (head_scales(query, key_width) * key_width ** (-0.5))
            key = key * head_scales(key, key_width)
            beta = sigmoid(info[span, h : h + 1])
            decay = -scalar_ref[0, h] * softplus(
                info[span, heads + h : heads + h + 1] + scalar_ref[1, h]
            )
            within, carried, ending = gates(
                decay, starts[span] - (base + c * CHUNK), rows, columns
            )
            query, key = low(query), low(key)
            strict = jnp.where(rows > columns, within * nt(key, key), 0.0) * beta
            mixed = low(within * nt(query, key))
            stricts.append(strict)
            local.append((query, key, value, beta, carried, ending, mixed))
    inverses = [low(a) for a in unit_lower_inverses(stricts, rows, columns)]
    each = range(heads)
    now = [state[h] for h in each]
    for c in range(chunks):
        span = slice(c * CHUNK, (c + 1) * CHUNK)
        here = [local[c * heads + h] for h in each]
        inverse = [inverses[c * heads + h] for h in each]
        now_low = [low(a) for a in now]
        read = [nn(here[h][1], now_low[h]) for h in each]
        asked = [nn(here[h][0], now_low[h]) for h in each]
        target = []
        for h in each:
            query, key, value, beta, carried, ending, mixed = here[h]
            gap = -(carried * beta) * read[h]
            target.append(
                jnp.concatenate(
                    [beta * value + gap[:, :value_width], gap[:, value_width:]], axis=1
                )
            )
        written = [nn(inverse[h], low(target[h])) for h in each]
        added = [tn(here[h][1], low(here[h][5] * written[h])) for h in each]
        inner = [nn(here[h][6], low(written[h])) for h in each]
        for h in each:
            carried = here[h][4]
            inverse_ref[span, h * CHUNK : (h + 1) * CHUNK] = inverse[h]
            state_ref[c, h] = now_low[h]
            written_ref[span, h * wide : (h + 1) * wide] = low(written[h])
            output = carried * asked[h] + inner[h]
            out_ref[span, h * value_width : (h + 1) * value_width] = output[:, :value_width]
            map_ref[span, h * key_width : (h + 1) * key_width] = low(output[:, value_width:])
        now = [here[h][4][CHUNK - 1 : CHUNK] * now[h] + added[h] for h in each]
    for h in each:
        state[h] = now[h]

    @pl.when(step == pl.num_programs(0) - 1)
    def _():
        final = state[...]
        end_ref[...] = final
        sent_ref[...] = low(final)
        sent_state_ref[...] = low(final[:, :, :value_width])


def backward_kernel(
    place,
    rows_ref,
    before_ref,
    halo_ref,
    column_ref,
    weight_ref,
    scalar_ref,
    grad_ref,
    written_ref,
    state_ref,
    inverse_ref,
    end_ref,
    entering_ref,
    *rest,
    hops,
    heads,
    key_width,
    value_width,
):
    got_refs, rest = rest[:hops], rest[hops:]
    out_ref, mix_ref, tail_ref, edge_ref, window, shifted, shifted_start, cotangent, ahead = rest
    step = pl.program_id(0)
    steps = pl.num_programs(0)
    wide = value_width + key_width
    base = (steps - 1 - step) * STEP
    rows, columns = iotas()
    qk_lanes = heads * key_width
    lanes = window.shape[1]
    taps = weight_ref.shape[0]

    @pl.when(step == 0)
    def _():
        shifted[STEP : STEP + 8, :] = jnp.zeros((8, lanes), single)
        shifted_start[STEP : STEP + 8, :] = jnp.zeros((8, 1), jnp.int32)
        for h in range(heads):
            passed = got_refs[0][h].astype(single)
            for hop in range(1, hops):
                passed = passed + got_refs[hop][h].astype(single)
            cotangent[h] = passed
            ahead[h] = end_ref[h, :, :value_width] + nn(
                low(end_ref[h, :, value_width:]), low(entering_ref[h])
            )

    @pl.when(step > 0)
    def _():
        shifted[STEP : STEP + 8, :] = shifted[0:8, :]
        shifted_start[STEP : STEP + 8, :] = shifted_start[0:8, :]

    window[0:HALO, :] = jnp.where(
        step == steps - 1, halo_ref[...].astype(single), before_ref[...].astype(single)
    )
    window[HALO:, :] = rows_ref[...].astype(single)
    info = column_ref[...]
    starts = info[:, 2 * heads : 2 * heads + 1].astype(jnp.int32)
    positions = base + lax.broadcasted_iota(jnp.int32, (STEP, 1), 0)
    before = convolved(window, starts, weight_ref[...], base)
    gate = sigmoid(before)
    active = before * gate
    slope = gate * (1.0 + before * (1.0 - gate))
    upper_ones = low((rows <= columns).astype(single))
    last_row = rows[:, :1] == CHUNK - 1
    chunks = STEP // CHUNK
    each = range(heads)
    items = [(c, h) for c in range(chunks) for h in each]
    spans = {item: slice(item[0] * CHUNK, (item[0] + 1) * CHUNK) for item in items}
    entering = [low(entering_ref[h]) for h in each]
    root = key_width ** (-0.5)

    def per(function):
        return {item: function(*item) for item in items}

    def q_lanes(h):
        return slice(h * key_width, (h + 1) * key_width)

    def k_lanes(h):
        return slice(qk_lanes + h * key_width, qk_lanes + (h + 1) * key_width)

    def v_lanes(h):
        return slice(2 * qk_lanes + h * value_width, 2 * qk_lanes + (h + 1) * value_width)

    def kept(c, h, part):
        return written_ref[spans[c, h], h * wide : (h + 1) * wide][:, part]

    values, maps = slice(0, value_width), slice(value_width, wide)
    query_raw = per(lambda c, h: active[spans[c, h], q_lanes(h)])
    key_raw = per(lambda c, h: active[spans[c, h], k_lanes(h)])
    query_scale = per(lambda c, h: head_scales(query_raw[c, h], key_width))
    key_scale = per(lambda c, h: head_scales(key_raw[c, h], key_width))
    query = per(lambda c, h: query_raw[c, h] * (query_scale[c, h] * root))
    key = per(lambda c, h: key_raw[c, h] * key_scale[c, h])
    query_low = per(lambda c, h: low(query[c, h]))
    key_low = per(lambda c, h: low(key[c, h]))
    beta = per(lambda c, h: sigmoid(info[spans[c, h], h : h + 1]))
    raw = per(lambda c, h: info[spans[c, h], heads + h : heads + h + 1] + scalar_ref[1, h])
    gated = per(
        lambda c, h: gates(
            -scalar_ref[0, h] * softplus(raw[c, h]),
            starts[spans[c, h]] - (base + c * CHUNK),
            rows,
            columns,
        )
    )
    within = per(lambda c, h: gated[c, h][0])
    carried = per(lambda c, h: gated[c, h][1])
    ending = per(lambda c, h: gated[c, h][2])
    mixed = per(lambda c, h: low(within[c, h] * nt(query_low[c, h], key_low[c, h])))
    written = per(
        lambda c, h: kept(c, h, values).astype(single) + nn(kept(c, h, maps), entering[h])
    )
    start_state = per(
        lambda c, h: state_ref[c, h][:, values].astype(single)
        + nn(state_ref[c, h][:, maps], entering[h])
    )
    written_low = per(lambda c, h: low(written[c, h]))
    start_low = per(lambda c, h: low(start_state[c, h]))
    grad = per(lambda c, h: grad_ref[spans[c, h], h * value_width : (h + 1) * value_width])
    grad_low = grad
    carried_grad = per(lambda c, h: low(carried[c, h] * grad[c, h].astype(single)))
    from_output = per(lambda c, h: tn(mixed[c, h], grad_low[c, h]))
    state_part = per(lambda c, h: tn(query_low[c, h], carried_grad[c, h]))
    mixed_grad = per(lambda c, h: low(within[c, h] * nt(grad_low[c, h], written_low[c, h])))
    query_grad = per(
        lambda c, h: nt(carried_grad[c, h], start_low[c, h]) + nn(mixed_grad[c, h], key_low[c, h])
    )
    key_write = per(lambda c, h: tn(mixed_grad[c, h], query_low[c, h]))
    later, later_low, solved, value_grad, read_grad = {}, {}, {}, {}, {}
    now = [cotangent[h] for h in each]
    for c in reversed(range(chunks)):
        for h in each:
            later[c, h], later_low[c, h] = now[h], low(now[h])
        from_state = [nn(key_low[c, h], later_low[c, h]) for h in each]
        written_grad = [low(from_output[c, h] + ending[c, h] * from_state[h]) for h in each]
        for h in each:
            inverse = inverse_ref[spans[c, h], h * CHUNK : (h + 1) * CHUNK]
            solved[c, h] = tn(inverse, written_grad[h])
        for h in each:
            value_grad[c, h] = beta[c, h] * solved[c, h]
            read_grad[c, h] = low(-carried[c, h] * value_grad[c, h])
        now = [
            carried[c, h][CHUNK - 1 : CHUNK] * now[h]
            + state_part[c, h]
            + tn(key_low[c, h], read_grad[c, h])
            for h in each
        ]
    following = {
        (c, h): start_state[c + 1, h] if c + 1 < chunks else ahead[h] for c, h in items
    }
    at_end = per(lambda c, h: jnp.sum(later[c, h] * following[c, h], keepdims=True))
    for h in each:
        cotangent[h] = now[h]
        ahead[h] = start_state[0, h]
    strict_grad = per(
        lambda c, h: low(
            jnp.where(
                rows > columns, -within[c, h] * nt(low(value_grad[c, h]), written_low[c, h]), 0.0
            )
        )
    )
    key_read = per(
        lambda c, h: nt(read_grad[c, h], start_low[c, h]) + nn(strict_grad[c, h], key_low[c, h])
    )
    key_write = per(
        lambda c, h: key_write[c, h]
        + tn(strict_grad[c, h], key_low[c, h])
        + nt(low(ending[c, h] * written[c, h]), later_low[c, h])
    )
    query_dot = per(
        lambda c, h: jnp.sum(query[c, h] * query_grad[c, h], axis=-1, keepdims=True)
    )
    running_grad = per(
        lambda c, h: query_dot[c, h]
        + jnp.sum(key[c, h] * (key_read[c, h] - key_write[c, h]), axis=-1, keepdims=True)
        + jnp.where(last_row, at_end[c, h], 0.0)
    )
    decay_sum = per(
        lambda c, h: ones_product(
            upper_ones, jnp.broadcast_to(running_grad[c, h], (CHUNK, CHUNK))
        )[:, :1]
    )
    decay_grad = per(
        lambda c, h: jnp.where(
            positions[spans[c, h]] == starts[spans[c, h]],
            0.0,
            -scalar_ref[0, h] * sigmoid(raw[c, h]) * decay_sum[c, h],
        )
    )
    beta_grad = per(
        lambda c, h: jnp.sum(solved[c, h] * written[c, h], axis=-1, keepdims=True)
        * sigmoid(-info[spans[c, h], h : h + 1])
    )
    for c, h in items:
        span = spans[c, h]
        key_grad = key_read[c, h] + key_write[c, h]
        key_dot = jnp.sum(key[c, h] * key_grad, axis=-1, keepdims=True)
        query_active = (query_scale[c, h] * root) * query_grad[c, h] - query_raw[c, h] * (
            query_scale[c, h] * query_scale[c, h] * query_dot[c, h]
        )
        key_active = key_scale[c, h] * (key_grad - key[c, h] * key_dot)
        shifted[span, q_lanes(h)] = query_active * slope[span, q_lanes(h)]
        shifted[span, k_lanes(h)] = key_active * slope[span, k_lanes(h)]
        shifted[span, v_lanes(h)] = value_grad[c, h] * slope[span, v_lanes(h)]
    for c in range(chunks):
        mix_ref[c * CHUNK : (c + 1) * CHUNK, :] = jnp.concatenate(
            [beta_grad[c, h] for h in each]
            + [decay_grad[c, h] for h in each]
            + [jnp.zeros((CHUNK, mix_ref.shape[1] - 2 * heads), single)],
            axis=1,
        )
    shifted_start[0:STEP, :] = starts
    total = None
    for tap in range(taps):
        back = taps - 1 - tap
        term = shifted[back : back + STEP, :] * weight_ref[tap : tap + 1, :]
        if back:
            term = jnp.where(positions >= shifted_start[back : back + STEP, :], term, 0.0)
        total = term if total is None else total + term
    out_ref[...] = low(total)

    @pl.when(step == 0)
    def _():
        tail_ref[...] = total[STEP - HALO :, :]

    @pl.when(step == steps - 1)
    def _():
        window[0:8, :] = jnp.zeros((8, lanes), single)
        window[8:16, :] = shifted[0:8, :]
        early = lax.broadcasted_iota(jnp.int32, (8, 1), 0) - 8
        collected = jnp.zeros((8, lanes), single)
        for tap in range(taps - 1):
            back = taps - 1 - tap
            reader = early + back
            reader_start = jnp.zeros((8, 1), jnp.int32)
            for t in range(back):
                reader_start = jnp.where(reader == t, shifted_start[t : t + 1, :], reader_start)
            term = window[back : back + 8, :] * weight_ref[tap : tap + 1, :]
            collected = collected + jnp.where(
                (reader >= 0) & (early >= reader_start), term, 0.0
            )
        edge_ref[0:8, :] = jnp.zeros((8, lanes), single)
        edge_ref[8:16, :] = collected


def block_place(step, place, per_quarter):
    return ((step // per_quarter) ^ place[0]) * per_quarter + step % per_quarter


def run_forward(place, rows, halo, columns, weights, scalars, heads, key_width, value_width, quarter):
    count, lanes = columns.shape[0], rows.shape[1]
    steps, per_quarter = count // STEP, quarter // STEP
    wide = value_width + key_width
    chunks = STEP // CHUNK
    at = lambda i, place: (block_place(i, place, per_quarter), 0)
    fixed = lambda i, place: (0, 0)
    body = functools.partial(
        forward_kernel, heads=heads, key_width=key_width, value_width=value_width
    )
    shapes = (
        jax.ShapeDtypeStruct((count, heads * value_width), single),
        jax.ShapeDtypeStruct((count, heads * key_width), bfloat),
        jax.ShapeDtypeStruct((count, heads * wide), bfloat),
        jax.ShapeDtypeStruct((count // CHUNK, heads, key_width, wide), bfloat),
        jax.ShapeDtypeStruct((count, heads * CHUNK), bfloat),
        jax.ShapeDtypeStruct((heads, key_width, wide), single),
        jax.ShapeDtypeStruct((heads, key_width, wide), bfloat),
        jax.ShapeDtypeStruct((heads, key_width, value_width), bfloat),
    )
    return pl.pallas_call(
        body,
        out_shape=shapes,
        grid_spec=pltpu.PrefetchScalarGridSpec(
            num_scalar_prefetch=1,
            grid=(steps,),
            in_specs=[
                pl.BlockSpec((STEP, lanes), at),
                pl.BlockSpec((HALO, lanes), lambda i, place: (0, 0)),
                pl.BlockSpec((STEP, columns.shape[1]), at),
                pl.BlockSpec(weights.shape, fixed),
                pl.BlockSpec(memory_space=pltpu.SMEM),
            ],
            out_specs=[
                pl.BlockSpec((STEP, heads * value_width), at),
                pl.BlockSpec((STEP, heads * key_width), at),
                pl.BlockSpec((STEP, heads * wide), at),
                pl.BlockSpec((chunks, heads, key_width, wide), lambda i, place: (i, 0, 0, 0)),
                pl.BlockSpec((STEP, heads * CHUNK), at),
                pl.BlockSpec((heads, key_width, wide), lambda i, place: (0, 0, 0)),
                pl.BlockSpec((heads, key_width, wide), lambda i, place: (0, 0, 0)),
                pl.BlockSpec((heads, key_width, value_width), lambda i, place: (0, 0, 0)),
            ],
            scratch_shapes=[
                pltpu.VMEM((STEP + HALO, lanes), single),
                pltpu.VMEM((heads, key_width, wide), single),
            ],
        ),
        compiler_params=pltpu.CompilerParams(
            dimension_semantics=("arbitrary",), vmem_limit_bytes=VMEM_LIMIT
        ),
        cost_estimate=pl.CostEstimate(
            flops=count * 2_000_000, bytes_accessed=count * 10_000, transcendentals=count * 2000
        ),
        name="delta_forward",
    )(place, rows, halo, columns, weights, scalars)


def run_backward(
    place, rows, halo, columns, weights, scalars, grad, saved, entering, got, heads,
    key_width, value_width, quarter,
):
    written, states, inverses, end = saved
    count, lanes = columns.shape[0], rows.shape[1]
    steps, per_quarter = count // STEP, quarter // STEP
    wide = value_width + key_width
    chunks = STEP // CHUNK

    def at(i, place):
        return (block_place(steps - 1 - i, place, per_quarter), 0)

    def halo_at(i, place):
        here = steps - 1 - i
        inner = block_place(jnp.maximum(here - 1, 0), place, per_quarter)
        ratio = STEP // HALO
        return (inner * ratio + ratio - 1, 0)

    fixed = lambda i, place: (0, 0)
    whole = lambda i, place: (0, 0, 0)
    body = functools.partial(
        backward_kernel,
        hops=len(got),
        heads=heads,
        key_width=key_width,
        value_width=value_width,
    )
    shapes = (
        jax.ShapeDtypeStruct((count, lanes), bfloat),
        jax.ShapeDtypeStruct((count, columns.shape[1]), single),
        jax.ShapeDtypeStruct((HALO, lanes), single),
        jax.ShapeDtypeStruct((HALO, lanes), single),
    )
    return pl.pallas_call(
        body,
        out_shape=shapes,
        grid_spec=pltpu.PrefetchScalarGridSpec(
            num_scalar_prefetch=1,
            grid=(steps,),
            in_specs=[
                pl.BlockSpec((STEP, lanes), at),
                pl.BlockSpec((HALO, lanes), halo_at),
                pl.BlockSpec((HALO, lanes), fixed),
                pl.BlockSpec((STEP, columns.shape[1]), at),
                pl.BlockSpec(weights.shape, fixed),
                pl.BlockSpec(memory_space=pltpu.SMEM),
                pl.BlockSpec((STEP, heads * value_width), at),
                pl.BlockSpec((STEP, heads * wide), at),
                pl.BlockSpec(
                    (chunks, heads, key_width, wide), lambda i, place: (steps - 1 - i, 0, 0, 0)
                ),
                pl.BlockSpec((STEP, heads * CHUNK), at),
                pl.BlockSpec(end.shape, whole),
                pl.BlockSpec(entering.shape, whole),
            ]
            + [pl.BlockSpec(part.shape, whole) for part in got],
            out_specs=[
                pl.BlockSpec((STEP, lanes), at),
                pl.BlockSpec((STEP, columns.shape[1]), at),
                pl.BlockSpec((HALO, lanes), fixed),
                pl.BlockSpec((HALO, lanes), fixed),
            ],
            scratch_shapes=[
                pltpu.VMEM((STEP + HALO, lanes), single),
                pltpu.VMEM((STEP + 8, lanes), single),
                pltpu.VMEM((STEP + 8, 1), jnp.int32),
                pltpu.VMEM((heads, key_width, value_width), single),
                pltpu.VMEM((heads, key_width, value_width), single),
            ],
        ),
        compiler_params=pltpu.CompilerParams(
            dimension_semantics=("arbitrary",), vmem_limit_bytes=VMEM_LIMIT
        ),
        cost_estimate=pl.CostEstimate(
            flops=count * 3_000_000, bytes_accessed=count * 12_000, transcendentals=count * 3000
        ),
        name="delta_backward",
    )(
        place, rows, rows, halo, columns, weights, scalars, grad, written, states, inverses, end,
        entering, *got,
    )


def chosen_columns(table, column_sets):
    return column_sets[0:1, :] == table[:, 1:2]


def masked(product, chosen):
    return low(jnp.where(chosen, product, 0.0))


def silu_parts(value):
    logistic = sigmoid(value)
    return logistic, value * logistic


def accumulate(ref, value, first):
    if first is True:
        ref[...] = value
    else:
        ref[...] = jnp.where(first, value, ref[...] + value)


def emit_blocks(parts, place, own_ref, far_ref, pair_ref):
    for k, part in enumerate(parts):
        rows, size = part.shape[0], part.shape[1] // 4
        lanes = slice(k * size, (k + 1) * size)
        for relative, target, row in (
            (0, own_ref, 0), (2, far_ref, 0), (1, pair_ref, 0), (3, pair_ref, rows)
        ):
            start = pl.multiple_of((place ^ relative) * size, 128)
            target[row : row + rows, lanes] = low(part[:, pl.ds(start, size)])


def at_end(fill):
    pl.when(pl.program_id(0) == pl.num_programs(0) - 1)(fill)


def at_start(fill):
    pl.when(pl.program_id(0) == 0)(fill)


def project_kernel(
    rows_ref, table_ref, sets_ref, down_mix_ref, wq_ref, wk_ref, wv_ref, up_qk_ref, up_value_ref,
    *rest, with_halo,
):
    low_rank = sets_ref.shape[1]
    width, q_width = wq_ref.shape
    v_width = wv_ref.shape[1]
    bounds = [0, q_width, 2 * q_width, 2 * q_width + v_width]
    if with_halo:
        halo_ref, halo_table_ref, pre_ref, inner_ref, column_ref, pre_halo_ref, joined = rest
    else:
        pre_ref, inner_ref, column_ref, joined = rest
    weights = (wq_ref, wk_ref, wv_ref)
    ups = (up_qk_ref[0], up_qk_ref[1], up_value_ref[...])
    for p in range(3):
        joined[:width, bounds[p] : bounds[p + 1]] = weights[p][...]
        joined[width:, bounds[p] : bounds[p + 1]] = ups[p]

    def projections(rows, table, store):
        chosen = chosen_columns(table, sets_ref[...])
        product = nt(rows, down_mix_ref[...])
        inner = [masked(product[:, p * low_rank : (p + 1) * low_rank], chosen) for p in range(3)]
        for p in range(3):
            store[:, bounds[p] : bounds[p + 1]] = low(
                nn(
                    jnp.concatenate([rows, inner[p]], axis=1),
                    joined[:, bounds[p] : bounds[p + 1]],
                )
            )
        return product, inner

    if with_halo:
        projections(halo_ref[...], halo_table_ref[...], pre_halo_ref)
    table = table_ref[...]
    product, inner = projections(rows_ref[...], table, pre_ref)
    for p in range(3):
        inner_ref[:, p * low_rank : (p + 1) * low_rank] = inner[p]
    column_ref[...] = jnp.concatenate(
        [product[:, 3 * low_rank : 3 * low_rank + 4], table[:, :4]], axis=1
    )


def gate_kernel(
    rows_ref, table_ref, sets_ref, down_ref, wg_ref, up_ref, gate_ref, inner_ref, joined
):
    width = wg_ref.shape[0]

    @at_start
    def _():
        joined[:width, :] = wg_ref[...]
        joined[width:, :] = up_ref[...]

    rows = rows_ref[...]
    inner = masked(nt(rows, down_ref[...]), chosen_columns(table_ref[...], sets_ref[...]))
    inner_ref[...] = inner
    gate_ref[...] = nn(jnp.concatenate([rows, inner], axis=1), joined[...])


def head_outputs(raw_ref, map_ref, entering_ref, heads, key_width, value_width):
    outputs = []
    for h in range(heads):
        outputs.append(
            raw_ref[:, h * value_width : (h + 1) * value_width]
            + nn(map_ref[:, h * key_width : (h + 1) * key_width], entering_ref[h])
        )
    return outputs


def attend_kernel(
    raw_ref, map_ref, gate_ref, table_ref, gain_ref, sets_ref, wo_ref, down_ref, up_ref, *rest,
    heads, key_width, value_width, hops,
):
    got_refs, rest = rest[:hops], rest[hops:]
    part_ref, z_ref, inner_ref, entering_ref, joined = rest
    value_lanes = wo_ref.shape[0]

    @at_start
    def _():
        joined[:value_lanes, :] = wo_ref[...]
        joined[value_lanes:, :] = up_ref[...]
        for h in range(heads):
            state = got_refs[hops - 1][h].astype(single)
            for hop in range(hops - 1, 0, -1):
                got = got_refs[hop - 1][h]
                state = got[:, :value_width].astype(single) + nn(got[:, value_width:], low(state))
            entering_ref[h] = low(state)

    chosen = chosen_columns(table_ref[...], sets_ref[...])
    outputs = head_outputs(raw_ref, map_ref, entering_ref, heads, key_width, value_width)
    parts = []
    for h, output in enumerate(outputs):
        lanes = slice(h * value_width, (h + 1) * value_width)
        scale = lax.rsqrt(jnp.mean(output * output, axis=-1, keepdims=True) + EPS)
        _, gate = silu_parts(gate_ref[:, lanes])
        parts.append(low(output * scale * gain_ref[0:1, :] * gate))
    z = jnp.concatenate(parts, axis=1)
    z_ref[...] = z
    inner = masked(nt(z, down_ref[...]), chosen)
    inner_ref[...] = inner
    part_ref[...] = low(nn(jnp.concatenate([z, inner], axis=1), joined[...]))


def feed_before_kernel(
    grad_ref, table_ref, sets_ref, wd_ref, down_ffd_t_ref, up_ref, hidden_grad_ref, du_ref, joined
):
    hidden, width = wd_ref.shape

    @at_start
    def _():
        joined[:hidden, :width] = wd_ref[...]
        joined[:hidden, width:] = down_ffd_t_ref[...]
        joined[hidden:, :] = jnp.zeros((joined.shape[0] - hidden, joined.shape[1]), bfloat)

    grad = grad_ref[...]
    du_down = masked(nt(grad, up_ref[...]), chosen_columns(table_ref[...], sets_ref[...]))
    du_ref[...] = du_down
    hidden_grad_ref[...] = nt(jnp.concatenate([grad, du_down], axis=1), joined[...])


def feed_kernel(
    rows_ref, hidden_grad_ref, table_ref, sets_ref, down_ref, wg_ref, wu_ref, up_t_ref, up_ref,
    back_ref, hidden_ref, ff_grad_ref, inner_ref, du_ref,
    joined_gate, joined_up, joined_back,
):
    low_rank = sets_ref.shape[1]
    hidden, width = wg_ref.shape
    padded = joined_gate.shape[0]

    @at_start
    def _():
        for p, (joined, weight) in enumerate(((joined_gate, wg_ref), (joined_up, wu_ref))):
            joined[:hidden, :width] = weight[...]
            joined[:hidden, width:] = up_t_ref[p]
            joined[hidden:, :] = jnp.zeros((padded - hidden, joined.shape[1]), bfloat)
            joined_back[p * padded : p * padded + hidden, :] = weight[...]
            joined_back[p * padded + hidden : (p + 1) * padded, :] = jnp.zeros(
                (padded - hidden, width), bfloat
            )
        joined_back[2 * padded :, :] = down_ref[...]

    chosen = chosen_columns(table_ref[...], sets_ref[...])
    both = jnp.concatenate([chosen, chosen], axis=1)
    rows = rows_ref[...]
    inner = masked(nt(rows, down_ref[...]), both)
    inner_ref[...] = inner
    gate = nt(jnp.concatenate([rows, inner[:, :low_rank]], axis=1), joined_gate[...])
    up = nt(jnp.concatenate([rows, inner[:, low_rank:]], axis=1), joined_up[...])
    logistic, active = silu_parts(gate)
    hidden_ref[...] = low(active * up)
    hidden_grad = hidden_grad_ref[...]
    gate_grad = low(hidden_grad * up * logistic * (1.0 + gate * (1.0 - logistic)))
    up_grad = low(hidden_grad * active)
    du_gate = masked(nt(gate_grad, up_ref[0]), chosen)
    du_up = masked(nt(up_grad, up_ref[1]), chosen)
    du_ref[:, :low_rank] = du_gate
    du_ref[:, low_rank:] = du_up
    ff_grad_ref[:, :padded] = gate_grad
    ff_grad_ref[:, padded:] = up_grad
    back_ref[...] = low(
        nn(jnp.concatenate([gate_grad, up_grad, du_gate, du_up], axis=1), joined_back[...])
    )


def feed_after_kernel(
    rows_ref, grad_ref, hidden_ref, ff_grad_ref, inner_ref, du_ref, du_down_ref, table_ref,
    sets_ref, place_ref, wd_ref, down_ffd_ref, up_ref,
    out_ref, own_ref, far_ref, pair_ref, flat_ref,
    joined, down_sum, res_sum, flat_sum,
):
    first = pl.program_id(0) == 0
    low_rank = sets_ref.shape[1]
    width_hidden = wd_ref.shape[0]
    padded = down_ffd_ref.shape[1]

    @at_start
    def _():
        joined[:width_hidden, :] = wd_ref[...]
        joined[width_hidden:padded, :] = jnp.zeros(
            (padded - width_hidden, joined.shape[1]), bfloat
        )
        joined[padded:, :] = up_ref[...]

    hidden = hidden_ref[...]
    inner = inner_ref[...]
    u_down = masked(
        nt(hidden, down_ffd_ref[...]), chosen_columns(table_ref[...], sets_ref[...])
    )
    out_ref[...] = low(nn(jnp.concatenate([hidden, u_down], axis=1), joined[...]))
    accumulate(down_sum, tn(du_ref[...], rows_ref[...]), first)
    accumulate(res_sum, tn(u_down, grad_ref[...]), first)
    for k, grown in enumerate(
        (
            tn(inner[:, :low_rank], ff_grad_ref[:, :padded]),
            tn(inner[:, low_rank:], ff_grad_ref[:, padded:]),
            tn(du_down_ref[...], hidden),
        )
    ):
        accumulate(flat_sum.at[:, k * padded : (k + 1) * padded], grown, first)

    @at_end
    def _():
        flat_ref[...] = low(flat_sum[...])
        emit_blocks(
            (down_sum.at[:low_rank], down_sum.at[low_rank:], res_sum),
            place_ref[0], own_ref, far_ref, pair_ref,
        )


def branch_kernel(
    branch_ref, raw_ref, map_ref, gate_ref, table_ref, entering_ref, gain_ref, sets_ref, wo_ref,
    down_out_t_ref, up_ref, up_gate_ref, *rest,
    heads, key_width, value_width, hops, last,
):
    if last:
        before_ref, *rest = rest
        got_refs, rest = rest[: hops - 1], rest[hops - 1 :]
        raw_grad_ref, gate_grad_ref, du_out_ref, du_gate_ref, *rest = rest
        sent_refs, (joined,) = rest[:hops], rest[hops:]
    else:
        raw_grad_ref, gate_grad_ref, du_out_ref, du_gate_ref, total_ref, joined = rest
    width = wo_ref.shape[1]

    @at_start
    def _():
        joined[:, :width] = wo_ref[...]
        joined[:, width:] = down_out_t_ref[...]

    chosen = chosen_columns(table_ref[...], sets_ref[...])
    branch = branch_ref[...]
    outputs = head_outputs(raw_ref, map_ref, entering_ref, heads, key_width, value_width)
    du_out = masked(nt(branch, up_ref[...]), chosen)
    du_out_ref[...] = du_out
    mixed_grad = nt(jnp.concatenate([branch, du_out], axis=1), joined[...])
    gain = gain_ref[0:1, :]
    gate_grads = []
    for h, output in enumerate(outputs):
        lanes = slice(h * value_width, (h + 1) * value_width)
        scale = lax.rsqrt(jnp.mean(output * output, axis=-1, keepdims=True) + EPS)
        value = gate_ref[:, lanes]
        logistic, active = silu_parts(value)
        incoming = mixed_grad[:, lanes]
        gate_grads.append(
            low(
                incoming
                * (output * scale * gain)
                * (logistic * (1.0 + value * (1.0 - logistic)))
            )
        )
        scaled = gain * (incoming * active)
        dot = jnp.mean(output * scaled, axis=-1, keepdims=True)
        raw_grad = low(scale * scaled - output * (scale * scale * scale * dot))
        raw_grad_ref[:, lanes] = raw_grad
        grown = tn(map_ref[:, h * key_width : (h + 1) * key_width], raw_grad)
        if not last:
            total_ref[h] = grown
        else:
            passed = low(before_ref[h] + grown)
            sent_refs[0][h] = passed
            for hop in range(1, hops):
                passed = low(tn(got_refs[hop - 1][h][:, value_width:], passed))
                sent_refs[hop][h] = passed
    gate_grad = jnp.concatenate(gate_grads, axis=1)
    gate_grad_ref[...] = gate_grad
    du_gate_ref[...] = masked(nt(gate_grad, up_gate_ref[...]), chosen)


def branch_after_kernel(
    branch_ref, z_ref, u_out_ref, rows_ref, inner_ref, du_out_ref, du_gate_ref, gate_grad_ref,
    down_grad_ref, res_grad_ref, flat_ref,
    flat_sum,
):
    lanes = z_ref.shape[1]
    accumulate(down_grad_ref, tn(du_gate_ref[...], rows_ref[...]), True)
    accumulate(res_grad_ref, tn(u_out_ref[...], branch_ref[...]), True)
    accumulate(flat_sum.at[:, :lanes], tn(du_out_ref[...], z_ref[...]), True)
    accumulate(flat_sum.at[:, lanes:], tn(inner_ref[...], gate_grad_ref[...]), True)

    @at_end
    def _():
        flat_ref[...] = low(flat_sum[...])


def settled_rows(pre_ref, tail_ref, arrived_ref, place_ref, quarter, window):
    block = window.shape[0]
    start = ((3 ^ place_ref[0]) + 1) * quarter - HALO - pl.program_id(0) * block
    window[...] = pre_ref[...]

    @pl.when((start >= 0) & (start < block))
    def _():
        window[pl.ds(pl.multiple_of(start, HALO), HALO), :] = low(tail_ref[...] + arrived_ref[...])

    return window[...]


def settle_grads_kernel(
    pre_ref, rows_ref, inner_ref, table_ref, tail_ref, arrived_ref, place_ref, sets_ref,
    up_qk_ref, up_value_ref, down_late_ref, res_late_ref,
    du_ref, own_ref, far_ref, pair_ref, flat_ref,
    window, down_sum, flat_sum,
    *, quarter,
):
    low_rank = sets_ref.shape[1]
    q_width = up_qk_ref.shape[2]
    chosen = chosen_columns(table_ref[...], sets_ref[...])
    pre = settled_rows(pre_ref, tail_ref, arrived_ref, place_ref, quarter, window)
    query, key, value = pre[:, :q_width], pre[:, q_width : 2 * q_width], pre[:, 2 * q_width :]
    inner = inner_ref[...]
    du = jnp.concatenate(
        [
            masked(nt(query, up_qk_ref[0]), chosen),
            masked(nt(key, up_qk_ref[1]), chosen),
            masked(nt(value, up_value_ref[...]), chosen),
        ],
        axis=1,
    )
    du_ref[...] = du
    accumulate(down_sum, tn(du, rows_ref[...]), True)
    at = 0
    for p, part in enumerate((query, key, value)):
        accumulate(
            flat_sum.at[:, at : at + part.shape[1]],
            tn(inner[:, p * low_rank : (p + 1) * low_rank], part),
            True,
        )
        at += part.shape[1]

    @at_end
    def _():
        flat_ref[...] = low(flat_sum[...])
        emit_blocks(
            [down_sum.at[p * low_rank : (p + 1) * low_rank] for p in range(3)]
            + [down_late_ref, res_late_ref],
            place_ref[0], own_ref, far_ref, pair_ref,
        )


def settle_kernel(
    pre_ref, gate_grad_ref, du_ref, du_gate_ref, mix_ref, tail_ref, arrived_ref, place_ref,
    down_mix_ref, wq_ref, wk_ref, wv_ref, wg_ref,
    part_ref,
    window, joined,
    *, quarter,
):
    q_width, v_width = wq_ref.shape[1], wv_ref.shape[1]

    @at_start
    def _():
        joined[:, :q_width] = wq_ref[...]
        joined[:, q_width : 2 * q_width] = wk_ref[...]
        joined[:, 2 * q_width : 2 * q_width + v_width] = wv_ref[...]
        joined[:, 2 * q_width + v_width :] = wg_ref[...]

    pre = settled_rows(pre_ref, tail_ref, arrived_ref, place_ref, quarter, window)
    mix = low(mix_ref[...])
    spare = down_mix_ref.shape[0] - du_ref.shape[1] - du_gate_ref.shape[1] - mix.shape[1]
    small = jnp.concatenate(
        [du_ref[...], mix, jnp.zeros((mix.shape[0], spare), bfloat), du_gate_ref[...]], axis=1
    )
    part_ref[...] = low(
        nt(jnp.concatenate([pre, gate_grad_ref[...]], axis=1), joined[...])
        + nn(small, down_mix_ref[...])
    )


def assemble_kernel(
    place_ref, *refs, padded,
):
    pieces_last, pieces_feed = refs[:4], refs[4:8]
    last_ref, feed_ref, branch_ref = refs[8:11]
    down_ref, qk_ref, vg_ref, ff_ref, out_ref, ffd_ref, res_ref = refs[11:]
    place = place_ref[0]
    size = pieces_last[0].shape[1] // 5
    first = [down_ref.at[p] for p in range(4)] + [res_ref.at[0]]
    second = [down_ref.at[4], down_ref.at[5], res_ref.at[1]]
    for relative in range(4):
        start = pl.multiple_of((place ^ relative) * size, 128)
        for targets, piece in ((first, pieces_last[relative]), (second, pieces_feed[relative])):
            for k, target in enumerate(targets):
                target[:, pl.ds(start, size)] = piece[:, k * size : (k + 1) * size].astype(single)
    qk, values, hidden = qk_ref.shape[2], vg_ref.shape[2], ff_ref.shape[2]

    def lanes(ref, start, width):
        return ref[:, start : start + width].astype(single)

    own = 5 * size
    qk_ref[0], qk_ref[1] = lanes(last_ref, own, qk), lanes(last_ref, own + qk, qk)
    vg_ref[0] = lanes(last_ref, own + 2 * qk, values)
    at = last_ref.shape[1]
    out_ref[...] = lanes(branch_ref, at, values)
    vg_ref[1] = lanes(branch_ref, at + values, values)
    own = 3 * size
    ff_ref[0] = lanes(feed_ref, own, hidden)
    ff_ref[1] = lanes(feed_ref, own + padded, hidden)
    ffd_ref[...] = lanes(feed_ref, own + 2 * padded, hidden)


def assemble(where, shared, last, feed, branch, padded, shapes):
    rows = last.shape[0]
    block = min(32, rows)

    def spec(shape):
        if len(shape) == 2:
            return pl.BlockSpec((block, shape[1]), lambda i: (i, 0))
        return pl.BlockSpec((shape[0], block, shape[2]), lambda i: (0, i, 0))

    arrays = [*shared, last, feed, branch]
    return pl.pallas_call(
        functools.partial(assemble_kernel, padded=padded),
        out_shape=tuple(jax.ShapeDtypeStruct(shape, single) for shape in shapes),
        grid=(rows // block,),
        in_specs=[pl.BlockSpec(memory_space=pltpu.SMEM)] + [spec(a.shape) for a in arrays],
        out_specs=[spec(shape) for shape in shapes],
        compiler_params=pltpu.CompilerParams(
            dimension_semantics=("arbitrary",), vmem_limit_bytes=VMEM_LIMIT
        ),
        name="assemble",
    )(where, *arrays)


WHOLE, SCALAR = "whole", "scalar"


def by_rows(width, lane_block=0):
    return ("rows", width, lane_block)


def pieces(width):
    return ("pieces", width)


def blocked_call(
    body, name, count, inputs, outputs, scratch, flops, block=STEP, half=None, into=()
):
    if half is not None:
        block = count // 2
    steps = count // block if half is None else 1
    offset = half or 0
    per = max(steps // 4, 1)
    in_specs, arrays, moved, groups_in, extra = [], [], 0, [], []
    for array, kind in inputs:
        members = array if isinstance(array, (list, tuple)) else [array]
        groups_in.append(len(members))
        arrays += members
        moved += sum(a.size * a.dtype.itemsize for a in members)
        if kind == WHOLE:
            zeros = (0,) * array.ndim
            in_specs.append(
                pl.BlockSpec(
                    array.shape, lambda i, zeros=zeros: zeros, pipeline_mode=pl.Buffered(1)
                )
            )
        elif kind == SCALAR:
            in_specs.append(pl.BlockSpec(memory_space=pltpu.SMEM))
        elif kind[0] == "rows":
            in_specs.append(
                pl.BlockSpec((block, kind[1]), lambda i, lane=kind[2]: (i + offset, lane))
            )
        else:
            for b, member in enumerate(members):
                if steps == 1:
                    in_specs.append(pl.BlockSpec(member.shape, lambda i: (0, 0)))
                else:
                    in_specs.append(
                        pl.BlockSpec(
                            (block, kind[1]),
                            lambda i, b=b: (jnp.clip(i - b * per, 0, per - 1), 0),
                        )
                    )
            extra.append(pltpu.VMEM((block, kind[1]), members[0].dtype))
    out_specs, shapes, groups_out, aliases = [], [], [], {}
    into = list(into)
    held_arrays = []
    for shape, dtype, kind in outputs:
        if kind == "parts":
            quarter = shape[0] // 4
            spec = (block, shape[1])
            if steps == 1:
                for _ in range(2):
                    shapes.append(jax.ShapeDtypeStruct((quarter, shape[1]), dtype))
                    out_specs.append(pl.BlockSpec((quarter, shape[1]), lambda i: (0, 0)))
                groups_out.append(2)
            else:
                for rows in (quarter, quarter, 2 * quarter):
                    shapes.append(jax.ShapeDtypeStruct((rows, shape[1]), dtype))
                out_specs += [
                    pl.BlockSpec(spec, lambda i: (jnp.clip(i, 0, per - 1), 0)),
                    pl.BlockSpec(spec, lambda i: (jnp.clip(i - 2 * per, 0, per - 1), 0)),
                    pl.BlockSpec(
                        spec,
                        lambda i: (
                            jnp.clip(i - per, 0, per - 1) + jnp.clip(i - 3 * per + 1, 0, per), 0
                        ),
                    ),
                ]
                groups_out.append(3)
            extra.append(pltpu.VMEM(spec, dtype))
        else:
            groups_out.append(1)
            shapes.append(jax.ShapeDtypeStruct(shape, dtype))
            if kind == "rows":
                if into:
                    aliases[len(arrays) + len(held_arrays)] = len(shapes) - 1
                    held_arrays.append(into.pop(0))
                out_specs.append(pl.BlockSpec((block, shape[1]), lambda i: (i + offset, 0)))
            else:
                zeros = (0,) * len(shape)
                out_specs.append(pl.BlockSpec(shape, lambda i, zeros=zeros: zeros))
    in_specs += [pl.BlockSpec(memory_space=pl.ANY) for _ in held_arrays]

    def wrapped(*refs):
        refs = list(refs)
        spare = refs[len(in_specs) + len(out_specs) + len(scratch) :]
        own_scratch = refs[len(in_specs) + len(out_specs) : len(refs) - len(spare)]
        quarter = pl.program_id(0) // per
        given, later, at, used = [], [], 0, 0
        for size, (_, kind) in zip(groups_in, inputs):
            if kind[0] != "pieces":
                given.append(refs[at])
            else:
                held = spare[used]
                used += 1
                if steps == 1:
                    for b in range(size):
                        piece = refs[at + b]
                        held[b * piece.shape[0] : (b + 1) * piece.shape[0], :] = piece[...]
                else:
                    for b in range(size):

                        @pl.when(quarter == b)
                        def _(held=held, source=refs[at + b]):
                            held[...] = source[...]

                given.append(held)
            at += size
        at += len(held_arrays)
        for size in groups_out:
            if size == 1:
                given.append(refs[at])
            else:
                given.append(spare[used])
                later.append((spare[used], refs[at : at + size]))
                used += 1
            at += size
        body(*given, *own_scratch)
        for held, targets in later:
            if len(targets) == 2:
                rows = targets[0].shape[0]
                targets[0][...], targets[1][...] = held[:rows, :], held[rows:, :]
                continue
            for b, target in ((0, targets[0]), (2, targets[1]), (1, targets[2]), (3, targets[2])):

                @pl.when(quarter == b)
                def _(held=held, target=target):
                    target[...] = held[...]

    results = pl.pallas_call(
        wrapped,
        out_shape=tuple(shapes),
        grid=(steps,),
        in_specs=in_specs,
        out_specs=out_specs,
        scratch_shapes=list(scratch) + extra,
        input_output_aliases=aliases,
        compiler_params=pltpu.CompilerParams(
            dimension_semantics=("arbitrary",), vmem_limit_bytes=VMEM_LIMIT
        ),
        cost_estimate=pl.CostEstimate(flops=flops, bytes_accessed=moved, transcendentals=0),
        name=name,
    )(*arrays, *held_arrays)
    grouped, at = [], 0
    for size in groups_out:
        grouped.append(results[at] if size == 1 else results[at : at + size])
        at += size
    return grouped


def flip(array, bit):
    groups = lax.axis_size("head")
    return lax.ppermute(array, "head", [(i, i ^ bit) for i in range(groups)])


def gather_rows(array):
    far = flip(array, 2)
    near = flip(array, 1)
    return [array, near, far, flip(far, 1)]


def tie(*arrays):
    return lax.optimization_barrier(arrays)


def near_sum(parts):
    own, far, pair = parts
    size = own.shape[0]
    arrived = flip(pair, 1)
    return (
        own.astype(single) + arrived[:size].astype(single),
        low(far.astype(single) + arrived[size:].astype(single)),
    )


def halves_sum(first, second):
    near, corner = tie(flip(first[1], 1), second[1])
    return (
        first[0].astype(single) + near.astype(single),
        low(second[0].astype(single) + flip(corner, 1).astype(single)),
    )


def far_sum(own, far):
    return own + flip(far, 2).astype(single)


def shifted_along(array, axis, by):
    length = lax.axis_size(axis)
    pairs = [(i, i + by) for i in range(length) if 0 <= i + by < length]
    return lax.ppermute(array, axis, pairs)


def seq_rows(flat):
    members = lax.axis_size("seq")
    return flat.reshape(members, flat.shape[0] // members, flat.shape[1])


def share_sum(parts):
    summed = low(jnp.sum(parts.astype(single), axis=0))
    return jnp.broadcast_to(summed[None], parts.shape)


def exchange(parts):
    return lax.all_to_all(parts, "seq", 0, 0)


def all_rows(parts):
    return parts.reshape(-1, parts.shape[-1])


def rms_scale(rows, gain):
    return rows * lax.rsqrt(jnp.mean(rows * rows, axis=-1, keepdims=True) + EPS) * gain


def rms_back(rows, gain, incoming):
    _, back = jax.vjp(lambda value: rms_scale(value, gain), rows)
    return back(incoming)[0]


def on_device(
    block_input,
    out_grad,
    lengths,
    doc_sets,
    norm1_gain,
    w_query,
    w_key,
    w_value,
    conv_query,
    conv_key,
    conv_value,
    w_decay_beta,
    decay_rate,
    decay_bias,
    w_gate_out,
    out_gain,
    w_out,
    norm2_gain,
    w_gate,
    w_up,
    w_down,
    adapt_down,
    adapt_up_qk,
    adapt_up_vg,
    adapt_up_ff,
    adapt_down_out,
    adapt_down_ffd,
    adapt_up_res,
):
    groups = lax.axis_size("head")
    members = lax.axis_size("seq")
    place = lax.axis_index("head")
    quarter, width = block_input.shape
    count = quarter * groups
    heads = decay_rate.shape[0]
    key_width = w_query.shape[1] // heads
    value_width = w_value.shape[1] // heads
    sets, rank = adapt_down.shape[1], adapt_down.shape[3]
    low_rank = sets * rank
    qk = heads * key_width
    device_start = lax.axis_index("seq") * count
    starts = jnp.sum(
        jnp.where(
            jnp.arange(lengths.shape[0])[None, :] < jnp.arange(lengths.shape[0])[:, None],
            lengths[None, :],
            0,
        ),
        axis=1,
    )
    order = jnp.arange(groups, dtype=jnp.int32) ^ place

    def tables(positions):
        reached = positions[:, None] >= starts[None, :]
        token_start = jnp.max(jnp.where(reached, starts[None, :], -1), axis=1)
        ended = positions[:, None] >= (starts + lengths)[None, :]
        token_set = jnp.sum(jnp.where(reached & ~ended, doc_sets[None, :], 0), axis=1)
        pair = jnp.stack([token_start - device_start, token_set], axis=1).astype(single)
        return jnp.pad(pair, ((0, 0), (0, 8 - pair.shape[1])))

    table = tables(
        (
            device_start + order[:, None] * quarter + jnp.arange(quarter, dtype=jnp.int32)[None, :]
        ).reshape(-1)
    )
    halo_table = tables(device_start + jnp.arange(-HALO, 0, dtype=jnp.int32))
    column_sets = jnp.broadcast_to(
        (jnp.arange(low_rank, dtype=jnp.int32) // rank).astype(single)[None, :], (8, low_rank)
    )

    down = adapt_down.transpose(0, 1, 3, 2).reshape(6 * low_rank, width)
    mixer_down, feed_down = down[: 4 * low_rank], down[4 * low_rank :]
    up_qk = adapt_up_qk.reshape(2, low_rank, -1)
    up_vg = adapt_up_vg.reshape(2, low_rank, -1)
    up_ff = adapt_up_ff.reshape(2, low_rank, -1)
    down_out = adapt_down_out.transpose(0, 2, 1).reshape(low_rank, -1)
    down_ffd = adapt_down_ffd.transpose(0, 2, 1).reshape(low_rank, -1)
    up_res = adapt_up_res.reshape(2, low_rank, width)
    conv = jnp.concatenate([conv_query, conv_key, conv_value], axis=1).astype(single)
    scalars = jnp.stack([decay_rate, decay_bias])
    where = place.reshape(1).astype(jnp.int32)
    down_mix = jnp.concatenate(
        [
            mixer_down[: 3 * low_rank],
            w_decay_beta.transpose(1, 2, 0).reshape(2 * heads, width),
            jnp.zeros((low_rank - 2 * heads, width), bfloat),
            mixer_down[3 * low_rank :],
        ],
        axis=0,
    )
    gain = jnp.broadcast_to(out_gain[None, :], (8, value_width))
    hidden_width = w_down.shape[0]
    padded = -(-hidden_width // 256) * 256
    value_lanes = heads * value_width
    block_width = width // groups
    widen = lambda a: jnp.pad(a, [(0, 0)] * (a.ndim - 1) + [(0, padded - hidden_width)])
    up_ff_padded, down_ffd_padded = widen(up_ff), widen(down_ffd)

    input_float = block_input.astype(single)
    normed = low(rms_scale(input_float, norm1_gain))
    tail = normed[quarter - HALO :]
    halo = sum(
        lax.ppermute(
            tail,
            ("seq", "head"),
            [((s * groups) + groups - 1, (s + 1) * groups + h) for s in range(members - 1)],
        )
        for h in range(groups)
    )
    normed_near, normed_far = flip(normed, 1), flip(normed, 2)
    project_inputs = [
        (table, by_rows(8)),
        (column_sets, WHOLE),
        (down_mix[: 4 * low_rank], WHOLE),
        (w_query, WHOLE),
        (w_key, WHOLE),
        (w_value, WHOLE),
        (up_qk, WHOLE),
        (up_vg[0], WHOLE),
    ]
    project_outputs = [
        ((count, 2 * qk + value_lanes), bfloat, "rows"),
        ((count, 3 * low_rank), bfloat, "rows"),
        ((count, 8), single, "rows"),
    ]
    project_scratch = [pltpu.VMEM((width + low_rank, 2 * qk + value_lanes), bfloat)]
    projected = blocked_call(
        functools.partial(project_kernel, with_halo=False),
        "project_near",
        count,
        [([normed, normed_near], pieces(width)), *project_inputs],
        project_outputs,
        project_scratch,
        count * 2_000_000,
        half=0,
    )
    normed_far, projected[2] = tie(normed_far, projected[2])
    normed_all = [normed, normed_near, normed_far, flip(normed_far, 1)]
    pre, inner, columns, pre_halo = blocked_call(
        functools.partial(project_kernel, with_halo=True),
        "project_far",
        count,
        [
            (normed_all[2:], pieces(width)),
            *project_inputs,
            (halo, WHOLE),
            (halo_table, WHOLE),
        ],
        project_outputs + [((HALO, 2 * qk + value_lanes), bfloat, "whole")],
        project_scratch,
        count * 2_000_000,
        half=1,
        into=projected,
    )
    out_grad_late, pre = tie(out_grad, pre)
    grad_near, grad_far = flip(out_grad_late, 1), flip(out_grad_late, 2)
    raw_local, mapped, *saved, sent, sent_state = run_forward(
        where, pre, pre_halo, columns, conv, scalars, heads, key_width, value_width, quarter
    )

    hops = min(members - 1, -(-(DOC_MAX - 1) // count))
    got = [shifted_along(sent, "seq", hop) for hop in range(1, hops)]
    got.append(shifted_along(sent_state, "seq", hops))
    grad_near, grad_far, sent_state = tie(grad_near, grad_far, sent_state)
    grad_all = [out_grad, grad_near, grad_far, flip(grad_far, 1)]
    hidden_grad, du_down = blocked_call(
        feed_before_kernel,
        "feed_before",
        count,
        [
            (grad_all, pieces(width)),
            (table, by_rows(8)),
            (column_sets, WHOLE),
            (w_down, WHOLE),
            (down_ffd.T, WHOLE),
            (up_res[1], WHOLE),
        ],
        [((count, padded), single, "rows"), ((count, low_rank), bfloat, "rows")],
        [pltpu.VMEM((padded, width + low_rank), bfloat)],
        count * 6_000_000,
    )
    gate_rows, sent_state = tie(normed_all[0], sent_state)
    gate_input, inner_gate = blocked_call(
        gate_kernel,
        "gate",
        count,
        [
            ([gate_rows, *normed_all[1:]], pieces(width)),
            (table, by_rows(8)),
            (column_sets, WHOLE),
            (mixer_down[3 * low_rank :], WHOLE),
            (w_gate_out, WHOLE),
            (up_vg[1], WHOLE),
        ],
        [((count, value_lanes), single, "rows"), ((count, low_rank), bfloat, "rows")],
        [pltpu.VMEM((width + low_rank, value_lanes), bfloat)],
        count * 3_000_000,
    )
    raw_local, hidden_grad = tie(raw_local, hidden_grad)

    sizes = dict(heads=heads, key_width=key_width, value_width=value_width)
    attention_part, mixed, u_out, entering = blocked_call(
        functools.partial(attend_kernel, hops=hops, **sizes),
        "attend",
        count,
        [
            (raw_local, by_rows(value_lanes)),
            (mapped, by_rows(qk)),
            (gate_input, by_rows(value_lanes)),
            (table, by_rows(8)),
            (gain, WHOLE),
            (column_sets, WHOLE),
            (w_out, WHOLE),
            (down_out, WHOLE),
            (up_res[0], WHOLE),
        ]
        + [(part, WHOLE) for part in got],
        [
            ((count, width), bfloat, "parts"),
            ((count, value_lanes), bfloat, "rows"),
            ((count, low_rank), bfloat, "rows"),
            ((heads, key_width, value_width), bfloat, "whole"),
        ],
        [pltpu.VMEM((value_lanes + low_rank, width), bfloat)],
        count * 5_000_000,
    )
    attention_own, attention_far = near_sum(attention_part)
    residual = input_float + far_sum(attention_own, attention_far)
    normed_mid = low(rms_scale(residual, norm2_gain))
    mid_near, mid_far = flip(normed_mid, 1), flip(normed_mid, 2)

    feed_inputs = [
        (hidden_grad, by_rows(padded)),
        (table, by_rows(8)),
        (column_sets, WHOLE),
        (feed_down, WHOLE),
        (w_gate.T, WHOLE),
        (w_up.T, WHOLE),
        (up_ff.transpose(0, 2, 1), WHOLE),
        (up_ff_padded, WHOLE),
    ]
    feed_outputs = [
        ((count, width), bfloat, "parts"),
        ((count, padded), bfloat, "rows"),
        ((count, 2 * padded), bfloat, "rows"),
        ((count, 2 * low_rank), bfloat, "rows"),
        ((count, 2 * low_rank), bfloat, "rows"),
    ]
    feed_scratch = [
        pltpu.VMEM((padded, width + low_rank), bfloat),
        pltpu.VMEM((padded, width + low_rank), bfloat),
        pltpu.VMEM((2 * padded + 2 * low_rank, width), bfloat),
    ]
    near_part, *fed = blocked_call(
        feed_kernel,
        "feed_near",
        count,
        [([normed_mid, mid_near], pieces(width)), *feed_inputs],
        feed_outputs,
        feed_scratch,
        count * 8_000_000,
        half=0,
    )
    mid_far, near_own = tie(mid_far, near_part[0])
    near_part = [near_own, near_part[1]]
    mid_all = [normed_mid, mid_near, mid_far, flip(mid_far, 1)]
    far_part, hidden, ff_grad, u_ff, du_ff = blocked_call(
        feed_kernel,
        "feed_far",
        count,
        [(mid_all[2:], pieces(width)), *feed_inputs],
        feed_outputs,
        feed_scratch,
        count * 8_000_000,
        half=1,
        into=fed,
    )
    grad_own, grad_sum = halves_sum(near_part, far_part)
    grad_sum, hidden = tie(grad_sum, hidden)
    grad_arrived = flip(grad_sum, 2)
    mid_grad = grad_own + grad_arrived.astype(single)
    out_part, feed_own, feed_far, feed_pair, feed_owned = blocked_call(
        feed_after_kernel,
        "feed_after",
        count,
        [
            (mid_all, pieces(width)),
            (grad_all, pieces(width)),
            (hidden, by_rows(padded)),
            (ff_grad, by_rows(2 * padded)),
            (u_ff, by_rows(2 * low_rank)),
            (du_ff, by_rows(2 * low_rank)),
            (du_down, by_rows(low_rank)),
            (table, by_rows(8)),
            (column_sets, WHOLE),
            (where, SCALAR),
            (w_down, WHOLE),
            (down_ffd_padded, WHOLE),
            (up_res[1], WHOLE),
        ],
        [
            ((count, width), bfloat, "parts"),
            ((low_rank, 3 * block_width), bfloat, "whole"),
            ((low_rank, 3 * block_width), bfloat, "whole"),
            ((2 * low_rank, 3 * block_width), bfloat, "whole"),
            ((low_rank, 3 * padded), bfloat, "whole"),
        ],
        [
            pltpu.VMEM((padded + low_rank, width), bfloat),
            pltpu.VMEM((2 * low_rank, width), single),
            pltpu.VMEM((low_rank, width), single),
            pltpu.VMEM((low_rank, 3 * padded), single),
        ],
        count * 16_000_000,
    )
    residual_grad = out_grad.astype(single) + rms_back(residual, norm2_gain, mid_grad)
    branch_low = low(residual_grad)
    branch_near, branch_far = flip(branch_low, 1), flip(branch_low, 2)
    feed_flat = jnp.concatenate(
        [
            low(far_sum(*near_sum((feed_own, feed_far, tie(feed_pair, grad_arrived)[0])))),
            feed_owned,
        ],
        axis=1,
    )
    branch_inputs = [
        (raw_local, by_rows(value_lanes)),
        (mapped, by_rows(qk)),
        (gate_input, by_rows(value_lanes)),
        (table, by_rows(8)),
        (entering, WHOLE),
        (gain, WHOLE),
        (column_sets, WHOLE),
        (w_out, WHOLE),
        (down_out.T, WHOLE),
        (up_res[0], WHOLE),
        (up_vg[1], WHOLE),
    ]
    branch_outputs = [
        ((count, value_lanes), bfloat, "rows"),
        ((count, value_lanes), bfloat, "rows"),
        ((count, low_rank), bfloat, "rows"),
        ((count, low_rank), bfloat, "rows"),
    ]
    branch_scratch = [pltpu.VMEM((value_lanes, width + low_rank), bfloat)]
    state_shape = (heads, key_width, value_width)
    *branched, state_near = blocked_call(
        functools.partial(branch_kernel, hops=hops, last=False, **sizes),
        "branch_near",
        count,
        [([branch_low, branch_near], pieces(width)), *branch_inputs],
        branch_outputs + [(state_shape, single, "whole")],
        branch_scratch,
        count * 4_000_000,
        half=0,
    )
    branch_far, state_near, feed_flat = tie(branch_far, state_near, feed_flat)
    feed_parts = exchange(seq_rows(feed_flat))
    branch_all = [branch_low, branch_near, branch_far, flip(branch_far, 1)]
    raw_grad, gate_grad, du_out, du_outgate, *state_grads = blocked_call(
        functools.partial(branch_kernel, hops=hops, last=True, **sizes),
        "branch_far",
        count,
        [(branch_all[2:], pieces(width)), *branch_inputs, (state_near, WHOLE)]
        + [(part, WHOLE) for part in got[:-1]],
        branch_outputs + [(state_shape, bfloat, "whole")] * hops,
        branch_scratch,
        count * 4_000_000,
        half=1,
        into=branched,
    )
    state_got = [
        shifted_along(part, "seq", -hop) for hop, part in enumerate(state_grads, start=1)
    ]
    du_out, feed_parts, out_pair = tie(du_out, feed_parts, out_part[2])
    out_own, out_far = near_sum((out_part[0], out_part[1], out_pair))
    mixer_down_late, branch_res_grad, branch_flat = blocked_call(
        branch_after_kernel,
        "branch_after",
        count,
        [
            (branch_all, pieces(width)),
            (mixed, by_rows(value_lanes)),
            (u_out, by_rows(low_rank)),
            (normed_all, pieces(width)),
            (inner_gate, by_rows(low_rank)),
            (du_out, by_rows(low_rank)),
            (du_outgate, by_rows(low_rank)),
            (gate_grad, by_rows(value_lanes)),
        ],
        [
            ((low_rank, width), single, "whole"),
            ((low_rank, width), single, "whole"),
            ((low_rank, 2 * value_lanes), bfloat, "whole"),
        ],
        [pltpu.VMEM((low_rank, 2 * value_lanes), single)],
        count * 20_000_000,
        block=count,
    )
    feed_lanes = feed_parts.shape[-1]
    both = jnp.concatenate([share_sum(feed_parts), seq_rows(branch_flat)], axis=2)
    raw_grad, both, out_far, *state_got = tie(raw_grad, both, out_far, *state_got)
    out_arrived = flip(out_far, 2)
    both = exchange(both)

    pre_grad, mix_grad, tail_grad, edge_grad = run_backward(
        where, pre, pre_halo, columns, conv, scalars, raw_grad, saved, entering, state_got,
        heads, key_width, value_width, quarter,
    )
    arrived = shifted_along(edge_grad, "seq", -1)
    arrived, both, out_arrived = tie(arrived, both, out_arrived)
    result = residual + (out_own + out_arrived.astype(single))
    branch_parts = both[:, :, feed_lanes:]
    settled = [
        (pre_grad, by_rows(2 * qk + value_lanes)),
        (tail_grad, WHOLE),
        (arrived, WHOLE),
        (where, SCALAR),
    ]
    du_mix, last_own, last_far, last_pair, last_owned = blocked_call(
        functools.partial(settle_grads_kernel, quarter=quarter),
        "settle_grads",
        count,
        [
            settled[0],
            (normed_all, pieces(width)),
            (inner, by_rows(3 * low_rank)),
            (table, by_rows(8)),
            *settled[1:],
            (column_sets, WHOLE),
            (up_qk, WHOLE),
            (up_vg[0], WHOLE),
            (mixer_down_late, WHOLE),
            (branch_res_grad, WHOLE),
        ],
        [
            ((count, 3 * low_rank), bfloat, "rows"),
            ((low_rank, 5 * block_width), bfloat, "whole"),
            ((low_rank, 5 * block_width), bfloat, "whole"),
            ((2 * low_rank, 5 * block_width), bfloat, "whole"),
            ((low_rank, 2 * qk + value_lanes), bfloat, "whole"),
        ],
        [
            pltpu.VMEM((count, 2 * qk + value_lanes), bfloat),
            pltpu.VMEM((3 * low_rank, width), single),
            pltpu.VMEM((low_rank, 2 * qk + value_lanes), single),
        ],
        count * 4_000_000,
        block=count,
    )
    last_own, last_far = near_sum((last_own, last_far, last_pair))
    last_far, gate_grad = tie(last_far, gate_grad)
    (normed_part,) = blocked_call(
        functools.partial(settle_kernel, quarter=quarter),
        "settle",
        count,
        [
            settled[0],
            (gate_grad, by_rows(value_lanes)),
            (du_mix, by_rows(3 * low_rank)),
            (du_outgate, by_rows(low_rank)),
            (mix_grad, by_rows(8)),
            *settled[1:],
            (down_mix, WHOLE),
            (w_query, WHOLE),
            (w_key, WHOLE),
            (w_value, WHOLE),
            (w_gate_out, WHOLE),
        ],
        [((count, width), bfloat, "parts")],
        [
            pltpu.VMEM((STEP, 2 * qk + value_lanes), bfloat),
            pltpu.VMEM((width, 2 * qk + 2 * value_lanes), bfloat),
        ],
        count * 10_000_000,
    )
    last_flat = jnp.concatenate([low(far_sum(last_own, last_far)), last_owned], axis=1)
    feed_rows = all_rows(both)
    feed_pieces = gather_rows(feed_rows[:, : 3 * block_width])
    last_lanes = last_flat.shape[1]
    both = exchange(jnp.concatenate([seq_rows(last_flat), share_sum(branch_parts)], axis=2))
    branch_rows = all_rows(both)
    last_parts = both[:, :, :last_lanes]
    normed_grad = far_sum(*near_sum(normed_part))
    input_grad = residual_grad + rms_back(input_float, norm1_gain, normed_grad)
    last_parts, *feed_pieces = tie(last_parts, *feed_pieces)
    last_rows = all_rows(exchange(share_sum(last_parts)))
    last_pieces = gather_rows(last_rows[:, : 5 * block_width])
    down_grad, qk_grad, vg_grad, ff_grads, out_grads, ffd_grads, res_grad = assemble(
        where,
        [*last_pieces, *feed_pieces],
        last_rows,
        feed_rows,
        branch_rows,
        padded,
        [
            (6, low_rank, width),
            (2, low_rank, qk),
            (2, low_rank, value_lanes),
            (2, low_rank, hidden_width),
            (low_rank, value_lanes),
            (low_rank, hidden_width),
            (2, low_rank, width),
        ],
    )

    def as_down(rows):
        return rows.reshape(rows.shape[:-2] + (sets, rank, -1)).swapaxes(-1, -2)

    def as_up(rows):
        return rows.reshape(rows.shape[0], sets, rank, -1)

    return (
        low(result),
        input_grad,
        as_down(down_grad),
        as_up(qk_grad),
        as_up(vg_grad),
        as_up(ff_grads),
        as_down(out_grads),
        as_down(ffd_grads),
        as_up(res_grad),
    )


def solution(mesh):
    rows = P(("seq", "head"), None)
    lanes = P(None, "head")
    last = P(None, None, None, "head")
    middle = P(None, "head", None)
    in_specs = (
        rows, rows, P(), P(), P(), lanes, lanes, lanes, lanes, lanes, lanes,
        P(None, None, "head"), P("head"), P("head"), lanes, P(), P("head", None), P(), lanes,
        lanes, P("head", None), P(), last, last, last, middle, middle, P(),
    )
    out_specs = (rows, rows, P(), last, last, last, middle, middle, P())
    return jax.shard_map(
        on_device, mesh=mesh, in_specs=in_specs, out_specs=out_specs, check_vma=False
    )
```

```python
import functools

import jax
import jax.numpy as jnp
from jax import lax
from jax.experimental import pallas as pl
from jax.experimental.pallas import tpu as pltpu
from jax.sharding import PartitionSpec as P

CHUNK = 128
STEP = 256
HALO = 16
DOC_MAX = 4096
EPS = 1e-06
VMEM_LIMIT = 56 * 1024 * 1024
bfloat = jnp.bfloat16
single = jnp.float32


def contract(left, right, left_dim, right_dim):
    return lax.dot_general(
        left,
        right,
        (((left_dim,), (right_dim,)), ((), ())),
        preferred_element_type=single,
    )


def nn(left, right):
    return contract(left, right, 1, 0)


def nt(left, right):
    return contract(left, right, 1, 1)


def tn(left, right):
    return contract(left, right, 0, 0)


def low(array):
    return array.astype(bfloat)


def iotas():
    rows = lax.broadcasted_iota(jnp.int32, (CHUNK, CHUNK), 0)
    columns = lax.broadcasted_iota(jnp.int32, (CHUNK, CHUNK), 1)
    return rows, columns


def split_two(array):
    high = low(array)
    return high, low(array - high.astype(single))


def near_exact(left, right):
    left_high, left_low = split_two(left)
    right_high, right_low = split_two(right)
    return nn(
        jnp.concatenate([left_high, left_high, left_low], axis=1),
        jnp.concatenate([right_high, right_low, right_high], axis=0),
    )


def ones_product(ones, array):
    high = low(array)
    rest = array - high.astype(single)
    middle = low(rest)
    lowest = low(rest - middle.astype(single))
    return nn(
        jnp.concatenate([ones, ones, ones], axis=1),
        jnp.concatenate([high, middle, lowest], axis=0),
    )


def unit_lower_inverses(stricts, rows, columns):
    eye = (rows == columns).astype(single)
    differ = rows ^ columns
    block = 8
    inner = [jnp.where(differ < block, strict, 0.0) for strict in stricts]
    second = [near_exact(a, a) for a in inner]
    inverse = [near_exact(eye - a, eye + b) for a, b in zip(inner, second)]
    fourth = [near_exact(b, b) for b in second]
    inverse = [near_exact(a, eye + b) for a, b in zip(inverse, fourth)]
    while block < CHUNK:
        between = (differ >= block) & (differ < 2 * block)
        off = [jnp.where(between, strict, 0.0) for strict in stricts]
        part = [near_exact(a, b) for a, b in zip(off, inverse)]
        inverse = [a - near_exact(a, b) for a, b in zip(inverse, part)]
        block = 2 * block
    return inverse


def softplus(value):
    return jnp.maximum(value, 0.0) + jnp.log(1.0 + jnp.exp(-jnp.abs(value)))


def sigmoid(value):
    return 1.0 / (1.0 + jnp.exp(-value))


def gates(decay, start, rows, columns):
    lower_ones = low((rows >= columns).astype(single))
    total = ones_product(lower_ones, jnp.broadcast_to(decay, (CHUNK, CHUNK)))
    linked = (rows >= columns) & (columns >= start)
    within = jnp.where(linked, jnp.exp(jnp.where(linked, total - total.T, 0.0)), 0.0)
    running = total[:, :1]
    carried = jnp.where(start < 0, jnp.exp(running), 0.0)
    last = running[CHUNK - 1 : CHUNK]
    ending = jnp.where(
        rows[:, :1] >= start[CHUNK - 1 : CHUNK], jnp.exp(jnp.minimum(last - running, 0.0)), 0.0
    )
    return within, carried, ending


def convolved(window, starts, weights, base):
    positions = base + lax.broadcasted_iota(jnp.int32, (STEP, 1), 0)
    taps = weights.shape[0]
    total = None
    for tap in range(taps):
        back = taps - 1 - tap
        term = window[HALO - back : HALO - back + STEP, :] * weights[tap : tap + 1, :]
        if back:
            term = jnp.where(positions - back >= starts, term, 0.0)
        total = term if total is None else total + term
    return total


def head_scales(rows, width):
    return lax.rsqrt(jnp.sum(rows * rows, axis=-1, keepdims=True) + EPS)


def forward_kernel(
    place,
    rows_ref,
    halo_ref,
    column_ref,
    weight_ref,
    scalar_ref,
    out_ref,
    map_ref,
    written_ref,
    state_ref,
    inverse_ref,
    end_ref,
    sent_ref,
    sent_state_ref,
    window,
    state,
    *,
    heads,
    key_width,
    value_width,
):
    step = pl.program_id(0)
    wide = value_width + key_width
    base = step * STEP
    rows, columns = iotas()

    @pl.when(step == 0)
    def _():
        window[0:HALO, :] = halo_ref[...].astype(single)
        for h in range(heads):
            state[h, :, :value_width] = jnp.zeros((key_width, value_width), single)
            state[h, :, value_width:] = (rows == columns).astype(single)

    @pl.when(step > 0)
    def _():
        window[0:HALO, :] = window[STEP : STEP + HALO, :]

    window[HALO:, :] = rows_ref[...].astype(single)
    info = column_ref[...]
    starts = info[:, 2 * heads : 2 * heads + 1].astype(jnp.int32)
    before = convolved(window, starts, weight_ref[...], base)
    active = before * sigmoid(before)
    qk_lanes = heads * key_width
    chunks = STEP // CHUNK
    local, stricts = [], []
    for c in range(chunks):
        span = slice(c * CHUNK, (c + 1) * CHUNK)
        for h in range(heads):
            query = active[span, h * key_width : (h + 1) * key_width]
            key = active[span, qk_lanes + h * key_width : qk_lanes + (h + 1) * key_width]
            value = active[
                span, 2 * qk_lanes + h * value_width : 2 * qk_lanes + (h + 1) * value_width
            ]
            query = query * (head_scales(query, key_width) * key_width ** (-0.5))
            key = key * head_scales(key, key_width)
            beta = sigmoid(info[span, h : h + 1])
            decay = -scalar_ref[0, h] * softplus(
                info[span, heads + h : heads + h + 1] + scalar_ref[1, h]
            )
            within, carried, ending = gates(
                decay, starts[span] - (base + c * CHUNK), rows, columns
            )
            query, key = low(query), low(key)
            strict = jnp.where(rows > columns, within * nt(key, key), 0.0) * beta
            mixed = low(within * nt(query, key))
            stricts.append(strict)
            local.append((query, key, value, beta, carried, ending, mixed))
    inverses = [low(a) for a in unit_lower_inverses(stricts, rows, columns)]
    each = range(heads)
    now = [state[h] for h in each]
    for c in range(chunks):
        span = slice(c * CHUNK, (c + 1) * CHUNK)
        here = [local[c * heads + h] for h in each]
        inverse = [inverses[c * heads + h] for h in each]
        now_low = [low(a) for a in now]
        read = [nn(here[h][1], now_low[h]) for h in each]
        asked = [nn(here[h][0], now_low[h]) for h in each]
        target = []
        for h in each:
            query, key, value, beta, carried, ending, mixed = here[h]
            gap = -(carried * beta) * read[h]
            target.append(
                jnp.concatenate(
                    [beta * value + gap[:, :value_width], gap[:, value_width:]], axis=1
                )
            )
        written = [nn(inverse[h], low(target[h])) for h in each]
        added = [tn(here[h][1], low(here[h][5] * written[h])) for h in each]
        inner = [nn(here[h][6], low(written[h])) for h in each]
        for h in each:
            carried = here[h][4]
            inverse_ref[span, h * CHUNK : (h + 1) * CHUNK] = inverse[h]
            state_ref[c, h] = now_low[h]
            written_ref[span, h * wide : (h + 1) * wide] = low(written[h])
            output = carried * asked[h] + inner[h]
            out_ref[span, h * value_width : (h + 1) * value_width] = output[:, :value_width]
            map_ref[span, h * key_width : (h + 1) * key_width] = low(output[:, value_width:])
        now = [here[h][4][CHUNK - 1 : CHUNK] * now[h] + added[h] for h in each]
    for h in each:
        state[h] = now[h]

    @pl.when(step == pl.num_programs(0) - 1)
    def _():
        final = state[...]
        end_ref[...] = final
        sent_ref[...] = low(final)
        sent_state_ref[...] = low(final[:, :, :value_width])


def backward_kernel(
    place,
    rows_ref,
    before_ref,
    halo_ref,
    column_ref,
    weight_ref,
    scalar_ref,
    grad_ref,
    written_ref,
    state_ref,
    inverse_ref,
    end_ref,
    entering_ref,
    *rest,
    hops,
    heads,
    key_width,
    value_width,
):
    got_refs, rest = rest[:hops], rest[hops:]
    out_ref, mix_ref, tail_ref, edge_ref, window, shifted, shifted_start, cotangent, ahead = rest
    step = pl.program_id(0)
    steps = pl.num_programs(0)
    wide = value_width + key_width
    base = (steps - 1 - step) * STEP
    rows, columns = iotas()
    qk_lanes = heads * key_width
    lanes = window.shape[1]
    taps = weight_ref.shape[0]

    @pl.when(step == 0)
    def _():
        shifted[STEP : STEP + 8, :] = jnp.zeros((8, lanes), single)
        shifted_start[STEP : STEP + 8, :] = jnp.zeros((8, 1), jnp.int32)
        for h in range(heads):
            passed = got_refs[0][h].astype(single)
            for hop in range(1, hops):
                passed = passed + got_refs[hop][h].astype(single)
            cotangent[h] = passed
            ahead[h] = end_ref[h, :, :value_width] + nn(
                low(end_ref[h, :, value_width:]), low(entering_ref[h])
            )

    @pl.when(step > 0)
    def _():
        shifted[STEP : STEP + 8, :] = shifted[0:8, :]
        shifted_start[STEP : STEP + 8, :] = shifted_start[0:8, :]

    window[0:HALO, :] = jnp.where(
        step == steps - 1, halo_ref[...].astype(single), before_ref[...].astype(single)
    )
    window[HALO:, :] = rows_ref[...].astype(single)
    info = column_ref[...]
    starts = info[:, 2 * heads : 2 * heads + 1].astype(jnp.int32)
    positions = base + lax.broadcasted_iota(jnp.int32, (STEP, 1), 0)
    before = convolved(window, starts, weight_ref[...], base)
    gate = sigmoid(before)
    active = before * gate
    slope = gate * (1.0 + before * (1.0 - gate))
    upper_ones = low((rows <= columns).astype(single))
    last_row = rows[:, :1] == CHUNK - 1
    chunks = STEP // CHUNK
    each = range(heads)
    items = [(c, h) for c in range(chunks) for h in each]
    spans = {item: slice(item[0] * CHUNK, (item[0] + 1) * CHUNK) for item in items}
    entering = [low(entering_ref[h]) for h in each]
    root = key_width ** (-0.5)

    def per(function):
        return {item: function(*item) for item in items}

    def q_lanes(h):
        return slice(h * key_width, (h + 1) * key_width)

    def k_lanes(h):
        return slice(qk_lanes + h * key_width, qk_lanes + (h + 1) * key_width)

    def v_lanes(h):
        return slice(2 * qk_lanes + h * value_width, 2 * qk_lanes + (h + 1) * value_width)

    def kept(c, h, part):
        return written_ref[spans[c, h], h * wide : (h + 1) * wide][:, part]

    values, maps = slice(0, value_width), slice(value_width, wide)
    query_raw = per(lambda c, h: active[spans[c, h], q_lanes(h)])
    key_raw = per(lambda c, h: active[spans[c, h], k_lanes(h)])
    query_scale = per(lambda c, h: head_scales(query_raw[c, h], key_width))
    key_scale = per(lambda c, h: head_scales(key_raw[c, h], key_width))
    query = per(lambda c, h: query_raw[c, h] * (query_scale[c, h] * root))
    key = per(lambda c, h: key_raw[c, h] * key_scale[c, h])
    query_low = per(lambda c, h: low(query[c, h]))
    key_low = per(lambda c, h: low(key[c, h]))
    beta = per(lambda c, h: sigmoid(info[spans[c, h], h : h + 1]))
    raw = per(lambda c, h: info[spans[c, h], heads + h : heads + h + 1] + scalar_ref[1, h])
    gated = per(
        lambda c, h: gates(
            -scalar_ref[0, h] * softplus(raw[c, h]),
            starts[spans[c, h]] - (base + c * CHUNK),
            rows,
            columns,
        )
    )
    within = per(lambda c, h: gated[c, h][0])
    carried = per(lambda c, h: gated[c, h][1])
    ending = per(lambda c, h: gated[c, h][2])
    mixed = per(lambda c, h: low(within[c, h] * nt(query_low[c, h], key_low[c, h])))
    written = per(
        lambda c, h: kept(c, h, values).astype(single) + nn(kept(c, h, maps), entering[h])
    )
    start_state = per(
        lambda c, h: state_ref[c, h][:, values].astype(single)
        + nn(state_ref[c, h][:, maps], entering[h])
    )
    written_low = per(lambda c, h: low(written[c, h]))
    start_low = per(lambda c, h: low(start_state[c, h]))
    grad = per(lambda c, h: grad_ref[spans[c, h], h * value_width : (h + 1) * value_width])
    grad_low = grad
    carried_grad = per(lambda c, h: low(carried[c, h] * grad[c, h].astype(single)))
    from_output = per(lambda c, h: tn(mixed[c, h], grad_low[c, h]))
    state_part = per(lambda c, h: tn(query_low[c, h], carried_grad[c, h]))
    mixed_grad = per(lambda c, h: low(within[c, h] * nt(grad_low[c, h], written_low[c, h])))
    query_grad = per(
        lambda c, h: nt(carried_grad[c, h], start_low[c, h]) + nn(mixed_grad[c, h], key_low[c, h])
    )
    key_write = per(lambda c, h: tn(mixed_grad[c, h], query_low[c, h]))
    later, later_low, solved, value_grad, read_grad = {}, {}, {}, {}, {}
    now = [cotangent[h] for h in each]
    for c in reversed(range(chunks)):
        for h in each:
            later[c, h], later_low[c, h] = now[h], low(now[h])
        from_state = [nn(key_low[c, h], later_low[c, h]) for h in each]
        written_grad = [low(from_output[c, h] + ending[c, h] * from_state[h]) for h in each]
        for h in each:
            inverse = inverse_ref[spans[c, h], h * CHUNK : (h + 1) * CHUNK]
            solved[c, h] = tn(inverse, written_grad[h])
        for h in each:
            value_grad[c, h] = beta[c, h] * solved[c, h]
            read_grad[c, h] = low(-carried[c, h] * value_grad[c, h])
        now = [
            carried[c, h][CHUNK - 1 : CHUNK] * now[h]
            + state_part[c, h]
            + tn(key_low[c, h], read_grad[c, h])
            for h in each
        ]
    following = {
        (c, h): start_state[c + 1, h] if c + 1 < chunks else ahead[h] for c, h in items
    }
    at_end = per(lambda c, h: jnp.sum(later[c, h] * following[c, h], keepdims=True))
    for h in each:
        cotangent[h] = now[h]
        ahead[h] = start_state[0, h]
    strict_grad = per(
        lambda c, h: low(
            jnp.where(
                rows > columns, -within[c, h] * nt(low(value_grad[c, h]), written_low[c, h]), 0.0
            )
        )
    )
    key_read = per(
        lambda c, h: nt(read_grad[c, h], start_low[c, h]) + nn(strict_grad[c, h], key_low[c, h])
    )
    key_write = per(
        lambda c, h: key_write[c, h]
        + tn(strict_grad[c, h], key_low[c, h])
        + nt(low(ending[c, h] * written[c, h]), later_low[c, h])
    )
    query_dot = per(
        lambda c, h: jnp.sum(query[c, h] * query_grad[c, h], axis=-1, keepdims=True)
    )
    running_grad = per(
        lambda c, h: query_dot[c, h]
        + jnp.sum(key[c, h] * (key_read[c, h] - key_write[c, h]), axis=-1, keepdims=True)
        + jnp.where(last_row, at_end[c, h], 0.0)
    )
    decay_sum = per(
        lambda c, h: ones_product(
            upper_ones, jnp.broadcast_to(running_grad[c, h], (CHUNK, CHUNK))
        )[:, :1]
    )
    decay_grad = per(
        lambda c, h: jnp.where(
            positions[spans[c, h]] == starts[spans[c, h]],
            0.0,
            -scalar_ref[0, h] * sigmoid(raw[c, h]) * decay_sum[c, h],
        )
    )
    beta_grad = per(
        lambda c, h: jnp.sum(solved[c, h] * written[c, h], axis=-1, keepdims=True)
        * sigmoid(-info[spans[c, h], h : h + 1])
    )
    for c, h in items:
        span = spans[c, h]
        key_grad = key_read[c, h] + key_write[c, h]
        key_dot = jnp.sum(key[c, h] * key_grad, axis=-1, keepdims=True)
        query_active = (query_scale[c, h] * root) * query_grad[c, h] - query_raw[c, h] * (
            query_scale[c, h] * query_scale[c, h] * query_dot[c, h]
        )
        key_active = key_scale[c, h] * (key_grad - key[c, h] * key_dot)
        shifted[span, q_lanes(h)] = query_active * slope[span, q_lanes(h)]
        shifted[span, k_lanes(h)] = key_active * slope[span, k_lanes(h)]
        shifted[span, v_lanes(h)] = value_grad[c, h] * slope[span, v_lanes(h)]
    for c in range(chunks):
        mix_ref[c * CHUNK : (c + 1) * CHUNK, :] = jnp.concatenate(
            [beta_grad[c, h] for h in each]
            + [decay_grad[c, h] for h in each]
            + [jnp.zeros((CHUNK, mix_ref.shape[1] - 2 * heads), single)],
            axis=1,
        )
    shifted_start[0:STEP, :] = starts
    total = None
    for tap in range(taps):
        back = taps - 1 - tap
        term = shifted[back : back + STEP, :] * weight_ref[tap : tap + 1, :]
        if back:
            term = jnp.where(positions >= shifted_start[back : back + STEP, :], term, 0.0)
        total = term if total is None else total + term
    out_ref[...] = low(total)

    @pl.when(step == 0)
    def _():
        tail_ref[...] = total[STEP - HALO :, :]

    @pl.when(step == steps - 1)
    def _():
        window[0:8, :] = jnp.zeros((8, lanes), single)
        window[8:16, :] = shifted[0:8, :]
        early = lax.broadcasted_iota(jnp.int32, (8, 1), 0) - 8
        collected = jnp.zeros((8, lanes), single)
        for tap in range(taps - 1):
            back = taps - 1 - tap
            reader = early + back
            reader_start = jnp.zeros((8, 1), jnp.int32)
            for t in range(back):
                reader_start = jnp.where(reader == t, shifted_start[t : t + 1, :], reader_start)
            term = window[back : back + 8, :] * weight_ref[tap : tap + 1, :]
            collected = collected + jnp.where(
                (reader >= 0) & (early >= reader_start), term, 0.0
            )
        edge_ref[0:8, :] = jnp.zeros((8, lanes), single)
        edge_ref[8:16, :] = collected


def block_place(step, place, per_quarter):
    return ((step // per_quarter) ^ place[0]) * per_quarter + step % per_quarter


def run_forward(place, rows, halo, columns, weights, scalars, heads, key_width, value_width, quarter):
    count, lanes = columns.shape[0], rows.shape[1]
    steps, per_quarter = count // STEP, quarter // STEP
    wide = value_width + key_width
    chunks = STEP // CHUNK
    at = lambda i, place: (block_place(i, place, per_quarter), 0)
    fixed = lambda i, place: (0, 0)
    body = functools.partial(
        forward_kernel, heads=heads, key_width=key_width, value_width=value_width
    )
    shapes = (
        jax.ShapeDtypeStruct((count, heads * value_width), single),
        jax.ShapeDtypeStruct((count, heads * key_width), bfloat),
        jax.ShapeDtypeStruct((count, heads * wide), bfloat),
        jax.ShapeDtypeStruct((count // CHUNK, heads, key_width, wide), bfloat),
        jax.ShapeDtypeStruct((count, heads * CHUNK), bfloat),
        jax.ShapeDtypeStruct((heads, key_width, wide), single),
        jax.ShapeDtypeStruct((heads, key_width, wide), bfloat),
        jax.ShapeDtypeStruct((heads, key_width, value_width), bfloat),
    )
    return pl.pallas_call(
        body,
        out_shape=shapes,
        grid_spec=pltpu.PrefetchScalarGridSpec(
            num_scalar_prefetch=1,
            grid=(steps,),
            in_specs=[
                pl.BlockSpec((STEP, lanes), at),
                pl.BlockSpec((HALO, lanes), lambda i, place: (0, 0)),
                pl.BlockSpec((STEP, columns.shape[1]), at),
                pl.BlockSpec(weights.shape, fixed),
                pl.BlockSpec(memory_space=pltpu.SMEM),
            ],
            out_specs=[
                pl.BlockSpec((STEP, heads * value_width), at),
                pl.BlockSpec((STEP, heads * key_width), at),
                pl.BlockSpec((STEP, heads * wide), at),
                pl.BlockSpec((chunks, heads, key_width, wide), lambda i, place: (i, 0, 0, 0)),
                pl.BlockSpec((STEP, heads * CHUNK), at),
                pl.BlockSpec((heads, key_width, wide), lambda i, place: (0, 0, 0)),
                pl.BlockSpec((heads, key_width, wide), lambda i, place: (0, 0, 0)),
                pl.BlockSpec((heads, key_width, value_width), lambda i, place: (0, 0, 0)),
            ],
            scratch_shapes=[
                pltpu.VMEM((STEP + HALO, lanes), single),
                pltpu.VMEM((heads, key_width, wide), single),
            ],
        ),
        compiler_params=pltpu.CompilerParams(
            dimension_semantics=("arbitrary",), vmem_limit_bytes=VMEM_LIMIT
        ),
        cost_estimate=pl.CostEstimate(
            flops=count * 2_000_000, bytes_accessed=count * 10_000, transcendentals=count * 2000
        ),
        name="delta_forward",
    )(place, rows, halo, columns, weights, scalars)


def run_backward(
    place, rows, halo, columns, weights, scalars, grad, saved, entering, got, heads,
    key_width, value_width, quarter,
):
    written, states, inverses, end = saved
    count, lanes = columns.shape[0], rows.shape[1]
    steps, per_quarter = count // STEP, quarter // STEP
    wide = value_width + key_width
    chunks = STEP // CHUNK

    def at(i, place):
        return (block_place(steps - 1 - i, place, per_quarter), 0)

    def halo_at(i, place):
        here = steps - 1 - i
        inner = block_place(jnp.maximum(here - 1, 0), place, per_quarter)
        ratio = STEP // HALO
        return (inner * ratio + ratio - 1, 0)

    fixed = lambda i, place: (0, 0)
    whole = lambda i, place: (0, 0, 0)
    body = functools.partial(
        backward_kernel,
        hops=len(got),
        heads=heads,
        key_width=key_width,
        value_width=value_width,
    )
    shapes = (
        jax.ShapeDtypeStruct((count, lanes), bfloat),
        jax.ShapeDtypeStruct((count, columns.shape[1]), single),
        jax.ShapeDtypeStruct((HALO, lanes), single),
        jax.ShapeDtypeStruct((HALO, lanes), single),
    )
    return pl.pallas_call(
        body,
        out_shape=shapes,
        grid_spec=pltpu.PrefetchScalarGridSpec(
            num_scalar_prefetch=1,
            grid=(steps,),
            in_specs=[
                pl.BlockSpec((STEP, lanes), at),
                pl.BlockSpec((HALO, lanes), halo_at),
                pl.BlockSpec((HALO, lanes), fixed),
                pl.BlockSpec((STEP, columns.shape[1]), at),
                pl.BlockSpec(weights.shape, fixed),
                pl.BlockSpec(memory_space=pltpu.SMEM),
                pl.BlockSpec((STEP, heads * value_width), at),
                pl.BlockSpec((STEP, heads * wide), at),
                pl.BlockSpec(
                    (chunks, heads, key_width, wide), lambda i, place: (steps - 1 - i, 0, 0, 0)
                ),
                pl.BlockSpec((STEP, heads * CHUNK), at),
                pl.BlockSpec(end.shape, whole),
                pl.BlockSpec(entering.shape, whole),
            ]
            + [pl.BlockSpec(part.shape, whole) for part in got],
            out_specs=[
                pl.BlockSpec((STEP, lanes), at),
                pl.BlockSpec((STEP, columns.shape[1]), at),
                pl.BlockSpec((HALO, lanes), fixed),
                pl.BlockSpec((HALO, lanes), fixed),
            ],
            scratch_shapes=[
                pltpu.VMEM((STEP + HALO, lanes), single),
                pltpu.VMEM((STEP + 8, lanes), single),
                pltpu.VMEM((STEP + 8, 1), jnp.int32),
                pltpu.VMEM((heads, key_width, value_width), single),
                pltpu.VMEM((heads, key_width, value_width), single),
            ],
        ),
        compiler_params=pltpu.CompilerParams(
            dimension_semantics=("arbitrary",), vmem_limit_bytes=VMEM_LIMIT
        ),
        cost_estimate=pl.CostEstimate(
            flops=count * 3_000_000, bytes_accessed=count * 12_000, transcendentals=count * 3000
        ),
        name="delta_backward",
    )(
        place, rows, rows, halo, columns, weights, scalars, grad, written, states, inverses, end,
        entering, *got,
    )


def chosen_columns(table, column_sets):
    return column_sets[0:1, :] == table[:, 1:2]


def masked(product, chosen):
    return low(jnp.where(chosen, product, 0.0))


def silu_parts(value):
    logistic = sigmoid(value)
    return logistic, value * logistic


def accumulate(ref, value, first):
    if first is True:
        ref[...] = value
    else:
        ref[...] = jnp.where(first, value, ref[...] + value)


def emit_blocks(parts, place, own_ref, far_ref, pair_ref):
    for k, part in enumerate(parts):
        rows, size = part.shape[0], part.shape[1] // 4
        lanes = slice(k * size, (k + 1) * size)
        for relative, target, row in (
            (0, own_ref, 0), (2, far_ref, 0), (1, pair_ref, 0), (3, pair_ref, rows)
        ):
            start = pl.multiple_of((place ^ relative) * size, 128)
            target[row : row + rows, lanes] = low(part[:, pl.ds(start, size)])


def at_end(fill):
    pl.when(pl.program_id(0) == pl.num_programs(0) - 1)(fill)


def at_start(fill):
    pl.when(pl.program_id(0) == 0)(fill)


def project_kernel(
    rows_ref, table_ref, sets_ref, down_ref, mix_ref, wq_ref, wk_ref, wv_ref, up_qk_ref,
    up_value_ref, *rest, with_halo,
):
    low_rank = sets_ref.shape[1]
    width, q_width = wq_ref.shape
    v_width = wv_ref.shape[1]
    bounds = [0, q_width, 2 * q_width, 2 * q_width + v_width]
    if with_halo:
        halo_ref, halo_table_ref, pre_ref, inner_ref, column_ref, pre_halo_ref, joined = rest
    else:
        pre_ref, inner_ref, column_ref, joined = rest
    weights = (wq_ref, wk_ref, wv_ref)
    ups = (up_qk_ref[0], up_qk_ref[1], up_value_ref[...])
    for p in range(3):
        joined[:width, bounds[p] : bounds[p + 1]] = weights[p][...]
        joined[width:, bounds[p] : bounds[p + 1]] = ups[p]

    def projections(rows, table, store):
        chosen = chosen_columns(table, sets_ref[...])
        product = nt(rows, down_ref[...])
        inner = [masked(product[:, p * low_rank : (p + 1) * low_rank], chosen) for p in range(3)]
        for p in range(3):
            store[:, bounds[p] : bounds[p + 1]] = low(
                nn(
                    jnp.concatenate([rows, inner[p]], axis=1),
                    joined[:, bounds[p] : bounds[p + 1]],
                )
            )
        return inner

    if with_halo:
        projections(halo_ref[...], halo_table_ref[...], pre_halo_ref)
    table = table_ref[...]
    rows = rows_ref[...]
    inner = projections(rows, table, pre_ref)
    for p in range(3):
        inner_ref[:, p * low_rank : (p + 1) * low_rank] = inner[p]
    column_ref[...] = jnp.concatenate([nt(rows, mix_ref[...])[:, :4], table[:, :4]], axis=1)


def gate_kernel(
    rows_ref, table_ref, sets_ref, down_ref, wg_ref, up_ref, gate_ref, inner_ref, joined
):
    width = wg_ref.shape[0]

    @at_start
    def _():
        joined[:width, :] = wg_ref[...]
        joined[width:, :] = up_ref[...]

    rows = rows_ref[...]
    inner = masked(nt(rows, down_ref[...]), chosen_columns(table_ref[...], sets_ref[...]))
    inner_ref[...] = inner
    gate_ref[...] = nn(jnp.concatenate([rows, inner], axis=1), joined[...])


def head_outputs(raw_ref, map_ref, entering_ref, heads, key_width, value_width):
    outputs = []
    for h in range(heads):
        outputs.append(
            raw_ref[:, h * value_width : (h + 1) * value_width]
            + nn(map_ref[:, h * key_width : (h + 1) * key_width], entering_ref[h])
        )
    return outputs


def attend_kernel(
    raw_ref, map_ref, gate_ref, table_ref, gain_ref, sets_ref, wo_ref, down_ref, up_ref, *rest,
    heads, key_width, value_width, hops,
):
    got_refs, rest = rest[:hops], rest[hops:]
    part_ref, z_ref, inner_ref, entering_ref, joined = rest
    value_lanes = wo_ref.shape[0]

    @at_start
    def _():
        joined[:value_lanes, :] = wo_ref[...]
        joined[value_lanes:, :] = up_ref[...]
        for h in range(heads):
            state = got_refs[hops - 1][h].astype(single)
            for hop in range(hops - 1, 0, -1):
                got = got_refs[hop - 1][h]
                state = got[:, :value_width].astype(single) + nn(got[:, value_width:], low(state))
            entering_ref[h] = low(state)

    chosen = chosen_columns(table_ref[...], sets_ref[...])
    outputs = head_outputs(raw_ref, map_ref, entering_ref, heads, key_width, value_width)
    parts = []
    for h, output in enumerate(outputs):
        lanes = slice(h * value_width, (h + 1) * value_width)
        scale = lax.rsqrt(jnp.mean(output * output, axis=-1, keepdims=True) + EPS)
        _, gate = silu_parts(gate_ref[:, lanes])
        parts.append(low(output * scale * gain_ref[0:1, :] * gate))
    z = jnp.concatenate(parts, axis=1)
    z_ref[...] = z
    inner = masked(nt(z, down_ref[...]), chosen)
    inner_ref[...] = inner
    part_ref[...] = low(nn(jnp.concatenate([z, inner], axis=1), joined[...]))


def feed_before_kernel(
    grad_ref, table_ref, sets_ref, wd_ref, down_ffd_t_ref, up_ref, hidden_grad_ref, du_ref, joined
):
    hidden, width = wd_ref.shape

    @at_start
    def _():
        joined[:hidden, :width] = wd_ref[...]
        joined[:hidden, width:] = down_ffd_t_ref[...]
        joined[hidden:, :] = jnp.zeros((joined.shape[0] - hidden, joined.shape[1]), bfloat)

    grad = grad_ref[...]
    du_down = masked(nt(grad, up_ref[...]), chosen_columns(table_ref[...], sets_ref[...]))
    du_ref[...] = du_down
    hidden_grad_ref[...] = nt(jnp.concatenate([grad, du_down], axis=1), joined[...])


def feed_kernel(
    rows_ref, hidden_grad_ref, table_ref, sets_ref, down_ref, wg_ref, wu_ref, up_t_ref, up_ref,
    back_ref, hidden_ref, ff_grad_ref, inner_ref, du_ref,
    joined_gate, joined_up, joined_back,
):
    low_rank = sets_ref.shape[1]
    hidden, width = wg_ref.shape
    padded = joined_gate.shape[0]

    @at_start
    def _():
        for p, (joined, weight) in enumerate(((joined_gate, wg_ref), (joined_up, wu_ref))):
            joined[:hidden, :width] = weight[...]
            joined[:hidden, width:] = up_t_ref[p]
            joined[hidden:, :] = jnp.zeros((padded - hidden, joined.shape[1]), bfloat)
            joined_back[p * padded : p * padded + hidden, :] = weight[...]
            joined_back[p * padded + hidden : (p + 1) * padded, :] = jnp.zeros(
                (padded - hidden, width), bfloat
            )
        joined_back[2 * padded :, :] = down_ref[...]

    chosen = chosen_columns(table_ref[...], sets_ref[...])
    both = jnp.concatenate([chosen, chosen], axis=1)
    rows = rows_ref[...]
    inner = masked(nt(rows, down_ref[...]), both)
    inner_ref[...] = inner
    gate = nt(jnp.concatenate([rows, inner[:, :low_rank]], axis=1), joined_gate[...])
    up = nt(jnp.concatenate([rows, inner[:, low_rank:]], axis=1), joined_up[...])
    logistic, active = silu_parts(gate)
    hidden_ref[...] = low(active * up)
    hidden_grad = hidden_grad_ref[...]
    gate_grad = low(hidden_grad * up * logistic * (1.0 + gate * (1.0 - logistic)))
    up_grad = low(hidden_grad * active)
    du_gate = masked(nt(gate_grad, up_ref[0]), chosen)
    du_up = masked(nt(up_grad, up_ref[1]), chosen)
    du_ref[:, :low_rank] = du_gate
    du_ref[:, low_rank:] = du_up
    ff_grad_ref[:, :padded] = gate_grad
    ff_grad_ref[:, padded:] = up_grad
    back_ref[...] = low(
        nn(jnp.concatenate([gate_grad, up_grad, du_gate, du_up], axis=1), joined_back[...])
    )


def feed_after_kernel(
    rows_ref, grad_ref, hidden_ref, ff_grad_ref, inner_ref, du_ref, du_down_ref, table_ref,
    sets_ref, place_ref, wd_ref, down_ffd_ref, up_ref,
    out_ref, own_ref, far_ref, pair_ref, flat_ref,
    joined, down_sum, res_sum, flat_sum,
):
    first = pl.program_id(0) == 0
    low_rank = sets_ref.shape[1]
    width_hidden = wd_ref.shape[0]
    padded = down_ffd_ref.shape[1]

    @at_start
    def _():
        joined[:width_hidden, :] = wd_ref[...]
        joined[width_hidden:padded, :] = jnp.zeros(
            (padded - width_hidden, joined.shape[1]), bfloat
        )
        joined[padded:, :] = up_ref[...]

    hidden = hidden_ref[...]
    inner = inner_ref[...]
    u_down = masked(
        nt(hidden, down_ffd_ref[...]), chosen_columns(table_ref[...], sets_ref[...])
    )
    out_ref[...] = low(nn(jnp.concatenate([hidden, u_down], axis=1), joined[...]))
    accumulate(down_sum, tn(du_ref[...], rows_ref[...]), first)
    accumulate(res_sum, tn(u_down, grad_ref[...]), first)
    for k, grown in enumerate(
        (
            tn(inner[:, :low_rank], ff_grad_ref[:, :padded]),
            tn(inner[:, low_rank:], ff_grad_ref[:, padded:]),
            tn(du_down_ref[...], hidden),
        )
    ):
        accumulate(flat_sum.at[:, k * padded : (k + 1) * padded], grown, first)

    @at_end
    def _():
        flat_ref[...] = low(flat_sum[...])
        emit_blocks(
            (down_sum.at[:low_rank], down_sum.at[low_rank:], res_sum),
            place_ref[0], own_ref, far_ref, pair_ref,
        )


def branch_kernel(
    branch_ref, raw_ref, map_ref, gate_ref, table_ref, entering_ref, gain_ref, sets_ref, wo_ref,
    down_out_t_ref, up_ref, up_gate_ref, *rest,
    heads, key_width, value_width, hops, last,
):
    if last:
        before_ref, *rest = rest
        got_refs, rest = rest[: hops - 1], rest[hops - 1 :]
        raw_grad_ref, gate_grad_ref, du_out_ref, du_gate_ref, *rest = rest
        sent_refs, (joined,) = rest[:hops], rest[hops:]
    else:
        raw_grad_ref, gate_grad_ref, du_out_ref, du_gate_ref, total_ref, joined = rest
    width = wo_ref.shape[1]

    @at_start
    def _():
        joined[:, :width] = wo_ref[...]
        joined[:, width:] = down_out_t_ref[...]

    chosen = chosen_columns(table_ref[...], sets_ref[...])
    branch = branch_ref[...]
    outputs = head_outputs(raw_ref, map_ref, entering_ref, heads, key_width, value_width)
    du_out = masked(nt(branch, up_ref[...]), chosen)
    du_out_ref[...] = du_out
    mixed_grad = nt(jnp.concatenate([branch, du_out], axis=1), joined[...])
    gain = gain_ref[0:1, :]
    gate_grads = []
    for h, output in enumerate(outputs):
        lanes = slice(h * value_width, (h + 1) * value_width)
        scale = lax.rsqrt(jnp.mean(output * output, axis=-1, keepdims=True) + EPS)
        value = gate_ref[:, lanes]
        logistic, active = silu_parts(value)
        incoming = mixed_grad[:, lanes]
        gate_grads.append(
            low(
                incoming
                * (output * scale * gain)
                * (logistic * (1.0 + value * (1.0 - logistic)))
            )
        )
        scaled = gain * (incoming * active)
        dot = jnp.mean(output * scaled, axis=-1, keepdims=True)
        raw_grad = low(scale * scaled - output * (scale * scale * scale * dot))
        raw_grad_ref[:, lanes] = raw_grad
        grown = tn(map_ref[:, h * key_width : (h + 1) * key_width], raw_grad)
        if not last:
            total_ref[h] = grown
        else:
            passed = low(before_ref[h] + grown)
            sent_refs[0][h] = passed
            for hop in range(1, hops):
                passed = low(tn(got_refs[hop - 1][h][:, value_width:], passed))
                sent_refs[hop][h] = passed
    gate_grad = jnp.concatenate(gate_grads, axis=1)
    gate_grad_ref[...] = gate_grad
    du_gate_ref[...] = masked(nt(gate_grad, up_gate_ref[...]), chosen)


def branch_after_kernel(
    branch_ref, z_ref, u_out_ref, rows_ref, inner_ref, du_out_ref, du_gate_ref, gate_grad_ref,
    down_grad_ref, res_grad_ref, flat_ref,
    flat_sum,
):
    lanes = z_ref.shape[1]
    accumulate(down_grad_ref, tn(du_gate_ref[...], rows_ref[...]), True)
    accumulate(res_grad_ref, tn(u_out_ref[...], branch_ref[...]), True)
    accumulate(flat_sum.at[:, :lanes], tn(du_out_ref[...], z_ref[...]), True)
    accumulate(flat_sum.at[:, lanes:], tn(inner_ref[...], gate_grad_ref[...]), True)

    @at_end
    def _():
        flat_ref[...] = low(flat_sum[...])


def settled_rows(pre_ref, tail_ref, arrived_ref, place_ref, quarter, window):
    block = window.shape[0]
    start = ((3 ^ place_ref[0]) + 1) * quarter - HALO - pl.program_id(0) * block
    window[...] = pre_ref[...]

    @pl.when((start >= 0) & (start < block))
    def _():
        window[pl.ds(pl.multiple_of(start, HALO), HALO), :] = low(tail_ref[...] + arrived_ref[...])

    return window[...]


def settle_grads_kernel(
    pre_ref, rows_ref, inner_ref, table_ref, tail_ref, arrived_ref, place_ref, sets_ref,
    up_qk_ref, up_value_ref, down_late_ref, res_late_ref,
    du_ref, own_ref, far_ref, pair_ref, flat_ref,
    window, down_sum, flat_sum,
    *, quarter,
):
    low_rank = sets_ref.shape[1]
    q_width = up_qk_ref.shape[2]
    chosen = chosen_columns(table_ref[...], sets_ref[...])
    pre = settled_rows(pre_ref, tail_ref, arrived_ref, place_ref, quarter, window)
    query, key, value = pre[:, :q_width], pre[:, q_width : 2 * q_width], pre[:, 2 * q_width :]
    inner = inner_ref[...]
    du = jnp.concatenate(
        [
            masked(nt(query, up_qk_ref[0]), chosen),
            masked(nt(key, up_qk_ref[1]), chosen),
            masked(nt(value, up_value_ref[...]), chosen),
        ],
        axis=1,
    )
    du_ref[...] = du
    accumulate(down_sum, tn(du, rows_ref[...]), True)
    at = 0
    for p, part in enumerate((query, key, value)):
        accumulate(
            flat_sum.at[:, at : at + part.shape[1]],
            tn(inner[:, p * low_rank : (p + 1) * low_rank], part),
            True,
        )
        at += part.shape[1]

    @at_end
    def _():
        flat_ref[...] = low(flat_sum[...])
        emit_blocks(
            [down_sum.at[p * low_rank : (p + 1) * low_rank] for p in range(3)]
            + [down_late_ref, res_late_ref],
            place_ref[0], own_ref, far_ref, pair_ref,
        )


def settle_kernel(
    pre_ref, gate_grad_ref, du_ref, du_gate_ref, mix_ref, tail_ref, arrived_ref, place_ref,
    down_ref, mix_weight_ref, wq_ref, wk_ref, wv_ref, wg_ref,
    part_ref,
    window, joined, joined_small,
    *, quarter,
):
    q_width, v_width = wq_ref.shape[1], wv_ref.shape[1]

    @at_start
    def _():
        joined[:, :q_width] = wq_ref[...]
        joined[:, q_width : 2 * q_width] = wk_ref[...]
        joined[:, 2 * q_width : 2 * q_width + v_width] = wv_ref[...]
        joined[:, 2 * q_width + v_width :] = wg_ref[...]
        maps, mixes = down_ref.shape[0], mix_weight_ref.shape[0]
        spare = joined_small.shape[0] - maps - mixes
        joined_small[:maps, :] = down_ref[...]
        joined_small[maps:, :] = jnp.concatenate(
            [mix_weight_ref[...], jnp.zeros((spare, joined_small.shape[1]), bfloat)], axis=0
        )

    pre = settled_rows(pre_ref, tail_ref, arrived_ref, place_ref, quarter, window)
    mix = low(mix_ref[...])
    spare = joined_small.shape[0] - down_ref.shape[0] - mix.shape[1]
    small = jnp.concatenate(
        [du_ref[...], du_gate_ref[...], mix, jnp.zeros((mix.shape[0], spare), bfloat)], axis=1
    )
    part_ref[...] = low(
        nt(jnp.concatenate([pre, gate_grad_ref[...]], axis=1), joined[...])
        + nn(small, joined_small[...])
    )


def assemble_kernel(
    place_ref, *refs, padded,
):
    pieces_last, pieces_feed = refs[:4], refs[4:8]
    last_ref, feed_ref, branch_ref = refs[8:11]
    down_ref, qk_ref, vg_ref, ff_ref, out_ref, ffd_ref, res_ref = refs[11:]
    place = place_ref[0]
    size = pieces_last[0].shape[1] // 5
    first = [down_ref.at[p] for p in range(4)] + [res_ref.at[0]]
    second = [down_ref.at[4], down_ref.at[5], res_ref.at[1]]
    for relative in range(4):
        start = pl.multiple_of((place ^ relative) * size, 128)
        for targets, piece in ((first, pieces_last[relative]), (second, pieces_feed[relative])):
            for k, target in enumerate(targets):
                target[:, pl.ds(start, size)] = piece[:, k * size : (k + 1) * size].astype(single)
    qk, values, hidden = qk_ref.shape[2], vg_ref.shape[2], ff_ref.shape[2]

    def lanes(ref, start, width):
        return ref[:, start : start + width].astype(single)

    own = 5 * size
    qk_ref[0], qk_ref[1] = lanes(last_ref, own, qk), lanes(last_ref, own + qk, qk)
    vg_ref[0] = lanes(last_ref, own + 2 * qk, values)
    at = last_ref.shape[1]
    out_ref[...] = lanes(branch_ref, at, values)
    vg_ref[1] = lanes(branch_ref, at + values, values)
    own = 3 * size
    ff_ref[0] = lanes(feed_ref, own, hidden)
    ff_ref[1] = lanes(feed_ref, own + padded, hidden)
    ffd_ref[...] = lanes(feed_ref, own + 2 * padded, hidden)


def assemble(where, shared, last, feed, branch, padded, shapes):
    rows = last.shape[0]
    block = min(32, rows)

    def spec(shape):
        if len(shape) == 2:
            return pl.BlockSpec((block, shape[1]), lambda i: (i, 0))
        return pl.BlockSpec((shape[0], block, shape[2]), lambda i: (0, i, 0))

    arrays = [*shared, last, feed, branch]
    return pl.pallas_call(
        functools.partial(assemble_kernel, padded=padded),
        out_shape=tuple(jax.ShapeDtypeStruct(shape, single) for shape in shapes),
        grid=(rows // block,),
        in_specs=[pl.BlockSpec(memory_space=pltpu.SMEM)] + [spec(a.shape) for a in arrays],
        out_specs=[spec(shape) for shape in shapes],
        compiler_params=pltpu.CompilerParams(
            dimension_semantics=("arbitrary",), vmem_limit_bytes=VMEM_LIMIT
        ),
        name="assemble",
    )(where, *arrays)


WHOLE, SCALAR = "whole", "scalar"


def by_rows(width, lane_block=0):
    return ("rows", width, lane_block)


def part(rows, index):
    return ("part", rows, index)


def pieces(width):
    return ("pieces", width)


def blocked_call(
    body, name, count, inputs, outputs, scratch, flops, block=STEP, half=None, into=()
):
    if half is not None:
        block = count // 2
    steps = count // block if half is None else 1
    offset = half or 0
    per = max(steps // 4, 1)
    in_specs, arrays, moved, groups_in, extra = [], [], 0, [], []
    for array, kind in inputs:
        members = array if isinstance(array, (list, tuple)) else [array]
        groups_in.append(len(members))
        arrays += members
        moved += sum(a.size * a.dtype.itemsize for a in members)
        if kind == WHOLE:
            zeros = (0,) * array.ndim
            in_specs.append(
                pl.BlockSpec(
                    array.shape, lambda i, zeros=zeros: zeros, pipeline_mode=pl.Buffered(1)
                )
            )
        elif kind == SCALAR:
            in_specs.append(pl.BlockSpec(memory_space=pltpu.SMEM))
        elif kind[0] == "part":
            in_specs.append(
                pl.BlockSpec(
                    (kind[1], array.shape[1]),
                    lambda i, at=kind[2]: (at, 0),
                    pipeline_mode=pl.Buffered(1),
                )
            )
        elif kind[0] == "rows":
            in_specs.append(
                pl.BlockSpec((block, kind[1]), lambda i, lane=kind[2]: (i + offset, lane))
            )
        else:
            for b, member in enumerate(members):
                if steps == 1:
                    in_specs.append(pl.BlockSpec(member.shape, lambda i: (0, 0)))
                else:
                    in_specs.append(
                        pl.BlockSpec(
                            (block, kind[1]),
                            lambda i, b=b: (jnp.clip(i - b * per, 0, per - 1), 0),
                        )
                    )
            extra.append(pltpu.VMEM((block, kind[1]), members[0].dtype))
    out_specs, shapes, groups_out, aliases = [], [], [], {}
    into = list(into)
    held_arrays = []
    for shape, dtype, kind in outputs:
        if kind == "parts":
            quarter = shape[0] // 4
            spec = (block, shape[1])
            if steps == 1:
                for _ in range(2):
                    shapes.append(jax.ShapeDtypeStruct((quarter, shape[1]), dtype))
                    out_specs.append(pl.BlockSpec((quarter, shape[1]), lambda i: (0, 0)))
                groups_out.append(2)
            else:
                for rows in (quarter, quarter, 2 * quarter):
                    shapes.append(jax.ShapeDtypeStruct((rows, shape[1]), dtype))
                out_specs += [
                    pl.BlockSpec(spec, lambda i: (jnp.clip(i, 0, per - 1), 0)),
                    pl.BlockSpec(spec, lambda i: (jnp.clip(i - 2 * per, 0, per - 1), 0)),
                    pl.BlockSpec(
                        spec,
                        lambda i: (
                            jnp.clip(i - per, 0, per - 1) + jnp.clip(i - 3 * per + 1, 0, per), 0
                        ),
                    ),
                ]
                groups_out.append(3)
            extra.append(pltpu.VMEM(spec, dtype))
        else:
            groups_out.append(1)
            shapes.append(jax.ShapeDtypeStruct(shape, dtype))
            if kind == "rows":
                if into:
                    aliases[len(arrays) + len(held_arrays)] = len(shapes) - 1
                    held_arrays.append(into.pop(0))
                out_specs.append(pl.BlockSpec((block, shape[1]), lambda i: (i + offset, 0)))
            else:
                zeros = (0,) * len(shape)
                out_specs.append(pl.BlockSpec(shape, lambda i, zeros=zeros: zeros))
    in_specs += [pl.BlockSpec(memory_space=pl.ANY) for _ in held_arrays]

    def wrapped(*refs):
        refs = list(refs)
        spare = refs[len(in_specs) + len(out_specs) + len(scratch) :]
        own_scratch = refs[len(in_specs) + len(out_specs) : len(refs) - len(spare)]
        quarter = pl.program_id(0) // per
        given, later, at, used = [], [], 0, 0
        for size, (_, kind) in zip(groups_in, inputs):
            if kind[0] != "pieces":
                given.append(refs[at])
            else:
                held = spare[used]
                used += 1
                if steps == 1:
                    for b in range(size):
                        piece = refs[at + b]
                        held[b * piece.shape[0] : (b + 1) * piece.shape[0], :] = piece[...]
                else:
                    for b in range(size):

                        @pl.when(quarter == b)
                        def _(held=held, source=refs[at + b]):
                            held[...] = source[...]

                given.append(held)
            at += size
        at += len(held_arrays)
        for size in groups_out:
            if size == 1:
                given.append(refs[at])
            else:
                given.append(spare[used])
                later.append((spare[used], refs[at : at + size]))
                used += 1
            at += size
        body(*given, *own_scratch)
        for held, targets in later:
            if len(targets) == 2:
                rows = targets[0].shape[0]
                targets[0][...], targets[1][...] = held[:rows, :], held[rows:, :]
                continue
            for b, target in ((0, targets[0]), (2, targets[1]), (1, targets[2]), (3, targets[2])):

                @pl.when(quarter == b)
                def _(held=held, target=target):
                    target[...] = held[...]

    results = pl.pallas_call(
        wrapped,
        out_shape=tuple(shapes),
        grid=(steps,),
        in_specs=in_specs,
        out_specs=out_specs,
        scratch_shapes=list(scratch) + extra,
        input_output_aliases=aliases,
        compiler_params=pltpu.CompilerParams(
            dimension_semantics=("arbitrary",), vmem_limit_bytes=VMEM_LIMIT
        ),
        cost_estimate=pl.CostEstimate(flops=flops, bytes_accessed=moved, transcendentals=0),
        name=name,
    )(*arrays, *held_arrays)
    grouped, at = [], 0
    for size in groups_out:
        grouped.append(results[at] if size == 1 else results[at : at + size])
        at += size
    return grouped


def flip(array, bit):
    groups = lax.axis_size("head")
    return lax.ppermute(array, "head", [(i, i ^ bit) for i in range(groups)])


def gather_rows(array):
    far = flip(array, 2)
    near = flip(array, 1)
    return [array, near, far, flip(far, 1)]


def tie(*arrays):
    return lax.optimization_barrier(arrays)


def near_sum(parts):
    own, far, pair = parts
    size = own.shape[0]
    arrived = flip(pair, 1)
    return (
        own.astype(single) + arrived[:size].astype(single),
        low(far.astype(single) + arrived[size:].astype(single)),
    )


def halves_sum(first, second):
    near, corner = tie(flip(first[1], 1), second[1])
    return (
        first[0].astype(single) + near.astype(single),
        low(second[0].astype(single) + flip(corner, 1).astype(single)),
    )


def far_sum(own, far):
    return own + flip(far, 2).astype(single)


def shifted_along(array, axis, by):
    length = lax.axis_size(axis)
    pairs = [(i, i + by) for i in range(length) if 0 <= i + by < length]
    return lax.ppermute(array, axis, pairs)


def seq_rows(flat):
    members = lax.axis_size("seq")
    return flat.reshape(members, flat.shape[0] // members, flat.shape[1])


def share_sum(parts):
    summed = low(jnp.sum(parts.astype(single), axis=0))
    return jnp.broadcast_to(summed[None], parts.shape)


def exchange(parts):
    return lax.all_to_all(parts, "seq", 0, 0)


def all_rows(parts):
    return parts.reshape(-1, parts.shape[-1])


def rms_scale(rows, gain):
    return rows * lax.rsqrt(jnp.mean(rows * rows, axis=-1, keepdims=True) + EPS) * gain


def rms_back(rows, gain, incoming):
    _, back = jax.vjp(lambda value: rms_scale(value, gain), rows)
    return back(incoming)[0]


def on_device(
    block_input,
    out_grad,
    lengths,
    doc_sets,
    norm1_gain,
    w_query,
    w_key,
    w_value,
    conv_query,
    conv_key,
    conv_value,
    w_decay_beta,
    decay_rate,
    decay_bias,
    w_gate_out,
    out_gain,
    w_out,
    norm2_gain,
    w_gate,
    w_up,
    w_down,
    adapt_down,
    adapt_up_qk,
    adapt_up_vg,
    adapt_up_ff,
    adapt_down_out,
    adapt_down_ffd,
    adapt_up_res,
):
    groups = lax.axis_size("head")
    members = lax.axis_size("seq")
    place = lax.axis_index("head")
    quarter, width = block_input.shape
    count = quarter * groups
    heads = decay_rate.shape[0]
    key_width = w_query.shape[1] // heads
    value_width = w_value.shape[1] // heads
    sets, rank = adapt_down.shape[1], adapt_down.shape[3]
    low_rank = sets * rank
    qk = heads * key_width
    device_start = lax.axis_index("seq") * count
    starts = jnp.sum(
        jnp.where(
            jnp.arange(lengths.shape[0])[None, :] < jnp.arange(lengths.shape[0])[:, None],
            lengths[None, :],
            0,
        ),
        axis=1,
    )
    order = jnp.arange(groups, dtype=jnp.int32) ^ place

    def tables(positions):
        reached = positions[:, None] >= starts[None, :]
        token_start = jnp.max(jnp.where(reached, starts[None, :], -1), axis=1)
        ended = positions[:, None] >= (starts + lengths)[None, :]
        token_set = jnp.sum(jnp.where(reached & ~ended, doc_sets[None, :], 0), axis=1)
        pair = jnp.stack([token_start - device_start, token_set], axis=1).astype(single)
        return jnp.pad(pair, ((0, 0), (0, 8 - pair.shape[1])))

    table = tables(
        (
            device_start + order[:, None] * quarter + jnp.arange(quarter, dtype=jnp.int32)[None, :]
        ).reshape(-1)
    )
    halo_table = tables(device_start + jnp.arange(-HALO, 0, dtype=jnp.int32))
    column_sets = jnp.broadcast_to(
        (jnp.arange(low_rank, dtype=jnp.int32) // rank).astype(single)[None, :], (8, low_rank)
    )

    down = adapt_down.transpose(0, 1, 3, 2).reshape(6 * low_rank, width)
    up_qk = adapt_up_qk.reshape(2, low_rank, -1)
    up_vg = adapt_up_vg.reshape(2 * low_rank, -1)
    up_ff = adapt_up_ff.reshape(2, low_rank, -1)
    down_out = adapt_down_out.transpose(0, 2, 1).reshape(low_rank, -1)
    down_ffd = adapt_down_ffd.transpose(0, 2, 1).reshape(low_rank, -1)
    up_res = adapt_up_res.reshape(2 * low_rank, width)
    conv = jnp.concatenate([conv_query, conv_key, conv_value], axis=1).astype(single)
    scalars = jnp.stack([decay_rate, decay_bias])
    where = place.reshape(1).astype(jnp.int32)
    weight_mix = jnp.pad(
        w_decay_beta.transpose(1, 2, 0).reshape(2 * heads, width), ((0, 8 - 2 * heads), (0, 0))
    )
    gain = jnp.broadcast_to(out_gain[None, :], (8, value_width))
    hidden_width = w_down.shape[0]
    padded = -(-hidden_width // 256) * 256
    value_lanes = heads * value_width
    block_width = width // groups
    widen = lambda a: jnp.pad(a, [(0, 0)] * (a.ndim - 1) + [(0, padded - hidden_width)])

    input_float = block_input.astype(single)
    normed = low(rms_scale(input_float, norm1_gain))
    tail = normed[quarter - HALO :]
    halo = sum(
        lax.ppermute(
            tail,
            ("seq", "head"),
            [((s * groups) + groups - 1, (s + 1) * groups + h) for s in range(members - 1)],
        )
        for h in range(groups)
    )
    normed_near, normed_far = flip(normed, 1), flip(normed, 2)
    project_inputs = [
        (table, by_rows(8)),
        (column_sets, WHOLE),
        (down, part(3 * low_rank, 0)),
        (weight_mix, WHOLE),
        (w_query, WHOLE),
        (w_key, WHOLE),
        (w_value, WHOLE),
        (up_qk, WHOLE),
        (up_vg, part(low_rank, 0)),
    ]
    project_outputs = [
        ((count, 2 * qk + value_lanes), bfloat, "rows"),
        ((count, 3 * low_rank), bfloat, "rows"),
        ((count, 8), single, "rows"),
    ]
    project_scratch = [pltpu.VMEM((width + low_rank, 2 * qk + value_lanes), bfloat)]
    projected = blocked_call(
        functools.partial(project_kernel, with_halo=False),
        "project_near",
        count,
        [([normed, normed_near], pieces(width)), *project_inputs],
        project_outputs,
        project_scratch,
        count * 2_000_000,
        half=0,
    )
    normed_far, projected[2] = tie(normed_far, projected[2])
    normed_all = [normed, normed_near, normed_far, flip(normed_far, 1)]
    pre, inner, columns, pre_halo = blocked_call(
        functools.partial(project_kernel, with_halo=True),
        "project_far",
        count,
        [
            (normed_all[2:], pieces(width)),
            *project_inputs,
            (halo, WHOLE),
            (halo_table, WHOLE),
        ],
        project_outputs + [((HALO, 2 * qk + value_lanes), bfloat, "whole")],
        project_scratch,
        count * 2_000_000,
        half=1,
        into=projected,
    )
    out_grad_late, pre = tie(out_grad, pre)
    grad_near, grad_far = flip(out_grad_late, 1), flip(out_grad_late, 2)
    raw_local, mapped, *saved, sent, sent_state = run_forward(
        where, pre, pre_halo, columns, conv, scalars, heads, key_width, value_width, quarter
    )

    hops = min(members - 1, -(-(DOC_MAX - 1) // count))
    got = [shifted_along(sent_state, "seq", hops)]
    got = [shifted_along(sent, "seq", hop) for hop in range(hops - 1, 0, -1)][::-1] + got
    grad_near, grad_far, sent_state = tie(grad_near, grad_far, sent_state)
    grad_all = [out_grad, grad_near, grad_far, flip(grad_far, 1)]
    hidden_grad, du_down = blocked_call(
        feed_before_kernel,
        "feed_before",
        count,
        [
            (grad_all, pieces(width)),
            (table, by_rows(8)),
            (column_sets, WHOLE),
            (w_down, WHOLE),
            (down_ffd.T, WHOLE),
            (up_res, part(low_rank, 1)),
        ],
        [((count, padded), single, "rows"), ((count, low_rank), bfloat, "rows")],
        [pltpu.VMEM((padded, width + low_rank), bfloat)],
        count * 6_000_000,
    )
    gate_rows, du_down = tie(normed_all[0], du_down)
    gate_input, inner_gate = blocked_call(
        gate_kernel,
        "gate",
        count,
        [
            ([gate_rows, *normed_all[1:]], pieces(width)),
            (table, by_rows(8)),
            (column_sets, WHOLE),
            (down, part(low_rank, 3)),
            (w_gate_out, WHOLE),
            (up_vg, part(low_rank, 1)),
        ],
        [((count, value_lanes), single, "rows"), ((count, low_rank), bfloat, "rows")],
        [pltpu.VMEM((width + low_rank, value_lanes), bfloat)],
        count * 3_000_000,
    )
    raw_local, hidden_grad = tie(raw_local, hidden_grad)

    sizes = dict(heads=heads, key_width=key_width, value_width=value_width)
    attention_part, mixed, u_out, entering = blocked_call(
        functools.partial(attend_kernel, hops=hops, **sizes),
        "attend",
        count,
        [
            (raw_local, by_rows(value_lanes)),
            (mapped, by_rows(qk)),
            (gate_input, by_rows(value_lanes)),
            (table, by_rows(8)),
            (gain, WHOLE),
            (column_sets, WHOLE),
            (w_out, WHOLE),
            (down_out, WHOLE),
            (up_res, part(low_rank, 0)),
        ]
        + [(sent_by, WHOLE) for sent_by in got],
        [
            ((count, width), bfloat, "parts"),
            ((count, value_lanes), bfloat, "rows"),
            ((count, low_rank), bfloat, "rows"),
            ((heads, key_width, value_width), bfloat, "whole"),
        ],
        [pltpu.VMEM((value_lanes + low_rank, width), bfloat)],
        count * 5_000_000,
    )
    attention_own, attention_far = near_sum(attention_part)
    attention_arrived, up_ff_t, up_ff_padded, down_ffd_padded, down_out_t = tie(
        flip(attention_far, 2),
        up_ff.transpose(0, 2, 1),
        widen(up_ff),
        widen(down_ffd),
        down_out.T,
    )
    residual = input_float + (attention_own + attention_arrived.astype(single))
    normed_mid = low(rms_scale(residual, norm2_gain))
    mid_near, mid_far = flip(normed_mid, 1), flip(normed_mid, 2)

    feed_inputs = [
        (hidden_grad, by_rows(padded)),
        (table, by_rows(8)),
        (column_sets, WHOLE),
        (down, part(2 * low_rank, 2)),
        (w_gate.T, WHOLE),
        (w_up.T, WHOLE),
        (up_ff_t, WHOLE),
        (up_ff_padded, WHOLE),
    ]
    feed_outputs = [
        ((count, width), bfloat, "parts"),
        ((count, padded), bfloat, "rows"),
        ((count, 2 * padded), bfloat, "rows"),
        ((count, 2 * low_rank), bfloat, "rows"),
        ((count, 2 * low_rank), bfloat, "rows"),
    ]
    feed_scratch = [
        pltpu.VMEM((padded, width + low_rank), bfloat),
        pltpu.VMEM((padded, width + low_rank), bfloat),
        pltpu.VMEM((2 * padded + 2 * low_rank, width), bfloat),
    ]
    near_part, *fed = blocked_call(
        feed_kernel,
        "feed_near",
        count,
        [([normed_mid, mid_near], pieces(width)), *feed_inputs],
        feed_outputs,
        feed_scratch,
        count * 8_000_000,
        half=0,
    )
    mid_far, near_own = tie(mid_far, near_part[0])
    near_part = [near_own, near_part[1]]
    mid_all = [normed_mid, mid_near, mid_far, flip(mid_far, 1)]
    far_part, hidden, ff_grad, u_ff, du_ff = blocked_call(
        feed_kernel,
        "feed_far",
        count,
        [(mid_all[2:], pieces(width)), *feed_inputs],
        feed_outputs,
        feed_scratch,
        count * 8_000_000,
        half=1,
        into=fed,
    )
    grad_own, grad_sum = halves_sum(near_part, far_part)
    grad_sum, hidden = tie(grad_sum, hidden)
    grad_arrived = flip(grad_sum, 2)
    mid_grad = grad_own + grad_arrived.astype(single)
    out_part, feed_own, feed_far, feed_pair, feed_owned = blocked_call(
        feed_after_kernel,
        "feed_after",
        count,
        [
            (mid_all, pieces(width)),
            (grad_all, pieces(width)),
            (hidden, by_rows(padded)),
            (ff_grad, by_rows(2 * padded)),
            (u_ff, by_rows(2 * low_rank)),
            (du_ff, by_rows(2 * low_rank)),
            (du_down, by_rows(low_rank)),
            (table, by_rows(8)),
            (column_sets, WHOLE),
            (where, SCALAR),
            (w_down, WHOLE),
            (down_ffd_padded, WHOLE),
            (up_res, part(low_rank, 1)),
        ],
        [
            ((count, width), bfloat, "parts"),
            ((low_rank, 3 * block_width), bfloat, "whole"),
            ((low_rank, 3 * block_width), bfloat, "whole"),
            ((2 * low_rank, 3 * block_width), bfloat, "whole"),
            ((low_rank, 3 * padded), bfloat, "whole"),
        ],
        [
            pltpu.VMEM((padded + low_rank, width), bfloat),
            pltpu.VMEM((2 * low_rank, width), single),
            pltpu.VMEM((low_rank, width), single),
            pltpu.VMEM((low_rank, 3 * padded), single),
        ],
        count * 16_000_000,
    )
    residual_grad = out_grad.astype(single) + rms_back(residual, norm2_gain, mid_grad)
    branch_low = low(residual_grad)
    branch_near, branch_far = flip(branch_low, 1), flip(branch_low, 2)
    out_own, out_far = near_sum(out_part)
    feed_flat = jnp.concatenate(
        [
            low(far_sum(*near_sum((feed_own, feed_far, tie(feed_pair, grad_arrived)[0])))),
            feed_owned,
        ],
        axis=1,
    )
    branch_inputs = [
        (raw_local, by_rows(value_lanes)),
        (mapped, by_rows(qk)),
        (gate_input, by_rows(value_lanes)),
        (table, by_rows(8)),
        (entering, WHOLE),
        (gain, WHOLE),
        (column_sets, WHOLE),
        (w_out, WHOLE),
        (down_out_t, WHOLE),
        (up_res, part(low_rank, 0)),
        (up_vg, part(low_rank, 1)),
    ]
    branch_outputs = [
        ((count, value_lanes), bfloat, "rows"),
        ((count, value_lanes), bfloat, "rows"),
        ((count, low_rank), bfloat, "rows"),
        ((count, low_rank), bfloat, "rows"),
    ]
    branch_scratch = [pltpu.VMEM((value_lanes, width + low_rank), bfloat)]
    state_shape = (heads, key_width, value_width)
    *branched, state_near = blocked_call(
        functools.partial(branch_kernel, hops=hops, last=False, **sizes),
        "branch_near",
        count,
        [([branch_low, branch_near], pieces(width)), *branch_inputs],
        branch_outputs + [(state_shape, single, "whole")],
        branch_scratch,
        count * 4_000_000,
        half=0,
    )
    branch_far, state_near = tie(branch_far, state_near)
    branch_corner, feed_flat, out_far = tie(flip(branch_far, 1), feed_flat, out_far)
    feed_parts = exchange(seq_rows(feed_flat))
    branch_all = [branch_low, branch_near, branch_far, branch_corner]
    raw_grad, gate_grad, du_out, du_outgate, *state_grads = blocked_call(
        functools.partial(branch_kernel, hops=hops, last=True, **sizes),
        "branch_far",
        count,
        [(branch_all[2:], pieces(width)), *branch_inputs, (state_near, WHOLE)]
        + [(sent_by, WHOLE) for sent_by in got[:-1]],
        branch_outputs + [(state_shape, bfloat, "whole")] * hops,
        branch_scratch,
        count * 4_000_000,
        half=1,
        into=branched,
    )
    state_got = [
        shifted_along(state_grads[hop - 1], "seq", -hop) for hop in range(hops, 0, -1)
    ][::-1]
    du_out, feed_parts = tie(du_out, feed_parts)
    mixer_down_late, branch_res_grad, branch_flat = blocked_call(
        branch_after_kernel,
        "branch_after",
        count,
        [
            (branch_all, pieces(width)),
            (mixed, by_rows(value_lanes)),
            (u_out, by_rows(low_rank)),
            (normed_all, pieces(width)),
            (inner_gate, by_rows(low_rank)),
            (du_out, by_rows(low_rank)),
            (du_outgate, by_rows(low_rank)),
            (gate_grad, by_rows(value_lanes)),
        ],
        [
            ((low_rank, width), single, "whole"),
            ((low_rank, width), single, "whole"),
            ((low_rank, 2 * value_lanes), bfloat, "whole"),
        ],
        [pltpu.VMEM((low_rank, 2 * value_lanes), single)],
        count * 20_000_000,
        block=count,
    )
    feed_lanes = feed_parts.shape[-1]
    both = jnp.concatenate([share_sum(feed_parts), seq_rows(branch_flat)], axis=2)
    raw_grad, both, out_far, *state_got = tie(raw_grad, both, out_far, *state_got)
    out_arrived = flip(out_far, 2)
    both = exchange(both)

    pre_grad, mix_grad, tail_grad, edge_grad = run_backward(
        where, pre, pre_halo, columns, conv, scalars, raw_grad, saved, entering, state_got,
        heads, key_width, value_width, quarter,
    )
    arrived = shifted_along(edge_grad, "seq", -1)
    arrived, both, out_arrived = tie(arrived, both, out_arrived)
    result = residual + (out_own + out_arrived.astype(single))
    branch_parts = both[:, :, feed_lanes:]
    settled = [
        (pre_grad, by_rows(2 * qk + value_lanes)),
        (tail_grad, WHOLE),
        (arrived, WHOLE),
        (where, SCALAR),
    ]
    du_mix, last_own, last_far, last_pair, last_owned = blocked_call(
        functools.partial(settle_grads_kernel, quarter=quarter),
        "settle_grads",
        count,
        [
            settled[0],
            (normed_all, pieces(width)),
            (inner, by_rows(3 * low_rank)),
            (table, by_rows(8)),
            *settled[1:],
            (column_sets, WHOLE),
            (up_qk, WHOLE),
            (up_vg, part(low_rank, 0)),
            (mixer_down_late, WHOLE),
            (branch_res_grad, WHOLE),
        ],
        [
            ((count, 3 * low_rank), bfloat, "rows"),
            ((low_rank, 5 * block_width), bfloat, "whole"),
            ((low_rank, 5 * block_width), bfloat, "whole"),
            ((2 * low_rank, 5 * block_width), bfloat, "whole"),
            ((low_rank, 2 * qk + value_lanes), bfloat, "whole"),
        ],
        [
            pltpu.VMEM((count, 2 * qk + value_lanes), bfloat),
            pltpu.VMEM((3 * low_rank, width), single),
            pltpu.VMEM((low_rank, 2 * qk + value_lanes), single),
        ],
        count * 4_000_000,
        block=count,
    )
    last_own, last_far = near_sum((last_own, last_far, last_pair))
    last_far, gate_grad = tie(last_far, gate_grad)
    (normed_part,) = blocked_call(
        functools.partial(settle_kernel, quarter=quarter),
        "settle",
        count,
        [
            settled[0],
            (gate_grad, by_rows(value_lanes)),
            (du_mix, by_rows(3 * low_rank)),
            (du_outgate, by_rows(low_rank)),
            (mix_grad, by_rows(8)),
            *settled[1:],
            (down, part(4 * low_rank, 0)),
            (weight_mix, WHOLE),
            (w_query, WHOLE),
            (w_key, WHOLE),
            (w_value, WHOLE),
            (w_gate_out, WHOLE),
        ],
        [((count, width), bfloat, "parts")],
        [
            pltpu.VMEM((STEP, 2 * qk + value_lanes), bfloat),
            pltpu.VMEM((width, 2 * qk + 2 * value_lanes), bfloat),
            pltpu.VMEM((5 * low_rank, width), bfloat),
        ],
        count * 10_000_000,
    )
    last_flat = jnp.concatenate([low(far_sum(last_own, last_far)), last_owned], axis=1)
    feed_rows = all_rows(both)
    feed_pieces = gather_rows(feed_rows[:, : 3 * block_width])
    last_lanes = last_flat.shape[1]
    both = exchange(jnp.concatenate([seq_rows(last_flat), share_sum(branch_parts)], axis=2))
    branch_rows = all_rows(both)
    last_parts = both[:, :, :last_lanes]
    normed_grad = far_sum(*near_sum(normed_part))
    input_grad = residual_grad + rms_back(input_float, norm1_gain, normed_grad)
    last_parts, *feed_pieces = tie(last_parts, *feed_pieces)
    last_rows = all_rows(exchange(share_sum(last_parts)))
    last_pieces = gather_rows(last_rows[:, : 5 * block_width])
    down_grad, qk_grad, vg_grad, ff_grads, out_grads, ffd_grads, res_grad = assemble(
        where,
        [*last_pieces, *feed_pieces],
        last_rows,
        feed_rows,
        branch_rows,
        padded,
        [
            (6, low_rank, width),
            (2, low_rank, qk),
            (2, low_rank, value_lanes),
            (2, low_rank, hidden_width),
            (low_rank, value_lanes),
            (low_rank, hidden_width),
            (2, low_rank, width),
        ],
    )

    def as_down(rows):
        return rows.reshape(rows.shape[:-2] + (sets, rank, -1)).swapaxes(-1, -2)

    def as_up(rows):
        return rows.reshape(rows.shape[0], sets, rank, -1)

    return (
        low(result),
        input_grad,
        as_down(down_grad),
        as_up(qk_grad),
        as_up(vg_grad),
        as_up(ff_grads),
        as_down(out_grads),
        as_down(ffd_grads),
        as_up(res_grad),
    )


def solution(mesh):
    rows = P(("seq", "head"), None)
    lanes = P(None, "head")
    last = P(None, None, None, "head")
    middle = P(None, "head", None)
    in_specs = (
        rows, rows, P(), P(), P(), lanes, lanes, lanes, lanes, lanes, lanes,
        P(None, None, "head"), P("head"), P("head"), lanes, P(), P("head", None), P(), lanes,
        lanes, P("head", None), P(), last, last, last, middle, middle, P(),
    )
    out_specs = (rows, rows, P(), last, last, last, middle, middle, P())
    return jax.shard_map(
        on_device, mesh=mesh, in_specs=in_specs, out_specs=out_specs, check_vma=False
    )
```

```python
import functools

import jax
import jax.numpy as jnp
from jax import lax
from jax.experimental import pallas as pl
from jax.experimental.pallas import tpu as pltpu
from jax.sharding import PartitionSpec as P

CHUNK = 128
STEP = 256
HALO = 16
DOC_MAX = 4096
EPS = 1e-06
VMEM_LIMIT = 56 * 1024 * 1024
bfloat = jnp.bfloat16
single = jnp.float32


def contract(left, right, left_dim, right_dim):
    return lax.dot_general(
        left,
        right,
        (((left_dim,), (right_dim,)), ((), ())),
        preferred_element_type=single,
    )


def nn(left, right):
    return contract(left, right, 1, 0)


def nt(left, right):
    return contract(left, right, 1, 1)


def tn(left, right):
    return contract(left, right, 0, 0)


def low(array):
    return array.astype(bfloat)


def iotas():
    rows = lax.broadcasted_iota(jnp.int32, (CHUNK, CHUNK), 0)
    columns = lax.broadcasted_iota(jnp.int32, (CHUNK, CHUNK), 1)
    return rows, columns


def split_two(array):
    high = low(array)
    return high, low(array - high.astype(single))


def near_exact(left, right):
    left_high, left_low = split_two(left)
    right_high, right_low = split_two(right)
    return nn(
        jnp.concatenate([left_high, left_high, left_low], axis=1),
        jnp.concatenate([right_high, right_low, right_high], axis=0),
    )


def ones_product(ones, array):
    high = low(array)
    rest = array - high.astype(single)
    middle = low(rest)
    lowest = low(rest - middle.astype(single))
    return nn(
        jnp.concatenate([ones, ones, ones], axis=1),
        jnp.concatenate([high, middle, lowest], axis=0),
    )


def unit_lower_inverses(stricts, rows, columns):
    eye = (rows == columns).astype(single)
    differ = rows ^ columns
    block = 8
    inner = [jnp.where(differ < block, strict, 0.0) for strict in stricts]
    second = [near_exact(a, a) for a in inner]
    inverse = [near_exact(eye - a, eye + b) for a, b in zip(inner, second)]
    fourth = [near_exact(b, b) for b in second]
    inverse = [near_exact(a, eye + b) for a, b in zip(inverse, fourth)]
    while block < CHUNK:
        between = (differ >= block) & (differ < 2 * block)
        off = [jnp.where(between, strict, 0.0) for strict in stricts]
        part = [near_exact(a, b) for a, b in zip(off, inverse)]
        inverse = [a - near_exact(a, b) for a, b in zip(inverse, part)]
        block = 2 * block
    return inverse


def softplus(value):
    return jnp.maximum(value, 0.0) + jnp.log(1.0 + jnp.exp(-jnp.abs(value)))


def sigmoid(value):
    return 1.0 / (1.0 + jnp.exp(-value))


def gates(decay, start, rows, columns):
    lower_ones = low((rows >= columns).astype(single))
    total = ones_product(lower_ones, jnp.broadcast_to(decay, (CHUNK, CHUNK)))
    linked = (rows >= columns) & (columns >= start)
    within = jnp.where(linked, jnp.exp(jnp.where(linked, total - total.T, 0.0)), 0.0)
    running = total[:, :1]
    carried = jnp.where(start < 0, jnp.exp(running), 0.0)
    last = running[CHUNK - 1 : CHUNK]
    ending = jnp.where(
        rows[:, :1] >= start[CHUNK - 1 : CHUNK], jnp.exp(jnp.minimum(last - running, 0.0)), 0.0
    )
    return within, carried, ending


def convolved(window, starts, weights, base):
    positions = base + lax.broadcasted_iota(jnp.int32, (STEP, 1), 0)
    taps = weights.shape[0]
    total = None
    for tap in range(taps):
        back = taps - 1 - tap
        term = window[HALO - back : HALO - back + STEP, :] * weights[tap : tap + 1, :]
        if back:
            term = jnp.where(positions - back >= starts, term, 0.0)
        total = term if total is None else total + term
    return total


def head_scales(rows, width):
    return lax.rsqrt(jnp.sum(rows * rows, axis=-1, keepdims=True) + EPS)


def forward_kernel(
    place,
    rows_ref,
    halo_ref,
    column_ref,
    weight_ref,
    scalar_ref,
    out_ref,
    map_ref,
    written_ref,
    state_ref,
    inverse_ref,
    end_ref,
    sent_ref,
    sent_state_ref,
    window,
    state,
    *,
    heads,
    key_width,
    value_width,
):
    step = pl.program_id(0)
    wide = value_width + key_width
    base = step * STEP
    rows, columns = iotas()

    @pl.when(step == 0)
    def _():
        window[0:HALO, :] = halo_ref[...].astype(single)
        for h in range(heads):
            state[h, :, :value_width] = jnp.zeros((key_width, value_width), single)
            state[h, :, value_width:] = (rows == columns).astype(single)

    @pl.when(step > 0)
    def _():
        window[0:HALO, :] = window[STEP : STEP + HALO, :]

    window[HALO:, :] = rows_ref[...].astype(single)
    info = column_ref[...]
    starts = info[:, 2 * heads : 2 * heads + 1].astype(jnp.int32)
    before = convolved(window, starts, weight_ref[...], base)
    active = before * sigmoid(before)
    qk_lanes = heads * key_width
    chunks = STEP // CHUNK
    local, stricts = [], []
    for c in range(chunks):
        span = slice(c * CHUNK, (c + 1) * CHUNK)
        for h in range(heads):
            query = active[span, h * key_width : (h + 1) * key_width]
            key = active[span, qk_lanes + h * key_width : qk_lanes + (h + 1) * key_width]
            value = active[
                span, 2 * qk_lanes + h * value_width : 2 * qk_lanes + (h + 1) * value_width
            ]
            query = query * (head_scales(query, key_width) * key_width ** (-0.5))
            key = key * head_scales(key, key_width)
            beta = sigmoid(info[span, h : h + 1])
            decay = -scalar_ref[0, h] * softplus(
                info[span, heads + h : heads + h + 1] + scalar_ref[1, h]
            )
            within, carried, ending = gates(
                decay, starts[span] - (base + c * CHUNK), rows, columns
            )
            query, key = low(query), low(key)
            strict = jnp.where(rows > columns, within * nt(key, key), 0.0) * beta
            mixed = low(within * nt(query, key))
            stricts.append(strict)
            local.append((query, key, value, beta, carried, ending, mixed))
    inverses = [low(a) for a in unit_lower_inverses(stricts, rows, columns)]
    each = range(heads)
    now = [state[h] for h in each]
    for c in range(chunks):
        span = slice(c * CHUNK, (c + 1) * CHUNK)
        here = [local[c * heads + h] for h in each]
        inverse = [inverses[c * heads + h] for h in each]
        now_low = [low(a) for a in now]
        read = [nn(here[h][1], now_low[h]) for h in each]
        asked = [nn(here[h][0], now_low[h]) for h in each]
        target = []
        for h in each:
            query, key, value, beta, carried, ending, mixed = here[h]
            gap = -(carried * beta) * read[h]
            target.append(
                jnp.concatenate(
                    [beta * value + gap[:, :value_width], gap[:, value_width:]], axis=1
                )
            )
        written = [nn(inverse[h], low(target[h])) for h in each]
        added = [tn(here[h][1], low(here[h][5] * written[h])) for h in each]
        inner = [nn(here[h][6], low(written[h])) for h in each]
        for h in each:
            carried = here[h][4]
            inverse_ref[span, h * CHUNK : (h + 1) * CHUNK] = inverse[h]
            state_ref[c, h] = now_low[h]
            written_ref[span, h * wide : (h + 1) * wide] = low(written[h])
            output = carried * asked[h] + inner[h]
            out_ref[span, h * value_width : (h + 1) * value_width] = output[:, :value_width]
            map_ref[span, h * key_width : (h + 1) * key_width] = low(output[:, value_width:])
        now = [here[h][4][CHUNK - 1 : CHUNK] * now[h] + added[h] for h in each]
    for h in each:
        state[h] = now[h]

    @pl.when(step == pl.num_programs(0) - 1)
    def _():
        final = state[...]
        end_ref[...] = final
        sent_ref[...] = low(final)
        sent_state_ref[...] = low(final[:, :, :value_width])


def backward_kernel(
    place,
    rows_ref,
    before_ref,
    halo_ref,
    column_ref,
    weight_ref,
    scalar_ref,
    grad_ref,
    written_ref,
    state_ref,
    inverse_ref,
    end_ref,
    entering_ref,
    *rest,
    hops,
    heads,
    key_width,
    value_width,
):
    got_refs, rest = rest[:hops], rest[hops:]
    out_ref, mix_ref, tail_ref, edge_ref, window, shifted, shifted_start, cotangent, ahead = rest
    step = pl.program_id(0)
    steps = pl.num_programs(0)
    wide = value_width + key_width
    base = (steps - 1 - step) * STEP
    rows, columns = iotas()
    qk_lanes = heads * key_width
    lanes = window.shape[1]
    taps = weight_ref.shape[0]

    @pl.when(step == 0)
    def _():
        shifted[STEP : STEP + 8, :] = jnp.zeros((8, lanes), single)
        shifted_start[STEP : STEP + 8, :] = jnp.zeros((8, 1), jnp.int32)
        for h in range(heads):
            passed = got_refs[0][h].astype(single)
            for hop in range(1, hops):
                passed = passed + got_refs[hop][h].astype(single)
            cotangent[h] = passed
            ahead[h] = end_ref[h, :, :value_width] + nn(
                low(end_ref[h, :, value_width:]), low(entering_ref[h])
            )

    @pl.when(step > 0)
    def _():
        shifted[STEP : STEP + 8, :] = shifted[0:8, :]
        shifted_start[STEP : STEP + 8, :] = shifted_start[0:8, :]

    window[0:HALO, :] = jnp.where(
        step == steps - 1, halo_ref[...].astype(single), before_ref[...].astype(single)
    )
    window[HALO:, :] = rows_ref[...].astype(single)
    info = column_ref[...]
    starts = info[:, 2 * heads : 2 * heads + 1].astype(jnp.int32)
    positions = base + lax.broadcasted_iota(jnp.int32, (STEP, 1), 0)
    before = convolved(window, starts, weight_ref[...], base)
    gate = sigmoid(before)
    active = before * gate
    slope = gate * (1.0 + before * (1.0 - gate))
    upper_ones = low((rows <= columns).astype(single))
    last_row = rows[:, :1] == CHUNK - 1
    chunks = STEP // CHUNK
    each = range(heads)
    items = [(c, h) for c in range(chunks) for h in each]
    spans = {item: slice(item[0] * CHUNK, (item[0] + 1) * CHUNK) for item in items}
    entering = [low(entering_ref[h]) for h in each]
    root = key_width ** (-0.5)

    def per(function):
        return {item: function(*item) for item in items}

    def q_lanes(h):
        return slice(h * key_width, (h + 1) * key_width)

    def k_lanes(h):
        return slice(qk_lanes + h * key_width, qk_lanes + (h + 1) * key_width)

    def v_lanes(h):
        return slice(2 * qk_lanes + h * value_width, 2 * qk_lanes + (h + 1) * value_width)

    def kept(c, h, part):
        return written_ref[spans[c, h], h * wide : (h + 1) * wide][:, part]

    values, maps = slice(0, value_width), slice(value_width, wide)
    query_raw = per(lambda c, h: active[spans[c, h], q_lanes(h)])
    key_raw = per(lambda c, h: active[spans[c, h], k_lanes(h)])
    query_scale = per(lambda c, h: head_scales(query_raw[c, h], key_width))
    key_scale = per(lambda c, h: head_scales(key_raw[c, h], key_width))
    query = per(lambda c, h: query_raw[c, h] * (query_scale[c, h] * root))
    key = per(lambda c, h: key_raw[c, h] * key_scale[c, h])
    query_low = per(lambda c, h: low(query[c, h]))
    key_low = per(lambda c, h: low(key[c, h]))
    beta = per(lambda c, h: sigmoid(info[spans[c, h], h : h + 1]))
    raw = per(lambda c, h: info[spans[c, h], heads + h : heads + h + 1] + scalar_ref[1, h])
    gated = per(
        lambda c, h: gates(
            -scalar_ref[0, h] * softplus(raw[c, h]),
            starts[spans[c, h]] - (base + c * CHUNK),
            rows,
            columns,
        )
    )
    within = per(lambda c, h: gated[c, h][0])
    carried = per(lambda c, h: gated[c, h][1])
    ending = per(lambda c, h: gated[c, h][2])
    mixed = per(lambda c, h: low(within[c, h] * nt(query_low[c, h], key_low[c, h])))
    written = per(
        lambda c, h: kept(c, h, values).astype(single) + nn(kept(c, h, maps), entering[h])
    )
    start_state = per(
        lambda c, h: state_ref[c, h][:, values].astype(single)
        + nn(state_ref[c, h][:, maps], entering[h])
    )
    written_low = per(lambda c, h: low(written[c, h]))
    start_low = per(lambda c, h: low(start_state[c, h]))
    grad = per(lambda c, h: grad_ref[spans[c, h], h * value_width : (h + 1) * value_width])
    grad_low = grad
    carried_grad = per(lambda c, h: low(carried[c, h] * grad[c, h].astype(single)))
    from_output = per(lambda c, h: tn(mixed[c, h], grad_low[c, h]))
    state_part = per(lambda c, h: tn(query_low[c, h], carried_grad[c, h]))
    mixed_grad = per(lambda c, h: low(within[c, h] * nt(grad_low[c, h], written_low[c, h])))
    query_grad = per(
        lambda c, h: nt(carried_grad[c, h], start_low[c, h]) + nn(mixed_grad[c, h], key_low[c, h])
    )
    key_write = per(lambda c, h: tn(mixed_grad[c, h], query_low[c, h]))
    later, later_low, solved, value_grad, read_grad = {}, {}, {}, {}, {}
    now = [cotangent[h] for h in each]
    for c in reversed(range(chunks)):
        for h in each:
            later[c, h], later_low[c, h] = now[h], low(now[h])
        from_state = [nn(key_low[c, h], later_low[c, h]) for h in each]
        written_grad = [low(from_output[c, h] + ending[c, h] * from_state[h]) for h in each]
        for h in each:
            inverse = inverse_ref[spans[c, h], h * CHUNK : (h + 1) * CHUNK]
            solved[c, h] = tn(inverse, written_grad[h])
        for h in each:
            value_grad[c, h] = beta[c, h] * solved[c, h]
            read_grad[c, h] = low(-carried[c, h] * value_grad[c, h])
        now = [
            carried[c, h][CHUNK - 1 : CHUNK] * now[h]
            + state_part[c, h]
            + tn(key_low[c, h], read_grad[c, h])
            for h in each
        ]
    following = {
        (c, h): start_state[c + 1, h] if c + 1 < chunks else ahead[h] for c, h in items
    }
    at_end = per(lambda c, h: jnp.sum(later[c, h] * following[c, h], keepdims=True))
    for h in each:
        cotangent[h] = now[h]
        ahead[h] = start_state[0, h]
    strict_grad = per(
        lambda c, h: low(
            jnp.where(
                rows > columns, -within[c, h] * nt(low(value_grad[c, h]), written_low[c, h]), 0.0
            )
        )
    )
    key_read = per(
        lambda c, h: nt(read_grad[c, h], start_low[c, h]) + nn(strict_grad[c, h], key_low[c, h])
    )
    key_write = per(
        lambda c, h: key_write[c, h]
        + tn(strict_grad[c, h], key_low[c, h])
        + nt(low(ending[c, h] * written[c, h]), later_low[c, h])
    )
    query_dot = per(
        lambda c, h: jnp.sum(query[c, h] * query_grad[c, h], axis=-1, keepdims=True)
    )
    running_grad = per(
        lambda c, h: query_dot[c, h]
        + jnp.sum(key[c, h] * (key_read[c, h] - key_write[c, h]), axis=-1, keepdims=True)
        + jnp.where(last_row, at_end[c, h], 0.0)
    )
    decay_sum = per(
        lambda c, h: ones_product(
            upper_ones, jnp.broadcast_to(running_grad[c, h], (CHUNK, CHUNK))
        )[:, :1]
    )
    decay_grad = per(
        lambda c, h: jnp.where(
            positions[spans[c, h]] == starts[spans[c, h]],
            0.0,
            -scalar_ref[0, h] * sigmoid(raw[c, h]) * decay_sum[c, h],
        )
    )
    beta_grad = per(
        lambda c, h: jnp.sum(solved[c, h] * written[c, h], axis=-1, keepdims=True)
        * sigmoid(-info[spans[c, h], h : h + 1])
    )
    for c, h in items:
        span = spans[c, h]
        key_grad = key_read[c, h] + key_write[c, h]
        key_dot = jnp.sum(key[c, h] * key_grad, axis=-1, keepdims=True)
        query_active = (query_scale[c, h] * root) * query_grad[c, h] - query_raw[c, h] * (
            query_scale[c, h] * query_scale[c, h] * query_dot[c, h]
        )
        key_active = key_scale[c, h] * (key_grad - key[c, h] * key_dot)
        shifted[span, q_lanes(h)] = query_active * slope[span, q_lanes(h)]
        shifted[span, k_lanes(h)] = key_active * slope[span, k_lanes(h)]
        shifted[span, v_lanes(h)] = value_grad[c, h] * slope[span, v_lanes(h)]
    for c in range(chunks):
        mix_ref[c * CHUNK : (c + 1) * CHUNK, :] = jnp.concatenate(
            [beta_grad[c, h] for h in each]
            + [decay_grad[c, h] for h in each]
            + [jnp.zeros((CHUNK, mix_ref.shape[1] - 2 * heads), single)],
            axis=1,
        )
    shifted_start[0:STEP, :] = starts
    total = None
    for tap in range(taps):
        back = taps - 1 - tap
        term = shifted[back : back + STEP, :] * weight_ref[tap : tap + 1, :]
        if back:
            term = jnp.where(positions >= shifted_start[back : back + STEP, :], term, 0.0)
        total = term if total is None else total + term
    out_ref[...] = low(total)

    @pl.when(step == 0)
    def _():
        tail_ref[...] = total[STEP - HALO :, :]

    @pl.when(step == steps - 1)
    def _():
        window[0:8, :] = jnp.zeros((8, lanes), single)
        window[8:16, :] = shifted[0:8, :]
        early = lax.broadcasted_iota(jnp.int32, (8, 1), 0) - 8
        collected = jnp.zeros((8, lanes), single)
        for tap in range(taps - 1):
            back = taps - 1 - tap
            reader = early + back
            reader_start = jnp.zeros((8, 1), jnp.int32)
            for t in range(back):
                reader_start = jnp.where(reader == t, shifted_start[t : t + 1, :], reader_start)
            term = window[back : back + 8, :] * weight_ref[tap : tap + 1, :]
            collected = collected + jnp.where(
                (reader >= 0) & (early >= reader_start), term, 0.0
            )
        edge_ref[0:8, :] = jnp.zeros((8, lanes), single)
        edge_ref[8:16, :] = collected


def block_place(step, place, per_quarter):
    return ((step // per_quarter) ^ place[0]) * per_quarter + step % per_quarter


def run_forward(place, rows, halo, columns, weights, scalars, heads, key_width, value_width, quarter):
    count, lanes = columns.shape[0], rows.shape[1]
    steps, per_quarter = count // STEP, quarter // STEP
    wide = value_width + key_width
    chunks = STEP // CHUNK
    at = lambda i, place: (block_place(i, place, per_quarter), 0)
    fixed = lambda i, place: (0, 0)
    body = functools.partial(
        forward_kernel, heads=heads, key_width=key_width, value_width=value_width
    )
    shapes = (
        jax.ShapeDtypeStruct((count, heads * value_width), single),
        jax.ShapeDtypeStruct((count, heads * key_width), bfloat),
        jax.ShapeDtypeStruct((count, heads * wide), bfloat),
        jax.ShapeDtypeStruct((count // CHUNK, heads, key_width, wide), bfloat),
        jax.ShapeDtypeStruct((count, heads * CHUNK), bfloat),
        jax.ShapeDtypeStruct((heads, key_width, wide), single),
        jax.ShapeDtypeStruct((heads, key_width, wide), bfloat),
        jax.ShapeDtypeStruct((heads, key_width, value_width), bfloat),
    )
    return pl.pallas_call(
        body,
        out_shape=shapes,
        grid_spec=pltpu.PrefetchScalarGridSpec(
            num_scalar_prefetch=1,
            grid=(steps,),
            in_specs=[
                pl.BlockSpec((STEP, lanes), at),
                pl.BlockSpec((HALO, lanes), lambda i, place: (0, 0)),
                pl.BlockSpec((STEP, columns.shape[1]), at),
                pl.BlockSpec(weights.shape, fixed),
                pl.BlockSpec(memory_space=pltpu.SMEM),
            ],
            out_specs=[
                pl.BlockSpec((STEP, heads * value_width), at),
                pl.BlockSpec((STEP, heads * key_width), at),
                pl.BlockSpec((STEP, heads * wide), at),
                pl.BlockSpec((chunks, heads, key_width, wide), lambda i, place: (i, 0, 0, 0)),
                pl.BlockSpec((STEP, heads * CHUNK), at),
                pl.BlockSpec((heads, key_width, wide), lambda i, place: (0, 0, 0)),
                pl.BlockSpec((heads, key_width, wide), lambda i, place: (0, 0, 0)),
                pl.BlockSpec((heads, key_width, value_width), lambda i, place: (0, 0, 0)),
            ],
            scratch_shapes=[
                pltpu.VMEM((STEP + HALO, lanes), single),
                pltpu.VMEM((heads, key_width, wide), single),
            ],
        ),
        compiler_params=pltpu.CompilerParams(
            dimension_semantics=("arbitrary",), vmem_limit_bytes=VMEM_LIMIT
        ),
        cost_estimate=pl.CostEstimate(
            flops=count * 2_000_000, bytes_accessed=count * 10_000, transcendentals=count * 2000
        ),
        name="delta_forward",
    )(place, rows, halo, columns, weights, scalars)


def run_backward(
    place, rows, halo, columns, weights, scalars, grad, saved, entering, got, heads,
    key_width, value_width, quarter,
):
    written, states, inverses, end = saved
    count, lanes = columns.shape[0], rows.shape[1]
    steps, per_quarter = count // STEP, quarter // STEP
    wide = value_width + key_width
    chunks = STEP // CHUNK

    def at(i, place):
        return (block_place(steps - 1 - i, place, per_quarter), 0)

    def halo_at(i, place):
        here = steps - 1 - i
        inner = block_place(jnp.maximum(here - 1, 0), place, per_quarter)
        ratio = STEP // HALO
        return (inner * ratio + ratio - 1, 0)

    fixed = lambda i, place: (0, 0)
    whole = lambda i, place: (0, 0, 0)
    body = functools.partial(
        backward_kernel,
        hops=len(got),
        heads=heads,
        key_width=key_width,
        value_width=value_width,
    )
    shapes = (
        jax.ShapeDtypeStruct((count, lanes), bfloat),
        jax.ShapeDtypeStruct((count, columns.shape[1]), single),
        jax.ShapeDtypeStruct((HALO, lanes), single),
        jax.ShapeDtypeStruct((HALO, lanes), single),
    )
    return pl.pallas_call(
        body,
        out_shape=shapes,
        grid_spec=pltpu.PrefetchScalarGridSpec(
            num_scalar_prefetch=1,
            grid=(steps,),
            in_specs=[
                pl.BlockSpec((STEP, lanes), at),
                pl.BlockSpec((HALO, lanes), halo_at),
                pl.BlockSpec((HALO, lanes), fixed),
                pl.BlockSpec((STEP, columns.shape[1]), at),
                pl.BlockSpec(weights.shape, fixed),
                pl.BlockSpec(memory_space=pltpu.SMEM),
                pl.BlockSpec((STEP, heads * value_width), at),
                pl.BlockSpec((STEP, heads * wide), at),
                pl.BlockSpec(
                    (chunks, heads, key_width, wide), lambda i, place: (steps - 1 - i, 0, 0, 0)
                ),
                pl.BlockSpec((STEP, heads * CHUNK), at),
                pl.BlockSpec(end.shape, whole),
                pl.BlockSpec(entering.shape, whole),
            ]
            + [pl.BlockSpec(part.shape, whole) for part in got],
            out_specs=[
                pl.BlockSpec((STEP, lanes), at),
                pl.BlockSpec((STEP, columns.shape[1]), at),
                pl.BlockSpec((HALO, lanes), fixed),
                pl.BlockSpec((HALO, lanes), fixed),
            ],
            scratch_shapes=[
                pltpu.VMEM((STEP + HALO, lanes), single),
                pltpu.VMEM((STEP + 8, lanes), single),
                pltpu.VMEM((STEP + 8, 1), jnp.int32),
                pltpu.VMEM((heads, key_width, value_width), single),
                pltpu.VMEM((heads, key_width, value_width), single),
            ],
        ),
        compiler_params=pltpu.CompilerParams(
            dimension_semantics=("arbitrary",), vmem_limit_bytes=VMEM_LIMIT
        ),
        cost_estimate=pl.CostEstimate(
            flops=count * 3_000_000, bytes_accessed=count * 12_000, transcendentals=count * 3000
        ),
        name="delta_backward",
    )(
        place, rows, rows, halo, columns, weights, scalars, grad, written, states, inverses, end,
        entering, *got,
    )


def chosen_columns(table, column_sets):
    return column_sets[0:1, :] == table[:, 1:2]


def masked(product, chosen):
    return low(jnp.where(chosen, product, 0.0))


def silu_parts(value):
    logistic = sigmoid(value)
    return logistic, value * logistic


def accumulate(ref, value, first):
    if first is True:
        ref[...] = value
    else:
        ref[...] = jnp.where(first, value, ref[...] + value)


def emit_blocks(parts, place, own_ref, far_ref, pair_ref):
    for k, part in enumerate(parts):
        rows, size = part.shape[0], part.shape[1] // 4
        lanes = slice(k * size, (k + 1) * size)
        for relative, target, row in (
            (0, own_ref, 0), (2, far_ref, 0), (1, pair_ref, 0), (3, pair_ref, rows)
        ):
            start = pl.multiple_of((place ^ relative) * size, 128)
            target[row : row + rows, lanes] = low(part[:, pl.ds(start, size)])


def at_end(fill):
    pl.when(pl.program_id(0) == pl.num_programs(0) - 1)(fill)


def at_start(fill):
    pl.when(pl.program_id(0) == 0)(fill)


def project_kernel(
    rows_ref, table_ref, sets_ref, down_ref, mix_ref, wq_ref, wk_ref, wv_ref, wg_ref, up_qk_ref,
    up_vg_ref, *rest, with_halo,
):
    low_rank = sets_ref.shape[1]
    width, q_width = wq_ref.shape
    v_width = wv_ref.shape[1]
    bounds = [0, q_width, 2 * q_width, 2 * q_width + v_width, 2 * q_width + 2 * v_width]
    if with_halo:
        halo_ref, halo_table_ref, *rest = rest
        pre_ref, inner_ref, column_ref, gate_ref, inner_gate_ref, pre_halo_ref, joined = rest
    else:
        pre_ref, inner_ref, column_ref, gate_ref, inner_gate_ref, joined = rest
    weights = (wq_ref, wk_ref, wv_ref, wg_ref)
    ups = (up_qk_ref[0], up_qk_ref[1], up_vg_ref[:low_rank, :], up_vg_ref[low_rank:, :])
    for p in range(4):
        joined[:width, bounds[p] : bounds[p + 1]] = weights[p][...]
        joined[width:, bounds[p] : bounds[p + 1]] = ups[p]

    def projections(rows, table, store, maps):
        chosen = chosen_columns(table, sets_ref[...])
        product = nt(rows, down_ref[: maps * low_rank, :])
        inner = [
            masked(product[:, p * low_rank : (p + 1) * low_rank], chosen) for p in range(maps)
        ]
        for p in range(maps):
            output = nn(
                jnp.concatenate([rows, inner[p]], axis=1), joined[:, bounds[p] : bounds[p + 1]]
            )
            if p < 3:
                store[:, bounds[p] : bounds[p + 1]] = low(output)
            else:
                gate_ref[...] = output
        return inner

    if with_halo:
        projections(halo_ref[...], halo_table_ref[...], pre_halo_ref, 3)
    table = table_ref[...]
    rows = rows_ref[...]
    inner = projections(rows, table, pre_ref, 4)
    inner_gate_ref[...] = inner[3]
    for p in range(3):
        inner_ref[:, p * low_rank : (p + 1) * low_rank] = inner[p]
    column_ref[...] = jnp.concatenate([nt(rows, mix_ref[...])[:, :4], table[:, :4]], axis=1)


def head_outputs(raw_ref, map_ref, entering_ref, heads, key_width, value_width):
    outputs = []
    for h in range(heads):
        outputs.append(
            raw_ref[:, h * value_width : (h + 1) * value_width]
            + nn(map_ref[:, h * key_width : (h + 1) * key_width], entering_ref[h])
        )
    return outputs


def attend_kernel(
    raw_ref, map_ref, gate_ref, table_ref, gain_ref, sets_ref, wo_ref, down_ref, up_ref, *rest,
    heads, key_width, value_width, hops,
):
    got_refs, rest = rest[:hops], rest[hops:]
    part_ref, z_ref, inner_ref, entering_ref, joined = rest
    value_lanes = wo_ref.shape[0]

    @at_start
    def _():
        joined[:value_lanes, :] = wo_ref[...]
        joined[value_lanes:, :] = up_ref[...]
        for h in range(heads):
            state = got_refs[hops - 1][h].astype(single)
            for hop in range(hops - 1, 0, -1):
                got = got_refs[hop - 1][h]
                state = got[:, :value_width].astype(single) + nn(got[:, value_width:], low(state))
            entering_ref[h] = low(state)

    chosen = chosen_columns(table_ref[...], sets_ref[...])
    outputs = head_outputs(raw_ref, map_ref, entering_ref, heads, key_width, value_width)
    parts = []
    for h, output in enumerate(outputs):
        lanes = slice(h * value_width, (h + 1) * value_width)
        scale = lax.rsqrt(jnp.mean(output * output, axis=-1, keepdims=True) + EPS)
        _, gate = silu_parts(gate_ref[:, lanes])
        parts.append(low(output * scale * gain_ref[0:1, :] * gate))
    z = jnp.concatenate(parts, axis=1)
    z_ref[...] = z
    inner = masked(nt(z, down_ref[...]), chosen)
    inner_ref[...] = inner
    part_ref[...] = low(nn(jnp.concatenate([z, inner], axis=1), joined[...]))


def feed_before_kernel(
    grad_ref, table_ref, sets_ref, wd_ref, down_ffd_t_ref, up_ref, hidden_grad_ref, du_ref, joined
):
    hidden, width = wd_ref.shape

    @at_start
    def _():
        joined[:hidden, :width] = wd_ref[...]
        joined[:hidden, width:] = down_ffd_t_ref[...]
        joined[hidden:, :] = jnp.zeros((joined.shape[0] - hidden, joined.shape[1]), bfloat)

    grad = grad_ref[...]
    du_down = masked(nt(grad, up_ref[...]), chosen_columns(table_ref[...], sets_ref[...]))
    du_ref[...] = du_down
    hidden_grad_ref[...] = nt(jnp.concatenate([grad, du_down], axis=1), joined[...])


def feed_kernel(
    rows_ref, hidden_grad_ref, table_ref, sets_ref, down_ref, wg_ref, wu_ref, up_t_ref, up_ref,
    back_ref, hidden_ref, ff_grad_ref, inner_ref, du_ref,
    joined_gate, joined_up, joined_back,
):
    low_rank = sets_ref.shape[1]
    hidden, width = wg_ref.shape
    padded = joined_gate.shape[0]

    @at_start
    def _():
        for p, (joined, weight) in enumerate(((joined_gate, wg_ref), (joined_up, wu_ref))):
            joined[:hidden, :width] = weight[...]
            joined[:hidden, width:] = up_t_ref[p]
            joined[hidden:, :] = jnp.zeros((padded - hidden, joined.shape[1]), bfloat)
            joined_back[p * padded : p * padded + hidden, :] = weight[...]
            joined_back[p * padded + hidden : (p + 1) * padded, :] = jnp.zeros(
                (padded - hidden, width), bfloat
            )
        joined_back[2 * padded :, :] = down_ref[...]

    chosen = chosen_columns(table_ref[...], sets_ref[...])
    both = jnp.concatenate([chosen, chosen], axis=1)
    rows = rows_ref[...]
    inner = masked(nt(rows, down_ref[...]), both)
    inner_ref[...] = inner
    gate = nt(jnp.concatenate([rows, inner[:, :low_rank]], axis=1), joined_gate[...])
    up = nt(jnp.concatenate([rows, inner[:, low_rank:]], axis=1), joined_up[...])
    logistic, active = silu_parts(gate)
    hidden_ref[...] = low(active * up)
    hidden_grad = hidden_grad_ref[...]
    gate_grad = low(hidden_grad * up * logistic * (1.0 + gate * (1.0 - logistic)))
    up_grad = low(hidden_grad * active)
    du_gate = masked(nt(gate_grad, up_ref[0]), chosen)
    du_up = masked(nt(up_grad, up_ref[1]), chosen)
    du_ref[:, :low_rank] = du_gate
    du_ref[:, low_rank:] = du_up
    ff_grad_ref[:, :padded] = gate_grad
    ff_grad_ref[:, padded:] = up_grad
    back_ref[...] = low(
        nn(jnp.concatenate([gate_grad, up_grad, du_gate, du_up], axis=1), joined_back[...])
    )


def feed_after_kernel(
    rows_ref, grad_ref, hidden_ref, ff_grad_ref, inner_ref, du_ref, du_down_ref, table_ref,
    sets_ref, place_ref, wd_ref, down_ffd_ref, up_ref,
    out_ref, own_ref, far_ref, pair_ref, flat_ref,
    joined, down_sum, res_sum, flat_sum,
):
    first = pl.program_id(0) == 0
    low_rank = sets_ref.shape[1]
    width_hidden = wd_ref.shape[0]
    padded = down_ffd_ref.shape[1]

    @at_start
    def _():
        joined[:width_hidden, :] = wd_ref[...]
        joined[width_hidden:padded, :] = jnp.zeros(
            (padded - width_hidden, joined.shape[1]), bfloat
        )
        joined[padded:, :] = up_ref[...]

    hidden = hidden_ref[...]
    inner = inner_ref[...]
    u_down = masked(
        nt(hidden, down_ffd_ref[...]), chosen_columns(table_ref[...], sets_ref[...])
    )
    out_ref[...] = low(nn(jnp.concatenate([hidden, u_down], axis=1), joined[...]))
    accumulate(down_sum, tn(du_ref[...], rows_ref[...]), first)
    accumulate(res_sum, tn(u_down, grad_ref[...]), first)
    for k, grown in enumerate(
        (
            tn(inner[:, :low_rank], ff_grad_ref[:, :padded]),
            tn(inner[:, low_rank:], ff_grad_ref[:, padded:]),
            tn(du_down_ref[...], hidden),
        )
    ):
        accumulate(flat_sum.at[:, k * padded : (k + 1) * padded], grown, first)

    @at_end
    def _():
        flat_ref[...] = low(flat_sum[...])
        emit_blocks(
            (down_sum.at[:low_rank], down_sum.at[low_rank:], res_sum),
            place_ref[0], own_ref, far_ref, pair_ref,
        )


def branch_kernel(
    branch_ref, raw_ref, map_ref, gate_ref, table_ref, entering_ref, gain_ref, sets_ref, wo_ref,
    down_out_t_ref, up_ref, up_gate_ref, *rest,
    heads, key_width, value_width, hops, last,
):
    if last:
        before_ref, *rest = rest
        got_refs, rest = rest[: hops - 1], rest[hops - 1 :]
        raw_grad_ref, gate_grad_ref, du_out_ref, du_gate_ref, *rest = rest
        sent_refs, (joined,) = rest[:hops], rest[hops:]
    else:
        raw_grad_ref, gate_grad_ref, du_out_ref, du_gate_ref, total_ref, joined = rest
    width = wo_ref.shape[1]

    @at_start
    def _():
        joined[:, :width] = wo_ref[...]
        joined[:, width:] = down_out_t_ref[...]

    chosen = chosen_columns(table_ref[...], sets_ref[...])
    branch = branch_ref[...]
    outputs = head_outputs(raw_ref, map_ref, entering_ref, heads, key_width, value_width)
    du_out = masked(nt(branch, up_ref[...]), chosen)
    du_out_ref[...] = du_out
    mixed_grad = nt(jnp.concatenate([branch, du_out], axis=1), joined[...])
    gain = gain_ref[0:1, :]
    gate_grads = []
    for h, output in enumerate(outputs):
        lanes = slice(h * value_width, (h + 1) * value_width)
        scale = lax.rsqrt(jnp.mean(output * output, axis=-1, keepdims=True) + EPS)
        value = gate_ref[:, lanes]
        logistic, active = silu_parts(value)
        incoming = mixed_grad[:, lanes]
        gate_grads.append(
            low(
                incoming
                * (output * scale * gain)
                * (logistic * (1.0 + value * (1.0 - logistic)))
            )
        )
        scaled = gain * (incoming * active)
        dot = jnp.mean(output * scaled, axis=-1, keepdims=True)
        raw_grad = low(scale * scaled - output * (scale * scale * scale * dot))
        raw_grad_ref[:, lanes] = raw_grad
        grown = tn(map_ref[:, h * key_width : (h + 1) * key_width], raw_grad)
        if not last:
            total_ref[h] = grown
        else:
            passed = low(before_ref[h] + grown)
            sent_refs[0][h] = passed
            for hop in range(1, hops):
                passed = low(tn(got_refs[hop - 1][h][:, value_width:], passed))
                sent_refs[hop][h] = passed
    gate_grad = jnp.concatenate(gate_grads, axis=1)
    gate_grad_ref[...] = gate_grad
    du_gate_ref[...] = masked(nt(gate_grad, up_gate_ref[...]), chosen)


def branch_after_kernel(
    branch_ref, z_ref, u_out_ref, rows_ref, inner_ref, du_out_ref, du_gate_ref, gate_grad_ref,
    down_grad_ref, res_grad_ref, flat_ref,
    flat_sum,
):
    lanes = z_ref.shape[1]
    accumulate(down_grad_ref, tn(du_gate_ref[...], rows_ref[...]), True)
    accumulate(res_grad_ref, tn(u_out_ref[...], branch_ref[...]), True)
    accumulate(flat_sum.at[:, :lanes], tn(du_out_ref[...], z_ref[...]), True)
    accumulate(flat_sum.at[:, lanes:], tn(inner_ref[...], gate_grad_ref[...]), True)

    @at_end
    def _():
        flat_ref[...] = low(flat_sum[...])


def settled_rows(pre_ref, tail_ref, arrived_ref, place_ref, quarter, window):
    block = window.shape[0]
    start = ((3 ^ place_ref[0]) + 1) * quarter - HALO - pl.program_id(0) * block
    window[...] = pre_ref[...]

    @pl.when((start >= 0) & (start < block))
    def _():
        window[pl.ds(pl.multiple_of(start, HALO), HALO), :] = low(tail_ref[...] + arrived_ref[...])

    return window[...]


def settle_grads_kernel(
    pre_ref, rows_ref, inner_ref, table_ref, tail_ref, arrived_ref, place_ref, sets_ref,
    up_qk_ref, up_value_ref, down_late_ref, res_late_ref,
    du_ref, own_ref, far_ref, pair_ref, flat_ref,
    window, down_sum, flat_sum,
    *, quarter,
):
    low_rank = sets_ref.shape[1]
    q_width = up_qk_ref.shape[2]
    chosen = chosen_columns(table_ref[...], sets_ref[...])
    pre = settled_rows(pre_ref, tail_ref, arrived_ref, place_ref, quarter, window)
    query, key, value = pre[:, :q_width], pre[:, q_width : 2 * q_width], pre[:, 2 * q_width :]
    inner = inner_ref[...]
    du = jnp.concatenate(
        [
            masked(nt(query, up_qk_ref[0]), chosen),
            masked(nt(key, up_qk_ref[1]), chosen),
            masked(nt(value, up_value_ref[...]), chosen),
        ],
        axis=1,
    )
    du_ref[...] = du
    accumulate(down_sum, tn(du, rows_ref[...]), True)
    at = 0
    for p, part in enumerate((query, key, value)):
        accumulate(
            flat_sum.at[:, at : at + part.shape[1]],
            tn(inner[:, p * low_rank : (p + 1) * low_rank], part),
            True,
        )
        at += part.shape[1]

    @at_end
    def _():
        flat_ref[...] = low(flat_sum[...])
        emit_blocks(
            [down_sum.at[p * low_rank : (p + 1) * low_rank] for p in range(3)]
            + [down_late_ref, res_late_ref],
            place_ref[0], own_ref, far_ref, pair_ref,
        )


def settle_kernel(
    pre_ref, gate_grad_ref, du_ref, du_gate_ref, mix_ref, tail_ref, arrived_ref, place_ref,
    down_ref, mix_weight_ref, wq_ref, wk_ref, wv_ref, wg_ref,
    part_ref,
    window, joined, joined_small,
    *, quarter,
):
    q_width, v_width = wq_ref.shape[1], wv_ref.shape[1]

    @at_start
    def _():
        joined[:, :q_width] = wq_ref[...]
        joined[:, q_width : 2 * q_width] = wk_ref[...]
        joined[:, 2 * q_width : 2 * q_width + v_width] = wv_ref[...]
        joined[:, 2 * q_width + v_width :] = wg_ref[...]
        maps, mixes = down_ref.shape[0], mix_weight_ref.shape[0]
        spare = joined_small.shape[0] - maps - mixes
        joined_small[:maps, :] = down_ref[...]
        joined_small[maps:, :] = jnp.concatenate(
            [mix_weight_ref[...], jnp.zeros((spare, joined_small.shape[1]), bfloat)], axis=0
        )

    pre = settled_rows(pre_ref, tail_ref, arrived_ref, place_ref, quarter, window)
    mix = low(mix_ref[...])
    spare = joined_small.shape[0] - down_ref.shape[0] - mix.shape[1]
    small = jnp.concatenate(
        [du_ref[...], du_gate_ref[...], mix, jnp.zeros((mix.shape[0], spare), bfloat)], axis=1
    )
    part_ref[...] = low(
        nt(jnp.concatenate([pre, gate_grad_ref[...]], axis=1), joined[...])
        + nn(small, joined_small[...])
    )


def assemble_kernel(
    place_ref, *refs, padded,
):
    pieces_last, pieces_feed = refs[:4], refs[4:8]
    last_ref, feed_ref, branch_ref = refs[8:11]
    down_ref, qk_ref, vg_ref, ff_ref, out_ref, ffd_ref, res_ref = refs[11:]
    place = place_ref[0]
    size = pieces_last[0].shape[1] // 5
    first = [down_ref.at[p] for p in range(4)] + [res_ref.at[0]]
    second = [down_ref.at[4], down_ref.at[5], res_ref.at[1]]
    for relative in range(4):
        start = pl.multiple_of((place ^ relative) * size, 128)
        for targets, piece in ((first, pieces_last[relative]), (second, pieces_feed[relative])):
            for k, target in enumerate(targets):
                target[:, pl.ds(start, size)] = piece[:, k * size : (k + 1) * size].astype(single)
    qk, values, hidden = qk_ref.shape[2], vg_ref.shape[2], ff_ref.shape[2]

    def lanes(ref, start, width):
        return ref[:, start : start + width].astype(single)

    own = 5 * size
    qk_ref[0], qk_ref[1] = lanes(last_ref, own, qk), lanes(last_ref, own + qk, qk)
    vg_ref[0] = lanes(last_ref, own + 2 * qk, values)
    at = last_ref.shape[1] + 3 * size
    out_ref[...] = lanes(branch_ref, at, values)
    vg_ref[1] = lanes(branch_ref, at + values, values)
    ff_ref[0] = lanes(feed_ref, 0, hidden)
    ff_ref[1] = lanes(feed_ref, padded, hidden)
    ffd_ref[...] = lanes(feed_ref, 2 * padded, hidden)


def assemble(where, shared, last, feed, branch, padded, shapes):
    rows = last.shape[0]
    block = min(32, rows)

    def spec(shape):
        if len(shape) == 2:
            return pl.BlockSpec((block, shape[1]), lambda i: (i, 0))
        return pl.BlockSpec((shape[0], block, shape[2]), lambda i: (0, i, 0))

    arrays = [*shared, last, feed, branch]
    return pl.pallas_call(
        functools.partial(assemble_kernel, padded=padded),
        out_shape=tuple(jax.ShapeDtypeStruct(shape, single) for shape in shapes),
        grid=(rows // block,),
        in_specs=[pl.BlockSpec(memory_space=pltpu.SMEM)] + [spec(a.shape) for a in arrays],
        out_specs=[spec(shape) for shape in shapes],
        compiler_params=pltpu.CompilerParams(
            dimension_semantics=("arbitrary",), vmem_limit_bytes=VMEM_LIMIT
        ),
        name="assemble",
    )(where, *arrays)


WHOLE, SCALAR = "whole", "scalar"


def by_rows(width, lane_block=0):
    return ("rows", width, lane_block)


def part(rows, index):
    return ("part", rows, index)


def pieces(width):
    return ("pieces", width)


def blocked_call(
    body, name, count, inputs, outputs, scratch, flops, block=STEP, half=None, into=()
):
    if half is not None:
        block = count // 2
    steps = count // block if half is None else 1
    offset = half or 0
    per = max(steps // 4, 1)
    in_specs, arrays, moved, groups_in, extra = [], [], 0, [], []
    for array, kind in inputs:
        members = array if isinstance(array, (list, tuple)) else [array]
        groups_in.append(len(members))
        arrays += members
        moved += sum(a.size * a.dtype.itemsize for a in members)
        if kind == WHOLE:
            zeros = (0,) * array.ndim
            in_specs.append(
                pl.BlockSpec(
                    array.shape, lambda i, zeros=zeros: zeros, pipeline_mode=pl.Buffered(1)
                )
            )
        elif kind == SCALAR:
            in_specs.append(pl.BlockSpec(memory_space=pltpu.SMEM))
        elif kind[0] == "part":
            in_specs.append(
                pl.BlockSpec(
                    (kind[1], array.shape[1]),
                    lambda i, at=kind[2]: (at, 0),
                    pipeline_mode=pl.Buffered(1),
                )
            )
        elif kind[0] == "rows":
            in_specs.append(
                pl.BlockSpec((block, kind[1]), lambda i, lane=kind[2]: (i + offset, lane))
            )
        else:
            for b, member in enumerate(members):
                if steps == 1:
                    in_specs.append(pl.BlockSpec(member.shape, lambda i: (0, 0)))
                else:
                    in_specs.append(
                        pl.BlockSpec(
                            (block, kind[1]),
                            lambda i, b=b: (jnp.clip(i - b * per, 0, per - 1), 0),
                        )
                    )
            extra.append(pltpu.VMEM((block, kind[1]), members[0].dtype))
    out_specs, shapes, groups_out, aliases = [], [], [], {}
    into = list(into)
    held_arrays = []
    for shape, dtype, kind in outputs:
        if kind == "parts":
            quarter = shape[0] // 4
            spec = (block, shape[1])
            if steps == 1:
                for _ in range(2):
                    shapes.append(jax.ShapeDtypeStruct((quarter, shape[1]), dtype))
                    out_specs.append(pl.BlockSpec((quarter, shape[1]), lambda i: (0, 0)))
                groups_out.append(2)
            else:
                for rows in (quarter, quarter, 2 * quarter):
                    shapes.append(jax.ShapeDtypeStruct((rows, shape[1]), dtype))
                out_specs += [
                    pl.BlockSpec(spec, lambda i: (jnp.clip(i, 0, per - 1), 0)),
                    pl.BlockSpec(spec, lambda i: (jnp.clip(i - 2 * per, 0, per - 1), 0)),
                    pl.BlockSpec(
                        spec,
                        lambda i: (
                            jnp.clip(i - per, 0, per - 1) + jnp.clip(i - 3 * per + 1, 0, per), 0
                        ),
                    ),
                ]
                groups_out.append(3)
            extra.append(pltpu.VMEM(spec, dtype))
        else:
            groups_out.append(1)
            shapes.append(jax.ShapeDtypeStruct(shape, dtype))
            if kind == "rows":
                if into:
                    aliases[len(arrays) + len(held_arrays)] = len(shapes) - 1
                    held_arrays.append(into.pop(0))
                out_specs.append(pl.BlockSpec((block, shape[1]), lambda i: (i + offset, 0)))
            else:
                zeros = (0,) * len(shape)
                out_specs.append(pl.BlockSpec(shape, lambda i, zeros=zeros: zeros))
    in_specs += [pl.BlockSpec(memory_space=pl.ANY) for _ in held_arrays]

    def wrapped(*refs):
        refs = list(refs)
        spare = refs[len(in_specs) + len(out_specs) + len(scratch) :]
        own_scratch = refs[len(in_specs) + len(out_specs) : len(refs) - len(spare)]
        quarter = pl.program_id(0) // per
        given, later, at, used = [], [], 0, 0
        for size, (_, kind) in zip(groups_in, inputs):
            if kind[0] != "pieces":
                given.append(refs[at])
            else:
                held = spare[used]
                used += 1
                if steps == 1:
                    for b in range(size):
                        piece = refs[at + b]
                        held[b * piece.shape[0] : (b + 1) * piece.shape[0], :] = piece[...]
                else:
                    for b in range(size):

                        @pl.when(quarter == b)
                        def _(held=held, source=refs[at + b]):
                            held[...] = source[...]

                given.append(held)
            at += size
        at += len(held_arrays)
        for size in groups_out:
            if size == 1:
                given.append(refs[at])
            else:
                given.append(spare[used])
                later.append((spare[used], refs[at : at + size]))
                used += 1
            at += size
        body(*given, *own_scratch)
        for held, targets in later:
            if len(targets) == 2:
                rows = targets[0].shape[0]
                targets[0][...], targets[1][...] = held[:rows, :], held[rows:, :]
                continue
            for b, target in ((0, targets[0]), (2, targets[1]), (1, targets[2]), (3, targets[2])):

                @pl.when(quarter == b)
                def _(held=held, target=target):
                    target[...] = held[...]

    results = pl.pallas_call(
        wrapped,
        out_shape=tuple(shapes),
        grid=(steps,),
        in_specs=in_specs,
        out_specs=out_specs,
        scratch_shapes=list(scratch) + extra,
        input_output_aliases=aliases,
        compiler_params=pltpu.CompilerParams(
            dimension_semantics=("arbitrary",), vmem_limit_bytes=VMEM_LIMIT
        ),
        cost_estimate=pl.CostEstimate(flops=flops, bytes_accessed=moved, transcendentals=0),
        name=name,
    )(*arrays, *held_arrays)
    grouped, at = [], 0
    for size in groups_out:
        grouped.append(results[at] if size == 1 else results[at : at + size])
        at += size
    return grouped


def flip(array, bit):
    groups = lax.axis_size("head")
    return lax.ppermute(array, "head", [(i, i ^ bit) for i in range(groups)])


def gather_rows(array):
    far = flip(array, 2)
    near = flip(array, 1)
    return [array, near, far, flip(far, 1)]


def tie(*arrays):
    return lax.optimization_barrier(arrays)


def near_sum(parts):
    own, far, pair = parts
    size = own.shape[0]
    arrived = flip(pair, 1)
    return (
        own.astype(single) + arrived[:size].astype(single),
        low(far.astype(single) + arrived[size:].astype(single)),
    )


def halves_sum(first, second):
    near, corner = tie(flip(first[1], 1), second[1])
    return (
        first[0].astype(single) + near.astype(single),
        low(second[0].astype(single) + flip(corner, 1).astype(single)),
    )


def far_sum(own, far):
    return own + flip(far, 2).astype(single)


def shifted_along(array, axis, by):
    length = lax.axis_size(axis)
    pairs = [(i, i + by) for i in range(length) if 0 <= i + by < length]
    return lax.ppermute(array, axis, pairs)


def seq_rows(flat):
    members = lax.axis_size("seq")
    return flat.reshape(members, flat.shape[0] // members, flat.shape[1])


def share_sum(parts):
    summed = low(jnp.sum(parts.astype(single), axis=0))
    return jnp.broadcast_to(summed[None], parts.shape)


def exchange(parts):
    return lax.all_to_all(parts, "seq", 0, 0)


def all_rows(parts):
    return parts.reshape(-1, parts.shape[-1])


def rms_scale(rows, gain):
    return rows * lax.rsqrt(jnp.mean(rows * rows, axis=-1, keepdims=True) + EPS) * gain


def rms_back(rows, gain, incoming):
    _, back = jax.vjp(lambda value: rms_scale(value, gain), rows)
    return back(incoming)[0]


def on_device(
    block_input,
    out_grad,
    lengths,
    doc_sets,
    norm1_gain,
    w_query,
    w_key,
    w_value,
    conv_query,
    conv_key,
    conv_value,
    w_decay_beta,
    decay_rate,
    decay_bias,
    w_gate_out,
    out_gain,
    w_out,
    norm2_gain,
    w_gate,
    w_up,
    w_down,
    adapt_down,
    adapt_up_qk,
    adapt_up_vg,
    adapt_up_ff,
    adapt_down_out,
    adapt_down_ffd,
    adapt_up_res,
):
    groups = lax.axis_size("head")
    members = lax.axis_size("seq")
    place = lax.axis_index("head")
    quarter, width = block_input.shape
    count = quarter * groups
    heads = decay_rate.shape[0]
    key_width = w_query.shape[1] // heads
    value_width = w_value.shape[1] // heads
    sets, rank = adapt_down.shape[1], adapt_down.shape[3]
    low_rank = sets * rank
    qk = heads * key_width
    device_start = lax.axis_index("seq") * count
    starts = jnp.sum(
        jnp.where(
            jnp.arange(lengths.shape[0])[None, :] < jnp.arange(lengths.shape[0])[:, None],
            lengths[None, :],
            0,
        ),
        axis=1,
    )
    order = jnp.arange(groups, dtype=jnp.int32) ^ place

    def tables(positions):
        reached = positions[:, None] >= starts[None, :]
        token_start = jnp.max(jnp.where(reached, starts[None, :], -1), axis=1)
        ended = positions[:, None] >= (starts + lengths)[None, :]
        token_set = jnp.sum(jnp.where(reached & ~ended, doc_sets[None, :], 0), axis=1)
        pair = jnp.stack([token_start - device_start, token_set], axis=1).astype(single)
        return jnp.pad(pair, ((0, 0), (0, 8 - pair.shape[1])))

    table = tables(
        (
            device_start + order[:, None] * quarter + jnp.arange(quarter, dtype=jnp.int32)[None, :]
        ).reshape(-1)
    )
    halo_table = tables(device_start + jnp.arange(-HALO, 0, dtype=jnp.int32))
    column_sets = jnp.broadcast_to(
        (jnp.arange(low_rank, dtype=jnp.int32) // rank).astype(single)[None, :], (8, low_rank)
    )

    down = adapt_down.transpose(0, 1, 3, 2).reshape(6 * low_rank, width)
    up_qk = adapt_up_qk.reshape(2, low_rank, -1)
    up_vg = adapt_up_vg.reshape(2 * low_rank, -1)
    up_ff = adapt_up_ff.reshape(2, low_rank, -1)
    down_out = adapt_down_out.transpose(0, 2, 1).reshape(low_rank, -1)
    down_ffd = adapt_down_ffd.transpose(0, 2, 1).reshape(low_rank, -1)
    up_res = adapt_up_res.reshape(2 * low_rank, width)
    conv = jnp.concatenate([conv_query, conv_key, conv_value], axis=1).astype(single)
    scalars = jnp.stack([decay_rate, decay_bias])
    where = place.reshape(1).astype(jnp.int32)
    weight_mix = jnp.pad(
        w_decay_beta.transpose(1, 2, 0).reshape(2 * heads, width), ((0, 8 - 2 * heads), (0, 0))
    )
    gain = jnp.broadcast_to(out_gain[None, :], (8, value_width))
    hidden_width = w_down.shape[0]
    padded = -(-hidden_width // 256) * 256
    value_lanes = heads * value_width
    block_width = width // groups
    widen = lambda a: jnp.pad(a, [(0, 0)] * (a.ndim - 1) + [(0, padded - hidden_width)])

    input_float = block_input.astype(single)
    normed = low(rms_scale(input_float, norm1_gain))
    tail = normed[quarter - HALO :]
    halo = sum(
        lax.ppermute(
            tail,
            ("seq", "head"),
            [((s * groups) + groups - 1, (s + 1) * groups + h) for s in range(members - 1)],
        )
        for h in range(groups)
    )
    normed_near, normed_far = flip(normed, 1), flip(normed, 2)
    project_inputs = [
        (table, by_rows(8)),
        (column_sets, WHOLE),
        (down, part(4 * low_rank, 0)),
        (weight_mix, WHOLE),
        (w_query, WHOLE),
        (w_key, WHOLE),
        (w_value, WHOLE),
        (w_gate_out, WHOLE),
        (up_qk, WHOLE),
        (up_vg, WHOLE),
    ]
    project_outputs = [
        ((count, 2 * qk + value_lanes), bfloat, "rows"),
        ((count, 3 * low_rank), bfloat, "rows"),
        ((count, 8), single, "rows"),
        ((count, value_lanes), single, "rows"),
        ((count, low_rank), bfloat, "rows"),
    ]
    project_scratch = [pltpu.VMEM((width + low_rank, 2 * qk + 2 * value_lanes), bfloat)]
    projected = blocked_call(
        functools.partial(project_kernel, with_halo=False),
        "project_near",
        count,
        [([normed, normed_near], pieces(width)), *project_inputs],
        project_outputs,
        project_scratch,
        count * 2_000_000,
        half=0,
    )
    normed_far, projected[2] = tie(normed_far, projected[2])
    normed_all = [normed, normed_near, normed_far, flip(normed_far, 1)]
    pre, inner, columns, gate_input, inner_gate, pre_halo = blocked_call(
        functools.partial(project_kernel, with_halo=True),
        "project_far",
        count,
        [
            (normed_all[2:], pieces(width)),
            *project_inputs,
            (halo, WHOLE),
            (halo_table, WHOLE),
        ],
        project_outputs + [((HALO, 2 * qk + value_lanes), bfloat, "whole")],
        project_scratch,
        count * 2_000_000,
        half=1,
        into=projected,
    )
    out_grad_late, grad_near, pre = tie(out_grad, flip(out_grad, 1), pre)
    grad_far, grad_corner = flip(out_grad_late, 2), flip(grad_near, 2)
    raw_local, mapped, *saved, sent, sent_state = run_forward(
        where, pre, pre_halo, columns, conv, scalars, heads, key_width, value_width, quarter
    )

    hops = min(members - 1, -(-(DOC_MAX - 1) // count))
    got = [shifted_along(sent_state, "seq", hops)]
    got = [shifted_along(sent, "seq", hop) for hop in range(hops - 1, 0, -1)][::-1] + got
    grad_far, grad_corner, sent_state = tie(grad_far, grad_corner, sent_state)
    grad_all = [out_grad, grad_near, grad_far, grad_corner]
    hidden_grad, du_down = blocked_call(
        feed_before_kernel,
        "feed_before",
        count,
        [
            (grad_all, pieces(width)),
            (table, by_rows(8)),
            (column_sets, WHOLE),
            (w_down, WHOLE),
            (down_ffd.T, WHOLE),
            (up_res, part(low_rank, 1)),
        ],
        [((count, padded), single, "rows"), ((count, low_rank), bfloat, "rows")],
        [pltpu.VMEM((padded, width + low_rank), bfloat)],
        count * 6_000_000,
    )
    raw_local, hidden_grad = tie(raw_local, hidden_grad)

    sizes = dict(heads=heads, key_width=key_width, value_width=value_width)
    attention_part, mixed, u_out, entering = blocked_call(
        functools.partial(attend_kernel, hops=hops, **sizes),
        "attend",
        count,
        [
            (raw_local, by_rows(value_lanes)),
            (mapped, by_rows(qk)),
            (gate_input, by_rows(value_lanes)),
            (table, by_rows(8)),
            (gain, WHOLE),
            (column_sets, WHOLE),
            (w_out, WHOLE),
            (down_out, WHOLE),
            (up_res, part(low_rank, 0)),
        ]
        + [(sent_by, WHOLE) for sent_by in got],
        [
            ((count, width), bfloat, "parts"),
            ((count, value_lanes), bfloat, "rows"),
            ((count, low_rank), bfloat, "rows"),
            ((heads, key_width, value_width), bfloat, "whole"),
        ],
        [pltpu.VMEM((value_lanes + low_rank, width), bfloat)],
        count * 5_000_000,
    )
    attention_own, attention_far = near_sum(attention_part)
    attention_arrived, up_ff_t, up_ff_padded, down_ffd_padded, down_out_t = tie(
        flip(attention_far, 2),
        up_ff.transpose(0, 2, 1),
        widen(up_ff),
        widen(down_ffd),
        down_out.T,
    )
    residual = input_float + (attention_own + attention_arrived.astype(single))
    normed_mid = low(rms_scale(residual, norm2_gain))
    mid_near, mid_far = flip(normed_mid, 1), flip(normed_mid, 2)

    feed_inputs = [
        (hidden_grad, by_rows(padded)),
        (table, by_rows(8)),
        (column_sets, WHOLE),
        (down, part(2 * low_rank, 2)),
        (w_gate.T, WHOLE),
        (w_up.T, WHOLE),
        (up_ff_t, WHOLE),
        (up_ff_padded, WHOLE),
    ]
    feed_outputs = [
        ((count, width), bfloat, "parts"),
        ((count, padded), bfloat, "rows"),
        ((count, 2 * padded), bfloat, "rows"),
        ((count, 2 * low_rank), bfloat, "rows"),
        ((count, 2 * low_rank), bfloat, "rows"),
    ]
    feed_scratch = [
        pltpu.VMEM((padded, width + low_rank), bfloat),
        pltpu.VMEM((padded, width + low_rank), bfloat),
        pltpu.VMEM((2 * padded + 2 * low_rank, width), bfloat),
    ]
    near_part, *fed = blocked_call(
        feed_kernel,
        "feed_near",
        count,
        [([normed_mid, mid_near], pieces(width)), *feed_inputs],
        feed_outputs,
        feed_scratch,
        count * 8_000_000,
        half=0,
    )
    mid_far, near_own = tie(mid_far, near_part[0])
    near_part = [near_own, near_part[1]]
    mid_all = [normed_mid, mid_near, mid_far, flip(mid_far, 1)]
    far_part, hidden, ff_grad, u_ff, du_ff = blocked_call(
        feed_kernel,
        "feed_far",
        count,
        [(mid_all[2:], pieces(width)), *feed_inputs],
        feed_outputs,
        feed_scratch,
        count * 8_000_000,
        half=1,
        into=fed,
    )
    grad_own, grad_sum = halves_sum(near_part, far_part)
    grad_sum, hidden = tie(grad_sum, hidden)
    grad_arrived = flip(grad_sum, 2)
    out_part, feed_own, feed_far, feed_pair, feed_owned = blocked_call(
        feed_after_kernel,
        "feed_after",
        count,
        [
            (mid_all, pieces(width)),
            (grad_all, pieces(width)),
            (hidden, by_rows(padded)),
            (ff_grad, by_rows(2 * padded)),
            (u_ff, by_rows(2 * low_rank)),
            (du_ff, by_rows(2 * low_rank)),
            (du_down, by_rows(low_rank)),
            (table, by_rows(8)),
            (column_sets, WHOLE),
            (where, SCALAR),
            (w_down, WHOLE),
            (down_ffd_padded, WHOLE),
            (up_res, part(low_rank, 1)),
        ],
        [
            ((count, width), bfloat, "parts"),
            ((low_rank, 3 * block_width), bfloat, "whole"),
            ((low_rank, 3 * block_width), bfloat, "whole"),
            ((2 * low_rank, 3 * block_width), bfloat, "whole"),
            ((low_rank, 3 * padded), bfloat, "whole"),
        ],
        [
            pltpu.VMEM((padded + low_rank, width), bfloat),
            pltpu.VMEM((2 * low_rank, width), single),
            pltpu.VMEM((low_rank, width), single),
            pltpu.VMEM((low_rank, 3 * padded), single),
        ],
        count * 16_000_000,
    )
    grad_landed, feed_far = tie(grad_arrived, feed_far)
    mid_grad = grad_own + grad_landed.astype(single)
    residual_grad = out_grad.astype(single) + rms_back(residual, norm2_gain, mid_grad)
    branch_low = low(residual_grad)
    branch_near, branch_far = flip(branch_low, 1), flip(branch_low, 2)
    out_own, out_far = near_sum(out_part)
    owned_parts = exchange(seq_rows(tie(feed_owned, branch_near)[0]))
    feed_sum, feed_sum_far = near_sum((feed_own, feed_far, tie(feed_pair, grad_arrived)[0]))
    feed_landed = flip(feed_sum_far, 2)

    branch_inputs = [
        (raw_local, by_rows(value_lanes)),
        (mapped, by_rows(qk)),
        (gate_input, by_rows(value_lanes)),
        (table, by_rows(8)),
        (entering, WHOLE),
        (gain, WHOLE),
        (column_sets, WHOLE),
        (w_out, WHOLE),
        (down_out_t, WHOLE),
        (up_res, part(low_rank, 0)),
        (up_vg, part(low_rank, 1)),
    ]
    branch_outputs = [
        ((count, value_lanes), bfloat, "rows"),
        ((count, value_lanes), bfloat, "rows"),
        ((count, low_rank), bfloat, "rows"),
        ((count, low_rank), bfloat, "rows"),
    ]
    branch_scratch = [pltpu.VMEM((value_lanes, width + low_rank), bfloat)]
    state_shape = (heads, key_width, value_width)
    *branched, state_near = blocked_call(
        functools.partial(branch_kernel, hops=hops, last=False, **sizes),
        "branch_near",
        count,
        [([branch_low, branch_near], pieces(width)), *branch_inputs],
        branch_outputs + [(state_shape, single, "whole")],
        branch_scratch,
        count * 12_000_000,
        half=0,
    )
    branch_far, state_near = tie(branch_far, state_near)
    branch_corner, owned_parts, out_far = tie(flip(branch_far, 1), owned_parts, out_far)
    branch_all = [branch_low, branch_near, branch_far, branch_corner]
    raw_grad, gate_grad, du_out, du_outgate, *state_grads = blocked_call(
        functools.partial(branch_kernel, hops=hops, last=True, **sizes),
        "branch_far",
        count,
        [(branch_all[2:], pieces(width)), *branch_inputs, (state_near, WHOLE)]
        + [(sent_by, WHOLE) for sent_by in got[:-1]],
        branch_outputs + [(state_shape, bfloat, "whole")] * hops,
        branch_scratch,
        count * 4_000_000,
        half=1,
        into=branched,
    )
    state_got = [
        shifted_along(state_grads[hop - 1], "seq", -hop) for hop in range(hops, 0, -1)
    ][::-1]
    mixer_down_late, branch_res_grad, branch_flat = blocked_call(
        branch_after_kernel,
        "branch_after",
        count,
        [
            (branch_all, pieces(width)),
            (mixed, by_rows(value_lanes)),
            (u_out, by_rows(low_rank)),
            (normed_all, pieces(width)),
            (inner_gate, by_rows(low_rank)),
            (du_out, by_rows(low_rank)),
            (du_outgate, by_rows(low_rank)),
            (gate_grad, by_rows(value_lanes)),
        ],
        [
            ((low_rank, width), single, "whole"),
            ((low_rank, width), single, "whole"),
            ((low_rank, 2 * value_lanes), bfloat, "whole"),
        ],
        [pltpu.VMEM((low_rank, 2 * value_lanes), single)],
        count * 20_000_000,
        block=count,
    )
    feed_landed, du_out = tie(feed_landed, du_out)
    feed_shared = low(feed_sum + feed_landed.astype(single))
    owned_lanes = owned_parts.shape[-1]
    both = jnp.concatenate(
        [share_sum(owned_parts), seq_rows(feed_shared), seq_rows(branch_flat)], axis=2
    )
    raw_grad, both, out_far, *state_got = tie(raw_grad, both, out_far, *state_got)
    out_arrived = flip(out_far, 2)
    both = exchange(both)

    pre_grad, mix_grad, tail_grad, edge_grad = run_backward(
        where, pre, pre_halo, columns, conv, scalars, raw_grad, saved, entering, state_got,
        heads, key_width, value_width, quarter,
    )
    arrived = shifted_along(edge_grad, "seq", -1)
    arrived, both, out_arrived = tie(arrived, both, out_arrived)
    result = residual + (out_own + out_arrived.astype(single))
    later_parts = both[:, :, owned_lanes:]
    settled = [
        (pre_grad, by_rows(2 * qk + value_lanes)),
        (tail_grad, WHOLE),
        (arrived, WHOLE),
        (where, SCALAR),
    ]
    du_mix, last_own, last_far, last_pair, last_owned = blocked_call(
        functools.partial(settle_grads_kernel, quarter=quarter),
        "settle_grads",
        count,
        [
            settled[0],
            (normed_all, pieces(width)),
            (inner, by_rows(3 * low_rank)),
            (table, by_rows(8)),
            *settled[1:],
            (column_sets, WHOLE),
            (up_qk, WHOLE),
            (up_vg, part(low_rank, 0)),
            (mixer_down_late, WHOLE),
            (branch_res_grad, WHOLE),
        ],
        [
            ((count, 3 * low_rank), bfloat, "rows"),
            ((low_rank, 5 * block_width), bfloat, "whole"),
            ((low_rank, 5 * block_width), bfloat, "whole"),
            ((2 * low_rank, 5 * block_width), bfloat, "whole"),
            ((low_rank, 2 * qk + value_lanes), bfloat, "whole"),
        ],
        [
            pltpu.VMEM((count, 2 * qk + value_lanes), bfloat),
            pltpu.VMEM((3 * low_rank, width), single),
            pltpu.VMEM((low_rank, 2 * qk + value_lanes), single),
        ],
        count * 4_000_000,
        block=count,
    )
    last_own, last_far = near_sum((last_own, last_far, last_pair))
    last_far, gate_grad = tie(last_far, gate_grad)
    (normed_part,) = blocked_call(
        functools.partial(settle_kernel, quarter=quarter),
        "settle",
        count,
        [
            settled[0],
            (gate_grad, by_rows(value_lanes)),
            (du_mix, by_rows(3 * low_rank)),
            (du_outgate, by_rows(low_rank)),
            (mix_grad, by_rows(8)),
            *settled[1:],
            (down, part(4 * low_rank, 0)),
            (weight_mix, WHOLE),
            (w_query, WHOLE),
            (w_key, WHOLE),
            (w_value, WHOLE),
            (w_gate_out, WHOLE),
        ],
        [((count, width), bfloat, "parts")],
        [
            pltpu.VMEM((STEP, 2 * qk + value_lanes), bfloat),
            pltpu.VMEM((width, 2 * qk + 2 * value_lanes), bfloat),
            pltpu.VMEM((5 * low_rank, width), bfloat),
        ],
        count * 10_000_000,
    )
    last_flat = jnp.concatenate([low(far_sum(last_own, last_far)), last_owned], axis=1)
    feed_rows = all_rows(both)
    last_lanes = last_flat.shape[1]
    both = exchange(jnp.concatenate([seq_rows(last_flat), share_sum(later_parts)], axis=2))
    normed_own, normed_sum_far = near_sum(normed_part)
    both, normed_sum_far = tie(both, normed_sum_far)
    normed_landed = flip(normed_sum_far, 2)
    branch_rows = all_rows(both)
    feed_piece = branch_rows[:, last_lanes : last_lanes + 3 * block_width]
    feed_piece_far = flip(feed_piece, 2)
    last_parts = both[:, :, :last_lanes]
    normed_landed, feed_piece_far = tie(normed_landed, feed_piece_far)
    feed_pieces = [feed_piece, flip(feed_piece, 1), feed_piece_far, flip(feed_piece_far, 1)]
    normed_grad = normed_own + normed_landed.astype(single)
    input_grad = residual_grad + rms_back(input_float, norm1_gain, normed_grad)
    last_rows = all_rows(exchange(share_sum(last_parts)))
    piece = last_rows[:, : 5 * block_width]
    piece_far, input_grad, feed_pieces[3] = tie(flip(piece, 2), input_grad, feed_pieces[3])
    last_pieces = [piece, flip(piece, 1), piece_far, flip(piece_far, 1)]
    down_grad, qk_grad, vg_grad, ff_grads, out_grads, ffd_grads, res_grad = assemble(
        where,
        [*last_pieces, *feed_pieces],
        last_rows,
        feed_rows,
        branch_rows,
        padded,
        [
            (6, low_rank, width),
            (2, low_rank, qk),
            (2, low_rank, value_lanes),
            (2, low_rank, hidden_width),
            (low_rank, value_lanes),
            (low_rank, hidden_width),
            (2, low_rank, width),
        ],
    )

    def as_down(rows):
        return rows.reshape(rows.shape[:-2] + (sets, rank, -1)).swapaxes(-1, -2)

    def as_up(rows):
        return rows.reshape(rows.shape[0], sets, rank, -1)

    return (
        low(result),
        input_grad,
        as_down(down_grad),
        as_up(qk_grad),
        as_up(vg_grad),
        as_up(ff_grads),
        as_down(out_grads),
        as_down(ffd_grads),
        as_up(res_grad),
    )


def solution(mesh):
    rows = P(("seq", "head"), None)
    lanes = P(None, "head")
    last = P(None, None, None, "head")
    middle = P(None, "head", None)
    in_specs = (
        rows, rows, P(), P(), P(), lanes, lanes, lanes, lanes, lanes, lanes,
        P(None, None, "head"), P("head"), P("head"), lanes, P(), P("head", None), P(), lanes,
        lanes, P("head", None), P(), last, last, last, middle, middle, P(),
    )
    out_specs = (rows, rows, P(), last, last, last, middle, middle, P())
    return jax.shard_map(
        on_device, mesh=mesh, in_specs=in_specs, out_specs=out_specs, check_vma=False
    )
```

```python
import functools

import jax
import jax.numpy as jnp
from jax import lax
from jax.experimental import pallas as pl
from jax.experimental.pallas import tpu as pltpu
from jax.sharding import PartitionSpec as P

CHUNK = 128
STEP = 256
HALO = 16
LANES = 256
DOC_MAX = 4096
EPS = 1e-06
VMEM_LIMIT = 56 * 1024 * 1024
bfloat = jnp.bfloat16
single = jnp.float32


def contract(left, right, left_dim, right_dim):
    return lax.dot_general(
        left,
        right,
        (((left_dim,), (right_dim,)), ((), ())),
        preferred_element_type=single,
    )


def nn(left, right):
    return contract(left, right, 1, 0)


def nt(left, right):
    return contract(left, right, 1, 1)


def tn(left, right):
    return contract(left, right, 0, 0)


def low(array):
    return array.astype(bfloat)


def iotas():
    rows = lax.broadcasted_iota(jnp.int32, (CHUNK, CHUNK), 0)
    columns = lax.broadcasted_iota(jnp.int32, (CHUNK, CHUNK), 1)
    return rows, columns


def split_two(array):
    high = low(array)
    return high, low(array - high.astype(single))


def near_exact(left, right):
    left_high, left_low = split_two(left)
    right_high, right_low = split_two(right)
    return nn(
        jnp.concatenate([left_high, left_high, left_low], axis=1),
        jnp.concatenate([right_high, right_low, right_high], axis=0),
    )


def ones_product(ones, array):
    high = low(array)
    rest = array - high.astype(single)
    middle = low(rest)
    lowest = low(rest - middle.astype(single))
    return nn(
        jnp.concatenate([ones, ones, ones], axis=1),
        jnp.concatenate([high, middle, lowest], axis=0),
    )


def unit_lower_inverses(stricts, rows, columns):
    eye = (rows == columns).astype(single)
    differ = rows ^ columns
    block = 8
    inner = [jnp.where(differ < block, strict, 0.0) for strict in stricts]
    second = [near_exact(a, a) for a in inner]
    inverse = [near_exact(eye - a, eye + b) for a, b in zip(inner, second)]
    fourth = [near_exact(b, b) for b in second]
    inverse = [near_exact(a, eye + b) for a, b in zip(inverse, fourth)]
    while block < CHUNK:
        between = (differ >= block) & (differ < 2 * block)
        off = [jnp.where(between, strict, 0.0) for strict in stricts]
        part = [near_exact(a, b) for a, b in zip(off, inverse)]
        inverse = [a - near_exact(a, b) for a, b in zip(inverse, part)]
        block = 2 * block
    return inverse


def softplus(value):
    return jnp.maximum(value, 0.0) + jnp.log(1.0 + jnp.exp(-jnp.abs(value)))


def sigmoid(value):
    return 1.0 / (1.0 + jnp.exp(-value))


def gates(decay, start, rows, columns):
    lower_ones = low((rows >= columns).astype(single))
    total = ones_product(lower_ones, jnp.broadcast_to(decay, (CHUNK, CHUNK)))
    linked = (rows >= columns) & (columns >= start)
    within = jnp.where(linked, jnp.exp(jnp.where(linked, total - total.T, 0.0)), 0.0)
    running = total[:, :1]
    carried = jnp.where(start < 0, jnp.exp(running), 0.0)
    last = running[CHUNK - 1 : CHUNK]
    ending = jnp.where(
        rows[:, :1] >= start[CHUNK - 1 : CHUNK], jnp.exp(jnp.minimum(last - running, 0.0)), 0.0
    )
    return within, carried, ending


def lane_chunks(lanes, body):
    def run(index, _):
        body(pl.ds(pl.multiple_of(index * LANES, LANES), LANES))
        return 0

    lax.fori_loop(0, lanes // LANES, run, 0)


def convolved(window, starts, weight_ref, base, lanes):
    positions = base + lax.broadcasted_iota(jnp.int32, (STEP, 1), 0)
    taps = weight_ref.shape[0]
    total = None
    for tap in range(taps):
        back = taps - 1 - tap
        term = window[HALO - back : HALO - back + STEP, lanes] * weight_ref[tap : tap + 1, lanes]
        if back:
            term = jnp.where(positions - back >= starts, term, 0.0)
        total = term if total is None else total + term
    return total


def head_scales(rows, width):
    return lax.rsqrt(jnp.sum(rows * rows, axis=-1, keepdims=True) + EPS)


def forward_kernel(
    place,
    rows_ref,
    halo_ref,
    column_ref,
    weight_ref,
    scalar_ref,
    out_ref,
    map_ref,
    written_ref,
    state_ref,
    inverse_ref,
    end_ref,
    sent_ref,
    sent_state_ref,
    window,
    state,
    active,
    *,
    heads,
    key_width,
    value_width,
):
    step = pl.program_id(0)
    wide = value_width + key_width
    base = step * STEP
    rows, columns = iotas()

    @pl.when(step == 0)
    def _():
        window[0:HALO, :] = halo_ref[...].astype(single)
        for h in range(heads):
            state[h, :, :value_width] = jnp.zeros((key_width, value_width), single)
            state[h, :, value_width:] = (rows == columns).astype(single)

    @pl.when(step > 0)
    def _():
        window[0:HALO, :] = window[STEP : STEP + HALO, :]

    window[HALO:, :] = rows_ref[...].astype(single)
    info = column_ref[...]
    starts = info[:, 2 * heads : 2 * heads + 1].astype(jnp.int32)

    def activate(lanes):
        before = convolved(window, starts, weight_ref, base, lanes)
        active[:, lanes] = before * sigmoid(before)

    lane_chunks(window.shape[1], activate)
    qk_lanes = heads * key_width
    chunks = STEP // CHUNK
    local, stricts = [], []
    for c in range(chunks):
        span = slice(c * CHUNK, (c + 1) * CHUNK)
        for h in range(heads):
            query = active[span, h * key_width : (h + 1) * key_width]
            key = active[span, qk_lanes + h * key_width : qk_lanes + (h + 1) * key_width]
            value = active[
                span, 2 * qk_lanes + h * value_width : 2 * qk_lanes + (h + 1) * value_width
            ]
            query = query * (head_scales(query, key_width) * key_width ** (-0.5))
            key = key * head_scales(key, key_width)
            beta = sigmoid(info[span, h : h + 1])
            decay = -scalar_ref[0, h] * softplus(
                info[span, heads + h : heads + h + 1] + scalar_ref[1, h]
            )
            within, carried, ending = gates(
                decay, starts[span] - (base + c * CHUNK), rows, columns
            )
            query, key = low(query), low(key)
            strict = jnp.where(rows > columns, within * nt(key, key), 0.0) * beta
            mixed = low(within * nt(query, key))
            stricts.append(strict)
            local.append((query, key, value, beta, carried, ending, mixed))
    inverses = [low(a) for a in unit_lower_inverses(stricts, rows, columns)]
    each = range(heads)
    now = [state[h] for h in each]
    for c in range(chunks):
        span = slice(c * CHUNK, (c + 1) * CHUNK)
        here = [local[c * heads + h] for h in each]
        inverse = [inverses[c * heads + h] for h in each]
        now_low = [low(a) for a in now]
        read = [nn(here[h][1], now_low[h]) for h in each]
        asked = [nn(here[h][0], now_low[h]) for h in each]
        target = []
        for h in each:
            query, key, value, beta, carried, ending, mixed = here[h]
            gap = -(carried * beta) * read[h]
            target.append(
                jnp.concatenate(
                    [beta * value + gap[:, :value_width], gap[:, value_width:]], axis=1
                )
            )
        written = [nn(inverse[h], low(target[h])) for h in each]
        added = [tn(here[h][1], low(here[h][5] * written[h])) for h in each]
        inner = [nn(here[h][6], low(written[h])) for h in each]
        for h in each:
            carried = here[h][4]
            inverse_ref[span, h * CHUNK : (h + 1) * CHUNK] = inverse[h]
            state_ref[c, h] = now_low[h]
            written_ref[span, h * wide : (h + 1) * wide] = low(written[h])
            output = carried * asked[h] + inner[h]
            out_ref[span, h * value_width : (h + 1) * value_width] = output[:, :value_width]
            map_ref[span, h * key_width : (h + 1) * key_width] = low(output[:, value_width:])
        now = [here[h][4][CHUNK - 1 : CHUNK] * now[h] + added[h] for h in each]
    for h in each:
        state[h] = now[h]

    @pl.when(step == pl.num_programs(0) - 1)
    def _():
        final = state[...]
        end_ref[...] = final
        sent_ref[...] = low(final)
        sent_state_ref[...] = low(final[:, :, :value_width])


def backward_kernel(
    place,
    rows_ref,
    before_ref,
    halo_ref,
    column_ref,
    weight_ref,
    scalar_ref,
    grad_ref,
    written_ref,
    state_ref,
    inverse_ref,
    end_ref,
    entering_ref,
    *rest,
    hops,
    heads,
    key_width,
    value_width,
):
    got_refs, rest = rest[:hops], rest[hops:]
    out_ref, mix_ref, tail_ref, edge_ref, window, shifted, shifted_start, *rest = rest
    cotangent, ahead, active, slope = rest
    step = pl.program_id(0)
    steps = pl.num_programs(0)
    wide = value_width + key_width
    base = (steps - 1 - step) * STEP
    rows, columns = iotas()
    qk_lanes = heads * key_width
    lanes = window.shape[1]
    taps = weight_ref.shape[0]

    @pl.when(step == 0)
    def _():
        shifted[STEP : STEP + 8, :] = jnp.zeros((8, lanes), single)
        shifted_start[STEP : STEP + 8, :] = jnp.zeros((8, 1), jnp.int32)
        for h in range(heads):
            passed = got_refs[0][h].astype(single)
            for hop in range(1, hops):
                passed = passed + got_refs[hop][h].astype(single)
            cotangent[h] = passed
            ahead[h] = end_ref[h, :, :value_width] + nn(
                low(end_ref[h, :, value_width:]), low(entering_ref[h])
            )

    @pl.when(step > 0)
    def _():
        shifted[STEP : STEP + 8, :] = shifted[0:8, :]
        shifted_start[STEP : STEP + 8, :] = shifted_start[0:8, :]

    window[0:HALO, :] = jnp.where(
        step == steps - 1, halo_ref[...].astype(single), before_ref[...].astype(single)
    )
    window[HALO:, :] = rows_ref[...].astype(single)
    info = column_ref[...]
    starts = info[:, 2 * heads : 2 * heads + 1].astype(jnp.int32)
    positions = base + lax.broadcasted_iota(jnp.int32, (STEP, 1), 0)

    def activate(lanes):
        before = convolved(window, starts, weight_ref, base, lanes)
        gate = sigmoid(before)
        active[:, lanes] = before * gate
        slope[:, lanes] = gate * (1.0 + before * (1.0 - gate))

    lane_chunks(lanes, activate)
    upper_ones = low((rows <= columns).astype(single))
    last_row = rows[:, :1] == CHUNK - 1
    chunks = STEP // CHUNK
    each = range(heads)
    items = [(c, h) for c in range(chunks) for h in each]
    spans = {item: slice(item[0] * CHUNK, (item[0] + 1) * CHUNK) for item in items}
    entering = [low(entering_ref[h]) for h in each]
    root = key_width ** (-0.5)

    def per(function):
        return {item: function(*item) for item in items}

    def q_lanes(h):
        return slice(h * key_width, (h + 1) * key_width)

    def k_lanes(h):
        return slice(qk_lanes + h * key_width, qk_lanes + (h + 1) * key_width)

    def v_lanes(h):
        return slice(2 * qk_lanes + h * value_width, 2 * qk_lanes + (h + 1) * value_width)

    def kept(c, h, part):
        return written_ref[spans[c, h], h * wide : (h + 1) * wide][:, part]

    values, maps = slice(0, value_width), slice(value_width, wide)
    query_raw = per(lambda c, h: active[spans[c, h], q_lanes(h)])
    key_raw = per(lambda c, h: active[spans[c, h], k_lanes(h)])
    query_scale = per(lambda c, h: head_scales(query_raw[c, h], key_width))
    key_scale = per(lambda c, h: head_scales(key_raw[c, h], key_width))
    query = per(lambda c, h: query_raw[c, h] * (query_scale[c, h] * root))
    key = per(lambda c, h: key_raw[c, h] * key_scale[c, h])
    query_low = per(lambda c, h: low(query[c, h]))
    key_low = per(lambda c, h: low(key[c, h]))
    beta = per(lambda c, h: sigmoid(info[spans[c, h], h : h + 1]))
    raw = per(lambda c, h: info[spans[c, h], heads + h : heads + h + 1] + scalar_ref[1, h])
    gated = per(
        lambda c, h: gates(
            -scalar_ref[0, h] * softplus(raw[c, h]),
            starts[spans[c, h]] - (base + c * CHUNK),
            rows,
            columns,
        )
    )
    within = per(lambda c, h: gated[c, h][0])
    carried = per(lambda c, h: gated[c, h][1])
    ending = per(lambda c, h: gated[c, h][2])
    mixed = per(lambda c, h: low(within[c, h] * nt(query_low[c, h], key_low[c, h])))
    written = per(
        lambda c, h: kept(c, h, values).astype(single) + nn(kept(c, h, maps), entering[h])
    )
    start_state = per(
        lambda c, h: state_ref[c, h][:, values].astype(single)
        + nn(state_ref[c, h][:, maps], entering[h])
    )
    written_low = per(lambda c, h: low(written[c, h]))
    start_low = per(lambda c, h: low(start_state[c, h]))
    grad = per(lambda c, h: grad_ref[spans[c, h], h * value_width : (h + 1) * value_width])
    grad_low = grad
    carried_grad = per(lambda c, h: low(carried[c, h] * grad[c, h].astype(single)))
    from_output = per(lambda c, h: tn(mixed[c, h], grad_low[c, h]))
    state_part = per(lambda c, h: tn(query_low[c, h], carried_grad[c, h]))
    mixed_grad = per(lambda c, h: low(within[c, h] * nt(grad_low[c, h], written_low[c, h])))
    query_grad = per(
        lambda c, h: nt(carried_grad[c, h], start_low[c, h]) + nn(mixed_grad[c, h], key_low[c, h])
    )
    key_write = per(lambda c, h: tn(mixed_grad[c, h], query_low[c, h]))
    later, later_low, solved, value_grad, read_grad = {}, {}, {}, {}, {}
    now = [cotangent[h] for h in each]
    for c in reversed(range(chunks)):
        for h in each:
            later[c, h], later_low[c, h] = now[h], low(now[h])
        from_state = [nn(key_low[c, h], later_low[c, h]) for h in each]
        written_grad = [low(from_output[c, h] + ending[c, h] * from_state[h]) for h in each]
        for h in each:
            inverse = inverse_ref[spans[c, h], h * CHUNK : (h + 1) * CHUNK]
            solved[c, h] = tn(inverse, written_grad[h])
        for h in each:
            value_grad[c, h] = beta[c, h] * solved[c, h]
            read_grad[c, h] = low(-carried[c, h] * value_grad[c, h])
        now = [
            carried[c, h][CHUNK - 1 : CHUNK] * now[h]
            + state_part[c, h]
            + tn(key_low[c, h], read_grad[c, h])
            for h in each
        ]
    following = {
        (c, h): start_state[c + 1, h] if c + 1 < chunks else ahead[h] for c, h in items
    }
    at_end = per(lambda c, h: jnp.sum(later[c, h] * following[c, h], keepdims=True))
    for h in each:
        cotangent[h] = now[h]
        ahead[h] = start_state[0, h]
    strict_grad = per(
        lambda c, h: low(
            jnp.where(
                rows > columns, -within[c, h] * nt(low(value_grad[c, h]), written_low[c, h]), 0.0
            )
        )
    )
    key_read = per(
        lambda c, h: nt(read_grad[c, h], start_low[c, h]) + nn(strict_grad[c, h], key_low[c, h])
    )
    key_write = per(
        lambda c, h: key_write[c, h]
        + tn(strict_grad[c, h], key_low[c, h])
        + nt(low(ending[c, h] * written[c, h]), later_low[c, h])
    )
    query_dot = per(
        lambda c, h: jnp.sum(query[c, h] * query_grad[c, h], axis=-1, keepdims=True)
    )
    running_grad = per(
        lambda c, h: query_dot[c, h]
        + jnp.sum(key[c, h] * (key_read[c, h] - key_write[c, h]), axis=-1, keepdims=True)
        + jnp.where(last_row, at_end[c, h], 0.0)
    )
    decay_sum = per(
        lambda c, h: ones_product(
            upper_ones, jnp.broadcast_to(running_grad[c, h], (CHUNK, CHUNK))
        )[:, :1]
    )
    decay_grad = per(
        lambda c, h: jnp.where(
            positions[spans[c, h]] == starts[spans[c, h]],
            0.0,
            -scalar_ref[0, h] * sigmoid(raw[c, h]) * decay_sum[c, h],
        )
    )
    beta_grad = per(
        lambda c, h: jnp.sum(solved[c, h] * written[c, h], axis=-1, keepdims=True)
        * sigmoid(-info[spans[c, h], h : h + 1])
    )
    for c, h in items:
        span = spans[c, h]
        key_grad = key_read[c, h] + key_write[c, h]
        key_dot = jnp.sum(key[c, h] * key_grad, axis=-1, keepdims=True)
        query_active = (query_scale[c, h] * root) * query_grad[c, h] - query_raw[c, h] * (
            query_scale[c, h] * query_scale[c, h] * query_dot[c, h]
        )
        key_active = key_scale[c, h] * (key_grad - key[c, h] * key_dot)
        shifted[span, q_lanes(h)] = query_active * slope[span, q_lanes(h)]
        shifted[span, k_lanes(h)] = key_active * slope[span, k_lanes(h)]
        shifted[span, v_lanes(h)] = value_grad[c, h] * slope[span, v_lanes(h)]
    for c in range(chunks):
        mix_ref[c * CHUNK : (c + 1) * CHUNK, :] = jnp.concatenate(
            [beta_grad[c, h] for h in each]
            + [decay_grad[c, h] for h in each]
            + [jnp.zeros((CHUNK, mix_ref.shape[1] - 2 * heads), single)],
            axis=1,
        )
    shifted_start[0:STEP, :] = starts

    def collect(lanes):
        total = None
        for tap in range(taps):
            back = taps - 1 - tap
            term = shifted[back : back + STEP, lanes] * weight_ref[tap : tap + 1, lanes]
            if back:
                term = jnp.where(positions >= shifted_start[back : back + STEP, :], term, 0.0)
            total = term if total is None else total + term
        out_ref[:, lanes] = low(total)

        @pl.when(step == 0)
        def _():
            tail_ref[:, lanes] = total[STEP - HALO :, :]

    lane_chunks(lanes, collect)

    @pl.when(step == steps - 1)
    def _():
        window[0:8, :] = jnp.zeros((8, lanes), single)
        window[8:16, :] = shifted[0:8, :]
        early = lax.broadcasted_iota(jnp.int32, (8, 1), 0) - 8
        collected = jnp.zeros((8, lanes), single)
        for tap in range(taps - 1):
            back = taps - 1 - tap
            reader = early + back
            reader_start = jnp.zeros((8, 1), jnp.int32)
            for t in range(back):
                reader_start = jnp.where(reader == t, shifted_start[t : t + 1, :], reader_start)
            term = window[back : back + 8, :] * weight_ref[tap : tap + 1, :]
            collected = collected + jnp.where(
                (reader >= 0) & (early >= reader_start), term, 0.0
            )
        edge_ref[0:8, :] = jnp.zeros((8, lanes), single)
        edge_ref[8:16, :] = collected


def block_place(step, place, per_quarter):
    return ((step // per_quarter) ^ place[0]) * per_quarter + step % per_quarter


def run_forward(place, rows, halo, columns, weights, scalars, heads, key_width, value_width, quarter):
    count, lanes = columns.shape[0], rows.shape[1]
    steps, per_quarter = count // STEP, quarter // STEP
    wide = value_width + key_width
    chunks = STEP // CHUNK
    at = lambda i, place: (block_place(i, place, per_quarter), 0)
    fixed = lambda i, place: (0, 0)
    body = functools.partial(
        forward_kernel, heads=heads, key_width=key_width, value_width=value_width
    )
    shapes = (
        jax.ShapeDtypeStruct((count, heads * value_width), single),
        jax.ShapeDtypeStruct((count, heads * key_width), bfloat),
        jax.ShapeDtypeStruct((count, heads * wide), bfloat),
        jax.ShapeDtypeStruct((count // CHUNK, heads, key_width, wide), bfloat),
        jax.ShapeDtypeStruct((count, heads * CHUNK), bfloat),
        jax.ShapeDtypeStruct((heads, key_width, wide), single),
        jax.ShapeDtypeStruct((heads, key_width, wide), bfloat),
        jax.ShapeDtypeStruct((heads, key_width, value_width), bfloat),
    )
    return pl.pallas_call(
        body,
        out_shape=shapes,
        grid_spec=pltpu.PrefetchScalarGridSpec(
            num_scalar_prefetch=1,
            grid=(steps,),
            in_specs=[
                pl.BlockSpec((STEP, lanes), at),
                pl.BlockSpec((HALO, lanes), lambda i, place: (0, 0)),
                pl.BlockSpec((STEP, columns.shape[1]), at),
                pl.BlockSpec(weights.shape, fixed),
                pl.BlockSpec(memory_space=pltpu.SMEM),
            ],
            out_specs=[
                pl.BlockSpec((STEP, heads * value_width), at),
                pl.BlockSpec((STEP, heads * key_width), at),
                pl.BlockSpec((STEP, heads * wide), at),
                pl.BlockSpec((chunks, heads, key_width, wide), lambda i, place: (i, 0, 0, 0)),
                pl.BlockSpec((STEP, heads * CHUNK), at),
                pl.BlockSpec((heads, key_width, wide), lambda i, place: (0, 0, 0)),
                pl.BlockSpec((heads, key_width, wide), lambda i, place: (0, 0, 0)),
                pl.BlockSpec((heads, key_width, value_width), lambda i, place: (0, 0, 0)),
            ],
            scratch_shapes=[
                pltpu.VMEM((STEP + HALO, lanes), single),
                pltpu.VMEM((heads, key_width, wide), single),
                pltpu.VMEM((STEP, lanes), single),
            ],
        ),
        compiler_params=pltpu.CompilerParams(
            dimension_semantics=("arbitrary",), vmem_limit_bytes=VMEM_LIMIT
        ),
        cost_estimate=pl.CostEstimate(
            flops=count * 2_000_000, bytes_accessed=count * 10_000, transcendentals=count * 2000
        ),
        name="delta_forward",
    )(place, rows, halo, columns, weights, scalars)


def run_backward(
    place, rows, halo, columns, weights, scalars, grad, saved, entering, got, heads,
    key_width, value_width, quarter,
):
    written, states, inverses, end = saved
    count, lanes = columns.shape[0], rows.shape[1]
    steps, per_quarter = count // STEP, quarter // STEP
    wide = value_width + key_width
    chunks = STEP // CHUNK

    def at(i, place):
        return (block_place(steps - 1 - i, place, per_quarter), 0)

    def halo_at(i, place):
        here = steps - 1 - i
        inner = block_place(jnp.maximum(here - 1, 0), place, per_quarter)
        ratio = STEP // HALO
        return (inner * ratio + ratio - 1, 0)

    fixed = lambda i, place: (0, 0)
    whole = lambda i, place: (0, 0, 0)
    body = functools.partial(
        backward_kernel,
        hops=len(got),
        heads=heads,
        key_width=key_width,
        value_width=value_width,
    )
    shapes = (
        jax.ShapeDtypeStruct((count, lanes), bfloat),
        jax.ShapeDtypeStruct((count, columns.shape[1]), single),
        jax.ShapeDtypeStruct((HALO, lanes), single),
        jax.ShapeDtypeStruct((HALO, lanes), single),
    )
    return pl.pallas_call(
        body,
        out_shape=shapes,
        grid_spec=pltpu.PrefetchScalarGridSpec(
            num_scalar_prefetch=1,
            grid=(steps,),
            in_specs=[
                pl.BlockSpec((STEP, lanes), at),
                pl.BlockSpec((HALO, lanes), halo_at),
                pl.BlockSpec((HALO, lanes), fixed),
                pl.BlockSpec((STEP, columns.shape[1]), at),
                pl.BlockSpec(weights.shape, fixed),
                pl.BlockSpec(memory_space=pltpu.SMEM),
                pl.BlockSpec((STEP, heads * value_width), at),
                pl.BlockSpec((STEP, heads * wide), at),
                pl.BlockSpec(
                    (chunks, heads, key_width, wide), lambda i, place: (steps - 1 - i, 0, 0, 0)
                ),
                pl.BlockSpec((STEP, heads * CHUNK), at),
                pl.BlockSpec(end.shape, whole),
                pl.BlockSpec(entering.shape, whole),
            ]
            + [pl.BlockSpec(part.shape, whole) for part in got],
            out_specs=[
                pl.BlockSpec((STEP, lanes), at),
                pl.BlockSpec((STEP, columns.shape[1]), at),
                pl.BlockSpec((HALO, lanes), fixed),
                pl.BlockSpec((HALO, lanes), fixed),
            ],
            scratch_shapes=[
                pltpu.VMEM((STEP + HALO, lanes), single),
                pltpu.VMEM((STEP + 8, lanes), single),
                pltpu.VMEM((STEP + 8, 1), jnp.int32),
                pltpu.VMEM((heads, key_width, value_width), single),
                pltpu.VMEM((heads, key_width, value_width), single),
                pltpu.VMEM((STEP, lanes), single),
                pltpu.VMEM((STEP, lanes), single),
            ],
        ),
        compiler_params=pltpu.CompilerParams(
            dimension_semantics=("arbitrary",), vmem_limit_bytes=VMEM_LIMIT
        ),
        cost_estimate=pl.CostEstimate(
            flops=count * 3_000_000, bytes_accessed=count * 12_000, transcendentals=count * 3000
        ),
        name="delta_backward",
    )(
        place, rows, rows, halo, columns, weights, scalars, grad, written, states, inverses, end,
        entering, *got,
    )


def chosen_columns(table, column_sets):
    return column_sets[0:1, :] == table[:, 1:2]


def masked(product, chosen):
    return low(jnp.where(chosen, product, 0.0))


def silu_parts(value):
    logistic = sigmoid(value)
    return logistic, value * logistic


def accumulate(ref, value, first):
    if first is True:
        ref[...] = value
    else:
        ref[...] = jnp.where(first, value, ref[...] + value)


def emit_blocks(parts, place, own_ref, far_ref, pair_ref):
    for k, part in enumerate(parts):
        rows, size = part.shape[0], part.shape[1] // 4
        lanes = slice(k * size, (k + 1) * size)
        for relative, target, row in (
            (0, own_ref, 0), (2, far_ref, 0), (1, pair_ref, 0), (3, pair_ref, rows)
        ):
            start = pl.multiple_of((place ^ relative) * size, 128)
            target[row : row + rows, lanes] = low(part[:, pl.ds(start, size)])


def copy_rows(target, row, source, lanes=slice(None)):
    size = 64

    def run(index, _):
        start = pl.multiple_of(index * size, size)
        target[pl.ds(pl.multiple_of(row + start, size), size), lanes] = source[pl.ds(start, size), :]
        return 0

    lax.fori_loop(0, source.shape[0] // size, run, 0)


def at_end(fill):
    pl.when(pl.program_id(0) == pl.num_programs(0) - 1)(fill)


def at_start(fill):
    pl.when(pl.program_id(0) == 0)(fill)


def project_kernel(
    rows_ref, table_ref, sets_ref, down_ref, mix_ref, wq_ref, wk_ref, wv_ref, wg_ref, up_qk_ref,
    up_vg_ref, *rest, with_halo,
):
    low_rank = sets_ref.shape[1]
    width, q_width = wq_ref.shape
    v_width = wv_ref.shape[1]
    bounds = [0, q_width, 2 * q_width, 2 * q_width + v_width, 2 * q_width + 2 * v_width]
    if with_halo:
        halo_ref, halo_table_ref, *rest = rest
        pre_ref, inner_ref, column_ref, gate_ref, inner_gate_ref, pre_halo_ref, joined = rest
    else:
        pre_ref, inner_ref, column_ref, gate_ref, inner_gate_ref, joined = rest
    weights = (wq_ref, wk_ref, wv_ref, wg_ref)
    ups = (
        up_qk_ref.at[0],
        up_qk_ref.at[1],
        up_vg_ref.at[:low_rank],
        up_vg_ref.at[low_rank:],
    )

    @at_start
    def _():
        for p in range(4):
            columns = slice(bounds[p], bounds[p + 1])
            copy_rows(joined, 0, weights[p], columns)
            copy_rows(joined, width, ups[p], columns)

    def projections(rows, table, store, maps):
        chosen = chosen_columns(table, sets_ref[...])
        product = nt(rows, down_ref[: maps * low_rank, :])
        inner = [
            masked(product[:, p * low_rank : (p + 1) * low_rank], chosen) for p in range(maps)
        ]
        for p in range(maps):
            output = nn(
                jnp.concatenate([rows, inner[p]], axis=1), joined[:, bounds[p] : bounds[p + 1]]
            )
            if p < 3:
                store[:, bounds[p] : bounds[p + 1]] = low(output)
            else:
                gate_ref[...] = output
        return inner

    if with_halo:

        @at_start
        def _():
            projections(halo_ref[...], halo_table_ref[...], pre_halo_ref, 3)

    table = table_ref[...]
    rows = rows_ref[...]
    inner = projections(rows, table, pre_ref, 4)
    inner_gate_ref[...] = inner[3]
    for p in range(3):
        inner_ref[:, p * low_rank : (p + 1) * low_rank] = inner[p]
    column_ref[...] = jnp.concatenate([nt(rows, mix_ref[...])[:, :4], table[:, :4]], axis=1)


def head_outputs(raw_ref, map_ref, entering_ref, heads, key_width, value_width):
    outputs = []
    for h in range(heads):
        outputs.append(
            raw_ref[:, h * value_width : (h + 1) * value_width]
            + nn(map_ref[:, h * key_width : (h + 1) * key_width], entering_ref[h])
        )
    return outputs


def attend_kernel(
    raw_ref, map_ref, gate_ref, table_ref, gain_ref, sets_ref, wo_ref, down_ref, up_ref, *rest,
    heads, key_width, value_width, hops,
):
    got_refs, rest = rest[:hops], rest[hops:]
    part_ref, z_ref, inner_ref, entering_ref, joined = rest
    value_lanes = wo_ref.shape[0]

    @at_start
    def _():
        copy_rows(joined, 0, wo_ref)
        copy_rows(joined, value_lanes, up_ref)
        for h in range(heads):
            state = got_refs[hops - 1][h].astype(single)
            for hop in range(hops - 1, 0, -1):
                got = got_refs[hop - 1][h]
                state = got[:, :value_width].astype(single) + nn(got[:, value_width:], low(state))
            entering_ref[h] = low(state)

    chosen = chosen_columns(table_ref[...], sets_ref[...])
    outputs = head_outputs(raw_ref, map_ref, entering_ref, heads, key_width, value_width)
    parts = []
    for h, output in enumerate(outputs):
        lanes = slice(h * value_width, (h + 1) * value_width)
        scale = lax.rsqrt(jnp.mean(output * output, axis=-1, keepdims=True) + EPS)
        _, gate = silu_parts(gate_ref[:, lanes])
        parts.append(low(output * scale * gain_ref[0:1, :] * gate))
    z = jnp.concatenate(parts, axis=1)
    z_ref[...] = z
    inner = masked(nt(z, down_ref[...]), chosen)
    inner_ref[...] = inner
    part_ref[...] = low(nn(jnp.concatenate([z, inner], axis=1), joined[...]))


def feed_before_kernel(
    grad_ref, table_ref, sets_ref, wd_ref, down_ffd_t_ref, up_ref, hidden_grad_ref, du_ref, joined
):
    hidden, width = wd_ref.shape

    @at_start
    def _():
        copy_rows(joined, 0, wd_ref, slice(0, width))
        copy_rows(joined, 0, down_ffd_t_ref, slice(width, None))
        joined[hidden:, :] = jnp.zeros((joined.shape[0] - hidden, joined.shape[1]), bfloat)

    grad = grad_ref[...]
    du_down = masked(nt(grad, up_ref[...]), chosen_columns(table_ref[...], sets_ref[...]))
    du_ref[...] = du_down
    hidden_grad_ref[...] = nt(jnp.concatenate([grad, du_down], axis=1), joined[...])


def feed_kernel(
    rows_ref, hidden_grad_ref, table_ref, sets_ref, down_ref, wg_ref, wu_ref, up_t_ref, up_ref,
    back_ref, hidden_ref, ff_grad_ref, inner_ref, du_ref,
    joined_gate, joined_up, joined_back,
):
    low_rank = sets_ref.shape[1]
    hidden, width = wg_ref.shape
    padded = joined_gate.shape[0]

    @at_start
    def _():
        for p, (joined, weight) in enumerate(((joined_gate, wg_ref), (joined_up, wu_ref))):
            copy_rows(joined, 0, weight, slice(0, width))
            copy_rows(joined, 0, up_t_ref.at[p], slice(width, None))
            joined[hidden:, :] = jnp.zeros((padded - hidden, joined.shape[1]), bfloat)
            copy_rows(joined_back, p * padded, weight)
            joined_back[p * padded + hidden : (p + 1) * padded, :] = jnp.zeros(
                (padded - hidden, width), bfloat
            )
        copy_rows(joined_back, 2 * padded, down_ref)

    chosen = chosen_columns(table_ref[...], sets_ref[...])
    both = jnp.concatenate([chosen, chosen], axis=1)
    rows = rows_ref[...]
    inner = masked(nt(rows, down_ref[...]), both)
    inner_ref[...] = inner
    gate = nt(jnp.concatenate([rows, inner[:, :low_rank]], axis=1), joined_gate[...])
    up = nt(jnp.concatenate([rows, inner[:, low_rank:]], axis=1), joined_up[...])
    logistic, active = silu_parts(gate)
    hidden_ref[...] = low(active * up)
    hidden_grad = hidden_grad_ref[...]
    gate_grad = low(hidden_grad * up * logistic * (1.0 + gate * (1.0 - logistic)))
    up_grad = low(hidden_grad * active)
    du_gate = masked(nt(gate_grad, up_ref[0]), chosen)
    du_up = masked(nt(up_grad, up_ref[1]), chosen)
    du_ref[:, :low_rank] = du_gate
    du_ref[:, low_rank:] = du_up
    ff_grad_ref[:, :padded] = gate_grad
    ff_grad_ref[:, padded:] = up_grad
    back_ref[...] = low(
        nn(jnp.concatenate([gate_grad, up_grad, du_gate, du_up], axis=1), joined_back[...])
    )


def feed_after_kernel(
    rows_ref, grad_ref, hidden_ref, ff_grad_ref, inner_ref, du_ref, du_down_ref, table_ref,
    sets_ref, place_ref, wd_ref, down_ffd_ref, up_ref,
    out_ref, own_ref, far_ref, pair_ref, flat_ref,
    joined, down_sum, res_sum, flat_sum,
):
    first = pl.program_id(0) == 0
    low_rank = sets_ref.shape[1]
    width_hidden = wd_ref.shape[0]
    padded = down_ffd_ref.shape[1]

    @at_start
    def _():
        copy_rows(joined, 0, wd_ref)
        joined[width_hidden:padded, :] = jnp.zeros(
            (padded - width_hidden, joined.shape[1]), bfloat
        )
        copy_rows(joined, padded, up_ref)

    hidden = hidden_ref[...]
    inner = inner_ref[...]
    u_down = masked(
        nt(hidden, down_ffd_ref[...]), chosen_columns(table_ref[...], sets_ref[...])
    )
    out_ref[...] = low(nn(jnp.concatenate([hidden, u_down], axis=1), joined[...]))
    accumulate(down_sum, tn(du_ref[...], rows_ref[...]), first)
    accumulate(res_sum, tn(u_down, grad_ref[...]), first)
    for k, grown in enumerate(
        (
            tn(inner[:, :low_rank], ff_grad_ref[:, :padded]),
            tn(inner[:, low_rank:], ff_grad_ref[:, padded:]),
            tn(du_down_ref[...], hidden),
        )
    ):
        accumulate(flat_sum.at[:, k * padded : (k + 1) * padded], grown, first)

    @at_end
    def _():
        flat_ref[...] = low(flat_sum[...])
        emit_blocks(
            (down_sum.at[:low_rank], down_sum.at[low_rank:], res_sum),
            place_ref[0], own_ref, far_ref, pair_ref,
        )


def branch_kernel(
    branch_ref, raw_ref, map_ref, gate_ref, table_ref, entering_ref, gain_ref, sets_ref, wo_ref,
    down_out_t_ref, up_ref, up_gate_ref, *rest,
    heads, key_width, value_width, hops, last,
):
    if last:
        before_ref, *rest = rest
        got_refs, rest = rest[: hops - 1], rest[hops - 1 :]
        raw_grad_ref, gate_grad_ref, du_out_ref, du_gate_ref, *rest = rest
        sent_refs, (joined, total_ref) = rest[:hops], rest[hops:]
    else:
        raw_grad_ref, gate_grad_ref, du_out_ref, du_gate_ref, total_ref, joined = rest
    width = wo_ref.shape[1]

    @at_start
    def _():
        copy_rows(joined, 0, wo_ref, slice(0, width))
        copy_rows(joined, 0, down_out_t_ref, slice(width, None))

    chosen = chosen_columns(table_ref[...], sets_ref[...])
    branch = branch_ref[...]
    outputs = head_outputs(raw_ref, map_ref, entering_ref, heads, key_width, value_width)
    du_out = masked(nt(branch, up_ref[...]), chosen)
    du_out_ref[...] = du_out
    mixed_grad = nt(jnp.concatenate([branch, du_out], axis=1), joined[...])
    gain = gain_ref[0:1, :]
    gate_grads = []
    for h, output in enumerate(outputs):
        lanes = slice(h * value_width, (h + 1) * value_width)
        scale = lax.rsqrt(jnp.mean(output * output, axis=-1, keepdims=True) + EPS)
        value = gate_ref[:, lanes]
        logistic, active = silu_parts(value)
        incoming = mixed_grad[:, lanes]
        gate_grads.append(
            low(
                incoming
                * (output * scale * gain)
                * (logistic * (1.0 + value * (1.0 - logistic)))
            )
        )
        scaled = gain * (incoming * active)
        dot = jnp.mean(output * scaled, axis=-1, keepdims=True)
        raw_grad = low(scale * scaled - output * (scale * scale * scale * dot))
        raw_grad_ref[:, lanes] = raw_grad
        grown = tn(map_ref[:, h * key_width : (h + 1) * key_width], raw_grad)
        accumulate(total_ref.at[h], grown, pl.program_id(0) == 0)
    gate_grad = jnp.concatenate(gate_grads, axis=1)
    gate_grad_ref[...] = gate_grad
    du_gate_ref[...] = masked(nt(gate_grad, up_gate_ref[...]), chosen)
    if last:

        @at_end
        def _():
            for h in range(heads):
                passed = low(before_ref[h] + total_ref[h])
                sent_refs[0][h] = passed
                for hop in range(1, hops):
                    passed = low(tn(got_refs[hop - 1][h][:, value_width:], passed))
                    sent_refs[hop][h] = passed


def branch_after_kernel(
    branch_ref, z_ref, u_out_ref, rows_ref, inner_ref, du_out_ref, du_gate_ref, gate_grad_ref,
    down_grad_ref, res_grad_ref, flat_ref,
    flat_sum,
):
    first = pl.program_id(0) == 0
    lanes = z_ref.shape[1]
    accumulate(down_grad_ref, tn(du_gate_ref[...], rows_ref[...]), first)
    accumulate(res_grad_ref, tn(u_out_ref[...], branch_ref[...]), first)
    accumulate(flat_sum.at[:, :lanes], tn(du_out_ref[...], z_ref[...]), first)
    accumulate(flat_sum.at[:, lanes:], tn(inner_ref[...], gate_grad_ref[...]), first)

    @at_end
    def _():
        flat_ref[...] = low(flat_sum[...])


def settled_rows(pre_ref, tail_ref, arrived_ref, place_ref, quarter, window):
    block = window.shape[0]
    start = ((3 ^ place_ref[0]) + 1) * quarter - HALO - pl.program_id(0) * block
    window[...] = pre_ref[...]

    @pl.when((start >= 0) & (start < block))
    def _():
        window[pl.ds(pl.multiple_of(start, HALO), HALO), :] = low(tail_ref[...] + arrived_ref[...])

    return window[...]


def settle_grads_kernel(
    pre_ref, rows_ref, inner_ref, table_ref, tail_ref, arrived_ref, place_ref, sets_ref,
    up_qk_ref, up_value_ref, down_late_ref, res_late_ref,
    du_ref, own_ref, far_ref, pair_ref, flat_ref,
    window, down_sum, flat_sum,
    *, quarter,
):
    first = pl.program_id(0) == 0
    low_rank = sets_ref.shape[1]
    q_width = up_qk_ref.shape[2]
    chosen = chosen_columns(table_ref[...], sets_ref[...])
    pre = settled_rows(pre_ref, tail_ref, arrived_ref, place_ref, quarter, window)
    query, key, value = pre[:, :q_width], pre[:, q_width : 2 * q_width], pre[:, 2 * q_width :]
    inner = inner_ref[...]
    du = jnp.concatenate(
        [
            masked(nt(query, up_qk_ref[0]), chosen),
            masked(nt(key, up_qk_ref[1]), chosen),
            masked(nt(value, up_value_ref[...]), chosen),
        ],
        axis=1,
    )
    du_ref[...] = du
    accumulate(down_sum, tn(du, rows_ref[...]), first)
    at = 0
    for p, part in enumerate((query, key, value)):
        accumulate(
            flat_sum.at[:, at : at + part.shape[1]],
            tn(inner[:, p * low_rank : (p + 1) * low_rank], part),
            first,
        )
        at += part.shape[1]

    @at_end
    def _():
        flat_ref[...] = low(flat_sum[...])
        emit_blocks(
            [down_sum.at[p * low_rank : (p + 1) * low_rank] for p in range(3)]
            + [down_late_ref, res_late_ref],
            place_ref[0], own_ref, far_ref, pair_ref,
        )


def settle_kernel(
    pre_ref, gate_grad_ref, du_ref, du_gate_ref, mix_ref, tail_ref, arrived_ref, place_ref,
    down_ref, mix_weight_ref, wq_ref, wk_ref, wv_ref, wg_ref,
    part_ref,
    window, joined, joined_small,
    *, quarter,
):
    q_width, v_width = wq_ref.shape[1], wv_ref.shape[1]

    @at_start
    def _():
        at = 0
        for weight in (wq_ref, wk_ref, wv_ref, wg_ref):
            copy_rows(joined, 0, weight, slice(at, at + weight.shape[1]))
            at += weight.shape[1]
        maps, mixes = down_ref.shape[0], mix_weight_ref.shape[0]
        spare = joined_small.shape[0] - maps - mixes
        copy_rows(joined_small, 0, down_ref)
        joined_small[maps:, :] = jnp.concatenate(
            [mix_weight_ref[...], jnp.zeros((spare, joined_small.shape[1]), bfloat)], axis=0
        )

    pre = settled_rows(pre_ref, tail_ref, arrived_ref, place_ref, quarter, window)
    mix = low(mix_ref[...])
    spare = joined_small.shape[0] - down_ref.shape[0] - mix.shape[1]
    small = jnp.concatenate(
        [du_ref[...], du_gate_ref[...], mix, jnp.zeros((mix.shape[0], spare), bfloat)], axis=1
    )
    part_ref[...] = low(
        nt(jnp.concatenate([pre, gate_grad_ref[...]], axis=1), joined[...])
        + nn(small, joined_small[...])
    )


def assemble_kernel(
    place_ref, *refs, padded,
):
    pieces_last, pieces_feed = refs[:4], refs[4:8]
    last_ref, feed_ref, branch_ref = refs[8:11]
    down_ref, qk_ref, vg_ref, ff_ref, out_ref, ffd_ref, res_ref = refs[11:]
    place = place_ref[0]
    size = pieces_last[0].shape[1] // 5
    first = [down_ref.at[p] for p in range(4)] + [res_ref.at[0]]
    second = [down_ref.at[4], down_ref.at[5], res_ref.at[1]]
    for relative in range(4):
        start = pl.multiple_of((place ^ relative) * size, 128)
        for targets, piece in ((first, pieces_last[relative]), (second, pieces_feed[relative])):
            for k, target in enumerate(targets):
                target[:, pl.ds(start, size)] = piece[:, k * size : (k + 1) * size].astype(single)
    qk, values, hidden = qk_ref.shape[2], vg_ref.shape[2], ff_ref.shape[2]

    def lanes(ref, start, width):
        return ref[:, start : start + width].astype(single)

    own = 5 * size
    qk_ref[0], qk_ref[1] = lanes(last_ref, own, qk), lanes(last_ref, own + qk, qk)
    vg_ref[0] = lanes(last_ref, own + 2 * qk, values)
    at = last_ref.shape[1] + 3 * size
    out_ref[...] = lanes(branch_ref, at, values)
    vg_ref[1] = lanes(branch_ref, at + values, values)
    ff_ref[0] = lanes(feed_ref, 0, hidden)
    ff_ref[1] = lanes(feed_ref, padded, hidden)
    ffd_ref[...] = lanes(feed_ref, 2 * padded, hidden)


def assemble(where, shared, last, feed, branch, padded, shapes):
    rows = last.shape[0]
    block = min(32, rows)

    def spec(shape):
        if len(shape) == 2:
            return pl.BlockSpec((block, shape[1]), lambda i: (i, 0))
        return pl.BlockSpec((shape[0], block, shape[2]), lambda i: (0, i, 0))

    arrays = [*shared, last, feed, branch]
    return pl.pallas_call(
        functools.partial(assemble_kernel, padded=padded),
        out_shape=tuple(jax.ShapeDtypeStruct(shape, single) for shape in shapes),
        grid=(rows // block,),
        in_specs=[pl.BlockSpec(memory_space=pltpu.SMEM)] + [spec(a.shape) for a in arrays],
        out_specs=[spec(shape) for shape in shapes],
        compiler_params=pltpu.CompilerParams(
            dimension_semantics=("arbitrary",), vmem_limit_bytes=VMEM_LIMIT
        ),
        name="assemble",
    )(where, *arrays)


WHOLE, SCALAR = "whole", "scalar"


def by_rows(width, lane_block=0):
    return ("rows", width, lane_block)


def part(rows, index):
    return ("part", rows, index)


def pieces(width):
    return ("pieces", width)


def blocked_call(
    body, name, count, inputs, outputs, scratch, flops, block=STEP, half=None, into=()
):
    count_pieces = 4 if half is None else 2
    steps = count * count_pieces // 4 // block
    offset = (half or 0) * steps
    per = max(steps // count_pieces, 1)
    in_specs, arrays, moved, groups_in, extra = [], [], 0, [], []
    for array, kind in inputs:
        members = array if isinstance(array, (list, tuple)) else [array]
        groups_in.append(len(members))
        arrays += members
        moved += sum(a.size * a.dtype.itemsize for a in members)
        if kind == WHOLE:
            zeros = (0,) * array.ndim
            in_specs.append(
                pl.BlockSpec(
                    array.shape, lambda i, zeros=zeros: zeros, pipeline_mode=pl.Buffered(1)
                )
            )
        elif kind == SCALAR:
            in_specs.append(pl.BlockSpec(memory_space=pltpu.SMEM))
        elif kind[0] == "part":
            in_specs.append(
                pl.BlockSpec(
                    (kind[1], array.shape[1]),
                    lambda i, at=kind[2]: (at, 0),
                    pipeline_mode=pl.Buffered(1),
                )
            )
        elif kind[0] == "rows":
            in_specs.append(
                pl.BlockSpec((block, kind[1]), lambda i, lane=kind[2]: (i + offset, lane))
            )
        else:
            for b, member in enumerate(members):
                if steps == 1:
                    in_specs.append(pl.BlockSpec(member.shape, lambda i: (0, 0)))
                else:
                    in_specs.append(
                        pl.BlockSpec(
                            (block, kind[1]),
                            lambda i, b=b: (jnp.clip(i - b * per, 0, per - 1), 0),
                        )
                    )
            extra.append(pltpu.VMEM((block, kind[1]), members[0].dtype))
    out_specs, shapes, groups_out, aliases = [], [], [], {}
    into = list(into)
    held_arrays = []
    for shape, dtype, kind in outputs:
        if kind == "parts":
            quarter = shape[0] // 4
            spec = (block, shape[1])
            if half is not None:
                for b in range(2):
                    shapes.append(jax.ShapeDtypeStruct((quarter, shape[1]), dtype))
                    out_specs.append(
                        pl.BlockSpec(spec, lambda i, b=b: (jnp.clip(i - b * per, 0, per - 1), 0))
                    )
                groups_out.append(2)
            else:
                for rows in (quarter, quarter, 2 * quarter):
                    shapes.append(jax.ShapeDtypeStruct((rows, shape[1]), dtype))
                out_specs += [
                    pl.BlockSpec(spec, lambda i: (jnp.clip(i, 0, per - 1), 0)),
                    pl.BlockSpec(spec, lambda i: (jnp.clip(i - 2 * per, 0, per - 1), 0)),
                    pl.BlockSpec(
                        spec,
                        lambda i: (
                            jnp.clip(i - per, 0, per - 1) + jnp.clip(i - 3 * per + 1, 0, per), 0
                        ),
                    ),
                ]
                groups_out.append(3)
            extra.append(pltpu.VMEM(spec, dtype))
        else:
            groups_out.append(1)
            shapes.append(jax.ShapeDtypeStruct(shape, dtype))
            if kind == "rows":
                if into:
                    aliases[len(arrays) + len(held_arrays)] = len(shapes) - 1
                    held_arrays.append(into.pop(0))
                out_specs.append(pl.BlockSpec((block, shape[1]), lambda i: (i + offset, 0)))
            else:
                zeros = (0,) * len(shape)
                out_specs.append(pl.BlockSpec(shape, lambda i, zeros=zeros: zeros))
    in_specs += [pl.BlockSpec(memory_space=pl.ANY) for _ in held_arrays]

    def wrapped(*refs):
        refs = list(refs)
        spare = refs[len(in_specs) + len(out_specs) + len(scratch) :]
        own_scratch = refs[len(in_specs) + len(out_specs) : len(refs) - len(spare)]
        quarter = pl.program_id(0) // per
        given, later, at, used = [], [], 0, 0
        for size, (_, kind) in zip(groups_in, inputs):
            if kind[0] != "pieces":
                given.append(refs[at])
            else:
                held = spare[used]
                used += 1
                if steps == 1:
                    for b in range(size):
                        piece = refs[at + b]
                        held[b * piece.shape[0] : (b + 1) * piece.shape[0], :] = piece[...]
                else:
                    for b in range(size):

                        @pl.when(quarter == b)
                        def _(held=held, source=refs[at + b]):
                            copy_rows(held, 0, source)

                given.append(held)
            at += size
        at += len(held_arrays)
        for size in groups_out:
            if size == 1:
                given.append(refs[at])
            else:
                given.append(spare[used])
                later.append((spare[used], refs[at : at + size]))
                used += 1
            at += size
        body(*given, *own_scratch)
        for held, targets in later:
            if len(targets) == 2:
                placed = ((0, targets[0]), (1, targets[1]))
            else:
                placed = ((0, targets[0]), (2, targets[1]), (1, targets[2]), (3, targets[2]))
            for b, target in placed:

                @pl.when(quarter == b)
                def _(held=held, target=target):
                    copy_rows(target, 0, held)

    results = pl.pallas_call(
        wrapped,
        out_shape=tuple(shapes),
        grid=(steps,),
        in_specs=in_specs,
        out_specs=out_specs,
        scratch_shapes=list(scratch) + extra,
        input_output_aliases=aliases,
        compiler_params=pltpu.CompilerParams(
            dimension_semantics=("arbitrary",), vmem_limit_bytes=VMEM_LIMIT
        ),
        cost_estimate=pl.CostEstimate(flops=flops, bytes_accessed=moved, transcendentals=0),
        name=name,
    )(*arrays, *held_arrays)
    grouped, at = [], 0
    for size in groups_out:
        grouped.append(results[at] if size == 1 else results[at : at + size])
        at += size
    return grouped


def flip(array, bit):
    groups = lax.axis_size("head")
    return lax.ppermute(array, "head", [(i, i ^ bit) for i in range(groups)])


def gather_rows(array):
    far = flip(array, 2)
    near = flip(array, 1)
    return [array, near, far, flip(far, 1)]


def tie(*arrays):
    return lax.optimization_barrier(arrays)


def near_sum(parts):
    own, far, pair = parts
    size = own.shape[0]
    arrived = flip(pair, 1)
    return (
        own.astype(single) + arrived[:size].astype(single),
        low(far.astype(single) + arrived[size:].astype(single)),
    )


def halves_sum(first, second):
    near, corner = tie(flip(first[1], 1), second[1])
    return (
        first[0].astype(single) + near.astype(single),
        low(second[0].astype(single) + flip(corner, 1).astype(single)),
    )


def far_sum(own, far):
    return own + flip(far, 2).astype(single)


def shifted_along(array, axis, by):
    length = lax.axis_size(axis)
    pairs = [(i, i + by) for i in range(length) if 0 <= i + by < length]
    return lax.ppermute(array, axis, pairs)


def seq_rows(flat):
    members = lax.axis_size("seq")
    return flat.reshape(members, flat.shape[0] // members, flat.shape[1])


def share_sum(parts):
    summed = low(jnp.sum(parts.astype(single), axis=0))
    return jnp.broadcast_to(summed[None], parts.shape)


def exchange(parts):
    return lax.all_to_all(parts, "seq", 0, 0)


def all_rows(parts):
    return parts.reshape(-1, parts.shape[-1])


def rms_scale(rows, gain):
    return rows * lax.rsqrt(jnp.mean(rows * rows, axis=-1, keepdims=True) + EPS) * gain


def rms_back(rows, gain, incoming):
    _, back = jax.vjp(lambda value: rms_scale(value, gain), rows)
    return back(incoming)[0]


def on_device(
    block_input,
    out_grad,
    lengths,
    doc_sets,
    norm1_gain,
    w_query,
    w_key,
    w_value,
    conv_query,
    conv_key,
    conv_value,
    w_decay_beta,
    decay_rate,
    decay_bias,
    w_gate_out,
    out_gain,
    w_out,
    norm2_gain,
    w_gate,
    w_up,
    w_down,
    adapt_down,
    adapt_up_qk,
    adapt_up_vg,
    adapt_up_ff,
    adapt_down_out,
    adapt_down_ffd,
    adapt_up_res,
):
    groups = lax.axis_size("head")
    members = lax.axis_size("seq")
    place = lax.axis_index("head")
    quarter, width = block_input.shape
    count = quarter * groups
    heads = decay_rate.shape[0]
    key_width = w_query.shape[1] // heads
    value_width = w_value.shape[1] // heads
    sets, rank = adapt_down.shape[1], adapt_down.shape[3]
    low_rank = sets * rank
    qk = heads * key_width
    device_start = lax.axis_index("seq") * count
    starts = jnp.sum(
        jnp.where(
            jnp.arange(lengths.shape[0])[None, :] < jnp.arange(lengths.shape[0])[:, None],
            lengths[None, :],
            0,
        ),
        axis=1,
    )
    order = jnp.arange(groups, dtype=jnp.int32) ^ place

    def tables(positions):
        reached = positions[:, None] >= starts[None, :]
        token_start = jnp.max(jnp.where(reached, starts[None, :], -1), axis=1)
        ended = positions[:, None] >= (starts + lengths)[None, :]
        token_set = jnp.sum(jnp.where(reached & ~ended, doc_sets[None, :], 0), axis=1)
        pair = jnp.stack([token_start - device_start, token_set], axis=1).astype(single)
        return jnp.pad(pair, ((0, 0), (0, 8 - pair.shape[1])))

    table = tables(
        (
            device_start + order[:, None] * quarter + jnp.arange(quarter, dtype=jnp.int32)[None, :]
        ).reshape(-1)
    )
    halo_table = tables(device_start + jnp.arange(-HALO, 0, dtype=jnp.int32))
    column_sets = jnp.broadcast_to(
        (jnp.arange(low_rank, dtype=jnp.int32) // rank).astype(single)[None, :], (8, low_rank)
    )

    down = adapt_down.transpose(0, 1, 3, 2).reshape(6 * low_rank, width)
    up_qk = adapt_up_qk.reshape(2, low_rank, -1)
    up_vg = adapt_up_vg.reshape(2 * low_rank, -1)
    up_ff = adapt_up_ff.reshape(2, low_rank, -1)
    down_out = adapt_down_out.transpose(0, 2, 1).reshape(low_rank, -1)
    down_ffd = adapt_down_ffd.transpose(0, 2, 1).reshape(low_rank, -1)
    up_res = adapt_up_res.reshape(2 * low_rank, width)
    conv = jnp.concatenate([conv_query, conv_key, conv_value], axis=1).astype(single)
    scalars = jnp.stack([decay_rate, decay_bias])
    where = place.reshape(1).astype(jnp.int32)
    weight_mix = jnp.pad(
        w_decay_beta.transpose(1, 2, 0).reshape(2 * heads, width), ((0, 8 - 2 * heads), (0, 0))
    )
    gain = jnp.broadcast_to(out_gain[None, :], (8, value_width))
    hidden_width = w_down.shape[0]
    padded = -(-hidden_width // 256) * 256
    value_lanes = heads * value_width
    block_width = width // groups
    widen = lambda a: jnp.pad(a, [(0, 0)] * (a.ndim - 1) + [(0, padded - hidden_width)])

    input_float = block_input.astype(single)
    normed = low(rms_scale(input_float, norm1_gain))
    tail = normed[quarter - HALO :]
    halo = sum(
        lax.ppermute(
            tail,
            ("seq", "head"),
            [((s * groups) + groups - 1, (s + 1) * groups + h) for s in range(members - 1)],
        )
        for h in range(groups)
    )
    normed_near, normed_far = flip(normed, 1), flip(normed, 2)
    project_inputs = [
        (table, by_rows(8)),
        (column_sets, WHOLE),
        (down, part(4 * low_rank, 0)),
        (weight_mix, WHOLE),
        (w_query, WHOLE),
        (w_key, WHOLE),
        (w_value, WHOLE),
        (w_gate_out, WHOLE),
        (up_qk, WHOLE),
        (up_vg, WHOLE),
    ]
    project_outputs = [
        ((count, 2 * qk + value_lanes), bfloat, "rows"),
        ((count, 3 * low_rank), bfloat, "rows"),
        ((count, 8), single, "rows"),
        ((count, value_lanes), single, "rows"),
        ((count, low_rank), bfloat, "rows"),
    ]
    project_scratch = [pltpu.VMEM((width + low_rank, 2 * qk + 2 * value_lanes), bfloat)]
    projected = blocked_call(
        functools.partial(project_kernel, with_halo=False),
        "project_near",
        count,
        [([normed, normed_near], pieces(width)), *project_inputs],
        project_outputs,
        project_scratch,
        count * 2_000_000,
        half=0,
    )
    normed_far, projected[2] = tie(normed_far, projected[2])
    normed_all = [normed, normed_near, normed_far, flip(normed_far, 1)]
    pre, inner, columns, gate_input, inner_gate, pre_halo = blocked_call(
        functools.partial(project_kernel, with_halo=True),
        "project_far",
        count,
        [
            (normed_all[2:], pieces(width)),
            *project_inputs,
            (halo, WHOLE),
            (halo_table, WHOLE),
        ],
        project_outputs + [((HALO, 2 * qk + value_lanes), bfloat, "whole")],
        project_scratch,
        count * 2_000_000,
        half=1,
        into=projected,
    )
    out_grad_late, grad_near, pre = tie(out_grad, flip(out_grad, 1), pre)
    grad_far, grad_corner = flip(out_grad_late, 2), flip(grad_near, 2)
    raw_local, mapped, *saved, sent, sent_state = run_forward(
        where, pre, pre_halo, columns, conv, scalars, heads, key_width, value_width, quarter
    )

    hops = min(members - 1, -(-(DOC_MAX - 1) // count))
    got = [shifted_along(sent_state, "seq", hops)]
    got = [shifted_along(sent, "seq", hop) for hop in range(hops - 1, 0, -1)][::-1] + got
    grad_far, grad_corner, sent_state = tie(grad_far, grad_corner, sent_state)
    grad_all = [out_grad, grad_near, grad_far, grad_corner]
    hidden_grad, du_down = blocked_call(
        feed_before_kernel,
        "feed_before",
        count,
        [
            (grad_all, pieces(width)),
            (table, by_rows(8)),
            (column_sets, WHOLE),
            (w_down, WHOLE),
            (down_ffd.T, WHOLE),
            (up_res, part(low_rank, 1)),
        ],
        [((count, padded), single, "rows"), ((count, low_rank), bfloat, "rows")],
        [pltpu.VMEM((padded, width + low_rank), bfloat)],
        count * 6_000_000,
    )
    raw_local, hidden_grad = tie(raw_local, hidden_grad)

    sizes = dict(heads=heads, key_width=key_width, value_width=value_width)
    attention_part, mixed, u_out, entering = blocked_call(
        functools.partial(attend_kernel, hops=hops, **sizes),
        "attend",
        count,
        [
            (raw_local, by_rows(value_lanes)),
            (mapped, by_rows(qk)),
            (gate_input, by_rows(value_lanes)),
            (table, by_rows(8)),
            (gain, WHOLE),
            (column_sets, WHOLE),
            (w_out, WHOLE),
            (down_out, WHOLE),
            (up_res, part(low_rank, 0)),
        ]
        + [(sent_by, WHOLE) for sent_by in got],
        [
            ((count, width), bfloat, "parts"),
            ((count, value_lanes), bfloat, "rows"),
            ((count, low_rank), bfloat, "rows"),
            ((heads, key_width, value_width), bfloat, "whole"),
        ],
        [pltpu.VMEM((value_lanes + low_rank, width), bfloat)],
        count * 5_000_000,
    )
    attention_own, attention_far = near_sum(attention_part)
    attention_arrived, up_ff_t, up_ff_padded, down_ffd_padded, down_out_t = tie(
        flip(attention_far, 2),
        up_ff.transpose(0, 2, 1),
        widen(up_ff),
        widen(down_ffd),
        down_out.T,
    )
    residual = input_float + (attention_own + attention_arrived.astype(single))
    normed_mid = low(rms_scale(residual, norm2_gain))
    mid_near, mid_far = flip(normed_mid, 1), flip(normed_mid, 2)

    feed_inputs = [
        (hidden_grad, by_rows(padded)),
        (table, by_rows(8)),
        (column_sets, WHOLE),
        (down, part(2 * low_rank, 2)),
        (w_gate.T, WHOLE),
        (w_up.T, WHOLE),
        (up_ff_t, WHOLE),
        (up_ff_padded, WHOLE),
    ]
    feed_outputs = [
        ((count, width), bfloat, "parts"),
        ((count, padded), bfloat, "rows"),
        ((count, 2 * padded), bfloat, "rows"),
        ((count, 2 * low_rank), bfloat, "rows"),
        ((count, 2 * low_rank), bfloat, "rows"),
    ]
    feed_scratch = [
        pltpu.VMEM((padded, width + low_rank), bfloat),
        pltpu.VMEM((padded, width + low_rank), bfloat),
        pltpu.VMEM((2 * padded + 2 * low_rank, width), bfloat),
    ]
    near_part, *fed = blocked_call(
        feed_kernel,
        "feed_near",
        count,
        [([normed_mid, mid_near], pieces(width)), *feed_inputs],
        feed_outputs,
        feed_scratch,
        count * 8_000_000,
        half=0,
    )
    mid_far, near_own = tie(mid_far, near_part[0])
    near_part = [near_own, near_part[1]]
    mid_all = [normed_mid, mid_near, mid_far, flip(mid_far, 1)]
    far_part, hidden, ff_grad, u_ff, du_ff = blocked_call(
        feed_kernel,
        "feed_far",
        count,
        [(mid_all[2:], pieces(width)), *feed_inputs],
        feed_outputs,
        feed_scratch,
        count * 8_000_000,
        half=1,
        into=fed,
    )
    grad_own, grad_sum = halves_sum(near_part, far_part)
    grad_sum, hidden = tie(grad_sum, hidden)
    grad_arrived = flip(grad_sum, 2)
    out_part, feed_own, feed_far, feed_pair, feed_owned = blocked_call(
        feed_after_kernel,
        "feed_after",
        count,
        [
            (mid_all, pieces(width)),
            (grad_all, pieces(width)),
            (hidden, by_rows(padded)),
            (ff_grad, by_rows(2 * padded)),
            (u_ff, by_rows(2 * low_rank)),
            (du_ff, by_rows(2 * low_rank)),
            (du_down, by_rows(low_rank)),
            (table, by_rows(8)),
            (column_sets, WHOLE),
            (where, SCALAR),
            (w_down, WHOLE),
            (down_ffd_padded, WHOLE),
            (up_res, part(low_rank, 1)),
        ],
        [
            ((count, width), bfloat, "parts"),
            ((low_rank, 3 * block_width), bfloat, "whole"),
            ((low_rank, 3 * block_width), bfloat, "whole"),
            ((2 * low_rank, 3 * block_width), bfloat, "whole"),
            ((low_rank, 3 * padded), bfloat, "whole"),
        ],
        [
            pltpu.VMEM((padded + low_rank, width), bfloat),
            pltpu.VMEM((2 * low_rank, width), single),
            pltpu.VMEM((low_rank, width), single),
            pltpu.VMEM((low_rank, 3 * padded), single),
        ],
        count * 16_000_000,
    )
    grad_landed, feed_far = tie(grad_arrived, feed_far)
    mid_grad = grad_own + grad_landed.astype(single)
    residual_grad = out_grad.astype(single) + rms_back(residual, norm2_gain, mid_grad)
    branch_low = low(residual_grad)
    branch_near, branch_far = flip(branch_low, 1), flip(branch_low, 2)
    out_own, out_far = near_sum(out_part)
    owned_parts = exchange(seq_rows(tie(feed_owned, branch_near)[0]))
    feed_sum, feed_sum_far = near_sum((feed_own, feed_far, tie(feed_pair, grad_arrived)[0]))
    feed_landed = flip(feed_sum_far, 2)

    branch_inputs = [
        (raw_local, by_rows(value_lanes)),
        (mapped, by_rows(qk)),
        (gate_input, by_rows(value_lanes)),
        (table, by_rows(8)),
        (entering, WHOLE),
        (gain, WHOLE),
        (column_sets, WHOLE),
        (w_out, WHOLE),
        (down_out_t, WHOLE),
        (up_res, part(low_rank, 0)),
        (up_vg, part(low_rank, 1)),
    ]
    branch_outputs = [
        ((count, value_lanes), bfloat, "rows"),
        ((count, value_lanes), bfloat, "rows"),
        ((count, low_rank), bfloat, "rows"),
        ((count, low_rank), bfloat, "rows"),
    ]
    branch_scratch = [pltpu.VMEM((value_lanes, width + low_rank), bfloat)]
    state_shape = (heads, key_width, value_width)
    *branched, state_near = blocked_call(
        functools.partial(branch_kernel, hops=hops, last=False, **sizes),
        "branch_near",
        count,
        [([branch_low, branch_near], pieces(width)), *branch_inputs],
        branch_outputs + [(state_shape, single, "whole")],
        branch_scratch,
        count * 12_000_000,
        half=0,
    )
    branch_far, state_near = tie(branch_far, state_near)
    branch_corner, owned_parts, out_far = tie(flip(branch_far, 1), owned_parts, out_far)
    branch_all = [branch_low, branch_near, branch_far, branch_corner]
    raw_grad, gate_grad, du_out, du_outgate, *state_grads = blocked_call(
        functools.partial(branch_kernel, hops=hops, last=True, **sizes),
        "branch_far",
        count,
        [(branch_all[2:], pieces(width)), *branch_inputs, (state_near, WHOLE)]
        + [(sent_by, WHOLE) for sent_by in got[:-1]],
        branch_outputs + [(state_shape, bfloat, "whole")] * hops,
        branch_scratch + [pltpu.VMEM(state_shape, single)],
        count * 4_000_000,
        half=1,
        into=branched,
    )
    state_got = [
        shifted_along(state_grads[hop - 1], "seq", -hop) for hop in range(hops, 0, -1)
    ][::-1]
    mixer_down_late, branch_res_grad, branch_flat = blocked_call(
        branch_after_kernel,
        "branch_after",
        count,
        [
            (branch_all, pieces(width)),
            (mixed, by_rows(value_lanes)),
            (u_out, by_rows(low_rank)),
            (normed_all, pieces(width)),
            (inner_gate, by_rows(low_rank)),
            (du_out, by_rows(low_rank)),
            (du_outgate, by_rows(low_rank)),
            (gate_grad, by_rows(value_lanes)),
        ],
        [
            ((low_rank, width), single, "whole"),
            ((low_rank, width), single, "whole"),
            ((low_rank, 2 * value_lanes), bfloat, "whole"),
        ],
        [pltpu.VMEM((low_rank, 2 * value_lanes), single)],
        count * 20_000_000,
    )
    feed_landed, du_out = tie(feed_landed, du_out)
    feed_shared = low(feed_sum + feed_landed.astype(single))
    owned_lanes = owned_parts.shape[-1]
    both = jnp.concatenate(
        [share_sum(owned_parts), seq_rows(feed_shared), seq_rows(branch_flat)], axis=2
    )
    raw_grad, both, out_far, *state_got = tie(raw_grad, both, out_far, *state_got)
    out_arrived = flip(out_far, 2)
    both = exchange(both)

    pre_grad, mix_grad, tail_grad, edge_grad = run_backward(
        where, pre, pre_halo, columns, conv, scalars, raw_grad, saved, entering, state_got,
        heads, key_width, value_width, quarter,
    )
    arrived = shifted_along(edge_grad, "seq", -1)
    arrived, both, out_arrived = tie(arrived, both, out_arrived)
    result = residual + (out_own + out_arrived.astype(single))
    later_parts = both[:, :, owned_lanes:]
    settled = [
        (pre_grad, by_rows(2 * qk + value_lanes)),
        (tail_grad, WHOLE),
        (arrived, WHOLE),
        (where, SCALAR),
    ]
    du_mix, last_own, last_far, last_pair, last_owned = blocked_call(
        functools.partial(settle_grads_kernel, quarter=quarter),
        "settle_grads",
        count,
        [
            settled[0],
            (normed_all, pieces(width)),
            (inner, by_rows(3 * low_rank)),
            (table, by_rows(8)),
            *settled[1:],
            (column_sets, WHOLE),
            (up_qk, WHOLE),
            (up_vg, part(low_rank, 0)),
            (mixer_down_late, WHOLE),
            (branch_res_grad, WHOLE),
        ],
        [
            ((count, 3 * low_rank), bfloat, "rows"),
            ((low_rank, 5 * block_width), bfloat, "whole"),
            ((low_rank, 5 * block_width), bfloat, "whole"),
            ((2 * low_rank, 5 * block_width), bfloat, "whole"),
            ((low_rank, 2 * qk + value_lanes), bfloat, "whole"),
        ],
        [
            pltpu.VMEM((STEP, 2 * qk + value_lanes), bfloat),
            pltpu.VMEM((3 * low_rank, width), single),
            pltpu.VMEM((low_rank, 2 * qk + value_lanes), single),
        ],
        count * 4_000_000,
    )
    last_own, last_far = near_sum((last_own, last_far, last_pair))
    last_far, gate_grad = tie(last_far, gate_grad)
    (normed_part,) = blocked_call(
        functools.partial(settle_kernel, quarter=quarter),
        "settle",
        count,
        [
            settled[0],
            (gate_grad, by_rows(value_lanes)),
            (du_mix, by_rows(3 * low_rank)),
            (du_outgate, by_rows(low_rank)),
            (mix_grad, by_rows(8)),
            *settled[1:],
            (down, part(4 * low_rank, 0)),
            (weight_mix, WHOLE),
            (w_query, WHOLE),
            (w_key, WHOLE),
            (w_value, WHOLE),
            (w_gate_out, WHOLE),
        ],
        [((count, width), bfloat, "parts")],
        [
            pltpu.VMEM((STEP, 2 * qk + value_lanes), bfloat),
            pltpu.VMEM((width, 2 * qk + 2 * value_lanes), bfloat),
            pltpu.VMEM((5 * low_rank, width), bfloat),
        ],
        count * 10_000_000,
    )
    last_flat = jnp.concatenate([low(far_sum(last_own, last_far)), last_owned], axis=1)
    feed_rows = all_rows(both)
    last_lanes = last_flat.shape[1]
    both = exchange(jnp.concatenate([seq_rows(last_flat), share_sum(later_parts)], axis=2))
    normed_own, normed_sum_far = near_sum(normed_part)
    both, normed_sum_far = tie(both, normed_sum_far)
    normed_landed = flip(normed_sum_far, 2)
    branch_rows = all_rows(both)
    feed_piece = branch_rows[:, last_lanes : last_lanes + 3 * block_width]
    feed_piece_far = flip(feed_piece, 2)
    last_parts = both[:, :, :last_lanes]
    normed_landed, feed_piece_far = tie(normed_landed, feed_piece_far)
    feed_pieces = [feed_piece, flip(feed_piece, 1), feed_piece_far, flip(feed_piece_far, 1)]
    normed_grad = normed_own + normed_landed.astype(single)
    input_grad = residual_grad + rms_back(input_float, norm1_gain, normed_grad)
    last_rows = all_rows(exchange(share_sum(last_parts)))
    piece = last_rows[:, : 5 * block_width]
    piece_far, input_grad, feed_pieces[3] = tie(flip(piece, 2), input_grad, feed_pieces[3])
    last_pieces = [piece, flip(piece, 1), piece_far, flip(piece_far, 1)]
    down_grad, qk_grad, vg_grad, ff_grads, out_grads, ffd_grads, res_grad = assemble(
        where,
        [*last_pieces, *feed_pieces],
        last_rows,
        feed_rows,
        branch_rows,
        padded,
        [
            (6, low_rank, width),
            (2, low_rank, qk),
            (2, low_rank, value_lanes),
            (2, low_rank, hidden_width),
            (low_rank, value_lanes),
            (low_rank, hidden_width),
            (2, low_rank, width),
        ],
    )

    def as_down(rows):
        return rows.reshape(rows.shape[:-2] + (sets, rank, -1)).swapaxes(-1, -2)

    def as_up(rows):
        return rows.reshape(rows.shape[0], sets, rank, -1)

    return (
        low(result),
        input_grad,
        as_down(down_grad),
        as_up(qk_grad),
        as_up(vg_grad),
        as_up(ff_grads),
        as_down(out_grads),
        as_down(ffd_grads),
        as_up(res_grad),
    )


def solution(mesh):
    rows = P(("seq", "head"), None)
    lanes = P(None, "head")
    last = P(None, None, None, "head")
    middle = P(None, "head", None)
    in_specs = (
        rows, rows, P(), P(), P(), lanes, lanes, lanes, lanes, lanes, lanes,
        P(None, None, "head"), P("head"), P("head"), lanes, P(), P("head", None), P(), lanes,
        lanes, P("head", None), P(), last, last, last, middle, middle, P(),
    )
    out_specs = (rows, rows, P(), last, last, last, middle, middle, P())
    return jax.shard_map(
        on_device, mesh=mesh, in_specs=in_specs, out_specs=out_specs, check_vma=False
    )
```

```python
import functools

import jax
import jax.numpy as jnp
from jax import lax
from jax.experimental import pallas as pl
from jax.experimental.pallas import tpu as pltpu
from jax.sharding import PartitionSpec as P

CHUNK = 128
STEP = 256
HALO = 16
DOC_MAX = 4096
EPS = 1e-06
VMEM_LIMIT = 56 * 1024 * 1024
bfloat = jnp.bfloat16
single = jnp.float32


def contract(left, right, left_dim, right_dim):
    return lax.dot_general(
        left,
        right,
        (((left_dim,), (right_dim,)), ((), ())),
        preferred_element_type=single,
    )


def nn(left, right):
    return contract(left, right, 1, 0)


def nt(left, right):
    return contract(left, right, 1, 1)


def tn(left, right):
    return contract(left, right, 0, 0)


def low(array):
    return array.astype(bfloat)


def iotas():
    rows = lax.broadcasted_iota(jnp.int32, (CHUNK, CHUNK), 0)
    columns = lax.broadcasted_iota(jnp.int32, (CHUNK, CHUNK), 1)
    return rows, columns


def split_two(array):
    high = low(array)
    return high, low(array - high.astype(single))


def near_exact(left, right):
    left_high, left_low = split_two(left)
    right_high, right_low = split_two(right)
    return nn(
        jnp.concatenate([left_high, left_high, left_low], axis=1),
        jnp.concatenate([right_high, right_low, right_high], axis=0),
    )


def ones_product(ones, array):
    high = low(array)
    rest = array - high.astype(single)
    middle = low(rest)
    lowest = low(rest - middle.astype(single))
    return nn(
        jnp.concatenate([ones, ones, ones], axis=1),
        jnp.concatenate([high, middle, lowest], axis=0),
    )


def unit_lower_inverses(stricts, rows, columns):
    eye = (rows == columns).astype(single)
    differ = rows ^ columns
    block = 8
    inner = [jnp.where(differ < block, strict, 0.0) for strict in stricts]
    second = [near_exact(a, a) for a in inner]
    inverse = [near_exact(eye - a, eye + b) for a, b in zip(inner, second)]
    fourth = [near_exact(b, b) for b in second]
    inverse = [near_exact(a, eye + b) for a, b in zip(inverse, fourth)]
    while block < CHUNK:
        between = (differ >= block) & (differ < 2 * block)
        off = [jnp.where(between, strict, 0.0) for strict in stricts]
        part = [near_exact(a, b) for a, b in zip(off, inverse)]
        inverse = [a - near_exact(a, b) for a, b in zip(inverse, part)]
        block = 2 * block
    return inverse


def softplus(value):
    return jnp.maximum(value, 0.0) + jnp.log(1.0 + jnp.exp(-jnp.abs(value)))


def sigmoid(value):
    return 1.0 / (1.0 + jnp.exp(-value))


def gates(decay, start, rows, columns):
    lower_ones = low((rows >= columns).astype(single))
    total = ones_product(lower_ones, jnp.broadcast_to(decay, (CHUNK, CHUNK)))
    linked = (rows >= columns) & (columns >= start)
    within = jnp.where(linked, jnp.exp(jnp.where(linked, total - total.T, 0.0)), 0.0)
    running = total[:, :1]
    carried = jnp.where(start < 0, jnp.exp(running), 0.0)
    last = running[CHUNK - 1 : CHUNK]
    ending = jnp.where(
        rows[:, :1] >= start[CHUNK - 1 : CHUNK], jnp.exp(jnp.minimum(last - running, 0.0)), 0.0
    )
    return within, carried, ending


def convolved(window, starts, weights, base):
    positions = base + lax.broadcasted_iota(jnp.int32, (STEP, 1), 0)
    taps = weights.shape[0]
    total = None
    for tap in range(taps):
        back = taps - 1 - tap
        term = window[HALO - back : HALO - back + STEP, :] * weights[tap : tap + 1, :]
        if back:
            term = jnp.where(positions - back >= starts, term, 0.0)
        total = term if total is None else total + term
    return total


def head_scales(rows, width):
    return lax.rsqrt(jnp.sum(rows * rows, axis=-1, keepdims=True) + EPS)


def forward_kernel(
    place,
    rows_ref,
    halo_ref,
    column_ref,
    weight_ref,
    scalar_ref,
    out_ref,
    map_ref,
    written_ref,
    state_ref,
    inverse_ref,
    end_ref,
    sent_ref,
    sent_state_ref,
    window,
    state,
    *,
    heads,
    key_width,
    value_width,
):
    step = pl.program_id(0)
    wide = value_width + key_width
    base = step * STEP
    rows, columns = iotas()

    @pl.when(step == 0)
    def _():
        window[0:HALO, :] = halo_ref[...].astype(single)
        for h in range(heads):
            state[h, :, :value_width] = jnp.zeros((key_width, value_width), single)
            state[h, :, value_width:] = (rows == columns).astype(single)

    @pl.when(step > 0)
    def _():
        window[0:HALO, :] = window[STEP : STEP + HALO, :]

    window[HALO:, :] = rows_ref[...].astype(single)
    info = column_ref[...]
    starts = info[:, 2 * heads : 2 * heads + 1].astype(jnp.int32)
    before = convolved(window, starts, weight_ref[...], base)
    active = before * sigmoid(before)
    qk_lanes = heads * key_width
    chunks = STEP // CHUNK
    local, stricts = [], []
    for c in range(chunks):
        span = slice(c * CHUNK, (c + 1) * CHUNK)
        for h in range(heads):
            query = active[span, h * key_width : (h + 1) * key_width]
            key = active[span, qk_lanes + h * key_width : qk_lanes + (h + 1) * key_width]
            value = active[
                span, 2 * qk_lanes + h * value_width : 2 * qk_lanes + (h + 1) * value_width
            ]
            query = query * (head_scales(query, key_width) * key_width ** (-0.5))
            key = key * head_scales(key, key_width)
            beta = sigmoid(info[span, h : h + 1])
            decay = -scalar_ref[0, h] * softplus(
                info[span, heads + h : heads + h + 1] + scalar_ref[1, h]
            )
            within, carried, ending = gates(
                decay, starts[span] - (base + c * CHUNK), rows, columns
            )
            query, key = low(query), low(key)
            strict = jnp.where(rows > columns, within * nt(key, key), 0.0) * beta
            mixed = low(within * nt(query, key))
            stricts.append(strict)
            local.append((query, key, value, beta, carried, ending, mixed))
    inverses = [low(a) for a in unit_lower_inverses(stricts, rows, columns)]
    each = range(heads)
    now = [state[h] for h in each]
    for c in range(chunks):
        span = slice(c * CHUNK, (c + 1) * CHUNK)
        here = [local[c * heads + h] for h in each]
        inverse = [inverses[c * heads + h] for h in each]
        now_low = [low(a) for a in now]
        read = [nn(here[h][1], now_low[h]) for h in each]
        asked = [nn(here[h][0], now_low[h]) for h in each]
        target = []
        for h in each:
            query, key, value, beta, carried, ending, mixed = here[h]
            gap = -(carried * beta) * read[h]
            target.append(
                jnp.concatenate(
                    [beta * value + gap[:, :value_width], gap[:, value_width:]], axis=1
                )
            )
        written = [nn(inverse[h], low(target[h])) for h in each]
        added = [tn(here[h][1], low(here[h][5] * written[h])) for h in each]
        inner = [nn(here[h][6], low(written[h])) for h in each]
        for h in each:
            carried = here[h][4]
            inverse_ref[span, h * CHUNK : (h + 1) * CHUNK] = inverse[h]
            state_ref[c, h] = now_low[h]
            written_ref[span, h * wide : (h + 1) * wide] = low(written[h])
            output = carried * asked[h] + inner[h]
            out_ref[span, h * value_width : (h + 1) * value_width] = output[:, :value_width]
            map_ref[span, h * key_width : (h + 1) * key_width] = low(output[:, value_width:])
        now = [here[h][4][CHUNK - 1 : CHUNK] * now[h] + added[h] for h in each]
    for h in each:
        state[h] = now[h]

    @pl.when(step == pl.num_programs(0) - 1)
    def _():
        final = state[...]
        end_ref[...] = final
        sent_ref[...] = low(final)
        sent_state_ref[...] = low(final[:, :, :value_width])


def backward_kernel(
    place,
    rows_ref,
    before_ref,
    halo_ref,
    column_ref,
    weight_ref,
    scalar_ref,
    grad_ref,
    written_ref,
    state_ref,
    inverse_ref,
    end_ref,
    entering_ref,
    *rest,
    hops,
    heads,
    key_width,
    value_width,
):
    got_refs, rest = rest[:hops], rest[hops:]
    out_ref, mix_ref, tail_ref, edge_ref, window, shifted, shifted_start, cotangent, ahead = rest
    step = pl.program_id(0)
    steps = pl.num_programs(0)
    wide = value_width + key_width
    base = (steps - 1 - step) * STEP
    rows, columns = iotas()
    qk_lanes = heads * key_width
    lanes = window.shape[1]
    taps = weight_ref.shape[0]

    @pl.when(step == 0)
    def _():
        shifted[STEP : STEP + 8, :] = jnp.zeros((8, lanes), single)
        shifted_start[STEP : STEP + 8, :] = jnp.zeros((8, 1), jnp.int32)
        for h in range(heads):
            passed = got_refs[0][h].astype(single)
            for hop in range(1, hops):
                passed = passed + got_refs[hop][h].astype(single)
            cotangent[h] = passed
            ahead[h] = end_ref[h, :, :value_width] + nn(
                low(end_ref[h, :, value_width:]), low(entering_ref[h])
            )

    @pl.when(step > 0)
    def _():
        shifted[STEP : STEP + 8, :] = shifted[0:8, :]
        shifted_start[STEP : STEP + 8, :] = shifted_start[0:8, :]

    window[0:HALO, :] = jnp.where(
        step == steps - 1, halo_ref[...].astype(single), before_ref[...].astype(single)
    )
    window[HALO:, :] = rows_ref[...].astype(single)
    info = column_ref[...]
    starts = info[:, 2 * heads : 2 * heads + 1].astype(jnp.int32)
    positions = base + lax.broadcasted_iota(jnp.int32, (STEP, 1), 0)
    before = convolved(window, starts, weight_ref[...], base)
    gate = sigmoid(before)
    active = before * gate
    slope = gate * (1.0 + before * (1.0 - gate))
    upper_ones = low((rows <= columns).astype(single))
    last_row = rows[:, :1] == CHUNK - 1
    chunks = STEP // CHUNK
    each = range(heads)
    items = [(c, h) for c in range(chunks) for h in each]
    spans = {item: slice(item[0] * CHUNK, (item[0] + 1) * CHUNK) for item in items}
    entering = [low(entering_ref[h]) for h in each]
    root = key_width ** (-0.5)

    def per(function):
        return {item: function(*item) for item in items}

    def q_lanes(h):
        return slice(h * key_width, (h + 1) * key_width)

    def k_lanes(h):
        return slice(qk_lanes + h * key_width, qk_lanes + (h + 1) * key_width)

    def v_lanes(h):
        return slice(2 * qk_lanes + h * value_width, 2 * qk_lanes + (h + 1) * value_width)

    def kept(c, h, part):
        return written_ref[spans[c, h], h * wide : (h + 1) * wide][:, part]

    values, maps = slice(0, value_width), slice(value_width, wide)
    query_raw = per(lambda c, h: active[spans[c, h], q_lanes(h)])
    key_raw = per(lambda c, h: active[spans[c, h], k_lanes(h)])
    query_scale = per(lambda c, h: head_scales(query_raw[c, h], key_width))
    key_scale = per(lambda c, h: head_scales(key_raw[c, h], key_width))
    query = per(lambda c, h: query_raw[c, h] * (query_scale[c, h] * root))
    key = per(lambda c, h: key_raw[c, h] * key_scale[c, h])
    query_low = per(lambda c, h: low(query[c, h]))
    key_low = per(lambda c, h: low(key[c, h]))
    beta = per(lambda c, h: sigmoid(info[spans[c, h], h : h + 1]))
    raw = per(lambda c, h: info[spans[c, h], heads + h : heads + h + 1] + scalar_ref[1, h])
    gated = per(
        lambda c, h: gates(
            -scalar_ref[0, h] * softplus(raw[c, h]),
            starts[spans[c, h]] - (base + c * CHUNK),
            rows,
            columns,
        )
    )
    within = per(lambda c, h: gated[c, h][0])
    carried = per(lambda c, h: gated[c, h][1])
    ending = per(lambda c, h: gated[c, h][2])
    mixed = per(lambda c, h: low(within[c, h] * nt(query_low[c, h], key_low[c, h])))
    written = per(
        lambda c, h: kept(c, h, values).astype(single) + nn(kept(c, h, maps), entering[h])
    )
    start_state = per(
        lambda c, h: state_ref[c, h][:, values].astype(single)
        + nn(state_ref[c, h][:, maps], entering[h])
    )
    written_low = per(lambda c, h: low(written[c, h]))
    start_low = per(lambda c, h: low(start_state[c, h]))
    grad = per(lambda c, h: grad_ref[spans[c, h], h * value_width : (h + 1) * value_width])
    grad_low = grad
    carried_grad = per(lambda c, h: low(carried[c, h] * grad[c, h].astype(single)))
    from_output = per(lambda c, h: tn(mixed[c, h], grad_low[c, h]))
    state_part = per(lambda c, h: tn(query_low[c, h], carried_grad[c, h]))
    mixed_grad = per(lambda c, h: low(within[c, h] * nt(grad_low[c, h], written_low[c, h])))
    query_grad = per(
        lambda c, h: nt(carried_grad[c, h], start_low[c, h]) + nn(mixed_grad[c, h], key_low[c, h])
    )
    key_write = per(lambda c, h: tn(mixed_grad[c, h], query_low[c, h]))
    later, later_low, solved, value_grad, read_grad = {}, {}, {}, {}, {}
    now = [cotangent[h] for h in each]
    for c in reversed(range(chunks)):
        for h in each:
            later[c, h], later_low[c, h] = now[h], low(now[h])
        from_state = [nn(key_low[c, h], later_low[c, h]) for h in each]
        written_grad = [low(from_output[c, h] + ending[c, h] * from_state[h]) for h in each]
        for h in each:
            inverse = inverse_ref[spans[c, h], h * CHUNK : (h + 1) * CHUNK]
            solved[c, h] = tn(inverse, written_grad[h])
        for h in each:
            value_grad[c, h] = beta[c, h] * solved[c, h]
            read_grad[c, h] = low(-carried[c, h] * value_grad[c, h])
        now = [
            carried[c, h][CHUNK - 1 : CHUNK] * now[h]
            + state_part[c, h]
            + tn(key_low[c, h], read_grad[c, h])
            for h in each
        ]
    following = {
        (c, h): start_state[c + 1, h] if c + 1 < chunks else ahead[h] for c, h in items
    }
    at_end = per(lambda c, h: jnp.sum(later[c, h] * following[c, h], keepdims=True))
    for h in each:
        cotangent[h] = now[h]
        ahead[h] = start_state[0, h]
    strict_grad = per(
        lambda c, h: low(
            jnp.where(
                rows > columns, -within[c, h] * nt(low(value_grad[c, h]), written_low[c, h]), 0.0
            )
        )
    )
    key_read = per(
        lambda c, h: nt(read_grad[c, h], start_low[c, h]) + nn(strict_grad[c, h], key_low[c, h])
    )
    key_write = per(
        lambda c, h: key_write[c, h]
        + tn(strict_grad[c, h], key_low[c, h])
        + nt(low(ending[c, h] * written[c, h]), later_low[c, h])
    )
    query_dot = per(
        lambda c, h: jnp.sum(query[c, h] * query_grad[c, h], axis=-1, keepdims=True)
    )
    running_grad = per(
        lambda c, h: query_dot[c, h]
        + jnp.sum(key[c, h] * (key_read[c, h] - key_write[c, h]), axis=-1, keepdims=True)
        + jnp.where(last_row, at_end[c, h], 0.0)
    )
    decay_sum = per(
        lambda c, h: ones_product(
            upper_ones, jnp.broadcast_to(running_grad[c, h], (CHUNK, CHUNK))
        )[:, :1]
    )
    decay_grad = per(
        lambda c, h: jnp.where(
            positions[spans[c, h]] == starts[spans[c, h]],
            0.0,
            -scalar_ref[0, h] * sigmoid(raw[c, h]) * decay_sum[c, h],
        )
    )
    beta_grad = per(
        lambda c, h: jnp.sum(solved[c, h] * written[c, h], axis=-1, keepdims=True)
        * sigmoid(-info[spans[c, h], h : h + 1])
    )
    for c, h in items:
        span = spans[c, h]
        key_grad = key_read[c, h] + key_write[c, h]
        key_dot = jnp.sum(key[c, h] * key_grad, axis=-1, keepdims=True)
        query_active = (query_scale[c, h] * root) * query_grad[c, h] - query_raw[c, h] * (
            query_scale[c, h] * query_scale[c, h] * query_dot[c, h]
        )
        key_active = key_scale[c, h] * (key_grad - key[c, h] * key_dot)
        shifted[span, q_lanes(h)] = query_active * slope[span, q_lanes(h)]
        shifted[span, k_lanes(h)] = key_active * slope[span, k_lanes(h)]
        shifted[span, v_lanes(h)] = value_grad[c, h] * slope[span, v_lanes(h)]
    for c in range(chunks):
        mix_ref[c * CHUNK : (c + 1) * CHUNK, :] = jnp.concatenate(
            [beta_grad[c, h] for h in each]
            + [decay_grad[c, h] for h in each]
            + [jnp.zeros((CHUNK, mix_ref.shape[1] - 2 * heads), single)],
            axis=1,
        )
    shifted_start[0:STEP, :] = starts
    total = None
    for tap in range(taps):
        back = taps - 1 - tap
        term = shifted[back : back + STEP, :] * weight_ref[tap : tap + 1, :]
        if back:
            term = jnp.where(positions >= shifted_start[back : back + STEP, :], term, 0.0)
        total = term if total is None else total + term
    out_ref[...] = low(total)

    @pl.when(step == 0)
    def _():
        tail_ref[...] = total[STEP - HALO :, :]

    @pl.when(step == steps - 1)
    def _():
        window[0:8, :] = jnp.zeros((8, lanes), single)
        window[8:16, :] = shifted[0:8, :]
        early = lax.broadcasted_iota(jnp.int32, (8, 1), 0) - 8
        collected = jnp.zeros((8, lanes), single)
        for tap in range(taps - 1):
            back = taps - 1 - tap
            reader = early + back
            reader_start = jnp.zeros((8, 1), jnp.int32)
            for t in range(back):
                reader_start = jnp.where(reader == t, shifted_start[t : t + 1, :], reader_start)
            term = window[back : back + 8, :] * weight_ref[tap : tap + 1, :]
            collected = collected + jnp.where(
                (reader >= 0) & (early >= reader_start), term, 0.0
            )
        edge_ref[0:8, :] = jnp.zeros((8, lanes), single)
        edge_ref[8:16, :] = collected


def block_place(step, place, per_quarter):
    return ((step // per_quarter) ^ place[0]) * per_quarter + step % per_quarter


def run_forward(place, rows, halo, columns, weights, scalars, heads, key_width, value_width, quarter):
    count, lanes = columns.shape[0], rows.shape[1]
    steps, per_quarter = count // STEP, quarter // STEP
    wide = value_width + key_width
    chunks = STEP // CHUNK
    at = lambda i, place: (block_place(i, place, per_quarter), 0)
    fixed = lambda i, place: (0, 0)
    body = functools.partial(
        forward_kernel, heads=heads, key_width=key_width, value_width=value_width
    )
    shapes = (
        jax.ShapeDtypeStruct((count, heads * value_width), single),
        jax.ShapeDtypeStruct((count, heads * key_width), bfloat),
        jax.ShapeDtypeStruct((count, heads * wide), bfloat),
        jax.ShapeDtypeStruct((count // CHUNK, heads, key_width, wide), bfloat),
        jax.ShapeDtypeStruct((count, heads * CHUNK), bfloat),
        jax.ShapeDtypeStruct((heads, key_width, wide), single),
        jax.ShapeDtypeStruct((heads, key_width, wide), bfloat),
        jax.ShapeDtypeStruct((heads, key_width, value_width), bfloat),
    )
    return pl.pallas_call(
        body,
        out_shape=shapes,
        grid_spec=pltpu.PrefetchScalarGridSpec(
            num_scalar_prefetch=1,
            grid=(steps,),
            in_specs=[
                pl.BlockSpec((STEP, lanes), at),
                pl.BlockSpec((HALO, lanes), lambda i, place: (0, 0)),
                pl.BlockSpec((STEP, columns.shape[1]), at),
                pl.BlockSpec(weights.shape, fixed),
                pl.BlockSpec(memory_space=pltpu.SMEM),
            ],
            out_specs=[
                pl.BlockSpec((STEP, heads * value_width), at),
                pl.BlockSpec((STEP, heads * key_width), at),
                pl.BlockSpec((STEP, heads * wide), at),
                pl.BlockSpec((chunks, heads, key_width, wide), lambda i, place: (i, 0, 0, 0)),
                pl.BlockSpec((STEP, heads * CHUNK), at),
                pl.BlockSpec((heads, key_width, wide), lambda i, place: (0, 0, 0)),
                pl.BlockSpec((heads, key_width, wide), lambda i, place: (0, 0, 0)),
                pl.BlockSpec((heads, key_width, value_width), lambda i, place: (0, 0, 0)),
            ],
            scratch_shapes=[
                pltpu.VMEM((STEP + HALO, lanes), single),
                pltpu.VMEM((heads, key_width, wide), single),
            ],
        ),
        compiler_params=pltpu.CompilerParams(
            dimension_semantics=("arbitrary",), vmem_limit_bytes=VMEM_LIMIT
        ),
        cost_estimate=pl.CostEstimate(
            flops=count * 2_000_000, bytes_accessed=count * 10_000, transcendentals=count * 2000
        ),
        name="delta_forward",
    )(place, rows, halo, columns, weights, scalars)


def run_backward(
    place, rows, halo, columns, weights, scalars, grad, saved, entering, got, heads,
    key_width, value_width, quarter,
):
    written, states, inverses, end = saved
    count, lanes = columns.shape[0], rows.shape[1]
    steps, per_quarter = count // STEP, quarter // STEP
    wide = value_width + key_width
    chunks = STEP // CHUNK

    def at(i, place):
        return (block_place(steps - 1 - i, place, per_quarter), 0)

    def halo_at(i, place):
        here = steps - 1 - i
        inner = block_place(jnp.maximum(here - 1, 0), place, per_quarter)
        ratio = STEP // HALO
        return (inner * ratio + ratio - 1, 0)

    fixed = lambda i, place: (0, 0)
    whole = lambda i, place: (0, 0, 0)
    body = functools.partial(
        backward_kernel,
        hops=len(got),
        heads=heads,
        key_width=key_width,
        value_width=value_width,
    )
    shapes = (
        jax.ShapeDtypeStruct((count, lanes), bfloat),
        jax.ShapeDtypeStruct((count, columns.shape[1]), single),
        jax.ShapeDtypeStruct((HALO, lanes), single),
        jax.ShapeDtypeStruct((HALO, lanes), single),
    )
    return pl.pallas_call(
        body,
        out_shape=shapes,
        grid_spec=pltpu.PrefetchScalarGridSpec(
            num_scalar_prefetch=1,
            grid=(steps,),
            in_specs=[
                pl.BlockSpec((STEP, lanes), at),
                pl.BlockSpec((HALO, lanes), halo_at),
                pl.BlockSpec((HALO, lanes), fixed),
                pl.BlockSpec((STEP, columns.shape[1]), at),
                pl.BlockSpec(weights.shape, fixed),
                pl.BlockSpec(memory_space=pltpu.SMEM),
                pl.BlockSpec((STEP, heads * value_width), at),
                pl.BlockSpec((STEP, heads * wide), at),
                pl.BlockSpec(
                    (chunks, heads, key_width, wide), lambda i, place: (steps - 1 - i, 0, 0, 0)
                ),
                pl.BlockSpec((STEP, heads * CHUNK), at),
                pl.BlockSpec(end.shape, whole),
                pl.BlockSpec(entering.shape, whole),
            ]
            + [pl.BlockSpec(part.shape, whole) for part in got],
            out_specs=[
                pl.BlockSpec((STEP, lanes), at),
                pl.BlockSpec((STEP, columns.shape[1]), at),
                pl.BlockSpec((HALO, lanes), fixed),
                pl.BlockSpec((HALO, lanes), fixed),
            ],
            scratch_shapes=[
                pltpu.VMEM((STEP + HALO, lanes), single),
                pltpu.VMEM((STEP + 8, lanes), single),
                pltpu.VMEM((STEP + 8, 1), jnp.int32),
                pltpu.VMEM((heads, key_width, value_width), single),
                pltpu.VMEM((heads, key_width, value_width), single),
            ],
        ),
        compiler_params=pltpu.CompilerParams(
            dimension_semantics=("arbitrary",), vmem_limit_bytes=VMEM_LIMIT
        ),
        cost_estimate=pl.CostEstimate(
            flops=count * 3_000_000, bytes_accessed=count * 12_000, transcendentals=count * 3000
        ),
        name="delta_backward",
    )(
        place, rows, rows, halo, columns, weights, scalars, grad, written, states, inverses, end,
        entering, *got,
    )


def chosen_columns(table, column_sets):
    return column_sets[0:1, :] == table[:, 1:2]


def masked(product, chosen):
    return low(jnp.where(chosen, product, 0.0))


def silu_parts(value):
    logistic = sigmoid(value)
    return logistic, value * logistic


def accumulate(ref, value, first):
    if first is True:
        ref[...] = value
    else:
        ref[...] = jnp.where(first, value, ref[...] + value)


def emit_blocks(parts, place, own_ref, far_ref, pair_ref):
    for k, part in enumerate(parts):
        rows, size = part.shape[0], part.shape[1] // 4
        lanes = slice(k * size, (k + 1) * size)
        for relative, target, row in (
            (0, own_ref, 0), (2, far_ref, 0), (1, pair_ref, 0), (3, pair_ref, rows)
        ):
            start = pl.multiple_of((place ^ relative) * size, 128)
            target[row : row + rows, lanes] = low(part[:, pl.ds(start, size)])


def copy_rows(target, row, source, lanes=slice(None)):
    size = 64

    def run(index, _):
        start = pl.multiple_of(index * size, size)
        target[pl.ds(pl.multiple_of(row + start, size), size), lanes] = source[pl.ds(start, size), :]
        return 0

    lax.fori_loop(0, source.shape[0] // size, run, 0)


def at_end(fill):
    pl.when(pl.program_id(0) == pl.num_programs(0) - 1)(fill)


def at_start(fill):
    pl.when(pl.program_id(0) == 0)(fill)


def project_kernel(
    rows_ref, table_ref, sets_ref, down_ref, mix_ref, wq_ref, wk_ref, wv_ref, wg_ref, up_qk_ref,
    up_vg_ref, *rest, with_halo,
):
    low_rank = sets_ref.shape[1]
    width, q_width = wq_ref.shape
    v_width = wv_ref.shape[1]
    bounds = [0, q_width, 2 * q_width, 2 * q_width + v_width, 2 * q_width + 2 * v_width]
    if with_halo:
        halo_ref, halo_table_ref, *rest = rest
        pre_ref, inner_ref, column_ref, gate_ref, inner_gate_ref, pre_halo_ref, joined = rest
    else:
        pre_ref, inner_ref, column_ref, gate_ref, inner_gate_ref, joined = rest
    weights = (wq_ref, wk_ref, wv_ref, wg_ref)
    ups = (
        up_qk_ref.at[0],
        up_qk_ref.at[1],
        up_vg_ref.at[:low_rank],
        up_vg_ref.at[low_rank:],
    )

    @at_start
    def _():
        for p in range(4):
            columns = slice(bounds[p], bounds[p + 1])
            copy_rows(joined, 0, weights[p], columns)
            copy_rows(joined, width, ups[p], columns)

    rows, table = rows_ref[...], table_ref[...]
    count = rows.shape[0]
    if with_halo:
        rows = jnp.concatenate([rows, halo_ref[...]], axis=0)
        table = jnp.concatenate([table, halo_table_ref[...]], axis=0)
    chosen = chosen_columns(table, sets_ref[...])
    product = nt(rows, down_ref[...])
    inner = [masked(product[:, p * low_rank : (p + 1) * low_rank], chosen) for p in range(4)]
    for p in range(4):
        columns = slice(bounds[p], bounds[p + 1])
        output = nn(jnp.concatenate([rows, inner[p]], axis=1), joined[:, columns])
        if p == 3:
            gate_ref[...] = output[:count]
            inner_gate_ref[...] = inner[p][:count]
            continue
        pre_ref[:, columns] = low(output[:count])
        if with_halo:
            pre_halo_ref[:, columns] = low(output[count:])
        inner_ref[:, p * low_rank : (p + 1) * low_rank] = inner[p][:count]
    column_ref[...] = jnp.concatenate(
        [nt(rows[:count], mix_ref[...])[:, :4], table[:count, :4]], axis=1
    )


def head_outputs(raw_ref, map_ref, entering_ref, heads, key_width, value_width):
    outputs = []
    for h in range(heads):
        outputs.append(
            raw_ref[:, h * value_width : (h + 1) * value_width]
            + nn(map_ref[:, h * key_width : (h + 1) * key_width], entering_ref[h])
        )
    return outputs


def attend_kernel(
    raw_ref, map_ref, gate_ref, table_ref, gain_ref, sets_ref, wo_ref, down_ref, up_ref, *rest,
    heads, key_width, value_width, hops,
):
    got_refs, rest = rest[:hops], rest[hops:]
    part_ref, z_ref, inner_ref, entering_ref, joined = rest
    value_lanes = wo_ref.shape[0]

    @at_start
    def _():
        copy_rows(joined, 0, wo_ref)
        copy_rows(joined, value_lanes, up_ref)
        for h in range(heads):
            state = got_refs[hops - 1][h].astype(single)
            for hop in range(hops - 1, 0, -1):
                got = got_refs[hop - 1][h]
                state = got[:, :value_width].astype(single) + nn(got[:, value_width:], low(state))
            entering_ref[h] = low(state)

    chosen = chosen_columns(table_ref[...], sets_ref[...])
    outputs = head_outputs(raw_ref, map_ref, entering_ref, heads, key_width, value_width)
    parts = []
    for h, output in enumerate(outputs):
        lanes = slice(h * value_width, (h + 1) * value_width)
        scale = lax.rsqrt(jnp.mean(output * output, axis=-1, keepdims=True) + EPS)
        _, gate = silu_parts(gate_ref[:, lanes])
        parts.append(low(output * scale * gain_ref[0:1, :] * gate))
    z = jnp.concatenate(parts, axis=1)
    z_ref[...] = z
    inner = masked(nt(z, down_ref[...]), chosen)
    inner_ref[...] = inner
    part_ref[...] = low(nn(jnp.concatenate([z, inner], axis=1), joined[...]))


def feed_before_kernel(
    grad_ref, table_ref, sets_ref, wd_ref, down_ffd_t_ref, up_ref, hidden_grad_ref, du_ref, joined
):
    hidden, width = wd_ref.shape

    @at_start
    def _():
        copy_rows(joined, 0, wd_ref, slice(0, width))
        copy_rows(joined, 0, down_ffd_t_ref, slice(width, None))
        joined[hidden:, :] = jnp.zeros((joined.shape[0] - hidden, joined.shape[1]), bfloat)

    grad = grad_ref[...]
    du_down = masked(nt(grad, up_ref[...]), chosen_columns(table_ref[...], sets_ref[...]))
    du_ref[...] = du_down
    hidden_grad_ref[...] = nt(jnp.concatenate([grad, du_down], axis=1), joined[...])


def feed_kernel(
    rows_ref, hidden_grad_ref, table_ref, sets_ref, down_ref, wg_ref, wu_ref, up_t_ref, up_ref,
    back_ref, hidden_ref, ff_grad_ref, inner_ref, du_ref,
    joined_gate, joined_up, joined_back,
):
    low_rank = sets_ref.shape[1]
    hidden, width = wg_ref.shape
    padded = joined_gate.shape[0]

    @at_start
    def _():
        for p, (joined, weight) in enumerate(((joined_gate, wg_ref), (joined_up, wu_ref))):
            copy_rows(joined, 0, weight, slice(0, width))
            copy_rows(joined, 0, up_t_ref.at[p], slice(width, None))
            joined[hidden:, :] = jnp.zeros((padded - hidden, joined.shape[1]), bfloat)
            copy_rows(joined_back, p * padded, weight)
            joined_back[p * padded + hidden : (p + 1) * padded, :] = jnp.zeros(
                (padded - hidden, width), bfloat
            )
        copy_rows(joined_back, 2 * padded, down_ref)

    chosen = chosen_columns(table_ref[...], sets_ref[...])
    both = jnp.concatenate([chosen, chosen], axis=1)
    rows = rows_ref[...]
    inner = masked(nt(rows, down_ref[...]), both)
    inner_ref[...] = inner
    gate = nt(jnp.concatenate([rows, inner[:, :low_rank]], axis=1), joined_gate[...])
    up = nt(jnp.concatenate([rows, inner[:, low_rank:]], axis=1), joined_up[...])
    logistic, active = silu_parts(gate)
    hidden_ref[...] = low(active * up)
    hidden_grad = hidden_grad_ref[...]
    gate_grad = low(hidden_grad * up * logistic * (1.0 + gate * (1.0 - logistic)))
    up_grad = low(hidden_grad * active)
    du_gate = masked(nt(gate_grad, up_ref[0]), chosen)
    du_up = masked(nt(up_grad, up_ref[1]), chosen)
    du_ref[:, :low_rank] = du_gate
    du_ref[:, low_rank:] = du_up
    ff_grad_ref[:, :padded] = gate_grad
    ff_grad_ref[:, padded:] = up_grad
    back_ref[...] = low(
        nn(jnp.concatenate([gate_grad, up_grad, du_gate, du_up], axis=1), joined_back[...])
    )


def feed_after_kernel(
    rows_ref, grad_ref, hidden_ref, ff_grad_ref, inner_ref, du_ref, du_down_ref, table_ref,
    sets_ref, place_ref, wd_ref, down_ffd_ref, up_ref,
    out_ref, own_ref, far_ref, pair_ref, flat_ref,
    joined, down_sum, res_sum, flat_sum,
):
    first = pl.program_id(0) == 0
    low_rank = sets_ref.shape[1]
    width_hidden = wd_ref.shape[0]
    padded = down_ffd_ref.shape[1]

    @at_start
    def _():
        copy_rows(joined, 0, wd_ref)
        joined[width_hidden:padded, :] = jnp.zeros(
            (padded - width_hidden, joined.shape[1]), bfloat
        )
        copy_rows(joined, padded, up_ref)

    hidden = hidden_ref[...]
    inner = inner_ref[...]
    u_down = masked(
        nt(hidden, down_ffd_ref[...]), chosen_columns(table_ref[...], sets_ref[...])
    )
    out_ref[...] = low(nn(jnp.concatenate([hidden, u_down], axis=1), joined[...]))
    accumulate(down_sum, tn(du_ref[...], rows_ref[...]), first)
    accumulate(res_sum, tn(u_down, grad_ref[...]), first)
    for k, grown in enumerate(
        (
            tn(inner[:, :low_rank], ff_grad_ref[:, :padded]),
            tn(inner[:, low_rank:], ff_grad_ref[:, padded:]),
            tn(du_down_ref[...], hidden),
        )
    ):
        accumulate(flat_sum.at[:, k * padded : (k + 1) * padded], grown, first)

    @at_end
    def _():
        flat_ref[...] = low(flat_sum[...])
        emit_blocks(
            (down_sum.at[:low_rank], down_sum.at[low_rank:], res_sum),
            place_ref[0], own_ref, far_ref, pair_ref,
        )


def branch_kernel(
    branch_ref, raw_ref, map_ref, gate_ref, table_ref, entering_ref, gain_ref, sets_ref, wo_ref,
    down_out_t_ref, up_ref, up_gate_ref, *rest,
    heads, key_width, value_width, hops, last,
):
    if last:
        before_ref, *rest = rest
        got_refs, rest = rest[: hops - 1], rest[hops - 1 :]
        raw_grad_ref, gate_grad_ref, du_out_ref, du_gate_ref, *rest = rest
        sent_refs, (joined, total_ref) = rest[:hops], rest[hops:]
    else:
        raw_grad_ref, gate_grad_ref, du_out_ref, du_gate_ref, total_ref, joined = rest
    width = wo_ref.shape[1]

    @at_start
    def _():
        copy_rows(joined, 0, wo_ref, slice(0, width))
        copy_rows(joined, 0, down_out_t_ref, slice(width, None))

    chosen = chosen_columns(table_ref[...], sets_ref[...])
    branch = branch_ref[...]
    outputs = head_outputs(raw_ref, map_ref, entering_ref, heads, key_width, value_width)
    du_out = masked(nt(branch, up_ref[...]), chosen)
    du_out_ref[...] = du_out
    mixed_grad = nt(jnp.concatenate([branch, du_out], axis=1), joined[...])
    gain = gain_ref[0:1, :]
    gate_grads = []
    for h, output in enumerate(outputs):
        lanes = slice(h * value_width, (h + 1) * value_width)
        scale = lax.rsqrt(jnp.mean(output * output, axis=-1, keepdims=True) + EPS)
        value = gate_ref[:, lanes]
        logistic, active = silu_parts(value)
        incoming = mixed_grad[:, lanes]
        gate_grads.append(
            low(
                incoming
                * (output * scale * gain)
                * (logistic * (1.0 + value * (1.0 - logistic)))
            )
        )
        scaled = gain * (incoming * active)
        dot = jnp.mean(output * scaled, axis=-1, keepdims=True)
        raw_grad = low(scale * scaled - output * (scale * scale * scale * dot))
        raw_grad_ref[:, lanes] = raw_grad
        grown = tn(map_ref[:, h * key_width : (h + 1) * key_width], raw_grad)
        accumulate(total_ref.at[h], grown, pl.program_id(0) == 0)
    gate_grad = jnp.concatenate(gate_grads, axis=1)
    gate_grad_ref[...] = gate_grad
    du_gate_ref[...] = masked(nt(gate_grad, up_gate_ref[...]), chosen)
    if last:

        @at_end
        def _():
            for h in range(heads):
                passed = low(before_ref[h] + total_ref[h])
                sent_refs[0][h] = passed
                for hop in range(1, hops):
                    passed = low(tn(got_refs[hop - 1][h][:, value_width:], passed))
                    sent_refs[hop][h] = passed


def branch_after_kernel(
    branch_ref, z_ref, u_out_ref, rows_ref, inner_ref, du_out_ref, du_gate_ref, gate_grad_ref,
    down_grad_ref, res_grad_ref, flat_ref,
    flat_sum,
):
    lanes = z_ref.shape[1]
    accumulate(down_grad_ref, tn(du_gate_ref[...], rows_ref[...]), True)
    accumulate(res_grad_ref, tn(u_out_ref[...], branch_ref[...]), True)
    accumulate(flat_sum.at[:, :lanes], tn(du_out_ref[...], z_ref[...]), True)
    accumulate(flat_sum.at[:, lanes:], tn(inner_ref[...], gate_grad_ref[...]), True)

    @at_end
    def _():
        flat_ref[...] = low(flat_sum[...])


def settled_rows(pre_ref, tail_ref, arrived_ref, place_ref, quarter, window):
    block = window.shape[0]
    start = ((3 ^ place_ref[0]) + 1) * quarter - HALO - pl.program_id(0) * block
    window[...] = pre_ref[...]

    @pl.when((start >= 0) & (start < block))
    def _():
        window[pl.ds(pl.multiple_of(start, HALO), HALO), :] = low(tail_ref[...] + arrived_ref[...])

    return window[...]


def settle_grads_kernel(
    pre_ref, rows_ref, inner_ref, table_ref, tail_ref, arrived_ref, place_ref, sets_ref,
    up_qk_ref, up_value_ref, down_late_ref, res_late_ref,
    du_ref, own_ref, far_ref, pair_ref, flat_ref,
    window, down_sum, flat_sum,
    *, quarter,
):
    first = pl.program_id(0) == 0
    low_rank = sets_ref.shape[1]
    q_width = up_qk_ref.shape[2]
    chosen = chosen_columns(table_ref[...], sets_ref[...])
    pre = settled_rows(pre_ref, tail_ref, arrived_ref, place_ref, quarter, window)
    query, key, value = pre[:, :q_width], pre[:, q_width : 2 * q_width], pre[:, 2 * q_width :]
    inner = inner_ref[...]
    du = jnp.concatenate(
        [
            masked(nt(query, up_qk_ref[0]), chosen),
            masked(nt(key, up_qk_ref[1]), chosen),
            masked(nt(value, up_value_ref[...]), chosen),
        ],
        axis=1,
    )
    du_ref[...] = du
    accumulate(down_sum, tn(du, rows_ref[...]), first)
    at = 0
    for p, part in enumerate((query, key, value)):
        accumulate(
            flat_sum.at[:, at : at + part.shape[1]],
            tn(inner[:, p * low_rank : (p + 1) * low_rank], part),
            first,
        )
        at += part.shape[1]

    @at_end
    def _():
        flat_ref[...] = low(flat_sum[...])
        emit_blocks(
            [down_sum.at[p * low_rank : (p + 1) * low_rank] for p in range(3)]
            + [down_late_ref, res_late_ref],
            place_ref[0], own_ref, far_ref, pair_ref,
        )


def settle_kernel(
    pre_ref, gate_grad_ref, du_ref, du_gate_ref, mix_ref, tail_ref, arrived_ref, place_ref,
    down_ref, mix_weight_ref, wq_ref, wk_ref, wv_ref, wg_ref,
    part_ref,
    window, joined, joined_small,
    *, quarter,
):
    q_width, v_width = wq_ref.shape[1], wv_ref.shape[1]

    @at_start
    def _():
        at = 0
        for weight in (wq_ref, wk_ref, wv_ref, wg_ref):
            copy_rows(joined, 0, weight, slice(at, at + weight.shape[1]))
            at += weight.shape[1]
        maps, mixes = down_ref.shape[0], mix_weight_ref.shape[0]
        spare = joined_small.shape[0] - maps - mixes
        copy_rows(joined_small, 0, down_ref)
        joined_small[maps:, :] = jnp.concatenate(
            [mix_weight_ref[...], jnp.zeros((spare, joined_small.shape[1]), bfloat)], axis=0
        )

    pre = settled_rows(pre_ref, tail_ref, arrived_ref, place_ref, quarter, window)
    mix = low(mix_ref[...])
    spare = joined_small.shape[0] - down_ref.shape[0] - mix.shape[1]
    small = jnp.concatenate(
        [du_ref[...], du_gate_ref[...], mix, jnp.zeros((mix.shape[0], spare), bfloat)], axis=1
    )
    part_ref[...] = low(
        nt(jnp.concatenate([pre, gate_grad_ref[...]], axis=1), joined[...])
        + nn(small, joined_small[...])
    )


def assemble_kernel(
    place_ref, *refs, padded,
):
    pieces_last, pieces_feed = refs[:4], refs[4:8]
    last_ref, feed_ref, branch_ref = refs[8:11]
    down_ref, qk_ref, vg_ref, ff_ref, out_ref, ffd_ref, res_ref = refs[11:]
    place = place_ref[0]
    size = pieces_last[0].shape[1] // 5
    first = [down_ref.at[p] for p in range(4)] + [res_ref.at[0]]
    second = [down_ref.at[4], down_ref.at[5], res_ref.at[1]]
    for relative in range(4):
        start = pl.multiple_of((place ^ relative) * size, 128)
        for targets, piece in ((first, pieces_last[relative]), (second, pieces_feed[relative])):
            for k, target in enumerate(targets):
                target[:, pl.ds(start, size)] = piece[:, k * size : (k + 1) * size].astype(single)
    qk, values, hidden = qk_ref.shape[2], vg_ref.shape[2], ff_ref.shape[2]

    def lanes(ref, start, width):
        return ref[:, start : start + width].astype(single)

    own = 5 * size
    qk_ref[0], qk_ref[1] = lanes(last_ref, own, qk), lanes(last_ref, own + qk, qk)
    vg_ref[0] = lanes(last_ref, own + 2 * qk, values)
    at = last_ref.shape[1] + 3 * size
    out_ref[...] = lanes(branch_ref, at, values)
    vg_ref[1] = lanes(branch_ref, at + values, values)
    ff_ref[0] = lanes(feed_ref, 0, hidden)
    ff_ref[1] = lanes(feed_ref, padded, hidden)
    ffd_ref[...] = lanes(feed_ref, 2 * padded, hidden)


def assemble(where, shared, last, feed, branch, padded, shapes):
    rows = last.shape[0]
    block = min(32, rows)

    def spec(shape):
        if len(shape) == 2:
            return pl.BlockSpec((block, shape[1]), lambda i: (i, 0))
        return pl.BlockSpec((shape[0], block, shape[2]), lambda i: (0, i, 0))

    arrays = [*shared, last, feed, branch]
    return pl.pallas_call(
        functools.partial(assemble_kernel, padded=padded),
        out_shape=tuple(jax.ShapeDtypeStruct(shape, single) for shape in shapes),
        grid=(rows // block,),
        in_specs=[pl.BlockSpec(memory_space=pltpu.SMEM)] + [spec(a.shape) for a in arrays],
        out_specs=[spec(shape) for shape in shapes],
        compiler_params=pltpu.CompilerParams(
            dimension_semantics=("arbitrary",), vmem_limit_bytes=VMEM_LIMIT
        ),
        name="assemble",
    )(where, *arrays)


WHOLE, SCALAR = "whole", "scalar"


def by_rows(width, lane_block=0):
    return ("rows", width, lane_block)


def part(rows, index):
    return ("part", rows, index)


def pieces(width):
    return ("pieces", width)


def blocked_call(
    body, name, count, inputs, outputs, scratch, flops, block=STEP, half=None, into=()
):
    count_pieces = 4 if half is None else 2
    steps = count * count_pieces // 4 // block
    offset = (half or 0) * steps
    per = max(steps // count_pieces, 1)
    in_specs, arrays, moved, groups_in, extra = [], [], 0, [], []
    for array, kind in inputs:
        members = array if isinstance(array, (list, tuple)) else [array]
        groups_in.append(len(members))
        arrays += members
        moved += sum(a.size * a.dtype.itemsize for a in members)
        if kind == WHOLE:
            zeros = (0,) * array.ndim
            in_specs.append(
                pl.BlockSpec(
                    array.shape, lambda i, zeros=zeros: zeros, pipeline_mode=pl.Buffered(1)
                )
            )
        elif kind == SCALAR:
            in_specs.append(pl.BlockSpec(memory_space=pltpu.SMEM))
        elif kind[0] == "part":
            in_specs.append(
                pl.BlockSpec(
                    (kind[1], array.shape[1]),
                    lambda i, at=kind[2]: (at, 0),
                    pipeline_mode=pl.Buffered(1),
                )
            )
        elif kind[0] == "rows":
            in_specs.append(
                pl.BlockSpec((block, kind[1]), lambda i, lane=kind[2]: (i + offset, lane))
            )
        else:
            for b, member in enumerate(members):
                if steps == 1:
                    in_specs.append(pl.BlockSpec(member.shape, lambda i: (0, 0)))
                else:
                    in_specs.append(
                        pl.BlockSpec(
                            (block, kind[1]),
                            lambda i, b=b: (jnp.clip(i - b * per, 0, per - 1), 0),
                        )
                    )
            extra.append(pltpu.VMEM((block, kind[1]), members[0].dtype))
    out_specs, shapes, groups_out, aliases = [], [], [], {}
    into = list(into)
    held_arrays = []
    for shape, dtype, kind in outputs:
        if kind == "parts":
            quarter = shape[0] // 4
            spec = (block, shape[1])
            if half is not None:
                for b in range(2):
                    shapes.append(jax.ShapeDtypeStruct((quarter, shape[1]), dtype))
                    out_specs.append(
                        pl.BlockSpec(spec, lambda i, b=b: (jnp.clip(i - b * per, 0, per - 1), 0))
                    )
                groups_out.append(2)
            else:
                for rows in (quarter, quarter, 2 * quarter):
                    shapes.append(jax.ShapeDtypeStruct((rows, shape[1]), dtype))
                out_specs += [
                    pl.BlockSpec(spec, lambda i: (jnp.clip(i, 0, per - 1), 0)),
                    pl.BlockSpec(spec, lambda i: (jnp.clip(i - 2 * per, 0, per - 1), 0)),
                    pl.BlockSpec(
                        spec,
                        lambda i: (
                            jnp.clip(i - per, 0, per - 1) + jnp.clip(i - 3 * per + 1, 0, per), 0
                        ),
                    ),
                ]
                groups_out.append(3)
            extra.append(pltpu.VMEM(spec, dtype))
        else:
            groups_out.append(1)
            shapes.append(jax.ShapeDtypeStruct(shape, dtype))
            if kind == "rows":
                if into:
                    aliases[len(arrays) + len(held_arrays)] = len(shapes) - 1
                    held_arrays.append(into.pop(0))
                out_specs.append(pl.BlockSpec((block, shape[1]), lambda i: (i + offset, 0)))
            else:
                zeros = (0,) * len(shape)
                out_specs.append(pl.BlockSpec(shape, lambda i, zeros=zeros: zeros))
    in_specs += [pl.BlockSpec(memory_space=pl.ANY) for _ in held_arrays]

    def wrapped(*refs):
        refs = list(refs)
        spare = refs[len(in_specs) + len(out_specs) + len(scratch) :]
        own_scratch = refs[len(in_specs) + len(out_specs) : len(refs) - len(spare)]
        quarter = pl.program_id(0) // per
        given, later, at, used = [], [], 0, 0
        for size, (_, kind) in zip(groups_in, inputs):
            if kind[0] != "pieces":
                given.append(refs[at])
            else:
                held = spare[used]
                used += 1
                if steps == 1:
                    for b in range(size):
                        piece = refs[at + b]
                        held[b * piece.shape[0] : (b + 1) * piece.shape[0], :] = piece[...]
                else:
                    for b in range(size):

                        @pl.when(quarter == b)
                        def _(held=held, source=refs[at + b]):
                            copy_rows(held, 0, source)

                given.append(held)
            at += size
        at += len(held_arrays)
        for size in groups_out:
            if size == 1:
                given.append(refs[at])
            else:
                given.append(spare[used])
                later.append((spare[used], refs[at : at + size]))
                used += 1
            at += size
        body(*given, *own_scratch)
        for held, targets in later:
            if len(targets) == 2:
                placed = ((0, targets[0]), (1, targets[1]))
            else:
                placed = ((0, targets[0]), (2, targets[1]), (1, targets[2]), (3, targets[2]))
            for b, target in placed:

                @pl.when(quarter == b)
                def _(held=held, target=target):
                    copy_rows(target, 0, held)

    results = pl.pallas_call(
        wrapped,
        out_shape=tuple(shapes),
        grid=(steps,),
        in_specs=in_specs,
        out_specs=out_specs,
        scratch_shapes=list(scratch) + extra,
        input_output_aliases=aliases,
        compiler_params=pltpu.CompilerParams(
            dimension_semantics=("arbitrary",), vmem_limit_bytes=VMEM_LIMIT
        ),
        cost_estimate=pl.CostEstimate(flops=flops, bytes_accessed=moved, transcendentals=0),
        name=name,
    )(*arrays, *held_arrays)
    grouped, at = [], 0
    for size in groups_out:
        grouped.append(results[at] if size == 1 else results[at : at + size])
        at += size
    return grouped


def flip(array, bit):
    groups = lax.axis_size("head")
    return lax.ppermute(array, "head", [(i, i ^ bit) for i in range(groups)])


def gather_rows(array):
    far = flip(array, 2)
    near = flip(array, 1)
    return [array, near, far, flip(far, 1)]


def tie(*arrays):
    return lax.optimization_barrier(arrays)


def near_sum(parts):
    own, far, pair = parts
    size = own.shape[0]
    arrived = flip(pair, 1)
    return (
        own.astype(single) + arrived[:size].astype(single),
        low(far.astype(single) + arrived[size:].astype(single)),
    )


def halves_sum(first, second):
    near, corner = tie(flip(first[1], 1), second[1])
    return (
        first[0].astype(single) + near.astype(single),
        low(second[0].astype(single) + flip(corner, 1).astype(single)),
    )


def far_sum(own, far):
    return own + flip(far, 2).astype(single)


def shifted_along(array, axis, by):
    length = lax.axis_size(axis)
    pairs = [(i, i + by) for i in range(length) if 0 <= i + by < length]
    return lax.ppermute(array, axis, pairs)


def seq_rows(flat):
    members = lax.axis_size("seq")
    return flat.reshape(members, flat.shape[0] // members, flat.shape[1])


def share_sum(parts):
    summed = low(jnp.sum(parts.astype(single), axis=0))
    return jnp.broadcast_to(summed[None], parts.shape)


def exchange(parts):
    return lax.all_to_all(parts, "seq", 0, 0)


def all_rows(parts):
    return parts.reshape(-1, parts.shape[-1])


def rms_scale(rows, gain):
    return rows * lax.rsqrt(jnp.mean(rows * rows, axis=-1, keepdims=True) + EPS) * gain


def rms_back(rows, gain, incoming):
    _, back = jax.vjp(lambda value: rms_scale(value, gain), rows)
    return back(incoming)[0]


def on_device(
    block_input,
    out_grad,
    lengths,
    doc_sets,
    norm1_gain,
    w_query,
    w_key,
    w_value,
    conv_query,
    conv_key,
    conv_value,
    w_decay_beta,
    decay_rate,
    decay_bias,
    w_gate_out,
    out_gain,
    w_out,
    norm2_gain,
    w_gate,
    w_up,
    w_down,
    adapt_down,
    adapt_up_qk,
    adapt_up_vg,
    adapt_up_ff,
    adapt_down_out,
    adapt_down_ffd,
    adapt_up_res,
):
    groups = lax.axis_size("head")
    members = lax.axis_size("seq")
    place = lax.axis_index("head")
    quarter, width = block_input.shape
    count = quarter * groups
    heads = decay_rate.shape[0]
    key_width = w_query.shape[1] // heads
    value_width = w_value.shape[1] // heads
    sets, rank = adapt_down.shape[1], adapt_down.shape[3]
    low_rank = sets * rank
    qk = heads * key_width
    device_start = lax.axis_index("seq") * count
    starts = jnp.sum(
        jnp.where(
            jnp.arange(lengths.shape[0])[None, :] < jnp.arange(lengths.shape[0])[:, None],
            lengths[None, :],
            0,
        ),
        axis=1,
    )
    order = jnp.arange(groups, dtype=jnp.int32) ^ place

    def tables(positions):
        reached = positions[:, None] >= starts[None, :]
        token_start = jnp.max(jnp.where(reached, starts[None, :], -1), axis=1)
        ended = positions[:, None] >= (starts + lengths)[None, :]
        token_set = jnp.sum(jnp.where(reached & ~ended, doc_sets[None, :], 0), axis=1)
        pair = jnp.stack([token_start - device_start, token_set], axis=1).astype(single)
        return jnp.pad(pair, ((0, 0), (0, 8 - pair.shape[1])))

    table = tables(
        (
            device_start + order[:, None] * quarter + jnp.arange(quarter, dtype=jnp.int32)[None, :]
        ).reshape(-1)
    )
    halo_table = tables(device_start + jnp.arange(-HALO, 0, dtype=jnp.int32))
    column_sets = jnp.broadcast_to(
        (jnp.arange(low_rank, dtype=jnp.int32) // rank).astype(single)[None, :], (8, low_rank)
    )

    down = adapt_down.transpose(0, 1, 3, 2).reshape(6 * low_rank, width)
    up_qk = adapt_up_qk.reshape(2, low_rank, -1)
    up_vg = adapt_up_vg.reshape(2 * low_rank, -1)
    up_ff = adapt_up_ff.reshape(2, low_rank, -1)
    down_out = adapt_down_out.transpose(0, 2, 1).reshape(low_rank, -1)
    down_ffd = adapt_down_ffd.transpose(0, 2, 1).reshape(low_rank, -1)
    up_res = adapt_up_res.reshape(2 * low_rank, width)
    conv = jnp.concatenate([conv_query, conv_key, conv_value], axis=1).astype(single)
    scalars = jnp.stack([decay_rate, decay_bias])
    where = place.reshape(1).astype(jnp.int32)
    weight_mix = jnp.pad(
        w_decay_beta.transpose(1, 2, 0).reshape(2 * heads, width), ((0, 8 - 2 * heads), (0, 0))
    )
    gain = jnp.broadcast_to(out_gain[None, :], (8, value_width))
    hidden_width = w_down.shape[0]
    padded = -(-hidden_width // 256) * 256
    value_lanes = heads * value_width
    block_width = width // groups
    widen = lambda a: jnp.pad(a, [(0, 0)] * (a.ndim - 1) + [(0, padded - hidden_width)])

    input_float = block_input.astype(single)
    normed = low(rms_scale(input_float, norm1_gain))
    tail = normed[quarter - HALO :]
    halo = sum(
        lax.ppermute(
            tail,
            ("seq", "head"),
            [((s * groups) + groups - 1, (s + 1) * groups + h) for s in range(members - 1)],
        )
        for h in range(groups)
    )
    normed_near, normed_far = flip(normed, 1), flip(normed, 2)
    project_inputs = [
        (table, by_rows(8)),
        (column_sets, WHOLE),
        (down, part(4 * low_rank, 0)),
        (weight_mix, WHOLE),
        (w_query, WHOLE),
        (w_key, WHOLE),
        (w_value, WHOLE),
        (w_gate_out, WHOLE),
        (up_qk, WHOLE),
        (up_vg, WHOLE),
    ]
    project_outputs = [
        ((count, 2 * qk + value_lanes), bfloat, "rows"),
        ((count, 3 * low_rank), bfloat, "rows"),
        ((count, 8), single, "rows"),
        ((count, value_lanes), single, "rows"),
        ((count, low_rank), bfloat, "rows"),
    ]
    project_scratch = [pltpu.VMEM((width + low_rank, 2 * qk + 2 * value_lanes), bfloat)]
    projected = blocked_call(
        functools.partial(project_kernel, with_halo=False),
        "project_near",
        count,
        [([normed, normed_near], pieces(width)), *project_inputs],
        project_outputs,
        project_scratch,
        count * 2_000_000,
        half=0,
    )
    normed_far, projected[2] = tie(normed_far, projected[2])
    normed_all = [normed, normed_near, normed_far, flip(normed_far, 1)]
    pre, inner, columns, gate_input, inner_gate, pre_halo = blocked_call(
        functools.partial(project_kernel, with_halo=True),
        "project_far",
        count,
        [
            (normed_all[2:], pieces(width)),
            *project_inputs,
            (halo, WHOLE),
            (halo_table, WHOLE),
        ],
        project_outputs + [((HALO, 2 * qk + value_lanes), bfloat, "whole")],
        project_scratch,
        count * 2_000_000,
        half=1,
        into=projected,
    )
    out_grad_late, grad_near, pre = tie(out_grad, flip(out_grad, 1), pre)
    grad_far, grad_corner = flip(out_grad_late, 2), flip(grad_near, 2)
    raw_local, mapped, *saved, sent, sent_state = run_forward(
        where, pre, pre_halo, columns, conv, scalars, heads, key_width, value_width, quarter
    )

    hops = min(members - 1, -(-(DOC_MAX - 1) // count))
    got = [shifted_along(sent_state, "seq", hops)]
    got = [shifted_along(sent, "seq", hop) for hop in range(hops - 1, 0, -1)][::-1] + got
    grad_far, grad_corner, sent_state = tie(grad_far, grad_corner, sent_state)
    grad_all = [out_grad, grad_near, grad_far, grad_corner]
    hidden_grad, du_down = blocked_call(
        feed_before_kernel,
        "feed_before",
        count,
        [
            (grad_all, pieces(width)),
            (table, by_rows(8)),
            (column_sets, WHOLE),
            (w_down, WHOLE),
            (down_ffd.T, WHOLE),
            (up_res, part(low_rank, 1)),
        ],
        [((count, padded), single, "rows"), ((count, low_rank), bfloat, "rows")],
        [pltpu.VMEM((padded, width + low_rank), bfloat)],
        count * 6_000_000,
    )
    raw_local, hidden_grad = tie(raw_local, hidden_grad)

    sizes = dict(heads=heads, key_width=key_width, value_width=value_width)
    attention_part, mixed, u_out, entering = blocked_call(
        functools.partial(attend_kernel, hops=hops, **sizes),
        "attend",
        count,
        [
            (raw_local, by_rows(value_lanes)),
            (mapped, by_rows(qk)),
            (gate_input, by_rows(value_lanes)),
            (table, by_rows(8)),
            (gain, WHOLE),
            (column_sets, WHOLE),
            (w_out, WHOLE),
            (down_out, WHOLE),
            (up_res, part(low_rank, 0)),
        ]
        + [(sent_by, WHOLE) for sent_by in got],
        [
            ((count, width), bfloat, "parts"),
            ((count, value_lanes), bfloat, "rows"),
            ((count, low_rank), bfloat, "rows"),
            ((heads, key_width, value_width), bfloat, "whole"),
        ],
        [pltpu.VMEM((value_lanes + low_rank, width), bfloat)],
        count * 5_000_000,
    )
    attention_own, attention_far = near_sum(attention_part)
    attention_arrived, up_ff_t, up_ff_padded, down_ffd_padded, down_out_t = tie(
        flip(attention_far, 2),
        up_ff.transpose(0, 2, 1),
        widen(up_ff),
        widen(down_ffd),
        down_out.T,
    )
    residual = input_float + (attention_own + attention_arrived.astype(single))
    normed_mid = low(rms_scale(residual, norm2_gain))
    mid_near, mid_far = flip(normed_mid, 1), flip(normed_mid, 2)

    feed_inputs = [
        (hidden_grad, by_rows(padded)),
        (table, by_rows(8)),
        (column_sets, WHOLE),
        (down, part(2 * low_rank, 2)),
        (w_gate.T, WHOLE),
        (w_up.T, WHOLE),
        (up_ff_t, WHOLE),
        (up_ff_padded, WHOLE),
    ]
    feed_outputs = [
        ((count, width), bfloat, "parts"),
        ((count, padded), bfloat, "rows"),
        ((count, 2 * padded), bfloat, "rows"),
        ((count, 2 * low_rank), bfloat, "rows"),
        ((count, 2 * low_rank), bfloat, "rows"),
    ]
    feed_scratch = [
        pltpu.VMEM((padded, width + low_rank), bfloat),
        pltpu.VMEM((padded, width + low_rank), bfloat),
        pltpu.VMEM((2 * padded + 2 * low_rank, width), bfloat),
    ]
    near_part, *fed = blocked_call(
        feed_kernel,
        "feed_near",
        count,
        [([normed_mid, mid_near], pieces(width)), *feed_inputs],
        feed_outputs,
        feed_scratch,
        count * 8_000_000,
        half=0,
    )
    mid_far, near_own = tie(mid_far, near_part[0])
    near_part = [near_own, near_part[1]]
    mid_all = [normed_mid, mid_near, mid_far, flip(mid_far, 1)]
    far_part, hidden, ff_grad, u_ff, du_ff = blocked_call(
        feed_kernel,
        "feed_far",
        count,
        [(mid_all[2:], pieces(width)), *feed_inputs],
        feed_outputs,
        feed_scratch,
        count * 8_000_000,
        half=1,
        into=fed,
    )
    grad_own, grad_sum = halves_sum(near_part, far_part)
    grad_sum, hidden = tie(grad_sum, hidden)
    grad_arrived = flip(grad_sum, 2)
    out_part, feed_own, feed_far, feed_pair, feed_owned = blocked_call(
        feed_after_kernel,
        "feed_after",
        count,
        [
            (mid_all, pieces(width)),
            (grad_all, pieces(width)),
            (hidden, by_rows(padded)),
            (ff_grad, by_rows(2 * padded)),
            (u_ff, by_rows(2 * low_rank)),
            (du_ff, by_rows(2 * low_rank)),
            (du_down, by_rows(low_rank)),
            (table, by_rows(8)),
            (column_sets, WHOLE),
            (where, SCALAR),
            (w_down, WHOLE),
            (down_ffd_padded, WHOLE),
            (up_res, part(low_rank, 1)),
        ],
        [
            ((count, width), bfloat, "parts"),
            ((low_rank, 3 * block_width), bfloat, "whole"),
            ((low_rank, 3 * block_width), bfloat, "whole"),
            ((2 * low_rank, 3 * block_width), bfloat, "whole"),
            ((low_rank, 3 * padded), bfloat, "whole"),
        ],
        [
            pltpu.VMEM((padded + low_rank, width), bfloat),
            pltpu.VMEM((2 * low_rank, width), single),
            pltpu.VMEM((low_rank, width), single),
            pltpu.VMEM((low_rank, 3 * padded), single),
        ],
        count * 16_000_000,
    )
    grad_landed, feed_far = tie(grad_arrived, feed_far)
    mid_grad = grad_own + grad_landed.astype(single)
    residual_grad = out_grad.astype(single) + rms_back(residual, norm2_gain, mid_grad)
    branch_low = low(residual_grad)
    branch_near, branch_far = flip(branch_low, 1), flip(branch_low, 2)
    out_own, out_far = near_sum(out_part)
    owned_parts = exchange(seq_rows(tie(feed_owned, branch_near)[0]))
    feed_sum, feed_sum_far = near_sum((feed_own, feed_far, tie(feed_pair, grad_arrived)[0]))
    feed_landed = flip(feed_sum_far, 2)

    branch_inputs = [
        (raw_local, by_rows(value_lanes)),
        (mapped, by_rows(qk)),
        (gate_input, by_rows(value_lanes)),
        (table, by_rows(8)),
        (entering, WHOLE),
        (gain, WHOLE),
        (column_sets, WHOLE),
        (w_out, WHOLE),
        (down_out_t, WHOLE),
        (up_res, part(low_rank, 0)),
        (up_vg, part(low_rank, 1)),
    ]
    branch_outputs = [
        ((count, value_lanes), bfloat, "rows"),
        ((count, value_lanes), bfloat, "rows"),
        ((count, low_rank), bfloat, "rows"),
        ((count, low_rank), bfloat, "rows"),
    ]
    branch_scratch = [pltpu.VMEM((value_lanes, width + low_rank), bfloat)]
    state_shape = (heads, key_width, value_width)
    *branched, state_near = blocked_call(
        functools.partial(branch_kernel, hops=hops, last=False, **sizes),
        "branch_near",
        count,
        [([branch_low, branch_near], pieces(width)), *branch_inputs],
        branch_outputs + [(state_shape, single, "whole")],
        branch_scratch,
        count * 12_000_000,
        half=0,
    )
    branch_far, state_near = tie(branch_far, state_near)
    branch_corner, owned_parts, out_far = tie(flip(branch_far, 1), owned_parts, out_far)
    branch_all = [branch_low, branch_near, branch_far, branch_corner]
    raw_grad, gate_grad, du_out, du_outgate, *state_grads = blocked_call(
        functools.partial(branch_kernel, hops=hops, last=True, **sizes),
        "branch_far",
        count,
        [(branch_all[2:], pieces(width)), *branch_inputs, (state_near, WHOLE)]
        + [(sent_by, WHOLE) for sent_by in got[:-1]],
        branch_outputs + [(state_shape, bfloat, "whole")] * hops,
        branch_scratch + [pltpu.VMEM(state_shape, single)],
        count * 4_000_000,
        half=1,
        into=branched,
    )
    state_got = [
        shifted_along(state_grads[hop - 1], "seq", -hop) for hop in range(hops, 0, -1)
    ][::-1]
    mixer_down_late, branch_res_grad, branch_flat = blocked_call(
        branch_after_kernel,
        "branch_after",
        count,
        [
            (branch_all, pieces(width)),
            (mixed, by_rows(value_lanes)),
            (u_out, by_rows(low_rank)),
            (normed_all, pieces(width)),
            (inner_gate, by_rows(low_rank)),
            (du_out, by_rows(low_rank)),
            (du_outgate, by_rows(low_rank)),
            (gate_grad, by_rows(value_lanes)),
        ],
        [
            ((low_rank, width), single, "whole"),
            ((low_rank, width), single, "whole"),
            ((low_rank, 2 * value_lanes), bfloat, "whole"),
        ],
        [pltpu.VMEM((low_rank, 2 * value_lanes), single)],
        count * 20_000_000,
        block=count,
    )
    feed_landed, du_out = tie(feed_landed, du_out)
    feed_shared = low(feed_sum + feed_landed.astype(single))
    owned_lanes = owned_parts.shape[-1]
    both = jnp.concatenate(
        [share_sum(owned_parts), seq_rows(feed_shared), seq_rows(branch_flat)], axis=2
    )
    raw_grad, both, out_far, *state_got = tie(raw_grad, both, out_far, *state_got)
    out_arrived = flip(out_far, 2)
    both = exchange(both)

    pre_grad, mix_grad, tail_grad, edge_grad = run_backward(
        where, pre, pre_halo, columns, conv, scalars, raw_grad, saved, entering, state_got,
        heads, key_width, value_width, quarter,
    )
    arrived = shifted_along(edge_grad, "seq", -1)
    arrived, both, out_arrived = tie(arrived, both, out_arrived)
    result = residual + (out_own + out_arrived.astype(single))
    later_parts = both[:, :, owned_lanes:]
    settled = [
        (pre_grad, by_rows(2 * qk + value_lanes)),
        (tail_grad, WHOLE),
        (arrived, WHOLE),
        (where, SCALAR),
    ]
    du_mix, last_own, last_far, last_pair, last_owned = blocked_call(
        functools.partial(settle_grads_kernel, quarter=quarter),
        "settle_grads",
        count,
        [
            settled[0],
            (normed_all, pieces(width)),
            (inner, by_rows(3 * low_rank)),
            (table, by_rows(8)),
            *settled[1:],
            (column_sets, WHOLE),
            (up_qk, WHOLE),
            (up_vg, part(low_rank, 0)),
            (mixer_down_late, WHOLE),
            (branch_res_grad, WHOLE),
        ],
        [
            ((count, 3 * low_rank), bfloat, "rows"),
            ((low_rank, 5 * block_width), bfloat, "whole"),
            ((low_rank, 5 * block_width), bfloat, "whole"),
            ((2 * low_rank, 5 * block_width), bfloat, "whole"),
            ((low_rank, 2 * qk + value_lanes), bfloat, "whole"),
        ],
        [
            pltpu.VMEM((STEP, 2 * qk + value_lanes), bfloat),
            pltpu.VMEM((3 * low_rank, width), single),
            pltpu.VMEM((low_rank, 2 * qk + value_lanes), single),
        ],
        count * 4_000_000,
    )
    last_own, last_far = near_sum((last_own, last_far, last_pair))
    last_far, gate_grad = tie(last_far, gate_grad)
    (normed_part,) = blocked_call(
        functools.partial(settle_kernel, quarter=quarter),
        "settle",
        count,
        [
            settled[0],
            (gate_grad, by_rows(value_lanes)),
            (du_mix, by_rows(3 * low_rank)),
            (du_outgate, by_rows(low_rank)),
            (mix_grad, by_rows(8)),
            *settled[1:],
            (down, part(4 * low_rank, 0)),
            (weight_mix, WHOLE),
            (w_query, WHOLE),
            (w_key, WHOLE),
            (w_value, WHOLE),
            (w_gate_out, WHOLE),
        ],
        [((count, width), bfloat, "parts")],
        [
            pltpu.VMEM((STEP, 2 * qk + value_lanes), bfloat),
            pltpu.VMEM((width, 2 * qk + 2 * value_lanes), bfloat),
            pltpu.VMEM((5 * low_rank, width), bfloat),
        ],
        count * 10_000_000,
    )
    last_flat = jnp.concatenate([low(far_sum(last_own, last_far)), last_owned], axis=1)
    feed_rows = all_rows(both)
    last_lanes = last_flat.shape[1]
    both = exchange(jnp.concatenate([seq_rows(last_flat), share_sum(later_parts)], axis=2))
    normed_own, normed_sum_far = near_sum(normed_part)
    both, normed_sum_far = tie(both, normed_sum_far)
    normed_landed = flip(normed_sum_far, 2)
    branch_rows = all_rows(both)
    feed_piece = branch_rows[:, last_lanes : last_lanes + 3 * block_width]
    feed_piece_far = flip(feed_piece, 2)
    last_parts = both[:, :, :last_lanes]
    last_rows = all_rows(exchange(share_sum(last_parts)))
    piece = last_rows[:, : 5 * block_width]
    piece_far = flip(piece, 2)
    normed_landed, feed_piece_far, _ = tie(normed_landed, feed_piece_far, piece)
    feed_pieces = [feed_piece, flip(feed_piece, 1), feed_piece_far, flip(feed_piece_far, 1)]
    normed_grad = normed_own + normed_landed.astype(single)
    input_grad = residual_grad + rms_back(input_float, norm1_gain, normed_grad)
    piece_far, input_grad, feed_pieces[3] = tie(piece_far, input_grad, feed_pieces[3])
    last_pieces = [piece, flip(piece, 1), piece_far, flip(piece_far, 1)]
    down_grad, qk_grad, vg_grad, ff_grads, out_grads, ffd_grads, res_grad = assemble(
        where,
        [*last_pieces, *feed_pieces],
        last_rows,
        feed_rows,
        branch_rows,
        padded,
        [
            (6, low_rank, width),
            (2, low_rank, qk),
            (2, low_rank, value_lanes),
            (2, low_rank, hidden_width),
            (low_rank, value_lanes),
            (low_rank, hidden_width),
            (2, low_rank, width),
        ],
    )

    def as_down(rows):
        return rows.reshape(rows.shape[:-2] + (sets, rank, -1)).swapaxes(-1, -2)

    def as_up(rows):
        return rows.reshape(rows.shape[0], sets, rank, -1)

    return (
        low(result),
        input_grad,
        as_down(down_grad),
        as_up(qk_grad),
        as_up(vg_grad),
        as_up(ff_grads),
        as_down(out_grads),
        as_down(ffd_grads),
        as_up(res_grad),
    )


def solution(mesh):
    rows = P(("seq", "head"), None)
    lanes = P(None, "head")
    last = P(None, None, None, "head")
    middle = P(None, "head", None)
    in_specs = (
        rows, rows, P(), P(), P(), lanes, lanes, lanes, lanes, lanes, lanes,
        P(None, None, "head"), P("head"), P("head"), lanes, P(), P("head", None), P(), lanes,
        lanes, P("head", None), P(), last, last, last, middle, middle, P(),
    )
    out_specs = (rows, rows, P(), last, last, last, middle, middle, P())
    return jax.shard_map(
        on_device, mesh=mesh, in_specs=in_specs, out_specs=out_specs, check_vma=False
    )
```

```python
import functools

import jax
import jax.numpy as jnp
from jax import lax
from jax.experimental import pallas as pl
from jax.experimental.pallas import tpu as pltpu
from jax.sharding import PartitionSpec as P

CHUNK = 128
STEP = 256
HALO = 16
DOC_MAX = 4096
EPS = 1e-06
VMEM_LIMIT = 56 * 1024 * 1024
bfloat = jnp.bfloat16
single = jnp.float32


def contract(left, right, left_dim, right_dim):
    return lax.dot_general(
        left,
        right,
        (((left_dim,), (right_dim,)), ((), ())),
        preferred_element_type=single,
    )


def nn(left, right):
    return contract(left, right, 1, 0)


def nt(left, right):
    return contract(left, right, 1, 1)


def tn(left, right):
    return contract(left, right, 0, 0)


def low(array):
    return array.astype(bfloat)


def iotas():
    rows = lax.broadcasted_iota(jnp.int32, (CHUNK, CHUNK), 0)
    columns = lax.broadcasted_iota(jnp.int32, (CHUNK, CHUNK), 1)
    return rows, columns


def split_two(array):
    high = low(array)
    return high, low(array - high.astype(single))


def near_exact(left, right):
    left_high, left_low = split_two(left)
    right_high, right_low = split_two(right)
    return nn(
        jnp.concatenate([left_high, left_high, left_low], axis=1),
        jnp.concatenate([right_high, right_low, right_high], axis=0),
    )


def ones_product(ones, array):
    high = low(array)
    rest = array - high.astype(single)
    middle = low(rest)
    lowest = low(rest - middle.astype(single))
    return nn(
        jnp.concatenate([ones, ones, ones], axis=1),
        jnp.concatenate([high, middle, lowest], axis=0),
    )


def unit_lower_inverses(stricts, rows, columns):
    eye = (rows == columns).astype(single)
    differ = rows ^ columns
    block = 8
    inner = [jnp.where(differ < block, strict, 0.0) for strict in stricts]
    second = [near_exact(a, a) for a in inner]
    inverse = [near_exact(eye - a, eye + b) for a, b in zip(inner, second)]
    fourth = [near_exact(b, b) for b in second]
    inverse = [near_exact(a, eye + b) for a, b in zip(inverse, fourth)]
    while block < CHUNK:
        between = (differ >= block) & (differ < 2 * block)
        off = [jnp.where(between, strict, 0.0) for strict in stricts]
        part = [near_exact(a, b) for a, b in zip(off, inverse)]
        inverse = [a - near_exact(a, b) for a, b in zip(inverse, part)]
        block = 2 * block
    return inverse


def softplus(value):
    return jnp.maximum(value, 0.0) + jnp.log(1.0 + jnp.exp(-jnp.abs(value)))


def sigmoid(value):
    return 1.0 / (1.0 + jnp.exp(-value))


def gates(decay, start, rows, columns):
    lower_ones = low((rows >= columns).astype(single))
    total = ones_product(lower_ones, jnp.broadcast_to(decay, (CHUNK, CHUNK)))
    linked = (rows >= columns) & (columns >= start)
    within = jnp.where(linked, jnp.exp(jnp.where(linked, total - total.T, 0.0)), 0.0)
    running = total[:, :1]
    carried = jnp.where(start < 0, jnp.exp(running), 0.0)
    last = running[CHUNK - 1 : CHUNK]
    ending = jnp.where(
        rows[:, :1] >= start[CHUNK - 1 : CHUNK], jnp.exp(jnp.minimum(last - running, 0.0)), 0.0
    )
    return within, carried, ending


def convolved(window, starts, weights, base):
    positions = base + lax.broadcasted_iota(jnp.int32, (STEP, 1), 0)
    taps = weights.shape[0]
    total = None
    for tap in range(taps):
        back = taps - 1 - tap
        term = window[HALO - back : HALO - back + STEP, :] * weights[tap : tap + 1, :]
        if back:
            term = jnp.where(positions - back >= starts, term, 0.0)
        total = term if total is None else total + term
    return total


def head_scales(rows, width):
    return lax.rsqrt(jnp.sum(rows * rows, axis=-1, keepdims=True) + EPS)


def forward_kernel(
    place,
    rows_ref,
    halo_ref,
    column_ref,
    weight_ref,
    scalar_ref,
    out_ref,
    map_ref,
    written_ref,
    state_ref,
    inverse_ref,
    end_ref,
    sent_ref,
    sent_state_ref,
    window,
    state,
    *,
    heads,
    key_width,
    value_width,
):
    step = pl.program_id(0)
    wide = value_width + key_width
    base = step * STEP
    rows, columns = iotas()

    @pl.when(step == 0)
    def _():
        window[0:HALO, :] = halo_ref[...].astype(single)
        for h in range(heads):
            state[h, :, :value_width] = jnp.zeros((key_width, value_width), single)
            state[h, :, value_width:] = (rows == columns).astype(single)

    @pl.when(step > 0)
    def _():
        window[0:HALO, :] = window[STEP : STEP + HALO, :]

    window[HALO:, :] = rows_ref[...].astype(single)
    info = column_ref[...]
    starts = info[:, 2 * heads : 2 * heads + 1].astype(jnp.int32)
    before = convolved(window, starts, weight_ref[...], base)
    active = before * sigmoid(before)
    qk_lanes = heads * key_width
    chunks = STEP // CHUNK
    local, stricts = [], []
    for c in range(chunks):
        span = slice(c * CHUNK, (c + 1) * CHUNK)
        for h in range(heads):
            query = active[span, h * key_width : (h + 1) * key_width]
            key = active[span, qk_lanes + h * key_width : qk_lanes + (h + 1) * key_width]
            value = active[
                span, 2 * qk_lanes + h * value_width : 2 * qk_lanes + (h + 1) * value_width
            ]
            query = query * (head_scales(query, key_width) * key_width ** (-0.5))
            key = key * head_scales(key, key_width)
            beta = sigmoid(info[span, h : h + 1])
            decay = -scalar_ref[0, h] * softplus(
                info[span, heads + h : heads + h + 1] + scalar_ref[1, h]
            )
            within, carried, ending = gates(
                decay, starts[span] - (base + c * CHUNK), rows, columns
            )
            query, key = low(query), low(key)
            strict = jnp.where(rows > columns, within * nt(key, key), 0.0) * beta
            mixed = low(within * nt(query, key))
            stricts.append(strict)
            local.append((query, key, value, beta, carried, ending, mixed))
    inverses = [low(a) for a in unit_lower_inverses(stricts, rows, columns)]
    each = range(heads)
    now = [state[h] for h in each]
    for c in range(chunks):
        span = slice(c * CHUNK, (c + 1) * CHUNK)
        here = [local[c * heads + h] for h in each]
        inverse = [inverses[c * heads + h] for h in each]
        now_low = [low(a) for a in now]
        read = [nn(here[h][1], now_low[h]) for h in each]
        asked = [nn(here[h][0], now_low[h]) for h in each]
        target = []
        for h in each:
            query, key, value, beta, carried, ending, mixed = here[h]
            gap = -(carried * beta) * read[h]
            target.append(
                jnp.concatenate(
                    [beta * value + gap[:, :value_width], gap[:, value_width:]], axis=1
                )
            )
        written = [nn(inverse[h], low(target[h])) for h in each]
        added = [tn(here[h][1], low(here[h][5] * written[h])) for h in each]
        inner = [nn(here[h][6], low(written[h])) for h in each]
        for h in each:
            carried = here[h][4]
            inverse_ref[span, h * CHUNK : (h + 1) * CHUNK] = inverse[h]
            state_ref[c, h] = now_low[h]
            written_ref[span, h * wide : (h + 1) * wide] = low(written[h])
            output = carried * asked[h] + inner[h]
            out_ref[span, h * value_width : (h + 1) * value_width] = output[:, :value_width]
            map_ref[span, h * key_width : (h + 1) * key_width] = low(output[:, value_width:])
        now = [here[h][4][CHUNK - 1 : CHUNK] * now[h] + added[h] for h in each]
    for h in each:
        state[h] = now[h]

    @pl.when(step == pl.num_programs(0) - 1)
    def _():
        final = state[...]
        end_ref[...] = final
        sent_ref[...] = low(final)
        sent_state_ref[...] = low(final[:, :, :value_width])


def backward_kernel(
    place,
    rows_ref,
    before_ref,
    halo_ref,
    column_ref,
    weight_ref,
    scalar_ref,
    grad_ref,
    written_ref,
    state_ref,
    inverse_ref,
    end_ref,
    entering_ref,
    *rest,
    hops,
    heads,
    key_width,
    value_width,
):
    got_refs, rest = rest[:hops], rest[hops:]
    out_ref, mix_ref, tail_ref, edge_ref, window, shifted, shifted_start, cotangent, ahead = rest
    step = pl.program_id(0)
    steps = pl.num_programs(0)
    wide = value_width + key_width
    base = (steps - 1 - step) * STEP
    rows, columns = iotas()
    qk_lanes = heads * key_width
    lanes = window.shape[1]
    taps = weight_ref.shape[0]

    @pl.when(step == 0)
    def _():
        shifted[STEP : STEP + 8, :] = jnp.zeros((8, lanes), single)
        shifted_start[STEP : STEP + 8, :] = jnp.zeros((8, 1), jnp.int32)
        for h in range(heads):
            passed = got_refs[0][h].astype(single)
            for hop in range(1, hops):
                passed = passed + got_refs[hop][h].astype(single)
            cotangent[h] = passed
            ahead[h] = end_ref[h, :, :value_width] + nn(
                low(end_ref[h, :, value_width:]), low(entering_ref[h])
            )

    @pl.when(step > 0)
    def _():
        shifted[STEP : STEP + 8, :] = shifted[0:8, :]
        shifted_start[STEP : STEP + 8, :] = shifted_start[0:8, :]

    window[0:HALO, :] = jnp.where(
        step == steps - 1, halo_ref[...].astype(single), before_ref[...].astype(single)
    )
    window[HALO:, :] = rows_ref[...].astype(single)
    info = column_ref[...]
    starts = info[:, 2 * heads : 2 * heads + 1].astype(jnp.int32)
    positions = base + lax.broadcasted_iota(jnp.int32, (STEP, 1), 0)
    before = convolved(window, starts, weight_ref[...], base)
    gate = sigmoid(before)
    active = before * gate
    slope = gate * (1.0 + before * (1.0 - gate))
    upper_ones = low((rows <= columns).astype(single))
    last_row = rows[:, :1] == CHUNK - 1
    chunks = STEP // CHUNK
    each = range(heads)
    items = [(c, h) for c in range(chunks) for h in each]
    spans = {item: slice(item[0] * CHUNK, (item[0] + 1) * CHUNK) for item in items}
    entering = [low(entering_ref[h]) for h in each]
    root = key_width ** (-0.5)

    def per(function):
        return {item: function(*item) for item in items}

    def q_lanes(h):
        return slice(h * key_width, (h + 1) * key_width)

    def k_lanes(h):
        return slice(qk_lanes + h * key_width, qk_lanes + (h + 1) * key_width)

    def v_lanes(h):
        return slice(2 * qk_lanes + h * value_width, 2 * qk_lanes + (h + 1) * value_width)

    def kept(c, h, part):
        return written_ref[spans[c, h], h * wide : (h + 1) * wide][:, part]

    values, maps = slice(0, value_width), slice(value_width, wide)
    query_raw = per(lambda c, h: active[spans[c, h], q_lanes(h)])
    key_raw = per(lambda c, h: active[spans[c, h], k_lanes(h)])
    query_scale = per(lambda c, h: head_scales(query_raw[c, h], key_width))
    key_scale = per(lambda c, h: head_scales(key_raw[c, h], key_width))
    query = per(lambda c, h: query_raw[c, h] * (query_scale[c, h] * root))
    key = per(lambda c, h: key_raw[c, h] * key_scale[c, h])
    query_low = per(lambda c, h: low(query[c, h]))
    key_low = per(lambda c, h: low(key[c, h]))
    beta = per(lambda c, h: sigmoid(info[spans[c, h], h : h + 1]))
    raw = per(lambda c, h: info[spans[c, h], heads + h : heads + h + 1] + scalar_ref[1, h])
    gated = per(
        lambda c, h: gates(
            -scalar_ref[0, h] * softplus(raw[c, h]),
            starts[spans[c, h]] - (base + c * CHUNK),
            rows,
            columns,
        )
    )
    within = per(lambda c, h: gated[c, h][0])
    carried = per(lambda c, h: gated[c, h][1])
    ending = per(lambda c, h: gated[c, h][2])
    mixed = per(lambda c, h: low(within[c, h] * nt(query_low[c, h], key_low[c, h])))
    written = per(
        lambda c, h: kept(c, h, values).astype(single) + nn(kept(c, h, maps), entering[h])
    )
    start_state = per(
        lambda c, h: state_ref[c, h][:, values].astype(single)
        + nn(state_ref[c, h][:, maps], entering[h])
    )
    written_low = per(lambda c, h: low(written[c, h]))
    start_low = per(lambda c, h: low(start_state[c, h]))
    grad = per(lambda c, h: grad_ref[spans[c, h], h * value_width : (h + 1) * value_width])
    grad_low = grad
    carried_grad = per(lambda c, h: low(carried[c, h] * grad[c, h].astype(single)))
    from_output = per(lambda c, h: tn(mixed[c, h], grad_low[c, h]))
    state_part = per(lambda c, h: tn(query_low[c, h], carried_grad[c, h]))
    mixed_grad = per(lambda c, h: low(within[c, h] * nt(grad_low[c, h], written_low[c, h])))
    query_grad = per(
        lambda c, h: nt(carried_grad[c, h], start_low[c, h]) + nn(mixed_grad[c, h], key_low[c, h])
    )
    key_write = per(lambda c, h: tn(mixed_grad[c, h], query_low[c, h]))
    later, later_low, solved, value_grad, read_grad = {}, {}, {}, {}, {}
    now = [cotangent[h] for h in each]
    for c in reversed(range(chunks)):
        for h in each:
            later[c, h], later_low[c, h] = now[h], low(now[h])
        from_state = [nn(key_low[c, h], later_low[c, h]) for h in each]
        written_grad = [low(from_output[c, h] + ending[c, h] * from_state[h]) for h in each]
        for h in each:
            inverse = inverse_ref[spans[c, h], h * CHUNK : (h + 1) * CHUNK]
            solved[c, h] = tn(inverse, written_grad[h])
        for h in each:
            value_grad[c, h] = beta[c, h] * solved[c, h]
            read_grad[c, h] = low(-carried[c, h] * value_grad[c, h])
        now = [
            carried[c, h][CHUNK - 1 : CHUNK] * now[h]
            + state_part[c, h]
            + tn(key_low[c, h], read_grad[c, h])
            for h in each
        ]
    following = {
        (c, h): start_state[c + 1, h] if c + 1 < chunks else ahead[h] for c, h in items
    }
    at_end = per(lambda c, h: jnp.sum(later[c, h] * following[c, h], keepdims=True))
    for h in each:
        cotangent[h] = now[h]
        ahead[h] = start_state[0, h]
    strict_grad = per(
        lambda c, h: low(
            jnp.where(
                rows > columns, -within[c, h] * nt(low(value_grad[c, h]), written_low[c, h]), 0.0
            )
        )
    )
    key_read = per(
        lambda c, h: nt(read_grad[c, h], start_low[c, h]) + nn(strict_grad[c, h], key_low[c, h])
    )
    key_write = per(
        lambda c, h: key_write[c, h]
        + tn(strict_grad[c, h], key_low[c, h])
        + nt(low(ending[c, h] * written[c, h]), later_low[c, h])
    )
    query_dot = per(
        lambda c, h: jnp.sum(query[c, h] * query_grad[c, h], axis=-1, keepdims=True)
    )
    running_grad = per(
        lambda c, h: query_dot[c, h]
        + jnp.sum(key[c, h] * (key_read[c, h] - key_write[c, h]), axis=-1, keepdims=True)
        + jnp.where(last_row, at_end[c, h], 0.0)
    )
    decay_sum = per(
        lambda c, h: ones_product(
            upper_ones, jnp.broadcast_to(running_grad[c, h], (CHUNK, CHUNK))
        )[:, :1]
    )
    decay_grad = per(
        lambda c, h: jnp.where(
            positions[spans[c, h]] == starts[spans[c, h]],
            0.0,
            -scalar_ref[0, h] * sigmoid(raw[c, h]) * decay_sum[c, h],
        )
    )
    beta_grad = per(
        lambda c, h: jnp.sum(solved[c, h] * written[c, h], axis=-1, keepdims=True)
        * sigmoid(-info[spans[c, h], h : h + 1])
    )
    for c, h in items:
        span = spans[c, h]
        key_grad = key_read[c, h] + key_write[c, h]
        key_dot = jnp.sum(key[c, h] * key_grad, axis=-1, keepdims=True)
        query_active = (query_scale[c, h] * root) * query_grad[c, h] - query_raw[c, h] * (
            query_scale[c, h] * query_scale[c, h] * query_dot[c, h]
        )
        key_active = key_scale[c, h] * (key_grad - key[c, h] * key_dot)
        shifted[span, q_lanes(h)] = query_active * slope[span, q_lanes(h)]
        shifted[span, k_lanes(h)] = key_active * slope[span, k_lanes(h)]
        shifted[span, v_lanes(h)] = value_grad[c, h] * slope[span, v_lanes(h)]
    for c in range(chunks):
        mix_ref[c * CHUNK : (c + 1) * CHUNK, :] = jnp.concatenate(
            [beta_grad[c, h] for h in each]
            + [decay_grad[c, h] for h in each]
            + [jnp.zeros((CHUNK, mix_ref.shape[1] - 2 * heads), single)],
            axis=1,
        )
    shifted_start[0:STEP, :] = starts
    def collect(index, _):
        lanes_here = pl.ds(pl.multiple_of(index * 256, 256), 256)
        total = None
        for tap in range(taps):
            back = taps - 1 - tap
            term = shifted[back : back + STEP, lanes_here] * weight_ref[tap : tap + 1, lanes_here]
            if back:
                term = jnp.where(positions >= shifted_start[back : back + STEP, :], term, 0.0)
            total = term if total is None else total + term
        out_ref[:, lanes_here] = low(total)

        @pl.when(step == 0)
        def _():
            tail_ref[:, lanes_here] = total[STEP - HALO :, :]

        return 0

    lax.fori_loop(0, lanes // 256, collect, 0)

    @pl.when(step == steps - 1)
    def _():
        window[0:8, :] = jnp.zeros((8, lanes), single)
        window[8:16, :] = shifted[0:8, :]
        early = lax.broadcasted_iota(jnp.int32, (8, 1), 0) - 8
        collected = jnp.zeros((8, lanes), single)
        for tap in range(taps - 1):
            back = taps - 1 - tap
            reader = early + back
            reader_start = jnp.zeros((8, 1), jnp.int32)
            for t in range(back):
                reader_start = jnp.where(reader == t, shifted_start[t : t + 1, :], reader_start)
            term = window[back : back + 8, :] * weight_ref[tap : tap + 1, :]
            collected = collected + jnp.where(
                (reader >= 0) & (early >= reader_start), term, 0.0
            )
        edge_ref[0:8, :] = jnp.zeros((8, lanes), single)
        edge_ref[8:16, :] = collected


def block_place(step, place, per_quarter):
    return ((step // per_quarter) ^ place[0]) * per_quarter + step % per_quarter


def run_forward(place, rows, halo, columns, weights, scalars, heads, key_width, value_width, quarter):
    count, lanes = columns.shape[0], rows.shape[1]
    steps, per_quarter = count // STEP, quarter // STEP
    wide = value_width + key_width
    chunks = STEP // CHUNK
    at = lambda i, place: (block_place(i, place, per_quarter), 0)
    fixed = lambda i, place: (0, 0)
    body = functools.partial(
        forward_kernel, heads=heads, key_width=key_width, value_width=value_width
    )
    shapes = (
        jax.ShapeDtypeStruct((count, heads * value_width), single),
        jax.ShapeDtypeStruct((count, heads * key_width), bfloat),
        jax.ShapeDtypeStruct((count, heads * wide), bfloat),
        jax.ShapeDtypeStruct((count // CHUNK, heads, key_width, wide), bfloat),
        jax.ShapeDtypeStruct((count, heads * CHUNK), bfloat),
        jax.ShapeDtypeStruct((heads, key_width, wide), single),
        jax.ShapeDtypeStruct((heads, key_width, wide), bfloat),
        jax.ShapeDtypeStruct((heads, key_width, value_width), bfloat),
    )
    return pl.pallas_call(
        body,
        out_shape=shapes,
        grid_spec=pltpu.PrefetchScalarGridSpec(
            num_scalar_prefetch=1,
            grid=(steps,),
            in_specs=[
                pl.BlockSpec((STEP, lanes), at),
                pl.BlockSpec((HALO, lanes), lambda i, place: (0, 0)),
                pl.BlockSpec((STEP, columns.shape[1]), at),
                pl.BlockSpec(weights.shape, fixed),
                pl.BlockSpec(memory_space=pltpu.SMEM),
            ],
            out_specs=[
                pl.BlockSpec((STEP, heads * value_width), at),
                pl.BlockSpec((STEP, heads * key_width), at),
                pl.BlockSpec((STEP, heads * wide), at),
                pl.BlockSpec((chunks, heads, key_width, wide), lambda i, place: (i, 0, 0, 0)),
                pl.BlockSpec((STEP, heads * CHUNK), at),
                pl.BlockSpec((heads, key_width, wide), lambda i, place: (0, 0, 0)),
                pl.BlockSpec((heads, key_width, wide), lambda i, place: (0, 0, 0)),
                pl.BlockSpec((heads, key_width, value_width), lambda i, place: (0, 0, 0)),
            ],
            scratch_shapes=[
                pltpu.VMEM((STEP + HALO, lanes), single),
                pltpu.VMEM((heads, key_width, wide), single),
            ],
        ),
        compiler_params=pltpu.CompilerParams(
            dimension_semantics=("arbitrary",), vmem_limit_bytes=VMEM_LIMIT
        ),
        cost_estimate=pl.CostEstimate(
            flops=count * 2_000_000, bytes_accessed=count * 10_000, transcendentals=count * 2000
        ),
        name="delta_forward",
    )(place, rows, halo, columns, weights, scalars)


def run_backward(
    place, rows, halo, columns, weights, scalars, grad, saved, entering, got, heads,
    key_width, value_width, quarter,
):
    written, states, inverses, end = saved
    count, lanes = columns.shape[0], rows.shape[1]
    steps, per_quarter = count // STEP, quarter // STEP
    wide = value_width + key_width
    chunks = STEP // CHUNK

    def at(i, place):
        return (block_place(steps - 1 - i, place, per_quarter), 0)

    def halo_at(i, place):
        here = steps - 1 - i
        inner = block_place(jnp.maximum(here - 1, 0), place, per_quarter)
        ratio = STEP // HALO
        return (inner * ratio + ratio - 1, 0)

    fixed = lambda i, place: (0, 0)
    whole = lambda i, place: (0, 0, 0)
    body = functools.partial(
        backward_kernel,
        hops=len(got),
        heads=heads,
        key_width=key_width,
        value_width=value_width,
    )
    shapes = (
        jax.ShapeDtypeStruct((count, lanes), bfloat),
        jax.ShapeDtypeStruct((count, columns.shape[1]), single),
        jax.ShapeDtypeStruct((HALO, lanes), single),
        jax.ShapeDtypeStruct((HALO, lanes), single),
    )
    return pl.pallas_call(
        body,
        out_shape=shapes,
        grid_spec=pltpu.PrefetchScalarGridSpec(
            num_scalar_prefetch=1,
            grid=(steps,),
            in_specs=[
                pl.BlockSpec((STEP, lanes), at),
                pl.BlockSpec((HALO, lanes), halo_at),
                pl.BlockSpec((HALO, lanes), fixed),
                pl.BlockSpec((STEP, columns.shape[1]), at),
                pl.BlockSpec(weights.shape, fixed),
                pl.BlockSpec(memory_space=pltpu.SMEM),
                pl.BlockSpec((STEP, heads * value_width), at),
                pl.BlockSpec((STEP, heads * wide), at),
                pl.BlockSpec(
                    (chunks, heads, key_width, wide), lambda i, place: (steps - 1 - i, 0, 0, 0)
                ),
                pl.BlockSpec((STEP, heads * CHUNK), at),
                pl.BlockSpec(end.shape, whole),
                pl.BlockSpec(entering.shape, whole),
            ]
            + [pl.BlockSpec(part.shape, whole) for part in got],
            out_specs=[
                pl.BlockSpec((STEP, lanes), at),
                pl.BlockSpec((STEP, columns.shape[1]), at),
                pl.BlockSpec((HALO, lanes), fixed),
                pl.BlockSpec((HALO, lanes), fixed),
            ],
            scratch_shapes=[
                pltpu.VMEM((STEP + HALO, lanes), single),
                pltpu.VMEM((STEP + 8, lanes), single),
                pltpu.VMEM((STEP + 8, 1), jnp.int32),
                pltpu.VMEM((heads, key_width, value_width), single),
                pltpu.VMEM((heads, key_width, value_width), single),
            ],
        ),
        compiler_params=pltpu.CompilerParams(
            dimension_semantics=("arbitrary",), vmem_limit_bytes=VMEM_LIMIT
        ),
        cost_estimate=pl.CostEstimate(
            flops=count * 3_000_000, bytes_accessed=count * 12_000, transcendentals=count * 3000
        ),
        name="delta_backward",
    )(
        place, rows, rows, halo, columns, weights, scalars, grad, written, states, inverses, end,
        entering, *got,
    )


def chosen_columns(table, column_sets):
    return column_sets[0:1, :] == table[:, 1:2]


def masked(product, chosen):
    return low(jnp.where(chosen, product, 0.0))


def silu_parts(value):
    logistic = sigmoid(value)
    return logistic, value * logistic


def accumulate(ref, value, first):
    if first is True:
        ref[...] = value
    else:
        ref[...] = jnp.where(first, value, ref[...] + value)


def emit_blocks(parts, place, own_ref, far_ref, pair_ref):
    for k, part in enumerate(parts):
        rows, size = part.shape[0], part.shape[1] // 4
        lanes = slice(k * size, (k + 1) * size)
        for relative, target, row in (
            (0, own_ref, 0), (2, far_ref, 0), (1, pair_ref, 0), (3, pair_ref, rows)
        ):
            start = pl.multiple_of((place ^ relative) * size, 128)
            target[row : row + rows, lanes] = low(part[:, pl.ds(start, size)])


def copy_rows(target, row, source, lanes=slice(None)):
    size = 32

    def run(index, _):
        start = pl.multiple_of(index * size, size)
        target[pl.ds(pl.multiple_of(row + start, size), size), lanes] = source[pl.ds(start, size), :]
        return 0

    lax.fori_loop(0, source.shape[0] // size, run, 0)


def at_end(fill):
    pl.when(pl.program_id(0) == pl.num_programs(0) - 1)(fill)


def at_start(fill):
    pl.when(pl.program_id(0) == 0)(fill)


def project_kernel(
    rows_ref, table_ref, sets_ref, down_ref, mix_ref, wq_ref, wk_ref, wv_ref, wg_ref, up_qk_ref,
    up_vg_ref, *rest, with_halo,
):
    low_rank = sets_ref.shape[1]
    width, q_width = wq_ref.shape
    v_width = wv_ref.shape[1]
    bounds = [0, q_width, 2 * q_width, 2 * q_width + v_width, 2 * q_width + 2 * v_width]
    if with_halo:
        halo_ref, halo_table_ref, *rest = rest
        pre_ref, inner_ref, column_ref, gate_ref, inner_gate_ref, pre_halo_ref, joined = rest
    else:
        pre_ref, inner_ref, column_ref, gate_ref, inner_gate_ref, joined = rest
    weights = (wq_ref, wk_ref, wv_ref, wg_ref)
    ups = (
        up_qk_ref.at[0],
        up_qk_ref.at[1],
        up_vg_ref.at[:low_rank],
        up_vg_ref.at[low_rank:],
    )

    @at_start
    def _():
        for p in range(4):
            columns = slice(bounds[p], bounds[p + 1])
            copy_rows(joined, 0, weights[p], columns)
            copy_rows(joined, width, ups[p], columns)

    rows, table = rows_ref[...], table_ref[...]
    count = rows.shape[0]
    if with_halo:
        rows = jnp.concatenate([rows, halo_ref[...]], axis=0)
        table = jnp.concatenate([table, halo_table_ref[...]], axis=0)
    chosen = chosen_columns(table, sets_ref[...])
    product = nt(rows, down_ref[...])
    inner = [masked(product[:, p * low_rank : (p + 1) * low_rank], chosen) for p in range(4)]
    for p in range(4):
        columns = slice(bounds[p], bounds[p + 1])
        output = nn(jnp.concatenate([rows, inner[p]], axis=1), joined[:, columns])
        if p == 3:
            gate_ref[...] = output[:count]
            inner_gate_ref[...] = inner[p][:count]
            continue
        pre_ref[:, columns] = low(output[:count])
        if with_halo:
            pre_halo_ref[:, columns] = low(output[count:])
        inner_ref[:, p * low_rank : (p + 1) * low_rank] = inner[p][:count]
    column_ref[...] = jnp.concatenate(
        [nt(rows[:count], mix_ref[...])[:, :4], table[:count, :4]], axis=1
    )


def head_outputs(raw_ref, map_ref, entering_ref, heads, key_width, value_width):
    outputs = []
    for h in range(heads):
        outputs.append(
            raw_ref[:, h * value_width : (h + 1) * value_width]
            + nn(map_ref[:, h * key_width : (h + 1) * key_width], entering_ref[h])
        )
    return outputs


def attend_kernel(
    raw_ref, map_ref, gate_ref, table_ref, gain_ref, sets_ref, wo_ref, down_ref, up_ref, *rest,
    heads, key_width, value_width, hops,
):
    got_refs, rest = rest[:hops], rest[hops:]
    part_ref, z_ref, inner_ref, entering_ref, joined = rest
    value_lanes = wo_ref.shape[0]

    @at_start
    def _():
        copy_rows(joined, 0, wo_ref)
        copy_rows(joined, value_lanes, up_ref)
        for h in range(heads):
            state = got_refs[hops - 1][h].astype(single)
            for hop in range(hops - 1, 0, -1):
                got = got_refs[hop - 1][h]
                state = got[:, :value_width].astype(single) + nn(got[:, value_width:], low(state))
            entering_ref[h] = low(state)

    chosen = chosen_columns(table_ref[...], sets_ref[...])
    outputs = head_outputs(raw_ref, map_ref, entering_ref, heads, key_width, value_width)
    parts = []
    for h, output in enumerate(outputs):
        lanes = slice(h * value_width, (h + 1) * value_width)
        scale = lax.rsqrt(jnp.mean(output * output, axis=-1, keepdims=True) + EPS)
        _, gate = silu_parts(gate_ref[:, lanes])
        parts.append(low(output * scale * gain_ref[0:1, :] * gate))
    z = jnp.concatenate(parts, axis=1)
    z_ref[...] = z
    inner = masked(nt(z, down_ref[...]), chosen)
    inner_ref[...] = inner
    part_ref[...] = low(nn(jnp.concatenate([z, inner], axis=1), joined[...]))


def feed_before_kernel(
    grad_ref, table_ref, sets_ref, wd_ref, down_ffd_t_ref, up_ref, hidden_grad_ref, du_ref, joined
):
    hidden, width = wd_ref.shape

    @at_start
    def _():
        copy_rows(joined, 0, wd_ref, slice(0, width))
        copy_rows(joined, 0, down_ffd_t_ref, slice(width, None))
        joined[hidden:, :] = jnp.zeros((joined.shape[0] - hidden, joined.shape[1]), bfloat)

    grad = grad_ref[...]
    du_down = masked(nt(grad, up_ref[...]), chosen_columns(table_ref[...], sets_ref[...]))
    du_ref[...] = du_down
    hidden_grad_ref[...] = nt(jnp.concatenate([grad, du_down], axis=1), joined[...])


def feed_kernel(
    rows_ref, hidden_grad_ref, table_ref, sets_ref, down_ref, wg_ref, wu_ref, up_t_ref, up_ref,
    back_ref, hidden_ref, ff_grad_ref, inner_ref, du_ref,
    joined_gate, joined_up, joined_back,
):
    low_rank = sets_ref.shape[1]
    hidden, width = wg_ref.shape
    padded = joined_gate.shape[0]

    @at_start
    def _():
        for p, (joined, weight) in enumerate(((joined_gate, wg_ref), (joined_up, wu_ref))):
            copy_rows(joined, 0, weight, slice(0, width))
            copy_rows(joined, 0, up_t_ref.at[p], slice(width, None))
            joined[hidden:, :] = jnp.zeros((padded - hidden, joined.shape[1]), bfloat)
            copy_rows(joined_back, p * padded, weight)
            joined_back[p * padded + hidden : (p + 1) * padded, :] = jnp.zeros(
                (padded - hidden, width), bfloat
            )
        copy_rows(joined_back, 2 * padded, down_ref)

    chosen = chosen_columns(table_ref[...], sets_ref[...])
    both = jnp.concatenate([chosen, chosen], axis=1)
    rows = rows_ref[...]
    inner = masked(nt(rows, down_ref[...]), both)
    inner_ref[...] = inner
    gate = nt(jnp.concatenate([rows, inner[:, :low_rank]], axis=1), joined_gate[...])
    up = nt(jnp.concatenate([rows, inner[:, low_rank:]], axis=1), joined_up[...])
    logistic, active = silu_parts(gate)
    hidden_ref[...] = low(active * up)
    hidden_grad = hidden_grad_ref[...]
    gate_grad = low(hidden_grad * up * logistic * (1.0 + gate * (1.0 - logistic)))
    up_grad = low(hidden_grad * active)
    du_gate = masked(nt(gate_grad, up_ref[0]), chosen)
    du_up = masked(nt(up_grad, up_ref[1]), chosen)
    du_ref[:, :low_rank] = du_gate
    du_ref[:, low_rank:] = du_up
    ff_grad_ref[:, :padded] = gate_grad
    ff_grad_ref[:, padded:] = up_grad
    back_ref[...] = low(
        nn(jnp.concatenate([gate_grad, up_grad, du_gate, du_up], axis=1), joined_back[...])
    )


def feed_after_kernel(
    rows_ref, grad_ref, hidden_ref, ff_grad_ref, inner_ref, du_ref, du_down_ref, table_ref,
    sets_ref, place_ref, wd_ref, down_ffd_ref, up_ref,
    out_ref, own_ref, far_ref, pair_ref, flat_ref,
    joined, down_sum, res_sum, flat_sum,
):
    first = pl.program_id(0) == 0
    low_rank = sets_ref.shape[1]
    width_hidden = wd_ref.shape[0]
    padded = down_ffd_ref.shape[1]

    @at_start
    def _():
        copy_rows(joined, 0, wd_ref)
        joined[width_hidden:padded, :] = jnp.zeros(
            (padded - width_hidden, joined.shape[1]), bfloat
        )
        copy_rows(joined, padded, up_ref)

    hidden = hidden_ref[...]
    inner = inner_ref[...]
    u_down = masked(
        nt(hidden, down_ffd_ref[...]), chosen_columns(table_ref[...], sets_ref[...])
    )
    out_ref[...] = low(nn(jnp.concatenate([hidden, u_down], axis=1), joined[...]))
    accumulate(down_sum, tn(du_ref[...], rows_ref[...]), first)
    accumulate(res_sum, tn(u_down, grad_ref[...]), first)
    for k, grown in enumerate(
        (
            tn(inner[:, :low_rank], ff_grad_ref[:, :padded]),
            tn(inner[:, low_rank:], ff_grad_ref[:, padded:]),
            tn(du_down_ref[...], hidden),
        )
    ):
        accumulate(flat_sum.at[:, k * padded : (k + 1) * padded], grown, first)

    @at_end
    def _():
        flat_ref[...] = low(flat_sum[...])
        emit_blocks(
            (down_sum.at[:low_rank], down_sum.at[low_rank:], res_sum),
            place_ref[0], own_ref, far_ref, pair_ref,
        )


def branch_kernel(
    branch_ref, raw_ref, map_ref, gate_ref, table_ref, entering_ref, gain_ref, sets_ref, wo_ref,
    down_out_t_ref, up_ref, up_gate_ref, *rest,
    heads, key_width, value_width, hops, last,
):
    if last:
        before_ref, *rest = rest
        got_refs, rest = rest[: hops - 1], rest[hops - 1 :]
        raw_grad_ref, gate_grad_ref, du_out_ref, du_gate_ref, *rest = rest
        sent_refs, (joined, total_ref) = rest[:hops], rest[hops:]
    else:
        raw_grad_ref, gate_grad_ref, du_out_ref, du_gate_ref, total_ref, joined = rest
    width = wo_ref.shape[1]

    @at_start
    def _():
        copy_rows(joined, 0, wo_ref, slice(0, width))
        copy_rows(joined, 0, down_out_t_ref, slice(width, None))

    chosen = chosen_columns(table_ref[...], sets_ref[...])
    branch = branch_ref[...]
    outputs = head_outputs(raw_ref, map_ref, entering_ref, heads, key_width, value_width)
    du_out = masked(nt(branch, up_ref[...]), chosen)
    du_out_ref[...] = du_out
    mixed_grad = nt(jnp.concatenate([branch, du_out], axis=1), joined[...])
    gain = gain_ref[0:1, :]
    gate_grads = []
    for h, output in enumerate(outputs):
        lanes = slice(h * value_width, (h + 1) * value_width)
        scale = lax.rsqrt(jnp.mean(output * output, axis=-1, keepdims=True) + EPS)
        value = gate_ref[:, lanes]
        logistic, active = silu_parts(value)
        incoming = mixed_grad[:, lanes]
        gate_grads.append(
            low(
                incoming
                * (output * scale * gain)
                * (logistic * (1.0 + value * (1.0 - logistic)))
            )
        )
        scaled = gain * (incoming * active)
        dot = jnp.mean(output * scaled, axis=-1, keepdims=True)
        raw_grad = low(scale * scaled - output * (scale * scale * scale * dot))
        raw_grad_ref[:, lanes] = raw_grad
        grown = tn(map_ref[:, h * key_width : (h + 1) * key_width], raw_grad)
        accumulate(total_ref.at[h], grown, pl.program_id(0) == 0)
    gate_grad = jnp.concatenate(gate_grads, axis=1)
    gate_grad_ref[...] = gate_grad
    du_gate_ref[...] = masked(nt(gate_grad, up_gate_ref[...]), chosen)
    if last:

        @at_end
        def _():
            for h in range(heads):
                passed = low(before_ref[h] + total_ref[h])
                sent_refs[0][h] = passed
                for hop in range(1, hops):
                    passed = low(tn(got_refs[hop - 1][h][:, value_width:], passed))
                    sent_refs[hop][h] = passed


def branch_after_kernel(
    branch_ref, z_ref, u_out_ref, rows_ref, inner_ref, du_out_ref, du_gate_ref, gate_grad_ref,
    down_grad_ref, res_grad_ref, flat_ref,
    flat_sum,
):
    lanes = z_ref.shape[1]
    accumulate(down_grad_ref, tn(du_gate_ref[...], rows_ref[...]), True)
    accumulate(res_grad_ref, tn(u_out_ref[...], branch_ref[...]), True)
    accumulate(flat_sum.at[:, :lanes], tn(du_out_ref[...], z_ref[...]), True)
    accumulate(flat_sum.at[:, lanes:], tn(inner_ref[...], gate_grad_ref[...]), True)

    @at_end
    def _():
        flat_ref[...] = low(flat_sum[...])


def settled_rows(pre_ref, tail_ref, arrived_ref, place_ref, quarter, window):
    block = window.shape[0]
    start = ((3 ^ place_ref[0]) + 1) * quarter - HALO - pl.program_id(0) * block
    window[...] = pre_ref[...]

    @pl.when((start >= 0) & (start < block))
    def _():
        window[pl.ds(pl.multiple_of(start, HALO), HALO), :] = low(tail_ref[...] + arrived_ref[...])

    return window[...]


def settle_grads_kernel(
    pre_ref, rows_ref, inner_ref, table_ref, tail_ref, arrived_ref, place_ref, sets_ref,
    up_qk_ref, up_value_ref, down_late_ref, res_late_ref,
    du_ref, own_ref, far_ref, pair_ref, flat_ref,
    window, down_sum, flat_sum,
    *, quarter,
):
    first = pl.program_id(0) == 0
    low_rank = sets_ref.shape[1]
    q_width = up_qk_ref.shape[2]
    chosen = chosen_columns(table_ref[...], sets_ref[...])
    pre = settled_rows(pre_ref, tail_ref, arrived_ref, place_ref, quarter, window)
    query, key, value = pre[:, :q_width], pre[:, q_width : 2 * q_width], pre[:, 2 * q_width :]
    inner = inner_ref[...]
    du = jnp.concatenate(
        [
            masked(nt(query, up_qk_ref[0]), chosen),
            masked(nt(key, up_qk_ref[1]), chosen),
            masked(nt(value, up_value_ref[...]), chosen),
        ],
        axis=1,
    )
    du_ref[...] = du
    accumulate(down_sum, tn(du, rows_ref[...]), first)
    at = 0
    for p, part in enumerate((query, key, value)):
        accumulate(
            flat_sum.at[:, at : at + part.shape[1]],
            tn(inner[:, p * low_rank : (p + 1) * low_rank], part),
            first,
        )
        at += part.shape[1]

    @at_end
    def _():
        flat_ref[...] = low(flat_sum[...])
        emit_blocks(
            [down_sum.at[p * low_rank : (p + 1) * low_rank] for p in range(3)]
            + [down_late_ref, res_late_ref],
            place_ref[0], own_ref, far_ref, pair_ref,
        )


def settle_kernel(
    pre_ref, gate_grad_ref, du_ref, du_gate_ref, mix_ref, tail_ref, arrived_ref, place_ref,
    down_ref, mix_weight_ref, wq_ref, wk_ref, wv_ref, wg_ref,
    part_ref,
    window, joined, joined_small,
    *, quarter,
):
    q_width, v_width = wq_ref.shape[1], wv_ref.shape[1]

    @at_start
    def _():
        at = 0
        for weight in (wq_ref, wk_ref, wv_ref, wg_ref):
            copy_rows(joined, 0, weight, slice(at, at + weight.shape[1]))
            at += weight.shape[1]
        maps, mixes = down_ref.shape[0], mix_weight_ref.shape[0]
        spare = joined_small.shape[0] - maps - mixes
        copy_rows(joined_small, 0, down_ref)
        joined_small[maps:, :] = jnp.concatenate(
            [mix_weight_ref[...], jnp.zeros((spare, joined_small.shape[1]), bfloat)], axis=0
        )

    pre = settled_rows(pre_ref, tail_ref, arrived_ref, place_ref, quarter, window)
    mix = low(mix_ref[...])
    spare = joined_small.shape[0] - down_ref.shape[0] - mix.shape[1]
    small = jnp.concatenate(
        [du_ref[...], du_gate_ref[...], mix, jnp.zeros((mix.shape[0], spare), bfloat)], axis=1
    )
    part_ref[...] = low(
        nt(jnp.concatenate([pre, gate_grad_ref[...]], axis=1), joined[...])
        + nn(small, joined_small[...])
    )


def assemble_kernel(
    place_ref, *refs, padded,
):
    pieces_last, pieces_feed = refs[:4], refs[4:8]
    last_ref, feed_ref, branch_ref = refs[8:11]
    down_ref, qk_ref, vg_ref, ff_ref, out_ref, ffd_ref, res_ref = refs[11:]
    place = place_ref[0]
    size = pieces_last[0].shape[1] // 5
    first = [down_ref.at[p] for p in range(4)] + [res_ref.at[0]]
    second = [down_ref.at[4], down_ref.at[5], res_ref.at[1]]
    for relative in range(4):
        start = pl.multiple_of((place ^ relative) * size, 128)
        for targets, piece in ((first, pieces_last[relative]), (second, pieces_feed[relative])):
            for k, target in enumerate(targets):
                target[:, pl.ds(start, size)] = piece[:, k * size : (k + 1) * size].astype(single)
    qk, values, hidden = qk_ref.shape[2], vg_ref.shape[2], ff_ref.shape[2]

    def lanes(ref, start, width):
        return ref[:, start : start + width].astype(single)

    own = 5 * size
    qk_ref[0], qk_ref[1] = lanes(last_ref, own, qk), lanes(last_ref, own + qk, qk)
    vg_ref[0] = lanes(last_ref, own + 2 * qk, values)
    at = last_ref.shape[1] + 3 * size
    out_ref[...] = lanes(branch_ref, at, values)
    vg_ref[1] = lanes(branch_ref, at + values, values)
    ff_ref[0] = lanes(feed_ref, 0, hidden)
    ff_ref[1] = lanes(feed_ref, padded, hidden)
    ffd_ref[...] = lanes(feed_ref, 2 * padded, hidden)


def assemble(where, shared, last, feed, branch, padded, shapes):
    rows = last.shape[0]
    block = min(32, rows)

    def spec(shape):
        if len(shape) == 2:
            return pl.BlockSpec((block, shape[1]), lambda i: (i, 0))
        return pl.BlockSpec((shape[0], block, shape[2]), lambda i: (0, i, 0))

    arrays = [*shared, last, feed, branch]
    return pl.pallas_call(
        functools.partial(assemble_kernel, padded=padded),
        out_shape=tuple(jax.ShapeDtypeStruct(shape, single) for shape in shapes),
        grid=(rows // block,),
        in_specs=[pl.BlockSpec(memory_space=pltpu.SMEM)] + [spec(a.shape) for a in arrays],
        out_specs=[spec(shape) for shape in shapes],
        compiler_params=pltpu.CompilerParams(
            dimension_semantics=("arbitrary",), vmem_limit_bytes=VMEM_LIMIT
        ),
        name="assemble",
    )(where, *arrays)


WHOLE, SCALAR = "whole", "scalar"


def by_rows(width, lane_block=0):
    return ("rows", width, lane_block)


def part(rows, index):
    return ("part", rows, index)


def pieces(width):
    return ("pieces", width)


def blocked_call(
    body, name, count, inputs, outputs, scratch, flops, block=STEP, half=None, into=()
):
    count_pieces = 4 if half is None else 2
    steps = count * count_pieces // 4 // block
    offset = (half or 0) * steps
    per = max(steps // count_pieces, 1)
    in_specs, arrays, moved, groups_in, extra = [], [], 0, [], []
    for array, kind in inputs:
        members = array if isinstance(array, (list, tuple)) else [array]
        groups_in.append(len(members))
        arrays += members
        moved += sum(a.size * a.dtype.itemsize for a in members)
        if kind == WHOLE:
            zeros = (0,) * array.ndim
            in_specs.append(
                pl.BlockSpec(
                    array.shape, lambda i, zeros=zeros: zeros, pipeline_mode=pl.Buffered(1)
                )
            )
        elif kind == SCALAR:
            in_specs.append(pl.BlockSpec(memory_space=pltpu.SMEM))
        elif kind[0] == "part":
            in_specs.append(
                pl.BlockSpec(
                    (kind[1], array.shape[1]),
                    lambda i, at=kind[2]: (at, 0),
                    pipeline_mode=pl.Buffered(1),
                )
            )
        elif kind[0] == "rows":
            in_specs.append(
                pl.BlockSpec((block, kind[1]), lambda i, lane=kind[2]: (i + offset, lane))
            )
        else:
            for b, member in enumerate(members):
                if steps == 1:
                    in_specs.append(pl.BlockSpec(member.shape, lambda i: (0, 0)))
                else:
                    in_specs.append(
                        pl.BlockSpec(
                            (block, kind[1]),
                            lambda i, b=b: (jnp.clip(i - b * per, 0, per - 1), 0),
                        )
                    )
            extra.append(pltpu.VMEM((block, kind[1]), members[0].dtype))
    out_specs, shapes, groups_out, aliases = [], [], [], {}
    into = list(into)
    held_arrays = []
    for shape, dtype, kind in outputs:
        if kind == "parts":
            quarter = shape[0] // 4
            spec = (block, shape[1])
            if half is not None:
                for b in range(2):
                    shapes.append(jax.ShapeDtypeStruct((quarter, shape[1]), dtype))
                    out_specs.append(
                        pl.BlockSpec(spec, lambda i, b=b: (jnp.clip(i - b * per, 0, per - 1), 0))
                    )
                groups_out.append(2)
            else:
                for rows in (quarter, quarter, 2 * quarter):
                    shapes.append(jax.ShapeDtypeStruct((rows, shape[1]), dtype))
                out_specs += [
                    pl.BlockSpec(spec, lambda i: (jnp.clip(i, 0, per - 1), 0)),
                    pl.BlockSpec(spec, lambda i: (jnp.clip(i - 2 * per, 0, per - 1), 0)),
                    pl.BlockSpec(
                        spec,
                        lambda i: (
                            jnp.clip(i - per, 0, per - 1) + jnp.clip(i - 3 * per + 1, 0, per), 0
                        ),
                    ),
                ]
                groups_out.append(3)
            extra.append(pltpu.VMEM(spec, dtype))
        else:
            groups_out.append(1)
            shapes.append(jax.ShapeDtypeStruct(shape, dtype))
            if kind == "rows":
                if into:
                    aliases[len(arrays) + len(held_arrays)] = len(shapes) - 1
                    held_arrays.append(into.pop(0))
                out_specs.append(pl.BlockSpec((block, shape[1]), lambda i: (i + offset, 0)))
            else:
                zeros = (0,) * len(shape)
                out_specs.append(pl.BlockSpec(shape, lambda i, zeros=zeros: zeros))
    in_specs += [pl.BlockSpec(memory_space=pl.ANY) for _ in held_arrays]

    def wrapped(*refs):
        refs = list(refs)
        spare = refs[len(in_specs) + len(out_specs) + len(scratch) :]
        own_scratch = refs[len(in_specs) + len(out_specs) : len(refs) - len(spare)]
        quarter = pl.program_id(0) // per
        given, later, at, used = [], [], 0, 0
        for size, (_, kind) in zip(groups_in, inputs):
            if kind[0] != "pieces":
                given.append(refs[at])
            else:
                held = spare[used]
                used += 1
                if steps == 1:
                    for b in range(size):
                        piece = refs[at + b]
                        held[b * piece.shape[0] : (b + 1) * piece.shape[0], :] = piece[...]
                else:
                    for b in range(size):

                        @pl.when(quarter == b)
                        def _(held=held, source=refs[at + b]):
                            copy_rows(held, 0, source)

                given.append(held)
            at += size
        at += len(held_arrays)
        for size in groups_out:
            if size == 1:
                given.append(refs[at])
            else:
                given.append(spare[used])
                later.append((spare[used], refs[at : at + size]))
                used += 1
            at += size
        body(*given, *own_scratch)
        for held, targets in later:
            if len(targets) == 2:
                placed = ((0, targets[0]), (1, targets[1]))
            else:
                placed = ((0, targets[0]), (2, targets[1]), (1, targets[2]), (3, targets[2]))
            for b, target in placed:

                @pl.when(quarter == b)
                def _(held=held, target=target):
                    copy_rows(target, 0, held)

    results = pl.pallas_call(
        wrapped,
        out_shape=tuple(shapes),
        grid=(steps,),
        in_specs=in_specs,
        out_specs=out_specs,
        scratch_shapes=list(scratch) + extra,
        input_output_aliases=aliases,
        compiler_params=pltpu.CompilerParams(
            dimension_semantics=("arbitrary",), vmem_limit_bytes=VMEM_LIMIT
        ),
        cost_estimate=pl.CostEstimate(flops=flops, bytes_accessed=moved, transcendentals=0),
        name=name,
    )(*arrays, *held_arrays)
    grouped, at = [], 0
    for size in groups_out:
        grouped.append(results[at] if size == 1 else results[at : at + size])
        at += size
    return grouped


def flip(array, bit):
    groups = lax.axis_size("head")
    return lax.ppermute(array, "head", [(i, i ^ bit) for i in range(groups)])


def gather_rows(array):
    far = flip(array, 2)
    near = flip(array, 1)
    return [array, near, far, flip(far, 1)]


def tie(*arrays):
    return lax.optimization_barrier(arrays)


def near_sum(parts):
    own, far, pair = parts
    size = own.shape[0]
    arrived = flip(pair, 1)
    return (
        own.astype(single) + arrived[:size].astype(single),
        low(far.astype(single) + arrived[size:].astype(single)),
    )


def halves_sum(first, second):
    near, corner = tie(flip(first[1], 1), second[1])
    return (
        first[0].astype(single) + near.astype(single),
        low(second[0].astype(single) + flip(corner, 1).astype(single)),
    )


def far_sum(own, far):
    return own + flip(far, 2).astype(single)


def shifted_along(array, axis, by):
    length = lax.axis_size(axis)
    pairs = [(i, i + by) for i in range(length) if 0 <= i + by < length]
    return lax.ppermute(array, axis, pairs)


def seq_rows(flat):
    members = lax.axis_size("seq")
    return flat.reshape(members, flat.shape[0] // members, flat.shape[1])


def share_sum(parts):
    summed = low(jnp.sum(parts.astype(single), axis=0))
    return jnp.broadcast_to(summed[None], parts.shape)


def exchange(parts):
    return lax.all_to_all(parts, "seq", 0, 0)


def all_rows(parts):
    return parts.reshape(-1, parts.shape[-1])


def rms_scale(rows, gain):
    return rows * lax.rsqrt(jnp.mean(rows * rows, axis=-1, keepdims=True) + EPS) * gain


def rms_back(rows, gain, incoming):
    _, back = jax.vjp(lambda value: rms_scale(value, gain), rows)
    return back(incoming)[0]


def on_device(
    block_input,
    out_grad,
    lengths,
    doc_sets,
    norm1_gain,
    w_query,
    w_key,
    w_value,
    conv_query,
    conv_key,
    conv_value,
    w_decay_beta,
    decay_rate,
    decay_bias,
    w_gate_out,
    out_gain,
    w_out,
    norm2_gain,
    w_gate,
    w_up,
    w_down,
    adapt_down,
    adapt_up_qk,
    adapt_up_vg,
    adapt_up_ff,
    adapt_down_out,
    adapt_down_ffd,
    adapt_up_res,
):
    groups = lax.axis_size("head")
    members = lax.axis_size("seq")
    place = lax.axis_index("head")
    quarter, width = block_input.shape
    count = quarter * groups
    heads = decay_rate.shape[0]
    key_width = w_query.shape[1] // heads
    value_width = w_value.shape[1] // heads
    sets, rank = adapt_down.shape[1], adapt_down.shape[3]
    low_rank = sets * rank
    qk = heads * key_width
    device_start = lax.axis_index("seq") * count
    starts = jnp.sum(
        jnp.where(
            jnp.arange(lengths.shape[0])[None, :] < jnp.arange(lengths.shape[0])[:, None],
            lengths[None, :],
            0,
        ),
        axis=1,
    )
    order = jnp.arange(groups, dtype=jnp.int32) ^ place

    def tables(positions):
        reached = positions[:, None] >= starts[None, :]
        token_start = jnp.max(jnp.where(reached, starts[None, :], -1), axis=1)
        ended = positions[:, None] >= (starts + lengths)[None, :]
        token_set = jnp.sum(jnp.where(reached & ~ended, doc_sets[None, :], 0), axis=1)
        pair = jnp.stack([token_start - device_start, token_set], axis=1).astype(single)
        return jnp.pad(pair, ((0, 0), (0, 8 - pair.shape[1])))

    table = tables(
        (
            device_start + order[:, None] * quarter + jnp.arange(quarter, dtype=jnp.int32)[None, :]
        ).reshape(-1)
    )
    halo_table = tables(device_start + jnp.arange(-HALO, 0, dtype=jnp.int32))
    column_sets = jnp.broadcast_to(
        (jnp.arange(low_rank, dtype=jnp.int32) // rank).astype(single)[None, :], (8, low_rank)
    )

    down = adapt_down.transpose(0, 1, 3, 2).reshape(6 * low_rank, width)
    up_qk = adapt_up_qk.reshape(2, low_rank, -1)
    up_vg = adapt_up_vg.reshape(2 * low_rank, -1)
    up_ff = adapt_up_ff.reshape(2, low_rank, -1)
    down_out = adapt_down_out.transpose(0, 2, 1).reshape(low_rank, -1)
    down_ffd = adapt_down_ffd.transpose(0, 2, 1).reshape(low_rank, -1)
    up_res = adapt_up_res.reshape(2 * low_rank, width)
    conv = jnp.concatenate([conv_query, conv_key, conv_value], axis=1).astype(single)
    scalars = jnp.stack([decay_rate, decay_bias])
    where = place.reshape(1).astype(jnp.int32)
    weight_mix = jnp.pad(
        w_decay_beta.transpose(1, 2, 0).reshape(2 * heads, width), ((0, 8 - 2 * heads), (0, 0))
    )
    gain = jnp.broadcast_to(out_gain[None, :], (8, value_width))
    hidden_width = w_down.shape[0]
    padded = -(-hidden_width // 256) * 256
    value_lanes = heads * value_width
    block_width = width // groups
    widen = lambda a: jnp.pad(a, [(0, 0)] * (a.ndim - 1) + [(0, padded - hidden_width)])

    input_float = block_input.astype(single)
    normed = low(rms_scale(input_float, norm1_gain))
    tail = normed[quarter - HALO :]
    halo = sum(
        lax.ppermute(
            tail,
            ("seq", "head"),
            [((s * groups) + groups - 1, (s + 1) * groups + h) for s in range(members - 1)],
        )
        for h in range(groups)
    )
    normed_near, normed_far = flip(normed, 1), flip(normed, 2)
    project_inputs = [
        (table, by_rows(8)),
        (column_sets, WHOLE),
        (down, part(4 * low_rank, 0)),
        (weight_mix, WHOLE),
        (w_query, WHOLE),
        (w_key, WHOLE),
        (w_value, WHOLE),
        (w_gate_out, WHOLE),
        (up_qk, WHOLE),
        (up_vg, WHOLE),
    ]
    project_outputs = [
        ((count, 2 * qk + value_lanes), bfloat, "rows"),
        ((count, 3 * low_rank), bfloat, "rows"),
        ((count, 8), single, "rows"),
        ((count, value_lanes), single, "rows"),
        ((count, low_rank), bfloat, "rows"),
    ]
    project_scratch = [pltpu.VMEM((width + low_rank, 2 * qk + 2 * value_lanes), bfloat)]
    projected = blocked_call(
        functools.partial(project_kernel, with_halo=False),
        "project_near",
        count,
        [([normed, normed_near], pieces(width)), *project_inputs],
        project_outputs,
        project_scratch,
        count * 2_000_000,
        half=0,
    )
    normed_far, projected[2] = tie(normed_far, projected[2])
    normed_all = [normed, normed_near, normed_far, flip(normed_far, 1)]
    pre, inner, columns, gate_input, inner_gate, pre_halo = blocked_call(
        functools.partial(project_kernel, with_halo=True),
        "project_far",
        count,
        [
            (normed_all[2:], pieces(width)),
            *project_inputs,
            (halo, WHOLE),
            (halo_table, WHOLE),
        ],
        project_outputs + [((HALO, 2 * qk + value_lanes), bfloat, "whole")],
        project_scratch,
        count * 2_000_000,
        half=1,
        into=projected,
    )
    out_grad_late, grad_near, pre = tie(out_grad, flip(out_grad, 1), pre)
    grad_far, grad_corner = flip(out_grad_late, 2), flip(grad_near, 2)
    raw_local, mapped, *saved, sent, sent_state = run_forward(
        where, pre, pre_halo, columns, conv, scalars, heads, key_width, value_width, quarter
    )

    hops = min(members - 1, -(-(DOC_MAX - 1) // count))
    got = [shifted_along(sent_state, "seq", hops)]
    got = [shifted_along(sent, "seq", hop) for hop in range(hops - 1, 0, -1)][::-1] + got
    grad_far, grad_corner, sent_state = tie(grad_far, grad_corner, sent_state)
    grad_all = [out_grad, grad_near, grad_far, grad_corner]
    hidden_grad, du_down = blocked_call(
        feed_before_kernel,
        "feed_before",
        count,
        [
            (grad_all, pieces(width)),
            (table, by_rows(8)),
            (column_sets, WHOLE),
            (w_down, WHOLE),
            (down_ffd.T, WHOLE),
            (up_res, part(low_rank, 1)),
        ],
        [((count, padded), single, "rows"), ((count, low_rank), bfloat, "rows")],
        [pltpu.VMEM((padded, width + low_rank), bfloat)],
        count * 6_000_000,
    )
    raw_local, hidden_grad = tie(raw_local, hidden_grad)

    sizes = dict(heads=heads, key_width=key_width, value_width=value_width)
    attention_part, mixed, u_out, entering = blocked_call(
        functools.partial(attend_kernel, hops=hops, **sizes),
        "attend",
        count,
        [
            (raw_local, by_rows(value_lanes)),
            (mapped, by_rows(qk)),
            (gate_input, by_rows(value_lanes)),
            (table, by_rows(8)),
            (gain, WHOLE),
            (column_sets, WHOLE),
            (w_out, WHOLE),
            (down_out, WHOLE),
            (up_res, part(low_rank, 0)),
        ]
        + [(sent_by, WHOLE) for sent_by in got],
        [
            ((count, width), bfloat, "parts"),
            ((count, value_lanes), bfloat, "rows"),
            ((count, low_rank), bfloat, "rows"),
            ((heads, key_width, value_width), bfloat, "whole"),
        ],
        [pltpu.VMEM((value_lanes + low_rank, width), bfloat)],
        count * 5_000_000,
    )
    attention_own, attention_far = near_sum(attention_part)
    attention_arrived, up_ff_t, up_ff_padded, down_ffd_padded, down_out_t = tie(
        flip(attention_far, 2),
        up_ff.transpose(0, 2, 1),
        widen(up_ff),
        widen(down_ffd),
        down_out.T,
    )
    residual = input_float + (attention_own + attention_arrived.astype(single))
    normed_mid = low(rms_scale(residual, norm2_gain))
    mid_near, mid_far = flip(normed_mid, 1), flip(normed_mid, 2)

    feed_inputs = [
        (hidden_grad, by_rows(padded)),
        (table, by_rows(8)),
        (column_sets, WHOLE),
        (down, part(2 * low_rank, 2)),
        (w_gate.T, WHOLE),
        (w_up.T, WHOLE),
        (up_ff_t, WHOLE),
        (up_ff_padded, WHOLE),
    ]
    feed_outputs = [
        ((count, width), bfloat, "parts"),
        ((count, padded), bfloat, "rows"),
        ((count, 2 * padded), bfloat, "rows"),
        ((count, 2 * low_rank), bfloat, "rows"),
        ((count, 2 * low_rank), bfloat, "rows"),
    ]
    feed_scratch = [
        pltpu.VMEM((padded, width + low_rank), bfloat),
        pltpu.VMEM((padded, width + low_rank), bfloat),
        pltpu.VMEM((2 * padded + 2 * low_rank, width), bfloat),
    ]
    near_part, *fed = blocked_call(
        feed_kernel,
        "feed_near",
        count,
        [([normed_mid, mid_near], pieces(width)), *feed_inputs],
        feed_outputs,
        feed_scratch,
        count * 8_000_000,
        half=0,
    )
    mid_far, near_own = tie(mid_far, near_part[0])
    near_part = [near_own, near_part[1]]
    mid_all = [normed_mid, mid_near, mid_far, flip(mid_far, 1)]
    far_part, hidden, ff_grad, u_ff, du_ff = blocked_call(
        feed_kernel,
        "feed_far",
        count,
        [(mid_all[2:], pieces(width)), *feed_inputs],
        feed_outputs,
        feed_scratch,
        count * 8_000_000,
        half=1,
        into=fed,
    )
    grad_own, grad_sum = halves_sum(near_part, far_part)
    grad_sum, hidden = tie(grad_sum, hidden)
    grad_arrived = flip(grad_sum, 2)
    out_part, feed_own, feed_far, feed_pair, feed_owned = blocked_call(
        feed_after_kernel,
        "feed_after",
        count,
        [
            (mid_all, pieces(width)),
            (grad_all, pieces(width)),
            (hidden, by_rows(padded)),
            (ff_grad, by_rows(2 * padded)),
            (u_ff, by_rows(2 * low_rank)),
            (du_ff, by_rows(2 * low_rank)),
            (du_down, by_rows(low_rank)),
            (table, by_rows(8)),
            (column_sets, WHOLE),
            (where, SCALAR),
            (w_down, WHOLE),
            (down_ffd_padded, WHOLE),
            (up_res, part(low_rank, 1)),
        ],
        [
            ((count, width), bfloat, "parts"),
            ((low_rank, 3 * block_width), bfloat, "whole"),
            ((low_rank, 3 * block_width), bfloat, "whole"),
            ((2 * low_rank, 3 * block_width), bfloat, "whole"),
            ((low_rank, 3 * padded), bfloat, "whole"),
        ],
        [
            pltpu.VMEM((padded + low_rank, width), bfloat),
            pltpu.VMEM((2 * low_rank, width), single),
            pltpu.VMEM((low_rank, width), single),
            pltpu.VMEM((low_rank, 3 * padded), single),
        ],
        count * 16_000_000,
    )
    grad_landed, feed_far = tie(grad_arrived, feed_far)
    mid_grad = grad_own + grad_landed.astype(single)
    residual_grad = out_grad.astype(single) + rms_back(residual, norm2_gain, mid_grad)
    branch_low = low(residual_grad)
    branch_near, branch_far = flip(branch_low, 1), flip(branch_low, 2)
    out_own, out_far = near_sum(out_part)
    owned_parts = exchange(seq_rows(tie(feed_owned, branch_near)[0]))
    feed_sum, feed_sum_far = near_sum((feed_own, feed_far, tie(feed_pair, grad_arrived)[0]))
    feed_landed = flip(feed_sum_far, 2)

    branch_inputs = [
        (raw_local, by_rows(value_lanes)),
        (mapped, by_rows(qk)),
        (gate_input, by_rows(value_lanes)),
        (table, by_rows(8)),
        (entering, WHOLE),
        (gain, WHOLE),
        (column_sets, WHOLE),
        (w_out, WHOLE),
        (down_out_t, WHOLE),
        (up_res, part(low_rank, 0)),
        (up_vg, part(low_rank, 1)),
    ]
    branch_outputs = [
        ((count, value_lanes), bfloat, "rows"),
        ((count, value_lanes), bfloat, "rows"),
        ((count, low_rank), bfloat, "rows"),
        ((count, low_rank), bfloat, "rows"),
    ]
    branch_scratch = [pltpu.VMEM((value_lanes, width + low_rank), bfloat)]
    state_shape = (heads, key_width, value_width)
    *branched, state_near = blocked_call(
        functools.partial(branch_kernel, hops=hops, last=False, **sizes),
        "branch_near",
        count,
        [([branch_low, branch_near], pieces(width)), *branch_inputs],
        branch_outputs + [(state_shape, single, "whole")],
        branch_scratch,
        count * 12_000_000,
        half=0,
    )
    branch_far, state_near = tie(branch_far, state_near)
    branch_corner, owned_parts, out_far = tie(flip(branch_far, 1), owned_parts, out_far)
    branch_all = [branch_low, branch_near, branch_far, branch_corner]
    raw_grad, gate_grad, du_out, du_outgate, *state_grads = blocked_call(
        functools.partial(branch_kernel, hops=hops, last=True, **sizes),
        "branch_far",
        count,
        [(branch_all[2:], pieces(width)), *branch_inputs, (state_near, WHOLE)]
        + [(sent_by, WHOLE) for sent_by in got[:-1]],
        branch_outputs + [(state_shape, bfloat, "whole")] * hops,
        branch_scratch + [pltpu.VMEM(state_shape, single)],
        count * 4_000_000,
        half=1,
        into=branched,
    )
    state_got = [
        shifted_along(state_grads[hop - 1], "seq", -hop) for hop in range(hops, 0, -1)
    ][::-1]
    mixer_down_late, branch_res_grad, branch_flat = blocked_call(
        branch_after_kernel,
        "branch_after",
        count,
        [
            (branch_all, pieces(width)),
            (mixed, by_rows(value_lanes)),
            (u_out, by_rows(low_rank)),
            (normed_all, pieces(width)),
            (inner_gate, by_rows(low_rank)),
            (du_out, by_rows(low_rank)),
            (du_outgate, by_rows(low_rank)),
            (gate_grad, by_rows(value_lanes)),
        ],
        [
            ((low_rank, width), single, "whole"),
            ((low_rank, width), single, "whole"),
            ((low_rank, 2 * value_lanes), bfloat, "whole"),
        ],
        [pltpu.VMEM((low_rank, 2 * value_lanes), single)],
        count * 20_000_000,
        block=count,
    )
    feed_landed, du_out = tie(feed_landed, du_out)
    feed_shared = low(feed_sum + feed_landed.astype(single))
    owned_lanes = owned_parts.shape[-1]
    both = jnp.concatenate(
        [share_sum(owned_parts), seq_rows(feed_shared), seq_rows(branch_flat)], axis=2
    )
    raw_grad, both, out_far, *state_got = tie(raw_grad, both, out_far, *state_got)
    out_arrived = flip(out_far, 2)
    both = exchange(both)

    pre_grad, mix_grad, tail_grad, edge_grad = run_backward(
        where, pre, pre_halo, columns, conv, scalars, raw_grad, saved, entering, state_got,
        heads, key_width, value_width, quarter,
    )
    arrived = shifted_along(edge_grad, "seq", -1)
    arrived, both, out_arrived = tie(arrived, both, out_arrived)
    result = residual + (out_own + out_arrived.astype(single))
    later_parts = both[:, :, owned_lanes:]
    settled = [
        (pre_grad, by_rows(2 * qk + value_lanes)),
        (tail_grad, WHOLE),
        (arrived, WHOLE),
        (where, SCALAR),
    ]
    du_mix, last_own, last_far, last_pair, last_owned = blocked_call(
        functools.partial(settle_grads_kernel, quarter=quarter),
        "settle_grads",
        count,
        [
            settled[0],
            (normed_all, pieces(width)),
            (inner, by_rows(3 * low_rank)),
            (table, by_rows(8)),
            *settled[1:],
            (column_sets, WHOLE),
            (up_qk, WHOLE),
            (up_vg, part(low_rank, 0)),
            (mixer_down_late, WHOLE),
            (branch_res_grad, WHOLE),
        ],
        [
            ((count, 3 * low_rank), bfloat, "rows"),
            ((low_rank, 5 * block_width), bfloat, "whole"),
            ((low_rank, 5 * block_width), bfloat, "whole"),
            ((2 * low_rank, 5 * block_width), bfloat, "whole"),
            ((low_rank, 2 * qk + value_lanes), bfloat, "whole"),
        ],
        [
            pltpu.VMEM((STEP, 2 * qk + value_lanes), bfloat),
            pltpu.VMEM((3 * low_rank, width), single),
            pltpu.VMEM((low_rank, 2 * qk + value_lanes), single),
        ],
        count * 4_000_000,
    )
    last_own, last_far = near_sum((last_own, last_far, last_pair))
    last_far, gate_grad = tie(last_far, gate_grad)
    (normed_part,) = blocked_call(
        functools.partial(settle_kernel, quarter=quarter),
        "settle",
        count,
        [
            settled[0],
            (gate_grad, by_rows(value_lanes)),
            (du_mix, by_rows(3 * low_rank)),
            (du_outgate, by_rows(low_rank)),
            (mix_grad, by_rows(8)),
            *settled[1:],
            (down, part(4 * low_rank, 0)),
            (weight_mix, WHOLE),
            (w_query, WHOLE),
            (w_key, WHOLE),
            (w_value, WHOLE),
            (w_gate_out, WHOLE),
        ],
        [((count, width), bfloat, "parts")],
        [
            pltpu.VMEM((STEP, 2 * qk + value_lanes), bfloat),
            pltpu.VMEM((width, 2 * qk + 2 * value_lanes), bfloat),
            pltpu.VMEM((5 * low_rank, width), bfloat),
        ],
        count * 10_000_000,
    )
    last_flat = jnp.concatenate([low(far_sum(last_own, last_far)), last_owned], axis=1)
    feed_rows = all_rows(both)
    last_lanes = last_flat.shape[1]
    both = exchange(jnp.concatenate([seq_rows(last_flat), share_sum(later_parts)], axis=2))
    normed_own, normed_sum_far = near_sum(normed_part)
    both, normed_sum_far = tie(both, normed_sum_far)
    normed_landed = flip(normed_sum_far, 2)
    branch_rows = all_rows(both)
    feed_piece = branch_rows[:, last_lanes : last_lanes + 3 * block_width]
    feed_piece_far = flip(feed_piece, 2)
    last_parts = both[:, :, :last_lanes]
    last_rows = all_rows(exchange(share_sum(last_parts)))
    piece = last_rows[:, : 5 * block_width]
    piece_far = flip(piece, 2)
    normed_landed, feed_piece_far, _ = tie(normed_landed, feed_piece_far, piece)
    feed_pieces = [feed_piece, flip(feed_piece, 1), feed_piece_far, flip(feed_piece_far, 1)]
    normed_grad = normed_own + normed_landed.astype(single)
    input_grad = residual_grad + rms_back(input_float, norm1_gain, normed_grad)
    piece_far, input_grad, feed_pieces[3] = tie(piece_far, input_grad, feed_pieces[3])
    last_pieces = [piece, flip(piece, 1), piece_far, flip(piece_far, 1)]
    down_grad, qk_grad, vg_grad, ff_grads, out_grads, ffd_grads, res_grad = assemble(
        where,
        [*last_pieces, *feed_pieces],
        last_rows,
        feed_rows,
        branch_rows,
        padded,
        [
            (6, low_rank, width),
            (2, low_rank, qk),
            (2, low_rank, value_lanes),
            (2, low_rank, hidden_width),
            (low_rank, value_lanes),
            (low_rank, hidden_width),
            (2, low_rank, width),
        ],
    )

    def as_down(rows):
        return rows.reshape(rows.shape[:-2] + (sets, rank, -1)).swapaxes(-1, -2)

    def as_up(rows):
        return rows.reshape(rows.shape[0], sets, rank, -1)

    return (
        low(result),
        input_grad,
        as_down(down_grad),
        as_up(qk_grad),
        as_up(vg_grad),
        as_up(ff_grads),
        as_down(out_grads),
        as_down(ffd_grads),
        as_up(res_grad),
    )


def solution(mesh):
    rows = P(("seq", "head"), None)
    lanes = P(None, "head")
    last = P(None, None, None, "head")
    middle = P(None, "head", None)
    in_specs = (
        rows, rows, P(), P(), P(), lanes, lanes, lanes, lanes, lanes, lanes,
        P(None, None, "head"), P("head"), P("head"), lanes, P(), P("head", None), P(), lanes,
        lanes, P("head", None), P(), last, last, last, middle, middle, P(),
    )
    out_specs = (rows, rows, P(), last, last, last, middle, middle, P())
    return jax.shard_map(
        on_device, mesh=mesh, in_specs=in_specs, out_specs=out_specs, check_vma=False
    )
```

```python
import functools

import jax
import jax.numpy as jnp
from jax import lax
from jax.experimental import pallas as pl
from jax.experimental.pallas import tpu as pltpu
from jax.sharding import PartitionSpec as P

CHUNK = 128
STEP = 256
HALO = 16
DOC_MAX = 4096
EPS = 1e-06
VMEM_LIMIT = 56 * 1024 * 1024
bfloat = jnp.bfloat16
single = jnp.float32


def contract(left, right, left_dim, right_dim):
    return lax.dot_general(
        left,
        right,
        (((left_dim,), (right_dim,)), ((), ())),
        preferred_element_type=single,
    )


def nn(left, right):
    return contract(left, right, 1, 0)


def nt(left, right):
    return contract(left, right, 1, 1)


def tn(left, right):
    return contract(left, right, 0, 0)


def low(array):
    return array.astype(bfloat)


def iotas():
    rows = lax.broadcasted_iota(jnp.int32, (CHUNK, CHUNK), 0)
    columns = lax.broadcasted_iota(jnp.int32, (CHUNK, CHUNK), 1)
    return rows, columns


def split_two(array):
    high = low(array)
    return high, low(array - high.astype(single))


def near_exact(left, right):
    left_high, left_low = split_two(left)
    right_high, right_low = split_two(right)
    return nn(
        jnp.concatenate([left_high, left_high, left_low], axis=1),
        jnp.concatenate([right_high, right_low, right_high], axis=0),
    )


def ones_product(ones, array):
    high = low(array)
    rest = array - high.astype(single)
    middle = low(rest)
    lowest = low(rest - middle.astype(single))
    return nn(
        jnp.concatenate([ones, ones, ones], axis=1),
        jnp.concatenate([high, middle, lowest], axis=0),
    )


def unit_lower_inverses(stricts, rows, columns):
    eye = (rows == columns).astype(single)
    differ = rows ^ columns
    block = 8
    inner = [jnp.where(differ < block, strict, 0.0) for strict in stricts]
    second = [near_exact(a, a) for a in inner]
    inverse = [near_exact(eye - a, eye + b) for a, b in zip(inner, second)]
    fourth = [near_exact(b, b) for b in second]
    inverse = [near_exact(a, eye + b) for a, b in zip(inverse, fourth)]
    while block < CHUNK:
        between = (differ >= block) & (differ < 2 * block)
        off = [jnp.where(between, strict, 0.0) for strict in stricts]
        part = [near_exact(a, b) for a, b in zip(off, inverse)]
        inverse = [a - near_exact(a, b) for a, b in zip(inverse, part)]
        block = 2 * block
    return inverse


def softplus(value):
    return jnp.maximum(value, 0.0) + jnp.log(1.0 + jnp.exp(-jnp.abs(value)))


def sigmoid(value):
    return 1.0 / (1.0 + jnp.exp(-value))


def gates(decay, start, rows, columns):
    lower_ones = low((rows >= columns).astype(single))
    total = ones_product(lower_ones, jnp.broadcast_to(decay, (CHUNK, CHUNK)))
    linked = (rows >= columns) & (columns >= start)
    within = jnp.where(linked, jnp.exp(jnp.where(linked, total - total.T, 0.0)), 0.0)
    running = total[:, :1]
    carried = jnp.where(start < 0, jnp.exp(running), 0.0)
    last = running[CHUNK - 1 : CHUNK]
    ending = jnp.where(
        rows[:, :1] >= start[CHUNK - 1 : CHUNK], jnp.exp(jnp.minimum(last - running, 0.0)), 0.0
    )
    return within, carried, ending


def convolved(window, starts, weights, base):
    positions = base + lax.broadcasted_iota(jnp.int32, (STEP, 1), 0)
    taps = weights.shape[0]
    total = None
    for tap in range(taps):
        back = taps - 1 - tap
        term = window[HALO - back : HALO - back + STEP, :] * weights[tap : tap + 1, :]
        if back:
            term = jnp.where(positions - back >= starts, term, 0.0)
        total = term if total is None else total + term
    return total


def head_scales(rows, width):
    return lax.rsqrt(jnp.sum(rows * rows, axis=-1, keepdims=True) + EPS)


def forward_kernel(
    place,
    rows_ref,
    halo_ref,
    column_ref,
    weight_ref,
    scalar_ref,
    out_ref,
    map_ref,
    written_ref,
    state_ref,
    inverse_ref,
    end_ref,
    sent_ref,
    sent_state_ref,
    window,
    state,
    *,
    heads,
    key_width,
    value_width,
):
    step = pl.program_id(0)
    wide = value_width + key_width
    base = step * STEP
    rows, columns = iotas()

    @pl.when(step == 0)
    def _():
        window[0:HALO, :] = halo_ref[...].astype(single)
        for h in range(heads):
            state[h, :, :value_width] = jnp.zeros((key_width, value_width), single)
            state[h, :, value_width:] = (rows == columns).astype(single)

    @pl.when(step > 0)
    def _():
        window[0:HALO, :] = window[STEP : STEP + HALO, :]

    window[HALO:, :] = rows_ref[...].astype(single)
    info = column_ref[...]
    starts = info[:, 2 * heads : 2 * heads + 1].astype(jnp.int32)
    before = convolved(window, starts, weight_ref[...], base)
    active = before * sigmoid(before)
    qk_lanes = heads * key_width
    chunks = STEP // CHUNK
    local, stricts = [], []
    for c in range(chunks):
        span = slice(c * CHUNK, (c + 1) * CHUNK)
        for h in range(heads):
            query = active[span, h * key_width : (h + 1) * key_width]
            key = active[span, qk_lanes + h * key_width : qk_lanes + (h + 1) * key_width]
            value = active[
                span, 2 * qk_lanes + h * value_width : 2 * qk_lanes + (h + 1) * value_width
            ]
            query = query * (head_scales(query, key_width) * key_width ** (-0.5))
            key = key * head_scales(key, key_width)
            beta = sigmoid(info[span, h : h + 1])
            decay = -scalar_ref[0, h] * softplus(
                info[span, heads + h : heads + h + 1] + scalar_ref[1, h]
            )
            within, carried, ending = gates(
                decay, starts[span] - (base + c * CHUNK), rows, columns
            )
            query, key = low(query), low(key)
            strict = jnp.where(rows > columns, within * nt(key, key), 0.0) * beta
            mixed = low(within * nt(query, key))
            stricts.append(strict)
            local.append((query, key, value, beta, carried, ending, mixed))
    inverses = [low(a) for a in unit_lower_inverses(stricts, rows, columns)]
    each = range(heads)
    now = [state[h] for h in each]
    for c in range(chunks):
        span = slice(c * CHUNK, (c + 1) * CHUNK)
        here = [local[c * heads + h] for h in each]
        inverse = [inverses[c * heads + h] for h in each]
        now_low = [low(a) for a in now]
        read = [nn(here[h][1], now_low[h]) for h in each]
        asked = [nn(here[h][0], now_low[h]) for h in each]
        target = []
        for h in each:
            query, key, value, beta, carried, ending, mixed = here[h]
            gap = -(carried * beta) * read[h]
            target.append(
                jnp.concatenate(
                    [beta * value + gap[:, :value_width], gap[:, value_width:]], axis=1
                )
            )
        written = [nn(inverse[h], low(target[h])) for h in each]
        added = [tn(here[h][1], low(here[h][5] * written[h])) for h in each]
        inner = [nn(here[h][6], low(written[h])) for h in each]
        for h in each:
            carried = here[h][4]
            inverse_ref[span, h * CHUNK : (h + 1) * CHUNK] = inverse[h]
            state_ref[c, h] = now_low[h]
            written_ref[span, h * wide : (h + 1) * wide] = low(written[h])
            output = carried * asked[h] + inner[h]
            out_ref[span, h * value_width : (h + 1) * value_width] = output[:, :value_width]
            map_ref[span, h * key_width : (h + 1) * key_width] = low(output[:, value_width:])
        now = [here[h][4][CHUNK - 1 : CHUNK] * now[h] + added[h] for h in each]
    for h in each:
        state[h] = now[h]

    @pl.when(step == pl.num_programs(0) - 1)
    def _():
        final = state[...]
        end_ref[...] = final
        sent_ref[...] = low(final)
        sent_state_ref[...] = low(final[:, :, :value_width])


def backward_kernel(
    place,
    rows_ref,
    before_ref,
    halo_ref,
    column_ref,
    weight_ref,
    scalar_ref,
    grad_ref,
    written_ref,
    state_ref,
    inverse_ref,
    end_ref,
    entering_ref,
    *rest,
    hops,
    heads,
    key_width,
    value_width,
):
    got_refs, rest = rest[:hops], rest[hops:]
    out_ref, mix_ref, tail_ref, edge_ref, window, shifted, shifted_start, cotangent, ahead = rest
    step = pl.program_id(0)
    steps = pl.num_programs(0)
    wide = value_width + key_width
    base = (steps - 1 - step) * STEP
    rows, columns = iotas()
    qk_lanes = heads * key_width
    lanes = window.shape[1]
    taps = weight_ref.shape[0]

    @pl.when(step == 0)
    def _():
        shifted[STEP : STEP + 8, :] = jnp.zeros((8, lanes), single)
        shifted_start[STEP : STEP + 8, :] = jnp.zeros((8, 1), jnp.int32)
        for h in range(heads):
            passed = got_refs[0][h].astype(single)
            for hop in range(1, hops):
                passed = passed + got_refs[hop][h].astype(single)
            cotangent[h] = passed
            ahead[h] = end_ref[h, :, :value_width] + nn(
                low(end_ref[h, :, value_width:]), low(entering_ref[h])
            )

    @pl.when(step > 0)
    def _():
        shifted[STEP : STEP + 8, :] = shifted[0:8, :]
        shifted_start[STEP : STEP + 8, :] = shifted_start[0:8, :]

    window[0:HALO, :] = jnp.where(
        step == steps - 1, halo_ref[...].astype(single), before_ref[...].astype(single)
    )
    window[HALO:, :] = rows_ref[...].astype(single)
    info = column_ref[...]
    starts = info[:, 2 * heads : 2 * heads + 1].astype(jnp.int32)
    positions = base + lax.broadcasted_iota(jnp.int32, (STEP, 1), 0)
    before = convolved(window, starts, weight_ref[...], base)
    gate = sigmoid(before)
    active = before * gate
    slope = gate * (1.0 + before * (1.0 - gate))
    upper_ones = low((rows <= columns).astype(single))
    last_row = rows[:, :1] == CHUNK - 1
    chunks = STEP // CHUNK
    each = range(heads)
    items = [(c, h) for c in range(chunks) for h in each]
    spans = {item: slice(item[0] * CHUNK, (item[0] + 1) * CHUNK) for item in items}
    entering = [low(entering_ref[h]) for h in each]
    root = key_width ** (-0.5)

    def per(function):
        return {item: function(*item) for item in items}

    def q_lanes(h):
        return slice(h * key_width, (h + 1) * key_width)

    def k_lanes(h):
        return slice(qk_lanes + h * key_width, qk_lanes + (h + 1) * key_width)

    def v_lanes(h):
        return slice(2 * qk_lanes + h * value_width, 2 * qk_lanes + (h + 1) * value_width)

    def kept(c, h, part):
        return written_ref[spans[c, h], h * wide : (h + 1) * wide][:, part]

    values, maps = slice(0, value_width), slice(value_width, wide)
    query_raw = per(lambda c, h: active[spans[c, h], q_lanes(h)])
    key_raw = per(lambda c, h: active[spans[c, h], k_lanes(h)])
    query_scale = per(lambda c, h: head_scales(query_raw[c, h], key_width))
    key_scale = per(lambda c, h: head_scales(key_raw[c, h], key_width))
    query = per(lambda c, h: query_raw[c, h] * (query_scale[c, h] * root))
    key = per(lambda c, h: key_raw[c, h] * key_scale[c, h])
    query_low = per(lambda c, h: low(query[c, h]))
    key_low = per(lambda c, h: low(key[c, h]))
    beta = per(lambda c, h: sigmoid(info[spans[c, h], h : h + 1]))
    raw = per(lambda c, h: info[spans[c, h], heads + h : heads + h + 1] + scalar_ref[1, h])
    gated = per(
        lambda c, h: gates(
            -scalar_ref[0, h] * softplus(raw[c, h]),
            starts[spans[c, h]] - (base + c * CHUNK),
            rows,
            columns,
        )
    )
    within = per(lambda c, h: gated[c, h][0])
    carried = per(lambda c, h: gated[c, h][1])
    ending = per(lambda c, h: gated[c, h][2])
    mixed = per(lambda c, h: low(within[c, h] * nt(query_low[c, h], key_low[c, h])))
    written = per(
        lambda c, h: kept(c, h, values).astype(single) + nn(kept(c, h, maps), entering[h])
    )
    start_state = per(
        lambda c, h: state_ref[c, h][:, values].astype(single)
        + nn(state_ref[c, h][:, maps], entering[h])
    )
    written_low = per(lambda c, h: low(written[c, h]))
    start_low = per(lambda c, h: low(start_state[c, h]))
    grad = per(lambda c, h: grad_ref[spans[c, h], h * value_width : (h + 1) * value_width])
    grad_low = grad
    carried_grad = per(lambda c, h: low(carried[c, h] * grad[c, h].astype(single)))
    from_output = per(lambda c, h: tn(mixed[c, h], grad_low[c, h]))
    state_part = per(lambda c, h: tn(query_low[c, h], carried_grad[c, h]))
    mixed_grad = per(lambda c, h: low(within[c, h] * nt(grad_low[c, h], written_low[c, h])))
    query_grad = per(
        lambda c, h: nt(carried_grad[c, h], start_low[c, h]) + nn(mixed_grad[c, h], key_low[c, h])
    )
    key_write = per(lambda c, h: tn(mixed_grad[c, h], query_low[c, h]))
    later, later_low, solved, value_grad, read_grad = {}, {}, {}, {}, {}
    now = [cotangent[h] for h in each]
    for c in reversed(range(chunks)):
        for h in each:
            later[c, h], later_low[c, h] = now[h], low(now[h])
        from_state = [nn(key_low[c, h], later_low[c, h]) for h in each]
        written_grad = [low(from_output[c, h] + ending[c, h] * from_state[h]) for h in each]
        for h in each:
            inverse = inverse_ref[spans[c, h], h * CHUNK : (h + 1) * CHUNK]
            solved[c, h] = tn(inverse, written_grad[h])
        for h in each:
            value_grad[c, h] = beta[c, h] * solved[c, h]
            read_grad[c, h] = low(-carried[c, h] * value_grad[c, h])
        now = [
            carried[c, h][CHUNK - 1 : CHUNK] * now[h]
            + state_part[c, h]
            + tn(key_low[c, h], read_grad[c, h])
            for h in each
        ]
    following = {
        (c, h): start_state[c + 1, h] if c + 1 < chunks else ahead[h] for c, h in items
    }
    at_end = per(lambda c, h: jnp.sum(later[c, h] * following[c, h], keepdims=True))
    for h in each:
        cotangent[h] = now[h]
        ahead[h] = start_state[0, h]
    strict_grad = per(
        lambda c, h: low(
            jnp.where(
                rows > columns, -within[c, h] * nt(low(value_grad[c, h]), written_low[c, h]), 0.0
            )
        )
    )
    key_read = per(
        lambda c, h: nt(read_grad[c, h], start_low[c, h]) + nn(strict_grad[c, h], key_low[c, h])
    )
    key_write = per(
        lambda c, h: key_write[c, h]
        + tn(strict_grad[c, h], key_low[c, h])
        + nt(low(ending[c, h] * written[c, h]), later_low[c, h])
    )
    query_dot = per(
        lambda c, h: jnp.sum(query[c, h] * query_grad[c, h], axis=-1, keepdims=True)
    )
    running_grad = per(
        lambda c, h: query_dot[c, h]
        + jnp.sum(key[c, h] * (key_read[c, h] - key_write[c, h]), axis=-1, keepdims=True)
        + jnp.where(last_row, at_end[c, h], 0.0)
    )
    decay_sum = per(
        lambda c, h: ones_product(
            upper_ones, jnp.broadcast_to(running_grad[c, h], (CHUNK, CHUNK))
        )[:, :1]
    )
    decay_grad = per(
        lambda c, h: jnp.where(
            positions[spans[c, h]] == starts[spans[c, h]],
            0.0,
            -scalar_ref[0, h] * sigmoid(raw[c, h]) * decay_sum[c, h],
        )
    )
    beta_grad = per(
        lambda c, h: jnp.sum(solved[c, h] * written[c, h], axis=-1, keepdims=True)
        * sigmoid(-info[spans[c, h], h : h + 1])
    )
    for c, h in items:
        span = spans[c, h]
        key_grad = key_read[c, h] + key_write[c, h]
        key_dot = jnp.sum(key[c, h] * key_grad, axis=-1, keepdims=True)
        query_active = (query_scale[c, h] * root) * query_grad[c, h] - query_raw[c, h] * (
            query_scale[c, h] * query_scale[c, h] * query_dot[c, h]
        )
        key_active = key_scale[c, h] * (key_grad - key[c, h] * key_dot)
        shifted[span, q_lanes(h)] = query_active * slope[span, q_lanes(h)]
        shifted[span, k_lanes(h)] = key_active * slope[span, k_lanes(h)]
        shifted[span, v_lanes(h)] = value_grad[c, h] * slope[span, v_lanes(h)]
    for c in range(chunks):
        mix_ref[c * CHUNK : (c + 1) * CHUNK, :] = jnp.concatenate(
            [beta_grad[c, h] for h in each]
            + [decay_grad[c, h] for h in each]
            + [jnp.zeros((CHUNK, mix_ref.shape[1] - 2 * heads), single)],
            axis=1,
        )
    shifted_start[0:STEP, :] = starts
    def collect(index, _):
        lanes_here = pl.ds(pl.multiple_of(index * 256, 256), 256)
        total = None
        for tap in range(taps):
            back = taps - 1 - tap
            term = shifted[back : back + STEP, lanes_here] * weight_ref[tap : tap + 1, lanes_here]
            if back:
                term = jnp.where(positions >= shifted_start[back : back + STEP, :], term, 0.0)
            total = term if total is None else total + term
        out_ref[:, lanes_here] = low(total)

        @pl.when(step == 0)
        def _():
            tail_ref[:, lanes_here] = total[STEP - HALO :, :]

        return 0

    lax.fori_loop(0, lanes // 256, collect, 0)

    @pl.when(step == steps - 1)
    def _():
        window[0:8, :] = jnp.zeros((8, lanes), single)
        window[8:16, :] = shifted[0:8, :]
        early = lax.broadcasted_iota(jnp.int32, (8, 1), 0) - 8
        collected = jnp.zeros((8, lanes), single)
        for tap in range(taps - 1):
            back = taps - 1 - tap
            reader = early + back
            reader_start = jnp.zeros((8, 1), jnp.int32)
            for t in range(back):
                reader_start = jnp.where(reader == t, shifted_start[t : t + 1, :], reader_start)
            term = window[back : back + 8, :] * weight_ref[tap : tap + 1, :]
            collected = collected + jnp.where(
                (reader >= 0) & (early >= reader_start), term, 0.0
            )
        edge_ref[0:8, :] = jnp.zeros((8, lanes), single)
        edge_ref[8:16, :] = collected


def block_place(step, place, per_quarter):
    return ((step // per_quarter) ^ place[0]) * per_quarter + step % per_quarter


def run_forward(place, rows, halo, columns, weights, scalars, heads, key_width, value_width, quarter):
    count, lanes = columns.shape[0], rows.shape[1]
    steps, per_quarter = count // STEP, quarter // STEP
    wide = value_width + key_width
    chunks = STEP // CHUNK
    at = lambda i, place: (block_place(i, place, per_quarter), 0)
    fixed = lambda i, place: (0, 0)
    body = functools.partial(
        forward_kernel, heads=heads, key_width=key_width, value_width=value_width
    )
    shapes = (
        jax.ShapeDtypeStruct((count, heads * value_width), single),
        jax.ShapeDtypeStruct((count, heads * key_width), bfloat),
        jax.ShapeDtypeStruct((count, heads * wide), bfloat),
        jax.ShapeDtypeStruct((count // CHUNK, heads, key_width, wide), bfloat),
        jax.ShapeDtypeStruct((count, heads * CHUNK), bfloat),
        jax.ShapeDtypeStruct((heads, key_width, wide), single),
        jax.ShapeDtypeStruct((heads, key_width, wide), bfloat),
        jax.ShapeDtypeStruct((heads, key_width, value_width), bfloat),
    )
    return pl.pallas_call(
        body,
        out_shape=shapes,
        grid_spec=pltpu.PrefetchScalarGridSpec(
            num_scalar_prefetch=1,
            grid=(steps,),
            in_specs=[
                pl.BlockSpec((STEP, lanes), at),
                pl.BlockSpec((HALO, lanes), lambda i, place: (0, 0)),
                pl.BlockSpec((STEP, columns.shape[1]), at),
                pl.BlockSpec(weights.shape, fixed),
                pl.BlockSpec(memory_space=pltpu.SMEM),
            ],
            out_specs=[
                pl.BlockSpec((STEP, heads * value_width), at),
                pl.BlockSpec((STEP, heads * key_width), at),
                pl.BlockSpec((STEP, heads * wide), at),
                pl.BlockSpec((chunks, heads, key_width, wide), lambda i, place: (i, 0, 0, 0)),
                pl.BlockSpec((STEP, heads * CHUNK), at),
                pl.BlockSpec((heads, key_width, wide), lambda i, place: (0, 0, 0)),
                pl.BlockSpec((heads, key_width, wide), lambda i, place: (0, 0, 0)),
                pl.BlockSpec((heads, key_width, value_width), lambda i, place: (0, 0, 0)),
            ],
            scratch_shapes=[
                pltpu.VMEM((STEP + HALO, lanes), single),
                pltpu.VMEM((heads, key_width, wide), single),
            ],
        ),
        compiler_params=pltpu.CompilerParams(
            dimension_semantics=("arbitrary",), vmem_limit_bytes=VMEM_LIMIT
        ),
        cost_estimate=pl.CostEstimate(
            flops=count * 2_000_000, bytes_accessed=count * 10_000, transcendentals=count * 2000
        ),
        name="delta_forward",
    )(place, rows, halo, columns, weights, scalars)


def run_backward(
    place, rows, halo, columns, weights, scalars, grad, saved, entering, got, heads,
    key_width, value_width, quarter,
):
    written, states, inverses, end = saved
    count, lanes = columns.shape[0], rows.shape[1]
    steps, per_quarter = count // STEP, quarter // STEP
    wide = value_width + key_width
    chunks = STEP // CHUNK

    def at(i, place):
        return (block_place(steps - 1 - i, place, per_quarter), 0)

    def halo_at(i, place):
        here = steps - 1 - i
        inner = block_place(jnp.maximum(here - 1, 0), place, per_quarter)
        ratio = STEP // HALO
        return (inner * ratio + ratio - 1, 0)

    fixed = lambda i, place: (0, 0)
    whole = lambda i, place: (0, 0, 0)
    body = functools.partial(
        backward_kernel,
        hops=len(got),
        heads=heads,
        key_width=key_width,
        value_width=value_width,
    )
    shapes = (
        jax.ShapeDtypeStruct((count, lanes), bfloat),
        jax.ShapeDtypeStruct((count, columns.shape[1]), single),
        jax.ShapeDtypeStruct((HALO, lanes), single),
        jax.ShapeDtypeStruct((HALO, lanes), single),
    )
    return pl.pallas_call(
        body,
        out_shape=shapes,
        grid_spec=pltpu.PrefetchScalarGridSpec(
            num_scalar_prefetch=1,
            grid=(steps,),
            in_specs=[
                pl.BlockSpec((STEP, lanes), at),
                pl.BlockSpec((HALO, lanes), halo_at),
                pl.BlockSpec((HALO, lanes), fixed),
                pl.BlockSpec((STEP, columns.shape[1]), at),
                pl.BlockSpec(weights.shape, fixed),
                pl.BlockSpec(memory_space=pltpu.SMEM),
                pl.BlockSpec((STEP, heads * value_width), at),
                pl.BlockSpec((STEP, heads * wide), at),
                pl.BlockSpec(
                    (chunks, heads, key_width, wide), lambda i, place: (steps - 1 - i, 0, 0, 0)
                ),
                pl.BlockSpec((STEP, heads * CHUNK), at),
                pl.BlockSpec(end.shape, whole),
                pl.BlockSpec(entering.shape, whole),
            ]
            + [pl.BlockSpec(part.shape, whole) for part in got],
            out_specs=[
                pl.BlockSpec((STEP, lanes), at),
                pl.BlockSpec((STEP, columns.shape[1]), at),
                pl.BlockSpec((HALO, lanes), fixed),
                pl.BlockSpec((HALO, lanes), fixed),
            ],
            scratch_shapes=[
                pltpu.VMEM((STEP + HALO, lanes), single),
                pltpu.VMEM((STEP + 8, lanes), single),
                pltpu.VMEM((STEP + 8, 1), jnp.int32),
                pltpu.VMEM((heads, key_width, value_width), single),
                pltpu.VMEM((heads, key_width, value_width), single),
            ],
        ),
        compiler_params=pltpu.CompilerParams(
            dimension_semantics=("arbitrary",), vmem_limit_bytes=VMEM_LIMIT
        ),
        cost_estimate=pl.CostEstimate(
            flops=count * 3_000_000, bytes_accessed=count * 12_000, transcendentals=count * 3000
        ),
        name="delta_backward",
    )(
        place, rows, rows, halo, columns, weights, scalars, grad, written, states, inverses, end,
        entering, *got,
    )


def chosen_columns(table, column_sets):
    return column_sets[0:1, :] == table[:, 1:2]


def masked(product, chosen):
    return low(jnp.where(chosen, product, 0.0))


def silu_parts(value):
    logistic = sigmoid(value)
    return logistic, value * logistic


def accumulate(ref, value, first):
    if first is True:
        ref[...] = value
    else:
        ref[...] = jnp.where(first, value, ref[...] + value)


def emit_blocks(parts, place, own_ref, far_ref, pair_ref):
    for k, part in enumerate(parts):
        rows, size = part.shape[0], part.shape[1] // 4
        lanes = slice(k * size, (k + 1) * size)
        for relative, target, row in (
            (0, own_ref, 0), (2, far_ref, 0), (1, pair_ref, 0), (3, pair_ref, rows)
        ):
            start = pl.multiple_of((place ^ relative) * size, 128)
            target[row : row + rows, lanes] = low(part[:, pl.ds(start, size)])


def copy_rows(target, row, source, lanes=slice(None)):
    size = 16

    def run(index, _):
        start = pl.multiple_of(index * size, size)
        target[pl.ds(pl.multiple_of(row + start, size), size), lanes] = source[pl.ds(start, size), :]
        return 0

    lax.fori_loop(0, source.shape[0] // size, run, 0)


def at_end(fill):
    pl.when(pl.program_id(0) == pl.num_programs(0) - 1)(fill)


def at_start(fill):
    pl.when(pl.program_id(0) == 0)(fill)


def project_kernel(
    rows_ref, table_ref, sets_ref, down_ref, mix_ref, wq_ref, wk_ref, wv_ref, wg_ref, up_qk_ref,
    up_vg_ref, *rest, with_halo,
):
    low_rank = sets_ref.shape[1]
    width, q_width = wq_ref.shape
    v_width = wv_ref.shape[1]
    bounds = [0, q_width, 2 * q_width, 2 * q_width + v_width, 2 * q_width + 2 * v_width]
    if with_halo:
        halo_ref, halo_table_ref, *rest = rest
        pre_ref, inner_ref, column_ref, gate_ref, inner_gate_ref, pre_halo_ref, joined = rest
    else:
        pre_ref, inner_ref, column_ref, gate_ref, inner_gate_ref, joined = rest
    weights = (wq_ref, wk_ref, wv_ref, wg_ref)
    ups = (
        up_qk_ref.at[0],
        up_qk_ref.at[1],
        up_vg_ref.at[:low_rank],
        up_vg_ref.at[low_rank:],
    )

    @at_start
    def _():
        for p in range(4):
            columns = slice(bounds[p], bounds[p + 1])
            copy_rows(joined, 0, weights[p], columns)
            copy_rows(joined, width, ups[p], columns)

    rows, table = rows_ref[...], table_ref[...]
    count = rows.shape[0]
    if with_halo:
        rows = jnp.concatenate([rows, halo_ref[...]], axis=0)
        table = jnp.concatenate([table, halo_table_ref[...]], axis=0)
    chosen = chosen_columns(table, sets_ref[...])
    product = nt(rows, down_ref[...])
    inner = [masked(product[:, p * low_rank : (p + 1) * low_rank], chosen) for p in range(4)]
    for p in range(4):
        columns = slice(bounds[p], bounds[p + 1])
        output = nn(jnp.concatenate([rows, inner[p]], axis=1), joined[:, columns])
        if p == 3:
            gate_ref[...] = output[:count]
            inner_gate_ref[...] = inner[p][:count]
            continue
        pre_ref[:, columns] = low(output[:count])
        if with_halo:
            pre_halo_ref[:, columns] = low(output[count:])
        inner_ref[:, p * low_rank : (p + 1) * low_rank] = inner[p][:count]
    column_ref[...] = jnp.concatenate(
        [nt(rows[:count], mix_ref[...])[:, :4], table[:count, :4]], axis=1
    )


def head_outputs(raw_ref, map_ref, entering_ref, heads, key_width, value_width):
    outputs = []
    for h in range(heads):
        outputs.append(
            raw_ref[:, h * value_width : (h + 1) * value_width]
            + nn(map_ref[:, h * key_width : (h + 1) * key_width], entering_ref[h])
        )
    return outputs


def attend_kernel(
    raw_ref, map_ref, gate_ref, table_ref, gain_ref, sets_ref, wo_ref, down_ref, up_ref, *rest,
    heads, key_width, value_width, hops,
):
    got_refs, rest = rest[:hops], rest[hops:]
    part_ref, z_ref, inner_ref, entering_ref, joined = rest
    value_lanes = wo_ref.shape[0]

    @at_start
    def _():
        copy_rows(joined, 0, wo_ref)
        copy_rows(joined, value_lanes, up_ref)
        for h in range(heads):
            state = got_refs[hops - 1][h].astype(single)
            for hop in range(hops - 1, 0, -1):
                got = got_refs[hop - 1][h]
                state = got[:, :value_width].astype(single) + nn(got[:, value_width:], low(state))
            entering_ref[h] = low(state)

    chosen = chosen_columns(table_ref[...], sets_ref[...])
    outputs = head_outputs(raw_ref, map_ref, entering_ref, heads, key_width, value_width)
    parts = []
    for h, output in enumerate(outputs):
        lanes = slice(h * value_width, (h + 1) * value_width)
        scale = lax.rsqrt(jnp.mean(output * output, axis=-1, keepdims=True) + EPS)
        _, gate = silu_parts(gate_ref[:, lanes])
        parts.append(low(output * scale * gain_ref[0:1, :] * gate))
    z = jnp.concatenate(parts, axis=1)
    z_ref[...] = z
    inner = masked(nt(z, down_ref[...]), chosen)
    inner_ref[...] = inner
    part_ref[...] = low(nn(jnp.concatenate([z, inner], axis=1), joined[...]))


def feed_before_kernel(
    grad_ref, table_ref, sets_ref, wd_ref, down_ffd_t_ref, up_ref, hidden_grad_ref, du_ref, joined
):
    hidden, width = wd_ref.shape

    @at_start
    def _():
        copy_rows(joined, 0, wd_ref, slice(0, width))
        copy_rows(joined, 0, down_ffd_t_ref, slice(width, None))
        joined[hidden:, :] = jnp.zeros((joined.shape[0] - hidden, joined.shape[1]), bfloat)

    grad = grad_ref[...]
    du_down = masked(nt(grad, up_ref[...]), chosen_columns(table_ref[...], sets_ref[...]))
    du_ref[...] = du_down
    hidden_grad_ref[...] = nt(jnp.concatenate([grad, du_down], axis=1), joined[...])


def feed_kernel(
    rows_ref, hidden_grad_ref, table_ref, sets_ref, down_ref, wg_ref, wu_ref, up_t_ref, up_ref,
    back_ref, hidden_ref, ff_grad_ref, inner_ref, du_ref,
    joined_gate, joined_up, joined_back,
):
    low_rank = sets_ref.shape[1]
    hidden, width = wg_ref.shape
    padded = joined_gate.shape[0]

    @at_start
    def _():
        for p, (joined, weight) in enumerate(((joined_gate, wg_ref), (joined_up, wu_ref))):
            copy_rows(joined, 0, weight, slice(0, width))
            copy_rows(joined, 0, up_t_ref.at[p], slice(width, None))
            joined[hidden:, :] = jnp.zeros((padded - hidden, joined.shape[1]), bfloat)
            copy_rows(joined_back, p * padded, weight)
            joined_back[p * padded + hidden : (p + 1) * padded, :] = jnp.zeros(
                (padded - hidden, width), bfloat
            )
        copy_rows(joined_back, 2 * padded, down_ref)

    chosen = chosen_columns(table_ref[...], sets_ref[...])
    both = jnp.concatenate([chosen, chosen], axis=1)
    rows = rows_ref[...]
    inner = masked(nt(rows, down_ref[...]), both)
    inner_ref[...] = inner
    gate = nt(jnp.concatenate([rows, inner[:, :low_rank]], axis=1), joined_gate[...])
    up = nt(jnp.concatenate([rows, inner[:, low_rank:]], axis=1), joined_up[...])
    logistic, active = silu_parts(gate)
    hidden_ref[...] = low(active * up)
    hidden_grad = hidden_grad_ref[...]
    gate_grad = low(hidden_grad * up * logistic * (1.0 + gate * (1.0 - logistic)))
    up_grad = low(hidden_grad * active)
    du_gate = masked(nt(gate_grad, up_ref[0]), chosen)
    du_up = masked(nt(up_grad, up_ref[1]), chosen)
    du_ref[:, :low_rank] = du_gate
    du_ref[:, low_rank:] = du_up
    ff_grad_ref[:, :padded] = gate_grad
    ff_grad_ref[:, padded:] = up_grad
    back_ref[...] = low(
        nn(jnp.concatenate([gate_grad, up_grad, du_gate, du_up], axis=1), joined_back[...])
    )


def feed_after_kernel(
    rows_ref, grad_ref, hidden_ref, ff_grad_ref, inner_ref, du_ref, du_down_ref, table_ref,
    sets_ref, place_ref, wd_ref, down_ffd_ref, up_ref,
    out_ref, own_ref, far_ref, pair_ref, flat_ref,
    joined, down_sum, res_sum, flat_sum,
):
    first = pl.program_id(0) == 0
    low_rank = sets_ref.shape[1]
    width_hidden = wd_ref.shape[0]
    padded = down_ffd_ref.shape[1]

    @at_start
    def _():
        copy_rows(joined, 0, wd_ref)
        joined[width_hidden:padded, :] = jnp.zeros(
            (padded - width_hidden, joined.shape[1]), bfloat
        )
        copy_rows(joined, padded, up_ref)

    hidden = hidden_ref[...]
    inner = inner_ref[...]
    u_down = masked(
        nt(hidden, down_ffd_ref[...]), chosen_columns(table_ref[...], sets_ref[...])
    )
    out_ref[...] = low(nn(jnp.concatenate([hidden, u_down], axis=1), joined[...]))
    accumulate(down_sum, tn(du_ref[...], rows_ref[...]), first)
    accumulate(res_sum, tn(u_down, grad_ref[...]), first)
    for k, grown in enumerate(
        (
            tn(inner[:, :low_rank], ff_grad_ref[:, :padded]),
            tn(inner[:, low_rank:], ff_grad_ref[:, padded:]),
            tn(du_down_ref[...], hidden),
        )
    ):
        accumulate(flat_sum.at[:, k * padded : (k + 1) * padded], grown, first)

    @at_end
    def _():
        flat_ref[...] = low(flat_sum[...])
        emit_blocks(
            (down_sum.at[:low_rank], down_sum.at[low_rank:], res_sum),
            place_ref[0], own_ref, far_ref, pair_ref,
        )


def branch_kernel(
    branch_ref, raw_ref, map_ref, gate_ref, table_ref, entering_ref, gain_ref, sets_ref, wo_ref,
    down_out_t_ref, up_ref, up_gate_ref, *rest,
    heads, key_width, value_width, hops, last,
):
    if last:
        before_ref, *rest = rest
        got_refs, rest = rest[: hops - 1], rest[hops - 1 :]
        raw_grad_ref, gate_grad_ref, du_out_ref, du_gate_ref, *rest = rest
        sent_refs, (joined, total_ref) = rest[:hops], rest[hops:]
    else:
        raw_grad_ref, gate_grad_ref, du_out_ref, du_gate_ref, total_ref, joined = rest
    width = wo_ref.shape[1]

    @at_start
    def _():
        copy_rows(joined, 0, wo_ref, slice(0, width))
        copy_rows(joined, 0, down_out_t_ref, slice(width, None))

    chosen = chosen_columns(table_ref[...], sets_ref[...])
    branch = branch_ref[...]
    outputs = head_outputs(raw_ref, map_ref, entering_ref, heads, key_width, value_width)
    du_out = masked(nt(branch, up_ref[...]), chosen)
    du_out_ref[...] = du_out
    mixed_grad = nt(jnp.concatenate([branch, du_out], axis=1), joined[...])
    gain = gain_ref[0:1, :]
    gate_grads = []
    for h, output in enumerate(outputs):
        lanes = slice(h * value_width, (h + 1) * value_width)
        scale = lax.rsqrt(jnp.mean(output * output, axis=-1, keepdims=True) + EPS)
        value = gate_ref[:, lanes]
        logistic, active = silu_parts(value)
        incoming = mixed_grad[:, lanes]
        gate_grads.append(
            low(
                incoming
                * (output * scale * gain)
                * (logistic * (1.0 + value * (1.0 - logistic)))
            )
        )
        scaled = gain * (incoming * active)
        dot = jnp.mean(output * scaled, axis=-1, keepdims=True)
        raw_grad = low(scale * scaled - output * (scale * scale * scale * dot))
        raw_grad_ref[:, lanes] = raw_grad
        grown = tn(map_ref[:, h * key_width : (h + 1) * key_width], raw_grad)
        accumulate(total_ref.at[h], grown, pl.program_id(0) == 0)
    gate_grad = jnp.concatenate(gate_grads, axis=1)
    gate_grad_ref[...] = gate_grad
    du_gate_ref[...] = masked(nt(gate_grad, up_gate_ref[...]), chosen)
    if last:

        @at_end
        def _():
            for h in range(heads):
                passed = low(before_ref[h] + total_ref[h])
                sent_refs[0][h] = passed
                for hop in range(1, hops):
                    passed = low(tn(got_refs[hop - 1][h][:, value_width:], passed))
                    sent_refs[hop][h] = passed


def branch_after_kernel(
    branch_ref, z_ref, u_out_ref, rows_ref, inner_ref, du_out_ref, du_gate_ref, gate_grad_ref,
    down_grad_ref, res_grad_ref, flat_ref,
    flat_sum,
):
    lanes = z_ref.shape[1]
    accumulate(down_grad_ref, tn(du_gate_ref[...], rows_ref[...]), True)
    accumulate(res_grad_ref, tn(u_out_ref[...], branch_ref[...]), True)
    accumulate(flat_sum.at[:, :lanes], tn(du_out_ref[...], z_ref[...]), True)
    accumulate(flat_sum.at[:, lanes:], tn(inner_ref[...], gate_grad_ref[...]), True)

    @at_end
    def _():
        flat_ref[...] = low(flat_sum[...])


def settled_rows(pre_ref, tail_ref, arrived_ref, place_ref, quarter, window):
    block = window.shape[0]
    start = ((3 ^ place_ref[0]) + 1) * quarter - HALO - pl.program_id(0) * block
    window[...] = pre_ref[...]

    @pl.when((start >= 0) & (start < block))
    def _():
        window[pl.ds(pl.multiple_of(start, HALO), HALO), :] = low(tail_ref[...] + arrived_ref[...])

    return window[...]


def settle_grads_kernel(
    pre_ref, rows_ref, inner_ref, table_ref, tail_ref, arrived_ref, place_ref, sets_ref,
    up_qk_ref, up_value_ref, down_late_ref, res_late_ref,
    du_ref, own_ref, far_ref, pair_ref, flat_ref,
    window, down_sum, flat_sum,
    *, quarter,
):
    first = pl.program_id(0) == 0
    low_rank = sets_ref.shape[1]
    q_width = up_qk_ref.shape[2]
    chosen = chosen_columns(table_ref[...], sets_ref[...])
    pre = settled_rows(pre_ref, tail_ref, arrived_ref, place_ref, quarter, window)
    query, key, value = pre[:, :q_width], pre[:, q_width : 2 * q_width], pre[:, 2 * q_width :]
    inner = inner_ref[...]
    du = jnp.concatenate(
        [
            masked(nt(query, up_qk_ref[0]), chosen),
            masked(nt(key, up_qk_ref[1]), chosen),
            masked(nt(value, up_value_ref[...]), chosen),
        ],
        axis=1,
    )
    du_ref[...] = du
    accumulate(down_sum, tn(du, rows_ref[...]), first)
    at = 0
    for p, part in enumerate((query, key, value)):
        accumulate(
            flat_sum.at[:, at : at + part.shape[1]],
            tn(inner[:, p * low_rank : (p + 1) * low_rank], part),
            first,
        )
        at += part.shape[1]

    @at_end
    def _():
        flat_ref[...] = low(flat_sum[...])
        emit_blocks(
            [down_sum.at[p * low_rank : (p + 1) * low_rank] for p in range(3)]
            + [down_late_ref, res_late_ref],
            place_ref[0], own_ref, far_ref, pair_ref,
        )


def settle_kernel(
    pre_ref, gate_grad_ref, du_ref, du_gate_ref, mix_ref, tail_ref, arrived_ref, place_ref,
    down_ref, mix_weight_ref, wq_ref, wk_ref, wv_ref, wg_ref,
    part_ref,
    window, joined, joined_small,
    *, quarter,
):
    q_width, v_width = wq_ref.shape[1], wv_ref.shape[1]

    @at_start
    def _():
        at = 0
        for weight in (wq_ref, wk_ref, wv_ref, wg_ref):
            copy_rows(joined, 0, weight, slice(at, at + weight.shape[1]))
            at += weight.shape[1]
        maps, mixes = down_ref.shape[0], mix_weight_ref.shape[0]
        spare = joined_small.shape[0] - maps - mixes
        copy_rows(joined_small, 0, down_ref)
        joined_small[maps:, :] = jnp.concatenate(
            [mix_weight_ref[...], jnp.zeros((spare, joined_small.shape[1]), bfloat)], axis=0
        )

    pre = settled_rows(pre_ref, tail_ref, arrived_ref, place_ref, quarter, window)
    mix = low(mix_ref[...])
    spare = joined_small.shape[0] - down_ref.shape[0] - mix.shape[1]
    small = jnp.concatenate(
        [du_ref[...], du_gate_ref[...], mix, jnp.zeros((mix.shape[0], spare), bfloat)], axis=1
    )
    part_ref[...] = low(
        nt(jnp.concatenate([pre, gate_grad_ref[...]], axis=1), joined[...])
        + nn(small, joined_small[...])
    )


def assemble_kernel(
    place_ref, *refs, padded,
):
    pieces_last, pieces_feed = refs[:4], refs[4:8]
    last_ref, feed_ref, branch_ref = refs[8:11]
    down_ref, qk_ref, vg_ref, ff_ref, out_ref, ffd_ref, res_ref = refs[11:]
    place = place_ref[0]
    size = pieces_last[0].shape[1] // 5
    first = [down_ref.at[p] for p in range(4)] + [res_ref.at[0]]
    second = [down_ref.at[4], down_ref.at[5], res_ref.at[1]]
    for relative in range(4):
        start = pl.multiple_of((place ^ relative) * size, 128)
        for targets, piece in ((first, pieces_last[relative]), (second, pieces_feed[relative])):
            for k, target in enumerate(targets):
                target[:, pl.ds(start, size)] = piece[:, k * size : (k + 1) * size].astype(single)
    qk, values, hidden = qk_ref.shape[2], vg_ref.shape[2], ff_ref.shape[2]

    def lanes(ref, start, width):
        return ref[:, start : start + width].astype(single)

    own = 5 * size
    qk_ref[0], qk_ref[1] = lanes(last_ref, own, qk), lanes(last_ref, own + qk, qk)
    vg_ref[0] = lanes(last_ref, own + 2 * qk, values)
    at = last_ref.shape[1] + 3 * size
    out_ref[...] = lanes(branch_ref, at, values)
    vg_ref[1] = lanes(branch_ref, at + values, values)
    ff_ref[0] = lanes(feed_ref, 0, hidden)
    ff_ref[1] = lanes(feed_ref, padded, hidden)
    ffd_ref[...] = lanes(feed_ref, 2 * padded, hidden)


def assemble(where, shared, last, feed, branch, padded, shapes):
    rows = last.shape[0]
    block = min(32, rows)

    def spec(shape):
        if len(shape) == 2:
            return pl.BlockSpec((block, shape[1]), lambda i: (i, 0))
        return pl.BlockSpec((shape[0], block, shape[2]), lambda i: (0, i, 0))

    arrays = [*shared, last, feed, branch]
    return pl.pallas_call(
        functools.partial(assemble_kernel, padded=padded),
        out_shape=tuple(jax.ShapeDtypeStruct(shape, single) for shape in shapes),
        grid=(rows // block,),
        in_specs=[pl.BlockSpec(memory_space=pltpu.SMEM)] + [spec(a.shape) for a in arrays],
        out_specs=[spec(shape) for shape in shapes],
        compiler_params=pltpu.CompilerParams(
            dimension_semantics=("arbitrary",), vmem_limit_bytes=VMEM_LIMIT
        ),
        name="assemble",
    )(where, *arrays)


WHOLE, SCALAR = "whole", "scalar"


def by_rows(width, lane_block=0):
    return ("rows", width, lane_block)


def part(rows, index):
    return ("part", rows, index)


def pieces(width):
    return ("pieces", width)


def blocked_call(
    body, name, count, inputs, outputs, scratch, flops, block=STEP, half=None, into=()
):
    count_pieces = 4 if half is None else 2
    steps = count * count_pieces // 4 // block
    offset = (half or 0) * steps
    per = max(steps // count_pieces, 1)
    in_specs, arrays, moved, groups_in, extra = [], [], 0, [], []
    for array, kind in inputs:
        members = array if isinstance(array, (list, tuple)) else [array]
        groups_in.append(len(members))
        arrays += members
        moved += sum(a.size * a.dtype.itemsize for a in members)
        if kind == WHOLE:
            zeros = (0,) * array.ndim
            in_specs.append(
                pl.BlockSpec(
                    array.shape, lambda i, zeros=zeros: zeros, pipeline_mode=pl.Buffered(1)
                )
            )
        elif kind == SCALAR:
            in_specs.append(pl.BlockSpec(memory_space=pltpu.SMEM))
        elif kind[0] == "part":
            in_specs.append(
                pl.BlockSpec(
                    (kind[1], array.shape[1]),
                    lambda i, at=kind[2]: (at, 0),
                    pipeline_mode=pl.Buffered(1),
                )
            )
        elif kind[0] == "rows":
            in_specs.append(
                pl.BlockSpec((block, kind[1]), lambda i, lane=kind[2]: (i + offset, lane))
            )
        else:
            for b, member in enumerate(members):
                if steps == 1:
                    in_specs.append(pl.BlockSpec(member.shape, lambda i: (0, 0)))
                else:
                    in_specs.append(
                        pl.BlockSpec(
                            (block, kind[1]),
                            lambda i, b=b: (jnp.clip(i - b * per, 0, per - 1), 0),
                        )
                    )
            extra.append(pltpu.VMEM((block, kind[1]), members[0].dtype))
    out_specs, shapes, groups_out, aliases = [], [], [], {}
    into = list(into)
    held_arrays = []
    for shape, dtype, kind in outputs:
        if kind == "parts":
            quarter = shape[0] // 4
            spec = (block, shape[1])
            if half is not None:
                for b in range(2):
                    shapes.append(jax.ShapeDtypeStruct((quarter, shape[1]), dtype))
                    out_specs.append(
                        pl.BlockSpec(spec, lambda i, b=b: (jnp.clip(i - b * per, 0, per - 1), 0))
                    )
                groups_out.append(2)
            else:
                for rows in (quarter, quarter, 2 * quarter):
                    shapes.append(jax.ShapeDtypeStruct((rows, shape[1]), dtype))
                out_specs += [
                    pl.BlockSpec(spec, lambda i: (jnp.clip(i, 0, per - 1), 0)),
                    pl.BlockSpec(spec, lambda i: (jnp.clip(i - 2 * per, 0, per - 1), 0)),
                    pl.BlockSpec(
                        spec,
                        lambda i: (
                            jnp.clip(i - per, 0, per - 1) + jnp.clip(i - 3 * per + 1, 0, per), 0
                        ),
                    ),
                ]
                groups_out.append(3)
            extra.append(pltpu.VMEM(spec, dtype))
        else:
            groups_out.append(1)
            shapes.append(jax.ShapeDtypeStruct(shape, dtype))
            if kind == "rows":
                if into:
                    aliases[len(arrays) + len(held_arrays)] = len(shapes) - 1
                    held_arrays.append(into.pop(0))
                out_specs.append(pl.BlockSpec((block, shape[1]), lambda i: (i + offset, 0)))
            else:
                zeros = (0,) * len(shape)
                out_specs.append(pl.BlockSpec(shape, lambda i, zeros=zeros: zeros))
    in_specs += [pl.BlockSpec(memory_space=pl.ANY) for _ in held_arrays]

    def wrapped(*refs):
        refs = list(refs)
        spare = refs[len(in_specs) + len(out_specs) + len(scratch) :]
        own_scratch = refs[len(in_specs) + len(out_specs) : len(refs) - len(spare)]
        quarter = pl.program_id(0) // per
        given, later, at, used = [], [], 0, 0
        for size, (_, kind) in zip(groups_in, inputs):
            if kind[0] != "pieces":
                given.append(refs[at])
            else:
                held = spare[used]
                used += 1
                if steps == 1:
                    for b in range(size):
                        piece = refs[at + b]
                        held[b * piece.shape[0] : (b + 1) * piece.shape[0], :] = piece[...]
                else:
                    for b in range(size):

                        @pl.when(quarter == b)
                        def _(held=held, source=refs[at + b]):
                            copy_rows(held, 0, source)

                given.append(held)
            at += size
        at += len(held_arrays)
        for size in groups_out:
            if size == 1:
                given.append(refs[at])
            else:
                given.append(spare[used])
                later.append((spare[used], refs[at : at + size]))
                used += 1
            at += size
        body(*given, *own_scratch)
        for held, targets in later:
            if len(targets) == 2:
                placed = ((0, targets[0]), (1, targets[1]))
            else:
                placed = ((0, targets[0]), (2, targets[1]), (1, targets[2]), (3, targets[2]))
            for b, target in placed:

                @pl.when(quarter == b)
                def _(held=held, target=target):
                    copy_rows(target, 0, held)

    results = pl.pallas_call(
        wrapped,
        out_shape=tuple(shapes),
        grid=(steps,),
        in_specs=in_specs,
        out_specs=out_specs,
        scratch_shapes=list(scratch) + extra,
        input_output_aliases=aliases,
        compiler_params=pltpu.CompilerParams(
            dimension_semantics=("arbitrary",), vmem_limit_bytes=VMEM_LIMIT
        ),
        cost_estimate=pl.CostEstimate(flops=flops, bytes_accessed=moved, transcendentals=0),
        name=name,
    )(*arrays, *held_arrays)
    grouped, at = [], 0
    for size in groups_out:
        grouped.append(results[at] if size == 1 else results[at : at + size])
        at += size
    return grouped


def flip(array, bit):
    groups = lax.axis_size("head")
    return lax.ppermute(array, "head", [(i, i ^ bit) for i in range(groups)])


def gather_rows(array):
    far = flip(array, 2)
    near = flip(array, 1)
    return [array, near, far, flip(far, 1)]


def tie(*arrays):
    return lax.optimization_barrier(arrays)


def near_sum(parts):
    own, far, pair = parts
    size = own.shape[0]
    arrived = flip(pair, 1)
    return (
        own.astype(single) + arrived[:size].astype(single),
        low(far.astype(single) + arrived[size:].astype(single)),
    )


def halves_sum(first, second):
    near, corner = tie(flip(first[1], 1), second[1])
    return (
        first[0].astype(single) + near.astype(single),
        low(second[0].astype(single) + flip(corner, 1).astype(single)),
    )


def far_sum(own, far):
    return own + flip(far, 2).astype(single)


def shifted_along(array, axis, by):
    length = lax.axis_size(axis)
    pairs = [(i, i + by) for i in range(length) if 0 <= i + by < length]
    return lax.ppermute(array, axis, pairs)


def seq_rows(flat):
    members = lax.axis_size("seq")
    return flat.reshape(members, flat.shape[0] // members, flat.shape[1])


def share_sum(parts):
    summed = low(jnp.sum(parts.astype(single), axis=0))
    return jnp.broadcast_to(summed[None], parts.shape)


def exchange(parts):
    return lax.all_to_all(parts, "seq", 0, 0)


def all_rows(parts):
    return parts.reshape(-1, parts.shape[-1])


def rms_scale(rows, gain):
    return rows * lax.rsqrt(jnp.mean(rows * rows, axis=-1, keepdims=True) + EPS) * gain


def rms_back(rows, gain, incoming):
    _, back = jax.vjp(lambda value: rms_scale(value, gain), rows)
    return back(incoming)[0]


def on_device(
    block_input,
    out_grad,
    lengths,
    doc_sets,
    norm1_gain,
    w_query,
    w_key,
    w_value,
    conv_query,
    conv_key,
    conv_value,
    w_decay_beta,
    decay_rate,
    decay_bias,
    w_gate_out,
    out_gain,
    w_out,
    norm2_gain,
    w_gate,
    w_up,
    w_down,
    adapt_down,
    adapt_up_qk,
    adapt_up_vg,
    adapt_up_ff,
    adapt_down_out,
    adapt_down_ffd,
    adapt_up_res,
):
    groups = lax.axis_size("head")
    members = lax.axis_size("seq")
    place = lax.axis_index("head")
    quarter, width = block_input.shape
    count = quarter * groups
    heads = decay_rate.shape[0]
    key_width = w_query.shape[1] // heads
    value_width = w_value.shape[1] // heads
    sets, rank = adapt_down.shape[1], adapt_down.shape[3]
    low_rank = sets * rank
    qk = heads * key_width
    device_start = lax.axis_index("seq") * count
    starts = jnp.sum(
        jnp.where(
            jnp.arange(lengths.shape[0])[None, :] < jnp.arange(lengths.shape[0])[:, None],
            lengths[None, :],
            0,
        ),
        axis=1,
    )
    order = jnp.arange(groups, dtype=jnp.int32) ^ place

    def tables(positions):
        reached = positions[:, None] >= starts[None, :]
        token_start = jnp.max(jnp.where(reached, starts[None, :], -1), axis=1)
        ended = positions[:, None] >= (starts + lengths)[None, :]
        token_set = jnp.sum(jnp.where(reached & ~ended, doc_sets[None, :], 0), axis=1)
        pair = jnp.stack([token_start - device_start, token_set], axis=1).astype(single)
        return jnp.pad(pair, ((0, 0), (0, 8 - pair.shape[1])))

    table = tables(
        (
            device_start + order[:, None] * quarter + jnp.arange(quarter, dtype=jnp.int32)[None, :]
        ).reshape(-1)
    )
    halo_table = tables(device_start + jnp.arange(-HALO, 0, dtype=jnp.int32))
    column_sets = jnp.broadcast_to(
        (jnp.arange(low_rank, dtype=jnp.int32) // rank).astype(single)[None, :], (8, low_rank)
    )

    down = adapt_down.transpose(0, 1, 3, 2).reshape(6 * low_rank, width)
    up_qk = adapt_up_qk.reshape(2, low_rank, -1)
    up_vg = adapt_up_vg.reshape(2 * low_rank, -1)
    up_ff = adapt_up_ff.reshape(2, low_rank, -1)
    down_out = adapt_down_out.transpose(0, 2, 1).reshape(low_rank, -1)
    down_ffd = adapt_down_ffd.transpose(0, 2, 1).reshape(low_rank, -1)
    up_res = adapt_up_res.reshape(2 * low_rank, width)
    conv = jnp.concatenate([conv_query, conv_key, conv_value], axis=1).astype(single)
    scalars = jnp.stack([decay_rate, decay_bias])
    where = place.reshape(1).astype(jnp.int32)
    weight_mix = jnp.pad(
        w_decay_beta.transpose(1, 2, 0).reshape(2 * heads, width), ((0, 8 - 2 * heads), (0, 0))
    )
    gain = jnp.broadcast_to(out_gain[None, :], (8, value_width))
    hidden_width = w_down.shape[0]
    padded = -(-hidden_width // 256) * 256
    value_lanes = heads * value_width
    block_width = width // groups
    widen = lambda a: jnp.pad(a, [(0, 0)] * (a.ndim - 1) + [(0, padded - hidden_width)])

    input_float = block_input.astype(single)
    normed = low(rms_scale(input_float, norm1_gain))
    tail = normed[quarter - HALO :]
    halo = sum(
        lax.ppermute(
            tail,
            ("seq", "head"),
            [((s * groups) + groups - 1, (s + 1) * groups + h) for s in range(members - 1)],
        )
        for h in range(groups)
    )
    normed_near, normed_far = flip(normed, 1), flip(normed, 2)
    project_inputs = [
        (table, by_rows(8)),
        (column_sets, WHOLE),
        (down, part(4 * low_rank, 0)),
        (weight_mix, WHOLE),
        (w_query, WHOLE),
        (w_key, WHOLE),
        (w_value, WHOLE),
        (w_gate_out, WHOLE),
        (up_qk, WHOLE),
        (up_vg, WHOLE),
    ]
    project_outputs = [
        ((count, 2 * qk + value_lanes), bfloat, "rows"),
        ((count, 3 * low_rank), bfloat, "rows"),
        ((count, 8), single, "rows"),
        ((count, value_lanes), single, "rows"),
        ((count, low_rank), bfloat, "rows"),
    ]
    project_scratch = [pltpu.VMEM((width + low_rank, 2 * qk + 2 * value_lanes), bfloat)]
    projected = blocked_call(
        functools.partial(project_kernel, with_halo=False),
        "project_near",
        count,
        [([normed, normed_near], pieces(width)), *project_inputs],
        project_outputs,
        project_scratch,
        count * 2_000_000,
        half=0,
    )
    normed_far, projected[2] = tie(normed_far, projected[2])
    normed_all = [normed, normed_near, normed_far, flip(normed_far, 1)]
    pre, inner, columns, gate_input, inner_gate, pre_halo = blocked_call(
        functools.partial(project_kernel, with_halo=True),
        "project_far",
        count,
        [
            (normed_all[2:], pieces(width)),
            *project_inputs,
            (halo, WHOLE),
            (halo_table, WHOLE),
        ],
        project_outputs + [((HALO, 2 * qk + value_lanes), bfloat, "whole")],
        project_scratch,
        count * 2_000_000,
        half=1,
        into=projected,
    )
    out_grad_late, grad_near, pre = tie(out_grad, flip(out_grad, 1), pre)
    grad_far, grad_corner = flip(out_grad_late, 2), flip(grad_near, 2)
    raw_local, mapped, *saved, sent, sent_state = run_forward(
        where, pre, pre_halo, columns, conv, scalars, heads, key_width, value_width, quarter
    )

    hops = min(members - 1, -(-(DOC_MAX - 1) // count))
    got = [shifted_along(sent_state, "seq", hops)]
    got = [shifted_along(sent, "seq", hop) for hop in range(hops - 1, 0, -1)][::-1] + got
    grad_far, grad_corner, sent_state = tie(grad_far, grad_corner, sent_state)
    grad_all = [out_grad, grad_near, grad_far, grad_corner]
    hidden_grad, du_down = blocked_call(
        feed_before_kernel,
        "feed_before",
        count,
        [
            (grad_all, pieces(width)),
            (table, by_rows(8)),
            (column_sets, WHOLE),
            (w_down, WHOLE),
            (down_ffd.T, WHOLE),
            (up_res, part(low_rank, 1)),
        ],
        [((count, padded), single, "rows"), ((count, low_rank), bfloat, "rows")],
        [pltpu.VMEM((padded, width + low_rank), bfloat)],
        count * 6_000_000,
        block=STEP // 2,
    )
    raw_local, hidden_grad = tie(raw_local, hidden_grad)

    sizes = dict(heads=heads, key_width=key_width, value_width=value_width)
    attention_part, mixed, u_out, entering = blocked_call(
        functools.partial(attend_kernel, hops=hops, **sizes),
        "attend",
        count,
        [
            (raw_local, by_rows(value_lanes)),
            (mapped, by_rows(qk)),
            (gate_input, by_rows(value_lanes)),
            (table, by_rows(8)),
            (gain, WHOLE),
            (column_sets, WHOLE),
            (w_out, WHOLE),
            (down_out, WHOLE),
            (up_res, part(low_rank, 0)),
        ]
        + [(sent_by, WHOLE) for sent_by in got],
        [
            ((count, width), bfloat, "parts"),
            ((count, value_lanes), bfloat, "rows"),
            ((count, low_rank), bfloat, "rows"),
            ((heads, key_width, value_width), bfloat, "whole"),
        ],
        [pltpu.VMEM((value_lanes + low_rank, width), bfloat)],
        count * 5_000_000,
    )
    attention_own, attention_far = near_sum(attention_part)
    attention_arrived, up_ff_t, up_ff_padded, down_ffd_padded, down_out_t = tie(
        flip(attention_far, 2),
        up_ff.transpose(0, 2, 1),
        widen(up_ff),
        widen(down_ffd),
        down_out.T,
    )
    residual = input_float + (attention_own + attention_arrived.astype(single))
    normed_mid = low(rms_scale(residual, norm2_gain))
    mid_near, mid_far = flip(normed_mid, 1), flip(normed_mid, 2)

    feed_inputs = [
        (hidden_grad, by_rows(padded)),
        (table, by_rows(8)),
        (column_sets, WHOLE),
        (down, part(2 * low_rank, 2)),
        (w_gate.T, WHOLE),
        (w_up.T, WHOLE),
        (up_ff_t, WHOLE),
        (up_ff_padded, WHOLE),
    ]
    feed_outputs = [
        ((count, width), bfloat, "parts"),
        ((count, padded), bfloat, "rows"),
        ((count, 2 * padded), bfloat, "rows"),
        ((count, 2 * low_rank), bfloat, "rows"),
        ((count, 2 * low_rank), bfloat, "rows"),
    ]
    feed_scratch = [
        pltpu.VMEM((padded, width + low_rank), bfloat),
        pltpu.VMEM((padded, width + low_rank), bfloat),
        pltpu.VMEM((2 * padded + 2 * low_rank, width), bfloat),
    ]
    near_part, *fed = blocked_call(
        feed_kernel,
        "feed_near",
        count,
        [([normed_mid, mid_near], pieces(width)), *feed_inputs],
        feed_outputs,
        feed_scratch,
        count * 8_000_000,
        half=0,
    )
    mid_far, near_own = tie(mid_far, near_part[0])
    near_part = [near_own, near_part[1]]
    mid_all = [normed_mid, mid_near, mid_far, flip(mid_far, 1)]
    far_part, hidden, ff_grad, u_ff, du_ff = blocked_call(
        feed_kernel,
        "feed_far",
        count,
        [(mid_all[2:], pieces(width)), *feed_inputs],
        feed_outputs,
        feed_scratch,
        count * 8_000_000,
        half=1,
        into=fed,
    )
    grad_own, grad_sum = halves_sum(near_part, far_part)
    grad_sum, hidden = tie(grad_sum, hidden)
    grad_arrived = flip(grad_sum, 2)
    out_part, feed_own, feed_far, feed_pair, feed_owned = blocked_call(
        feed_after_kernel,
        "feed_after",
        count,
        [
            (mid_all, pieces(width)),
            (grad_all, pieces(width)),
            (hidden, by_rows(padded)),
            (ff_grad, by_rows(2 * padded)),
            (u_ff, by_rows(2 * low_rank)),
            (du_ff, by_rows(2 * low_rank)),
            (du_down, by_rows(low_rank)),
            (table, by_rows(8)),
            (column_sets, WHOLE),
            (where, SCALAR),
            (w_down, WHOLE),
            (down_ffd_padded, WHOLE),
            (up_res, part(low_rank, 1)),
        ],
        [
            ((count, width), bfloat, "parts"),
            ((low_rank, 3 * block_width), bfloat, "whole"),
            ((low_rank, 3 * block_width), bfloat, "whole"),
            ((2 * low_rank, 3 * block_width), bfloat, "whole"),
            ((low_rank, 3 * padded), bfloat, "whole"),
        ],
        [
            pltpu.VMEM((padded + low_rank, width), bfloat),
            pltpu.VMEM((2 * low_rank, width), single),
            pltpu.VMEM((low_rank, width), single),
            pltpu.VMEM((low_rank, 3 * padded), single),
        ],
        count * 16_000_000,
    )
    grad_landed, feed_far = tie(grad_arrived, feed_far)
    mid_grad = grad_own + grad_landed.astype(single)
    residual_grad = out_grad.astype(single) + rms_back(residual, norm2_gain, mid_grad)
    branch_low = low(residual_grad)
    branch_near, branch_far = flip(branch_low, 1), flip(branch_low, 2)
    out_own, out_far = near_sum(out_part)
    owned_parts = exchange(seq_rows(tie(feed_owned, branch_near)[0]))
    feed_sum, feed_sum_far = near_sum((feed_own, feed_far, tie(feed_pair, grad_arrived)[0]))
    feed_landed = flip(feed_sum_far, 2)

    branch_inputs = [
        (raw_local, by_rows(value_lanes)),
        (mapped, by_rows(qk)),
        (gate_input, by_rows(value_lanes)),
        (table, by_rows(8)),
        (entering, WHOLE),
        (gain, WHOLE),
        (column_sets, WHOLE),
        (w_out, WHOLE),
        (down_out_t, WHOLE),
        (up_res, part(low_rank, 0)),
        (up_vg, part(low_rank, 1)),
    ]
    branch_outputs = [
        ((count, value_lanes), bfloat, "rows"),
        ((count, value_lanes), bfloat, "rows"),
        ((count, low_rank), bfloat, "rows"),
        ((count, low_rank), bfloat, "rows"),
    ]
    branch_scratch = [pltpu.VMEM((value_lanes, width + low_rank), bfloat)]
    state_shape = (heads, key_width, value_width)
    *branched, state_near = blocked_call(
        functools.partial(branch_kernel, hops=hops, last=False, **sizes),
        "branch_near",
        count,
        [([branch_low, branch_near], pieces(width)), *branch_inputs],
        branch_outputs + [(state_shape, single, "whole")],
        branch_scratch,
        count * 12_000_000,
        half=0,
    )
    branch_far, state_near = tie(branch_far, state_near)
    branch_corner, owned_parts, out_far = tie(flip(branch_far, 1), owned_parts, out_far)
    branch_all = [branch_low, branch_near, branch_far, branch_corner]
    raw_grad, gate_grad, du_out, du_outgate, *state_grads = blocked_call(
        functools.partial(branch_kernel, hops=hops, last=True, **sizes),
        "branch_far",
        count,
        [(branch_all[2:], pieces(width)), *branch_inputs, (state_near, WHOLE)]
        + [(sent_by, WHOLE) for sent_by in got[:-1]],
        branch_outputs + [(state_shape, bfloat, "whole")] * hops,
        branch_scratch + [pltpu.VMEM(state_shape, single)],
        count * 4_000_000,
        half=1,
        into=branched,
    )
    state_got = [
        shifted_along(state_grads[hop - 1], "seq", -hop) for hop in range(hops, 0, -1)
    ][::-1]
    mixer_down_late, branch_res_grad, branch_flat = blocked_call(
        branch_after_kernel,
        "branch_after",
        count,
        [
            (branch_all, pieces(width)),
            (mixed, by_rows(value_lanes)),
            (u_out, by_rows(low_rank)),
            (normed_all, pieces(width)),
            (inner_gate, by_rows(low_rank)),
            (du_out, by_rows(low_rank)),
            (du_outgate, by_rows(low_rank)),
            (gate_grad, by_rows(value_lanes)),
        ],
        [
            ((low_rank, width), single, "whole"),
            ((low_rank, width), single, "whole"),
            ((low_rank, 2 * value_lanes), bfloat, "whole"),
        ],
        [pltpu.VMEM((low_rank, 2 * value_lanes), single)],
        count * 20_000_000,
        block=count,
    )
    feed_landed, du_out = tie(feed_landed, du_out)
    feed_shared = low(feed_sum + feed_landed.astype(single))
    owned_lanes = owned_parts.shape[-1]
    both = jnp.concatenate(
        [share_sum(owned_parts), seq_rows(feed_shared), seq_rows(branch_flat)], axis=2
    )
    raw_grad, both, out_far, *state_got = tie(raw_grad, both, out_far, *state_got)
    out_arrived = flip(out_far, 2)
    both = exchange(both)

    pre_grad, mix_grad, tail_grad, edge_grad = run_backward(
        where, pre, pre_halo, columns, conv, scalars, raw_grad, saved, entering, state_got,
        heads, key_width, value_width, quarter,
    )
    arrived = shifted_along(edge_grad, "seq", -1)
    arrived, both, out_arrived = tie(arrived, both, out_arrived)
    result = residual + (out_own + out_arrived.astype(single))
    later_parts = both[:, :, owned_lanes:]
    settled = [
        (pre_grad, by_rows(2 * qk + value_lanes)),
        (tail_grad, WHOLE),
        (arrived, WHOLE),
        (where, SCALAR),
    ]
    du_mix, last_own, last_far, last_pair, last_owned = blocked_call(
        functools.partial(settle_grads_kernel, quarter=quarter),
        "settle_grads",
        count,
        [
            settled[0],
            (normed_all, pieces(width)),
            (inner, by_rows(3 * low_rank)),
            (table, by_rows(8)),
            *settled[1:],
            (column_sets, WHOLE),
            (up_qk, WHOLE),
            (up_vg, part(low_rank, 0)),
            (mixer_down_late, WHOLE),
            (branch_res_grad, WHOLE),
        ],
        [
            ((count, 3 * low_rank), bfloat, "rows"),
            ((low_rank, 5 * block_width), bfloat, "whole"),
            ((low_rank, 5 * block_width), bfloat, "whole"),
            ((2 * low_rank, 5 * block_width), bfloat, "whole"),
            ((low_rank, 2 * qk + value_lanes), bfloat, "whole"),
        ],
        [
            pltpu.VMEM((STEP, 2 * qk + value_lanes), bfloat),
            pltpu.VMEM((3 * low_rank, width), single),
            pltpu.VMEM((low_rank, 2 * qk + value_lanes), single),
        ],
        count * 4_000_000,
    )
    last_own, last_far = near_sum((last_own, last_far, last_pair))
    last_far, gate_grad = tie(last_far, gate_grad)
    (normed_part,) = blocked_call(
        functools.partial(settle_kernel, quarter=quarter),
        "settle",
        count,
        [
            settled[0],
            (gate_grad, by_rows(value_lanes)),
            (du_mix, by_rows(3 * low_rank)),
            (du_outgate, by_rows(low_rank)),
            (mix_grad, by_rows(8)),
            *settled[1:],
            (down, part(4 * low_rank, 0)),
            (weight_mix, WHOLE),
            (w_query, WHOLE),
            (w_key, WHOLE),
            (w_value, WHOLE),
            (w_gate_out, WHOLE),
        ],
        [((count, width), bfloat, "parts")],
        [
            pltpu.VMEM((STEP // 2, 2 * qk + value_lanes), bfloat),
            pltpu.VMEM((width, 2 * qk + 2 * value_lanes), bfloat),
            pltpu.VMEM((5 * low_rank, width), bfloat),
        ],
        count * 10_000_000,
        block=STEP // 2,
    )
    last_flat = jnp.concatenate([low(far_sum(last_own, last_far)), last_owned], axis=1)
    feed_rows = all_rows(both)
    last_lanes = last_flat.shape[1]
    both = exchange(jnp.concatenate([seq_rows(last_flat), share_sum(later_parts)], axis=2))
    normed_own, normed_sum_far = near_sum(normed_part)
    both, normed_sum_far = tie(both, normed_sum_far)
    normed_landed = flip(normed_sum_far, 2)
    branch_rows = all_rows(both)
    feed_piece = branch_rows[:, last_lanes : last_lanes + 3 * block_width]
    feed_piece_far = flip(feed_piece, 2)
    last_parts = both[:, :, :last_lanes]
    last_rows = all_rows(exchange(share_sum(last_parts)))
    piece = last_rows[:, : 5 * block_width]
    piece_far = flip(piece, 2)
    normed_landed, feed_piece_far, _ = tie(normed_landed, feed_piece_far, piece)
    feed_pieces = [feed_piece, flip(feed_piece, 1), feed_piece_far, flip(feed_piece_far, 1)]
    normed_grad = normed_own + normed_landed.astype(single)
    input_grad = residual_grad + rms_back(input_float, norm1_gain, normed_grad)
    piece_far, input_grad, feed_pieces[3] = tie(piece_far, input_grad, feed_pieces[3])
    last_pieces = [piece, flip(piece, 1), piece_far, flip(piece_far, 1)]
    down_grad, qk_grad, vg_grad, ff_grads, out_grads, ffd_grads, res_grad = assemble(
        where,
        [*last_pieces, *feed_pieces],
        last_rows,
        feed_rows,
        branch_rows,
        padded,
        [
            (6, low_rank, width),
            (2, low_rank, qk),
            (2, low_rank, value_lanes),
            (2, low_rank, hidden_width),
            (low_rank, value_lanes),
            (low_rank, hidden_width),
            (2, low_rank, width),
        ],
    )

    def as_down(rows):
        return rows.reshape(rows.shape[:-2] + (sets, rank, -1)).swapaxes(-1, -2)

    def as_up(rows):
        return rows.reshape(rows.shape[0], sets, rank, -1)

    return (
        low(result),
        input_grad,
        as_down(down_grad),
        as_up(qk_grad),
        as_up(vg_grad),
        as_up(ff_grads),
        as_down(out_grads),
        as_down(ffd_grads),
        as_up(res_grad),
    )


def solution(mesh):
    rows = P(("seq", "head"), None)
    lanes = P(None, "head")
    last = P(None, None, None, "head")
    middle = P(None, "head", None)
    in_specs = (
        rows, rows, P(), P(), P(), lanes, lanes, lanes, lanes, lanes, lanes,
        P(None, None, "head"), P("head"), P("head"), lanes, P(), P("head", None), P(), lanes,
        lanes, P("head", None), P(), last, last, last, middle, middle, P(),
    )
    out_specs = (rows, rows, P(), last, last, last, middle, middle, P())
    return jax.shard_map(
        on_device, mesh=mesh, in_specs=in_specs, out_specs=out_specs, check_vma=False
    )
```
